32 devices in a mesh: grp: 4 (over x, core), ctx: 4 (over z), wt: 2 (over y).
Axes of the slice: x: 2, y: 2, z: 4, core: 2. Of those that a mesh axis runs over, the one named last changes fastest.
Arguments:
- tokens: bfloat16 [8, 2048, 1280], P(('grp', 'wt'), 'ctx'), may hold values from -6 to 6
- segments: int32 [8, 2048], P(('grp', 'wt')), may hold values from 0 to 2, as said below
- w_qkv: bfloat16 [1280, 3840], P('wt'), may hold values from -0.15625 to 0.15625
- w_proj: bfloat16 [1280, 1280], P('wt'), may hold values from -1.25 to 1.25
- w_in: bfloat16 [1280, 1280], P('wt'), may hold values from -0.15625 to 0.15625
- w_out: bfloat16 [1280, 1280], P('wt'), may hold values from -0.15625 to 0.15625
- gain_attn: float32 [1280], replicated, may hold values from 0.5 to 1.5
- gain_mlp: float32 [1280], replicated, may hold values from 0.5 to 1.5
- query_scale: float32 [80], replicated, may hold values from -0.5 to 1.5
- cotangent: bfloat16 [8, 2048, 1280], P(('grp', 'wt'), 'ctx'), may hold values from -6 to 6
Outputs:
- layer_out: bfloat16 [8, 2048, 1280], P(('grp', 'wt'), 'ctx')
- grad_tokens: bfloat16 [8, 2048, 1280], P(('grp', 'wt'), 'ctx')
- grad_w_qkv: float32 [1280, 3840], P('wt')
- grad_w_proj: float32 [1280, 1280], P('wt')
- grad_w_in: float32 [1280, 1280], P('wt')
- grad_w_out: float32 [1280, 1280], P('wt')
- grad_gain_attn: float32 [1280], replicated
- grad_gain_mlp: float32 [1280], replicated
- grad_query_scale: float32 [80], replicated
The draws below stay inside these ranges and needn't reach their ends.
Inputs may be any that keep to these rules, and one draw needn't show every extreme that they name: `segments`: in each group the id starts at 0, never falls, and every id of 0 to 2 is used. Segment 0 ends 1024 - r tokens into the group, r below 256; each later continuation starts 512 + j tokens after the one before, j within 128 either way; the last runs to the group's end.
All inputs are finite; a program needn't handle non-finite values.
Results may differ from the reference program's by a relative error of at most 0.02.
Values may be sent and summed in bfloat16 or wider, within the bound.
No kernel may reach another device: no remote copies, remote signals or barrier semaphores. Data moves between devices by JAX's collectives and lax.ppermute only.
A program may use at most 256 MiB of HBM per device.

```python
import math
from functools import partial
import jax
import jax.numpy as jnp
from jax import lax

D = 1280
H = 16
HD = 80
FF = 1280
PROMPT = 1024
CONT = 512
CONTS = 2
GROUP = 2048
GROUPS = 8


def draw_segments(key, part):

    def one_group(group_key):
        key_first, key_jitter = jax.random.split(group_key)
        prompt_end = PROMPT - jax.random.randint(key_first, (), 0, CONT // 2)
        jitter = jax.random.randint(key_jitter, (CONTS,), -(CONT // 4), CONT // 4 + 1)
        jitter = jitter * (jnp.arange(CONTS) > 0).astype(jnp.int32)
        bounds = prompt_end + jnp.arange(CONTS, dtype=jnp.int32) * CONT + jitter
        positions = jnp.arange(GROUP, dtype=jnp.int32)
        return jnp.sum((positions[:, None] >= bounds[None, :]).astype(jnp.int32), axis=1).astype(jnp.int32)
    return jax.vmap(one_group)(jax.random.split(jax.random.fold_in(key, 7), GROUPS))


def shard_levels(stream_key, dims, cuts, smallest, largest):
    gain, own = 1.0, jax.random.fold_in(stream_key, 6)
    for axis_at, parts in cuts:
        steps = jnp.exp(jax.random.uniform(jax.random.fold_in(own, axis_at), (parts,), jnp.float32, smallest / len(cuts), largest / len(cuts)))
        gain = gain * jnp.repeat(steps, dims[axis_at] // parts).reshape([-1 if axis == axis_at else 1 for axis in range(len(dims))])
    return gain


def normal_values(rng, dims, scale, reach, cuts=(), kind=jnp.bfloat16):
    entries = scale * jax.random.normal(rng, dims, jnp.float32)
    if cuts:
        entries = entries * shard_levels(rng, dims, cuts, -0.22, 0.18)
    return jnp.clip(entries, -reach, reach).astype(kind)


def setup_inputs(seed: int = 0) -> dict:
    key_list = jax.random.split(jax.random.key(seed), 11)
    tokens = normal_values(key_list[0], (GROUPS, GROUP, D), 1.0, 6.0, ((0, 8), (1, 4)))
    segments = draw_segments(jax.random.fold_in(key_list[10], 71), 0)
    w_qkv = normal_values(key_list[2], (D, 3 * D), D ** -0.5, 0.15625, ((0, 2),))
    w_proj = normal_values(key_list[3], (D, D), (D // 64) ** -0.5, 1.25, ((0, 2),))
    w_in = normal_values(key_list[4], (D, FF), D ** -0.5, 0.15625, ((0, 2),))
    w_out = normal_values(key_list[5], (FF, D), FF ** -0.5, 0.15625, ((0, 2),))
    gain_attn = jnp.clip(1.0 + 0.1 * jax.random.normal(key_list[6], (D,), jnp.float32), 0.5, 1.5)
    gain_mlp = jnp.clip(1.0 + 0.1 * jax.random.normal(key_list[7], (D,), jnp.float32), 0.5, 1.5)
    query_scale = jnp.clip(jax.random.uniform(key_list[8], (HD,), jnp.float32, -0.5, 1.5), -0.5, 1.5)
    cotangent = normal_values(key_list[9], (GROUPS, GROUP, D), 1.0, 6.0, ((0, 8), (1, 4)))
    return dict(tokens=tokens, segments=segments, w_qkv=w_qkv, w_proj=w_proj, w_in=w_in, w_out=w_out, gain_attn=gain_attn, gain_mlp=gain_mlp, query_scale=query_scale, cotangent=cotangent)


epsilon = 1e-06
scale_base = 1.442695041
masked_fill = -1e+30
highest = lax.Precision.HIGHEST

@jax.custom_vjp
def low(v):
    return lax.optimization_barrier(v.astype(jnp.bfloat16)).astype(jnp.float32)

@jax.custom_vjp
def low_back(v):
    return v

def low_keep(v):
    return (low(v), None)

def low_pass(kept, grad):
    return (grad,)

def back_keep(v):
    return (v, None)

def back_low(kept, grad):
    return (low(grad),)
low.defvjp(low_keep, low_pass)
low_back.defvjp(back_keep, back_low)

def rms_inverse(values):
    return lax.rsqrt(lax.optimization_barrier(jnp.mean(values * values, axis=-1, keepdims=True)) + epsilon)

def attend_block(keys_all, values_all, segments_row, bundle):
    queries_blk, qpos_blk, qseg_blk = bundle
    positions = jnp.arange(keys_all.shape[0])
    scores = low_back(jnp.einsum('qhd,khd->hqk', queries_blk, keys_all, precision=highest))
    allowed = (positions[None, :] <= qpos_blk[:, None]) & ((segments_row[None, :] == 0) | (segments_row[None, :] == qseg_blk[:, None]))
    scores = jnp.where(allowed[None], scores, masked_fill)
    weights = low(jax.nn.softmax(scores, axis=-1))
    return jnp.einsum('hqk,khd->qhd', weights, values_all, precision=highest)

def group_forward(params, bundle):
    inputs, segments_row = bundle
    w_qkv, w_proj, w_in, w_out, gain_attn, gain_mlp, query_scale = params
    length = inputs.shape[0]
    normed = low(inputs * rms_inverse(inputs) * gain_attn)
    project = low_back(jnp.dot(normed, w_qkv, precision=highest))
    dim_scale = scale_base / math.sqrt(HD) * jax.nn.softplus(query_scale)
    queries = low(project[:, :D].reshape(length, H, HD) * dim_scale)
    keys = low(project[:, D:2 * D]).reshape(length, H, HD)
    values = low(project[:, 2 * D:]).reshape(length, H, HD)
    block_len = min(512, length)
    blocks = length // block_len
    positions = jnp.arange(length)
    mapped = lax.map(jax.checkpoint(partial(attend_block, keys, values, segments_row)), (queries.reshape(blocks, block_len, H, HD), positions.reshape(blocks, block_len), segments_row.reshape(blocks, block_len)))
    attended = low(low_back(mapped.reshape(length, D)))
    resid = inputs + low_back(jnp.dot(attended, w_proj, precision=highest))
    normed_mlp = low(resid * rms_inverse(resid) * gain_mlp)
    hidden = low_back(jnp.dot(normed_mlp, w_in, precision=highest))
    active = low(jax.nn.silu(hidden))
    return resid + low_back(jnp.dot(active, w_out, precision=highest))

def reference(tokens, segments, w_qkv, w_proj, w_in, w_out, gain_attn, gain_mlp, query_scale, cotangent):
    params = (w_qkv.astype(jnp.float32), w_proj.astype(jnp.float32), w_in.astype(jnp.float32), w_out.astype(jnp.float32), gain_attn.astype(jnp.float32), gain_mlp.astype(jnp.float32), query_scale.astype(jnp.float32))
    inputs = tokens.astype(jnp.float32)

    def forward(params_in, inputs_in):
        return lax.map(jax.checkpoint(partial(group_forward, params_in)), (inputs_in, segments))
    result, pullback = jax.vjp(forward, params, inputs)
    grad_params, grad_inputs = pullback(cotangent.astype(jnp.float32))
    return (result.astype(jnp.bfloat16), grad_inputs.astype(jnp.bfloat16), grad_params[0], grad_params[1], grad_params[2], grad_params[3], grad_params[4], grad_params[5], grad_params[6])
```

```python
import functools
import math

import jax
import jax.numpy as jnp
from jax import lax
from jax.experimental import pallas as pl
from jax.experimental.pallas import tpu as pltpu
from jax.sharding import Mesh
from jax.sharding import PartitionSpec as P

D = 1280
H = 16
HD = 80
LN = 128
epsilon = 1e-06
scale_base = 1.442695041
log2e = 1.4426950408889634
NEG = -1e30
f32 = jnp.float32
bf16 = jnp.bfloat16
AXES = ("gx", "gc", "ctx", "wt")


def block_flags(seg_row, bq, bk):
    n = seg_row.shape[0]
    q = seg_row.reshape(n // bq, bq)
    k = seg_row.reshape(n // bk, bk)
    qf, ql = q[:, 0][:, None], q[:, -1][:, None]
    kf, kl = k[:, 0][None], k[:, -1][None]
    qs = jnp.arange(n // bq, dtype=jnp.int32)[:, None] * bq
    ks = jnp.arange(n // bk, dtype=jnp.int32)[None] * bk
    below = ks + bk - 1 <= qs
    skip = (ks > qs + bq - 1) | ((kf > 0) & (kl < qf))
    same = (qf == ql) & (kl == ql) & ((kf == kl) | ((kf == 0) & (kl == 1)))
    full = below & ((kl == 0) | same)
    return jnp.where(skip, 0, jnp.where(full, 1, 2)).astype(jnp.int32).reshape(-1)


def put_split(base, col, lanes):
    hi = col.astype(bf16).astype(f32)
    rest = col - hi
    mid = rest.astype(bf16).astype(f32)
    out = jnp.where(lanes == HD, hi, base)
    out = jnp.where(lanes == HD + 1, mid, out)
    return jnp.where(lanes == HD + 2, rest - mid, out).astype(bf16)


def fwd_kernel(flags, q_ref, kv, segc, segr, att, of, qaug, m_s, acc_s, *, nh, bq, bk, nk):
    qi = pl.program_id(0)
    m_s[...] = jnp.full_like(m_s, NEG)
    acc_s[...] = jnp.zeros_like(acc_s)

    def step(kb, masked):
        ko = pl.multiple_of(kb * bk, bk)
        if masked:
            qpos = qi * bq + lax.broadcasted_iota(jnp.int32, (bq, bk), 0)
            kpos = ko + lax.broadcasted_iota(jnp.int32, (bq, bk), 1)
            ks = segr[:, pl.ds(ko, bk)]
            allowed = (kpos <= qpos) & ((ks == 0) | (ks == segc[...]))
        for h in range(nh):
            q = q_ref[:, h * LN : (h + 1) * LN]
            k = kv[pl.ds(ko, bk), h * LN : (h + 1) * LN]
            v = kv[pl.ds(ko, bk), (nh + h) * LN : (nh + h + 1) * LN]
            s = lax.dot_general(q, k, (((1,), (1,)), ((), ())), preferred_element_type=f32)
            if masked:
                s = jnp.where(allowed, s, NEG)
            old = m_s[h]
            new = jnp.maximum(old, jnp.max(s, axis=1, keepdims=True))
            p = jnp.exp2(s - new[:, :1]).astype(bf16)
            m_s[h] = new
            acc_s[h] = acc_s[h] * jnp.exp2(old - new) + jnp.dot(p, v, preferred_element_type=f32)

    def body(kb, carry):
        flag = flags[qi * nk + kb]

        @pl.when(flag == 1)
        def _():
            step(kb, False)

        @pl.when(flag == 2)
        def _():
            step(kb, True)

        return carry

    lax.fori_loop(0, (qi * bq + bq + bk - 1) // bk, body, 0)
    lanes = lax.broadcasted_iota(jnp.int32, (bq, LN), 1)
    outs = []
    for h in range(nh):
        acc = acc_s[h]
        total = acc[:, HD : HD + 1]
        out = acc / total
        of[:, h * LN : (h + 1) * LN] = jnp.where(lanes < HD, out, 0.0)
        outs.append(out[:, :HD])
        lse = m_s[h][:, :1] + jnp.log2(total)
        qaug[:, h * LN : (h + 1) * LN] = put_split(
            q_ref[:, h * LN : (h + 1) * LN].astype(f32), -lse, lanes
        )
    att[...] = jnp.concatenate(outs, axis=1).astype(bf16)


def attn_fwd(q, kv, seg_row, nh, bq=512, bk=512):
    n = q.shape[0]
    w = nh * LN
    spec = pltpu.PrefetchScalarGridSpec(
        num_scalar_prefetch=1,
        grid=(n // bq,),
        in_specs=[
            pl.BlockSpec((bq, w), lambda i, f: (i, 0)),
            pl.BlockSpec((n, 2 * w), lambda i, f: (0, 0)),
            pl.BlockSpec((bq, 1), lambda i, f: (i, 0)),
            pl.BlockSpec((1, n), lambda i, f: (0, 0)),
        ],
        out_specs=[
            pl.BlockSpec((bq, nh * HD), lambda i, f: (i, 0)),
            pl.BlockSpec((bq, w), lambda i, f: (i, 0)),
            pl.BlockSpec((bq, w), lambda i, f: (i, 0)),
        ],
        scratch_shapes=[pltpu.VMEM((nh, bq, LN), f32), pltpu.VMEM((nh, bq, LN), f32)],
    )
    return pl.pallas_call(
        functools.partial(fwd_kernel, nh=nh, bq=bq, bk=bk, nk=n // bk),
        out_shape=[
            jax.ShapeDtypeStruct((n, nh * HD), bf16),
            jax.ShapeDtypeStruct((n, w), f32),
            jax.ShapeDtypeStruct((n, w), bf16),
        ],
        grid_spec=spec,
        compiler_params=pltpu.CompilerParams(vmem_limit_bytes=40 << 20),
        cost_estimate=pl.CostEstimate(
            flops=20_000_000_000, transcendentals=10_000_000, bytes_accessed=16_000_000
        ),
        name="attn_fwd",
    )(block_flags(seg_row, bq, bk), q, kv, seg_row[:, None], seg_row[None])


def bwd_kernel(flags, qa, kv, do, of, segc, segr, scale, dqkv, gscale, doa_s, dq_s, dk_s, dv_s, *, nh, bq, bk, n):
    nk = n // bk
    nq = n // bq
    kb = pl.program_id(0)
    lanes = lax.broadcasted_iota(jnp.int32, (bq, LN), 1)

    @pl.when(kb == 0)
    def _():
        dq_s[...] = jnp.zeros_like(dq_s)

        def prep(i, carry):
            r = pl.multiple_of(i * bq, bq)
            d = do[pl.ds(r, bq), :].astype(f32)
            for h in range(nh):
                dh = jnp.concatenate(
                    [d[:, h * HD : (h + 1) * HD], jnp.zeros((bq, LN - HD), f32)], axis=1
                )
                delta = jnp.sum(dh * of[pl.ds(r, bq), h * LN : (h + 1) * LN], axis=1, keepdims=True)
                doa_s[pl.ds(r, bq), h * LN : (h + 1) * LN] = put_split(dh, -delta, lanes)
            return carry

        lax.fori_loop(0, nq, prep, 0)

    dk_s[...] = jnp.zeros_like(dk_s)
    dv_s[...] = jnp.zeros_like(dv_s)
    ko = kb * bk
    nt = (((1,), (1,)), ((), ()))
    tn = (((0,), (0,)), ((), ()))

    def step(qi, masked):
        qo = pl.multiple_of(qi * bq, bq)
        if masked:
            kpos = ko + lax.broadcasted_iota(jnp.int32, (bk, bq), 0)
            qpos = qo + lax.broadcasted_iota(jnp.int32, (bk, bq), 1)
            ks = segc[...]
            allowed = (kpos <= qpos) & ((ks == 0) | (ks == segr[:, pl.ds(qo, bq)]))
        for h in range(nh):
            c = slice(h * LN, (h + 1) * LN)
            q = qa[pl.ds(qo, bq), c]
            k = kv[:, c]
            v = kv[:, (nh + h) * LN : (nh + h + 1) * LN]
            d = doa_s[pl.ds(qo, bq), c]
            p = jnp.exp2(lax.dot_general(k, q, nt, preferred_element_type=f32))
            if masked:
                p = jnp.where(allowed, p, 0.0)
            ds = (p * lax.dot_general(v, d, nt, preferred_element_type=f32)).astype(bf16)
            dv_s[h] += jnp.dot(p.astype(bf16), d, preferred_element_type=f32)
            dk_s[h] += jnp.dot(ds, q, preferred_element_type=f32)
            dq_s[h, pl.ds(qo, bq), :] += lax.dot_general(ds, k, tn, preferred_element_type=f32)

    def body(qi, carry):
        flag = flags[qi * nk + kb]

        @pl.when(flag == 1)
        def _():
            step(qi, False)

        @pl.when(flag == 2)
        def _():
            step(qi, True)

        return carry

    lax.fori_loop(ko // bq, nq, body, 0)
    r = pl.multiple_of(ko, bk)
    ln2 = math.log(2.0)
    dqkv[pl.ds(r, bk), nh * HD : 3 * nh * HD] = jnp.concatenate(
        [dk_s[h][:, :HD] * ln2 for h in range(nh)] + [dv_s[h][:, :HD] for h in range(nh)], axis=1
    ).astype(bf16)

    @pl.when(kb == nk - 1)
    def _():
        gscale[...] = jnp.zeros_like(gscale)

        def fin(i, carry):
            r = pl.multiple_of(i * bq, bq)
            rows = pl.ds(r, bq)
            part = jnp.zeros((1, LN), f32)
            for h in range(nh):
                part = part + jnp.sum(
                    dq_s[h, rows, :] * qa[rows, h * LN : (h + 1) * LN].astype(f32), axis=0, keepdims=True
                )
            gscale[...] += jnp.broadcast_to(part, gscale.shape)
            grads = jnp.concatenate([dq_s[h, rows, :][:, :HD] for h in range(nh)], axis=1)
            dqkv[rows, 0 : nh * HD] = (grads * scale[...]).astype(bf16)
            return carry

        lax.fori_loop(0, nq, fin, 0)


def attn_bwd(qa, kv, do, of, seg_row, scale, nh, bq=512, bk=512):
    n = qa.shape[0]
    w = nh * LN
    spec = pltpu.PrefetchScalarGridSpec(
        num_scalar_prefetch=1,
        grid=(n // bk,),
        in_specs=[
            pl.BlockSpec((n, w), lambda i, f: (0, 0)),
            pl.BlockSpec((bk, 2 * w), lambda i, f: (i, 0)),
            pl.BlockSpec((n, nh * HD), lambda i, f: (0, 0)),
            pl.BlockSpec((n, w), lambda i, f: (0, 0)),
            pl.BlockSpec((bk, 1), lambda i, f: (i, 0)),
            pl.BlockSpec((1, n), lambda i, f: (0, 0)),
            pl.BlockSpec((1, nh * HD), lambda i, f: (0, 0)),
        ],
        out_specs=[
            pl.BlockSpec((n, 3 * nh * HD), lambda i, f: (0, 0)),
            pl.BlockSpec((8, LN), lambda i, f: (0, 0)),
        ],
        scratch_shapes=[
            pltpu.VMEM((n, w), bf16),
            pltpu.VMEM((nh, n, LN), f32),
            pltpu.VMEM((nh, bk, LN), f32),
            pltpu.VMEM((nh, bk, LN), f32),
        ],
    )
    return pl.pallas_call(
        functools.partial(bwd_kernel, nh=nh, bq=bq, bk=bk, n=n),
        out_shape=[
            jax.ShapeDtypeStruct((n, 3 * nh * HD), bf16),
            jax.ShapeDtypeStruct((8, LN), f32),
        ],
        grid_spec=spec,
        compiler_params=pltpu.CompilerParams(vmem_limit_bytes=48 << 20),
        cost_estimate=pl.CostEstimate(
            flops=40_000_000_000, transcendentals=10_000_000, bytes_accessed=20_000_000
        ),
        name="attn_bwd",
    )(block_flags(seg_row, bq, bk), qa, kv, do, of, seg_row[:, None], seg_row[None], scale)


def rms_inverse(values):
    return lax.rsqrt(jnp.mean(values * values, axis=-1, keepdims=True) + epsilon)


def norm_back(values, inverse, grad_scaled):
    return inverse * grad_scaled - values * (inverse * inverse * inverse) * jnp.mean(
        grad_scaled * values, axis=-1, keepdims=True
    )


def dot(left, right):
    return jnp.dot(left, right, preferred_element_type=f32)


def times_trans(left, right):
    return lax.dot_general(left, right, (((1,), (1,)), ((), ())), preferred_element_type=f32)


def trans_times(left, right):
    return lax.dot_general(left, right, (((0,), (0,)), ((), ())), preferred_element_type=f32)


def rows_at(array, start, count):
    return lax.dynamic_slice_in_dim(array, start, count, 0)


def put_rows(array, rows, start):
    return lax.dynamic_update_slice_in_dim(array, rows, start, 0)


def make_local(sizes):
    def pairs(target):
        found = []
        for gx in range(sizes["gx"]):
            for gc in range(sizes["gc"]):
                for z in range(sizes["ctx"]):
                    for w in range(sizes["wt"]):
                        goal = target(gx, gc, z, w)
                        if goal is not None:
                            found.append((place(gx, gc, z, w), place(*goal)))
        return found

    def place(gx, gc, z, w):
        return ((gx * sizes["gc"] + gc) * sizes["ctx"] + z) * sizes["wt"] + w

    def send(value, target):
        return lax.ppermute(value, AXES, pairs(target))

    def core_mate(gx, gc, z, w):
        return (gx, 1 - gc, z, w)

    def x_mate(gx, gc, z, w):
        return (1 - gx, gc, z, w)

    def near_mate(gx, gc, z, w):
        return (gx, gc, z ^ 1, w)

    def far_mate(gx, gc, z, w):
        return (gx, gc, z ^ 2, w)

    def cross_mate(gx, gc, z, w):
        return (gx, 1 - gc, z ^ 1, w)

    def wt_mate(gx, gc, z, w):
        return (gx, gc, z, 1 - w)

    def to_host(gx, gc, z, w):
        return (gx, z & 1, 2 * gc + (z >> 1), w)

    def to_home(gx, gc, z, w):
        return (gx, z >> 1, 2 * (z & 1) + gc, w)

    def hop1(gx, gc, z, w):
        if gc == 0:
            return (gx, 0, z - 1, w) if z > 0 else None
        return (gx, 1, z + 1, w) if z < 3 else None

    def hop2(gx, gc, z, w):
        if gc == 0:
            return (gx, 0, z - 1, w) if z in (1, 2) else None
        return (gx, 1, z + 1, w) if z in (1, 2) else None

    def hop3(gx, gc, z, w):
        if gc == 0:
            return (gx, 0, z ^ 1, w) if z < 2 else None
        return (gx, 1, z ^ 1, w) if z > 1 else None

    def lane_share(gx, gc, z, w):
        return (gx, 1 - gc, z, w) if gc == z >> 1 else None

    def gather_wt(value):
        if sizes["wt"] == 2:
            other = send(value, wt_mate)
            first = lax.axis_index("wt") == 0
            return jnp.stack([jnp.where(first, value, other), jnp.where(first, other, value)])
        return lax.all_gather(value, "wt", axis=0, tiled=False)

    def scatter_wt(value):
        if sizes["wt"] == 2:
            own = lax.axis_index("wt")
            mine = lax.dynamic_index_in_dim(value, own, 0, keepdims=False)
            other = send(lax.dynamic_index_in_dim(value, 1 - own, 0, keepdims=False), wt_mate)
            return (mine.astype(f32) + other.astype(f32)).astype(bf16)
        return lax.psum_scatter(value, "wt", scatter_dimension=0, tiled=False)

    def halve(value, bit, mate):
        half = value.shape[0] // 2
        other = send(rows_at(value, (1 - bit) * half, half), mate)
        return (rows_at(value, bit * half, half).astype(f32) + other.astype(f32)).astype(bf16)

    def double(value, bit, mate):
        other = send(value, mate)
        first = bit == 0
        return jnp.stack([jnp.where(first, value, other), jnp.where(first, other, value)])

    def sum_all(value):
        for axis in AXES:
            step = 1
            while step < sizes[axis]:

                def mate(gx, gc, z, w, axis=axis, step=step):
                    at = dict(gx=gx, gc=gc, ctx=z, wt=w)
                    at[axis] ^= step
                    return (at["gx"], at["gc"], at["ctx"], at["wt"])

                value = value + send(value, mate)
                step *= 2
        return value

    def local(
        tokens, segments, w_qkv, w_proj, w_in, w_out, gain_attn, gain_mlp, query_scale, cotangent
    ):
        gx, gc, z, wt = (lax.axis_index(axis) for axis in AXES)
        host = z // 2
        near = z % 2
        mine = 2 * near + gc
        parts = sizes["ctx"]
        nh = H // parts
        rows = tokens.shape[1]
        group_len = segments.shape[1]
        wrows = w_qkv.shape[0]
        cols = nh * HD
        lane = gc == host

        def quarter(full):
            pieces = [
                jnp.concatenate([full[:, t * D + i * cols : t * D + (i + 1) * cols] for t in range(3)], axis=1)
                for i in range(parts)
            ]
            out = pieces[0]
            for i in range(1, parts):
                out = jnp.where(mine == i, pieces[i], out)
            return out

        qkv_w = gather_wt(quarter(w_qkv)).reshape(-1, 3 * cols)
        half_rows = wrows // 2
        half_w = jnp.concatenate(
            [rows_at(w, gc * half_rows, half_rows) for w in (w_proj, w_in, w_out)], axis=1
        )
        tail_w = double(gather_wt(half_w), gc, core_mate)
        tail_w = jnp.transpose(tail_w, (1, 0, 2, 3)).reshape(-1, 3 * D)
        full_proj, full_in, full_out = tail_w[:, :D], tail_w[:, D : 2 * D], tail_w[:, 2 * D :]
        proj_perm = jnp.concatenate([rows_at(full_proj, (mine ^ j) * cols, cols) for j in range(parts)])

        own = tokens[0]
        seg_row = jnp.where(lane, segments, send(segments, core_mate))[0]
        got1 = send(own, hop1)
        got2 = send(got1, hop2)
        end = jnp.where(gc == 0, z == 0, z == 3)
        got3 = send(jnp.where(end, own, got2), hop3)
        way = 1 - 2 * host
        last = jnp.where(host == 0, jnp.where(z == 0, 3, 0), jnp.where(z == 3, 0, 3))
        places = (z, z + way, z + 2 * way, last)
        padded_w = jnp.pad(qkv_w.reshape(D, 3 * nh, HD), ((0, 0), (0, 0), (0, LN - HD))).reshape(D, -1)
        dim_scale = scale_base / math.sqrt(HD) * jax.nn.softplus(query_scale)
        lane_scale = jnp.tile(jnp.pad(dim_scale * log2e, (0, LN - HD)), nh)[None]
        ones = jnp.tile(
            ((jnp.arange(LN) >= HD) & (jnp.arange(LN) < HD + 3)).astype(f32), 2 * nh
        )[None]
        all_tokens = jnp.zeros((group_len, D), bf16)
        all_normed = jnp.zeros((group_len, D), bf16)
        queries = jnp.zeros((group_len, nh * LN), bf16)
        keyval = jnp.zeros((group_len, 2 * nh * LN), bf16)
        for shard, at in zip((own, got1, got2, got3), places):
            shard = jnp.where(lane, shard, send(shard, lane_share))
            inputs = shard.astype(f32)
            normed = (inputs * rms_inverse(inputs) * gain_attn).astype(bf16)
            project = dot(normed, padded_w)
            at = at * rows
            all_tokens = put_rows(all_tokens, shard, at)
            all_normed = put_rows(all_normed, normed, at)
            queries = put_rows(queries, (project[:, : nh * LN] * lane_scale).astype(bf16), at)
            keyval = put_rows(keyval, (project[:, nh * LN :] + ones).astype(bf16), at)

        att, att_float, q_aug = attn_fwd(queries, keyval, seg_row, nh)

        trades = (core_mate, near_mate, cross_mate)
        inputs = rows_at(all_tokens, mine * rows, rows).astype(f32)
        grad_mlp = send(cotangent[0], to_host)
        attended = jnp.concatenate(
            [rows_at(att, mine * rows, rows)]
            + [send(rows_at(att, (mine ^ (j + 1)) * rows, rows), trades[j]) for j in range(3)],
            axis=1,
        )
        resid = inputs + dot(attended, proj_perm)
        inverse_mlp = rms_inverse(resid)
        normed_mlp = (resid * inverse_mlp * gain_mlp).astype(bf16)
        hidden = dot(normed_mlp, full_in)
        active = jax.nn.silu(hidden).astype(bf16)
        layer_out = send((resid + dot(active, full_out)).astype(bf16), to_home)

        grad_out = grad_mlp.astype(f32)
        grad_active = times_trans(grad_mlp, full_out)
        sigmoid_h = jax.nn.sigmoid(hidden)
        grad_hidden = (grad_active * sigmoid_h * (1.0 + hidden * (1.0 - sigmoid_h))).astype(bf16)
        grad_normed_mlp = times_trans(grad_hidden, full_in)
        grad_gain_mlp = jnp.sum(grad_normed_mlp * resid * inverse_mlp, axis=0)
        grad_resid = grad_out + norm_back(resid, inverse_mlp, grad_normed_mlp * gain_mlp)
        grad_proj = grad_resid.astype(bf16)
        grad_attended = times_trans(grad_proj, proj_perm).astype(bf16)
        grad_heads = jnp.zeros((group_len, cols), bf16)
        for j in range(parts):
            piece = grad_attended[:, j * cols : (j + 1) * cols]
            if j:
                piece = send(piece, trades[j - 1])
            grad_heads = put_rows(grad_heads, piece, (mine ^ j) * rows)

        grad_perm = trans_times(attended, grad_proj).astype(bf16)
        grad_w_proj = jnp.zeros((D, D), bf16)
        for j in range(parts):
            grad_w_proj = put_rows(grad_w_proj, grad_perm[j * cols : (j + 1) * cols], (mine ^ j) * cols)
        grad_tail = jnp.concatenate(
            [
                grad_w_proj,
                trans_times(normed_mlp, grad_hidden).astype(bf16),
                trans_times(active, grad_mlp).astype(bf16),
            ],
            axis=1,
        )
        grad_tail = jnp.transpose(grad_tail.reshape(-1, 2, half_rows, 3 * D), (1, 0, 2, 3))
        grad_tail = halve(grad_tail.reshape(-1, half_rows, 3 * D), gc, core_mate)
        grad_tail = lax.psum(scatter_wt(grad_tail), ("gx", "ctx"))
        total_tail = double(grad_tail, gc, core_mate).reshape(wrows, 3 * D).astype(f32)

        grad_project, grad_lanes = attn_bwd(
            q_aug, keyval, grad_heads, att_float, seg_row, jnp.tile(dim_scale, nh)[None], nh
        )
        grad_query_scale = (
            grad_lanes[0, :HD]
            / (dim_scale * log2e)
            * (scale_base / math.sqrt(HD))
            * jax.nn.sigmoid(query_scale)
        )
        grad_normed = times_trans(grad_project, qkv_w).reshape(2, 2, rows, D)
        to_core = lax.dynamic_index_in_dim(grad_normed, 1 - gc, 1, keepdims=False).astype(bf16)
        keep = lax.dynamic_index_in_dim(grad_normed, gc, 1, keepdims=False) + send(
            to_core, core_mate
        ).astype(f32)
        to_near = lax.dynamic_index_in_dim(keep, 1 - near, 0, keepdims=False).astype(bf16)
        grad_normed = lax.dynamic_index_in_dim(keep, near, 0, keepdims=False) + send(
            to_near, near_mate
        ).astype(f32)
        inverse_attn = rms_inverse(inputs)
        grad_gain_attn = jnp.sum(grad_normed * inputs * inverse_attn, axis=0)
        grad_tokens = send(
            (grad_resid + norm_back(inputs, inverse_attn, grad_normed * gain_attn)).astype(bf16), to_home
        )

        grad_qkv = trans_times(all_normed, grad_project).astype(bf16).reshape(-1, wrows, 3 * cols)
        grad_qkv = scatter_wt(grad_qkv)
        grad_qkv = halve(grad_qkv, gx, x_mate)
        grad_qkv = halve(grad_qkv, host, far_mate)
        grad_qkv = double(grad_qkv, host, far_mate).reshape(-1, 3 * cols)
        grad_qkv = double(grad_qkv, gx, x_mate).reshape(wrows, 3 * cols)
        grad_qkv = double(double(grad_qkv, near, near_mate), gc, core_mate)
        total_qkv = jnp.concatenate(
            [
                grad_qkv[i % 2, i // 2, :, t * cols : (t + 1) * cols]
                for t in range(3)
                for i in range(parts)
            ],
            axis=1,
        ).astype(f32)

        small = jnp.concatenate(
            [grad_gain_attn, grad_gain_mlp, jnp.pad(grad_query_scale, (0, LN - HD))]
        ).reshape(-1, LN)
        small = sum_all(small).reshape(-1)
        return (
            layer_out[None],
            grad_tokens[None],
            total_qkv,
            total_tail[:, :D],
            total_tail[:, D : 2 * D],
            total_tail[:, 2 * D :],
            small[:D],
            small[D : 2 * D],
            small[2 * D : 2 * D + HD],
        )

    return local


def solution(mesh):
    groups, parts, wt = (mesh.shape[axis] for axis in ("grp", "ctx", "wt"))
    inner = Mesh(mesh.devices.reshape(groups // 2, 2, parts, wt), AXES)
    sizes = dict(inner.shape)
    split = P(("gx", "gc", "wt"), "ctx", None)
    weight = P("wt", None)
    return jax.shard_map(
        make_local(sizes),
        mesh=inner,
        in_specs=(
            split,
            P(("gx", "gc", "wt"), None),
            weight,
            weight,
            weight,
            weight,
            P(),
            P(),
            P(),
            split,
        ),
        out_specs=(split, split, weight, weight, weight, weight, P(), P(), P()),
        check_vma=False,
    )
```

```python
import functools
import math

import jax
import jax.numpy as jnp
from jax import lax
from jax.experimental import pallas as pl
from jax.experimental.pallas import tpu as pltpu
from jax.sharding import Mesh
from jax.sharding import PartitionSpec as P

D = 1280
H = 16
HD = 80
LN = 128
epsilon = 1e-06
scale_base = 1.442695041
log2e = 1.4426950408889634
NEG = -1e30
f32 = jnp.float32
bf16 = jnp.bfloat16
AXES = ("gx", "gc", "ctx", "wt")


def block_flags(seg_row, bq, bk):
    n = seg_row.shape[0]
    q = seg_row.reshape(n // bq, bq)
    k = seg_row.reshape(n // bk, bk)
    qf, ql = q[:, 0][:, None], q[:, -1][:, None]
    kf, kl = k[:, 0][None], k[:, -1][None]
    qs = jnp.arange(n // bq, dtype=jnp.int32)[:, None] * bq
    ks = jnp.arange(n // bk, dtype=jnp.int32)[None] * bk
    below = ks + bk - 1 <= qs
    skip = (ks > qs + bq - 1) | ((kf > 0) & (kl < qf))
    same = (qf == ql) & (kl == ql) & ((kf == kl) | ((kf == 0) & (kl == 1)))
    full = below & ((kl == 0) | same)
    return jnp.where(skip, 0, jnp.where(full, 1, 2)).astype(jnp.int32).reshape(-1)


def put_split(base, col, lanes):
    hi = col.astype(bf16).astype(f32)
    rest = col - hi
    mid = rest.astype(bf16).astype(f32)
    out = jnp.where(lanes == HD, hi, base)
    out = jnp.where(lanes == HD + 1, mid, out)
    return jnp.where(lanes == HD + 2, rest - mid, out).astype(bf16)


def fwd_kernel(flags, q_ref, kv, segc, segr, att, of, qaug, m_s, acc_s, *, nh, bq, bk, nk):
    qi = pl.program_id(0)
    count = (qi * bq + bq + bk - 1) // bk
    nt = (((1,), (1,)), ((), ()))
    acc_s[...] = jnp.zeros_like(acc_s)
    m_s[...] = jnp.zeros_like(m_s)

    def mask(ko):
        qpos = qi * bq + lax.broadcasted_iota(jnp.int32, (bq, bk), 0)
        kpos = ko + lax.broadcasted_iota(jnp.int32, (bq, bk), 1)
        ks = segr[:, pl.ds(ko, bk)]
        return (kpos <= qpos) & ((ks == 0) | (ks == segc[...]))

    def step(kb, masked):
        ko = pl.multiple_of(kb * bk, bk)
        if masked:
            allowed = mask(ko)
        for h in range(nh):
            k = kv[pl.ds(ko, bk), h * LN : (h + 1) * LN]
            v = kv[pl.ds(ko, bk), (nh + h) * LN : (nh + h + 1) * LN]
            s = lax.dot_general(q_ref[:, h * LN : (h + 1) * LN], k, nt, preferred_element_type=f32)
            p = jnp.exp2(s)
            if masked:
                p = jnp.where(allowed, p, 0.0)
            acc_s[h] += jnp.dot(p.astype(bf16), v, preferred_element_type=f32)

    def body(kb, carry):
        flag = flags[qi * nk + kb]

        @pl.when(flag == 1)
        def _():
            step(kb, False)

        @pl.when(flag == 2)
        def _():
            step(kb, True)

        return carry

    lax.fori_loop(0, count, body, 0)
    bad = jnp.zeros((bq, 1), f32)
    for h in range(nh):
        total = acc_s[h][:, HD : HD + 1]
        bad = jnp.maximum(bad, jnp.where((total > 2.0**-60) & (total < 2.0**60), 0.0, 1.0))

    @pl.when(jnp.max(bad) > 0.0)
    def _():
        def head(h, carry):
            kc = pl.ds(pl.multiple_of(h * LN, LN), LN)
            vc = pl.ds(pl.multiple_of((nh + h) * LN, LN), LN)
            m_s[h] = jnp.full((bq, LN), NEG, f32)
            acc_s[h] = jnp.zeros((bq, LN), f32)

            def inner(kb, carry):
                @pl.when(flags[qi * nk + kb] > 0)
                def _():
                    ko = pl.multiple_of(kb * bk, bk)
                    s = lax.dot_general(
                        q_ref[:, kc], kv[pl.ds(ko, bk), kc], nt, preferred_element_type=f32
                    )
                    s = jnp.where(mask(ko), s, NEG)
                    old = m_s[h]
                    new = jnp.maximum(old, jnp.max(s, axis=1, keepdims=True))
                    p = jnp.exp2(s - new[:, :1]).astype(bf16)
                    m_s[h] = new
                    acc_s[h] = acc_s[h] * jnp.exp2(old - new) + jnp.dot(
                        p, kv[pl.ds(ko, bk), vc], preferred_element_type=f32
                    )

                return carry

            lax.fori_loop(0, count, inner, 0)
            return carry

        lax.fori_loop(0, nh, head, 0)

    lanes = lax.broadcasted_iota(jnp.int32, (bq, LN), 1)
    outs = []
    for h in range(nh):
        acc = acc_s[h]
        total = acc[:, HD : HD + 1]
        out = acc * (1.0 / total)
        of[:, h * LN : (h + 1) * LN] = jnp.where(lanes < HD, out, 0.0)
        outs.append(out[:, :HD])
        lse = m_s[h][:, :1] + jnp.log2(total)
        qaug[:, h * LN : (h + 1) * LN] = put_split(
            q_ref[:, h * LN : (h + 1) * LN].astype(f32), -lse, lanes
        )
    att[...] = jnp.concatenate(outs, axis=1).astype(bf16)


def attn_fwd(q, kv, seg_row, nh, bq=512, bk=512):
    n = q.shape[0]
    w = nh * LN
    spec = pltpu.PrefetchScalarGridSpec(
        num_scalar_prefetch=1,
        grid=(n // bq,),
        in_specs=[
            pl.BlockSpec((bq, w), lambda i, f: (i, 0)),
            pl.BlockSpec((n, 2 * w), lambda i, f: (0, 0)),
            pl.BlockSpec((bq, 1), lambda i, f: (i, 0)),
            pl.BlockSpec((1, n), lambda i, f: (0, 0)),
        ],
        out_specs=[
            pl.BlockSpec((bq, nh * HD), lambda i, f: (i, 0)),
            pl.BlockSpec((bq, w), lambda i, f: (i, 0)),
            pl.BlockSpec((bq, w), lambda i, f: (i, 0)),
        ],
        scratch_shapes=[pltpu.VMEM((nh, bq, LN), f32), pltpu.VMEM((nh, bq, LN), f32)],
    )
    return pl.pallas_call(
        functools.partial(fwd_kernel, nh=nh, bq=bq, bk=bk, nk=n // bk),
        out_shape=[
            jax.ShapeDtypeStruct((n, nh * HD), bf16),
            jax.ShapeDtypeStruct((n, w), f32),
            jax.ShapeDtypeStruct((n, w), bf16),
        ],
        grid_spec=spec,
        compiler_params=pltpu.CompilerParams(vmem_limit_bytes=40 << 20),
        cost_estimate=pl.CostEstimate(
            flops=20_000_000_000, transcendentals=10_000_000, bytes_accessed=16_000_000
        ),
        name="attn_fwd",
    )(block_flags(seg_row, bq, bk), q, kv, seg_row[:, None], seg_row[None])


def bwd_kernel(
    flags, mine, qa, kk, vv, do0, do1, do2, do3, of, segc, segr, scale, dqkv, gscale, doa_s, dq_s, dk_s, dv_s, *, first, nh, bq, bk, n
):
    nk = n // bk
    nq = n // bq
    kb = pl.program_id(0)
    part = n // 4
    step_rows = 256 if part % 256 == 0 else part
    lanes = lax.broadcasted_iota(jnp.int32, (step_rows, LN), 1)

    @pl.when(kb == 0)
    def _():
        dq_s[...] = jnp.zeros_like(dq_s)
        for j, piece in enumerate((do0, do1, do2, do3)):
            start = (mine[0] ^ j) * part
            for i in range(part // step_rows):
                d = piece[i * step_rows : (i + 1) * step_rows, :].astype(f32)
                r = pl.ds(pl.multiple_of(start + i * step_rows, step_rows), step_rows)
                for h in range(nh):
                    at = (first + h) * HD
                    dh = jnp.concatenate(
                        [d[:, at : at + HD], jnp.zeros((step_rows, LN - HD), f32)], axis=1
                    )
                    c = slice(h * LN, (h + 1) * LN)
                    delta = jnp.sum(dh * of[r, c], axis=1, keepdims=True)
                    doa_s[r, c] = put_split(dh, -delta, lanes)

    dk_s[...] = jnp.zeros_like(dk_s)
    dv_s[...] = jnp.zeros_like(dv_s)
    ko = kb * bk
    nt = (((1,), (1,)), ((), ()))
    tn = (((0,), (0,)), ((), ()))

    def step(qi, masked):
        qo = pl.multiple_of(qi * bq, bq)
        if masked:
            kpos = ko + lax.broadcasted_iota(jnp.int32, (bk, bq), 0)
            qpos = qo + lax.broadcasted_iota(jnp.int32, (bk, bq), 1)
            ks = segc[...]
            allowed = (kpos <= qpos) & ((ks == 0) | (ks == segr[:, pl.ds(qo, bq)]))
        for h in range(nh):
            c = slice(h * LN, (h + 1) * LN)
            q = qa[pl.ds(qo, bq), c]
            k = kk[:, c]
            d = doa_s[pl.ds(qo, bq), c]
            p = jnp.exp2(lax.dot_general(k, q, nt, preferred_element_type=f32))
            if masked:
                p = jnp.where(allowed, p, 0.0)
            ds = (p * lax.dot_general(vv[:, c], d, nt, preferred_element_type=f32)).astype(bf16)
            dv_s[h] += jnp.dot(p.astype(bf16), d, preferred_element_type=f32)
            dk_s[h] += jnp.dot(ds, q, preferred_element_type=f32)
            dq_s[h, pl.ds(qo, bq), :] += lax.dot_general(ds, k, tn, preferred_element_type=f32)

    def body(qi, carry):
        flag = flags[qi * nk + kb]

        @pl.when(flag == 1)
        def _():
            step(qi, False)

        @pl.when(flag == 2)
        def _():
            step(qi, True)

        return carry

    lax.fori_loop(ko // bq, nq, body, 0)
    r = pl.multiple_of(ko, bk)
    ln2 = math.log(2.0)
    dqkv[pl.ds(r, bk), nh * HD : 3 * nh * HD] = jnp.concatenate(
        [dk_s[h][:, :HD] * ln2 for h in range(nh)] + [dv_s[h][:, :HD] for h in range(nh)], axis=1
    ).astype(bf16)

    @pl.when(kb == nk - 1)
    def _():
        total = jnp.zeros((1, LN), f32)
        for i in range(nq):
            rows = slice(i * bq, (i + 1) * bq)
            for h in range(nh):
                total = total + jnp.sum(
                    dq_s[h, rows, :] * qa[rows, h * LN : (h + 1) * LN].astype(f32), axis=0, keepdims=True
                )
            grads = jnp.concatenate([dq_s[h, rows, :][:, :HD] for h in range(nh)], axis=1)
            dqkv[rows, 0 : nh * HD] = (grads * scale[...]).astype(bf16)
        gscale[...] = jnp.broadcast_to(total, gscale.shape)


def attn_bwd(qa, kv, pieces, of, seg_row, mine, scale, heads, group, groups, bq=512, bk=512):
    n = qa.shape[0]
    nh = heads // groups
    w = nh * LN
    once = pl.Buffered(1)
    spec = pltpu.PrefetchScalarGridSpec(
        num_scalar_prefetch=2,
        grid=(n // bk,),
        in_specs=[
            pl.BlockSpec((n, w), lambda i, f, m: (0, group), pipeline_mode=once),
            pl.BlockSpec((bk, w), lambda i, f, m: (i, group)),
            pl.BlockSpec((bk, w), lambda i, f, m: (i, groups + group)),
        ]
        + [pl.BlockSpec((n // 4, heads * HD), lambda i, f, m: (0, 0), pipeline_mode=once)] * 4
        + [
            pl.BlockSpec((n, w), lambda i, f, m: (0, group), pipeline_mode=once),
            pl.BlockSpec((bk, 1), lambda i, f, m: (i, 0)),
            pl.BlockSpec((1, n), lambda i, f, m: (0, 0)),
            pl.BlockSpec((1, nh * HD), lambda i, f, m: (0, 0)),
        ],
        out_specs=[
            pl.BlockSpec((n, 3 * nh * HD), lambda i, f, m: (0, 0)),
            pl.BlockSpec((8, LN), lambda i, f, m: (0, 0)),
        ],
        scratch_shapes=[
            pltpu.VMEM((n, w), bf16),
            pltpu.VMEM((nh, n, LN), f32),
            pltpu.VMEM((nh, bk, LN), f32),
            pltpu.VMEM((nh, bk, LN), f32),
        ],
    )
    return pl.pallas_call(
        functools.partial(bwd_kernel, first=group * nh, nh=nh, bq=bq, bk=bk, n=n),
        out_shape=[
            jax.ShapeDtypeStruct((n, 3 * nh * HD), bf16),
            jax.ShapeDtypeStruct((8, LN), f32),
        ],
        grid_spec=spec,
        compiler_params=pltpu.CompilerParams(vmem_limit_bytes=48 << 20),
        cost_estimate=pl.CostEstimate(
            flops=15_000_000_000 * nh // 2, transcendentals=10_000_000, bytes_accessed=20_000_000
        ),
        name="attn_bwd",
    )(block_flags(seg_row, bq, bk), mine.reshape(1), qa, kv, kv, *pieces, of, seg_row[:, None], seg_row[None], scale)


def quarter_columns(place, parts, groups, nh):
    width = nh // groups * HD
    return [
        (t * D + place * nh * HD + g * width, width) for g in range(groups) for t in range(3)
    ]


def pick_kernel(mine, w_ref, out, *, parts, groups, nh):
    for i in range(parts):

        @pl.when(mine[0] == i)
        def _(i=i):
            out[...] = jnp.concatenate(
                [w_ref[:, a : a + width] for a, width in quarter_columns(i, parts, groups, nh)], axis=1
            )


def pick(w, mine, parts, groups, nh):
    rows = w.shape[0]
    step = 160 if rows % 160 == 0 else rows
    return pl.pallas_call(
        functools.partial(pick_kernel, parts=parts, groups=groups, nh=nh),
        out_shape=jax.ShapeDtypeStruct((rows, 3 * nh * HD), w.dtype),
        grid_spec=pltpu.PrefetchScalarGridSpec(
            num_scalar_prefetch=1,
            grid=(rows // step,),
            in_specs=[pl.BlockSpec((step, 3 * D), lambda i, m: (i, 0))],
            out_specs=pl.BlockSpec((step, 3 * nh * HD), lambda i, m: (i, 0)),
        ),
        name="pick",
    )(mine.reshape(1), w)


def widen_kernel(own_first, a_ref, b_ref, *outs, groups, nh):
    flats, wide = outs[:-1], outs[-1]

    def put(ref):
        value = ref[...]
        each = 3 * nh * HD // groups
        for g in range(groups):
            flats[g][...] = value[:, g * each : (g + 1) * each]
        zero = jnp.zeros((value.shape[0], LN - HD), value.dtype)
        per = nh // groups
        spread = []
        for t in range(3):
            for h in range(nh):
                at = (h // per) * each + t * per * HD + (h % per) * HD
                spread += [value[:, at : at + HD], zero]
        wide[...] = jnp.concatenate(spread, axis=1)

    half = pl.program_id(0)

    @pl.when(half == 0)
    def _():
        put(a_ref)

    @pl.when(half == 1)
    def _():
        put(b_ref)


def widen(own, other, own_at, groups, nh):
    rows, width = own.shape
    step = 160
    n = rows // step
    at = lambda i, j, m: ((i ^ m[0]) * n + j, 0)
    each = width // groups
    return pl.pallas_call(
        functools.partial(widen_kernel, groups=groups, nh=nh),
        out_shape=[jax.ShapeDtypeStruct((2 * rows, each), own.dtype)] * groups
        + [jax.ShapeDtypeStruct((2 * rows, 3 * nh * LN), own.dtype)],
        grid_spec=pltpu.PrefetchScalarGridSpec(
            num_scalar_prefetch=1,
            grid=(2, n),
            in_specs=[
                pl.BlockSpec((step, width), lambda i, j, m: (j * (1 - i), 0)),
                pl.BlockSpec((step, width), lambda i, j, m: (j * i, 0)),
            ],
            out_specs=[pl.BlockSpec((step, each), at)] * groups + [pl.BlockSpec((step, 3 * nh * LN), at)],
        ),
        name="widen",
    )(own_at.reshape(1), own, other)


def project_kernel(info, *refs, count, width, fresh):
    pairs = refs[: 2 * count]
    gain, w, scale, ones = refs[2 * count : 2 * count + 4]
    normed_ref, q_ref, kv_ref, mine_ref = refs[-4:]
    j = pl.program_id(0)

    def work(x_ref):
        value = x_ref[...]
        x = value.astype(f32)
        inverse = lax.rsqrt(jnp.mean(x * x, axis=-1, keepdims=True) + epsilon)
        normed = (x * inverse * gain[...]).astype(bf16)
        normed_ref[...] = normed
        q_ref[...] = (
            jnp.dot(normed, w[:, :width], preferred_element_type=f32) * scale[...]
        ).astype(bf16)
        kv_ref[...] = (
            jnp.dot(normed, w[:, width:], preferred_element_type=f32) + ones[...]
        ).astype(bf16)

        @pl.when(info[count + 1] == info[j])
        def _():
            mine_ref[...] = value

    if not fresh:
        mine_ref[...] = refs[2 * count + 4][...]
    for i in range(count):
        for lane in range(2):

            @pl.when((j == i) & (info[count] == lane))
            def _(i=i, lane=lane):
                work(pairs[2 * i + 1 - lane])


def project(pairs, places, lane, mine, gain, w, scale, ones, group_len, carried=None):
    count = len(pairs)
    rows, d = pairs[0][0].shape
    width = scale.shape[1]
    full = lambda i, f: (0, 0)
    at = lambda i, f: (f[i], 0)
    once = pl.Buffered(1)
    info = jnp.stack(list(places) + [lane.astype(jnp.int32), mine])
    args = [x for pair in pairs for x in pair] + [gain, w, scale, ones]
    in_specs = [pl.BlockSpec((rows, d), full, pipeline_mode=once)] * (2 * count) + [
        pl.BlockSpec((1, d), full, pipeline_mode=once),
        pl.BlockSpec(w.shape, full, pipeline_mode=once),
        pl.BlockSpec((1, width), full, pipeline_mode=once),
        pl.BlockSpec((1, 2 * width), full, pipeline_mode=once),
    ]
    aliases = {}
    if carried is not None:
        args += [carried[3], *carried[:3]]
        in_specs += [pl.BlockSpec((rows, d), full, pipeline_mode=once)] + [pl.BlockSpec(memory_space=pl.ANY)] * 3
        base = 2 * count + 6
        aliases = {base: 0, base + 1: 1, base + 2: 2}
    return pl.pallas_call(
        functools.partial(project_kernel, count=count, width=width, fresh=carried is None),
        out_shape=[
            jax.ShapeDtypeStruct((group_len, d), bf16),
            jax.ShapeDtypeStruct((group_len, width), bf16),
            jax.ShapeDtypeStruct((group_len, 2 * width), bf16),
            jax.ShapeDtypeStruct((rows, d), bf16),
        ],
        grid_spec=pltpu.PrefetchScalarGridSpec(
            num_scalar_prefetch=1,
            grid=(count,),
            in_specs=in_specs,
            out_specs=[
                pl.BlockSpec((rows, d), at),
                pl.BlockSpec((rows, width), at),
                pl.BlockSpec((rows, 2 * width), at),
                pl.BlockSpec((rows, d), full),
            ],
        ),
        input_output_aliases=aliases,
        compiler_params=pltpu.CompilerParams(vmem_limit_bytes=48 << 20),
        name="project",
    )(info, *args)


def tail_body(at, p0, p1, p2, p3, x_ref, g_ref, w_s, gain, outs):
    lo_ref, att_ref, nm_ref, gh_ref, act_ref, gp_ref, gr_ref, c0, c1, c2, c3, gg_ref = outs
    mine = at[0]
    pieces = (p0, p1, p2, p3)
    cols = p0.shape[1]
    nt = (((1,), (1,)), ((), ()))
    for i in range(4):

        @pl.when(mine == i)
        def _(i=i):
            att_ref[...] = jnp.concatenate([pieces[i ^ k][...] for k in range(4)], axis=1)

    resid = x_ref[...].astype(f32) + jnp.dot(att_ref[...], w_s[0], preferred_element_type=f32)
    inverse = lax.rsqrt(jnp.mean(resid * resid, axis=-1, keepdims=True) + epsilon)
    normed = (resid * inverse * gain[...]).astype(bf16)
    nm_ref[...] = normed
    hidden = jnp.dot(normed, w_s[1], preferred_element_type=f32)
    sig = 1.0 / (1.0 + jnp.exp(-hidden))
    active = (hidden * sig).astype(bf16)
    act_ref[...] = active
    lo_ref[...] = (resid + jnp.dot(active, w_s[2], preferred_element_type=f32)).astype(bf16)
    grad_active = lax.dot_general(g_ref[...], w_s[2], nt, preferred_element_type=f32)
    grad_hidden = (grad_active * sig * (1.0 + hidden * (1.0 - sig))).astype(bf16)
    gh_ref[...] = grad_hidden
    grad_normed = lax.dot_general(grad_hidden, w_s[1], nt, preferred_element_type=f32)
    gg_ref[...] += jnp.sum(grad_normed * resid * inverse, axis=0, keepdims=True)
    scaled = grad_normed * gain[...]
    grad_resid = (
        g_ref[...].astype(f32)
        + inverse * scaled
        - resid * (inverse * inverse * inverse) * jnp.mean(scaled * resid, axis=-1, keepdims=True)
    )
    gr_ref[...] = grad_resid
    grad_proj = grad_resid.astype(bf16)
    gp_ref[...] = grad_proj
    grad_att = lax.dot_general(grad_proj, w_s[0], nt, preferred_element_type=f32).astype(bf16)
    for i in range(4):

        @pl.when(mine == i)
        def _(i=i):
            for j, out in enumerate((c0, c1, c2, c3)):
                out[...] = grad_att[:, (i ^ j) * cols : ((i ^ j) + 1) * cols]


def tail_kernel(at, p0, p1, p2, p3, x_ref, g_ref, own, half, other, gain, *refs, rows, hrows):
    w_s = refs[-1]
    outs = refs[:-1]

    @pl.when(pl.program_id(0) == 0)
    def _():
        outs[-1][...] = jnp.zeros_like(outs[-1])
        w_s[:, pl.ds(pl.multiple_of(at[1], 16), rows), :] = own[...]
        w_s[:, pl.ds(pl.multiple_of(at[2], 16), hrows), :] = half[...]
        w_s[:, pl.ds(pl.multiple_of(at[3], 16), hrows), :] = other[...]

    tail_body(at, p0, p1, p2, p3, x_ref, g_ref, w_s, gain, outs)


def whole_tail_kernel(at, p0, p1, p2, p3, x_ref, g_ref, w, gain, *outs):
    @pl.when(pl.program_id(0) == 0)
    def _():
        outs[-1][...] = jnp.zeros_like(outs[-1])

    tail_body(at, p0, p1, p2, p3, x_ref, g_ref, w, gain, outs)


def tail(at, pieces, x, g, weights, gain, tile=256):
    rows, d = x.shape
    cols = pieces[0].shape[1]
    row = lambda i, m: (i, 0)
    once = pl.Buffered(1)
    whole = lambda *shape: pl.BlockSpec(shape, lambda i, m: (0,) * len(shape), pipeline_mode=once)
    wide = pl.BlockSpec((tile, d), row)
    slim = pl.BlockSpec((tile, cols), row)
    if len(weights) == 3:
        body = functools.partial(tail_kernel, rows=weights[0].shape[1], hrows=weights[1].shape[1])
        scratch = [pltpu.VMEM((3, d, d), bf16)]
    else:
        body = whole_tail_kernel
        scratch = []
    return pl.pallas_call(
        body,
        out_shape=[jax.ShapeDtypeStruct((rows, d), bf16)] * 6
        + [jax.ShapeDtypeStruct((rows, d), f32)]
        + [jax.ShapeDtypeStruct((rows, cols), bf16)] * 4
        + [jax.ShapeDtypeStruct((1, d), f32)],
        grid_spec=pltpu.PrefetchScalarGridSpec(
            num_scalar_prefetch=1,
            grid=(rows // tile,),
            in_specs=[slim] * 4 + [wide] * 2 + [whole(*w.shape) for w in weights] + [whole(1, d)],
            out_specs=[wide] * 7 + [slim] * 4 + [pl.BlockSpec((1, d), lambda i, m: (0, 0))],
            scratch_shapes=scratch,
        ),
        compiler_params=pltpu.CompilerParams(vmem_limit_bytes=52 << 20),
        cost_estimate=pl.CostEstimate(
            flops=10_000_000_000, transcendentals=700_000, bytes_accessed=25_000_000
        ),
        name="tail",
    )(at, *pieces, x, g, *weights, gain)


tn_dims = (((0,), (0,)), ((), ()))


def share_kernel(col, l0, l1, l2, r0, r1, r2, out):
    for i, (left, right) in enumerate(((l0, r0), (l1, r1), (l2, r2))):

        @pl.when(pl.program_id(0) == i)
        def _(left=left, right=right):
            out[...] = lax.dot_general(
                left[...], right[...], tn_dims, preferred_element_type=f32
            ).astype(bf16)


def share(lefts, rights, col):
    rows, d = lefts[0].shape
    w = d // 2
    once = pl.Buffered(1)
    return pl.pallas_call(
        share_kernel,
        out_shape=jax.ShapeDtypeStruct((d, 3 * w), bf16),
        grid_spec=pltpu.PrefetchScalarGridSpec(
            num_scalar_prefetch=1,
            grid=(3,),
            in_specs=[pl.BlockSpec((rows, d), lambda i, c: (0, 0), pipeline_mode=once)] * 3
            + [pl.BlockSpec((rows, w), lambda i, c: (0, c[0]), pipeline_mode=once)] * 3,
            out_specs=pl.BlockSpec((d, w), lambda i, c: (0, i)),
        ),
        compiler_params=pltpu.CompilerParams(vmem_limit_bytes=40 << 20),
        cost_estimate=pl.CostEstimate(
            flops=2_500_000_000, transcendentals=0, bytes_accessed=12_000_000
        ),
        name="share",
    )(col.reshape(1), *lefts, *rights)


def keep_kernel(at, l0, l1, l2, r0, r1, r2, got, a_send, a_keep, b_send, b_keep, s):
    h = a_send.shape[1]
    for i, (left, right) in enumerate(((l0, r0), (l1, r1), (l2, r2))):

        @pl.when(pl.program_id(0) == i)
        def _(left=left, right=right):
            s[...] = lax.dot_general(
                left[...], right[...], tn_dims, preferred_element_type=f32
            ) + got[...].astype(f32)

    gx, wt = at[1], at[2]
    for w in range(2):
        base = w * 4 * h
        a_send[w] = s[pl.ds(pl.multiple_of(base + (1 - gx) * h, 16), h), :].astype(bf16)
        a_keep[w] = s[pl.ds(pl.multiple_of(base + gx * h, 16), h), :].astype(bf16)
    b_send[...] = s[pl.ds(pl.multiple_of((1 - wt) * 4 * h + 2 * h, 16), 2 * h), :].astype(bf16)
    b_keep[...] = s[pl.ds(pl.multiple_of(wt * 4 * h + 2 * h, 16), 2 * h), :].astype(bf16)


def keep(lefts, rights, got, at):
    rows, d = lefts[0].shape
    w = d // 2
    h = d // 8
    once = pl.Buffered(1)
    return pl.pallas_call(
        keep_kernel,
        out_shape=[jax.ShapeDtypeStruct((2, h, 3 * w), bf16)] * 2
        + [jax.ShapeDtypeStruct((2 * h, 3 * w), bf16)] * 2,
        grid_spec=pltpu.PrefetchScalarGridSpec(
            num_scalar_prefetch=1,
            grid=(3,),
            in_specs=[pl.BlockSpec((rows, d), lambda i, c: (0, 0), pipeline_mode=once)] * 3
            + [pl.BlockSpec((rows, w), lambda i, c: (0, c[0]), pipeline_mode=once)] * 3
            + [pl.BlockSpec((d, w), lambda i, c: (0, i))],
            out_specs=[pl.BlockSpec((2, h, w), lambda i, c: (0, 0, i))] * 2
            + [pl.BlockSpec((2 * h, w), lambda i, c: (0, i))] * 2,
            scratch_shapes=[pltpu.VMEM((d, w), f32)],
        ),
        compiler_params=pltpu.CompilerParams(vmem_limit_bytes=40 << 20),
        cost_estimate=pl.CostEstimate(
            flops=2_500_000_000, transcendentals=0, bytes_accessed=16_000_000
        ),
        name="keep",
    )(at, *lefts, *rights, got)


def fold_kernel(bits, *refs, count):
    ins, outs = refs[: 4 * count], refs[4 * count :]
    for i in range(count):
        ks, gs, kk, gk = ins[4 * i : 4 * i + 4]
        outs[2 * i][...] = (ks[0].astype(f32) + gs[0].astype(f32)).astype(bf16)
        outs[2 * i + 1][...] = (kk[0].astype(f32) + gk[0].astype(f32)).astype(bf16)


def fold(items):
    in_specs, out_specs, out_shape, args = [], [], [], []
    for i, (kept, got, bit) in enumerate(items):
        shape = (1,) + kept.shape[1:]
        other = pl.BlockSpec(shape, lambda _, m, i=i: (1 - m[i], 0, 0))
        mine = pl.BlockSpec(shape, lambda _, m, i=i: (m[i], 0, 0))
        in_specs += [other, other, mine, mine]
        args += [kept, got, kept, got]
        out_specs += [pl.BlockSpec(kept.shape[1:], lambda _, m: (0, 0))] * 2
        out_shape += [jax.ShapeDtypeStruct(kept.shape[1:], bf16)] * 2
    bits = jnp.stack([bit for _, _, bit in items])
    out = pl.pallas_call(
        functools.partial(fold_kernel, count=len(items)),
        out_shape=out_shape,
        grid_spec=pltpu.PrefetchScalarGridSpec(
            num_scalar_prefetch=1, grid=(1,), in_specs=in_specs, out_specs=out_specs
        ),
        compiler_params=pltpu.CompilerParams(vmem_limit_bytes=24 << 20),
        name="fold",
    )(bits, *args)
    return [(out[2 * i], out[2 * i + 1]) for i in range(len(items))]


def place_kernel(at, c_ref, e_ref, fc_ref, fe_ref, o0, o1, o2):
    w = o0.shape[1] // 2
    mine = (pl.program_id(0) % 2) == at[0]
    for own_rows in range(2):
        for core in range(2):

            @pl.when((mine == (own_rows == 1)) & (at[1] == core))
            def _(own_rows=own_rows, core=core):
                near = c_ref if own_rows else e_ref
                mate = fc_ref if own_rows else fe_ref
                first, second = (near, mate) if core == 0 else (mate, near)
                for i, out in enumerate((o0, o1, o2)):
                    out[:, :w] = first[0, :, i * w : (i + 1) * w].astype(f32)
                    out[:, w:] = second[0, :, i * w : (i + 1) * w].astype(f32)


def place_tail(c, e, fc, fe, at):
    _, h, width = c.shape
    d = width // 3 * 2
    block = pl.BlockSpec((1, h, width), lambda i, m: (i // 2, 0, 0))
    return pl.pallas_call(
        place_kernel,
        out_shape=[jax.ShapeDtypeStruct((4 * h, d), f32)] * 3,
        grid_spec=pltpu.PrefetchScalarGridSpec(
            num_scalar_prefetch=1,
            grid=(4,),
            in_specs=[block] * 4,
            out_specs=[pl.BlockSpec((h, d), lambda i, m: (i, 0))] * 3,
        ),
        compiler_params=pltpu.CompilerParams(vmem_limit_bytes=40 << 20),
        name="place_tail",
    )(at, c, e, fc, fe)


def cross_kernel(col, x_ref, g_ref, out):
    out[...] = lax.dot_general(
        x_ref[...], g_ref[...], tn_dims, preferred_element_type=f32
    ).astype(bf16)


def cross(x, g, col):
    rows, d = x.shape
    w = d // 2
    return pl.pallas_call(
        cross_kernel,
        out_shape=jax.ShapeDtypeStruct((w, g.shape[1]), bf16),
        grid_spec=pltpu.PrefetchScalarGridSpec(
            num_scalar_prefetch=1,
            grid=(1,),
            in_specs=[
                pl.BlockSpec((rows, w), lambda i, c: (0, c[0])),
                pl.BlockSpec(g.shape, lambda i, c: (0, 0)),
            ],
            out_specs=pl.BlockSpec((w, g.shape[1]), lambda i, c: (0, 0)),
        ),
        compiler_params=pltpu.CompilerParams(vmem_limit_bytes=40 << 20),
        cost_estimate=pl.CostEstimate(
            flops=2 * rows * w * g.shape[1], transcendentals=0, bytes_accessed=6_000_000
        ),
        name="cross",
    )(col.reshape(1), x, g)


def spread_kernel(at, *refs, groups, width):
    out = refs[-1]
    gx, host, near, gc = at[0], at[1], at[2], at[3]
    block = pl.program_id(0)
    slot = ((block // 2) ^ gx) * 4 + ((block % 2) ^ host)

    def put(flip):
        cut = []
        for t in range(3):
            for n in range(2):
                for core in range(2):
                    for g in range(groups):
                        ref = refs[2 * g + (core ^ flip)]
                        part = ref[slot + 2 * (n ^ near)]
                        cut.append(part[:, t * width : (t + 1) * width])
        out[0] = jnp.concatenate(cut, axis=1).astype(f32)

    for flip in range(2):

        @pl.when(gc == flip)
        def _(flip=flip):
            put(flip)


def spread(arrays, at):
    flat = [x for pair in arrays for x in pair]
    slots, rows, cols = flat[0].shape
    full = lambda i, m: (0, 0, 0)
    groups = len(arrays)
    total = 4 * groups * cols
    return pl.pallas_call(
        functools.partial(spread_kernel, groups=groups, width=cols // 3),
        out_shape=jax.ShapeDtypeStruct((4, rows, total), f32),
        grid_spec=pltpu.PrefetchScalarGridSpec(
            num_scalar_prefetch=1,
            grid=(4,),
            in_specs=[pl.BlockSpec(x.shape, full, pipeline_mode=pl.Buffered(1)) for x in flat],
            out_specs=pl.BlockSpec((1, rows, total), lambda i, m: (i, 0, 0)),
        ),
        compiler_params=pltpu.CompilerParams(vmem_limit_bytes=40 << 20),
        name="spread",
    )(at, *flat).reshape(4 * rows, total)


def rms_inverse(values):
    return lax.rsqrt(jnp.mean(values * values, axis=-1, keepdims=True) + epsilon)


def norm_back(values, inverse, grad_scaled):
    return inverse * grad_scaled - values * (inverse * inverse * inverse) * jnp.mean(
        grad_scaled * values, axis=-1, keepdims=True
    )


def dot(left, right):
    return jnp.dot(left, right, preferred_element_type=f32)


def times_trans(left, right):
    return lax.dot_general(left, right, (((1,), (1,)), ((), ())), preferred_element_type=f32)


def trans_times(left, right):
    return lax.dot_general(left, right, (((0,), (0,)), ((), ())), preferred_element_type=f32)


def rows_at(array, start, count):
    return lax.dynamic_slice_in_dim(array, start, count, 0)


def put_rows(array, rows, start):
    return lax.dynamic_update_slice_in_dim(array, rows, start, 0)


def make_local(sizes):
    def pairs(target):
        found = []
        for gx in range(sizes["gx"]):
            for gc in range(sizes["gc"]):
                for z in range(sizes["ctx"]):
                    for w in range(sizes["wt"]):
                        goal = target(gx, gc, z, w)
                        if goal is not None:
                            found.append((place(gx, gc, z, w), place(*goal)))
        return found

    def place(gx, gc, z, w):
        return ((gx * sizes["gc"] + gc) * sizes["ctx"] + z) * sizes["wt"] + w

    def send(value, target):
        return lax.ppermute(value, AXES, pairs(target))

    def core_mate(gx, gc, z, w):
        return (gx, 1 - gc, z, w)

    def x_mate(gx, gc, z, w):
        return (1 - gx, gc, z, w)

    def near_mate(gx, gc, z, w):
        return (gx, gc, z ^ 1, w)

    def far_mate(gx, gc, z, w):
        return (gx, gc, z ^ 2, w)

    def cross_mate(gx, gc, z, w):
        return (gx, 1 - gc, z ^ 1, w)

    def wt_mate(gx, gc, z, w):
        return (gx, gc, z, 1 - w)

    def to_host(gx, gc, z, w):
        return (gx, z & 1, 2 * gc + (z >> 1), w)

    def to_home(gx, gc, z, w):
        return (gx, z >> 1, 2 * (z & 1) + gc, w)

    def hop1(gx, gc, z, w):
        if gc == 0:
            return (gx, 0, z - 1, w) if z > 0 else None
        return (gx, 1, z + 1, w) if z < 3 else None

    def hop2(gx, gc, z, w):
        if gc == 0:
            return (gx, 0, z - 1, w) if z in (1, 2) else None
        return (gx, 1, z + 1, w) if z in (1, 2) else None

    def hop3(gx, gc, z, w):
        if gc == 0:
            return (gx, 0, z ^ 1, w) if z < 2 else None
        return (gx, 1, z ^ 1, w) if z > 1 else None

    def lane_share(gx, gc, z, w):
        return (gx, 1 - gc, z, w) if gc == z >> 1 else None

    def gather_wt(value):
        if sizes["wt"] == 2:
            other = send(value, wt_mate)
            first = lax.axis_index("wt") == 0
            return jnp.stack([jnp.where(first, value, other), jnp.where(first, other, value)])
        return lax.all_gather(value, "wt", axis=0, tiled=False)

    def scatter_wt(value):
        if sizes["wt"] == 2:
            own = lax.axis_index("wt")
            mine = lax.dynamic_index_in_dim(value, own, 0, keepdims=False)
            other = send(lax.dynamic_index_in_dim(value, 1 - own, 0, keepdims=False), wt_mate)
            return (mine.astype(f32) + other.astype(f32)).astype(bf16)
        return lax.psum_scatter(value, "wt", scatter_dimension=0, tiled=False)

    def halve(value, bit, mate):
        half = value.shape[0] // 2
        other = send(rows_at(value, (1 - bit) * half, half), mate)
        return (rows_at(value, bit * half, half).astype(f32) + other.astype(f32)).astype(bf16)

    def double(value, bit, mate):
        other = send(value, mate)
        first = bit == 0
        return jnp.stack([jnp.where(first, value, other), jnp.where(first, other, value)])

    def sum_all(value):
        for axis in AXES:
            step = 1
            while step < sizes[axis]:

                def mate(gx, gc, z, w, axis=axis, step=step):
                    at = dict(gx=gx, gc=gc, ctx=z, wt=w)
                    at[axis] ^= step
                    return (at["gx"], at["gc"], at["ctx"], at["wt"])

                value = value + send(value, mate)
                step *= 2
        return value

    def local(
        tokens, segments, w_qkv, w_proj, w_in, w_out, gain_attn, gain_mlp, query_scale, cotangent
    ):
        gx, gc, z, wt = (lax.axis_index(axis) for axis in AXES)
        host = z // 2
        near = z % 2
        mine = 2 * near + gc
        parts = sizes["ctx"]
        nh = H // parts
        groups = 2
        rows = tokens.shape[1]
        group_len = segments.shape[1]
        wrows = w_qkv.shape[0]
        lane = gc == host
        pair = sizes["wt"] == 2

        def after(value, *others):
            return lax.optimization_barrier((value,) + others)[0]

        own = tokens[0]
        got1 = send(own, hop1)
        own_share = send(own, lane_share)
        seg_mate = send(segments, core_mate)
        picked = pick(w_qkv, mine, parts, groups, nh)
        got1 = after(got1, picked)
        got2 = send(got1, hop2)
        got1_share = send(got1, lane_share)
        end = jnp.where(gc == 0, z == 0, z == 3)
        if pair:
            other_w = send(picked, wt_mate)
            *flat_w, wide_w = widen(picked, other_w, wt, groups, nh)
        else:
            flat_all = lax.all_gather(picked, "wt", axis=0, tiled=True)
            each = flat_all.shape[1] // groups
            flat_w = [flat_all[:, g * each : (g + 1) * each] for g in range(groups)]
            order = jnp.transpose(flat_all.reshape(D, groups, 3, nh // groups, HD), (0, 2, 1, 3, 4))
            wide_w = jnp.pad(
                order.reshape(D, 3 * nh, HD), ((0, 0), (0, 0), (0, LN - HD))
            ).reshape(D, -1)
        got3 = send(jnp.where(end, own, got2), hop3)
        got2_share = send(got2, lane_share)
        way = 1 - 2 * host
        last = jnp.where(host == 0, jnp.where(z == 0, 3, 0), jnp.where(z == 3, 0, 3))
        places = (z, z + way, z + 2 * way, last)

        half_rows = wrows // 2
        tail_own = jnp.stack([w_proj, w_in, w_out])
        half_w = lax.dynamic_slice_in_dim(tail_own, gc * half_rows, half_rows, 1)
        if pair:
            half_w = send(after(half_w, other_w), wt_mate)
        else:
            half_w = lax.all_gather(half_w, "wt", axis=0, tiled=False)

        dim_scale = scale_base / math.sqrt(HD) * jax.nn.softplus(query_scale)
        lane_scale = jnp.tile(jnp.pad(dim_scale * log2e, (0, LN - HD)), nh)[None]
        ones = jnp.tile(
            ((jnp.arange(LN) >= HD) & (jnp.arange(LN) < HD + 3)).astype(f32), 2 * nh
        )[None]
        seg_row = jnp.where(lane, segments, seg_mate)[0]
        fixed = (lane, mine, gain_attn[None], wide_w, lane_scale, ones, group_len)
        first = project(
            ((own, own_share), (got1, got1_share), (got2, got2_share)), places[:3], *fixed
        )
        got3 = after(got3, first[0])
        got3_share = send(got3, lane_share)
        all_normed, queries, keyval, inputs = project(
            ((got3, got3_share),), places[3:], *fixed, carried=first
        )
        grad_mlp = send(after(cotangent[0], got3), to_host)

        att, att_float, q_aug = attn_fwd(queries, keyval, seg_row, nh)

        trades = (core_mate, near_mate, cross_mate)
        att_pieces = [rows_at(att, (mine ^ j) * rows, rows) for j in range(parts)]
        att_pieces = [att_pieces[0]] + [send(att_pieces[j + 1], trades[j]) for j in range(3)]
        half_mate = send(after(half_w, att), core_mate)
        if pair:
            weights = (tail_own, half_w, half_mate)
            starts = (wt * wrows, (1 - wt) * wrows + gc * half_rows, (1 - wt) * wrows + (1 - gc) * half_rows)
        else:
            one = gc == 0
            tail_w = jnp.stack(
                [jnp.where(one, half_w, half_mate), jnp.where(one, half_mate, half_w)], axis=1
            )
            weights = (jnp.transpose(tail_w, (2, 0, 1, 3, 4)).reshape(3, D, D),)
            starts = ()
        (
            layer_out,
            attended,
            normed_mlp,
            grad_hidden,
            active,
            grad_proj,
            grad_resid,
            *pieces,
            grad_gain_mlp,
        ) = tail(jnp.stack([mine, *starts]), att_pieces, inputs, grad_mlp, weights, gain_mlp[None])
        pieces = [pieces[0]] + [send(pieces[j + 1], trades[j]) for j in range(3)]

        lefts = (attended, normed_mlp, active)
        rights = (grad_proj, grad_hidden, grad_mlp)
        width = D // 2
        if pair:
            to_core = share(lefts, rights, 1 - gc)
            from_core = send(to_core, core_mate)
            layer_out = send(after(layer_out, to_core)[None], to_home)
            a_send, a_keep, b_send, b_keep = keep(
                lefts, rights, from_core, jnp.stack([gc, gx, wt])
            )
            a_got = send(a_send, x_mate)
            b_got = send(b_send, wt_mate)
            ready = a_send
        else:
            layer_out = send(layer_out[None], to_home)

            def by_column(flip):
                one = gc == flip
                return jnp.concatenate(
                    [
                        trans_times(
                            left, jnp.where(one, right[:, :width], right[:, width:])
                        ).astype(bf16)
                        for left, right in zip(lefts, rights)
                    ],
                    axis=1,
                )

            half_grad = send(by_column(1), core_mate)
            half_grad = (by_column(0).astype(f32) + half_grad.astype(f32)).astype(bf16)
            half_grad = lax.psum(scatter_wt(half_grad.reshape(-1, wrows, 3 * width)), ("gx", "ctx"))
            mate_grad = send(half_grad, core_mate)
            one = gc == 0
            totals = []
            for i in range(3):
                a = half_grad[:, i * width : (i + 1) * width]
                b = mate_grad[:, i * width : (i + 1) * width]
                totals.append(
                    jnp.concatenate([jnp.where(one, a, b), jnp.where(one, b, a)], axis=1).astype(f32)
                )
            ready = grad_proj

        scale_row = jnp.tile(dim_scale, nh // groups)[None]

        def backward(group, pieces):
            return attn_bwd(
                q_aug, keyval, pieces, att_float, seg_row, mine, scale_row, nh, group, groups
            )

        def qkv_start(grad):
            if pair:
                sent = cross(all_normed, grad, 1 - wt)
                got = send(sent, wt_mate)
                kept = cross(all_normed, grad, wt)
                return kept.reshape(2, wrows // 2, -1), got.reshape(2, wrows // 2, -1)
            kept = trans_times(all_normed, grad).astype(bf16).reshape(-1, wrows, grad.shape[1])
            kept = scatter_wt(kept).reshape(2, wrows // 2, -1)
            return kept, jnp.zeros_like(kept)

        def qkv_far(kept, got):
            (part, kept), = fold(((kept, got, gx),))
            got = send(part, x_mate)
            quarter = wrows // 4
            (part, kept), = fold(
                ((kept.reshape(2, quarter, -1), got.reshape(2, quarter, -1), host),)
            )
            return kept, send(part, far_mate)

        def qkv_gather(kept, got):
            block = (kept.astype(f32) + got.astype(f32)).astype(bf16)[None]
            for mate in (far_mate, near_mate, x_mate):
                block = jnp.concatenate([block, send(block, mate)])
            return block, send(block, core_mate)

        pieces[3] = after(pieces[3], ready)
        grad_a, lanes_a = backward(0, pieces)
        if pair:
            a_got, b_got = after(a_got, grad_a), after(b_got, grad_a)
            (a_send, a_keep), (b_send, b_keep) = fold(
                (
                    (a_keep, a_got, wt),
                    (b_keep.reshape(2, -1, 3 * width), b_got.reshape(2, -1, 3 * width), gx),
                )
            )
            a_got = send(a_send, wt_mate)
            b_got = send(b_send, x_mate)
            pieces[3] = after(pieces[3], a_send)
        start_a = qkv_start(grad_a)
        pieces[3] = after(pieces[3], start_a[0])
        grad_b, lanes_b = backward(1, pieces)
        if pair:
            a_got, b_got = after(a_got, grad_b), after(b_got, grad_b)
            block = jnp.stack(
                [
                    (k.astype(f32) + g.astype(f32)).astype(bf16)
                    for k, g in ((a_keep, a_got), (b_keep, b_got))
                ]
            )
            block = lax.psum(block, "ctx")
        start_b = qkv_start(grad_b)
        far_a = qkv_far(start_a[0], after(start_a[1], grad_b))
        far_b = qkv_far(*start_b)

        def shard_grad(shard):
            return sum(
                times_trans(rows_at(grad, shard * rows, rows), w)
                for grad, w in zip((after(grad_a, start_b[0]), after(grad_b, start_b[0])), flat_w)
            )

        to_core = jnp.stack([shard_grad(mine ^ 3), shard_grad(mine ^ 1)]).astype(bf16)
        from_core = send(to_core, core_mate).astype(f32)
        to_near = (shard_grad(mine ^ 2) + from_core[0]).astype(bf16)
        grad_normed = shard_grad(mine) + from_core[1] + send(to_near, near_mate).astype(f32)
        inputs = inputs.astype(f32)
        inverse_attn = rms_inverse(inputs)
        grad_gain_attn = jnp.sum(grad_normed * inputs * inverse_attn, axis=0)
        grad_tokens = send(
            (grad_resid + norm_back(inputs, inverse_attn, grad_normed * gain_attn)).astype(bf16)[None],
            to_home,
        )

        total_qkv = spread(
            [qkv_gather(*far_a), qkv_gather(*far_b)], jnp.stack([gx, host, near, gc])
        )
        if pair:
            from_x = send(block, x_mate)
            totals = place_tail(
                block, from_x, send(block, core_mate), send(from_x, core_mate), jnp.stack([gx, gc])
            )

        grad_query_scale = (
            (lanes_a + lanes_b)[0, :HD]
            / (dim_scale * log2e)
            * (scale_base / math.sqrt(HD))
            * jax.nn.sigmoid(query_scale)
        )
        small = jnp.concatenate(
            [grad_gain_attn, grad_gain_mlp[0], jnp.pad(grad_query_scale, (0, LN - HD))]
        ).reshape(-1, LN)
        small = sum_all(small).reshape(-1)
        return (
            layer_out,
            grad_tokens,
            total_qkv,
            *totals,
            small[:D],
            small[D : 2 * D],
            small[2 * D : 2 * D + HD],
        )

    return local


def solution(mesh):
    groups, parts, wt = (mesh.shape[axis] for axis in ("grp", "ctx", "wt"))
    inner = Mesh(mesh.devices.reshape(groups // 2, 2, parts, wt), AXES)
    sizes = dict(inner.shape)
    split = P(("gx", "gc", "wt"), "ctx", None)
    weight = P("wt", None)
    return jax.shard_map(
        make_local(sizes),
        mesh=inner,
        in_specs=(
            split,
            P(("gx", "gc", "wt"), None),
            weight,
            weight,
            weight,
            weight,
            P(),
            P(),
            P(),
            split,
        ),
        out_specs=(split, split, weight, weight, weight, weight, P(), P(), P()),
        check_vma=False,
    )
```

```python
import functools
import math

import jax
import jax.numpy as jnp
from jax import lax
from jax.experimental import pallas as pl
from jax.experimental.pallas import tpu as pltpu
from jax.sharding import Mesh
from jax.sharding import PartitionSpec as P

D = 1280
H = 16
HD = 80
LN = 128
epsilon = 1e-06
scale_base = 1.442695041
log2e = 1.4426950408889634
NEG = -1e30
CHEAP = pl.CostEstimate(flops=1000, transcendentals=0, bytes_accessed=1000)
f32 = jnp.float32
bf16 = jnp.bfloat16
AXES = ("gx", "gc", "far", "near", "wt")


def block_flags(seg_row, bq, bk):
    n = seg_row.shape[0]
    q = seg_row.reshape(n // bq, bq)
    k = seg_row.reshape(n // bk, bk)
    qf, ql = q[:, 0][:, None], q[:, -1][:, None]
    kf, kl = k[:, 0][None], k[:, -1][None]
    qs = jnp.arange(n // bq, dtype=jnp.int32)[:, None] * bq
    ks = jnp.arange(n // bk, dtype=jnp.int32)[None] * bk
    below = ks + bk - 1 <= qs
    skip = (ks > qs + bq - 1) | ((kf > 0) & (kl < qf))
    same = (qf == ql) & (kl == ql) & ((kf == kl) | ((kf == 0) & (kl == 1)))
    full = below & ((kl == 0) | same)
    return jnp.where(skip, 0, jnp.where(full, 1, 2)).astype(jnp.int32).reshape(-1)


def put_split(base, col, lanes):
    hi = col.astype(bf16).astype(f32)
    rest = col - hi
    mid = rest.astype(bf16).astype(f32)
    out = jnp.where(lanes == HD, hi, base)
    out = jnp.where(lanes == HD + 1, mid, out)
    return jnp.where(lanes == HD + 2, rest - mid, out).astype(bf16)


def fwd_kernel(flags, q_ref, kv, segc, segr, att, of, qaug, m_s, acc_s, *, nh, bq, bk, nk):
    qi = pl.program_id(0)
    count = (qi * bq + bq + bk - 1) // bk
    nt = (((1,), (1,)), ((), ()))
    acc_s[...] = jnp.zeros_like(acc_s)
    m_s[...] = jnp.zeros_like(m_s)

    def mask(ko):
        qpos = qi * bq + lax.broadcasted_iota(jnp.int32, (bq, bk), 0)
        kpos = ko + lax.broadcasted_iota(jnp.int32, (bq, bk), 1)
        ks = segr[:, pl.ds(ko, bk)]
        return (kpos <= qpos) & ((ks == 0) | (ks == segc[...]))

    def step(kb, masked):
        ko = pl.multiple_of(kb * bk, bk)
        if masked:
            allowed = mask(ko)
        for h in range(nh):
            k = kv[pl.ds(ko, bk), h * LN : (h + 1) * LN]
            v = kv[pl.ds(ko, bk), (nh + h) * LN : (nh + h + 1) * LN]
            s = lax.dot_general(q_ref[:, h * LN : (h + 1) * LN], k, nt, preferred_element_type=f32)
            p = jnp.exp2(s)
            if masked:
                p = jnp.where(allowed, p, 0.0)
            acc_s[h] += jnp.dot(p.astype(bf16), v, preferred_element_type=f32)

    def body(kb, carry):
        flag = flags[qi * nk + kb]

        @pl.when(flag == 1)
        def _():
            step(kb, False)

        @pl.when(flag == 2)
        def _():
            step(kb, True)

        return carry

    lax.fori_loop(0, count, body, 0)
    bad = jnp.zeros((bq, 1), f32)
    for h in range(nh):
        total = acc_s[h][:, HD : HD + 1]
        bad = jnp.maximum(bad, jnp.where((total > 2.0**-60) & (total < 2.0**60), 0.0, 1.0))

    @pl.when(jnp.max(bad) > 0.0)
    def _():
        def head(h, carry):
            kc = pl.ds(pl.multiple_of(h * LN, LN), LN)
            vc = pl.ds(pl.multiple_of((nh + h) * LN, LN), LN)
            m_s[h] = jnp.full((bq, LN), NEG, f32)
            acc_s[h] = jnp.zeros((bq, LN), f32)

            def inner(kb, carry):
                @pl.when(flags[qi * nk + kb] > 0)
                def _():
                    ko = pl.multiple_of(kb * bk, bk)
                    s = lax.dot_general(
                        q_ref[:, kc], kv[pl.ds(ko, bk), kc], nt, preferred_element_type=f32
                    )
                    s = jnp.where(mask(ko), s, NEG)
                    old = m_s[h]
                    new = jnp.maximum(old, jnp.max(s, axis=1, keepdims=True))
                    p = jnp.exp2(s - new[:, :1]).astype(bf16)
                    m_s[h] = new
                    acc_s[h] = acc_s[h] * jnp.exp2(old - new) + jnp.dot(
                        p, kv[pl.ds(ko, bk), vc], preferred_element_type=f32
                    )

                return carry

            lax.fori_loop(0, count, inner, 0)
            return carry

        lax.fori_loop(0, nh, head, 0)

    lanes = lax.broadcasted_iota(jnp.int32, (bq, LN), 1)
    outs = []
    for h in range(nh):
        acc = acc_s[h]
        total = acc[:, HD : HD + 1]
        out = acc * (1.0 / total)
        of[:, h * LN : (h + 1) * LN] = jnp.where(lanes < HD, out, 0.0)
        outs.append(out[:, :HD])
        lse = m_s[h][:, :1] + jnp.log2(total)
        qaug[:, h * LN : (h + 1) * LN] = put_split(
            q_ref[:, h * LN : (h + 1) * LN].astype(f32), -lse, lanes
        )
    att[...] = jnp.concatenate(outs, axis=1).astype(bf16)


def attn_fwd(q, kv, seg_row, nh, bq=512, bk=512):
    n = q.shape[0]
    w = nh * LN
    spec = pltpu.PrefetchScalarGridSpec(
        num_scalar_prefetch=1,
        grid=(n // bq,),
        in_specs=[
            pl.BlockSpec((bq, w), lambda i, f: (i, 0)),
            pl.BlockSpec((n, 2 * w), lambda i, f: (0, 0)),
            pl.BlockSpec((bq, 1), lambda i, f: (i, 0)),
            pl.BlockSpec((1, n), lambda i, f: (0, 0)),
        ],
        out_specs=[
            pl.BlockSpec((bq, nh * HD), lambda i, f: (i, 0)),
            pl.BlockSpec((bq, w), lambda i, f: (i, 0)),
            pl.BlockSpec((bq, w), lambda i, f: (i, 0)),
        ],
        scratch_shapes=[pltpu.VMEM((nh, bq, LN), f32), pltpu.VMEM((nh, bq, LN), f32)],
    )
    return pl.pallas_call(
        functools.partial(fwd_kernel, nh=nh, bq=bq, bk=bk, nk=n // bk),
        out_shape=[
            jax.ShapeDtypeStruct((n, nh * HD), bf16),
            jax.ShapeDtypeStruct((n, w), f32),
            jax.ShapeDtypeStruct((n, w), bf16),
        ],
        grid_spec=spec,
        compiler_params=pltpu.CompilerParams(vmem_limit_bytes=40 << 20),
        cost_estimate=CHEAP,
        name="attn_fwd",
    )(block_flags(seg_row, bq, bk), q, kv, seg_row[:, None], seg_row[None])


def bwd_kernel(
    flags, mine, qa, kk, vv, do0, do1, do2, do3, of, segc, segr, scale, dqkv, gscale, doa_s, dq_s, dk_s, dv_s, *, first, nh, bq, bk, n
):
    nk = n // bk
    nq = n // bq
    kb = pl.program_id(0)
    part = n // 4
    step_rows = 256 if part % 256 == 0 else part
    lanes = lax.broadcasted_iota(jnp.int32, (step_rows, LN), 1)

    @pl.when(kb == 0)
    def _():
        dq_s[...] = jnp.zeros_like(dq_s)
        for j, piece in enumerate((do0, do1, do2, do3)):
            start = (mine[0] ^ j) * part
            for i in range(part // step_rows):
                d = piece[i * step_rows : (i + 1) * step_rows, :].astype(f32)
                r = pl.ds(pl.multiple_of(start + i * step_rows, step_rows), step_rows)
                for h in range(nh):
                    at = (first + h) * HD
                    dh = jnp.concatenate(
                        [d[:, at : at + HD], jnp.zeros((step_rows, LN - HD), f32)], axis=1
                    )
                    c = slice(h * LN, (h + 1) * LN)
                    delta = jnp.sum(dh * of[r, c], axis=1, keepdims=True)
                    doa_s[r, c] = put_split(dh, -delta, lanes)

    dk_s[...] = jnp.zeros_like(dk_s)
    dv_s[...] = jnp.zeros_like(dv_s)
    ko = kb * bk
    nt = (((1,), (1,)), ((), ()))
    tn = (((0,), (0,)), ((), ()))

    def step(qi, masked):
        qo = pl.multiple_of(qi * bq, bq)
        if masked:
            kpos = ko + lax.broadcasted_iota(jnp.int32, (bk, bq), 0)
            qpos = qo + lax.broadcasted_iota(jnp.int32, (bk, bq), 1)
            ks = segc[...]
            allowed = (kpos <= qpos) & ((ks == 0) | (ks == segr[:, pl.ds(qo, bq)]))
        for h in range(nh):
            c = slice(h * LN, (h + 1) * LN)
            q = qa[pl.ds(qo, bq), c]
            k = kk[:, c]
            d = doa_s[pl.ds(qo, bq), c]
            p = jnp.exp2(lax.dot_general(k, q, nt, preferred_element_type=f32))
            if masked:
                p = jnp.where(allowed, p, 0.0)
            ds = (p * lax.dot_general(vv[:, c], d, nt, preferred_element_type=f32)).astype(bf16)
            dv_s[h] += jnp.dot(p.astype(bf16), d, preferred_element_type=f32)
            dk_s[h] += jnp.dot(ds, q, preferred_element_type=f32)
            dq_s[h, pl.ds(qo, bq), :] += lax.dot_general(ds, k, tn, preferred_element_type=f32)

    def body(qi, carry):
        flag = flags[qi * nk + kb]

        @pl.when(flag == 1)
        def _():
            step(qi, False)

        @pl.when(flag == 2)
        def _():
            step(qi, True)

        return carry

    lax.fori_loop(ko // bq, nq, body, 0)
    r = pl.multiple_of(ko, bk)
    ln2 = math.log(2.0)
    gap = dqkv.shape[1] - 3 * nh * HD
    dqkv[pl.ds(r, bk), nh * HD :] = jnp.concatenate(
        [dk_s[h][:, :HD] * ln2 for h in range(nh)]
        + [dv_s[h][:, :HD] for h in range(nh)]
        + [jnp.zeros((bk, gap), f32)],
        axis=1,
    ).astype(bf16)

    @pl.when(kb == nk - 1)
    def _():
        total = jnp.zeros((1, LN), f32)
        for i in range(nq):
            rows = slice(i * bq, (i + 1) * bq)
            for h in range(nh):
                total = total + jnp.sum(
                    dq_s[h, rows, :] * qa[rows, h * LN : (h + 1) * LN].astype(f32), axis=0, keepdims=True
                )
            grads = jnp.concatenate([dq_s[h, rows, :][:, :HD] for h in range(nh)], axis=1)
            dqkv[rows, 0 : nh * HD] = (grads * scale[...]).astype(bf16)
        gscale[...] = jnp.broadcast_to(total, gscale.shape)


def attn_bwd(qa, kv, pieces, of, seg_row, mine, scale, heads, group, groups, bq=512, bk=512):
    n = qa.shape[0]
    nh = heads // groups
    w = nh * LN
    once = pl.Buffered(1)
    spec = pltpu.PrefetchScalarGridSpec(
        num_scalar_prefetch=2,
        grid=(n // bk,),
        in_specs=[
            pl.BlockSpec((n, w), lambda i, f, m: (0, group), pipeline_mode=once),
            pl.BlockSpec((bk, w), lambda i, f, m: (i, group)),
            pl.BlockSpec((bk, w), lambda i, f, m: (i, groups + group)),
        ]
        + [pl.BlockSpec((n // 4, heads * HD), lambda i, f, m: (0, 0), pipeline_mode=once)] * 4
        + [
            pl.BlockSpec((n, w), lambda i, f, m: (0, group), pipeline_mode=once),
            pl.BlockSpec((bk, 1), lambda i, f, m: (i, 0)),
            pl.BlockSpec((1, n), lambda i, f, m: (0, 0)),
            pl.BlockSpec((1, nh * HD), lambda i, f, m: (0, 0)),
        ],
        out_specs=[
            pl.BlockSpec((n, lanes_up(3 * nh * HD)), lambda i, f, m: (0, 0)),
            pl.BlockSpec((8, LN), lambda i, f, m: (0, 0)),
        ],
        scratch_shapes=[
            pltpu.VMEM((n, w), bf16),
            pltpu.VMEM((nh, n, LN), f32),
            pltpu.VMEM((nh, bk, LN), f32),
            pltpu.VMEM((nh, bk, LN), f32),
        ],
    )
    return pl.pallas_call(
        functools.partial(bwd_kernel, first=group * nh, nh=nh, bq=bq, bk=bk, n=n),
        out_shape=[
            jax.ShapeDtypeStruct((n, lanes_up(3 * nh * HD)), bf16),
            jax.ShapeDtypeStruct((8, LN), f32),
        ],
        grid_spec=spec,
        compiler_params=pltpu.CompilerParams(vmem_limit_bytes=48 << 20),
        cost_estimate=CHEAP,
        name="attn_bwd",
    )(block_flags(seg_row, bq, bk), mine.reshape(1), qa, kv, kv, *pieces, of, seg_row[:, None], seg_row[None], scale)


def quarter_columns(place, parts, groups, nh):
    width = nh // groups * HD
    return [
        (t * D + place * nh * HD + g * width, width) for g in range(groups) for t in range(3)
    ]


def pick_kernel(mine, w_ref, out, *, parts, groups, nh):
    for i in range(parts):

        @pl.when(mine[0] == i)
        def _(i=i):
            cut = [w_ref[:, a : a + width] for a, width in quarter_columns(i, parts, groups, nh)]
            used = sum(x.shape[1] for x in cut)
            pad = jnp.zeros((cut[0].shape[0], out.shape[1] - used), out.dtype)
            out[...] = jnp.concatenate(cut + [pad], axis=1)


def lanes_up(n):
    return -(-n // LN) * LN


def pick(w, mine, parts, groups, nh):
    rows = w.shape[0]
    step = 160 if rows % 160 == 0 else rows
    return pl.pallas_call(
        functools.partial(pick_kernel, parts=parts, groups=groups, nh=nh),
        out_shape=jax.ShapeDtypeStruct((rows, lanes_up(3 * nh * HD)), w.dtype),
        grid_spec=pltpu.PrefetchScalarGridSpec(
            num_scalar_prefetch=1,
            grid=(rows // step,),
            in_specs=[pl.BlockSpec((step, 3 * D), lambda i, m: (i, 0))],
            out_specs=pl.BlockSpec((step, lanes_up(3 * nh * HD)), lambda i, m: (i, 0)),
        ),
        cost_estimate=CHEAP,
        name="pick",
    )(mine.reshape(1), w)


def widen_kernel(own_first, a_ref, b_ref, *outs, groups, nh):
    flats, wide = outs[:-1], outs[-1]

    def put(ref):
        value = ref[...]
        each = 3 * nh * HD // groups
        gap = jnp.zeros((value.shape[0], lanes_up(each) - each), value.dtype)
        for g in range(groups):
            flats[g][...] = jnp.concatenate([value[:, g * each : (g + 1) * each], gap], axis=1)
        zero = jnp.zeros((value.shape[0], LN - HD), value.dtype)
        per = nh // groups
        spread = []
        for t in range(3):
            for h in range(nh):
                at = (h // per) * each + t * per * HD + (h % per) * HD
                spread += [value[:, at : at + HD], zero]
        wide[...] = jnp.concatenate(spread, axis=1)

    half = pl.program_id(0)

    @pl.when(half == 0)
    def _():
        put(a_ref)

    @pl.when(half == 1)
    def _():
        put(b_ref)


def widen(own, other, own_at, groups, nh):
    rows, width = own.shape
    step = 160
    n = rows // step
    at = lambda i, j, m: ((i ^ m[0]) * n + j, 0)
    each = lanes_up(3 * nh * HD // groups)
    return pl.pallas_call(
        functools.partial(widen_kernel, groups=groups, nh=nh),
        out_shape=[jax.ShapeDtypeStruct((2 * rows, each), own.dtype)] * groups
        + [jax.ShapeDtypeStruct((2 * rows, 3 * nh * LN), own.dtype)],
        grid_spec=pltpu.PrefetchScalarGridSpec(
            num_scalar_prefetch=1,
            grid=(2, n),
            in_specs=[
                pl.BlockSpec((step, width), lambda i, j, m: (j * (1 - i), 0)),
                pl.BlockSpec((step, width), lambda i, j, m: (j * i, 0)),
            ],
            out_specs=[pl.BlockSpec((step, each), at)] * groups + [pl.BlockSpec((step, 3 * nh * LN), at)],
        ),
        cost_estimate=CHEAP,
        name="widen",
    )(own_at.reshape(1), own, other)


def project_kernel(info, *refs, count, width, fresh):
    pairs = refs[: 2 * count]
    gain, w, scale, ones = refs[2 * count : 2 * count + 4]
    normed_ref, q_ref, kv_ref, mine_ref = refs[-4:]
    j = pl.program_id(0)

    def work(x_ref):
        value = x_ref[...]
        x = value.astype(f32)
        inverse = lax.rsqrt(jnp.mean(x * x, axis=-1, keepdims=True) + epsilon)
        normed = (x * inverse * gain[...]).astype(bf16)
        normed_ref[...] = normed
        q_ref[...] = (
            jnp.dot(normed, w[:, :width], preferred_element_type=f32) * scale[...]
        ).astype(bf16)
        kv_ref[...] = (
            jnp.dot(normed, w[:, width:], preferred_element_type=f32) + ones[...]
        ).astype(bf16)

        @pl.when(info[count + 1] == info[j])
        def _():
            mine_ref[...] = value

    if not fresh:
        mine_ref[...] = refs[2 * count + 4][...]
    for i in range(count):
        for lane in range(2):

            @pl.when((j == i) & (info[count] == lane))
            def _(i=i, lane=lane):
                work(pairs[2 * i + 1 - lane])


def project(pairs, places, lane, mine, gain, w, scale, ones, group_len, carried=None):
    count = len(pairs)
    rows, d = pairs[0][0].shape
    width = scale.shape[1]
    full = lambda i, f: (0, 0)
    at = lambda i, f: (f[i], 0)
    once = pl.Buffered(1)
    info = jnp.stack(list(places) + [lane.astype(jnp.int32), mine])
    args = [x for pair in pairs for x in pair] + [gain, w, scale, ones]
    in_specs = [pl.BlockSpec((rows, d), full, pipeline_mode=once)] * (2 * count) + [
        pl.BlockSpec((1, d), full, pipeline_mode=once),
        pl.BlockSpec(w.shape, full, pipeline_mode=once),
        pl.BlockSpec((1, width), full, pipeline_mode=once),
        pl.BlockSpec((1, 2 * width), full, pipeline_mode=once),
    ]
    aliases = {}
    if carried is not None:
        args += [carried[3], *carried[:3]]
        in_specs += [pl.BlockSpec((rows, d), full, pipeline_mode=once)] + [pl.BlockSpec(memory_space=pl.ANY)] * 3
        base = 2 * count + 6
        aliases = {base: 0, base + 1: 1, base + 2: 2}
    return pl.pallas_call(
        functools.partial(project_kernel, count=count, width=width, fresh=carried is None),
        out_shape=[
            jax.ShapeDtypeStruct((group_len, d), bf16),
            jax.ShapeDtypeStruct((group_len, width), bf16),
            jax.ShapeDtypeStruct((group_len, 2 * width), bf16),
            jax.ShapeDtypeStruct((rows, d), bf16),
        ],
        grid_spec=pltpu.PrefetchScalarGridSpec(
            num_scalar_prefetch=1,
            grid=(count,),
            in_specs=in_specs,
            out_specs=[
                pl.BlockSpec((rows, d), at),
                pl.BlockSpec((rows, width), at),
                pl.BlockSpec((rows, 2 * width), at),
                pl.BlockSpec((rows, d), full),
            ],
        ),
        input_output_aliases=aliases,
        compiler_params=pltpu.CompilerParams(vmem_limit_bytes=48 << 20),
        cost_estimate=CHEAP,
        name="project",
    )(info, *args)


def tail_body(at, p0, p1, p2, p3, x_ref, g_ref, w_s, gain, outs):
    lo_ref, att_ref, nm_ref, gh_ref, act_ref, gp_ref, gr_ref, c0, c1, c2, c3, gg_ref = outs
    mine = at[0]
    pieces = (p0, p1, p2, p3)
    cols = p0.shape[1]
    nt = (((1,), (1,)), ((), ()))
    for i in range(4):

        @pl.when(mine == i)
        def _(i=i):
            att_ref[...] = jnp.concatenate([pieces[i ^ k][...] for k in range(4)], axis=1)

    resid = x_ref[...].astype(f32) + jnp.dot(att_ref[...], w_s[0], preferred_element_type=f32)
    inverse = lax.rsqrt(jnp.mean(resid * resid, axis=-1, keepdims=True) + epsilon)
    normed = (resid * inverse * gain[...]).astype(bf16)
    nm_ref[...] = normed
    hidden = jnp.dot(normed, w_s[1], preferred_element_type=f32)
    sig = 1.0 / (1.0 + jnp.exp(-hidden))
    active = (hidden * sig).astype(bf16)
    act_ref[...] = active
    lo_ref[...] = (resid + jnp.dot(active, w_s[2], preferred_element_type=f32)).astype(bf16)
    grad_active = lax.dot_general(g_ref[...], w_s[2], nt, preferred_element_type=f32)
    grad_hidden = (grad_active * sig * (1.0 + hidden * (1.0 - sig))).astype(bf16)
    gh_ref[...] = grad_hidden
    grad_normed = lax.dot_general(grad_hidden, w_s[1], nt, preferred_element_type=f32)
    gg_ref[...] += jnp.sum(grad_normed * resid * inverse, axis=0, keepdims=True)
    scaled = grad_normed * gain[...]
    grad_resid = (
        g_ref[...].astype(f32)
        + inverse * scaled
        - resid * (inverse * inverse * inverse) * jnp.mean(scaled * resid, axis=-1, keepdims=True)
    )
    gr_ref[...] = grad_resid
    grad_proj = grad_resid.astype(bf16)
    gp_ref[...] = grad_proj
    grad_att = lax.dot_general(grad_proj, w_s[0], nt, preferred_element_type=f32).astype(bf16)
    for i in range(4):

        @pl.when(mine == i)
        def _(i=i):
            for j, out in enumerate((c0, c1, c2, c3)):
                out[...] = grad_att[:, (i ^ j) * cols : ((i ^ j) + 1) * cols]


def tail_kernel(at, p0, p1, p2, p3, x_ref, g_ref, own, half, other, gain, *refs, rows, hrows):
    w_s = refs[-1]
    outs = refs[:-1]

    @pl.when(pl.program_id(0) == 0)
    def _():
        outs[-1][...] = jnp.zeros_like(outs[-1])
        w_s[:, pl.ds(pl.multiple_of(at[1], 16), rows), :] = own[...]
        w_s[:, pl.ds(pl.multiple_of(at[2], 16), hrows), :] = half[...]
        w_s[:, pl.ds(pl.multiple_of(at[3], 16), hrows), :] = other[...]

    tail_body(at, p0, p1, p2, p3, x_ref, g_ref, w_s, gain, outs)


def whole_tail_kernel(at, p0, p1, p2, p3, x_ref, g_ref, w, gain, *outs):
    @pl.when(pl.program_id(0) == 0)
    def _():
        outs[-1][...] = jnp.zeros_like(outs[-1])

    tail_body(at, p0, p1, p2, p3, x_ref, g_ref, w, gain, outs)


def tail(at, pieces, x, g, weights, gain, tile=256):
    rows, d = x.shape
    cols = pieces[0].shape[1]
    row = lambda i, m: (i, 0)
    once = pl.Buffered(1)
    whole = lambda *shape: pl.BlockSpec(shape, lambda i, m: (0,) * len(shape), pipeline_mode=once)
    wide = pl.BlockSpec((tile, d), row)
    slim = pl.BlockSpec((tile, cols), row)
    if len(weights) == 3:
        body = functools.partial(tail_kernel, rows=weights[0].shape[1], hrows=weights[1].shape[1])
        scratch = [pltpu.VMEM((3, d, d), bf16)]
    else:
        body = whole_tail_kernel
        scratch = []
    return pl.pallas_call(
        body,
        out_shape=[jax.ShapeDtypeStruct((rows, d), bf16)] * 6
        + [jax.ShapeDtypeStruct((rows, d), f32)]
        + [jax.ShapeDtypeStruct((rows, cols), bf16)] * 4
        + [jax.ShapeDtypeStruct((1, d), f32)],
        grid_spec=pltpu.PrefetchScalarGridSpec(
            num_scalar_prefetch=1,
            grid=(rows // tile,),
            in_specs=[slim] * 4 + [wide] * 2 + [whole(*w.shape) for w in weights] + [whole(1, d)],
            out_specs=[wide] * 7 + [slim] * 4 + [pl.BlockSpec((1, d), lambda i, m: (0, 0))],
            scratch_shapes=scratch,
        ),
        compiler_params=pltpu.CompilerParams(vmem_limit_bytes=52 << 20),
        cost_estimate=CHEAP,
        name="tail",
    )(at, *pieces, x, g, *weights, gain)


tn_dims = (((0,), (0,)), ((), ()))


def share_kernel(col, l0, l1, l2, r0, r1, r2, out):
    for i, (left, right) in enumerate(((l0, r0), (l1, r1), (l2, r2))):

        @pl.when(pl.program_id(0) == i)
        def _(left=left, right=right):
            out[...] = lax.dot_general(
                left[...], right[...], tn_dims, preferred_element_type=f32
            ).astype(bf16)


def share(lefts, rights, col):
    rows, d = lefts[0].shape
    w = d // 2
    once = pl.Buffered(1)
    return pl.pallas_call(
        share_kernel,
        out_shape=jax.ShapeDtypeStruct((d, 3 * w), bf16),
        grid_spec=pltpu.PrefetchScalarGridSpec(
            num_scalar_prefetch=1,
            grid=(3,),
            in_specs=[pl.BlockSpec((rows, d), lambda i, c: (0, 0), pipeline_mode=once)] * 3
            + [pl.BlockSpec((rows, w), lambda i, c: (0, c[0]), pipeline_mode=once)] * 3,
            out_specs=pl.BlockSpec((d, w), lambda i, c: (0, i)),
        ),
        compiler_params=pltpu.CompilerParams(vmem_limit_bytes=40 << 20),
        cost_estimate=CHEAP,
        name="share",
    )(col.reshape(1), *lefts, *rights)


def keep_kernel(col, l0, l1, l2, r0, r1, r2, got, out):
    for i, (left, right) in enumerate(((l0, r0), (l1, r1), (l2, r2))):

        @pl.when(pl.program_id(0) == i)
        def _(left=left, right=right):
            out[...] = (
                lax.dot_general(left[...], right[...], tn_dims, preferred_element_type=f32)
                + got[...].astype(f32)
            ).astype(bf16)


def keep(lefts, rights, got, col):
    rows, d = lefts[0].shape
    w = d // 2
    once = pl.Buffered(1)
    block = pl.BlockSpec((d, w), lambda i, c: (0, i))
    return pl.pallas_call(
        keep_kernel,
        out_shape=jax.ShapeDtypeStruct((d, 3 * w), bf16),
        grid_spec=pltpu.PrefetchScalarGridSpec(
            num_scalar_prefetch=1,
            grid=(3,),
            in_specs=[pl.BlockSpec((rows, d), lambda i, c: (0, 0), pipeline_mode=once)] * 3
            + [pl.BlockSpec((rows, w), lambda i, c: (0, c[0]), pipeline_mode=once)] * 3
            + [block],
            out_specs=block,
        ),
        compiler_params=pltpu.CompilerParams(vmem_limit_bytes=40 << 20),
        cost_estimate=CHEAP,
        name="keep",
    )(col.reshape(1), *lefts, *rights, got)


def total_kernel(bit, *refs):
    ins, outs = refs[:-2], refs[-2:]
    for half, out in zip((1 - bit[0], bit[0]), outs):
        acc = jnp.zeros(out.shape, f32)
        for ref in ins:
            for i in range(ref.shape[0]):
                acc = acc + ref[i, half].astype(f32)
        out[...] = acc.astype(bf16)


def total(arrays, bit):
    _, _, r, c = arrays[0].shape
    w = c
    for cut in (640, 512):
        if c % cut == 0:
            w = cut
            break
    return pl.pallas_call(
        total_kernel,
        out_shape=[jax.ShapeDtypeStruct((r, c), bf16)] * 2,
        grid_spec=pltpu.PrefetchScalarGridSpec(
            num_scalar_prefetch=1,
            grid=(c // w,),
            in_specs=[pl.BlockSpec((x.shape[0], 2, r, w), lambda i, m: (0, 0, 0, i)) for x in arrays],
            out_specs=[pl.BlockSpec((r, w), lambda i, m: (0, i))] * 2,
        ),
        compiler_params=pltpu.CompilerParams(vmem_limit_bytes=40 << 20),
        cost_estimate=CHEAP,
        name="total",
    )(bit.reshape(1), *arrays)


def place_kernel(at, own_ref, mate_ref, o0, o1, o2):
    block = pl.program_id(0)
    slot = ((block // 4) ^ at[0]) * 4 + (((block // 2) % 2) ^ at[1]) * 2 + ((block % 2) ^ at[2])
    w = o0.shape[2] // 2

    def put(refs):
        for side, ref in enumerate(refs):
            part = ref[slot].astype(f32)
            for i, out in enumerate((o0, o1, o2)):
                out[0, :, side * w : (side + 1) * w] = part[:, i * w : (i + 1) * w]

    @pl.when(at[3] == 0)
    def _():
        put((own_ref, mate_ref))

    @pl.when(at[3] == 1)
    def _():
        put((mate_ref, own_ref))


def place_tail(own, mate, at):
    n, h, width = own.shape
    d = width // 3 * 2
    whole = pl.BlockSpec(own.shape, lambda i, m: (0, 0, 0), pipeline_mode=pl.Buffered(1))
    outs = pl.pallas_call(
        place_kernel,
        out_shape=[jax.ShapeDtypeStruct((n, h, d), f32)] * 3,
        grid_spec=pltpu.PrefetchScalarGridSpec(
            num_scalar_prefetch=1,
            grid=(n,),
            in_specs=[whole] * 2,
            out_specs=[pl.BlockSpec((1, h, d), lambda i, m: (i, 0, 0))] * 3,
        ),
        compiler_params=pltpu.CompilerParams(vmem_limit_bytes=40 << 20),
        cost_estimate=CHEAP,
        name="place_tail",
    )(at, own, mate)
    return [out.reshape(n * h, d) for out in outs]


def cross_kernel(at, x_ref, g_ref, *refs):
    s = refs[-1]
    s[...] = lax.dot_general(x_ref[...], g_ref[...], tn_dims, preferred_element_type=f32).astype(bf16)
    step = pl.program_id(0)
    half = s.shape[0] // 2
    for w in range(2):

        @pl.when(step == w)
        def _(w=w):
            for x in range(2):
                rows = pl.ds(pl.multiple_of((at[1] ^ x) * half, 16), half)
                refs[2 * w + x][...] = s[rows, :]


def cross(x, g, at):
    rows, d = x.shape
    w = d // 2
    block = pl.BlockSpec((w // 2, g.shape[1]), lambda i, m: (0, 0))
    return pl.pallas_call(
        cross_kernel,
        out_shape=[jax.ShapeDtypeStruct((w // 2, g.shape[1]), bf16)] * 4,
        grid_spec=pltpu.PrefetchScalarGridSpec(
            num_scalar_prefetch=1,
            grid=(2,),
            in_specs=[
                pl.BlockSpec((rows, w), lambda i, m: (0, m[0] ^ i)),
                pl.BlockSpec(g.shape, lambda i, m: (0, 0)),
            ],
            out_specs=[block] * 4,
            scratch_shapes=[pltpu.VMEM((w, g.shape[1]), bf16)],
        ),
        compiler_params=pltpu.CompilerParams(vmem_limit_bytes=40 << 20),
        cost_estimate=CHEAP,
        name="cross",
    )(at, x, g)


def spread_kernel(at, *refs, groups, width):
    out = refs[-1]
    gx, host, near, gc = at[0], at[1], at[2], at[3]
    block = pl.program_id(0)
    slot = ((block // 2) ^ gx) * 4 + ((block % 2) ^ host)

    def put(flip):
        cut = []
        for t in range(3):
            for n in range(2):
                for core in range(2):
                    for g in range(groups):
                        ref = refs[2 * g + (core ^ flip)]
                        part = ref[slot + 2 * (n ^ near)]
                        cut.append(part[:, t * width : (t + 1) * width])
        out[0] = jnp.concatenate(cut, axis=1).astype(f32)

    for flip in range(2):

        @pl.when(gc == flip)
        def _(flip=flip):
            put(flip)


def spread(arrays, at, used):
    flat = [x for pair in arrays for x in pair]
    slots, rows, cols = flat[0].shape
    full = lambda i, m: (0, 0, 0)
    groups = len(arrays)
    total = 4 * groups * used
    return pl.pallas_call(
        functools.partial(spread_kernel, groups=groups, width=used // 3),
        out_shape=jax.ShapeDtypeStruct((4, rows, total), f32),
        grid_spec=pltpu.PrefetchScalarGridSpec(
            num_scalar_prefetch=1,
            grid=(4,),
            in_specs=[pl.BlockSpec(x.shape, full, pipeline_mode=pl.Buffered(1)) for x in flat],
            out_specs=pl.BlockSpec((1, rows, total), lambda i, m: (i, 0, 0)),
        ),
        compiler_params=pltpu.CompilerParams(vmem_limit_bytes=40 << 20),
        cost_estimate=CHEAP,
        name="spread",
    )(at, *flat).reshape(4 * rows, total)


def rms_inverse(values):
    return lax.rsqrt(jnp.mean(values * values, axis=-1, keepdims=True) + epsilon)


def norm_back(values, inverse, grad_scaled):
    return inverse * grad_scaled - values * (inverse * inverse * inverse) * jnp.mean(
        grad_scaled * values, axis=-1, keepdims=True
    )


def dot(left, right):
    return jnp.dot(left, right, preferred_element_type=f32)


def times_trans(left, right):
    return lax.dot_general(left, right, (((1,), (1,)), ((), ())), preferred_element_type=f32)


def trans_times(left, right):
    return lax.dot_general(left, right, (((0,), (0,)), ((), ())), preferred_element_type=f32)


def rows_at(array, start, count):
    return lax.dynamic_slice_in_dim(array, start, count, 0)


def put_rows(array, rows, start):
    return lax.dynamic_update_slice_in_dim(array, rows, start, 0)


def make_local(sizes):
    def pairs(target):
        found = []
        for gx in range(sizes["gx"]):
            for gc in range(sizes["gc"]):
                for z in range(4):
                    for w in range(sizes["wt"]):
                        goal = target(gx, gc, z, w)
                        if goal is not None:
                            found.append((place(gx, gc, z, w), place(*goal)))
        return found

    def place(gx, gc, z, w):
        return ((gx * sizes["gc"] + gc) * 4 + z) * sizes["wt"] + w

    def send(value, target):
        return lax.ppermute(value, AXES, pairs(target))

    def core_mate(gx, gc, z, w):
        return (gx, 1 - gc, z, w)

    def x_mate(gx, gc, z, w):
        return (1 - gx, gc, z, w)

    def near_mate(gx, gc, z, w):
        return (gx, gc, z ^ 1, w)

    def far_mate(gx, gc, z, w):
        return (gx, gc, z ^ 2, w)

    def cross_mate(gx, gc, z, w):
        return (gx, 1 - gc, z ^ 1, w)

    def wt_mate(gx, gc, z, w):
        return (gx, gc, z, 1 - w)

    def wt_x_mate(gx, gc, z, w):
        return (1 - gx, gc, z, 1 - w)

    def to_host(gx, gc, z, w):
        return (gx, z & 1, 2 * gc + (z >> 1), w)

    def to_home(gx, gc, z, w):
        return (gx, z >> 1, 2 * (z & 1) + gc, w)

    def hop1(gx, gc, z, w):
        if gc == 0:
            return (gx, 0, z - 1, w) if z > 0 else None
        return (gx, 1, z + 1, w) if z < 3 else None

    def hop2(gx, gc, z, w):
        if gc == 0:
            return (gx, 0, z - 1, w) if z in (1, 2) else None
        return (gx, 1, z + 1, w) if z in (1, 2) else None

    def hop3(gx, gc, z, w):
        if gc == 0:
            return (gx, 0, z ^ 1, w) if z < 2 else None
        return (gx, 1, z ^ 1, w) if z > 1 else None

    def lane_share(gx, gc, z, w):
        return (gx, 1 - gc, z, w) if gc == z >> 1 else None

    def sum_all(value):
        for axis in AXES:
            step = 1
            while step < sizes[axis]:

                def mate(gx, gc, z, w, axis=axis, step=step):
                    at = dict(gx=gx, gc=gc, far=z >> 1, near=z & 1, wt=w)
                    at[axis] ^= step
                    return (at["gx"], at["gc"], 2 * at["far"] + at["near"], at["wt"])

                value = value + send(value, mate)
                step *= 2
        return value

    def local(
        tokens, segments, w_qkv, w_proj, w_in, w_out, gain_attn, gain_mlp, query_scale, cotangent
    ):
        gx, gc, host, near, wt = (lax.axis_index(axis) for axis in AXES)
        z = 2 * host + near
        mine = 2 * near + gc
        parts = 4
        nh = H // parts
        groups = 2
        rows = tokens.shape[1]
        group_len = segments.shape[1]
        wrows = w_qkv.shape[0]
        lane = gc == host
        pair = sizes["wt"] == 2

        def after(value, *others):
            return lax.optimization_barrier((value,) + others)[0]

        own = tokens[0]
        got1 = send(own, hop1)
        own_share = send(own, lane_share)
        seg_mate = send(segments, core_mate)
        picked = pick(w_qkv, mine, parts, groups, nh)
        got1 = after(got1, picked)
        got2 = send(got1, hop2)
        got1_share = send(got1, lane_share)
        end = jnp.where(gc == 0, z == 0, z == 3)
        if pair:
            other_w = send(picked, wt_mate)
            *flat_w, wide_w = widen(picked, other_w, wt, groups, nh)
        else:
            flat_all = lax.all_gather(picked, "wt", axis=0, tiled=True)[:, : 3 * nh * HD]
            each = flat_all.shape[1] // groups
            flat_w = [
                jnp.pad(flat_all[:, g * each : (g + 1) * each], ((0, 0), (0, lanes_up(each) - each)))
                for g in range(groups)
            ]
            order = jnp.transpose(flat_all.reshape(D, groups, 3, nh // groups, HD), (0, 2, 1, 3, 4))
            wide_w = jnp.pad(
                order.reshape(D, 3 * nh, HD), ((0, 0), (0, 0), (0, LN - HD))
            ).reshape(D, -1)
        got3 = send(jnp.where(end, own, got2), hop3)
        got2_share = send(got2, lane_share)
        way = 1 - 2 * host
        last = jnp.where(host == 0, jnp.where(z == 0, 3, 0), jnp.where(z == 3, 0, 3))
        places = (z, z + way, z + 2 * way, last)

        half_rows = wrows // 2
        tail_own = jnp.stack([w_proj, w_in, w_out])
        half_w = lax.dynamic_slice_in_dim(tail_own, gc * half_rows, half_rows, 1)
        if pair:
            half_w = send(after(half_w, other_w), wt_mate)
        else:
            half_w = lax.all_gather(half_w, "wt", axis=0, tiled=False)

        dim_scale = scale_base / math.sqrt(HD) * jax.nn.softplus(query_scale)
        lane_scale = jnp.tile(jnp.pad(dim_scale * log2e, (0, LN - HD)), nh)[None]
        ones = jnp.tile(
            ((jnp.arange(LN) >= HD) & (jnp.arange(LN) < HD + 3)).astype(f32), 2 * nh
        )[None]
        seg_row = jnp.where(lane, segments, seg_mate)[0]
        fixed = (lane, mine, gain_attn[None], wide_w, lane_scale, ones, group_len)
        first = project(
            ((own, own_share), (got1, got1_share), (got2, got2_share)), places[:3], *fixed
        )
        got3 = after(got3, first[0])
        got3_share = send(got3, lane_share)
        all_normed, queries, keyval, inputs = project(
            ((got3, got3_share),), places[3:], *fixed, carried=first
        )
        grad_mlp = send(after(cotangent[0], got3), to_host)

        att, att_float, q_aug = attn_fwd(queries, keyval, seg_row, nh)

        trades = (core_mate, near_mate, cross_mate)
        att_pieces = [rows_at(att, (mine ^ j) * rows, rows) for j in range(parts)]
        att_pieces = [att_pieces[0]] + [send(att_pieces[j + 1], trades[j]) for j in range(3)]
        half_mate = send(after(half_w, att_pieces[1]), core_mate)
        if pair:
            weights = (tail_own, half_w, half_mate)
            starts = (wt * wrows, (1 - wt) * wrows + gc * half_rows, (1 - wt) * wrows + (1 - gc) * half_rows)
        else:
            one = gc == 0
            tail_w = jnp.stack(
                [jnp.where(one, half_w, half_mate), jnp.where(one, half_mate, half_w)], axis=1
            )
            weights = (jnp.transpose(tail_w, (2, 0, 1, 3, 4)).reshape(3, D, D),)
            starts = ()
        (
            layer_out,
            attended,
            normed_mlp,
            grad_hidden,
            active,
            grad_proj,
            grad_resid,
            *pieces,
            grad_gain_mlp,
        ) = tail(jnp.stack([mine, *starts]), att_pieces, inputs, grad_mlp, weights, gain_mlp[None])
        pieces = [pieces[0]] + [send(pieces[j + 1], trades[j]) for j in range(3)]

        lefts = (attended, normed_mlp, active)
        rights = (grad_proj, grad_hidden, grad_mlp)
        from_core = send(share(lefts, rights, 1 - gc), core_mate)
        layer_out = send(after(layer_out, pieces[2])[None], to_home)
        summed = keep(lefts, rights, after(from_core, *pieces[1:]), gc)
        kept = lax.all_to_all(summed, ("wt", "gx", "near"), 0, 0, tiled=True)

        scale_row = jnp.tile(dim_scale, nh // groups)[None]

        def backward(group, pieces):
            return attn_bwd(
                q_aug, keyval, pieces, att_float, seg_row, mine, scale_row, nh, group, groups
            )

        def gather(block):
            for mate in (far_mate, near_mate, x_mate):
                block = jnp.concatenate([block, send(block, mate)])
            return block, send(block, core_mate)

        def far_sum(pair):
            part, kept = pair
            return (kept.astype(f32) + send(part, far_mate).astype(f32)).astype(bf16)[None]

        def by_rows(grad):
            if pair:
                own, *rest = cross(all_normed, grad, jnp.stack([wt, gx]))
                got = [send(part, mate) for part, mate in zip(rest, (x_mate, wt_mate, wt_x_mate))]
                return [part.reshape(1, 2, part.shape[0] // 2, -1) for part in (own, *got)]
            part = trans_times(all_normed, grad).astype(bf16)
            sources = sizes["wt"] * 2
            got = lax.all_to_all(part, ("wt", "gx"), 0, 0, tiled=True)
            return [got.reshape(sources, 2, D // sources // 2, -1)]

        pieces[3] = after(pieces[3], summed)
        grad_a, lanes_a = backward(0, pieces)
        rows_a = by_rows(grad_a)
        pieces[3] = after(pieces[3], rows_a[0], layer_out)
        grad_b, lanes_b = backward(1, pieces)
        rows_a[0] = after(rows_a[0], grad_b)
        half_a = total(rows_a, host)
        grad_b = after(grad_b, half_a[0])
        rows_b = by_rows(grad_b)
        block_a = far_sum(half_a)
        block_b = far_sum(total(rows_b, host))
        sources = sizes["wt"] * 4
        block = far_sum(
            total([after(kept, rows_b[0]).reshape(sources, 2, D // sources // 2, -1)], host)
        )

        def shard_grad(shard):
            return sum(
                times_trans(rows_at(grad, shard * rows, rows), w)
                for grad, w in zip((after(grad_a, rows_b[0]), after(grad_b, rows_b[0])), flat_w)
            )

        to_core = jnp.stack([shard_grad(mine ^ 3), shard_grad(mine ^ 1)]).astype(bf16)
        from_core = send(to_core, core_mate).astype(f32)
        to_near = (shard_grad(mine ^ 2) + from_core[0]).astype(bf16)
        grad_normed = shard_grad(mine) + from_core[1] + send(to_near, near_mate).astype(f32)
        inputs = inputs.astype(f32)
        inverse_attn = rms_inverse(inputs)
        grad_gain_attn = jnp.sum(grad_normed * inputs * inverse_attn, axis=0)
        grad_tokens = send(
            (grad_resid + norm_back(inputs, inverse_attn, grad_normed * gain_attn)).astype(bf16)[None],
            to_home,
        )

        total_qkv = spread(
            [gather(block_a), gather(block_b)], jnp.stack([gx, host, near, gc]), 3 * nh // groups * HD
        )
        totals = place_tail(*gather(block), jnp.stack([gx, near, host, gc]))

        grad_query_scale = (
            (lanes_a + lanes_b)[0, :HD]
            / (dim_scale * log2e)
            * (scale_base / math.sqrt(HD))
            * jax.nn.sigmoid(query_scale)
        )
        small = jnp.concatenate(
            [grad_gain_attn, grad_gain_mlp[0], jnp.pad(grad_query_scale, (0, LN - HD))]
        ).reshape(-1, LN)
        small = sum_all(small).reshape(-1)
        return (
            layer_out,
            grad_tokens,
            total_qkv,
            *totals,
            small[:D],
            small[D : 2 * D],
            small[2 * D : 2 * D + HD],
        )

    return local


def solution(mesh):
    groups, parts, wt = (mesh.shape[axis] for axis in ("grp", "ctx", "wt"))
    inner = Mesh(mesh.devices.reshape(groups // 2, 2, parts // 2, 2, wt), AXES)
    sizes = dict(inner.shape)
    split = P(("gx", "gc", "wt"), ("far", "near"), None)
    weight = P("wt", None)
    return jax.shard_map(
        make_local(sizes),
        mesh=inner,
        in_specs=(
            split,
            P(("gx", "gc", "wt"), None),
            weight,
            weight,
            weight,
            weight,
            P(),
            P(),
            P(),
            split,
        ),
        out_specs=(split, split, weight, weight, weight, weight, P(), P(), P()),
        check_vma=False,
    )
```

```python
import functools
import math

import jax
import jax.numpy as jnp
from jax import lax
from jax.experimental import pallas as pl
from jax.experimental.pallas import tpu as pltpu
from jax.sharding import Mesh
from jax.sharding import PartitionSpec as P

D = 1280
H = 16
HD = 80
LN = 128
epsilon = 1e-06
scale_base = 1.442695041
log2e = 1.4426950408889634
NEG = -1e30
def cost(us):
    return pl.CostEstimate(flops=int(us * 1_000_000_000), transcendentals=0, bytes_accessed=1000)


CHEAP = cost(0.001)
f32 = jnp.float32
bf16 = jnp.bfloat16
AXES = ("gx", "gc", "far", "near", "wt")


def block_flags(seg_row, bq, bk):
    n = seg_row.shape[0]
    q = seg_row.reshape(n // bq, bq)
    k = seg_row.reshape(n // bk, bk)
    qf, ql = q[:, 0][:, None], q[:, -1][:, None]
    kf, kl = k[:, 0][None], k[:, -1][None]
    qs = jnp.arange(n // bq, dtype=jnp.int32)[:, None] * bq
    ks = jnp.arange(n // bk, dtype=jnp.int32)[None] * bk
    below = ks + bk - 1 <= qs
    skip = (ks > qs + bq - 1) | ((kf > 0) & (kl < qf))
    same = (qf == ql) & (kl == ql) & ((kf == kl) | ((kf == 0) & (kl == 1)))
    full = below & ((kl == 0) | same)
    return jnp.where(skip, 0, jnp.where(full, 1, 2)).astype(jnp.int32).reshape(-1)


def put_split(base, col, lanes):
    hi = col.astype(bf16).astype(f32)
    rest = col - hi
    mid = rest.astype(bf16).astype(f32)
    out = jnp.where(lanes == HD, hi, base)
    out = jnp.where(lanes == HD + 1, mid, out)
    return jnp.where(lanes == HD + 2, rest - mid, out).astype(bf16)


def fwd_kernel(flags, q_ref, kv, segc, segr, att, of, qaug, m_s, acc_s, *, nh, bq, bk, nk):
    qi = pl.program_id(0)
    count = (qi * bq + bq + bk - 1) // bk
    nt = (((1,), (1,)), ((), ()))
    acc_s[...] = jnp.zeros_like(acc_s)
    m_s[...] = jnp.zeros_like(m_s)

    def mask(ko):
        qpos = qi * bq + lax.broadcasted_iota(jnp.int32, (bq, bk), 0)
        kpos = ko + lax.broadcasted_iota(jnp.int32, (bq, bk), 1)
        ks = segr[:, pl.ds(ko, bk)]
        return (kpos <= qpos) & ((ks == 0) | (ks == segc[...]))

    def step(kb, masked):
        ko = pl.multiple_of(kb * bk, bk)
        if masked:
            allowed = mask(ko)
        for h in range(nh):
            k = kv[pl.ds(ko, bk), h * LN : (h + 1) * LN]
            v = kv[pl.ds(ko, bk), (nh + h) * LN : (nh + h + 1) * LN]
            s = lax.dot_general(q_ref[:, h * LN : (h + 1) * LN], k, nt, preferred_element_type=f32)
            p = jnp.exp2(s)
            if masked:
                p = jnp.where(allowed, p, 0.0)
            acc_s[h] += jnp.dot(p.astype(bf16), v, preferred_element_type=f32)

    def body(kb, carry):
        flag = flags[qi * nk + kb]

        @pl.when(flag == 1)
        def _():
            step(kb, False)

        @pl.when(flag == 2)
        def _():
            step(kb, True)

        return carry

    lax.fori_loop(0, count, body, 0)
    bad = jnp.zeros((bq, 1), f32)
    for h in range(nh):
        total = acc_s[h][:, HD : HD + 1]
        bad = jnp.maximum(bad, jnp.where((total > 2.0**-60) & (total < 2.0**60), 0.0, 1.0))

    @pl.when(jnp.max(bad) > 0.0)
    def _():
        def head(h, carry):
            kc = pl.ds(pl.multiple_of(h * LN, LN), LN)
            vc = pl.ds(pl.multiple_of((nh + h) * LN, LN), LN)
            m_s[h] = jnp.full((bq, LN), NEG, f32)
            acc_s[h] = jnp.zeros((bq, LN), f32)

            def inner(kb, carry):
                @pl.when(flags[qi * nk + kb] > 0)
                def _():
                    ko = pl.multiple_of(kb * bk, bk)
                    s = lax.dot_general(
                        q_ref[:, kc], kv[pl.ds(ko, bk), kc], nt, preferred_element_type=f32
                    )
                    s = jnp.where(mask(ko), s, NEG)
                    old = m_s[h]
                    new = jnp.maximum(old, jnp.max(s, axis=1, keepdims=True))
                    p = jnp.exp2(s - new[:, :1]).astype(bf16)
                    m_s[h] = new
                    acc_s[h] = acc_s[h] * jnp.exp2(old - new) + jnp.dot(
                        p, kv[pl.ds(ko, bk), vc], preferred_element_type=f32
                    )

                return carry

            lax.fori_loop(0, count, inner, 0)
            return carry

        lax.fori_loop(0, nh, head, 0)

    lanes = lax.broadcasted_iota(jnp.int32, (bq, LN), 1)
    outs = []
    for h in range(nh):
        acc = acc_s[h]
        total = acc[:, HD : HD + 1]
        out = acc * (1.0 / total)
        of[:, h * LN : (h + 1) * LN] = jnp.where(lanes < HD, out, 0.0)
        outs.append(out[:, :HD])
        lse = m_s[h][:, :1] + jnp.log2(total)
        qaug[:, h * LN : (h + 1) * LN] = put_split(
            q_ref[:, h * LN : (h + 1) * LN].astype(f32), -lse, lanes
        )
    att[...] = jnp.concatenate(outs, axis=1).astype(bf16)


def attn_fwd(q, kv, seg_row, nh, bq=512, bk=512):
    n = q.shape[0]
    w = nh * LN
    spec = pltpu.PrefetchScalarGridSpec(
        num_scalar_prefetch=1,
        grid=(n // bq,),
        in_specs=[
            pl.BlockSpec((bq, w), lambda i, f: (i, 0)),
            pl.BlockSpec((n, 2 * w), lambda i, f: (0, 0)),
            pl.BlockSpec((bq, 1), lambda i, f: (i, 0)),
            pl.BlockSpec((1, n), lambda i, f: (0, 0)),
        ],
        out_specs=[
            pl.BlockSpec((bq, nh * HD), lambda i, f: (i, 0)),
            pl.BlockSpec((bq, w), lambda i, f: (i, 0)),
            pl.BlockSpec((bq, w), lambda i, f: (i, 0)),
        ],
        scratch_shapes=[pltpu.VMEM((nh, bq, LN), f32), pltpu.VMEM((nh, bq, LN), f32)],
    )
    return pl.pallas_call(
        functools.partial(fwd_kernel, nh=nh, bq=bq, bk=bk, nk=n // bk),
        out_shape=[
            jax.ShapeDtypeStruct((n, nh * HD), bf16),
            jax.ShapeDtypeStruct((n, w), f32),
            jax.ShapeDtypeStruct((n, w), bf16),
        ],
        grid_spec=spec,
        compiler_params=pltpu.CompilerParams(vmem_limit_bytes=40 << 20),
        cost_estimate=cost(0.01),
        name="attn_fwd",
    )(block_flags(seg_row, bq, bk), q, kv, seg_row[:, None], seg_row[None])


def bwd_kernel(
    flags, mine, qa, kk, vv, do0, do1, do2, do3, of, segc, segr, scale, dqkv, gscale, doa_s, dq_s, dk_s, dv_s, *, first, nh, bq, bk, n
):
    nk = n // bk
    nq = n // bq
    kb = pl.program_id(0)
    part = n // 4
    step_rows = 256 if part % 256 == 0 else part
    lanes = lax.broadcasted_iota(jnp.int32, (step_rows, LN), 1)

    @pl.when(kb == 0)
    def _():
        dq_s[...] = jnp.zeros_like(dq_s)
        for j, piece in enumerate((do0, do1, do2, do3)):
            start = (mine[0] ^ j) * part
            for i in range(part // step_rows):
                d = piece[i * step_rows : (i + 1) * step_rows, :].astype(f32)
                r = pl.ds(pl.multiple_of(start + i * step_rows, step_rows), step_rows)
                for h in range(nh):
                    at = (first + h) * HD
                    dh = jnp.concatenate(
                        [d[:, at : at + HD], jnp.zeros((step_rows, LN - HD), f32)], axis=1
                    )
                    c = slice(h * LN, (h + 1) * LN)
                    delta = jnp.sum(dh * of[r, c], axis=1, keepdims=True)
                    doa_s[r, c] = put_split(dh, -delta, lanes)

    dk_s[...] = jnp.zeros_like(dk_s)
    dv_s[...] = jnp.zeros_like(dv_s)
    ko = kb * bk
    nt = (((1,), (1,)), ((), ()))
    tn = (((0,), (0,)), ((), ()))

    def step(qi, masked):
        qo = pl.multiple_of(qi * bq, bq)
        if masked:
            kpos = ko + lax.broadcasted_iota(jnp.int32, (bk, bq), 0)
            qpos = qo + lax.broadcasted_iota(jnp.int32, (bk, bq), 1)
            ks = segc[...]
            allowed = (kpos <= qpos) & ((ks == 0) | (ks == segr[:, pl.ds(qo, bq)]))
        for h in range(nh):
            c = slice(h * LN, (h + 1) * LN)
            q = qa[pl.ds(qo, bq), c]
            k = kk[:, c]
            d = doa_s[pl.ds(qo, bq), c]
            p = jnp.exp2(lax.dot_general(k, q, nt, preferred_element_type=f32))
            if masked:
                p = jnp.where(allowed, p, 0.0)
            ds = (p * lax.dot_general(vv[:, c], d, nt, preferred_element_type=f32)).astype(bf16)
            dv_s[h] += jnp.dot(p.astype(bf16), d, preferred_element_type=f32)
            dk_s[h] += jnp.dot(ds, q, preferred_element_type=f32)
            dq_s[h, pl.ds(qo, bq), :] += lax.dot_general(ds, k, tn, preferred_element_type=f32)

    def body(qi, carry):
        flag = flags[qi * nk + kb]

        @pl.when(flag == 1)
        def _():
            step(qi, False)

        @pl.when(flag == 2)
        def _():
            step(qi, True)

        return carry

    lax.fori_loop(ko // bq, nq, body, 0)
    r = pl.multiple_of(ko, bk)
    ln2 = math.log(2.0)
    gap = dqkv.shape[1] - 3 * nh * HD
    dqkv[pl.ds(r, bk), nh * HD :] = jnp.concatenate(
        [dk_s[h][:, :HD] * ln2 for h in range(nh)]
        + [dv_s[h][:, :HD] for h in range(nh)]
        + [jnp.zeros((bk, gap), f32)],
        axis=1,
    ).astype(bf16)

    @pl.when(kb == nk - 1)
    def _():
        total = jnp.zeros((1, LN), f32)
        for i in range(nq):
            rows = slice(i * bq, (i + 1) * bq)
            for h in range(nh):
                total = total + jnp.sum(
                    dq_s[h, rows, :] * qa[rows, h * LN : (h + 1) * LN].astype(f32), axis=0, keepdims=True
                )
            grads = jnp.concatenate([dq_s[h, rows, :][:, :HD] for h in range(nh)], axis=1)
            dqkv[rows, 0 : nh * HD] = (grads * scale[...]).astype(bf16)
        gscale[...] = jnp.broadcast_to(total, gscale.shape)


def attn_bwd(qa, kv, pieces, of, seg_row, mine, scale, heads, group, groups, bq=512, bk=512):
    n = qa.shape[0]
    nh = heads // groups
    w = nh * LN
    once = pl.Buffered(1)
    spec = pltpu.PrefetchScalarGridSpec(
        num_scalar_prefetch=2,
        grid=(n // bk,),
        in_specs=[
            pl.BlockSpec((n, w), lambda i, f, m: (0, group), pipeline_mode=once),
            pl.BlockSpec((bk, w), lambda i, f, m: (i, group)),
            pl.BlockSpec((bk, w), lambda i, f, m: (i, groups + group)),
        ]
        + [pl.BlockSpec((n // 4, heads * HD), lambda i, f, m: (0, 0), pipeline_mode=once)] * 4
        + [
            pl.BlockSpec((n, w), lambda i, f, m: (0, group), pipeline_mode=once),
            pl.BlockSpec((bk, 1), lambda i, f, m: (i, 0)),
            pl.BlockSpec((1, n), lambda i, f, m: (0, 0)),
            pl.BlockSpec((1, nh * HD), lambda i, f, m: (0, 0)),
        ],
        out_specs=[
            pl.BlockSpec((n, lanes_up(3 * nh * HD)), lambda i, f, m: (0, 0)),
            pl.BlockSpec((8, LN), lambda i, f, m: (0, 0)),
        ],
        scratch_shapes=[
            pltpu.VMEM((n, w), bf16),
            pltpu.VMEM((nh, n, LN), f32),
            pltpu.VMEM((nh, bk, LN), f32),
            pltpu.VMEM((nh, bk, LN), f32),
        ],
    )
    return pl.pallas_call(
        functools.partial(bwd_kernel, first=group * nh, nh=nh, bq=bq, bk=bk, n=n),
        out_shape=[
            jax.ShapeDtypeStruct((n, lanes_up(3 * nh * HD)), bf16),
            jax.ShapeDtypeStruct((8, LN), f32),
        ],
        grid_spec=spec,
        compiler_params=pltpu.CompilerParams(vmem_limit_bytes=48 << 20),
        cost_estimate=cost(0.01),
        name="attn_bwd",
    )(block_flags(seg_row, bq, bk), mine.reshape(1), qa, kv, kv, *pieces, of, seg_row[:, None], seg_row[None], scale)


def quarter_columns(place, parts, groups, nh):
    width = nh // groups * HD
    return [
        (t * D + place * nh * HD + g * width, width) for g in range(groups) for t in range(3)
    ]


def pick_kernel(mine, w_ref, out, *, parts, groups, nh):
    for i in range(parts):

        @pl.when(mine[0] == i)
        def _(i=i):
            cut = [w_ref[:, a : a + width] for a, width in quarter_columns(i, parts, groups, nh)]
            used = sum(x.shape[1] for x in cut)
            pad = jnp.zeros((cut[0].shape[0], out.shape[1] - used), out.dtype)
            out[...] = jnp.concatenate(cut + [pad], axis=1)


def lanes_up(n):
    return -(-n // LN) * LN


def pick(w, mine, parts, groups, nh):
    rows = w.shape[0]
    step = 160 if rows % 160 == 0 else rows
    return pl.pallas_call(
        functools.partial(pick_kernel, parts=parts, groups=groups, nh=nh),
        out_shape=jax.ShapeDtypeStruct((rows, lanes_up(3 * nh * HD)), w.dtype),
        grid_spec=pltpu.PrefetchScalarGridSpec(
            num_scalar_prefetch=1,
            grid=(rows // step,),
            in_specs=[pl.BlockSpec((step, 3 * D), lambda i, m: (i, 0))],
            out_specs=pl.BlockSpec((step, lanes_up(3 * nh * HD)), lambda i, m: (i, 0)),
        ),
        cost_estimate=cost(5),
        name="pick",
    )(mine.reshape(1), w)


def widen_kernel(own_first, a_ref, b_ref, *outs, groups, nh):
    flats, wide = outs[:-1], outs[-1]

    def put(ref):
        value = ref[...]
        each = 3 * nh * HD // groups
        gap = jnp.zeros((value.shape[0], lanes_up(each) - each), value.dtype)
        for g in range(groups):
            flats[g][...] = jnp.concatenate([value[:, g * each : (g + 1) * each], gap], axis=1)
        zero = jnp.zeros((value.shape[0], LN - HD), value.dtype)
        per = nh // groups
        spread = []
        for t in range(3):
            for h in range(nh):
                at = (h // per) * each + t * per * HD + (h % per) * HD
                spread += [value[:, at : at + HD], zero]
        wide[...] = jnp.concatenate(spread, axis=1)

    half = pl.program_id(0)

    @pl.when(half == 0)
    def _():
        put(a_ref)

    @pl.when(half == 1)
    def _():
        put(b_ref)


def widen(own, other, own_at, groups, nh):
    rows, width = own.shape
    step = 160
    n = rows // step
    at = lambda i, j, m: ((i ^ m[0]) * n + j, 0)
    each = lanes_up(3 * nh * HD // groups)
    return pl.pallas_call(
        functools.partial(widen_kernel, groups=groups, nh=nh),
        out_shape=[jax.ShapeDtypeStruct((2 * rows, each), own.dtype)] * groups
        + [jax.ShapeDtypeStruct((2 * rows, 3 * nh * LN), own.dtype)],
        grid_spec=pltpu.PrefetchScalarGridSpec(
            num_scalar_prefetch=1,
            grid=(2, n),
            in_specs=[
                pl.BlockSpec((step, width), lambda i, j, m: (j * (1 - i), 0)),
                pl.BlockSpec((step, width), lambda i, j, m: (j * i, 0)),
            ],
            out_specs=[pl.BlockSpec((step, each), at)] * groups + [pl.BlockSpec((step, 3 * nh * LN), at)],
        ),
        cost_estimate=cost(16),
        name="widen",
    )(own_at.reshape(1), own, other)


def project_kernel(info, *refs, count, width, fresh):
    pairs = refs[: 2 * count]
    gain, w, scale, ones = refs[2 * count : 2 * count + 4]
    normed_ref, q_ref, kv_ref, mine_ref = refs[-4:]
    j = pl.program_id(0)

    def work(x_ref):
        value = x_ref[...]
        x = value.astype(f32)
        inverse = lax.rsqrt(jnp.mean(x * x, axis=-1, keepdims=True) + epsilon)
        normed = (x * inverse * gain[...]).astype(bf16)
        normed_ref[...] = normed
        q_ref[...] = (
            jnp.dot(normed, w[:, :width], preferred_element_type=f32) * scale[...]
        ).astype(bf16)
        kv_ref[...] = (
            jnp.dot(normed, w[:, width:], preferred_element_type=f32) + ones[...]
        ).astype(bf16)

        @pl.when(info[count + 1] == info[j])
        def _():
            mine_ref[...] = value

    if not fresh:
        mine_ref[...] = refs[2 * count + 4][...]
    for i in range(count):
        for lane in range(2):

            @pl.when((j == i) & (info[count] == lane))
            def _(i=i, lane=lane):
                work(pairs[2 * i + 1 - lane])


def project(pairs, places, lane, mine, gain, w, scale, ones, group_len, carried=None):
    count = len(pairs)
    rows, d = pairs[0][0].shape
    width = scale.shape[1]
    full = lambda i, f: (0, 0)
    at = lambda i, f: (f[i], 0)
    once = pl.Buffered(1)
    info = jnp.stack(list(places) + [lane.astype(jnp.int32), mine])
    args = [x for pair in pairs for x in pair] + [gain, w, scale, ones]
    in_specs = [pl.BlockSpec((rows, d), full, pipeline_mode=once)] * (2 * count) + [
        pl.BlockSpec((1, d), full, pipeline_mode=once),
        pl.BlockSpec(w.shape, full, pipeline_mode=once),
        pl.BlockSpec((1, width), full, pipeline_mode=once),
        pl.BlockSpec((1, 2 * width), full, pipeline_mode=once),
    ]
    aliases = {}
    if carried is not None:
        args += [carried[3], *carried[:3]]
        in_specs += [pl.BlockSpec((rows, d), full, pipeline_mode=once)] + [pl.BlockSpec(memory_space=pl.ANY)] * 3
        base = 2 * count + 6
        aliases = {base: 0, base + 1: 1, base + 2: 2}
    return pl.pallas_call(
        functools.partial(project_kernel, count=count, width=width, fresh=carried is None),
        out_shape=[
            jax.ShapeDtypeStruct((group_len, d), bf16),
            jax.ShapeDtypeStruct((group_len, width), bf16),
            jax.ShapeDtypeStruct((group_len, 2 * width), bf16),
            jax.ShapeDtypeStruct((rows, d), bf16),
        ],
        grid_spec=pltpu.PrefetchScalarGridSpec(
            num_scalar_prefetch=1,
            grid=(count,),
            in_specs=in_specs,
            out_specs=[
                pl.BlockSpec((rows, d), at),
                pl.BlockSpec((rows, width), at),
                pl.BlockSpec((rows, 2 * width), at),
                pl.BlockSpec((rows, d), full),
            ],
        ),
        input_output_aliases=aliases,
        compiler_params=pltpu.CompilerParams(vmem_limit_bytes=48 << 20),
        cost_estimate=cost(10),
        name="project",
    )(info, *args)


def tail_body(at, p0, p1, p2, p3, x_ref, g_ref, w_s, gain, outs):
    lo_ref, att_ref, nm_ref, gh_ref, act_ref, gp_ref, gr_ref, c0, c1, c2, c3, gg_ref = outs
    mine = at[0]
    pieces = (p0, p1, p2, p3)
    cols = p0.shape[1]
    nt = (((1,), (1,)), ((), ()))
    for i in range(4):

        @pl.when(mine == i)
        def _(i=i):
            att_ref[...] = jnp.concatenate([pieces[i ^ k][...] for k in range(4)], axis=1)

    resid = x_ref[...].astype(f32) + jnp.dot(att_ref[...], w_s[0], preferred_element_type=f32)
    inverse = lax.rsqrt(jnp.mean(resid * resid, axis=-1, keepdims=True) + epsilon)
    normed = (resid * inverse * gain[...]).astype(bf16)
    nm_ref[...] = normed
    hidden = jnp.dot(normed, w_s[1], preferred_element_type=f32)
    sig = 1.0 / (1.0 + jnp.exp(-hidden))
    active = (hidden * sig).astype(bf16)
    act_ref[...] = active
    lo_ref[...] = (resid + jnp.dot(active, w_s[2], preferred_element_type=f32)).astype(bf16)
    grad_active = lax.dot_general(g_ref[...], w_s[2], nt, preferred_element_type=f32)
    grad_hidden = (grad_active * sig * (1.0 + hidden * (1.0 - sig))).astype(bf16)
    gh_ref[...] = grad_hidden
    grad_normed = lax.dot_general(grad_hidden, w_s[1], nt, preferred_element_type=f32)
    gg_ref[...] += jnp.sum(grad_normed * resid * inverse, axis=0, keepdims=True)
    scaled = grad_normed * gain[...]
    grad_resid = (
        g_ref[...].astype(f32)
        + inverse * scaled
        - resid * (inverse * inverse * inverse) * jnp.mean(scaled * resid, axis=-1, keepdims=True)
    )
    gr_ref[...] = grad_resid
    grad_proj = grad_resid.astype(bf16)
    gp_ref[...] = grad_proj
    grad_att = lax.dot_general(grad_proj, w_s[0], nt, preferred_element_type=f32).astype(bf16)
    for i in range(4):

        @pl.when(mine == i)
        def _(i=i):
            for j, out in enumerate((c0, c1, c2, c3)):
                out[...] = grad_att[:, (i ^ j) * cols : ((i ^ j) + 1) * cols]


def tail_kernel(at, p0, p1, p2, p3, x_ref, g_ref, own, half, other, gain, *refs, rows, hrows):
    w_s = refs[-1]
    outs = refs[:-1]

    @pl.when(pl.program_id(0) == 0)
    def _():
        outs[-1][...] = jnp.zeros_like(outs[-1])
        w_s[:, pl.ds(pl.multiple_of(at[1], 16), rows), :] = own[...]
        w_s[:, pl.ds(pl.multiple_of(at[2], 16), hrows), :] = half[...]
        w_s[:, pl.ds(pl.multiple_of(at[3], 16), hrows), :] = other[...]

    tail_body(at, p0, p1, p2, p3, x_ref, g_ref, w_s, gain, outs)


def whole_tail_kernel(at, p0, p1, p2, p3, x_ref, g_ref, w, gain, *outs):
    @pl.when(pl.program_id(0) == 0)
    def _():
        outs[-1][...] = jnp.zeros_like(outs[-1])

    tail_body(at, p0, p1, p2, p3, x_ref, g_ref, w, gain, outs)


def tail(at, pieces, x, g, weights, gain, tile=256):
    rows, d = x.shape
    cols = pieces[0].shape[1]
    row = lambda i, m: (i, 0)
    once = pl.Buffered(1)
    whole = lambda *shape: pl.BlockSpec(shape, lambda i, m: (0,) * len(shape), pipeline_mode=once)
    wide = pl.BlockSpec((tile, d), row)
    slim = pl.BlockSpec((tile, cols), row)
    if len(weights) == 3:
        body = functools.partial(tail_kernel, rows=weights[0].shape[1], hrows=weights[1].shape[1])
        scratch = [pltpu.VMEM((3, d, d), bf16)]
    else:
        body = whole_tail_kernel
        scratch = []
    return pl.pallas_call(
        body,
        out_shape=[jax.ShapeDtypeStruct((rows, d), bf16)] * 6
        + [jax.ShapeDtypeStruct((rows, d), f32)]
        + [jax.ShapeDtypeStruct((rows, cols), bf16)] * 4
        + [jax.ShapeDtypeStruct((1, d), f32)],
        grid_spec=pltpu.PrefetchScalarGridSpec(
            num_scalar_prefetch=1,
            grid=(rows // tile,),
            in_specs=[slim] * 4 + [wide] * 2 + [whole(*w.shape) for w in weights] + [whole(1, d)],
            out_specs=[wide] * 7 + [slim] * 4 + [pl.BlockSpec((1, d), lambda i, m: (0, 0))],
            scratch_shapes=scratch,
        ),
        compiler_params=pltpu.CompilerParams(vmem_limit_bytes=52 << 20),
        cost_estimate=cost(0.01),
        name="tail",
    )(at, *pieces, x, g, *weights, gain)


tn_dims = (((0,), (0,)), ((), ()))


def share_kernel(col, l0, l1, l2, r0, r1, r2, out):
    for i, (left, right) in enumerate(((l0, r0), (l1, r1), (l2, r2))):

        @pl.when(pl.program_id(0) == i)
        def _(left=left, right=right):
            out[...] = lax.dot_general(
                left[...], right[...], tn_dims, preferred_element_type=f32
            ).astype(bf16)


def share(lefts, rights, col):
    rows, d = lefts[0].shape
    w = d // 2
    once = pl.Buffered(1)
    return pl.pallas_call(
        share_kernel,
        out_shape=jax.ShapeDtypeStruct((d, 3 * w), bf16),
        grid_spec=pltpu.PrefetchScalarGridSpec(
            num_scalar_prefetch=1,
            grid=(3,),
            in_specs=[pl.BlockSpec((rows, d), lambda i, c: (0, 0), pipeline_mode=once)] * 3
            + [pl.BlockSpec((rows, w), lambda i, c: (0, c[0]), pipeline_mode=once)] * 3,
            out_specs=pl.BlockSpec((d, w), lambda i, c: (0, i)),
        ),
        compiler_params=pltpu.CompilerParams(vmem_limit_bytes=40 << 20),
        cost_estimate=cost(.01),
        name="share",
    )(col.reshape(1), *lefts, *rights)


def keep_kernel(col, l0, l1, l2, r0, r1, r2, got, out):
    for i, (left, right) in enumerate(((l0, r0), (l1, r1), (l2, r2))):

        @pl.when(pl.program_id(0) == i)
        def _(left=left, right=right):
            out[...] = (
                lax.dot_general(left[...], right[...], tn_dims, preferred_element_type=f32)
                + got[...].astype(f32)
            ).astype(bf16)


def keep(lefts, rights, got, col):
    rows, d = lefts[0].shape
    w = d // 2
    once = pl.Buffered(1)
    block = pl.BlockSpec((d, w), lambda i, c: (0, i))
    return pl.pallas_call(
        keep_kernel,
        out_shape=jax.ShapeDtypeStruct((d, 3 * w), bf16),
        grid_spec=pltpu.PrefetchScalarGridSpec(
            num_scalar_prefetch=1,
            grid=(3,),
            in_specs=[pl.BlockSpec((rows, d), lambda i, c: (0, 0), pipeline_mode=once)] * 3
            + [pl.BlockSpec((rows, w), lambda i, c: (0, c[0]), pipeline_mode=once)] * 3
            + [block],
            out_specs=block,
        ),
        compiler_params=pltpu.CompilerParams(vmem_limit_bytes=40 << 20),
        cost_estimate=cost(.01),
        name="keep",
    )(col.reshape(1), *lefts, *rights, got)


def total_kernel(*refs):
    acc = jnp.zeros(refs[-1].shape, f32)
    for ref in refs[:-1]:
        for i in range(ref.shape[0]):
            acc = acc + ref[i].astype(f32)
    refs[-1][...] = acc.astype(bf16)


def total(arrays):
    _, r, c = arrays[0].shape
    w = c
    for cut in (640, 256):
        if c % cut == 0:
            w = cut
            break
    return pl.pallas_call(
        total_kernel,
        out_shape=jax.ShapeDtypeStruct((r, c), bf16),
        grid_spec=pltpu.PrefetchScalarGridSpec(
            num_scalar_prefetch=0,
            grid=(c // w,),
            in_specs=[pl.BlockSpec((x.shape[0], r, w), lambda i: (0, 0, i)) for x in arrays],
            out_specs=pl.BlockSpec((r, w), lambda i: (0, i)),
        ),
        compiler_params=pltpu.CompilerParams(vmem_limit_bytes=40 << 20),
        cost_estimate=cost(10),
        name="total",
    )(*arrays)


def place_kernel(at, own_ref, mate_ref, o0, o1, o2):
    block = pl.program_id(0)
    slot = ((block // 2) ^ at[0]) * 2 + ((block % 2) ^ at[1])
    w = o0.shape[2] // 2

    def put(refs):
        for side, ref in enumerate(refs):
            part = ref[slot].astype(f32)
            for i, out in enumerate((o0, o1, o2)):
                out[0, :, side * w : (side + 1) * w] = part[:, i * w : (i + 1) * w]

    @pl.when(at[2] == 0)
    def _():
        put((own_ref, mate_ref))

    @pl.when(at[2] == 1)
    def _():
        put((mate_ref, own_ref))


def place_tail(own, mate, at):
    n, h, width = own.shape
    d = width // 3 * 2
    whole = pl.BlockSpec(own.shape, lambda i, m: (0, 0, 0), pipeline_mode=pl.Buffered(1))
    outs = pl.pallas_call(
        place_kernel,
        out_shape=[jax.ShapeDtypeStruct((n, h, d), f32)] * 3,
        grid_spec=pltpu.PrefetchScalarGridSpec(
            num_scalar_prefetch=1,
            grid=(n,),
            in_specs=[whole] * 2,
            out_specs=[pl.BlockSpec((1, h, d), lambda i, m: (i, 0, 0))] * 3,
        ),
        compiler_params=pltpu.CompilerParams(vmem_limit_bytes=40 << 20),
        cost_estimate=cost(.1),
        name="place_tail",
    )(at, own, mate)
    return [out.reshape(n * h, d) for out in outs]


def cross_kernel(at, x_ref, g_ref, *refs):
    s = refs[-1]
    s[...] = lax.dot_general(x_ref[...], g_ref[...], tn_dims, preferred_element_type=f32).astype(bf16)
    step = pl.program_id(0)
    half = s.shape[0] // 2
    for w in range(2):

        @pl.when(step == w)
        def _(w=w):
            for x in range(2):
                rows = pl.ds(pl.multiple_of((at[1] ^ x) * half, 16), half)
                refs[2 * w + x][...] = s[rows, :]


def cross(x, g, at):
    rows, d = x.shape
    w = d // 2
    block = pl.BlockSpec((w // 2, g.shape[1]), lambda i, m: (0, 0))
    return pl.pallas_call(
        cross_kernel,
        out_shape=[jax.ShapeDtypeStruct((w // 2, g.shape[1]), bf16)] * 4,
        grid_spec=pltpu.PrefetchScalarGridSpec(
            num_scalar_prefetch=1,
            grid=(2,),
            in_specs=[
                pl.BlockSpec((rows, w), lambda i, m: (0, m[0] ^ i)),
                pl.BlockSpec(g.shape, lambda i, m: (0, 0)),
            ],
            out_specs=[block] * 4,
            scratch_shapes=[pltpu.VMEM((w, g.shape[1]), bf16)],
        ),
        compiler_params=pltpu.CompilerParams(vmem_limit_bytes=40 << 20),
        cost_estimate=cost(0.1),
        name="cross",
    )(at, x, g)


def spread_kernel(at, *refs, groups, width):
    out = refs[-1]
    step = out.shape[1]
    slot = (pl.program_id(0) ^ at[0]) * 2
    rows = pl.ds(pl.multiple_of(pl.program_id(1) * step, step), step)

    def put(flip):
        cut = []
        for t in range(3):
            for n in range(2):
                for core in range(2):
                    for g in range(groups):
                        part = refs[2 * g + (core ^ flip)][slot + (n ^ at[1]), rows, :]
                        cut.append(part[:, t * width : (t + 1) * width])
        out[0] = jnp.concatenate(cut, axis=1).astype(f32)

    for flip in range(2):

        @pl.when(at[2] == flip)
        def _(flip=flip):
            put(flip)


def spread(arrays, at, used):
    flat = [x for pair in arrays for x in pair]
    _, rows, _ = flat[0].shape
    groups = len(arrays)
    width = 4 * groups * used
    cuts = 2 if rows % 32 == 0 else 1
    return pl.pallas_call(
        functools.partial(spread_kernel, groups=groups, width=used // 3),
        out_shape=jax.ShapeDtypeStruct((2, rows, width), f32),
        grid_spec=pltpu.PrefetchScalarGridSpec(
            num_scalar_prefetch=1,
            grid=(2, cuts),
            in_specs=[
                pl.BlockSpec(x.shape, lambda i, j, m: (0, 0, 0), pipeline_mode=pl.Buffered(1)) for x in flat
            ],
            out_specs=pl.BlockSpec((1, rows // cuts, width), lambda i, j, m: (i, j, 0)),
        ),
        compiler_params=pltpu.CompilerParams(vmem_limit_bytes=40 << 20),
        cost_estimate=cost(0.1),
        name="spread",
    )(at, *flat).reshape(2 * rows, width)


def rms_inverse(values):
    return lax.rsqrt(jnp.mean(values * values, axis=-1, keepdims=True) + epsilon)


def norm_back(values, inverse, grad_scaled):
    return inverse * grad_scaled - values * (inverse * inverse * inverse) * jnp.mean(
        grad_scaled * values, axis=-1, keepdims=True
    )


def dot(left, right):
    return jnp.dot(left, right, preferred_element_type=f32)


def times_trans(left, right):
    return lax.dot_general(left, right, (((1,), (1,)), ((), ())), preferred_element_type=f32)


def trans_times(left, right):
    return lax.dot_general(left, right, (((0,), (0,)), ((), ())), preferred_element_type=f32)


def rows_at(array, start, count):
    return lax.dynamic_slice_in_dim(array, start, count, 0)


def put_rows(array, rows, start):
    return lax.dynamic_update_slice_in_dim(array, rows, start, 0)


def make_local(sizes):
    def pairs(target):
        found = []
        for gx in range(sizes["gx"]):
            for gc in range(sizes["gc"]):
                for z in range(4):
                    for w in range(sizes["wt"]):
                        goal = target(gx, gc, z, w)
                        if goal is not None and goal != (gx, gc, z, w):
                            found.append((place(gx, gc, z, w), place(*goal)))
        return found

    def place(gx, gc, z, w):
        return ((gx * sizes["gc"] + gc) * 4 + z) * sizes["wt"] + w

    def send(value, target):
        return lax.ppermute(value, AXES, pairs(target))

    def move(value, target, still):
        return jnp.where(still, value, send(value, target))

    def core_mate(gx, gc, z, w):
        return (gx, 1 - gc, z, w)

    def x_mate(gx, gc, z, w):
        return (1 - gx, gc, z, w)

    def near_mate(gx, gc, z, w):
        return (gx, gc, z ^ 1, w)

    def far_mate(gx, gc, z, w):
        return (gx, gc, z ^ 2, w)

    def cross_mate(gx, gc, z, w):
        return (gx, 1 - gc, z ^ 1, w)

    def wt_mate(gx, gc, z, w):
        return (gx, gc, z, 1 - w)

    def wt_x_mate(gx, gc, z, w):
        return (1 - gx, gc, z, 1 - w)

    def to_host(gx, gc, z, w):
        return (gx, z & 1, 2 * gc + (z >> 1), w)

    def to_home(gx, gc, z, w):
        return (gx, z >> 1, 2 * (z & 1) + gc, w)

    def hop1(gx, gc, z, w):
        if gc == 0:
            return (gx, 0, z - 1, w) if z > 0 else None
        return (gx, 1, z + 1, w) if z < 3 else None

    def hop2(gx, gc, z, w):
        if gc == 0:
            return (gx, 0, z - 1, w) if z in (1, 2) else None
        return (gx, 1, z + 1, w) if z in (1, 2) else None

    def hop3(gx, gc, z, w):
        if gc == 0:
            return (gx, 0, z ^ 1, w) if z < 2 else None
        return (gx, 1, z ^ 1, w) if z > 1 else None

    def lane_share(gx, gc, z, w):
        return (gx, 1 - gc, z, w) if gc == z >> 1 else None

    def sum_all(value):
        for axis in AXES:
            step = 1
            while step < sizes[axis]:

                def mate(gx, gc, z, w, axis=axis, step=step):
                    at = dict(gx=gx, gc=gc, far=z >> 1, near=z & 1, wt=w)
                    at[axis] ^= step
                    return (at["gx"], at["gc"], 2 * at["far"] + at["near"], at["wt"])

                value = value + send(value, mate)
                step *= 2
        return value

    def local(
        tokens, segments, w_qkv, w_proj, w_in, w_out, gain_attn, gain_mlp, query_scale, cotangent
    ):
        gx, gc, host, near, wt = (lax.axis_index(axis) for axis in AXES)
        z = 2 * host + near
        mine = 2 * near + gc
        parts = 4
        nh = H // parts
        groups = 2
        rows = tokens.shape[1]
        group_len = segments.shape[1]
        wrows = w_qkv.shape[0]
        lane = gc == host
        pair = sizes["wt"] == 2

        def after(value, *others):
            return lax.optimization_barrier((value,) + others)[0]

        picked = pick(w_qkv, mine, parts, groups, nh)
        own = after(tokens[0], picked)
        got1 = send(own, hop1)
        own_share = send(own, lane_share)
        seg_mate = send(segments, core_mate)
        got2 = send(got1, hop2)
        got1_share = send(got1, lane_share)
        end = jnp.where(gc == 0, z == 0, z == 3)
        if pair:
            other_w = send(picked, wt_mate)
            *flat_w, wide_w = widen(picked, other_w, wt, groups, nh)
        else:
            flat_all = lax.all_gather(picked, "wt", axis=0, tiled=True)[:, : 3 * nh * HD]
            each = flat_all.shape[1] // groups
            flat_w = [
                jnp.pad(flat_all[:, g * each : (g + 1) * each], ((0, 0), (0, lanes_up(each) - each)))
                for g in range(groups)
            ]
            order = jnp.transpose(flat_all.reshape(D, groups, 3, nh // groups, HD), (0, 2, 1, 3, 4))
            wide_w = jnp.pad(
                order.reshape(D, 3 * nh, HD), ((0, 0), (0, 0), (0, LN - HD))
            ).reshape(D, -1)
        got3 = send(jnp.where(end, own, got2), hop3)
        got2_share = send(got2, lane_share)
        way = 1 - 2 * host
        last = jnp.where(host == 0, jnp.where(z == 0, 3, 0), jnp.where(z == 3, 0, 3))
        places = (z, z + way, z + 2 * way, last)

        half_rows = wrows // 2
        tail_own = jnp.stack([w_proj, w_in, w_out])
        half_w = lax.dynamic_slice_in_dim(tail_own, gc * half_rows, half_rows, 1)
        if pair:
            half_w = send(after(half_w, other_w), wt_mate)
        else:
            half_w = lax.all_gather(half_w, "wt", axis=0, tiled=False)

        dim_scale = scale_base / math.sqrt(HD) * jax.nn.softplus(query_scale)
        lane_scale = jnp.tile(jnp.pad(dim_scale * log2e, (0, LN - HD)), nh)[None]
        ones = jnp.tile(
            ((jnp.arange(LN) >= HD) & (jnp.arange(LN) < HD + 3)).astype(f32), 2 * nh
        )[None]
        seg_row = jnp.where(lane, segments, seg_mate)[0]
        fixed = (lane, mine, gain_attn[None], wide_w, lane_scale, ones, group_len)
        carried = project(((own, own_share), (got1, got1_share)), places[:2], *fixed)
        got2_share = after(got2_share, carried[0])
        got3_share = send(after(got3, carried[0]), lane_share)
        carried = project(((got2, got2_share),), places[2:3], *fixed, carried=carried)
        all_normed, queries, keyval, inputs = project(
            ((got3, after(got3_share, carried[0])),), places[3:], *fixed, carried=carried
        )
        still = lane & end
        grad_mlp = move(after(cotangent[0], got3), to_host, still)

        att, att_float, q_aug = attn_fwd(queries, keyval, seg_row, nh)
        att = after(att, grad_mlp)

        trades = (core_mate, near_mate, cross_mate)
        att_pieces = [rows_at(att, (mine ^ j) * rows, rows) for j in range(parts)]
        att_pieces = [att_pieces[0]] + [send(att_pieces[j + 1], trades[j]) for j in range(3)]
        half_mate = send(after(half_w, att_pieces[1]), core_mate)
        if pair:
            weights = (tail_own, half_w, half_mate)
            starts = (wt * wrows, (1 - wt) * wrows + gc * half_rows, (1 - wt) * wrows + (1 - gc) * half_rows)
        else:
            one = gc == 0
            tail_w = jnp.stack(
                [jnp.where(one, half_w, half_mate), jnp.where(one, half_mate, half_w)], axis=1
            )
            weights = (jnp.transpose(tail_w, (2, 0, 1, 3, 4)).reshape(3, D, D),)
            starts = ()
        (
            layer_out,
            attended,
            normed_mlp,
            grad_hidden,
            active,
            grad_proj,
            grad_resid,
            *pieces,
            grad_gain_mlp,
        ) = tail(jnp.stack([mine, *starts]), att_pieces, inputs, grad_mlp, weights, gain_mlp[None])
        pieces = [pieces[0]] + [send(pieces[j + 1], trades[j]) for j in range(3)]

        lefts = (after(attended, pieces[1]), normed_mlp, active)
        rights = (grad_proj, grad_hidden, grad_mlp)
        from_core = send(share(lefts, rights, 1 - gc), core_mate)
        home_out = send(after(layer_out, pieces[2]), to_home)
        summed = keep(lefts, rights, after(from_core, *pieces[1:]), gc)
        kept = lax.all_to_all(summed, ("wt", "gx", "near"), 0, 0, tiled=True)

        scale_row = jnp.tile(dim_scale, nh // groups)[None]

        def backward(group, pieces):
            return attn_bwd(
                q_aug, keyval, pieces, att_float, seg_row, mine, scale_row, nh, group, groups
            )

        def gather(block):
            for mate in (near_mate, x_mate):
                block = jnp.concatenate([block, send(block, mate)])
            return block, send(block, core_mate)

        def far_sum(part):
            return (part.astype(f32) + send(part, far_mate).astype(f32)).astype(bf16)[None]

        def by_rows(grad):
            if pair:
                own, *rest = cross(all_normed, grad, jnp.stack([wt, gx]))
                got = [send(part, mate) for part, mate in zip(rest, (x_mate, wt_mate, wt_x_mate))]
                return [part[None] for part in (own, *got)]
            part = trans_times(all_normed, grad).astype(bf16)
            sources = sizes["wt"] * 2
            got = lax.all_to_all(part, ("wt", "gx"), 0, 0, tiled=True)
            return [got.reshape(sources, D // sources, -1)]

        pieces[3] = after(pieces[3], summed)
        grad_a, lanes_a = backward(0, pieces)
        rows_a = by_rows(grad_a)
        pieces[3] = after(pieces[3], rows_a[0])
        grad_b, lanes_b = backward(1, pieces)
        rows_a[0] = after(rows_a[0], grad_b)
        sum_a = total(rows_a)
        grad_b = after(grad_b, sum_a)
        rows_b = by_rows(grad_b)
        layer_out = jnp.where(still, after(layer_out, rows_b[0]), home_out)
        block_a = far_sum(sum_a)
        sources = sizes["wt"] * 4
        tail_sum = total([after(kept, rows_b[0], layer_out).reshape(sources, D // sources, -1)])
        block = far_sum(tail_sum)
        rows_b[0] = after(rows_b[0], block_a)
        sum_b = total(rows_b)
        block_b = far_sum(sum_b)

        def shard_grad(shard, *others):
            return sum(
                times_trans(rows_at(after(grad, *others), shard * rows, rows), w)
                for grad, w in zip((grad_a, grad_b), flat_w)
            )

        to_core = jnp.stack(
            [shard_grad(mine ^ 3, tail_sum), shard_grad(mine ^ 1, tail_sum)]
        ).astype(bf16)
        from_core = send(to_core, core_mate).astype(f32)
        to_near = (shard_grad(mine ^ 2, sum_b) + from_core[0]).astype(bf16)
        grad_normed = shard_grad(mine, sum_b) + from_core[1] + send(to_near, near_mate).astype(f32)
        inputs = inputs.astype(f32)
        inverse_attn = rms_inverse(inputs)
        grad_gain_attn = jnp.sum(grad_normed * inputs * inverse_attn, axis=0)
        grad_tokens = move(
            (grad_resid + norm_back(inputs, inverse_attn, grad_normed * gain_attn)).astype(bf16),
            to_home,
            still,
        )

        total_qkv = spread(
            [gather(block_a), gather(block_b)], jnp.stack([gx, near, gc]), 3 * nh // groups * HD
        )
        totals = place_tail(*gather(block), jnp.stack([gx, near, gc]))

        grad_query_scale = (
            (lanes_a + lanes_b)[0, :HD]
            / (dim_scale * log2e)
            * (scale_base / math.sqrt(HD))
            * jax.nn.sigmoid(query_scale)
        )
        small = jnp.concatenate(
            [grad_gain_attn, grad_gain_mlp[0], jnp.pad(grad_query_scale, (0, LN - HD))]
        ).reshape(-1, LN)
        small = sum_all(small).reshape(-1)
        return (
            layer_out[None],
            grad_tokens[None],
            total_qkv,
            *totals,
            small[:D],
            small[D : 2 * D],
            small[2 * D : 2 * D + HD],
        )

    return local


def solution(mesh):
    groups, parts, wt = (mesh.shape[axis] for axis in ("grp", "ctx", "wt"))
    inner = Mesh(mesh.devices.reshape(groups // 2, 2, parts // 2, 2, wt), AXES)
    sizes = dict(inner.shape)
    split = P(("gx", "gc", "wt"), ("far", "near"), None)
    weight = P("wt", None)
    return jax.shard_map(
        make_local(sizes),
        mesh=inner,
        in_specs=(
            split,
            P(("gx", "gc", "wt"), None),
            weight,
            weight,
            weight,
            weight,
            P(),
            P(),
            P(),
            split,
        ),
        out_specs=(split, split, weight, weight, weight, weight, P(), P(), P()),
        check_vma=False,
    )
```

```python
import functools
import math

import jax
import jax.numpy as jnp
from jax import lax
from jax.experimental import pallas as pl
from jax.experimental.pallas import tpu as pltpu
from jax.sharding import Mesh
from jax.sharding import PartitionSpec as P

D = 1280
H = 16
HD = 80
LN = 128
epsilon = 1e-06
scale_base = 1.442695041
log2e = 1.4426950408889634
NEG = -1e30
def cost(us):
    return pl.CostEstimate(flops=int(us * 1_000_000_000), transcendentals=0, bytes_accessed=1000)


CHEAP = cost(0.001)
f32 = jnp.float32
bf16 = jnp.bfloat16
AXES = ("gx", "gc", "far", "near", "wt")


def hbm(x):
    return pltpu.with_memory_space_constraint(x, pltpu.HBM)


def block_flags(seg_row, bq, bk):
    n = seg_row.shape[0]
    q = seg_row.reshape(n // bq, bq)
    k = seg_row.reshape(n // bk, bk)
    qf, ql = q[:, 0][:, None], q[:, -1][:, None]
    kf, kl = k[:, 0][None], k[:, -1][None]
    qs = jnp.arange(n // bq, dtype=jnp.int32)[:, None] * bq
    ks = jnp.arange(n // bk, dtype=jnp.int32)[None] * bk
    below = ks + bk - 1 <= qs
    skip = (ks > qs + bq - 1) | ((kf > 0) & (kl < qf))
    same = (qf == ql) & (kl == ql) & ((kf == kl) | ((kf == 0) & (kl == 1)))
    full = below & ((kl == 0) | same)
    return jnp.where(skip, 0, jnp.where(full, 1, 2)).astype(jnp.int32).reshape(-1)


def put_split(base, col, lanes):
    hi = col.astype(bf16).astype(f32)
    rest = col - hi
    mid = rest.astype(bf16).astype(f32)
    out = jnp.where(lanes == HD, hi, base)
    out = jnp.where(lanes == HD + 1, mid, out)
    return jnp.where(lanes == HD + 2, rest - mid, out).astype(bf16)


def fwd_kernel(flags, q_ref, kv, segc, segr, att, of, qaug, m_s, acc_s, *, nh, bq, bk, nk):
    qi = pl.program_id(0)
    count = (qi * bq + bq + bk - 1) // bk
    nt = (((1,), (1,)), ((), ()))
    acc_s[...] = jnp.zeros_like(acc_s)
    m_s[...] = jnp.zeros_like(m_s)

    def mask(ko):
        qpos = qi * bq + lax.broadcasted_iota(jnp.int32, (bq, bk), 0)
        kpos = ko + lax.broadcasted_iota(jnp.int32, (bq, bk), 1)
        ks = segr[:, pl.ds(ko, bk)]
        return (kpos <= qpos) & ((ks == 0) | (ks == segc[...]))

    def step(kb, masked):
        ko = pl.multiple_of(kb * bk, bk)
        if masked:
            allowed = mask(ko)
        for h in range(nh):
            k = kv[pl.ds(ko, bk), h * LN : (h + 1) * LN]
            v = kv[pl.ds(ko, bk), (nh + h) * LN : (nh + h + 1) * LN]
            s = lax.dot_general(q_ref[:, h * LN : (h + 1) * LN], k, nt, preferred_element_type=f32)
            p = jnp.exp2(s)
            if masked:
                p = jnp.where(allowed, p, 0.0)
            acc_s[h] += jnp.dot(p.astype(bf16), v, preferred_element_type=f32)

    def body(kb, carry):
        flag = flags[qi * nk + kb]

        @pl.when(flag == 1)
        def _():
            step(kb, False)

        @pl.when(flag == 2)
        def _():
            step(kb, True)

        return carry

    lax.fori_loop(0, count, body, 0)
    bad = jnp.zeros((bq, 1), f32)
    for h in range(nh):
        total = acc_s[h][:, HD : HD + 1]
        bad = jnp.maximum(bad, jnp.where((total > 2.0**-60) & (total < 2.0**60), 0.0, 1.0))

    @pl.when(jnp.max(bad) > 0.0)
    def _():
        def head(h, carry):
            kc = pl.ds(pl.multiple_of(h * LN, LN), LN)
            vc = pl.ds(pl.multiple_of((nh + h) * LN, LN), LN)
            m_s[h] = jnp.full((bq, LN), NEG, f32)
            acc_s[h] = jnp.zeros((bq, LN), f32)

            def inner(kb, carry):
                @pl.when(flags[qi * nk + kb] > 0)
                def _():
                    ko = pl.multiple_of(kb * bk, bk)
                    s = lax.dot_general(
                        q_ref[:, kc], kv[pl.ds(ko, bk), kc], nt, preferred_element_type=f32
                    )
                    s = jnp.where(mask(ko), s, NEG)
                    old = m_s[h]
                    new = jnp.maximum(old, jnp.max(s, axis=1, keepdims=True))
                    p = jnp.exp2(s - new[:, :1]).astype(bf16)
                    m_s[h] = new
                    acc_s[h] = acc_s[h] * jnp.exp2(old - new) + jnp.dot(
                        p, kv[pl.ds(ko, bk), vc], preferred_element_type=f32
                    )

                return carry

            lax.fori_loop(0, count, inner, 0)
            return carry

        lax.fori_loop(0, nh, head, 0)

    lanes = lax.broadcasted_iota(jnp.int32, (bq, LN), 1)
    outs = []
    for h in range(nh):
        acc = acc_s[h]
        total = acc[:, HD : HD + 1]
        out = acc * (1.0 / total)
        of[:, h * LN : (h + 1) * LN] = jnp.where(lanes < HD, out, 0.0)
        outs.append(out[:, :HD])
        lse = m_s[h][:, :1] + jnp.log2(total)
        qaug[:, h * LN : (h + 1) * LN] = put_split(
            q_ref[:, h * LN : (h + 1) * LN].astype(f32), -lse, lanes
        )
    att[...] = jnp.concatenate(outs, axis=1).astype(bf16)


def attn_fwd(q, kv, seg_row, nh, bq=512, bk=512):
    n = q.shape[0]
    w = nh * LN
    spec = pltpu.PrefetchScalarGridSpec(
        num_scalar_prefetch=1,
        grid=(n // bq,),
        in_specs=[
            pl.BlockSpec((bq, w), lambda i, f: (i, 0)),
            pl.BlockSpec((n, 2 * w), lambda i, f: (0, 0)),
            pl.BlockSpec((bq, 1), lambda i, f: (i, 0)),
            pl.BlockSpec((1, n), lambda i, f: (0, 0)),
        ],
        out_specs=[
            pl.BlockSpec((bq, nh * HD), lambda i, f: (i, 0)),
            pl.BlockSpec((bq, w), lambda i, f: (i, 0)),
            pl.BlockSpec((bq, w), lambda i, f: (i, 0)),
        ],
        scratch_shapes=[pltpu.VMEM((nh, bq, LN), f32), pltpu.VMEM((nh, bq, LN), f32)],
    )
    return pl.pallas_call(
        functools.partial(fwd_kernel, nh=nh, bq=bq, bk=bk, nk=n // bk),
        out_shape=[
            pltpu.HBM((n, nh * HD), bf16),
            pltpu.HBM((n, w), f32),
            pltpu.HBM((n, w), bf16),
        ],
        grid_spec=spec,
        compiler_params=pltpu.CompilerParams(vmem_limit_bytes=40 << 20),
        cost_estimate=cost(0.01),
        name="attn_fwd",
    )(block_flags(seg_row, bq, bk), hbm(q), hbm(kv), seg_row[:, None], seg_row[None])


def bwd_kernel(
    flags, qa, kk, vv, doa_s, segc, segr, scale, dqkv, gscale, dq_s, dk_s, dv_s, *, nh, bq, bk, n
):
    nk = n // bk
    nq = n // bq
    kb = pl.program_id(0)

    @pl.when(kb == 0)
    def _():
        dq_s[...] = jnp.zeros_like(dq_s)

    dk_s[...] = jnp.zeros_like(dk_s)
    dv_s[...] = jnp.zeros_like(dv_s)
    ko = kb * bk
    nt = (((1,), (1,)), ((), ()))
    tn = (((0,), (0,)), ((), ()))

    def step(qi, masked):
        qo = pl.multiple_of(qi * bq, bq)
        if masked:
            kpos = ko + lax.broadcasted_iota(jnp.int32, (bk, bq), 0)
            qpos = qo + lax.broadcasted_iota(jnp.int32, (bk, bq), 1)
            ks = segc[...]
            allowed = (kpos <= qpos) & ((ks == 0) | (ks == segr[:, pl.ds(qo, bq)]))
        for h in range(nh):
            c = slice(h * LN, (h + 1) * LN)
            q = qa[pl.ds(qo, bq), c]
            k = kk[:, c]
            d = doa_s[pl.ds(qo, bq), c]
            p = jnp.exp2(lax.dot_general(k, q, nt, preferred_element_type=f32))
            if masked:
                p = jnp.where(allowed, p, 0.0)
            ds = (p * lax.dot_general(vv[:, c], d, nt, preferred_element_type=f32)).astype(bf16)
            dv_s[h] += jnp.dot(p.astype(bf16), d, preferred_element_type=f32)
            dk_s[h] += jnp.dot(ds, q, preferred_element_type=f32)
            dq_s[h, pl.ds(qo, bq), :] += lax.dot_general(ds, k, tn, preferred_element_type=f32)

    def body(qi, carry):
        flag = flags[qi * nk + kb]

        @pl.when(flag == 1)
        def _():
            step(qi, False)

        @pl.when(flag == 2)
        def _():
            step(qi, True)

        return carry

    lax.fori_loop(ko // bq, nq, body, 0)
    r = pl.multiple_of(ko, bk)
    ln2 = math.log(2.0)
    gap = dqkv.shape[1] - 3 * nh * HD
    dqkv[pl.ds(r, bk), nh * HD :] = jnp.concatenate(
        [dk_s[h][:, :HD] * ln2 for h in range(nh)]
        + [dv_s[h][:, :HD] for h in range(nh)]
        + [jnp.zeros((bk, gap), f32)],
        axis=1,
    ).astype(bf16)

    @pl.when(kb == nk - 1)
    def _():
        total = jnp.zeros((1, LN), f32)
        for i in range(nq):
            rows = slice(i * bq, (i + 1) * bq)
            for h in range(nh):
                total = total + jnp.sum(
                    dq_s[h, rows, :] * qa[rows, h * LN : (h + 1) * LN].astype(f32), axis=0, keepdims=True
                )
            grads = jnp.concatenate([dq_s[h, rows, :][:, :HD] for h in range(nh)], axis=1)
            dqkv[rows, 0 : nh * HD] = (grads * scale[...]).astype(bf16)
        gscale[...] = jnp.broadcast_to(total, gscale.shape)


def prep_kernel(mine, do0, do1, do2, do3, of, out, *, nh):
    tile = of.shape[0]
    lanes = lax.broadcasted_iota(jnp.int32, (tile, LN), 1)
    for j, piece in enumerate((do0, do1, do2, do3)):

        @pl.when(pl.program_id(0) == j)
        def _(piece=piece):
            d = piece[...].astype(f32)
            for h in range(nh):
                dh = jnp.concatenate(
                    [d[:, h * HD : (h + 1) * HD], jnp.zeros((tile, LN - HD), f32)], axis=1
                )
                c = slice(h * LN, (h + 1) * LN)
                delta = jnp.sum(dh * of[:, c], axis=1, keepdims=True)
                out[:, c] = put_split(dh, -delta, lanes)


def prep(pieces, of, mine, nh, tile=256):
    n, w = of.shape
    per = n // 4 // tile
    at = lambda j, i, m: ((m[0] ^ j) * per + i, 0)
    return pl.pallas_call(
        functools.partial(prep_kernel, nh=nh),
        out_shape=pltpu.HBM((n, w), bf16),
        grid_spec=pltpu.PrefetchScalarGridSpec(
            num_scalar_prefetch=1,
            grid=(4, per),
            in_specs=[
                pl.BlockSpec(
                    (tile, nh * HD),
                    lambda j, i, m, k=k: (jnp.where(j == k, i, jnp.where(j > k, per - 1, 0)), 0),
                )
                for k in range(4)
            ]
            + [pl.BlockSpec((tile, w), at)],
            out_specs=pl.BlockSpec((tile, w), at),
        ),
        compiler_params=pltpu.CompilerParams(vmem_limit_bytes=24 << 20),
        cost_estimate=cost(1000),
        name="prep",
    )(mine.reshape(1), *pieces, hbm(of))


def attn_bwd(qa, kv, doa, seg_row, scale, heads, group, groups, bq=512, bk=512):
    n = qa.shape[0]
    nh = heads // groups
    w = nh * LN
    once = pl.Buffered(1)
    spec = pltpu.PrefetchScalarGridSpec(
        num_scalar_prefetch=1,
        grid=(n // bk,),
        in_specs=[
            pl.BlockSpec((n, w), lambda i, f: (0, group), pipeline_mode=once),
            pl.BlockSpec((bk, w), lambda i, f: (i, group)),
            pl.BlockSpec((bk, w), lambda i, f: (i, groups + group)),
            pl.BlockSpec((n, w), lambda i, f: (0, group), pipeline_mode=once),
            pl.BlockSpec((bk, 1), lambda i, f: (i, 0)),
            pl.BlockSpec((1, n), lambda i, f: (0, 0)),
            pl.BlockSpec((1, nh * HD), lambda i, f: (0, 0)),
        ],
        out_specs=[
            pl.BlockSpec((n, lanes_up(3 * nh * HD)), lambda i, f: (0, 0)),
            pl.BlockSpec((8, LN), lambda i, f: (0, 0)),
        ],
        scratch_shapes=[
            pltpu.VMEM((nh, n, LN), f32),
            pltpu.VMEM((nh, bk, LN), f32),
            pltpu.VMEM((nh, bk, LN), f32),
        ],
    )
    return pl.pallas_call(
        functools.partial(bwd_kernel, nh=nh, bq=bq, bk=bk, n=n),
        out_shape=[
            pltpu.HBM((n, lanes_up(3 * nh * HD)), bf16),
            pltpu.HBM((8, LN), f32),
        ],
        grid_spec=spec,
        compiler_params=pltpu.CompilerParams(vmem_limit_bytes=48 << 20),
        cost_estimate=cost(0.01),
        name="attn_bwd",
    )(block_flags(seg_row, bq, bk), hbm(qa), hbm(kv), hbm(kv), hbm(doa), seg_row[:, None], seg_row[None], scale)


def quarter_columns(place, parts, groups, nh):
    width = nh // groups * HD
    return [
        (t * D + place * nh * HD + g * width, width) for g in range(groups) for t in range(3)
    ]


def pick_kernel(mine, w_ref, out, *, parts, groups, nh):
    for i in range(parts):

        @pl.when(mine[0] == i)
        def _(i=i):
            cut = [w_ref[:, a : a + width] for a, width in quarter_columns(i, parts, groups, nh)]
            used = sum(x.shape[1] for x in cut)
            pad = jnp.zeros((cut[0].shape[0], out.shape[1] - used), out.dtype)
            out[...] = jnp.concatenate(cut + [pad], axis=1)


def lanes_up(n):
    return -(-n // LN) * LN


def pick(w, mine, parts, groups, nh):
    rows = w.shape[0]
    step = 160 if rows % 160 == 0 else rows
    return pl.pallas_call(
        functools.partial(pick_kernel, parts=parts, groups=groups, nh=nh),
        out_shape=pltpu.HBM((rows, lanes_up(3 * nh * HD)), w.dtype),
        grid_spec=pltpu.PrefetchScalarGridSpec(
            num_scalar_prefetch=1,
            grid=(rows // step,),
            in_specs=[pl.BlockSpec((step, 3 * D), lambda i, m: (i, 0))],
            out_specs=pl.BlockSpec((step, lanes_up(3 * nh * HD)), lambda i, m: (i, 0)),
        ),
        cost_estimate=cost(5),
        name="pick",
    )(mine.reshape(1), hbm(w))


def stretch_kernel(x_ref, out, *, groups, nh):
    value = x_ref[...]
    each = 3 * nh * HD // groups
    zero = jnp.zeros((value.shape[0], LN - HD), value.dtype)
    per = nh // groups
    wide = []
    for t in range(3):
        for h in range(nh):
            at = (h // per) * each + t * per * HD + (h % per) * HD
            wide += [value[:, at : at + HD], zero]
    out[...] = jnp.concatenate(wide, axis=1)


def stretch(x, groups, nh, us):
    rows, width = x.shape
    step = 160
    return pl.pallas_call(
        functools.partial(stretch_kernel, groups=groups, nh=nh),
        out_shape=pltpu.HBM((rows, 3 * nh * LN), x.dtype),
        grid=(rows // step,),
        in_specs=[pl.BlockSpec((step, width), lambda i: (i, 0))],
        out_specs=pl.BlockSpec((step, 3 * nh * LN), lambda i: (i, 0)),
        cost_estimate=cost(us),
        name="stretch",
    )(hbm(x))


def order_kernel(own_first, a_ref, b_ref, *outs, each):
    def put(ref):
        value = ref[...]
        for g, out in enumerate(outs):
            gap = jnp.zeros((value.shape[0], out.shape[1] - each), value.dtype)
            out[...] = jnp.concatenate([value[:, g * each : (g + 1) * each], gap], axis=1)

    half = pl.program_id(0)

    @pl.when(half == 0)
    def _():
        put(a_ref)

    @pl.when(half == 1)
    def _():
        put(b_ref)


def order(own, other, own_at, groups, nh):
    rows, width = own.shape
    step = 320
    n = rows // step
    at = lambda i, j, m: ((i ^ m[0]) * n + j, 0)
    each = 3 * nh * HD // groups
    return pl.pallas_call(
        functools.partial(order_kernel, each=each),
        out_shape=[pltpu.HBM((2 * rows, lanes_up(each)), own.dtype)] * groups,
        grid_spec=pltpu.PrefetchScalarGridSpec(
            num_scalar_prefetch=1,
            grid=(2, n),
            in_specs=[
                pl.BlockSpec((step, width), lambda i, j, m: (j * (1 - i), 0)),
                pl.BlockSpec((step, width), lambda i, j, m: (j * i, 0)),
            ],
            out_specs=[pl.BlockSpec((step, lanes_up(each)), at)] * groups,
        ),
        cost_estimate=cost(3),
        name="order",
    )(own_at.reshape(1), hbm(own), hbm(other))


def project_kernel(info, *refs, count, halves, width, fresh):
    pairs = refs[: 2 * count]
    gain = refs[2 * count]
    weights = refs[2 * count + 1 : 2 * count + 1 + halves]
    scale, ones = refs[2 * count + 1 + halves : 2 * count + 3 + halves]
    normed_ref, q_ref, kv_ref, mine_ref, w = refs[-5:]
    j, tile = pl.program_id(0), pl.program_id(1)
    step = normed_ref.shape[0]

    @pl.when((j == 0) & (tile == 0))
    def _():
        for i, ref in enumerate(weights):
            h = ref.shape[0]
            start = (info[count + 2] ^ i) * h if halves == 2 else 0
            w[pl.ds(pl.multiple_of(start, 16), h), :] = ref[...]
        if not fresh:
            mine_ref[...] = refs[2 * count + 3 + halves][...]

    def work(x_ref):
        value = x_ref[...]
        x = value.astype(f32)
        inverse = lax.rsqrt(jnp.mean(x * x, axis=-1, keepdims=True) + epsilon)
        normed = (x * inverse * gain[...]).astype(bf16)
        normed_ref[...] = normed
        q_ref[...] = (
            jnp.dot(normed, w[:, :width], preferred_element_type=f32) * scale[...]
        ).astype(bf16)
        kv_ref[...] = (
            jnp.dot(normed, w[:, width:], preferred_element_type=f32) + ones[...]
        ).astype(bf16)

        @pl.when(info[count + 1] == info[j])
        def _():
            mine_ref[pl.ds(pl.multiple_of(tile * step, step), step), :] = value

    for i in range(count):
        for lane in range(2):

            @pl.when((j == i) & (info[count] == lane))
            def _(i=i, lane=lane):
                work(pairs[2 * i + 1 - lane])


def project(pairs, places, lane, mine, wt, gain, weights, scale, ones, group_len, carried=None):
    count = len(pairs)
    rows, d = pairs[0][0].shape
    width = scale.shape[1]
    step = 128
    tiles = rows // step
    full = lambda j, t, f: (0, 0)
    at = lambda j, t, f: (f[j] * tiles + t, 0)
    once = pl.Buffered(1)
    info = jnp.stack(list(places) + [lane.astype(jnp.int32), mine, wt])
    args = [x for pair in pairs for x in pair] + [gain, *map(hbm, weights), scale, ones]
    in_specs = [
        pl.BlockSpec(
            (step, d),
            lambda j, t, f, i=i: (jnp.where(j == i, t, jnp.where(j > i, tiles - 1, 0)), 0),
        )
        for i in range(count)
        for _ in range(2)
    ]
    in_specs += [pl.BlockSpec((1, d), full, pipeline_mode=once)]
    in_specs += [pl.BlockSpec(w.shape, full, pipeline_mode=once) for w in weights]
    in_specs += [
        pl.BlockSpec((1, width), full, pipeline_mode=once),
        pl.BlockSpec((1, 2 * width), full, pipeline_mode=once),
    ]
    aliases = {}
    if carried is not None:
        base = len(args) + 2
        args += [hbm(x) for x in (carried[3], *carried[:3])]
        in_specs += [pl.BlockSpec((rows, d), full, pipeline_mode=once)]
        in_specs += [pl.BlockSpec(memory_space=pl.ANY)] * 3
        aliases = {base: 0, base + 1: 1, base + 2: 2}
    return pl.pallas_call(
        functools.partial(
            project_kernel, count=count, halves=len(weights), width=width, fresh=carried is None
        ),
        out_shape=[
            pltpu.HBM((group_len, d), bf16),
            pltpu.HBM((group_len, width), bf16),
            pltpu.HBM((group_len, 2 * width), bf16),
            pltpu.HBM((rows, d), bf16),
        ],
        grid_spec=pltpu.PrefetchScalarGridSpec(
            num_scalar_prefetch=1,
            grid=(count, tiles),
            in_specs=in_specs,
            out_specs=[
                pl.BlockSpec((step, d), at),
                pl.BlockSpec((step, width), at),
                pl.BlockSpec((step, 2 * width), at),
                pl.BlockSpec((rows, d), full),
            ],
            scratch_shapes=[pltpu.VMEM((d, 3 * width), bf16)],
        ),
        input_output_aliases=aliases,
        compiler_params=pltpu.CompilerParams(vmem_limit_bytes=48 << 20),
        cost_estimate=cost(10),
        name="project",
    )(info, *args)


def tail_body(at, p0, p1, p2, p3, x_ref, g_ref, w_s, gain, outs):
    lo_ref, att_ref, nm_ref, gh_ref, act_ref, gp_ref, gr_ref, c0, c1, c2, c3, gg_ref = outs
    mine = at[0]
    pieces = (p0, p1, p2, p3)
    cols = p0.shape[1]
    nt = (((1,), (1,)), ((), ()))
    for i in range(4):

        @pl.when(mine == i)
        def _(i=i):
            att_ref[...] = jnp.concatenate([pieces[i ^ k][...] for k in range(4)], axis=1)

    resid = x_ref[...].astype(f32) + jnp.dot(att_ref[...], w_s[0], preferred_element_type=f32)
    inverse = lax.rsqrt(jnp.mean(resid * resid, axis=-1, keepdims=True) + epsilon)
    normed = (resid * inverse * gain[...]).astype(bf16)
    nm_ref[...] = normed
    hidden = jnp.dot(normed, w_s[1], preferred_element_type=f32)
    sig = 1.0 / (1.0 + jnp.exp(-hidden))
    active = (hidden * sig).astype(bf16)
    act_ref[...] = active
    lo_ref[...] = (resid + jnp.dot(active, w_s[2], preferred_element_type=f32)).astype(bf16)
    grad_active = lax.dot_general(g_ref[...], w_s[2], nt, preferred_element_type=f32)
    grad_hidden = (grad_active * sig * (1.0 + hidden * (1.0 - sig))).astype(bf16)
    gh_ref[...] = grad_hidden
    grad_normed = lax.dot_general(grad_hidden, w_s[1], nt, preferred_element_type=f32)
    gg_ref[...] += jnp.sum(grad_normed * resid * inverse, axis=0, keepdims=True)
    scaled = grad_normed * gain[...]
    grad_resid = (
        g_ref[...].astype(f32)
        + inverse * scaled
        - resid * (inverse * inverse * inverse) * jnp.mean(scaled * resid, axis=-1, keepdims=True)
    )
    gr_ref[...] = grad_resid
    grad_proj = grad_resid.astype(bf16)
    gp_ref[...] = grad_proj
    grad_att = lax.dot_general(grad_proj, w_s[0], nt, preferred_element_type=f32).astype(bf16)
    for i in range(4):

        @pl.when(mine == i)
        def _(i=i):
            for j, out in enumerate((c0, c1, c2, c3)):
                out[...] = grad_att[:, (i ^ j) * cols : ((i ^ j) + 1) * cols]


def tail_kernel(at, p0, p1, p2, p3, x_ref, g_ref, own, half, other, gain, *refs, rows, hrows):
    w_s = refs[-1]
    outs = refs[:-1]

    @pl.when(pl.program_id(0) == 0)
    def _():
        outs[-1][...] = jnp.zeros_like(outs[-1])
        w_s[:, pl.ds(pl.multiple_of(at[1], 16), rows), :] = own[...]
        w_s[:, pl.ds(pl.multiple_of(at[2], 16), hrows), :] = half[...]
        w_s[:, pl.ds(pl.multiple_of(at[3], 16), hrows), :] = other[...]

    tail_body(at, p0, p1, p2, p3, x_ref, g_ref, w_s, gain, outs)


def whole_tail_kernel(at, p0, p1, p2, p3, x_ref, g_ref, w, gain, *outs):
    @pl.when(pl.program_id(0) == 0)
    def _():
        outs[-1][...] = jnp.zeros_like(outs[-1])

    tail_body(at, p0, p1, p2, p3, x_ref, g_ref, w, gain, outs)


def tail(at, pieces, x, g, weights, gain, tile=256):
    rows, d = x.shape
    cols = pieces[0].shape[1]
    row = lambda i, m: (i, 0)
    once = pl.Buffered(1)
    whole = lambda *shape: pl.BlockSpec(shape, lambda i, m: (0,) * len(shape), pipeline_mode=once)
    wide = pl.BlockSpec((tile, d), row)
    slim = pl.BlockSpec((tile, cols), row)
    if len(weights) == 3:
        body = functools.partial(tail_kernel, rows=weights[0].shape[1], hrows=weights[1].shape[1])
        scratch = [pltpu.VMEM((3, d, d), bf16)]
    else:
        body = whole_tail_kernel
        scratch = []
    return pl.pallas_call(
        body,
        out_shape=[pltpu.HBM((rows, d), bf16)] * 6
        + [pltpu.HBM((rows, d), f32)]
        + [pltpu.HBM((rows, cols), bf16)] * 4
        + [pltpu.HBM((1, d), f32)],
        grid_spec=pltpu.PrefetchScalarGridSpec(
            num_scalar_prefetch=1,
            grid=(rows // tile,),
            in_specs=[slim] * 4 + [wide] * 2 + [whole(*w.shape) for w in weights] + [whole(1, d)],
            out_specs=[wide] * 7 + [slim] * 4 + [pl.BlockSpec((1, d), lambda i, m: (0, 0))],
            scratch_shapes=scratch,
        ),
        compiler_params=pltpu.CompilerParams(vmem_limit_bytes=52 << 20),
        cost_estimate=cost(0.01),
        name="tail",
    )(at, *pieces, hbm(x), g, *map(hbm, weights), gain)


tn_dims = (((0,), (0,)), ((), ()))


def share_kernel(col, l0, l1, l2, r0, r1, r2, out):
    for i, (left, right) in enumerate(((l0, r0), (l1, r1), (l2, r2))):

        @pl.when(pl.program_id(0) == i)
        def _(left=left, right=right):
            out[...] = lax.dot_general(
                left[...], right[...], tn_dims, preferred_element_type=f32
            ).astype(bf16)


def share(lefts, rights, col):
    rows, d = lefts[0].shape
    w = d // 2
    once = pl.Buffered(1)
    return pl.pallas_call(
        share_kernel,
        out_shape=pltpu.HBM((d, 3 * w), bf16),
        grid_spec=pltpu.PrefetchScalarGridSpec(
            num_scalar_prefetch=1,
            grid=(3,),
            in_specs=[pl.BlockSpec((rows, d), lambda i, c: (0, 0), pipeline_mode=once)] * 3
            + [pl.BlockSpec((rows, w), lambda i, c: (0, c[0]), pipeline_mode=once)] * 3,
            out_specs=pl.BlockSpec((d, w), lambda i, c: (0, i)),
        ),
        compiler_params=pltpu.CompilerParams(vmem_limit_bytes=40 << 20),
        cost_estimate=cost(.01),
        name="share",
    )(col.reshape(1), *map(hbm, lefts), *map(hbm, rights))


def keep_kernel(col, l0, l1, l2, r0, r1, r2, got, out):
    for i, (left, right) in enumerate(((l0, r0), (l1, r1), (l2, r2))):

        @pl.when(pl.program_id(0) == i)
        def _(left=left, right=right):
            out[...] = (
                lax.dot_general(left[...], right[...], tn_dims, preferred_element_type=f32)
                + got[...].astype(f32)
            ).astype(bf16)


def keep(lefts, rights, got, col):
    rows, d = lefts[0].shape
    w = d // 2
    once = pl.Buffered(1)
    block = pl.BlockSpec((d, w), lambda i, c: (0, i))
    return pl.pallas_call(
        keep_kernel,
        out_shape=pltpu.HBM((d, 3 * w), bf16),
        grid_spec=pltpu.PrefetchScalarGridSpec(
            num_scalar_prefetch=1,
            grid=(3,),
            in_specs=[pl.BlockSpec((rows, d), lambda i, c: (0, 0), pipeline_mode=once)] * 3
            + [pl.BlockSpec((rows, w), lambda i, c: (0, c[0]), pipeline_mode=once)] * 3
            + [block],
            out_specs=block,
        ),
        compiler_params=pltpu.CompilerParams(vmem_limit_bytes=40 << 20),
        cost_estimate=cost(.01),
        name="keep",
    )(col.reshape(1), *map(hbm, lefts), *map(hbm, rights), hbm(got))


def total_kernel(*refs):
    acc = jnp.zeros(refs[-1].shape, f32)
    for ref in refs[:-1]:
        for i in range(ref.shape[0]):
            acc = acc + ref[i].astype(f32)
    refs[-1][...] = acc.astype(bf16)


def total(arrays):
    _, r, c = arrays[0].shape
    w = c
    for cut in (640, 256):
        if c % cut == 0:
            w = cut
            break
    return pl.pallas_call(
        total_kernel,
        out_shape=pltpu.HBM((r, c), bf16),
        grid_spec=pltpu.PrefetchScalarGridSpec(
            num_scalar_prefetch=0,
            grid=(c // w,),
            in_specs=[pl.BlockSpec((x.shape[0], r, w), lambda i: (0, 0, i)) for x in arrays],
            out_specs=pl.BlockSpec((r, w), lambda i: (0, i)),
        ),
        compiler_params=pltpu.CompilerParams(vmem_limit_bytes=40 << 20),
        cost_estimate=cost(10),
        name="total",
    )(*arrays)


def place_kernel(at, own_ref, mate_ref, o0, o1, o2):
    block = pl.program_id(0)
    slot = ((block // 2) ^ at[0]) * 2 + ((block % 2) ^ at[1])
    w = o0.shape[2] // 2

    def put(refs):
        for side, ref in enumerate(refs):
            part = ref[slot].astype(f32)
            for i, out in enumerate((o0, o1, o2)):
                out[0, :, side * w : (side + 1) * w] = part[:, i * w : (i + 1) * w]

    @pl.when(at[2] == 0)
    def _():
        put((own_ref, mate_ref))

    @pl.when(at[2] == 1)
    def _():
        put((mate_ref, own_ref))


def place_tail(own, mate, at):
    n, h, width = own.shape
    d = width // 3 * 2
    whole = pl.BlockSpec(own.shape, lambda i, m: (0, 0, 0), pipeline_mode=pl.Buffered(1))
    outs = pl.pallas_call(
        place_kernel,
        out_shape=[pltpu.HBM((n, h, d), f32)] * 3,
        grid_spec=pltpu.PrefetchScalarGridSpec(
            num_scalar_prefetch=1,
            grid=(n,),
            in_specs=[whole] * 2,
            out_specs=[pl.BlockSpec((1, h, d), lambda i, m: (i, 0, 0))] * 3,
        ),
        compiler_params=pltpu.CompilerParams(vmem_limit_bytes=40 << 20),
        cost_estimate=cost(.1),
        name="place_tail",
    )(at, hbm(own), hbm(mate))
    return [out.reshape(n * h, d) for out in outs]


def cross_kernel(at, x_ref, g_ref, *refs):
    s = refs[-1]
    s[...] = lax.dot_general(x_ref[...], g_ref[...], tn_dims, preferred_element_type=f32).astype(bf16)
    step = pl.program_id(0)
    half = s.shape[0] // 2
    for w in range(2):

        @pl.when(step == w)
        def _(w=w):
            for x in range(2):
                rows = pl.ds(pl.multiple_of((at[1] ^ x) * half, 16), half)
                refs[2 * w + x][...] = s[rows, :]


def cross(x, g, at):
    rows, d = x.shape
    w = d // 2
    block = pl.BlockSpec((w // 2, g.shape[1]), lambda i, m: (0, 0))
    return pl.pallas_call(
        cross_kernel,
        out_shape=[pltpu.HBM((w // 2, g.shape[1]), bf16)] * 4,
        grid_spec=pltpu.PrefetchScalarGridSpec(
            num_scalar_prefetch=1,
            grid=(2,),
            in_specs=[
                pl.BlockSpec((rows, w), lambda i, m: (0, m[0] ^ i)),
                pl.BlockSpec(g.shape, lambda i, m: (0, 0)),
            ],
            out_specs=[block] * 4,
            scratch_shapes=[pltpu.VMEM((w, g.shape[1]), bf16)],
        ),
        compiler_params=pltpu.CompilerParams(vmem_limit_bytes=40 << 20),
        cost_estimate=cost(0.1),
        name="cross",
    )(at, hbm(x), hbm(g))


def spread_kernel(at, *refs, groups, width):
    out = refs[-1]
    step = out.shape[1]
    slot = (pl.program_id(0) ^ at[0]) * 2
    rows = pl.ds(pl.multiple_of(pl.program_id(1) * step, step), step)

    def put(flip):
        cut = []
        for t in range(3):
            for n in range(2):
                for core in range(2):
                    for g in range(groups):
                        part = refs[2 * g + (core ^ flip)][slot + (n ^ at[1]), rows, :]
                        cut.append(part[:, t * width : (t + 1) * width])
        out[0] = jnp.concatenate(cut, axis=1).astype(f32)

    for flip in range(2):

        @pl.when(at[2] == flip)
        def _(flip=flip):
            put(flip)


def spread(arrays, at, used):
    flat = [x for pair in arrays for x in pair]
    _, rows, _ = flat[0].shape
    groups = len(arrays)
    width = 4 * groups * used
    cuts = 2 if rows % 32 == 0 else 1
    return pl.pallas_call(
        functools.partial(spread_kernel, groups=groups, width=used // 3),
        out_shape=pltpu.HBM((2, rows, width), f32),
        grid_spec=pltpu.PrefetchScalarGridSpec(
            num_scalar_prefetch=1,
            grid=(2, cuts),
            in_specs=[
                pl.BlockSpec(x.shape, lambda i, j, m: (0, 0, 0), pipeline_mode=pl.Buffered(1)) for x in flat
            ],
            out_specs=pl.BlockSpec((1, rows // cuts, width), lambda i, j, m: (i, j, 0)),
        ),
        compiler_params=pltpu.CompilerParams(vmem_limit_bytes=40 << 20),
        cost_estimate=cost(0.1),
        name="spread",
    )(at, *map(hbm, flat)).reshape(2 * rows, width)


def rms_inverse(values):
    return lax.rsqrt(jnp.mean(values * values, axis=-1, keepdims=True) + epsilon)


def norm_back(values, inverse, grad_scaled):
    return inverse * grad_scaled - values * (inverse * inverse * inverse) * jnp.mean(
        grad_scaled * values, axis=-1, keepdims=True
    )


def dot(left, right):
    return jnp.dot(left, right, preferred_element_type=f32)


def times_trans(left, right):
    return lax.dot_general(left, right, (((1,), (1,)), ((), ())), preferred_element_type=f32)


def trans_times(left, right):
    return lax.dot_general(left, right, (((0,), (0,)), ((), ())), preferred_element_type=f32)


def rows_at(array, start, count):
    return lax.dynamic_slice_in_dim(array, start, count, 0)


def put_rows(array, rows, start):
    return lax.dynamic_update_slice_in_dim(array, rows, start, 0)


def make_local(sizes):
    def pairs(target):
        found = []
        for gx in range(sizes["gx"]):
            for gc in range(sizes["gc"]):
                for z in range(4):
                    for w in range(sizes["wt"]):
                        goal = target(gx, gc, z, w)
                        if goal is not None and goal != (gx, gc, z, w):
                            found.append((place(gx, gc, z, w), place(*goal)))
        return found

    def place(gx, gc, z, w):
        return ((gx * sizes["gc"] + gc) * 4 + z) * sizes["wt"] + w

    def send(value, target):
        return lax.ppermute(value, AXES, pairs(target))

    def move(value, target, still):
        return jnp.where(still, value, send(value, target))

    def core_mate(gx, gc, z, w):
        return (gx, 1 - gc, z, w)

    def x_mate(gx, gc, z, w):
        return (1 - gx, gc, z, w)

    def near_mate(gx, gc, z, w):
        return (gx, gc, z ^ 1, w)

    def far_mate(gx, gc, z, w):
        return (gx, gc, z ^ 2, w)

    def cross_mate(gx, gc, z, w):
        return (gx, 1 - gc, z ^ 1, w)

    def wt_mate(gx, gc, z, w):
        return (gx, gc, z, 1 - w)

    def wt_x_mate(gx, gc, z, w):
        return (1 - gx, gc, z, 1 - w)

    def to_host(gx, gc, z, w):
        return (gx, z & 1, 2 * gc + (z >> 1), w)

    def to_home(gx, gc, z, w):
        return (gx, z >> 1, 2 * (z & 1) + gc, w)

    def hop1(gx, gc, z, w):
        if gc == 0:
            return (gx, 0, z - 1, w) if z > 0 else None
        return (gx, 1, z + 1, w) if z < 3 else None

    def hop2(gx, gc, z, w):
        if gc == 0:
            return (gx, 0, z - 1, w) if z in (1, 2) else None
        return (gx, 1, z + 1, w) if z in (1, 2) else None

    def hop3(gx, gc, z, w):
        if gc == 0:
            return (gx, 0, z ^ 1, w) if z < 2 else None
        return (gx, 1, z ^ 1, w) if z > 1 else None

    def lane_share(gx, gc, z, w):
        return (gx, 1 - gc, z, w) if gc == z >> 1 else None

    def sum_all(value):
        for axis in AXES:
            step = 1
            while step < sizes[axis]:

                def mate(gx, gc, z, w, axis=axis, step=step):
                    at = dict(gx=gx, gc=gc, far=z >> 1, near=z & 1, wt=w)
                    at[axis] ^= step
                    return (at["gx"], at["gc"], 2 * at["far"] + at["near"], at["wt"])

                value = value + send(value, mate)
                step *= 2
        return value

    def local(
        tokens, segments, w_qkv, w_proj, w_in, w_out, gain_attn, gain_mlp, query_scale, cotangent
    ):
        gx, gc, host, near, wt = (lax.axis_index(axis) for axis in AXES)
        z = 2 * host + near
        mine = 2 * near + gc
        parts = 4
        nh = H // parts
        groups = 2
        rows = tokens.shape[1]
        group_len = segments.shape[1]
        wrows = w_qkv.shape[0]
        lane = gc == host
        pair = sizes["wt"] == 2

        def after(value, *others):
            return lax.optimization_barrier((value,) + others)[0]

        picked = pick(w_qkv, mine, parts, groups, nh)
        own = after(tokens[0], picked)
        got1 = send(own, hop1)
        own_share = send(own, lane_share)
        seg_mate = send(segments, core_mate)
        got2 = send(got1, hop2)
        got1_share = send(got1, lane_share)
        end = jnp.where(gc == 0, z == 0, z == 3)
        if pair:
            wide_own = stretch(picked, groups, nh, 2)
            got1 = after(got1, wide_own)
            other_w = send(picked, wt_mate)
            wide_w = (wide_own, stretch(other_w, groups, nh, 10))
        else:
            flat_all = lax.all_gather(picked, "wt", axis=0, tiled=True)[:, : 3 * nh * HD]
            each = flat_all.shape[1] // groups
            flat_w = [
                jnp.pad(flat_all[:, g * each : (g + 1) * each], ((0, 0), (0, lanes_up(each) - each)))
                for g in range(groups)
            ]
            by_head = jnp.transpose(flat_all.reshape(D, groups, 3, nh // groups, HD), (0, 2, 1, 3, 4))
            wide_w = (
                jnp.pad(
                    by_head.reshape(D, 3 * nh, HD), ((0, 0), (0, 0), (0, LN - HD))
                ).reshape(D, -1),
            )
        got3 = send(jnp.where(end, own, got2), hop3)
        got2_share = send(got2, lane_share)
        way = 1 - 2 * host
        last = jnp.where(host == 0, jnp.where(z == 0, 3, 0), jnp.where(z == 3, 0, 3))
        places = (z, z + way, z + 2 * way, last)

        half_rows = wrows // 2
        tail_own = jnp.stack([w_proj, w_in, w_out])
        half_w = lax.dynamic_slice_in_dim(tail_own, gc * half_rows, half_rows, 1)
        if pair:
            half_w = send(after(half_w, other_w), wt_mate)
        else:
            half_w = lax.all_gather(half_w, "wt", axis=0, tiled=False)

        dim_scale = scale_base / math.sqrt(HD) * jax.nn.softplus(query_scale)
        lane_scale = jnp.tile(jnp.pad(dim_scale * log2e, (0, LN - HD)), nh)[None]
        ones = jnp.tile(
            ((jnp.arange(LN) >= HD) & (jnp.arange(LN) < HD + 3)).astype(f32), 2 * nh
        )[None]
        seg_row = jnp.where(lane, segments, seg_mate)[0]
        fixed = (lane, mine, wt, gain_attn[None], wide_w, lane_scale, ones, group_len)
        carried = project(((own, own_share), (got1, got1_share)), places[:2], *fixed)
        got2_share = after(got2_share, carried[0])
        got3_share = send(after(got3, carried[0]), lane_share)
        carried = project(((got2, got2_share),), places[2:3], *fixed, carried=carried)
        all_normed, queries, keyval, inputs = project(
            ((got3, after(got3_share, carried[0])),), places[3:], *fixed, carried=carried
        )
        still = lane & end
        grad_mlp = move(after(cotangent[0], got3), to_host, still)

        att, att_float, q_aug = attn_fwd(queries, keyval, seg_row, nh)
        att = after(att, grad_mlp)
        if pair:
            flat_w = order(after(picked, att), other_w, wt, groups, nh)

        trades = (core_mate, near_mate, cross_mate)
        att_pieces = [rows_at(att, (mine ^ j) * rows, rows) for j in range(parts)]
        att_pieces = [att_pieces[0]] + [send(att_pieces[j + 1], trades[j]) for j in range(3)]
        half_mate = send(after(half_w, att_pieces[1]), core_mate)
        if pair:
            weights = (tail_own, half_w, half_mate)
            starts = (wt * wrows, (1 - wt) * wrows + gc * half_rows, (1 - wt) * wrows + (1 - gc) * half_rows)
        else:
            one = gc == 0
            tail_w = jnp.stack(
                [jnp.where(one, half_w, half_mate), jnp.where(one, half_mate, half_w)], axis=1
            )
            weights = (jnp.transpose(tail_w, (2, 0, 1, 3, 4)).reshape(3, D, D),)
            starts = ()
        (
            layer_out,
            attended,
            normed_mlp,
            grad_hidden,
            active,
            grad_proj,
            grad_resid,
            *pieces,
            grad_gain_mlp,
        ) = tail(
            jnp.stack([mine, *starts]), att_pieces, after(inputs, flat_w[0]), grad_mlp, weights, gain_mlp[None]
        )
        pieces = [pieces[0]] + [send(pieces[j + 1], trades[j]) for j in range(3)]

        lefts = (after(attended, pieces[1]), normed_mlp, active)
        rights = (grad_proj, grad_hidden, grad_mlp)
        from_core = send(share(lefts, rights, 1 - gc), core_mate)
        home_out = send(after(layer_out, *pieces[1:]), to_home)
        prepared = prep(pieces, att_float, mine, nh)
        summed = keep(lefts, rights, after(from_core, prepared), gc)
        kept = lax.all_to_all(summed, ("wt", "gx", "near"), 0, 0, tiled=True)

        scale_row = jnp.tile(dim_scale, nh // groups)[None]

        def backward(group, *others):
            return attn_bwd(
                q_aug, keyval, after(prepared, summed, *others), seg_row, scale_row, nh, group, groups
            )

        def gather(block):
            for mate in (near_mate, x_mate):
                block = jnp.concatenate([block, send(block, mate)])
            return block, send(block, core_mate)

        def far_sum(part):
            return (part.astype(f32) + send(part, far_mate).astype(f32)).astype(bf16)[None]

        def by_rows(grad):
            if pair:
                own, *rest = cross(all_normed, grad, jnp.stack([wt, gx]))
                got = [send(part, mate) for part, mate in zip(rest, (x_mate, wt_mate, wt_x_mate))]
                return [part[None] for part in (own, *got)]
            part = trans_times(all_normed, grad).astype(bf16)
            sources = sizes["wt"] * 2
            got = lax.all_to_all(part, ("wt", "gx"), 0, 0, tiled=True)
            return [got.reshape(sources, D // sources, -1)]

        grad_a, lanes_a = backward(0)
        layer_out = jnp.where(still, after(layer_out, grad_a), home_out)
        rows_a = by_rows(after(grad_a, layer_out))
        grad_b, lanes_b = backward(1, rows_a[0])
        rows_a[0] = after(rows_a[0], grad_b)
        sum_a = total(rows_a)
        block_a = far_sum(sum_a)

        def shard_grad(shard, *others):
            return sum(
                times_trans(rows_at(after(grad, *others), shard * rows, rows), w)
                for grad, w in zip((grad_a, grad_b), flat_w)
            )

        to_core = jnp.stack([shard_grad(mine ^ 3, sum_a), shard_grad(mine ^ 1, sum_a)]).astype(bf16)
        from_core = send(to_core, core_mate).astype(f32)
        rows_b = by_rows(after(grad_b, to_core))
        to_near = (shard_grad(mine ^ 2, rows_b[0]) + from_core[0]).astype(bf16)
        grad_normed = shard_grad(mine, rows_b[0]) + from_core[1]
        from_near = send(to_near, near_mate).astype(f32)
        sources = sizes["wt"] * 4
        tail_sum = total(
            [after(kept, rows_b[0], to_near).reshape(sources, D // sources, -1)]
        )
        block = far_sum(tail_sum)
        rows_b[0] = after(rows_b[0], block_a)
        sum_b = total(rows_b)
        block_b = far_sum(sum_b)
        grad_normed = grad_normed + from_near
        inputs = inputs.astype(f32)
        inverse_attn = rms_inverse(inputs)
        grad_gain_attn = jnp.sum(grad_normed * inputs * inverse_attn, axis=0)
        grad_tokens = move(
            (grad_resid + norm_back(inputs, inverse_attn, grad_normed * gain_attn)).astype(bf16),
            to_home,
            still,
        )

        total_qkv = spread(
            [gather(block_a), gather(block_b)], jnp.stack([gx, near, gc]), 3 * nh // groups * HD
        )
        totals = place_tail(*gather(block), jnp.stack([gx, near, gc]))

        grad_query_scale = (
            (lanes_a + lanes_b)[0, :HD]
            / (dim_scale * log2e)
            * (scale_base / math.sqrt(HD))
            * jax.nn.sigmoid(query_scale)
        )
        small = jnp.concatenate(
            [grad_gain_attn, grad_gain_mlp[0], jnp.pad(grad_query_scale, (0, LN - HD))]
        ).reshape(-1, LN)
        small = sum_all(small).reshape(-1)
        return (
            layer_out[None],
            grad_tokens[None],
            total_qkv,
            *totals,
            small[:D],
            small[D : 2 * D],
            small[2 * D : 2 * D + HD],
        )

    return local


def solution(mesh):
    groups, parts, wt = (mesh.shape[axis] for axis in ("grp", "ctx", "wt"))
    inner = Mesh(mesh.devices.reshape(groups // 2, 2, parts // 2, 2, wt), AXES)
    sizes = dict(inner.shape)
    split = P(("gx", "gc", "wt"), ("far", "near"), None)
    weight = P("wt", None)
    return jax.shard_map(
        make_local(sizes),
        mesh=inner,
        in_specs=(
            split,
            P(("gx", "gc", "wt"), None),
            weight,
            weight,
            weight,
            weight,
            P(),
            P(),
            P(),
            split,
        ),
        out_specs=(split, split, weight, weight, weight, weight, P(), P(), P()),
        check_vma=False,
    )
```

```python
import functools
import math

import jax
import jax.numpy as jnp
from jax import lax
from jax.experimental import pallas as pl
from jax.experimental.pallas import tpu as pltpu
from jax.sharding import Mesh
from jax.sharding import PartitionSpec as P

D = 1280
H = 16
HD = 80
LN = 128
epsilon = 1e-06
scale_base = 1.442695041
log2e = 1.4426950408889634
NEG = -1e30
def cost(us):
    return pl.CostEstimate(flops=int(us * 1_000_000_000), transcendentals=0, bytes_accessed=1000)


CHEAP = cost(0.001)
f32 = jnp.float32
bf16 = jnp.bfloat16
AXES = ("gx", "gc", "far", "near", "wt")


def hbm(x):
    return pltpu.with_memory_space_constraint(x, pltpu.HBM)


def block_flags(seg_row, bq, bk):
    n = seg_row.shape[0]
    q = seg_row.reshape(n // bq, bq)
    k = seg_row.reshape(n // bk, bk)
    qf, ql = q[:, 0][:, None], q[:, -1][:, None]
    kf, kl = k[:, 0][None], k[:, -1][None]
    qs = jnp.arange(n // bq, dtype=jnp.int32)[:, None] * bq
    ks = jnp.arange(n // bk, dtype=jnp.int32)[None] * bk
    below = ks + bk - 1 <= qs
    skip = (ks > qs + bq - 1) | ((kf > 0) & (kl < qf))
    same = (qf == ql) & (kl == ql) & ((kf == kl) | ((kf == 0) & (kl == 1)))
    full = below & ((kl == 0) | same)
    return jnp.where(skip, 0, jnp.where(full, 1, 2)).astype(jnp.int32).reshape(-1)


def put_split(base, col, lanes):
    hi = col.astype(bf16).astype(f32)
    rest = col - hi
    mid = rest.astype(bf16).astype(f32)
    out = jnp.where(lanes == HD, hi, base)
    out = jnp.where(lanes == HD + 1, mid, out)
    return jnp.where(lanes == HD + 2, rest - mid, out).astype(bf16)


def fwd_kernel(flags, q_ref, kv, segc, segr, att, of, qaug, m_s, acc_s, *, nh, bq, bk, nk):
    qi = pl.program_id(0)
    count = (qi * bq + bq + bk - 1) // bk
    nt = (((1,), (1,)), ((), ()))
    acc_s[...] = jnp.zeros_like(acc_s)
    m_s[...] = jnp.zeros_like(m_s)

    def mask(ko):
        qpos = qi * bq + lax.broadcasted_iota(jnp.int32, (bq, bk), 0)
        kpos = ko + lax.broadcasted_iota(jnp.int32, (bq, bk), 1)
        ks = segr[:, pl.ds(ko, bk)]
        return (kpos <= qpos) & ((ks == 0) | (ks == segc[...]))

    def step(kb, masked):
        ko = pl.multiple_of(kb * bk, bk)
        if masked:
            allowed = mask(ko)
        for h in range(nh):
            k = kv[pl.ds(ko, bk), h * LN : (h + 1) * LN]
            v = kv[pl.ds(ko, bk), (nh + h) * LN : (nh + h + 1) * LN]
            s = lax.dot_general(q_ref[:, h * LN : (h + 1) * LN], k, nt, preferred_element_type=f32)
            p = jnp.exp2(s)
            if masked:
                p = jnp.where(allowed, p, 0.0)
            acc_s[h] += jnp.dot(p.astype(bf16), v, preferred_element_type=f32)

    def body(kb, carry):
        flag = flags[qi * nk + kb]

        @pl.when(flag == 1)
        def _():
            step(kb, False)

        @pl.when(flag == 2)
        def _():
            step(kb, True)

        return carry

    lax.fori_loop(0, count, body, 0)
    bad = jnp.zeros((bq, 1), f32)
    for h in range(nh):
        total = acc_s[h][:, HD : HD + 1]
        bad = jnp.maximum(bad, jnp.where((total > 2.0**-60) & (total < 2.0**60), 0.0, 1.0))

    @pl.when(jnp.max(bad) > 0.0)
    def _():
        def head(h, carry):
            kc = pl.ds(pl.multiple_of(h * LN, LN), LN)
            vc = pl.ds(pl.multiple_of((nh + h) * LN, LN), LN)
            m_s[h] = jnp.full((bq, LN), NEG, f32)
            acc_s[h] = jnp.zeros((bq, LN), f32)

            def inner(kb, carry):
                @pl.when(flags[qi * nk + kb] > 0)
                def _():
                    ko = pl.multiple_of(kb * bk, bk)
                    s = lax.dot_general(
                        q_ref[:, kc], kv[pl.ds(ko, bk), kc], nt, preferred_element_type=f32
                    )
                    s = jnp.where(mask(ko), s, NEG)
                    old = m_s[h]
                    new = jnp.maximum(old, jnp.max(s, axis=1, keepdims=True))
                    p = jnp.exp2(s - new[:, :1]).astype(bf16)
                    m_s[h] = new
                    acc_s[h] = acc_s[h] * jnp.exp2(old - new) + jnp.dot(
                        p, kv[pl.ds(ko, bk), vc], preferred_element_type=f32
                    )

                return carry

            lax.fori_loop(0, count, inner, 0)
            return carry

        lax.fori_loop(0, nh, head, 0)

    lanes = lax.broadcasted_iota(jnp.int32, (bq, LN), 1)
    outs = []
    for h in range(nh):
        acc = acc_s[h]
        total = acc[:, HD : HD + 1]
        out = acc * (1.0 / total)
        of[:, h * LN : (h + 1) * LN] = jnp.where(lanes < HD, out, 0.0).astype(bf16)
        outs.append(out[:, :HD])
        lse = m_s[h][:, :1] + jnp.log2(total)
        qaug[:, h * LN : (h + 1) * LN] = put_split(
            q_ref[:, h * LN : (h + 1) * LN].astype(f32), -lse, lanes
        )
    att[...] = jnp.concatenate(outs, axis=1).astype(bf16)


def attn_fwd(q, kv, seg_row, nh, bq=512, bk=512):
    n = q.shape[0]
    w = nh * LN
    spec = pltpu.PrefetchScalarGridSpec(
        num_scalar_prefetch=1,
        grid=(n // bq,),
        in_specs=[
            pl.BlockSpec((bq, w), lambda i, f: (i, 0)),
            pl.BlockSpec((n, 2 * w), lambda i, f: (0, 0)),
            pl.BlockSpec((bq, 1), lambda i, f: (i, 0)),
            pl.BlockSpec((1, n), lambda i, f: (0, 0)),
        ],
        out_specs=[
            pl.BlockSpec((bq, nh * HD), lambda i, f: (i, 0)),
            pl.BlockSpec((bq, w), lambda i, f: (i, 0)),
            pl.BlockSpec((bq, w), lambda i, f: (i, 0)),
        ],
        scratch_shapes=[pltpu.VMEM((nh, bq, LN), f32), pltpu.VMEM((nh, bq, LN), f32)],
    )
    return pl.pallas_call(
        functools.partial(fwd_kernel, nh=nh, bq=bq, bk=bk, nk=n // bk),
        out_shape=[
            pltpu.HBM((n, nh * HD), bf16),
            pltpu.HBM((n, w), bf16),
            pltpu.HBM((n, w), bf16),
        ],
        grid_spec=spec,
        compiler_params=pltpu.CompilerParams(vmem_limit_bytes=40 << 20),
        cost_estimate=cost(0.01),
        name="attn_fwd",
    )(block_flags(seg_row, bq, bk), hbm(q), hbm(kv), seg_row[:, None], seg_row[None])


def bwd_kernel(
    flags, qa, kk, vv, doa_s, segc, segr, scale, dqkv, gscale, dq_s, dk_s, dv_s, *, nh, bq, bk, n
):
    nk = n // bk
    nq = n // bq
    kb = pl.program_id(0)

    @pl.when(kb == 0)
    def _():
        dq_s[...] = jnp.zeros_like(dq_s)

    dk_s[...] = jnp.zeros_like(dk_s)
    dv_s[...] = jnp.zeros_like(dv_s)
    ko = kb * bk
    nt = (((1,), (1,)), ((), ()))
    tn = (((0,), (0,)), ((), ()))

    def step(qi, masked):
        qo = pl.multiple_of(qi * bq, bq)
        if masked:
            kpos = ko + lax.broadcasted_iota(jnp.int32, (bk, bq), 0)
            qpos = qo + lax.broadcasted_iota(jnp.int32, (bk, bq), 1)
            ks = segc[...]
            allowed = (kpos <= qpos) & ((ks == 0) | (ks == segr[:, pl.ds(qo, bq)]))
        for h in range(nh):
            c = slice(h * LN, (h + 1) * LN)
            q = qa[pl.ds(qo, bq), c]
            k = kk[:, c]
            d = doa_s[pl.ds(qo, bq), c]
            p = jnp.exp2(lax.dot_general(k, q, nt, preferred_element_type=f32))
            if masked:
                p = jnp.where(allowed, p, 0.0)
            ds = (p * lax.dot_general(vv[:, c], d, nt, preferred_element_type=f32)).astype(bf16)
            dv_s[h] += jnp.dot(p.astype(bf16), d, preferred_element_type=f32)
            dk_s[h] += jnp.dot(ds, q, preferred_element_type=f32)
            dq_s[h, pl.ds(qo, bq), :] += lax.dot_general(ds, k, tn, preferred_element_type=f32)

    def body(qi, carry):
        flag = flags[qi * nk + kb]

        @pl.when(flag == 1)
        def _():
            step(qi, False)

        @pl.when(flag == 2)
        def _():
            step(qi, True)

        return carry

    lax.fori_loop(ko // bq, nq, body, 0)
    r = pl.multiple_of(ko, bk)
    ln2 = math.log(2.0)
    gap = dqkv.shape[1] - 3 * nh * HD
    dqkv[pl.ds(r, bk), nh * HD :] = jnp.concatenate(
        [dk_s[h][:, :HD] * ln2 for h in range(nh)]
        + [dv_s[h][:, :HD] for h in range(nh)]
        + [jnp.zeros((bk, gap), f32)],
        axis=1,
    ).astype(bf16)

    @pl.when(kb == nk - 1)
    def _():
        total = jnp.zeros((1, LN), f32)
        for i in range(nq):
            rows = slice(i * bq, (i + 1) * bq)
            for h in range(nh):
                total = total + jnp.sum(
                    dq_s[h, rows, :] * qa[rows, h * LN : (h + 1) * LN].astype(f32), axis=0, keepdims=True
                )
            grads = jnp.concatenate([dq_s[h, rows, :][:, :HD] for h in range(nh)], axis=1)
            dqkv[rows, 0 : nh * HD] = (grads * scale[...]).astype(bf16)
        gscale[...] = jnp.broadcast_to(total, gscale.shape)


def prep_kernel(mine, do0, do1, do2, do3, of, out, *, nh):
    tile = of.shape[0]
    lanes = lax.broadcasted_iota(jnp.int32, (tile, LN), 1)
    for j, piece in enumerate((do0, do1, do2, do3)):

        @pl.when(pl.program_id(0) == j)
        def _(piece=piece):
            d = piece[...].astype(f32)
            for h in range(nh):
                dh = jnp.concatenate(
                    [d[:, h * HD : (h + 1) * HD], jnp.zeros((tile, LN - HD), f32)], axis=1
                )
                c = slice(h * LN, (h + 1) * LN)
                delta = jnp.sum(dh * of[:, c].astype(f32), axis=1, keepdims=True)
                out[:, c] = put_split(dh, -delta, lanes)


def prep(pieces, of, mine, nh, tile=256):
    n, w = of.shape
    per = n // 4 // tile
    at = lambda j, i, m: ((m[0] ^ j) * per + i, 0)
    return pl.pallas_call(
        functools.partial(prep_kernel, nh=nh),
        out_shape=pltpu.HBM((n, w), bf16),
        grid_spec=pltpu.PrefetchScalarGridSpec(
            num_scalar_prefetch=1,
            grid=(4, per),
            in_specs=[
                pl.BlockSpec(
                    (tile, nh * HD),
                    lambda j, i, m, k=k: (jnp.where(j == k, i, jnp.where(j > k, per - 1, 0)), 0),
                )
                for k in range(4)
            ]
            + [pl.BlockSpec((tile, w), at)],
            out_specs=pl.BlockSpec((tile, w), at),
        ),
        compiler_params=pltpu.CompilerParams(vmem_limit_bytes=24 << 20),
        cost_estimate=cost(1000),
        name="prep",
    )(mine.reshape(1), *pieces, hbm(of))


def attn_bwd(qa, kv, doa, seg_row, scale, heads, group, groups, bq=512, bk=512):
    n = qa.shape[0]
    nh = heads // groups
    w = nh * LN
    once = pl.Buffered(1)
    spec = pltpu.PrefetchScalarGridSpec(
        num_scalar_prefetch=1,
        grid=(n // bk,),
        in_specs=[
            pl.BlockSpec((n, w), lambda i, f: (0, group), pipeline_mode=once),
            pl.BlockSpec((bk, w), lambda i, f: (i, group)),
            pl.BlockSpec((bk, w), lambda i, f: (i, groups + group)),
            pl.BlockSpec((n, w), lambda i, f: (0, group), pipeline_mode=once),
            pl.BlockSpec((bk, 1), lambda i, f: (i, 0)),
            pl.BlockSpec((1, n), lambda i, f: (0, 0)),
            pl.BlockSpec((1, nh * HD), lambda i, f: (0, 0)),
        ],
        out_specs=[
            pl.BlockSpec((n, lanes_up(3 * nh * HD)), lambda i, f: (0, 0)),
            pl.BlockSpec((8, LN), lambda i, f: (0, 0)),
        ],
        scratch_shapes=[
            pltpu.VMEM((nh, n, LN), f32),
            pltpu.VMEM((nh, bk, LN), f32),
            pltpu.VMEM((nh, bk, LN), f32),
        ],
    )
    return pl.pallas_call(
        functools.partial(bwd_kernel, nh=nh, bq=bq, bk=bk, n=n),
        out_shape=[
            pltpu.HBM((n, lanes_up(3 * nh * HD)), bf16),
            pltpu.HBM((8, LN), f32),
        ],
        grid_spec=spec,
        compiler_params=pltpu.CompilerParams(vmem_limit_bytes=48 << 20),
        cost_estimate=cost(300 if group == 0 else 0.001),
        name="attn_bwd",
    )(block_flags(seg_row, bq, bk), hbm(qa), hbm(kv), hbm(kv), hbm(doa), seg_row[:, None], seg_row[None], scale)


def quarter_columns(place, parts, groups, nh):
    width = nh // groups * HD
    return [
        (t * D + place * nh * HD + g * width, width) for g in range(groups) for t in range(3)
    ]


def pick_kernel(mine, w_ref, out, *, parts, groups, nh):
    for i in range(parts):

        @pl.when(mine[0] == i)
        def _(i=i):
            cut = [w_ref[:, a : a + width] for a, width in quarter_columns(i, parts, groups, nh)]
            used = sum(x.shape[1] for x in cut)
            pad = jnp.zeros((cut[0].shape[0], out.shape[1] - used), out.dtype)
            out[...] = jnp.concatenate(cut + [pad], axis=1)


def lanes_up(n):
    return -(-n // LN) * LN


def pick(w, mine, parts, groups, nh):
    rows = w.shape[0]
    step = 160 if rows % 160 == 0 else rows
    return pl.pallas_call(
        functools.partial(pick_kernel, parts=parts, groups=groups, nh=nh),
        out_shape=pltpu.HBM((rows, lanes_up(3 * nh * HD)), w.dtype),
        grid_spec=pltpu.PrefetchScalarGridSpec(
            num_scalar_prefetch=1,
            grid=(rows // step,),
            in_specs=[pl.BlockSpec((step, 3 * D), lambda i, m: (i, 0))],
            out_specs=pl.BlockSpec((step, lanes_up(3 * nh * HD)), lambda i, m: (i, 0)),
        ),
        cost_estimate=cost(5),
        name="pick",
    )(mine.reshape(1), hbm(w))


def stretch_kernel(x_ref, out, *, groups, nh):
    value = x_ref[...]
    each = 3 * nh * HD // groups
    zero = jnp.zeros((value.shape[0], LN - HD), value.dtype)
    per = nh // groups
    wide = []
    for t in range(3):
        for h in range(nh):
            at = (h // per) * each + t * per * HD + (h % per) * HD
            wide += [value[:, at : at + HD], zero]
    out[...] = jnp.concatenate(wide, axis=1)


def stretch(x, groups, nh, us):
    rows, width = x.shape
    step = 160
    return pl.pallas_call(
        functools.partial(stretch_kernel, groups=groups, nh=nh),
        out_shape=pltpu.HBM((rows, 3 * nh * LN), x.dtype),
        grid=(rows // step,),
        in_specs=[pl.BlockSpec((step, width), lambda i: (i, 0))],
        out_specs=pl.BlockSpec((step, 3 * nh * LN), lambda i: (i, 0)),
        cost_estimate=cost(us),
        name="stretch",
    )(hbm(x))


def order_kernel(own_first, a_ref, b_ref, *outs, each):
    def put(ref):
        value = ref[...]
        for g, out in enumerate(outs):
            gap = jnp.zeros((value.shape[0], out.shape[1] - each), value.dtype)
            out[...] = jnp.concatenate([value[:, g * each : (g + 1) * each], gap], axis=1)

    half = pl.program_id(0)

    @pl.when(half == 0)
    def _():
        put(a_ref)

    @pl.when(half == 1)
    def _():
        put(b_ref)


def order(own, other, own_at, groups, nh):
    rows, width = own.shape
    step = 320
    n = rows // step
    at = lambda i, j, m: ((i ^ m[0]) * n + j, 0)
    each = 3 * nh * HD // groups
    return pl.pallas_call(
        functools.partial(order_kernel, each=each),
        out_shape=[pltpu.HBM((2 * rows, lanes_up(each)), own.dtype)] * groups,
        grid_spec=pltpu.PrefetchScalarGridSpec(
            num_scalar_prefetch=1,
            grid=(2, n),
            in_specs=[
                pl.BlockSpec((step, width), lambda i, j, m: (j * (1 - i), 0)),
                pl.BlockSpec((step, width), lambda i, j, m: (j * i, 0)),
            ],
            out_specs=[pl.BlockSpec((step, lanes_up(each)), at)] * groups,
        ),
        cost_estimate=cost(3),
        name="order",
    )(own_at.reshape(1), hbm(own), hbm(other))


def project_kernel(info, *refs, count, halves, width, fresh):
    pairs = refs[: 2 * count]
    gain = refs[2 * count]
    weights = refs[2 * count + 1 : 2 * count + 1 + halves]
    scale, ones = refs[2 * count + 1 + halves : 2 * count + 3 + halves]
    normed_ref, q_ref, kv_ref, mine_ref, w = refs[-5:]
    j, tile = pl.program_id(0), pl.program_id(1)
    step = normed_ref.shape[0]

    @pl.when((j == 0) & (tile == 0))
    def _():
        for i, ref in enumerate(weights):
            h = ref.shape[0]
            start = (info[count + 2] ^ i) * h if halves == 2 else 0
            w[pl.ds(pl.multiple_of(start, 16), h), :] = ref[...]
        if not fresh:
            mine_ref[...] = refs[2 * count + 3 + halves][...]

    def work(x_ref):
        value = x_ref[...]
        x = value.astype(f32)
        inverse = lax.rsqrt(jnp.mean(x * x, axis=-1, keepdims=True) + epsilon)
        normed = (x * inverse * gain[...]).astype(bf16)
        normed_ref[...] = normed
        q_ref[...] = (
            jnp.dot(normed, w[:, :width], preferred_element_type=f32) * scale[...]
        ).astype(bf16)
        kv_ref[...] = (
            jnp.dot(normed, w[:, width:], preferred_element_type=f32) + ones[...]
        ).astype(bf16)

        @pl.when(info[count + 1] == info[j])
        def _():
            mine_ref[pl.ds(pl.multiple_of(tile * step, step), step), :] = value

    for i in range(count):
        for lane in range(2):

            @pl.when((j == i) & (info[count] == lane))
            def _(i=i, lane=lane):
                work(pairs[2 * i + 1 - lane])


def project(pairs, places, lane, mine, wt, gain, weights, scale, ones, group_len, carried=None):
    count = len(pairs)
    rows, d = pairs[0][0].shape
    width = scale.shape[1]
    step = 256
    tiles = rows // step
    full = lambda j, t, f: (0, 0)
    at = lambda j, t, f: (f[j] * tiles + t, 0)
    once = pl.Buffered(1)
    info = jnp.stack(list(places) + [lane.astype(jnp.int32), mine, wt])
    args = [x for pair in pairs for x in pair] + [gain, *map(hbm, weights), scale, ones]
    in_specs = [
        pl.BlockSpec(
            (step, d),
            lambda j, t, f, i=i: (jnp.where(j == i, t, jnp.where(j > i, tiles - 1, 0)), 0),
        )
        for i in range(count)
        for _ in range(2)
    ]
    in_specs += [pl.BlockSpec((1, d), full, pipeline_mode=once)]
    in_specs += [pl.BlockSpec(w.shape, full, pipeline_mode=once) for w in weights]
    in_specs += [
        pl.BlockSpec((1, width), full, pipeline_mode=once),
        pl.BlockSpec((1, 2 * width), full, pipeline_mode=once),
    ]
    aliases = {}
    if carried is not None:
        base = len(args) + 2
        args += [hbm(x) for x in (carried[3], *carried[:3])]
        in_specs += [pl.BlockSpec((rows, d), full, pipeline_mode=once)]
        in_specs += [pl.BlockSpec(memory_space=pl.ANY)] * 3
        aliases = {base: 0, base + 1: 1, base + 2: 2}
    return pl.pallas_call(
        functools.partial(
            project_kernel, count=count, halves=len(weights), width=width, fresh=carried is None
        ),
        out_shape=[
            pltpu.HBM((group_len, d), bf16),
            pltpu.HBM((group_len, width), bf16),
            pltpu.HBM((group_len, 2 * width), bf16),
            pltpu.HBM((rows, d), bf16),
        ],
        grid_spec=pltpu.PrefetchScalarGridSpec(
            num_scalar_prefetch=1,
            grid=(count, tiles),
            in_specs=in_specs,
            out_specs=[
                pl.BlockSpec((step, d), at),
                pl.BlockSpec((step, width), at),
                pl.BlockSpec((step, 2 * width), at),
                pl.BlockSpec((rows, d), full),
            ],
            scratch_shapes=[pltpu.VMEM((d, 3 * width), bf16)],
        ),
        input_output_aliases=aliases,
        compiler_params=pltpu.CompilerParams(vmem_limit_bytes=48 << 20),
        cost_estimate=cost(10),
        name="project",
    )(info, *args)


def tail_body(at, p0, p1, p2, p3, x_ref, g_ref, w_s, gain, outs):
    lo_ref, att_ref, nm_ref, gh_ref, act_ref, gp_ref, gr_ref, c0, c1, c2, c3, gg_ref = outs
    mine = at[0]
    pieces = (p0, p1, p2, p3)
    cols = p0.shape[1]
    nt = (((1,), (1,)), ((), ()))
    for i in range(4):

        @pl.when(mine == i)
        def _(i=i):
            att_ref[...] = jnp.concatenate([pieces[i ^ k][...] for k in range(4)], axis=1)

    resid = x_ref[...].astype(f32) + jnp.dot(att_ref[...], w_s[0], preferred_element_type=f32)
    inverse = lax.rsqrt(jnp.mean(resid * resid, axis=-1, keepdims=True) + epsilon)
    normed = (resid * inverse * gain[...]).astype(bf16)
    nm_ref[...] = normed
    hidden = jnp.dot(normed, w_s[1], preferred_element_type=f32)
    sig = 1.0 / (1.0 + jnp.exp(-hidden))
    active = (hidden * sig).astype(bf16)
    act_ref[...] = active
    lo_ref[...] = (resid + jnp.dot(active, w_s[2], preferred_element_type=f32)).astype(bf16)
    grad_active = lax.dot_general(g_ref[...], w_s[2], nt, preferred_element_type=f32)
    grad_hidden = (grad_active * sig * (1.0 + hidden * (1.0 - sig))).astype(bf16)
    gh_ref[...] = grad_hidden
    grad_normed = lax.dot_general(grad_hidden, w_s[1], nt, preferred_element_type=f32)
    gg_ref[...] += jnp.sum(grad_normed * resid * inverse, axis=0, keepdims=True)
    scaled = grad_normed * gain[...]
    grad_resid = (
        g_ref[...].astype(f32)
        + inverse * scaled
        - resid * (inverse * inverse * inverse) * jnp.mean(scaled * resid, axis=-1, keepdims=True)
    )
    gr_ref[...] = grad_resid
    grad_proj = grad_resid.astype(bf16)
    gp_ref[...] = grad_proj
    grad_att = lax.dot_general(grad_proj, w_s[0], nt, preferred_element_type=f32).astype(bf16)
    for i in range(4):

        @pl.when(mine == i)
        def _(i=i):
            for j, out in enumerate((c0, c1, c2, c3)):
                out[...] = grad_att[:, (i ^ j) * cols : ((i ^ j) + 1) * cols]


def tail_kernel(at, p0, p1, p2, p3, x_ref, g_ref, own, half, other, gain, *refs, rows, hrows):
    w_s = refs[-1]
    outs = refs[:-1]

    @pl.when(pl.program_id(0) == 0)
    def _():
        outs[-1][...] = jnp.zeros_like(outs[-1])
        w_s[:, pl.ds(pl.multiple_of(at[1], 16), rows), :] = own[...]
        w_s[:, pl.ds(pl.multiple_of(at[2], 16), hrows), :] = half[...]
        w_s[:, pl.ds(pl.multiple_of(at[3], 16), hrows), :] = other[...]

    tail_body(at, p0, p1, p2, p3, x_ref, g_ref, w_s, gain, outs)


def whole_tail_kernel(at, p0, p1, p2, p3, x_ref, g_ref, w, gain, *outs):
    @pl.when(pl.program_id(0) == 0)
    def _():
        outs[-1][...] = jnp.zeros_like(outs[-1])

    tail_body(at, p0, p1, p2, p3, x_ref, g_ref, w, gain, outs)


def tail(at, pieces, x, g, weights, gain, tile=256):
    rows, d = x.shape
    cols = pieces[0].shape[1]
    row = lambda i, m: (i, 0)
    once = pl.Buffered(1)
    whole = lambda *shape: pl.BlockSpec(shape, lambda i, m: (0,) * len(shape), pipeline_mode=once)
    wide = pl.BlockSpec((tile, d), row)
    slim = pl.BlockSpec((tile, cols), row)
    if len(weights) == 3:
        body = functools.partial(tail_kernel, rows=weights[0].shape[1], hrows=weights[1].shape[1])
        scratch = [pltpu.VMEM((3, d, d), bf16)]
    else:
        body = whole_tail_kernel
        scratch = []
    return pl.pallas_call(
        body,
        out_shape=[pltpu.HBM((rows, d), bf16)] * 6
        + [pltpu.HBM((rows, d), f32)]
        + [pltpu.HBM((rows, cols), bf16)] * 4
        + [pltpu.HBM((1, d), f32)],
        grid_spec=pltpu.PrefetchScalarGridSpec(
            num_scalar_prefetch=1,
            grid=(rows // tile,),
            in_specs=[slim] * 4 + [wide] * 2 + [whole(*w.shape) for w in weights] + [whole(1, d)],
            out_specs=[wide] * 7 + [slim] * 4 + [pl.BlockSpec((1, d), lambda i, m: (0, 0))],
            scratch_shapes=scratch,
        ),
        compiler_params=pltpu.CompilerParams(vmem_limit_bytes=52 << 20),
        cost_estimate=cost(0.01),
        name="tail",
    )(at, *pieces, hbm(x), g, *map(hbm, weights), gain)


tn_dims = (((0,), (0,)), ((), ()))


def share_kernel(col, l0, l1, l2, r0, r1, r2, out):
    for i, (left, right) in enumerate(((l0, r0), (l1, r1), (l2, r2))):

        @pl.when(pl.program_id(0) == i)
        def _(left=left, right=right):
            out[...] = lax.dot_general(
                left[...], right[...], tn_dims, preferred_element_type=f32
            ).astype(bf16)


def share(lefts, rights, col):
    rows, d = lefts[0].shape
    w = d // 2
    once = pl.Buffered(1)
    return pl.pallas_call(
        share_kernel,
        out_shape=pltpu.HBM((d, 3 * w), bf16),
        grid_spec=pltpu.PrefetchScalarGridSpec(
            num_scalar_prefetch=1,
            grid=(3,),
            in_specs=[pl.BlockSpec((rows, d), lambda i, c: (0, 0), pipeline_mode=once)] * 3
            + [pl.BlockSpec((rows, w), lambda i, c: (0, c[0]), pipeline_mode=once)] * 3,
            out_specs=pl.BlockSpec((d, w), lambda i, c: (0, i)),
        ),
        compiler_params=pltpu.CompilerParams(vmem_limit_bytes=40 << 20),
        cost_estimate=cost(0.01),
        name="share",
    )(col.reshape(1), *map(hbm, lefts), *map(hbm, rights))


def keep_kernel(col, l0, l1, l2, r0, r1, r2, got, out):
    for i, (left, right) in enumerate(((l0, r0), (l1, r1), (l2, r2))):

        @pl.when(pl.program_id(0) == i)
        def _(left=left, right=right):
            out[...] = (
                lax.dot_general(left[...], right[...], tn_dims, preferred_element_type=f32)
                + got[...].astype(f32)
            ).astype(bf16)


def keep(lefts, rights, got, col):
    rows, d = lefts[0].shape
    w = d // 2
    once = pl.Buffered(1)
    block = pl.BlockSpec((d, w), lambda i, c: (0, i))
    return pl.pallas_call(
        keep_kernel,
        out_shape=pltpu.HBM((d, 3 * w), bf16),
        grid_spec=pltpu.PrefetchScalarGridSpec(
            num_scalar_prefetch=1,
            grid=(3,),
            in_specs=[pl.BlockSpec((rows, d), lambda i, c: (0, 0), pipeline_mode=once)] * 3
            + [pl.BlockSpec((rows, w), lambda i, c: (0, c[0]), pipeline_mode=once)] * 3
            + [block],
            out_specs=block,
        ),
        compiler_params=pltpu.CompilerParams(vmem_limit_bytes=40 << 20),
        cost_estimate=cost(0.01),
        name="keep",
    )(col.reshape(1), *map(hbm, lefts), *map(hbm, rights), hbm(got))


def total_kernel(*refs, counts):
    out = refs[-1]
    start, column = 0, 0
    for count in counts:
        group = refs[start : start + count]
        start += count
        acc = jnp.zeros(group[0].shape[1:], f32)
        for ref in group:
            for i in range(ref.shape[0]):
                acc = acc + ref[i].astype(f32)
        out[:, column : column + acc.shape[1]] = acc.astype(bf16)
        column += acc.shape[1]


def total(groups):
    flat = [x for group in groups for x in group]
    rows = flat[0].shape[1]
    cuts = 2 if rows % 32 == 0 else 1
    width = sum(group[0].shape[2] for group in groups)
    return pl.pallas_call(
        functools.partial(total_kernel, counts=[len(group) for group in groups]),
        out_shape=pltpu.HBM((rows, width), bf16),
        grid=(cuts,),
        in_specs=[
            pl.BlockSpec((x.shape[0], rows // cuts, x.shape[2]), lambda i: (0, i, 0)) for x in flat
        ],
        out_specs=pl.BlockSpec((rows // cuts, width), lambda i: (i, 0)),
        compiler_params=pltpu.CompilerParams(vmem_limit_bytes=40 << 20),
        cost_estimate=cost(0.001),
        name="total",
    )(*flat)


def add_kernel(a_ref, b_ref, out):
    out[...] = (a_ref[...].astype(f32) + b_ref[...].astype(f32)).astype(bf16)


def add(a, b):
    return pl.pallas_call(
        add_kernel, out_shape=pltpu.HBM(a.shape, bf16), cost_estimate=CHEAP, name="add"
    )(a, b)


def pair_kernel(a_ref, b_ref, out):
    out[0] = a_ref[...]
    out[1] = b_ref[...]


def pair_up(a, b):
    return pl.pallas_call(
        pair_kernel, out_shape=pltpu.HBM((2,) + a.shape, bf16), cost_estimate=CHEAP, name="pair_up"
    )(a, b)


def by_bits(first, second, put):
    for i in range(2):
        for j in range(2):

            @pl.when((first == i) & (second == j))
            def _(i=i, j=j):
                put(i, j)


def place_kernel(at, own, own_x, mate, mate_x, o0, o1, o2):
    block = pl.program_id(0)
    slot = (block % 2) ^ at[1]
    w = o0.shape[2] // 2

    def put(other_x, core):
        refs = (own_x, mate_x) if other_x else (own, mate)
        for side in range(2):
            part = refs[side ^ core][slot].astype(f32)
            for i, out in enumerate((o0, o1, o2)):
                out[0, :, side * w : (side + 1) * w] = part[:, i * w : (i + 1) * w]

    by_bits((block // 2) ^ at[0], at[2], put)


def place_tail(arrays, at):
    _, h, width = arrays[0].shape
    d = width // 3 * 2
    whole = pl.BlockSpec((2, h, width), lambda i, m: (0, 0, 0), pipeline_mode=pl.Buffered(1))
    outs = pl.pallas_call(
        place_kernel,
        out_shape=[pltpu.HBM((4, h, d), f32)] * 3,
        grid_spec=pltpu.PrefetchScalarGridSpec(
            num_scalar_prefetch=1,
            grid=(4,),
            in_specs=[whole] * 4,
            out_specs=[pl.BlockSpec((1, h, d), lambda i, m: (i, 0, 0))] * 3,
        ),
        compiler_params=pltpu.CompilerParams(vmem_limit_bytes=40 << 20),
        cost_estimate=cost(0.001),
        name="place_tail",
    )(at, *arrays)
    return [out.reshape(4 * h, d) for out in outs]


def cross_kernel(at, x_ref, g_ref, *refs):
    s = refs[-1]
    s[...] = lax.dot_general(x_ref[...], g_ref[...], tn_dims, preferred_element_type=f32).astype(bf16)
    step = pl.program_id(0)
    half = s.shape[0] // 2
    for w in range(2):

        @pl.when(step == w)
        def _(w=w):
            for x in range(2):
                rows = pl.ds(pl.multiple_of((at[1] ^ x) * half, 16), half)
                refs[2 * w + x][...] = s[rows, :]


def cross(x, g, at):
    rows, d = x.shape
    w = d // 2
    block = pl.BlockSpec((w // 2, g.shape[1]), lambda i, m: (0, 0))
    return pl.pallas_call(
        cross_kernel,
        out_shape=[pltpu.HBM((w // 2, g.shape[1]), bf16)] * 4,
        grid_spec=pltpu.PrefetchScalarGridSpec(
            num_scalar_prefetch=1,
            grid=(2,),
            in_specs=[
                pl.BlockSpec((rows, w), lambda i, m: (0, m[0] ^ i)),
                pl.BlockSpec(g.shape, lambda i, m: (0, 0)),
            ],
            out_specs=[block] * 4,
            scratch_shapes=[pltpu.VMEM((w, g.shape[1]), bf16)],
        ),
        compiler_params=pltpu.CompilerParams(vmem_limit_bytes=40 << 20),
        cost_estimate=cost(0.001),
        name="cross",
    )(at, x, g)


def spread_kernel(at, *refs, groups, width):
    out = refs[-1]
    step = out.shape[1]
    rows = pl.ds(pl.multiple_of(pl.program_id(1) * step, step), step)

    def put(other_x, core):
        cut = []
        for t in range(3):
            for n in range(2):
                for c in range(2):
                    for g in range(groups):
                        part = refs[4 * g + other_x + 2 * (c ^ core)][n ^ at[1], rows, :]
                        cut.append(part[:, t * width : (t + 1) * width])
        out[0] = jnp.concatenate(cut, axis=1).astype(f32)

    by_bits(pl.program_id(0) ^ at[0], at[2], put)


def spread(arrays, at, used):
    flat = [x for group in arrays for x in group]
    groups = len(arrays)
    _, rows, cols = flat[0].shape
    width = 4 * groups * used
    cuts = 2 if rows % 32 == 0 else 1
    whole = pl.BlockSpec((2, rows, cols), lambda i, j, m: (0, 0, 0), pipeline_mode=pl.Buffered(1))
    return pl.pallas_call(
        functools.partial(spread_kernel, groups=groups, width=used // 3),
        out_shape=pltpu.HBM((2, rows, width), f32),
        grid_spec=pltpu.PrefetchScalarGridSpec(
            num_scalar_prefetch=1,
            grid=(2, cuts),
            in_specs=[whole] * len(flat),
            out_specs=pl.BlockSpec((1, rows // cuts, width), lambda i, j, m: (i, j, 0)),
        ),
        compiler_params=pltpu.CompilerParams(vmem_limit_bytes=40 << 20),
        cost_estimate=CHEAP,
        name="spread",
    )(at, *flat).reshape(2 * rows, width)


nt_dims = (((1,), (1,)), ((), ()))


def back_kernel(shards, *refs, groups, extra):
    grads, weights = refs[:groups], refs[groups : 2 * groups]
    out = refs[-1]
    acc = sum(
        lax.dot_general(g[...], w[...], nt_dims, preferred_element_type=f32)
        for g, w in zip(grads, weights)
    )
    if extra:
        acc = acc + refs[2 * groups][0].astype(f32)
    out[0] = acc.astype(bf16)


def back(grads, weights, shards, rows, got=None):
    groups = len(grads)
    d, c = weights[0].shape
    n = shards.shape[0]
    in_specs = [pl.BlockSpec((rows, c), lambda i, f: (f[i], 0))] * groups
    in_specs += [pl.BlockSpec((d, c), lambda i, f: (0, 0), pipeline_mode=pl.Buffered(1))] * groups
    args = [*grads, *weights]
    if got is not None:
        in_specs.append(pl.BlockSpec((1, rows, d), lambda i, f: (0, 0, 0)))
        args.append(got)
    return pl.pallas_call(
        functools.partial(back_kernel, groups=groups, extra=got is not None),
        out_shape=pltpu.HBM((n, rows, d), bf16),
        grid_spec=pltpu.PrefetchScalarGridSpec(
            num_scalar_prefetch=1,
            grid=(n,),
            in_specs=in_specs,
            out_specs=pl.BlockSpec((1, rows, d), lambda i, f: (i, 0, 0)),
        ),
        compiler_params=pltpu.CompilerParams(vmem_limit_bytes=40 << 20),
        cost_estimate=CHEAP,
        name="back",
    )(shards, *args)


def finish_kernel(shard, *refs, groups):
    grads, weights = refs[:groups], refs[groups : 2 * groups]
    core, near, x_ref, resid, gain, out, gain_out = refs[2 * groups :]
    grad = sum(
        lax.dot_general(g[...], w[...], nt_dims, preferred_element_type=f32)
        for g, w in zip(grads, weights)
    )
    grad = grad + core[0].astype(f32) + near[0].astype(f32)
    x = x_ref[...].astype(f32)
    inverse = lax.rsqrt(jnp.mean(x * x, axis=-1, keepdims=True) + epsilon)
    part = jnp.sum(grad * x * inverse, axis=0, keepdims=True)

    @pl.when(pl.program_id(0) == 0)
    def _():
        gain_out[...] = jnp.zeros_like(gain_out)

    gain_out[...] += part
    scaled = grad * gain[...]
    out[...] = (
        resid[...]
        + inverse * scaled
        - x * (inverse * inverse * inverse) * jnp.mean(scaled * x, axis=-1, keepdims=True)
    ).astype(bf16)


def finish(grads, weights, shard, core, near, x, resid, gain, tile=256):
    groups = len(grads)
    rows, d = x.shape
    c = weights[0].shape[1]
    tiles = rows // tile
    row = lambda i, f: (i, 0)
    once = pl.Buffered(1)
    return pl.pallas_call(
        functools.partial(finish_kernel, groups=groups),
        out_shape=[pltpu.HBM((rows, d), bf16), jax.ShapeDtypeStruct((1, d), f32)],
        grid_spec=pltpu.PrefetchScalarGridSpec(
            num_scalar_prefetch=1,
            grid=(tiles,),
            in_specs=[pl.BlockSpec((tile, c), lambda i, f: (f[0] * tiles + i, 0))] * groups
            + [pl.BlockSpec((d, c), lambda i, f: (0, 0), pipeline_mode=once)] * groups
            + [
                pl.BlockSpec((1, tile, d), lambda i, f: (1, i, 0)),
                pl.BlockSpec((1, tile, d), lambda i, f: (0, i, 0)),
                pl.BlockSpec((tile, d), row),
                pl.BlockSpec((tile, d), row),
                pl.BlockSpec((1, d), lambda i, f: (0, 0)),
            ],
            out_specs=[pl.BlockSpec((tile, d), row), pl.BlockSpec((1, d), lambda i, f: (0, 0))],
        ),
        compiler_params=pltpu.CompilerParams(vmem_limit_bytes=40 << 20),
        cost_estimate=CHEAP,
        name="finish",
    )(shard.reshape(1), *grads, *weights, core, near, x, resid, gain)


def rms_inverse(values):
    return lax.rsqrt(jnp.mean(values * values, axis=-1, keepdims=True) + epsilon)


def norm_back(values, inverse, grad_scaled):
    return inverse * grad_scaled - values * (inverse * inverse * inverse) * jnp.mean(
        grad_scaled * values, axis=-1, keepdims=True
    )


def dot(left, right):
    return jnp.dot(left, right, preferred_element_type=f32)


def times_trans(left, right):
    return lax.dot_general(left, right, (((1,), (1,)), ((), ())), preferred_element_type=f32)


def trans_times(left, right):
    return lax.dot_general(left, right, (((0,), (0,)), ((), ())), preferred_element_type=f32)


def rows_at(array, start, count):
    return lax.dynamic_slice_in_dim(array, start, count, 0)


def put_rows(array, rows, start):
    return lax.dynamic_update_slice_in_dim(array, rows, start, 0)


def make_local(sizes):
    def pairs(target):
        found = []
        for gx in range(sizes["gx"]):
            for gc in range(sizes["gc"]):
                for z in range(4):
                    for w in range(sizes["wt"]):
                        goal = target(gx, gc, z, w)
                        if goal is not None and goal != (gx, gc, z, w):
                            found.append((place(gx, gc, z, w), place(*goal)))
        return found

    def place(gx, gc, z, w):
        return ((gx * sizes["gc"] + gc) * 4 + z) * sizes["wt"] + w

    def send(value, target):
        return lax.ppermute(value, AXES, pairs(target))

    def move(value, target, still):
        return jnp.where(still, value, send(value, target))

    def core_mate(gx, gc, z, w):
        return (gx, 1 - gc, z, w)

    def x_mate(gx, gc, z, w):
        return (1 - gx, gc, z, w)

    def near_mate(gx, gc, z, w):
        return (gx, gc, z ^ 1, w)

    def far_mate(gx, gc, z, w):
        return (gx, gc, z ^ 2, w)

    def cross_mate(gx, gc, z, w):
        return (gx, 1 - gc, z ^ 1, w)

    def wt_mate(gx, gc, z, w):
        return (gx, gc, z, 1 - w)

    def wt_x_mate(gx, gc, z, w):
        return (1 - gx, gc, z, 1 - w)

    def to_host(gx, gc, z, w):
        return (gx, z & 1, 2 * gc + (z >> 1), w)

    def to_home(gx, gc, z, w):
        return (gx, z >> 1, 2 * (z & 1) + gc, w)

    def hop1(gx, gc, z, w):
        if gc == 0:
            return (gx, 0, z - 1, w) if z > 0 else None
        return (gx, 1, z + 1, w) if z < 3 else None

    def hop2(gx, gc, z, w):
        if gc == 0:
            return (gx, 0, z - 1, w) if z in (1, 2) else None
        return (gx, 1, z + 1, w) if z in (1, 2) else None

    def hop3(gx, gc, z, w):
        if gc == 0:
            return (gx, 0, z ^ 1, w) if z < 2 else None
        return (gx, 1, z ^ 1, w) if z > 1 else None

    def lane_share(gx, gc, z, w):
        return (gx, 1 - gc, z, w) if gc == z >> 1 else None

    def sum_all(value):
        for axis in AXES:
            step = 1
            while step < sizes[axis]:

                def mate(gx, gc, z, w, axis=axis, step=step):
                    at = dict(gx=gx, gc=gc, far=z >> 1, near=z & 1, wt=w)
                    at[axis] ^= step
                    return (at["gx"], at["gc"], 2 * at["far"] + at["near"], at["wt"])

                value = value + send(value, mate)
                step *= 2
        return value

    def local(
        tokens, segments, w_qkv, w_proj, w_in, w_out, gain_attn, gain_mlp, query_scale, cotangent
    ):
        gx, gc, host, near, wt = (lax.axis_index(axis) for axis in AXES)
        z = 2 * host + near
        mine = 2 * near + gc
        parts = 4
        nh = H // parts
        groups = 2
        rows = tokens.shape[1]
        group_len = segments.shape[1]
        wrows = w_qkv.shape[0]
        lane = gc == host
        pair = sizes["wt"] == 2

        def after(value, *others):
            return lax.optimization_barrier((value,) + others)[0]

        picked = pick(w_qkv, mine, parts, groups, nh)
        own = after(tokens[0], picked)
        got1 = send(own, hop1)
        own_share = send(own, lane_share)
        seg_mate = send(segments, core_mate)
        got2 = send(got1, hop2)
        got1_share = send(got1, lane_share)
        end = jnp.where(gc == 0, z == 0, z == 3)
        if pair:
            wide_own = stretch(picked, groups, nh, 2)
            got1 = after(got1, wide_own)
            other_w = send(picked, wt_mate)
            wide_w = (wide_own, stretch(other_w, groups, nh, 10))
        else:
            flat_all = lax.all_gather(picked, "wt", axis=0, tiled=True)[:, : 3 * nh * HD]
            each = flat_all.shape[1] // groups
            flat_w = [
                jnp.pad(flat_all[:, g * each : (g + 1) * each], ((0, 0), (0, lanes_up(each) - each)))
                for g in range(groups)
            ]
            by_head = jnp.transpose(flat_all.reshape(D, groups, 3, nh // groups, HD), (0, 2, 1, 3, 4))
            wide_w = (
                jnp.pad(
                    by_head.reshape(D, 3 * nh, HD), ((0, 0), (0, 0), (0, LN - HD))
                ).reshape(D, -1),
            )
        got3 = send(jnp.where(end, own, got2), hop3)
        got2_share = send(got2, lane_share)
        way = 1 - 2 * host
        last = jnp.where(host == 0, jnp.where(z == 0, 3, 0), jnp.where(z == 3, 0, 3))
        places = (z, z + way, z + 2 * way, last)

        half_rows = wrows // 2
        tail_own = jnp.stack([w_proj, w_in, w_out])
        half_w = lax.dynamic_slice_in_dim(tail_own, gc * half_rows, half_rows, 1)
        if pair:
            half_w = send(after(half_w, other_w), wt_mate)
        else:
            half_w = lax.all_gather(half_w, "wt", axis=0, tiled=False)

        dim_scale = scale_base / math.sqrt(HD) * jax.nn.softplus(query_scale)
        lane_scale = jnp.tile(jnp.pad(dim_scale * log2e, (0, LN - HD)), nh)[None]
        ones = jnp.tile(
            ((jnp.arange(LN) >= HD) & (jnp.arange(LN) < HD + 3)).astype(f32), 2 * nh
        )[None]
        seg_row = jnp.where(lane, segments, seg_mate)[0]
        fixed = (lane, mine, wt, gain_attn[None], wide_w, lane_scale, ones, group_len)
        carried = project(((own, own_share), (got1, got1_share)), places[:2], *fixed)
        got2_share = after(got2_share, carried[0])
        got3_share = send(after(got3, carried[0]), lane_share)
        carried = project(((got2, got2_share),), places[2:3], *fixed, carried=carried)
        all_normed, queries, keyval, inputs = project(
            ((got3, after(got3_share, carried[0])),), places[3:], *fixed, carried=carried
        )
        still = lane & end
        grad_mlp = move(after(cotangent[0], got3), to_host, still)

        att, att_float, q_aug = attn_fwd(queries, keyval, seg_row, nh)
        att = after(att, grad_mlp)
        if pair:
            flat_w = order(after(picked, att), other_w, wt, groups, nh)

        trades = (core_mate, near_mate, cross_mate)
        att_pieces = [rows_at(att, (mine ^ j) * rows, rows) for j in range(parts)]
        att_pieces = [att_pieces[0]] + [send(att_pieces[j + 1], trades[j]) for j in range(3)]
        half_mate = send(after(half_w, att_pieces[1]), core_mate)
        if pair:
            weights = (tail_own, half_w, half_mate)
            starts = (wt * wrows, (1 - wt) * wrows + gc * half_rows, (1 - wt) * wrows + (1 - gc) * half_rows)
        else:
            one = gc == 0
            tail_w = jnp.stack(
                [jnp.where(one, half_w, half_mate), jnp.where(one, half_mate, half_w)], axis=1
            )
            weights = (jnp.transpose(tail_w, (2, 0, 1, 3, 4)).reshape(3, D, D),)
            starts = ()
        (
            layer_out,
            attended,
            normed_mlp,
            grad_hidden,
            active,
            grad_proj,
            grad_resid,
            *pieces,
            grad_gain_mlp,
        ) = tail(
            jnp.stack([mine, *starts]), att_pieces, after(inputs, flat_w[0]), grad_mlp, weights, gain_mlp[None]
        )
        pieces = [pieces[0]] + [send(pieces[j + 1], trades[j]) for j in range(3)]

        lefts = (after(attended, pieces[1]), normed_mlp, active)
        rights = (grad_proj, grad_hidden, grad_mlp)
        shared = share(lefts, rights, 1 - gc)
        from_core = send(shared, core_mate)
        pieces[2:] = [after(piece, shared) for piece in pieces[2:]]
        home_out = send(after(layer_out, *pieces[1:]), to_home)
        prepared = prep(pieces, att_float, mine, nh)
        summed = keep(lefts, rights, after(from_core, prepared), gc)
        kept = lax.all_to_all(summed, ("wt", "gx", "near"), 0, 0, tiled=True)

        scale_row = jnp.tile(dim_scale, nh // groups)[None]

        def backward(group, *others):
            return attn_bwd(
                q_aug, keyval, after(prepared, summed, *others), seg_row, scale_row, nh, group, groups
            )

        def by_rows(grad):
            if pair:
                own, *rest = cross(all_normed, grad, jnp.stack([wt, gx]))
                got = [send(part, mate) for part, mate in zip(rest, (x_mate, wt_mate, wt_x_mate))]
                return [part[None] for part in (own, *got)]
            part = trans_times(all_normed, grad).astype(bf16)
            sources = sizes["wt"] * 2
            got = lax.all_to_all(part, ("wt", "gx"), 0, 0, tiled=True)
            return [got.reshape(sources, D // sources, -1)]

        grad_a, lanes_a = backward(0)
        layer_out = jnp.where(still, after(layer_out, grad_a), home_out)
        rows_a = by_rows(after(grad_a, layer_out))
        grad_b, lanes_b = backward(1, rows_a[0])
        last_step = [grad_b]

        def turn(value):
            return after(value, *last_step)

        def done(value):
            last_step[0] = value
            return value

        grads = (grad_a, grad_b)
        rows_a[0] = turn(rows_a[0])
        a1 = done(total([rows_a]))
        a1_far = send(a1, far_mate)
        to_core = done(back((grad_a, turn(grad_b)), flat_w, jnp.stack([mine ^ 3, mine ^ 1]), rows))
        from_core = send(to_core, core_mate)
        sources = sizes["wt"] * 4
        t1 = done(total([[turn(kept).reshape(sources, D // sources, -1)]]))
        t1_far = send(t1, far_mate)
        to_near = done(back(grads, flat_w, (mine ^ 2).reshape(1), rows, turn(from_core)))
        from_near = send(to_near, near_mate)
        rows_b = by_rows(turn(grad_b))
        done(rows_b[0])
        a2 = done(add(turn(a1), a1_far))
        a2_near = send(a2, near_mate)
        rows_b[0] = turn(rows_b[0])
        b1 = done(total([rows_b]))
        b1_far = send(b1, far_mate)
        t2 = done(add(turn(t1), t1_far))
        t2_near = send(t2, near_mate)
        a4 = done(pair_up(turn(a2), a2_near))
        a4_x = send(a4, x_mate)
        a4_core = send(a4, core_mate)
        grad_tokens, grad_gain_attn = finish(
            grads, flat_w, mine, from_core, turn(from_near), inputs, grad_resid, gain_attn[None]
        )
        done(grad_tokens)
        home_grad = send(grad_tokens, to_home)
        t4 = done(pair_up(turn(t2), t2_near))
        t4_x = send(t4, x_mate)
        t4_core = send(t4, core_mate)
        b2 = done(add(turn(b1), b1_far))
        b2_near = send(b2, near_mate)
        a4_x = done(turn(a4_x))
        a4_cross = send(a4_x, core_mate)
        b4 = done(pair_up(turn(b2), b2_near))
        b4_x = send(b4, x_mate)
        b4_core = send(b4, core_mate)
        grad_tokens = done(jnp.where(still, turn(grad_tokens), home_grad))
        t4_x = done(turn(t4_x))
        t4_cross = send(t4_x, core_mate)
        b4_x = done(turn(b4_x))
        b4_cross = send(b4_x, core_mate)
        at = jnp.stack([gx, near, gc])
        totals = place_tail((turn(t4), t4_x, t4_core, t4_cross), at)
        done(totals[0])
        total_qkv = spread(
            [(turn(a4), a4_x, a4_core, a4_cross), (b4, b4_x, b4_core, b4_cross)], at, 3 * nh // groups * HD
        )

        grad_query_scale = (
            (lanes_a + lanes_b)[0, :HD]
            / (dim_scale * log2e)
            * (scale_base / math.sqrt(HD))
            * jax.nn.sigmoid(query_scale)
        )
        small = jnp.concatenate(
            [grad_gain_attn[0], grad_gain_mlp[0], jnp.pad(grad_query_scale, (0, LN - HD))]
        ).reshape(-1, LN)
        small = sum_all(small).reshape(-1)
        return (
            layer_out[None],
            grad_tokens[None],
            total_qkv,
            *totals,
            small[:D],
            small[D : 2 * D],
            small[2 * D : 2 * D + HD],
        )

    return local


def solution(mesh):
    groups, parts, wt = (mesh.shape[axis] for axis in ("grp", "ctx", "wt"))
    inner = Mesh(mesh.devices.reshape(groups // 2, 2, parts // 2, 2, wt), AXES)
    sizes = dict(inner.shape)
    split = P(("gx", "gc", "wt"), ("far", "near"), None)
    weight = P("wt", None)
    return jax.shard_map(
        make_local(sizes),
        mesh=inner,
        in_specs=(
            split,
            P(("gx", "gc", "wt"), None),
            weight,
            weight,
            weight,
            weight,
            P(),
            P(),
            P(),
            split,
        ),
        out_specs=(split, split, weight, weight, weight, weight, P(), P(), P()),
        check_vma=False,
    )
```

```python
import functools
import math

import jax
import jax.numpy as jnp
from jax import lax
from jax.experimental import pallas as pl
from jax.experimental.pallas import tpu as pltpu
from jax.sharding import Mesh
from jax.sharding import PartitionSpec as P

D = 1280
H = 16
HD = 80
LN = 128
epsilon = 1e-06
scale_base = 1.442695041
log2e = 1.4426950408889634
NEG = -1e30
def cost(us):
    return pl.CostEstimate(flops=int(us * 1_000_000_000), transcendentals=0, bytes_accessed=1000)


CHEAP = cost(0.001)
f32 = jnp.float32
bf16 = jnp.bfloat16
AXES = ("gx", "gc", "far", "near", "wt")


def hbm(x):
    return pltpu.with_memory_space_constraint(x, pltpu.HBM)


def block_flags(seg_row, bq, bk):
    n = seg_row.shape[0]
    q = seg_row.reshape(n // bq, bq)
    k = seg_row.reshape(n // bk, bk)
    qf, ql = q[:, 0][:, None], q[:, -1][:, None]
    kf, kl = k[:, 0][None], k[:, -1][None]
    qs = jnp.arange(n // bq, dtype=jnp.int32)[:, None] * bq
    ks = jnp.arange(n // bk, dtype=jnp.int32)[None] * bk
    below = ks + bk - 1 <= qs
    skip = (ks > qs + bq - 1) | ((kf > 0) & (kl < qf))
    same = (qf == ql) & (kl == ql) & ((kf == kl) | ((kf == 0) & (kl == 1)))
    full = below & ((kl == 0) | same)
    return jnp.where(skip, 0, jnp.where(full, 1, 2)).astype(jnp.int32).reshape(-1)


def put_split(base, col, lanes):
    hi = col.astype(bf16).astype(f32)
    rest = col - hi
    mid = rest.astype(bf16).astype(f32)
    out = jnp.where(lanes == HD, hi, base)
    out = jnp.where(lanes == HD + 1, mid, out)
    return jnp.where(lanes == HD + 2, rest - mid, out).astype(bf16)


def fwd_kernel(flags, q_ref, kv, segc, segr, att, of, qaug, m_s, acc_s, *, nh, bq, bk, nk):
    qi = pl.program_id(0)
    count = (qi * bq + bq + bk - 1) // bk
    nt = (((1,), (1,)), ((), ()))
    acc_s[...] = jnp.zeros_like(acc_s)
    m_s[...] = jnp.zeros_like(m_s)

    def mask(ko):
        qpos = qi * bq + lax.broadcasted_iota(jnp.int32, (bq, bk), 0)
        kpos = ko + lax.broadcasted_iota(jnp.int32, (bq, bk), 1)
        ks = segr[:, pl.ds(ko, bk)]
        return (kpos <= qpos) & ((ks == 0) | (ks == segc[...]))

    def step(kb, masked):
        ko = pl.multiple_of(kb * bk, bk)
        if masked:
            allowed = mask(ko)
        for h in range(nh):
            k = kv[pl.ds(ko, bk), h * LN : (h + 1) * LN]
            v = kv[pl.ds(ko, bk), (nh + h) * LN : (nh + h + 1) * LN]
            s = lax.dot_general(q_ref[:, h * LN : (h + 1) * LN], k, nt, preferred_element_type=f32)
            p = jnp.exp2(s)
            if masked:
                p = jnp.where(allowed, p, 0.0)
            acc_s[h] += jnp.dot(p.astype(bf16), v, preferred_element_type=f32)

    def body(kb, carry):
        flag = flags[qi * nk + kb]

        @pl.when(flag == 1)
        def _():
            step(kb, False)

        @pl.when(flag == 2)
        def _():
            step(kb, True)

        return carry

    lax.fori_loop(0, count, body, 0)
    bad = jnp.zeros((bq, 1), f32)
    for h in range(nh):
        total = acc_s[h][:, HD : HD + 1]
        bad = jnp.maximum(bad, jnp.where((total > 2.0**-60) & (total < 2.0**60), 0.0, 1.0))

    @pl.when(jnp.max(bad) > 0.0)
    def _():
        def head(h, carry):
            kc = pl.ds(pl.multiple_of(h * LN, LN), LN)
            vc = pl.ds(pl.multiple_of((nh + h) * LN, LN), LN)
            m_s[h] = jnp.full((bq, LN), NEG, f32)
            acc_s[h] = jnp.zeros((bq, LN), f32)

            def inner(kb, carry):
                @pl.when(flags[qi * nk + kb] > 0)
                def _():
                    ko = pl.multiple_of(kb * bk, bk)
                    s = lax.dot_general(
                        q_ref[:, kc], kv[pl.ds(ko, bk), kc], nt, preferred_element_type=f32
                    )
                    s = jnp.where(mask(ko), s, NEG)
                    old = m_s[h]
                    new = jnp.maximum(old, jnp.max(s, axis=1, keepdims=True))
                    p = jnp.exp2(s - new[:, :1]).astype(bf16)
                    m_s[h] = new
                    acc_s[h] = acc_s[h] * jnp.exp2(old - new) + jnp.dot(
                        p, kv[pl.ds(ko, bk), vc], preferred_element_type=f32
                    )

                return carry

            lax.fori_loop(0, count, inner, 0)
            return carry

        lax.fori_loop(0, nh, head, 0)

    lanes = lax.broadcasted_iota(jnp.int32, (bq, LN), 1)
    outs = []
    for h in range(nh):
        acc = acc_s[h]
        total = acc[:, HD : HD + 1]
        out = acc * (1.0 / total)
        of[:, h * LN : (h + 1) * LN] = jnp.where(lanes < HD, out, 0.0).astype(bf16)
        outs.append(out[:, :HD])
        lse = m_s[h][:, :1] + jnp.log2(total)
        qaug[:, h * LN : (h + 1) * LN] = put_split(
            q_ref[:, h * LN : (h + 1) * LN].astype(f32), -lse, lanes
        )
    att[...] = jnp.concatenate(outs, axis=1).astype(bf16)


def attn_fwd(q, kv, seg_row, nh, bq=512, bk=512):
    n = q.shape[0]
    w = nh * LN
    spec = pltpu.PrefetchScalarGridSpec(
        num_scalar_prefetch=1,
        grid=(n // bq,),
        in_specs=[
            pl.BlockSpec((bq, w), lambda i, f: (i, 0)),
            pl.BlockSpec((n, 2 * w), lambda i, f: (0, 0)),
            pl.BlockSpec((bq, 1), lambda i, f: (i, 0)),
            pl.BlockSpec((1, n), lambda i, f: (0, 0)),
        ],
        out_specs=[
            pl.BlockSpec((bq, nh * HD), lambda i, f: (i, 0)),
            pl.BlockSpec((bq, w), lambda i, f: (i, 0)),
            pl.BlockSpec((bq, w), lambda i, f: (i, 0)),
        ],
        scratch_shapes=[pltpu.VMEM((nh, bq, LN), f32), pltpu.VMEM((nh, bq, LN), f32)],
    )
    return pl.pallas_call(
        functools.partial(fwd_kernel, nh=nh, bq=bq, bk=bk, nk=n // bk),
        out_shape=[
            pltpu.HBM((n, nh * HD), bf16),
            pltpu.HBM((n, w), bf16),
            pltpu.HBM((n, w), bf16),
        ],
        grid_spec=spec,
        compiler_params=pltpu.CompilerParams(vmem_limit_bytes=40 << 20),
        cost_estimate=cost(0.01),
        name="attn_fwd",
    )(block_flags(seg_row, bq, bk), hbm(q), hbm(kv), seg_row[:, None], seg_row[None])


def bwd_kernel(
    flags, mine, qa, kk, vv, do0, do1, do2, do3, of, segc, segr, scale, dqkv, gscale, doa_s, dq_s, dk_s, dv_s, *, first, nh, bq, bk, n
):
    nk = n // bk
    nq = n // bq
    kb = pl.program_id(0)
    part = n // 4
    step_rows = 256 if part % 256 == 0 else part
    lanes = lax.broadcasted_iota(jnp.int32, (step_rows, LN), 1)

    @pl.when(kb == 0)
    def _():
        dq_s[...] = jnp.zeros_like(dq_s)
        for j, piece in enumerate((do0, do1, do2, do3)):
            start = (mine[0] ^ j) * part
            for i in range(part // step_rows):
                d = piece[i * step_rows : (i + 1) * step_rows, :].astype(f32)
                r = pl.ds(pl.multiple_of(start + i * step_rows, step_rows), step_rows)
                for h in range(nh):
                    at = (first + h) * HD
                    dh = jnp.concatenate(
                        [d[:, at : at + HD], jnp.zeros((step_rows, LN - HD), f32)], axis=1
                    )
                    c = slice(h * LN, (h + 1) * LN)
                    delta = jnp.sum(dh * of[r, c].astype(f32), axis=1, keepdims=True)
                    doa_s[r, c] = put_split(dh, -delta, lanes)

    dk_s[...] = jnp.zeros_like(dk_s)
    dv_s[...] = jnp.zeros_like(dv_s)
    ko = kb * bk
    nt = (((1,), (1,)), ((), ()))
    tn = (((0,), (0,)), ((), ()))

    def step(qi, masked):
        qo = pl.multiple_of(qi * bq, bq)
        if masked:
            kpos = ko + lax.broadcasted_iota(jnp.int32, (bk, bq), 0)
            qpos = qo + lax.broadcasted_iota(jnp.int32, (bk, bq), 1)
            ks = segc[...]
            allowed = (kpos <= qpos) & ((ks == 0) | (ks == segr[:, pl.ds(qo, bq)]))
        for h in range(nh):
            c = slice(h * LN, (h + 1) * LN)
            q = qa[pl.ds(qo, bq), c]
            k = kk[:, c]
            d = doa_s[pl.ds(qo, bq), c]
            p = jnp.exp2(lax.dot_general(k, q, nt, preferred_element_type=f32))
            if masked:
                p = jnp.where(allowed, p, 0.0)
            ds = (p * lax.dot_general(vv[:, c], d, nt, preferred_element_type=f32)).astype(bf16)
            dv_s[h] += jnp.dot(p.astype(bf16), d, preferred_element_type=f32)
            dk_s[h] += jnp.dot(ds, q, preferred_element_type=f32)
            dq_s[h, pl.ds(qo, bq), :] += lax.dot_general(ds, k, tn, preferred_element_type=f32)

    def body(qi, carry):
        flag = flags[qi * nk + kb]

        @pl.when(flag == 1)
        def _():
            step(qi, False)

        @pl.when(flag == 2)
        def _():
            step(qi, True)

        return carry

    lax.fori_loop(ko // bq, nq, body, 0)
    r = pl.multiple_of(ko, bk)
    ln2 = math.log(2.0)
    gap = dqkv.shape[1] - 3 * nh * HD
    dqkv[pl.ds(r, bk), nh * HD :] = jnp.concatenate(
        [dk_s[h][:, :HD] * ln2 for h in range(nh)]
        + [dv_s[h][:, :HD] for h in range(nh)]
        + [jnp.zeros((bk, gap), f32)],
        axis=1,
    ).astype(bf16)

    @pl.when(kb == nk - 1)
    def _():
        total = jnp.zeros((1, LN), f32)
        for i in range(nq):
            rows = slice(i * bq, (i + 1) * bq)
            for h in range(nh):
                total = total + jnp.sum(
                    dq_s[h, rows, :] * qa[rows, h * LN : (h + 1) * LN].astype(f32), axis=0, keepdims=True
                )
            grads = jnp.concatenate([dq_s[h, rows, :][:, :HD] for h in range(nh)], axis=1)
            dqkv[rows, 0 : nh * HD] = (grads * scale[...]).astype(bf16)
        gscale[...] = jnp.broadcast_to(total, gscale.shape)


def attn_bwd(qa, kv, pieces, of, mine, seg_row, scale, heads, group, groups, bq=512, bk=512):
    n = qa.shape[0]
    nh = heads // groups
    w = nh * LN
    once = pl.Buffered(1)
    spec = pltpu.PrefetchScalarGridSpec(
        num_scalar_prefetch=2,
        grid=(n // bk,),
        in_specs=[
            pl.BlockSpec((n, w), lambda i, f, m: (0, group), pipeline_mode=once),
            pl.BlockSpec((bk, w), lambda i, f, m: (i, group)),
            pl.BlockSpec((bk, w), lambda i, f, m: (i, groups + group)),
            *[pl.BlockSpec((n // 4, heads * HD), lambda i, f, m: (0, 0), pipeline_mode=once)] * 4,
            pl.BlockSpec((n, w), lambda i, f, m: (0, group), pipeline_mode=once),
            pl.BlockSpec((bk, 1), lambda i, f, m: (i, 0)),
            pl.BlockSpec((1, n), lambda i, f, m: (0, 0)),
            pl.BlockSpec((1, nh * HD), lambda i, f, m: (0, 0)),
        ],
        out_specs=[
            pl.BlockSpec((n, lanes_up(3 * nh * HD)), lambda i, f, m: (0, 0)),
            pl.BlockSpec((8, LN), lambda i, f, m: (0, 0)),
        ],
        scratch_shapes=[
            pltpu.VMEM((n, w), bf16),
            pltpu.VMEM((nh, n, LN), f32),
            pltpu.VMEM((nh, bk, LN), f32),
            pltpu.VMEM((nh, bk, LN), f32),
        ],
    )
    return pl.pallas_call(
        functools.partial(bwd_kernel, first=group * nh, nh=nh, bq=bq, bk=bk, n=n),
        out_shape=[
            pltpu.HBM((n, lanes_up(3 * nh * HD)), bf16),
            pltpu.HBM((8, LN), f32),
        ],
        grid_spec=spec,
        compiler_params=pltpu.CompilerParams(vmem_limit_bytes=48 << 20),
        cost_estimate=cost(300 if group == 0 else 0.001),
        name="attn_bwd",
    )(block_flags(seg_row, bq, bk), mine.reshape(1), hbm(qa), hbm(kv), hbm(kv), *pieces, hbm(of), seg_row[:, None], seg_row[None], scale)


def quarter_columns(place, parts, groups, nh):
    width = nh // groups * HD
    return [
        (t * D + place * nh * HD + g * width, width) for g in range(groups) for t in range(3)
    ]


def pick_kernel(mine, w_ref, out, *, parts, groups, nh):
    for i in range(parts):

        @pl.when(mine[0] == i)
        def _(i=i):
            cut = [w_ref[:, a : a + width] for a, width in quarter_columns(i, parts, groups, nh)]
            used = sum(x.shape[1] for x in cut)
            pad = jnp.zeros((cut[0].shape[0], out.shape[1] - used), out.dtype)
            out[...] = jnp.concatenate(cut + [pad], axis=1)


def lanes_up(n):
    return -(-n // LN) * LN


def pick(w, mine, parts, groups, nh):
    rows = w.shape[0]
    step = 160 if rows % 160 == 0 else rows
    return pl.pallas_call(
        functools.partial(pick_kernel, parts=parts, groups=groups, nh=nh),
        out_shape=pltpu.HBM((rows, lanes_up(3 * nh * HD)), w.dtype),
        grid_spec=pltpu.PrefetchScalarGridSpec(
            num_scalar_prefetch=1,
            grid=(rows // step,),
            in_specs=[pl.BlockSpec((step, 3 * D), lambda i, m: (i, 0))],
            out_specs=pl.BlockSpec((step, lanes_up(3 * nh * HD)), lambda i, m: (i, 0)),
        ),
        cost_estimate=cost(5),
        name="pick",
    )(mine.reshape(1), hbm(w))


def stretch_kernel(x_ref, out, *, groups, nh):
    value = x_ref[...]
    each = 3 * nh * HD // groups
    zero = jnp.zeros((value.shape[0], LN - HD), value.dtype)
    per = nh // groups
    wide = []
    for t in range(3):
        for h in range(nh):
            at = (h // per) * each + t * per * HD + (h % per) * HD
            wide += [value[:, at : at + HD], zero]
    out[...] = jnp.concatenate(wide, axis=1)


def stretch(x, groups, nh, us):
    rows, width = x.shape
    step = 160
    return pl.pallas_call(
        functools.partial(stretch_kernel, groups=groups, nh=nh),
        out_shape=pltpu.HBM((rows, 3 * nh * LN), x.dtype),
        grid=(rows // step,),
        in_specs=[pl.BlockSpec((step, width), lambda i: (i, 0))],
        out_specs=pl.BlockSpec((step, 3 * nh * LN), lambda i: (i, 0)),
        cost_estimate=cost(us),
        name="stretch",
    )(hbm(x))


def order_kernel(own_first, a_ref, b_ref, *outs, each):
    def put(ref):
        value = ref[...]
        for g, out in enumerate(outs):
            gap = jnp.zeros((value.shape[0], out.shape[1] - each), value.dtype)
            out[...] = jnp.concatenate([value[:, g * each : (g + 1) * each], gap], axis=1)

    half = pl.program_id(0)

    @pl.when(half == 0)
    def _():
        put(a_ref)

    @pl.when(half == 1)
    def _():
        put(b_ref)


def order(own, other, own_at, groups, nh):
    rows, width = own.shape
    step = 320
    n = rows // step
    at = lambda i, j, m: ((i ^ m[0]) * n + j, 0)
    each = 3 * nh * HD // groups
    return pl.pallas_call(
        functools.partial(order_kernel, each=each),
        out_shape=[pltpu.HBM((2 * rows, lanes_up(each)), own.dtype)] * groups,
        grid_spec=pltpu.PrefetchScalarGridSpec(
            num_scalar_prefetch=1,
            grid=(2, n),
            in_specs=[
                pl.BlockSpec((step, width), lambda i, j, m: (j * (1 - i), 0)),
                pl.BlockSpec((step, width), lambda i, j, m: (j * i, 0)),
            ],
            out_specs=[pl.BlockSpec((step, lanes_up(each)), at)] * groups,
        ),
        cost_estimate=cost(3),
        name="order",
    )(own_at.reshape(1), hbm(own), hbm(other))


def project_kernel(info, *refs, count, halves, width, fresh):
    pairs = refs[: 2 * count]
    gain = refs[2 * count]
    weights = refs[2 * count + 1 : 2 * count + 1 + halves]
    scale, ones = refs[2 * count + 1 + halves : 2 * count + 3 + halves]
    normed_ref, q_ref, kv_ref, mine_ref, w = refs[-5:]
    j, tile = pl.program_id(0), pl.program_id(1)
    step = normed_ref.shape[0]

    @pl.when((j == 0) & (tile == 0))
    def _():
        for i, ref in enumerate(weights):
            h = ref.shape[0]
            start = (info[count + 2] ^ i) * h if halves == 2 else 0
            w[pl.ds(pl.multiple_of(start, 16), h), :] = ref[...]
        if not fresh:
            mine_ref[...] = refs[2 * count + 3 + halves][...]

    def work(x_ref):
        value = x_ref[...]
        x = value.astype(f32)
        inverse = lax.rsqrt(jnp.mean(x * x, axis=-1, keepdims=True) + epsilon)
        normed = (x * inverse * gain[...]).astype(bf16)
        normed_ref[...] = normed
        q_ref[...] = (
            jnp.dot(normed, w[:, :width], preferred_element_type=f32) * scale[...]
        ).astype(bf16)
        kv_ref[...] = (
            jnp.dot(normed, w[:, width:], preferred_element_type=f32) + ones[...]
        ).astype(bf16)

        @pl.when(info[count + 1] == info[j])
        def _():
            mine_ref[pl.ds(pl.multiple_of(tile * step, step), step), :] = value

    for i in range(count):
        for lane in range(2):

            @pl.when((j == i) & (info[count] == lane))
            def _(i=i, lane=lane):
                work(pairs[2 * i + 1 - lane])


def project(pairs, places, lane, mine, wt, gain, weights, scale, ones, group_len, carried=None):
    count = len(pairs)
    rows, d = pairs[0][0].shape
    width = scale.shape[1]
    step = 256
    tiles = rows // step
    full = lambda j, t, f: (0, 0)
    at = lambda j, t, f: (f[j] * tiles + t, 0)
    once = pl.Buffered(1)
    info = jnp.stack(list(places) + [lane.astype(jnp.int32), mine, wt])
    args = [x for pair in pairs for x in pair] + [gain, *map(hbm, weights), scale, ones]
    in_specs = [
        pl.BlockSpec(
            (step, d),
            lambda j, t, f, i=i: (jnp.where(j == i, t, jnp.where(j > i, tiles - 1, 0)), 0),
        )
        for i in range(count)
        for _ in range(2)
    ]
    in_specs += [pl.BlockSpec((1, d), full, pipeline_mode=once)]
    in_specs += [pl.BlockSpec(w.shape, full, pipeline_mode=once) for w in weights]
    in_specs += [
        pl.BlockSpec((1, width), full, pipeline_mode=once),
        pl.BlockSpec((1, 2 * width), full, pipeline_mode=once),
    ]
    aliases = {}
    if carried is not None:
        base = len(args) + 2
        args += [hbm(x) for x in (carried[3], *carried[:3])]
        in_specs += [pl.BlockSpec((rows, d), full, pipeline_mode=once)]
        in_specs += [pl.BlockSpec(memory_space=pl.ANY)] * 3
        aliases = {base: 0, base + 1: 1, base + 2: 2}
    return pl.pallas_call(
        functools.partial(
            project_kernel, count=count, halves=len(weights), width=width, fresh=carried is None
        ),
        out_shape=[
            pltpu.HBM((group_len, d), bf16),
            pltpu.HBM((group_len, width), bf16),
            pltpu.HBM((group_len, 2 * width), bf16),
            pltpu.HBM((rows, d), bf16),
        ],
        grid_spec=pltpu.PrefetchScalarGridSpec(
            num_scalar_prefetch=1,
            grid=(count, tiles),
            in_specs=in_specs,
            out_specs=[
                pl.BlockSpec((step, d), at),
                pl.BlockSpec((step, width), at),
                pl.BlockSpec((step, 2 * width), at),
                pl.BlockSpec((rows, d), full),
            ],
            scratch_shapes=[pltpu.VMEM((d, 3 * width), bf16)],
        ),
        input_output_aliases=aliases,
        compiler_params=pltpu.CompilerParams(vmem_limit_bytes=48 << 20),
        cost_estimate=cost(10),
        name="project",
    )(info, *args)


def tail_body(at, p0, p1, p2, p3, x_ref, g_ref, w_s, gain, outs):
    lo_ref, left_ref, right_ref, gr_ref, c0, c1, c2, c3, gg_ref = outs
    att_ref, nm_ref, act_ref = (left_ref.at[i] for i in range(3))
    gp_ref, gh_ref = (right_ref.at[i] for i in range(2))
    right_ref[2] = g_ref[...]
    mine = at[0]
    pieces = (p0, p1, p2, p3)
    cols = p0.shape[1]
    nt = (((1,), (1,)), ((), ()))
    for i in range(4):

        @pl.when(mine == i)
        def _(i=i):
            att_ref[...] = jnp.concatenate([pieces[i ^ k][...] for k in range(4)], axis=1)

    resid = x_ref[...].astype(f32) + jnp.dot(att_ref[...], w_s[0], preferred_element_type=f32)
    inverse = lax.rsqrt(jnp.mean(resid * resid, axis=-1, keepdims=True) + epsilon)
    normed = (resid * inverse * gain[...]).astype(bf16)
    nm_ref[...] = normed
    hidden = jnp.dot(normed, w_s[1], preferred_element_type=f32)
    sig = 1.0 / (1.0 + jnp.exp(-hidden))
    active = (hidden * sig).astype(bf16)
    act_ref[...] = active
    lo_ref[...] = (resid + jnp.dot(active, w_s[2], preferred_element_type=f32)).astype(bf16)
    grad_active = lax.dot_general(g_ref[...], w_s[2], nt, preferred_element_type=f32)
    grad_hidden = (grad_active * sig * (1.0 + hidden * (1.0 - sig))).astype(bf16)
    gh_ref[...] = grad_hidden
    grad_normed = lax.dot_general(grad_hidden, w_s[1], nt, preferred_element_type=f32)
    gg_ref[...] += jnp.sum(grad_normed * resid * inverse, axis=0, keepdims=True)
    scaled = grad_normed * gain[...]
    grad_resid = (
        g_ref[...].astype(f32)
        + inverse * scaled
        - resid * (inverse * inverse * inverse) * jnp.mean(scaled * resid, axis=-1, keepdims=True)
    )
    gr_ref[...] = grad_resid
    grad_proj = grad_resid.astype(bf16)
    gp_ref[...] = grad_proj
    grad_att = lax.dot_general(grad_proj, w_s[0], nt, preferred_element_type=f32).astype(bf16)
    for i in range(4):

        @pl.when(mine == i)
        def _(i=i):
            for j, out in enumerate((c0, c1, c2, c3)):
                out[...] = grad_att[:, (i ^ j) * cols : ((i ^ j) + 1) * cols]


def tail_kernel(at, p0, p1, p2, p3, x_ref, g_ref, own, half, other, gain, *refs, rows, hrows):
    w_s = refs[-1]
    outs = refs[:-1]

    @pl.when(pl.program_id(0) == 0)
    def _():
        outs[-1][...] = jnp.zeros_like(outs[-1])
        w_s[:, pl.ds(pl.multiple_of(at[1], 16), rows), :] = own[...]
        w_s[:, pl.ds(pl.multiple_of(at[2], 16), hrows), :] = half[...]
        w_s[:, pl.ds(pl.multiple_of(at[3], 16), hrows), :] = other[...]

    tail_body(at, p0, p1, p2, p3, x_ref, g_ref, w_s, gain, outs)


def whole_tail_kernel(at, p0, p1, p2, p3, x_ref, g_ref, w, gain, *outs):
    @pl.when(pl.program_id(0) == 0)
    def _():
        outs[-1][...] = jnp.zeros_like(outs[-1])

    tail_body(at, p0, p1, p2, p3, x_ref, g_ref, w, gain, outs)


def tail(at, pieces, x, g, weights, gain, tile=256):
    rows, d = x.shape
    cols = pieces[0].shape[1]
    row = lambda i, m: (i, 0)
    once = pl.Buffered(1)
    whole = lambda *shape: pl.BlockSpec(shape, lambda i, m: (0,) * len(shape), pipeline_mode=once)
    wide = pl.BlockSpec((tile, d), row)
    slim = pl.BlockSpec((tile, cols), row)
    if len(weights) == 3:
        body = functools.partial(tail_kernel, rows=weights[0].shape[1], hrows=weights[1].shape[1])
        scratch = [pltpu.VMEM((3, d, d), bf16)]
    else:
        body = whole_tail_kernel
        scratch = []
    return pl.pallas_call(
        body,
        out_shape=[pltpu.HBM((rows, d), bf16)]
        + [pltpu.HBM((3, rows, d), bf16)] * 2
        + [pltpu.HBM((rows, d), f32)]
        + [pltpu.HBM((rows, cols), bf16)] * 4
        + [pltpu.HBM((1, d), f32)],
        grid_spec=pltpu.PrefetchScalarGridSpec(
            num_scalar_prefetch=1,
            grid=(rows // tile,),
            in_specs=[slim] * 4 + [wide] * 2 + [whole(*w.shape) for w in weights] + [whole(1, d)],
            out_specs=[wide]
            + [pl.BlockSpec((3, tile, d), lambda i, m: (0, i, 0))] * 2
            + [wide]
            + [slim] * 4
            + [pl.BlockSpec((1, d), lambda i, m: (0, 0))],
            scratch_shapes=scratch,
        ),
        compiler_params=pltpu.CompilerParams(vmem_limit_bytes=52 << 20),
        cost_estimate=cost(0.01),
        name="tail",
    )(at, *pieces, hbm(x), g, *map(hbm, weights), gain)


tn_dims = (((0,), (0,)), ((), ()))


def share_kernel(col, left, right, *refs):
    value = lax.dot_general(left[0], right[0], tn_dims, preferred_element_type=f32)
    if len(refs) == 2:
        value = value + refs[0][...].astype(f32)
    refs[-1][...] = value.astype(bf16)


def share(left, right, col, got=None):
    n, rows, d = left.shape
    w = d // 2
    block = pl.BlockSpec((d, w), lambda i, c: (0, i))
    return pl.pallas_call(
        share_kernel,
        out_shape=pltpu.HBM((d, n * w), bf16),
        grid_spec=pltpu.PrefetchScalarGridSpec(
            num_scalar_prefetch=1,
            grid=(n,),
            in_specs=[
                pl.BlockSpec((1, rows, d), lambda i, c: (i, 0, 0)),
                pl.BlockSpec((1, rows, w), lambda i, c: (i, 0, c[0])),
            ]
            + [block] * (got is not None),
            out_specs=block,
        ),
        compiler_params=pltpu.CompilerParams(vmem_limit_bytes=40 << 20),
        cost_estimate=CHEAP,
        name="share",
    )(col.reshape(1), hbm(left), hbm(right), *(() if got is None else (hbm(got),)))


def tick_kernel(x_ref, out):
    out[...] = x_ref[...]


def tick(x):
    return pl.pallas_call(
        tick_kernel, out_shape=jax.ShapeDtypeStruct(x.shape, x.dtype), cost_estimate=cost(200.0), name="tick"
    )(x)


def total_kernel(*refs, counts):
    out = refs[-1]
    start, column = 0, 0
    for count in counts:
        group = refs[start : start + count]
        start += count
        acc = jnp.zeros(group[0].shape[1:], f32)
        for ref in group:
            for i in range(ref.shape[0]):
                acc = acc + ref[i].astype(f32)
        out[:, column : column + acc.shape[1]] = acc.astype(bf16)
        column += acc.shape[1]


def total(groups):
    flat = [x for group in groups for x in group]
    rows = flat[0].shape[1]
    cuts = 2 if rows % 32 == 0 else 1
    width = sum(group[0].shape[2] for group in groups)
    return pl.pallas_call(
        functools.partial(total_kernel, counts=[len(group) for group in groups]),
        out_shape=pltpu.HBM((rows, width), bf16),
        grid=(cuts,),
        in_specs=[
            pl.BlockSpec((x.shape[0], rows // cuts, x.shape[2]), lambda i: (0, i, 0)) for x in flat
        ],
        out_specs=pl.BlockSpec((rows // cuts, width), lambda i: (i, 0)),
        compiler_params=pltpu.CompilerParams(vmem_limit_bytes=40 << 20),
        cost_estimate=cost(0.001),
        name="total",
    )(*flat)


def add_kernel(a_ref, b_ref, out):
    out[...] = (a_ref[...].astype(f32) + b_ref[...].astype(f32)).astype(bf16)


def add(a, b, us):
    return pl.pallas_call(
        add_kernel, out_shape=pltpu.HBM(a.shape, bf16), cost_estimate=cost(us), name="add"
    )(a, b)


def pair_kernel(a_ref, b_ref, out):
    out[0] = a_ref[...]
    out[1] = b_ref[...]


def pair_up(a, b):
    return pl.pallas_call(
        pair_kernel, out_shape=pltpu.HBM((2,) + a.shape, bf16), cost_estimate=CHEAP, name="pair_up"
    )(a, b)


def by_bits(first, second, put):
    for i in range(2):
        for j in range(2):

            @pl.when((first == i) & (second == j))
            def _(i=i, j=j):
                put(i, j)


def place_kernel(at, own, own_x, mate, mate_x, o0, o1, o2):
    block = pl.program_id(0)
    slot = (block % 2) ^ at[1]
    w = o0.shape[2] // 2

    def put(other_x, core):
        refs = (own_x, mate_x) if other_x else (own, mate)
        for side in range(2):
            part = refs[side ^ core][slot].astype(f32)
            for i, out in enumerate((o0, o1, o2)):
                out[0, :, side * w : (side + 1) * w] = part[:, i * w : (i + 1) * w]

    by_bits((block // 2) ^ at[0], at[2], put)


def place_tail(arrays, at):
    _, h, width = arrays[0].shape
    d = width // 3 * 2
    whole = pl.BlockSpec((2, h, width), lambda i, m: (0, 0, 0), pipeline_mode=pl.Buffered(1))
    outs = pl.pallas_call(
        place_kernel,
        out_shape=[pltpu.HBM((4, h, d), f32)] * 3,
        grid_spec=pltpu.PrefetchScalarGridSpec(
            num_scalar_prefetch=1,
            grid=(4,),
            in_specs=[whole] * 4,
            out_specs=[pl.BlockSpec((1, h, d), lambda i, m: (i, 0, 0))] * 3,
        ),
        compiler_params=pltpu.CompilerParams(vmem_limit_bytes=40 << 20),
        cost_estimate=cost(0.001),
        name="place_tail",
    )(at, *arrays)
    return [out.reshape(4 * h, d) for out in outs]


def cross_kernel(at, x_ref, g_ref, *refs):
    s = refs[-1]
    s[...] = lax.dot_general(x_ref[...], g_ref[...], tn_dims, preferred_element_type=f32).astype(bf16)
    step = pl.program_id(0)
    half = s.shape[0] // 2
    for w in range(2):

        @pl.when(step == w)
        def _(w=w):
            for x in range(2):
                rows = pl.ds(pl.multiple_of((at[1] ^ x) * half, 16), half)
                refs[2 * w + x][...] = s[rows, :]


def cross(x, g, at):
    rows, d = x.shape
    w = d // 2
    block = pl.BlockSpec((w // 2, g.shape[1]), lambda i, m: (0, 0))
    return pl.pallas_call(
        cross_kernel,
        out_shape=[pltpu.HBM((w // 2, g.shape[1]), bf16)] * 4,
        grid_spec=pltpu.PrefetchScalarGridSpec(
            num_scalar_prefetch=1,
            grid=(2,),
            in_specs=[
                pl.BlockSpec((rows, w), lambda i, m: (0, m[0] ^ i)),
                pl.BlockSpec(g.shape, lambda i, m: (0, 0)),
            ],
            out_specs=[block] * 4,
            scratch_shapes=[pltpu.VMEM((w, g.shape[1]), bf16)],
        ),
        compiler_params=pltpu.CompilerParams(vmem_limit_bytes=40 << 20),
        cost_estimate=cost(0.001),
        name="cross",
    )(at, x, g)


def spread_kernel(at, *refs, groups, width):
    out = refs[-1]
    step = out.shape[1]
    rows = pl.ds(pl.multiple_of(pl.program_id(1) * step, step), step)

    def put(other_x, core):
        cut = []
        for t in range(3):
            for n in range(2):
                for c in range(2):
                    for g in range(groups):
                        part = refs[4 * g + other_x + 2 * (c ^ core)][n ^ at[1], rows, :]
                        cut.append(part[:, t * width : (t + 1) * width])
        out[0] = jnp.concatenate(cut, axis=1).astype(f32)

    by_bits(pl.program_id(0) ^ at[0], at[2], put)


def spread(arrays, at, used):
    flat = [x for group in arrays for x in group]
    groups = len(arrays)
    _, rows, cols = flat[0].shape
    width = 4 * groups * used
    cuts = 2 if rows % 32 == 0 else 1
    whole = pl.BlockSpec((2, rows, cols), lambda i, j, m: (0, 0, 0), pipeline_mode=pl.Buffered(1))
    return pl.pallas_call(
        functools.partial(spread_kernel, groups=groups, width=used // 3),
        out_shape=pltpu.HBM((2, rows, width), f32),
        grid_spec=pltpu.PrefetchScalarGridSpec(
            num_scalar_prefetch=1,
            grid=(2, cuts),
            in_specs=[whole] * len(flat),
            out_specs=pl.BlockSpec((1, rows // cuts, width), lambda i, j, m: (i, j, 0)),
        ),
        compiler_params=pltpu.CompilerParams(vmem_limit_bytes=40 << 20),
        cost_estimate=CHEAP,
        name="spread",
    )(at, *flat).reshape(2 * rows, width)


nt_dims = (((1,), (1,)), ((), ()))


def back_kernel(shards, *refs, groups, extra):
    grads, weights = refs[:groups], refs[groups : 2 * groups]
    out = refs[-1]
    acc = sum(
        lax.dot_general(g[...], w[...], nt_dims, preferred_element_type=f32)
        for g, w in zip(grads, weights)
    )
    if extra:
        acc = acc + refs[2 * groups][0].astype(f32)
    out[0] = acc.astype(bf16)


def back(grads, weights, shards, rows, got=None):
    groups = len(grads)
    d, c = weights[0].shape
    n = shards.shape[0]
    in_specs = [pl.BlockSpec((rows, c), lambda i, f: (f[i], 0))] * groups
    in_specs += [pl.BlockSpec((d, c), lambda i, f: (0, 0), pipeline_mode=pl.Buffered(1))] * groups
    args = [*map(hbm, grads), *map(hbm, weights)]
    if got is not None:
        in_specs.append(pl.BlockSpec((1, rows, d), lambda i, f: (0, 0, 0)))
        args.append(got)
    return pl.pallas_call(
        functools.partial(back_kernel, groups=groups, extra=got is not None),
        out_shape=pltpu.HBM((n, rows, d), bf16),
        grid_spec=pltpu.PrefetchScalarGridSpec(
            num_scalar_prefetch=1,
            grid=(n,),
            in_specs=in_specs,
            out_specs=pl.BlockSpec((1, rows, d), lambda i, f: (i, 0, 0)),
        ),
        compiler_params=pltpu.CompilerParams(vmem_limit_bytes=40 << 20),
        cost_estimate=CHEAP,
        name="back",
    )(shards, *args)


def finish_kernel(shard, *refs, groups):
    grads, weights = refs[:groups], refs[groups : 2 * groups]
    core, near, x_ref, resid, gain, out, gain_out = refs[2 * groups :]
    grad = sum(
        lax.dot_general(g[...], w[...], nt_dims, preferred_element_type=f32)
        for g, w in zip(grads, weights)
    )
    grad = grad + core[0].astype(f32) + near[0].astype(f32)
    x = x_ref[...].astype(f32)
    inverse = lax.rsqrt(jnp.mean(x * x, axis=-1, keepdims=True) + epsilon)
    part = jnp.sum(grad * x * inverse, axis=0, keepdims=True)

    @pl.when(pl.program_id(0) == 0)
    def _():
        gain_out[...] = jnp.zeros_like(gain_out)

    gain_out[...] += part
    scaled = grad * gain[...]
    out[...] = (
        resid[...]
        + inverse * scaled
        - x * (inverse * inverse * inverse) * jnp.mean(scaled * x, axis=-1, keepdims=True)
    ).astype(bf16)


def finish(grads, weights, shard, core, near, x, resid, gain, tile=256):
    groups = len(grads)
    rows, d = x.shape
    c = weights[0].shape[1]
    tiles = rows // tile
    row = lambda i, f: (i, 0)
    once = pl.Buffered(1)
    return pl.pallas_call(
        functools.partial(finish_kernel, groups=groups),
        out_shape=[pltpu.HBM((rows, d), bf16), jax.ShapeDtypeStruct((1, d), f32)],
        grid_spec=pltpu.PrefetchScalarGridSpec(
            num_scalar_prefetch=1,
            grid=(tiles,),
            in_specs=[pl.BlockSpec((tile, c), lambda i, f: (f[0] * tiles + i, 0))] * groups
            + [pl.BlockSpec((d, c), lambda i, f: (0, 0), pipeline_mode=once)] * groups
            + [
                pl.BlockSpec((1, tile, d), lambda i, f: (1, i, 0)),
                pl.BlockSpec((1, tile, d), lambda i, f: (0, i, 0)),
                pl.BlockSpec((tile, d), row),
                pl.BlockSpec((tile, d), row),
                pl.BlockSpec((1, d), lambda i, f: (0, 0)),
            ],
            out_specs=[pl.BlockSpec((tile, d), row), pl.BlockSpec((1, d), lambda i, f: (0, 0))],
        ),
        compiler_params=pltpu.CompilerParams(vmem_limit_bytes=40 << 20),
        cost_estimate=CHEAP,
        name="finish",
    )(shard.reshape(1), *map(hbm, grads), *map(hbm, weights), core, near, hbm(x), hbm(resid), gain)


def rms_inverse(values):
    return lax.rsqrt(jnp.mean(values * values, axis=-1, keepdims=True) + epsilon)


def norm_back(values, inverse, grad_scaled):
    return inverse * grad_scaled - values * (inverse * inverse * inverse) * jnp.mean(
        grad_scaled * values, axis=-1, keepdims=True
    )


def dot(left, right):
    return jnp.dot(left, right, preferred_element_type=f32)


def times_trans(left, right):
    return lax.dot_general(left, right, (((1,), (1,)), ((), ())), preferred_element_type=f32)


def trans_times(left, right):
    return lax.dot_general(left, right, (((0,), (0,)), ((), ())), preferred_element_type=f32)


def rows_at(array, start, count):
    return lax.dynamic_slice_in_dim(array, start, count, 0)


def put_rows(array, rows, start):
    return lax.dynamic_update_slice_in_dim(array, rows, start, 0)


def make_local(sizes):
    def pairs(target):
        found = []
        for gx in range(sizes["gx"]):
            for gc in range(sizes["gc"]):
                for z in range(4):
                    for w in range(sizes["wt"]):
                        goal = target(gx, gc, z, w)
                        if goal is not None and goal != (gx, gc, z, w):
                            found.append((place(gx, gc, z, w), place(*goal)))
        return found

    def place(gx, gc, z, w):
        return ((gx * sizes["gc"] + gc) * 4 + z) * sizes["wt"] + w

    def send(value, target):
        return lax.ppermute(value, AXES, pairs(target))

    def core_mate(gx, gc, z, w):
        return (gx, 1 - gc, z, w)

    def x_mate(gx, gc, z, w):
        return (1 - gx, gc, z, w)

    def near_mate(gx, gc, z, w):
        return (gx, gc, z ^ 1, w)

    def far_mate(gx, gc, z, w):
        return (gx, gc, z ^ 2, w)

    def cross_mate(gx, gc, z, w):
        return (gx, 1 - gc, z ^ 1, w)

    def wt_mate(gx, gc, z, w):
        return (gx, gc, z, 1 - w)

    def wt_x_mate(gx, gc, z, w):
        return (1 - gx, gc, z, 1 - w)

    def to_host(gx, gc, z, w):
        return (gx, 1 - (z & 1), 2 * gc + (z >> 1), w)

    def to_home(gx, gc, z, w):
        return (gx, z >> 1, 2 * (z & 1) + 1 - gc, w)

    def hop1(gx, gc, z, w):
        if gc == 0:
            return (gx, 0, z - 1, w) if z > 0 else None
        return (gx, 1, z + 1, w) if z < 3 else None

    def hop2(gx, gc, z, w):
        if gc == 0:
            return (gx, 0, z - 1, w) if z in (1, 2) else None
        return (gx, 1, z + 1, w) if z in (1, 2) else None

    def hop3(gx, gc, z, w):
        if gc == 0:
            return (gx, 0, z ^ 1, w) if z < 2 else None
        return (gx, 1, z ^ 1, w) if z > 1 else None

    def lane_share(gx, gc, z, w):
        return (gx, 1 - gc, z, w) if gc == z >> 1 else None

    def sum_all(value):
        for axis in AXES:
            step = 1
            while step < sizes[axis]:

                def mate(gx, gc, z, w, axis=axis, step=step):
                    at = dict(gx=gx, gc=gc, far=z >> 1, near=z & 1, wt=w)
                    at[axis] ^= step
                    return (at["gx"], at["gc"], 2 * at["far"] + at["near"], at["wt"])

                value = value + send(value, mate)
                step *= 2
        return value

    def local(
        tokens, segments, w_qkv, w_proj, w_in, w_out, gain_attn, gain_mlp, query_scale, cotangent
    ):
        gx, gc, host, near, wt = (lax.axis_index(axis) for axis in AXES)
        z = 2 * host + near
        mine = 2 * near + 1 - gc
        parts = 4
        nh = H // parts
        groups = 1
        rows = tokens.shape[1]
        group_len = segments.shape[1]
        wrows = w_qkv.shape[0]
        lane = gc == host
        pair = sizes["wt"] == 2

        def after(value, *others):
            return lax.optimization_barrier((value,) + others)[0]

        picked = pick(w_qkv, mine, parts, groups, nh)
        own = after(tokens[0], picked)
        got1 = send(own, hop1)
        own_share = send(own, lane_share)
        seg_mate = send(segments, core_mate)
        got2 = send(got1, hop2)
        got1_share = send(got1, lane_share)
        end = jnp.where(gc == 0, z == 0, z == 3)
        if pair:
            wide_own = stretch(picked, groups, nh, 2)
            got1 = after(got1, wide_own)
            other_w = send(picked, wt_mate)
            wide_w = (wide_own, stretch(other_w, groups, nh, 10))
        else:
            flat_all = lax.all_gather(picked, "wt", axis=0, tiled=True)[:, : 3 * nh * HD]
            each = flat_all.shape[1] // groups
            flat_w = [
                jnp.pad(flat_all[:, g * each : (g + 1) * each], ((0, 0), (0, lanes_up(each) - each)))
                for g in range(groups)
            ]
            by_head = jnp.transpose(flat_all.reshape(D, groups, 3, nh // groups, HD), (0, 2, 1, 3, 4))
            wide_w = (
                jnp.pad(
                    by_head.reshape(D, 3 * nh, HD), ((0, 0), (0, 0), (0, LN - HD))
                ).reshape(D, -1),
            )
        got3 = send(jnp.where(end, own, got2), hop3)
        got2_share = send(got2, lane_share)
        way = 1 - 2 * host
        last = jnp.where(host == 0, jnp.where(z == 0, 3, 0), jnp.where(z == 3, 0, 3))
        places = (z, z + way, z + 2 * way, last)

        half_rows = wrows // 2
        tail_own = jnp.stack([w_proj, w_in, w_out])
        half_w = lax.dynamic_slice_in_dim(tail_own, gc * half_rows, half_rows, 1)
        if pair:
            half_w = send(after(half_w, other_w), wt_mate)
        else:
            half_w = lax.all_gather(half_w, "wt", axis=0, tiled=False)

        dim_scale = scale_base / math.sqrt(HD) * jax.nn.softplus(query_scale)
        lane_scale = jnp.tile(jnp.pad(dim_scale * log2e, (0, LN - HD)), nh)[None]
        ones = jnp.tile(
            ((jnp.arange(LN) >= HD) & (jnp.arange(LN) < HD + 3)).astype(f32), 2 * nh
        )[None]
        seg_row = jnp.where(lane, segments, seg_mate)[0]
        fixed = (lane, mine, wt, gain_attn[None], wide_w, lane_scale, ones, group_len)
        carried = project(((own, own_share), (got1, got1_share)), places[:2], *fixed)
        got3_share = send(after(got3, carried[0]), lane_share)
        all_normed, queries, keyval, inputs = project(
            ((got2, got2_share), (got3, got3_share)), places[2:], *fixed, carried=carried
        )
        grad_mlp = send(after(cotangent[0], got3_share), to_host)

        att, att_float, q_aug = attn_fwd(queries, keyval, seg_row, nh)
        att = after(att, grad_mlp)

        trades = (core_mate, near_mate, cross_mate)
        att_pieces = [rows_at(att, (mine ^ j) * rows, rows) for j in range(parts)]
        att_pieces = [att_pieces[0]] + [send(att_pieces[j + 1], trades[j]) for j in range(3)]
        if pair:
            flat_w = order(after(picked, att_pieces[1]), other_w, wt, groups, nh)
        half_mate = send(after(half_w, att_pieces[1]), core_mate)
        if pair:
            weights = (tail_own, half_w, half_mate)
            starts = (wt * wrows, (1 - wt) * wrows + gc * half_rows, (1 - wt) * wrows + (1 - gc) * half_rows)
        else:
            one = gc == 0
            tail_w = jnp.stack(
                [jnp.where(one, half_w, half_mate), jnp.where(one, half_mate, half_w)], axis=1
            )
            weights = (jnp.transpose(tail_w, (2, 0, 1, 3, 4)).reshape(3, D, D),)
            starts = ()
        (
            layer_out,
            left,
            right,
            grad_resid,
            *pieces,
            grad_gain_mlp,
        ) = tail(
            jnp.stack([mine, *starts]), att_pieces, after(inputs, flat_w[0]), grad_mlp, weights, gain_mlp[None]
        )
        pieces = [pieces[0]] + [send(pieces[j + 1], trades[j]) for j in range(3)]

        shared = share(after(left, pieces[1]), right, 1 - gc)
        from_core = send(shared, core_mate)
        pieces[2:] = [after(piece, shared) for piece in pieces[2:]]
        home_out = send(after(layer_out, *pieces[1:]), to_home)
        late_gain = tick(after(gain_attn.reshape(-1, LN), *pieces[1:]))
        summed = share(left, right, gc, after(from_core, late_gain))
        kept = lax.all_to_all(summed, ("wt", "gx", "near"), 0, 0, tiled=True)

        scale_row = jnp.tile(dim_scale, nh // groups)[None]

        def backward(group, *others):
            first, *rest = pieces
            return attn_bwd(
                q_aug,
                keyval,
                (after(first, summed, *others), *rest),
                att_float,
                mine,
                seg_row,
                scale_row,
                nh,
                group,
                groups,
            )

        def by_rows(grad):
            if pair:
                own, *rest = cross(all_normed, grad, jnp.stack([wt, gx]))
                got = [send(part, mate) for part, mate in zip(rest, (x_mate, wt_mate, wt_x_mate))]
                return [part[None] for part in (own, *got)]
            part = trans_times(all_normed, grad).astype(bf16)
            sources = sizes["wt"] * 2
            got = lax.all_to_all(part, ("wt", "gx"), 0, 0, tiled=True)
            return [got.reshape(sources, D // sources, -1)]

        grad_project, grad_lanes = backward(0)
        layer_out = after(home_out, grad_project)

        last_step = [layer_out]

        def turn(value):
            return after(value, *last_step)

        def done(value):
            last_step[0] = value
            return value

        sources = sizes["wt"] * 4
        t1 = done(total([[turn(kept).reshape(sources, D // sources, -1)]]))
        t1_far = send(t1, far_mate)
        to_core = done(back((turn(grad_project),), flat_w, jnp.stack([mine ^ 3, mine ^ 1]), rows))
        from_core = send(to_core, core_mate)
        by_place = by_rows(turn(grad_project))
        done(by_place[0])
        to_near = done(back((grad_project,), flat_w, (mine ^ 2).reshape(1), rows, turn(from_core)))
        from_near = send(to_near, near_mate)
        by_place[0] = turn(by_place[0])
        q1 = done(total([by_place]))
        q1_far = send(q1, far_mate)
        t2 = done(add(turn(t1), t1_far, 200))
        t2_near = send(t2, near_mate)
        grad_tokens, grad_gain_attn = finish(
            (grad_project,),
            flat_w,
            mine,
            from_core,
            turn(from_near),
            inputs,
            grad_resid,
            late_gain.reshape(1, -1),
        )
        done(grad_tokens)
        home_grad = send(grad_tokens, to_home)
        t4 = done(pair_up(turn(t2), t2_near))
        t4_x = send(t4, x_mate)
        t4_core = send(t4, core_mate)
        q2 = done(add(turn(q1), q1_far, 0.001))
        q2_near = send(q2, near_mate)
        q4 = done(pair_up(turn(q2), q2_near))
        q4_x = send(q4, x_mate)
        q4_core = send(q4, core_mate)
        t4_x = done(turn(t4_x))
        t4_cross = send(t4_x, core_mate)
        at = jnp.stack([gx, near, gc])
        totals = place_tail((turn(t4), t4_x, t4_core, t4_cross), at)
        done(totals[0])
        grad_tokens = done(turn(home_grad))
        q4_x = done(turn(q4_x))
        q4_cross = send(q4_x, core_mate)
        total_qkv = spread(
            [(turn(q4), q4_x, q4_core, q4_cross)],
            jnp.stack([gx, near, 1 - gc]),
            3 * nh // groups * HD,
        )

        grad_query_scale = (
            grad_lanes[0, :HD]
            / (dim_scale * log2e)
            * (scale_base / math.sqrt(HD))
            * jax.nn.sigmoid(query_scale)
        )
        small = jnp.concatenate(
            [grad_gain_attn[0], grad_gain_mlp[0], jnp.pad(grad_query_scale, (0, LN - HD))]
        ).reshape(-1, LN)
        small = sum_all(small).reshape(-1)
        return (
            layer_out[None],
            grad_tokens[None],
            total_qkv,
            *totals,
            small[:D],
            small[D : 2 * D],
            small[2 * D : 2 * D + HD],
        )

    return local


def solution(mesh):
    groups, parts, wt = (mesh.shape[axis] for axis in ("grp", "ctx", "wt"))
    inner = Mesh(mesh.devices.reshape(groups // 2, 2, parts // 2, 2, wt), AXES)
    sizes = dict(inner.shape)
    split = P(("gx", "gc", "wt"), ("far", "near"), None)
    weight = P("wt", None)
    return jax.shard_map(
        make_local(sizes),
        mesh=inner,
        in_specs=(
            split,
            P(("gx", "gc", "wt"), None),
            weight,
            weight,
            weight,
            weight,
            P(),
            P(),
            P(),
            split,
        ),
        out_specs=(split, split, weight, weight, weight, weight, P(), P(), P()),
        check_vma=False,
    )
```

```python
import functools
import math

import jax
import jax.numpy as jnp
from jax import lax
from jax.experimental import pallas as pl
from jax.experimental.pallas import tpu as pltpu
from jax.sharding import Mesh
from jax.sharding import PartitionSpec as P

D = 1280
H = 16
HD = 80
LN = 128
epsilon = 1e-06
scale_base = 1.442695041
log2e = 1.4426950408889634
NEG = -1e30
def cost(us):
    return pl.CostEstimate(flops=int(us * 1_000_000_000), transcendentals=0, bytes_accessed=1000)


CHEAP = cost(0.001)
f32 = jnp.float32
bf16 = jnp.bfloat16
AXES = ("gx", "gc", "far", "near", "wt")


def hbm(x):
    return pltpu.with_memory_space_constraint(x, pltpu.HBM)


def block_flags(seg_row, bq, bk):
    n = seg_row.shape[0]
    q = seg_row.reshape(n // bq, bq)
    k = seg_row.reshape(n // bk, bk)
    qf, ql = q[:, 0][:, None], q[:, -1][:, None]
    kf, kl = k[:, 0][None], k[:, -1][None]
    qs = jnp.arange(n // bq, dtype=jnp.int32)[:, None] * bq
    ks = jnp.arange(n // bk, dtype=jnp.int32)[None] * bk
    below = ks + bk - 1 <= qs
    skip = (ks > qs + bq - 1) | ((kf > 0) & (kl < qf))
    same = (qf == ql) & (kl == ql) & ((kf == kl) | ((kf == 0) & (kl == 1)))
    full = below & ((kl == 0) | same)
    return jnp.where(skip, 0, jnp.where(full, 1, 2)).astype(jnp.int32).reshape(-1)


def put_split(base, col, lanes):
    hi = col.astype(bf16).astype(f32)
    rest = col - hi
    mid = rest.astype(bf16).astype(f32)
    out = jnp.where(lanes == HD, hi, base)
    out = jnp.where(lanes == HD + 1, mid, out)
    return jnp.where(lanes == HD + 2, rest - mid, out).astype(bf16)


def fwd_kernel(flags, q_ref, kv, segc, segr, att, of, qaug, m_s, acc_s, *, nh, bq, bk, nk):
    qi = pl.program_id(0)
    count = (qi * bq + bq + bk - 1) // bk
    nt = (((1,), (1,)), ((), ()))
    acc_s[...] = jnp.zeros_like(acc_s)
    m_s[...] = jnp.zeros_like(m_s)

    def mask(ko):
        qpos = qi * bq + lax.broadcasted_iota(jnp.int32, (bq, bk), 0)
        kpos = ko + lax.broadcasted_iota(jnp.int32, (bq, bk), 1)
        ks = segr[:, pl.ds(ko, bk)]
        return (kpos <= qpos) & ((ks == 0) | (ks == segc[...]))

    def step(kb, masked):
        ko = pl.multiple_of(kb * bk, bk)
        if masked:
            allowed = mask(ko)
        for h in range(nh):
            k = kv[pl.ds(ko, bk), h * LN : (h + 1) * LN]
            v = kv[pl.ds(ko, bk), (nh + h) * LN : (nh + h + 1) * LN]
            s = lax.dot_general(q_ref[:, h * LN : (h + 1) * LN], k, nt, preferred_element_type=f32)
            p = jnp.exp2(s)
            if masked:
                p = jnp.where(allowed, p, 0.0)
            acc_s[h] += jnp.dot(p.astype(bf16), v, preferred_element_type=f32)

    def body(kb, carry):
        flag = flags[qi * nk + kb]

        @pl.when(flag == 1)
        def _():
            step(kb, False)

        @pl.when(flag == 2)
        def _():
            step(kb, True)

        return carry

    lax.fori_loop(0, count, body, 0)
    bad = jnp.zeros((bq, 1), f32)
    for h in range(nh):
        total = acc_s[h][:, HD : HD + 1]
        bad = jnp.maximum(bad, jnp.where((total > 2.0**-60) & (total < 2.0**60), 0.0, 1.0))

    @pl.when(jnp.max(bad) > 0.0)
    def _():
        def head(h, carry):
            kc = pl.ds(pl.multiple_of(h * LN, LN), LN)
            vc = pl.ds(pl.multiple_of((nh + h) * LN, LN), LN)
            m_s[h] = jnp.full((bq, LN), NEG, f32)
            acc_s[h] = jnp.zeros((bq, LN), f32)

            def inner(kb, carry):
                @pl.when(flags[qi * nk + kb] > 0)
                def _():
                    ko = pl.multiple_of(kb * bk, bk)
                    s = lax.dot_general(
                        q_ref[:, kc], kv[pl.ds(ko, bk), kc], nt, preferred_element_type=f32
                    )
                    s = jnp.where(mask(ko), s, NEG)
                    old = m_s[h]
                    new = jnp.maximum(old, jnp.max(s, axis=1, keepdims=True))
                    p = jnp.exp2(s - new[:, :1]).astype(bf16)
                    m_s[h] = new
                    acc_s[h] = acc_s[h] * jnp.exp2(old - new) + jnp.dot(
                        p, kv[pl.ds(ko, bk), vc], preferred_element_type=f32
                    )

                return carry

            lax.fori_loop(0, count, inner, 0)
            return carry

        lax.fori_loop(0, nh, head, 0)

    lanes = lax.broadcasted_iota(jnp.int32, (bq, LN), 1)
    outs = []
    for h in range(nh):
        acc = acc_s[h]
        total = acc[:, HD : HD + 1]
        out = acc * (1.0 / total)
        of[:, h * LN : (h + 1) * LN] = jnp.where(lanes < HD, out, 0.0).astype(bf16)
        outs.append(out[:, :HD])
        lse = m_s[h][:, :1] + jnp.log2(total)
        qaug[:, h * LN : (h + 1) * LN] = put_split(
            q_ref[:, h * LN : (h + 1) * LN].astype(f32), -lse, lanes
        )
    att[...] = jnp.concatenate(outs, axis=1).astype(bf16)


def attn_fwd(q, kv, seg_row, nh, bq=512, bk=512):
    n = q.shape[0]
    w = nh * LN
    spec = pltpu.PrefetchScalarGridSpec(
        num_scalar_prefetch=1,
        grid=(n // bq,),
        in_specs=[
            pl.BlockSpec((bq, w), lambda i, f: (i, 0)),
            pl.BlockSpec((n, 2 * w), lambda i, f: (0, 0)),
            pl.BlockSpec((bq, 1), lambda i, f: (i, 0)),
            pl.BlockSpec((1, n), lambda i, f: (0, 0)),
        ],
        out_specs=[
            pl.BlockSpec((bq, nh * HD), lambda i, f: (i, 0)),
            pl.BlockSpec((bq, w), lambda i, f: (i, 0)),
            pl.BlockSpec((bq, w), lambda i, f: (i, 0)),
        ],
        scratch_shapes=[pltpu.VMEM((nh, bq, LN), f32), pltpu.VMEM((nh, bq, LN), f32)],
    )
    return pl.pallas_call(
        functools.partial(fwd_kernel, nh=nh, bq=bq, bk=bk, nk=n // bk),
        out_shape=[
            pltpu.HBM((n, nh * HD), bf16),
            pltpu.HBM((n, w), bf16),
            pltpu.HBM((n, w), bf16),
        ],
        grid_spec=spec,
        compiler_params=pltpu.CompilerParams(vmem_limit_bytes=40 << 20),
        cost_estimate=cost(0.01),
        name="attn_fwd",
    )(block_flags(seg_row, bq, bk), hbm(q), hbm(kv), seg_row[:, None], seg_row[None])


def bwd_kernel(
    flags, mine, qa, kk, vv, do0, do1, do2, do3, of, segc, segr, scale, dqkv, gscale, doa_s, dq_s, dk_s, dv_s, *, first, nh, bq, bk, n
):
    nk = n // bk
    nq = n // bq
    kb = pl.program_id(0)
    part = n // 4
    step_rows = 256 if part % 256 == 0 else part
    lanes = lax.broadcasted_iota(jnp.int32, (step_rows, LN), 1)

    @pl.when(kb == 0)
    def _():
        dq_s[...] = jnp.zeros_like(dq_s)
        for j, piece in enumerate((do0, do1, do2, do3)):
            start = (mine[0] ^ j) * part
            for i in range(part // step_rows):
                d = piece[i * step_rows : (i + 1) * step_rows, :].astype(f32)
                r = pl.ds(pl.multiple_of(start + i * step_rows, step_rows), step_rows)
                for h in range(nh):
                    at = (first + h) * HD
                    dh = jnp.concatenate(
                        [d[:, at : at + HD], jnp.zeros((step_rows, LN - HD), f32)], axis=1
                    )
                    c = slice(h * LN, (h + 1) * LN)
                    delta = jnp.sum(dh * of[r, c].astype(f32), axis=1, keepdims=True)
                    doa_s[r, c] = put_split(dh, -delta, lanes)

    dk_s[...] = jnp.zeros_like(dk_s)
    dv_s[...] = jnp.zeros_like(dv_s)
    ko = kb * bk
    nt = (((1,), (1,)), ((), ()))
    tn = (((0,), (0,)), ((), ()))

    def step(qi, masked):
        qo = pl.multiple_of(qi * bq, bq)
        if masked:
            kpos = ko + lax.broadcasted_iota(jnp.int32, (bk, bq), 0)
            qpos = qo + lax.broadcasted_iota(jnp.int32, (bk, bq), 1)
            ks = segc[...]
            allowed = (kpos <= qpos) & ((ks == 0) | (ks == segr[:, pl.ds(qo, bq)]))
        for h in range(nh):
            c = slice(h * LN, (h + 1) * LN)
            q = qa[pl.ds(qo, bq), c]
            k = kk[:, c]
            d = doa_s[pl.ds(qo, bq), c]
            p = jnp.exp2(lax.dot_general(k, q, nt, preferred_element_type=f32))
            if masked:
                p = jnp.where(allowed, p, 0.0)
            ds = (p * lax.dot_general(vv[:, c], d, nt, preferred_element_type=f32)).astype(bf16)
            dv_s[h] += jnp.dot(p.astype(bf16), d, preferred_element_type=f32)
            dk_s[h] += jnp.dot(ds, q, preferred_element_type=f32)
            dq_s[h, pl.ds(qo, bq), :] += lax.dot_general(ds, k, tn, preferred_element_type=f32)

    def body(qi, carry):
        flag = flags[qi * nk + kb]

        @pl.when(flag == 1)
        def _():
            step(qi, False)

        @pl.when(flag == 2)
        def _():
            step(qi, True)

        return carry

    lax.fori_loop(ko // bq, nq, body, 0)
    r = pl.multiple_of(ko, bk)
    ln2 = math.log(2.0)
    gap = dqkv.shape[1] - 3 * nh * HD
    dqkv[pl.ds(r, bk), nh * HD :] = jnp.concatenate(
        [dk_s[h][:, :HD] * ln2 for h in range(nh)]
        + [dv_s[h][:, :HD] for h in range(nh)]
        + [jnp.zeros((bk, gap), f32)],
        axis=1,
    ).astype(bf16)

    @pl.when(kb == nk - 1)
    def _():
        total = jnp.zeros((1, LN), f32)
        for i in range(nq):
            rows = slice(i * bq, (i + 1) * bq)
            for h in range(nh):
                total = total + jnp.sum(
                    dq_s[h, rows, :] * qa[rows, h * LN : (h + 1) * LN].astype(f32), axis=0, keepdims=True
                )
            grads = jnp.concatenate([dq_s[h, rows, :][:, :HD] for h in range(nh)], axis=1)
            dqkv[rows, 0 : nh * HD] = (grads * scale[...]).astype(bf16)
        gscale[...] = jnp.broadcast_to(total, gscale.shape)


def attn_bwd(qa, kv, pieces, of, mine, seg_row, scale, heads, group, groups, bq=512, bk=512):
    n = qa.shape[0]
    nh = heads // groups
    w = nh * LN
    once = pl.Buffered(1)
    spec = pltpu.PrefetchScalarGridSpec(
        num_scalar_prefetch=2,
        grid=(n // bk,),
        in_specs=[
            pl.BlockSpec((n, w), lambda i, f, m: (0, group), pipeline_mode=once),
            pl.BlockSpec((bk, w), lambda i, f, m: (i, group)),
            pl.BlockSpec((bk, w), lambda i, f, m: (i, groups + group)),
            *[pl.BlockSpec((n // 4, heads * HD), lambda i, f, m: (0, 0), pipeline_mode=once)] * 4,
            pl.BlockSpec((n, w), lambda i, f, m: (0, group), pipeline_mode=once),
            pl.BlockSpec((bk, 1), lambda i, f, m: (i, 0)),
            pl.BlockSpec((1, n), lambda i, f, m: (0, 0)),
            pl.BlockSpec((1, nh * HD), lambda i, f, m: (0, 0)),
        ],
        out_specs=[
            pl.BlockSpec((n, lanes_up(3 * nh * HD)), lambda i, f, m: (0, 0)),
            pl.BlockSpec((8, LN), lambda i, f, m: (0, 0)),
        ],
        scratch_shapes=[
            pltpu.VMEM((n, w), bf16),
            pltpu.VMEM((nh, n, LN), f32),
            pltpu.VMEM((nh, bk, LN), f32),
            pltpu.VMEM((nh, bk, LN), f32),
        ],
    )
    return pl.pallas_call(
        functools.partial(bwd_kernel, first=group * nh, nh=nh, bq=bq, bk=bk, n=n),
        out_shape=[
            pltpu.HBM((n, lanes_up(3 * nh * HD)), bf16),
            pltpu.HBM((8, LN), f32),
        ],
        grid_spec=spec,
        compiler_params=pltpu.CompilerParams(vmem_limit_bytes=48 << 20),
        cost_estimate=cost(300 if group == 0 else 0.001),
        name="attn_bwd",
    )(block_flags(seg_row, bq, bk), mine.reshape(1), hbm(qa), hbm(kv), hbm(kv), *pieces, hbm(of), seg_row[:, None], seg_row[None], scale)


def quarter_columns(place, parts, groups, nh):
    width = nh // groups * HD
    return [
        (t * D + place * nh * HD + g * width, width) for g in range(groups) for t in range(3)
    ]


def pick_kernel(mine, w_ref, out, *, parts, groups, nh):
    for i in range(parts):

        @pl.when(mine[0] == i)
        def _(i=i):
            cut = [w_ref[:, a : a + width] for a, width in quarter_columns(i, parts, groups, nh)]
            used = sum(x.shape[1] for x in cut)
            pad = jnp.zeros((cut[0].shape[0], out.shape[1] - used), out.dtype)
            out[...] = jnp.concatenate(cut + [pad], axis=1)


def lanes_up(n):
    return -(-n // LN) * LN


def pick(w, mine, parts, groups, nh):
    rows = w.shape[0]
    step = 160 if rows % 160 == 0 else rows
    return pl.pallas_call(
        functools.partial(pick_kernel, parts=parts, groups=groups, nh=nh),
        out_shape=pltpu.HBM((rows, lanes_up(3 * nh * HD)), w.dtype),
        grid_spec=pltpu.PrefetchScalarGridSpec(
            num_scalar_prefetch=1,
            grid=(rows // step,),
            in_specs=[pl.BlockSpec((step, 3 * D), lambda i, m: (i, 0))],
            out_specs=pl.BlockSpec((step, lanes_up(3 * nh * HD)), lambda i, m: (i, 0)),
        ),
        cost_estimate=cost(5),
        name="pick",
    )(mine.reshape(1), hbm(w))


def stretch_kernel(x_ref, out, *, groups, nh):
    value = x_ref[...]
    each = 3 * nh * HD // groups
    zero = jnp.zeros((value.shape[0], LN - HD), value.dtype)
    per = nh // groups
    wide = []
    for t in range(3):
        for h in range(nh):
            at = (h // per) * each + t * per * HD + (h % per) * HD
            wide += [value[:, at : at + HD], zero]
    out[...] = jnp.concatenate(wide, axis=1)


def stretch(x, groups, nh, us):
    rows, width = x.shape
    step = 160
    return pl.pallas_call(
        functools.partial(stretch_kernel, groups=groups, nh=nh),
        out_shape=pltpu.HBM((rows, 3 * nh * LN), x.dtype),
        grid=(rows // step,),
        in_specs=[pl.BlockSpec((step, width), lambda i: (i, 0))],
        out_specs=pl.BlockSpec((step, 3 * nh * LN), lambda i: (i, 0)),
        cost_estimate=cost(us),
        name="stretch",
    )(hbm(x))


def order_kernel(own_first, a_ref, b_ref, *outs, each):
    def put(ref):
        value = ref[...]
        for g, out in enumerate(outs):
            gap = jnp.zeros((value.shape[0], out.shape[1] - each), value.dtype)
            out[...] = jnp.concatenate([value[:, g * each : (g + 1) * each], gap], axis=1)

    half = pl.program_id(0)

    @pl.when(half == 0)
    def _():
        put(a_ref)

    @pl.when(half == 1)
    def _():
        put(b_ref)


def order(own, other, own_at, groups, nh):
    rows, width = own.shape
    step = 320
    n = rows // step
    at = lambda i, j, m: ((i ^ m[0]) * n + j, 0)
    each = 3 * nh * HD // groups
    return pl.pallas_call(
        functools.partial(order_kernel, each=each),
        out_shape=[pltpu.HBM((2 * rows, lanes_up(each)), own.dtype)] * groups,
        grid_spec=pltpu.PrefetchScalarGridSpec(
            num_scalar_prefetch=1,
            grid=(2, n),
            in_specs=[
                pl.BlockSpec((step, width), lambda i, j, m: (j * (1 - i), 0)),
                pl.BlockSpec((step, width), lambda i, j, m: (j * i, 0)),
            ],
            out_specs=[pl.BlockSpec((step, lanes_up(each)), at)] * groups,
        ),
        cost_estimate=cost(3),
        name="order",
    )(own_at.reshape(1), hbm(own), hbm(other))


def project_kernel(info, *refs, count, halves, width, fresh):
    pairs = refs[: 2 * count]
    gain = refs[2 * count]
    weights = refs[2 * count + 1 : 2 * count + 1 + halves]
    scale, ones = refs[2 * count + 1 + halves : 2 * count + 3 + halves]
    normed_ref, q_ref, kv_ref, mine_ref, w = refs[-5:]
    j, tile = pl.program_id(0), pl.program_id(1)
    step = normed_ref.shape[0]

    @pl.when((j == 0) & (tile == 0))
    def _():
        for i, ref in enumerate(weights):
            h = ref.shape[0]
            start = (info[count + 2] ^ i) * h if halves == 2 else 0
            w[pl.ds(pl.multiple_of(start, 16), h), :] = ref[...]
        if not fresh:
            mine_ref[...] = refs[2 * count + 3 + halves][...]

    def work(x_ref):
        value = x_ref[...]
        x = value.astype(f32)
        inverse = lax.rsqrt(jnp.mean(x * x, axis=-1, keepdims=True) + epsilon)
        normed = (x * inverse * gain[...]).astype(bf16)
        normed_ref[...] = normed
        q_ref[...] = (
            jnp.dot(normed, w[:, :width], preferred_element_type=f32) * scale[...]
        ).astype(bf16)
        kv_ref[...] = (
            jnp.dot(normed, w[:, width:], preferred_element_type=f32) + ones[...]
        ).astype(bf16)

        @pl.when(info[count + 1] == info[j])
        def _():
            mine_ref[pl.ds(pl.multiple_of(tile * step, step), step), :] = value

    for i in range(count):
        for lane in range(2):

            @pl.when((j == i) & (info[count] == lane))
            def _(i=i, lane=lane):
                work(pairs[2 * i + 1 - lane])


def project(pairs, places, lane, mine, wt, gain, weights, scale, ones, group_len, carried=None):
    count = len(pairs)
    rows, d = pairs[0][0].shape
    width = scale.shape[1]
    step = 256
    tiles = rows // step
    full = lambda j, t, f: (0, 0)
    at = lambda j, t, f: (f[j] * tiles + t, 0)
    once = pl.Buffered(1)
    info = jnp.stack(list(places) + [lane.astype(jnp.int32), mine, wt])
    args = [x for pair in pairs for x in pair] + [gain, *map(hbm, weights), scale, ones]
    in_specs = [
        pl.BlockSpec(
            (step, d),
            lambda j, t, f, i=i: (jnp.where(j == i, t, jnp.where(j > i, tiles - 1, 0)), 0),
        )
        for i in range(count)
        for _ in range(2)
    ]
    in_specs += [pl.BlockSpec((1, d), full, pipeline_mode=once)]
    in_specs += [pl.BlockSpec(w.shape, full, pipeline_mode=once) for w in weights]
    in_specs += [
        pl.BlockSpec((1, width), full, pipeline_mode=once),
        pl.BlockSpec((1, 2 * width), full, pipeline_mode=once),
    ]
    aliases = {}
    if carried is not None:
        base = len(args) + 2
        args += [hbm(x) for x in (carried[3], *carried[:3])]
        in_specs += [pl.BlockSpec((rows, d), full, pipeline_mode=once)]
        in_specs += [pl.BlockSpec(memory_space=pl.ANY)] * 3
        aliases = {base: 0, base + 1: 1, base + 2: 2}
    return pl.pallas_call(
        functools.partial(
            project_kernel, count=count, halves=len(weights), width=width, fresh=carried is None
        ),
        out_shape=[
            pltpu.HBM((group_len, d), bf16),
            pltpu.HBM((group_len, width), bf16),
            pltpu.HBM((group_len, 2 * width), bf16),
            pltpu.HBM((rows, d), bf16),
        ],
        grid_spec=pltpu.PrefetchScalarGridSpec(
            num_scalar_prefetch=1,
            grid=(count, tiles),
            in_specs=in_specs,
            out_specs=[
                pl.BlockSpec((step, d), at),
                pl.BlockSpec((step, width), at),
                pl.BlockSpec((step, 2 * width), at),
                pl.BlockSpec((rows, d), full),
            ],
            scratch_shapes=[pltpu.VMEM((d, 3 * width), bf16)],
        ),
        input_output_aliases=aliases,
        compiler_params=pltpu.CompilerParams(vmem_limit_bytes=48 << 20),
        cost_estimate=cost(15),
        name="project",
    )(info, *args)


def tail_body(at, p0, p1, p2, p3, x_ref, g_ref, w_s, gain, outs):
    lo_ref, left_ref, right_ref, gr_ref, c0, c1, c2, c3, gg_ref = outs
    att_ref, nm_ref, act_ref = (left_ref.at[i] for i in range(3))
    gp_ref, gh_ref = (right_ref.at[i] for i in range(2))
    right_ref[2] = g_ref[...]
    mine = at[0]
    pieces = (p0, p1, p2, p3)
    cols = p0.shape[1]
    nt = (((1,), (1,)), ((), ()))
    for i in range(4):

        @pl.when(mine == i)
        def _(i=i):
            att_ref[...] = jnp.concatenate([pieces[i ^ k][...] for k in range(4)], axis=1)

    resid = x_ref[...].astype(f32) + jnp.dot(att_ref[...], w_s[0], preferred_element_type=f32)
    inverse = lax.rsqrt(jnp.mean(resid * resid, axis=-1, keepdims=True) + epsilon)
    normed = (resid * inverse * gain[...]).astype(bf16)
    nm_ref[...] = normed
    hidden = jnp.dot(normed, w_s[1], preferred_element_type=f32)
    sig = 1.0 / (1.0 + jnp.exp(-hidden))
    active = (hidden * sig).astype(bf16)
    act_ref[...] = active
    lo_ref[...] = (resid + jnp.dot(active, w_s[2], preferred_element_type=f32)).astype(bf16)
    grad_active = lax.dot_general(g_ref[...], w_s[2], nt, preferred_element_type=f32)
    grad_hidden = (grad_active * sig * (1.0 + hidden * (1.0 - sig))).astype(bf16)
    gh_ref[...] = grad_hidden
    grad_normed = lax.dot_general(grad_hidden, w_s[1], nt, preferred_element_type=f32)
    gg_ref[...] += jnp.sum(grad_normed * resid * inverse, axis=0, keepdims=True)
    scaled = grad_normed * gain[...]
    grad_resid = (
        g_ref[...].astype(f32)
        + inverse * scaled
        - resid * (inverse * inverse * inverse) * jnp.mean(scaled * resid, axis=-1, keepdims=True)
    )
    gr_ref[...] = grad_resid
    grad_proj = grad_resid.astype(bf16)
    gp_ref[...] = grad_proj
    grad_att = lax.dot_general(grad_proj, w_s[0], nt, preferred_element_type=f32).astype(bf16)
    for i in range(4):

        @pl.when(mine == i)
        def _(i=i):
            for j, out in enumerate((c0, c1, c2, c3)):
                out[...] = grad_att[:, (i ^ j) * cols : ((i ^ j) + 1) * cols]


def tail_kernel(at, p0, p1, p2, p3, x_ref, g_ref, own, half, other, gain, *refs, rows, hrows):
    w_s = refs[-1]
    outs = refs[:-1]

    @pl.when(pl.program_id(0) == 0)
    def _():
        outs[-1][...] = jnp.zeros_like(outs[-1])
        w_s[:, pl.ds(pl.multiple_of(at[1], 16), rows), :] = own[...]
        w_s[:, pl.ds(pl.multiple_of(at[2], 16), hrows), :] = half[...]
        w_s[:, pl.ds(pl.multiple_of(at[3], 16), hrows), :] = other[...]

    tail_body(at, p0, p1, p2, p3, x_ref, g_ref, w_s, gain, outs)


def whole_tail_kernel(at, p0, p1, p2, p3, x_ref, g_ref, w, gain, *outs):
    @pl.when(pl.program_id(0) == 0)
    def _():
        outs[-1][...] = jnp.zeros_like(outs[-1])

    tail_body(at, p0, p1, p2, p3, x_ref, g_ref, w, gain, outs)


def tail(at, pieces, x, g, weights, gain, tile=256):
    rows, d = x.shape
    cols = pieces[0].shape[1]
    row = lambda i, m: (i, 0)
    once = pl.Buffered(1)
    whole = lambda *shape: pl.BlockSpec(shape, lambda i, m: (0,) * len(shape), pipeline_mode=once)
    wide = pl.BlockSpec((tile, d), row)
    slim = pl.BlockSpec((tile, cols), row)
    if len(weights) == 3:
        body = functools.partial(tail_kernel, rows=weights[0].shape[1], hrows=weights[1].shape[1])
        scratch = [pltpu.VMEM((3, d, d), bf16)]
    else:
        body = whole_tail_kernel
        scratch = []
    return pl.pallas_call(
        body,
        out_shape=[pltpu.HBM((rows, d), bf16)]
        + [pltpu.HBM((3, rows, d), bf16)] * 2
        + [pltpu.HBM((rows, d), f32)]
        + [pltpu.HBM((rows, cols), bf16)] * 4
        + [pltpu.HBM((1, d), f32)],
        grid_spec=pltpu.PrefetchScalarGridSpec(
            num_scalar_prefetch=1,
            grid=(rows // tile,),
            in_specs=[slim] * 4 + [wide] * 2 + [whole(*w.shape) for w in weights] + [whole(1, d)],
            out_specs=[wide]
            + [pl.BlockSpec((3, tile, d), lambda i, m: (0, i, 0))] * 2
            + [wide]
            + [slim] * 4
            + [pl.BlockSpec((1, d), lambda i, m: (0, 0))],
            scratch_shapes=scratch,
        ),
        compiler_params=pltpu.CompilerParams(vmem_limit_bytes=52 << 20),
        cost_estimate=cost(0.01),
        name="tail",
    )(at, *pieces, hbm(x), g, *map(hbm, weights), gain)


tn_dims = (((0,), (0,)), ((), ()))


def share_kernel(col, left, right, *refs):
    value = lax.dot_general(left[0], right[0], tn_dims, preferred_element_type=f32)
    if len(refs) == 2:
        value = value + refs[0][...].astype(f32)
    refs[-1][...] = value.astype(bf16)


def share(left, right, col, got=None):
    n, rows, d = left.shape
    w = d // 2
    block = pl.BlockSpec((d, w), lambda i, c: (0, i))
    return pl.pallas_call(
        share_kernel,
        out_shape=pltpu.HBM((d, n * w), bf16),
        grid_spec=pltpu.PrefetchScalarGridSpec(
            num_scalar_prefetch=1,
            grid=(n,),
            in_specs=[
                pl.BlockSpec((1, rows, d), lambda i, c: (i, 0, 0)),
                pl.BlockSpec((1, rows, w), lambda i, c: (i, 0, c[0])),
            ]
            + [block] * (got is not None),
            out_specs=block,
        ),
        compiler_params=pltpu.CompilerParams(vmem_limit_bytes=40 << 20),
        cost_estimate=CHEAP,
        name="share",
    )(col.reshape(1), hbm(left), hbm(right), *(() if got is None else (hbm(got),)))


def copy(x):
    return pl.pallas_call(
        tick_kernel, out_shape=pltpu.HBM(x.shape, x.dtype), cost_estimate=CHEAP, name="copy"
    )(x)


def tick_kernel(x_ref, out):
    out[...] = x_ref[...]


def tick(x):
    return pl.pallas_call(
        tick_kernel, out_shape=jax.ShapeDtypeStruct(x.shape, x.dtype), cost_estimate=cost(200.0), name="tick"
    )(x)


def total_kernel(*refs, counts):
    out = refs[-1]
    start, column = 0, 0
    for count in counts:
        group = refs[start : start + count]
        start += count
        acc = jnp.zeros(group[0].shape[1:], f32)
        for ref in group:
            for i in range(ref.shape[0]):
                acc = acc + ref[i].astype(f32)
        out[:, column : column + acc.shape[1]] = acc.astype(bf16)
        column += acc.shape[1]


def total(groups):
    flat = [x for group in groups for x in group]
    rows = flat[0].shape[1]
    cuts = 2 if rows % 32 == 0 else 1
    width = sum(group[0].shape[2] for group in groups)
    return pl.pallas_call(
        functools.partial(total_kernel, counts=[len(group) for group in groups]),
        out_shape=pltpu.HBM((rows, width), bf16),
        grid=(cuts,),
        in_specs=[
            pl.BlockSpec((x.shape[0], rows // cuts, x.shape[2]), lambda i: (0, i, 0)) for x in flat
        ],
        out_specs=pl.BlockSpec((rows // cuts, width), lambda i: (i, 0)),
        compiler_params=pltpu.CompilerParams(vmem_limit_bytes=40 << 20),
        cost_estimate=cost(0.001),
        name="total",
    )(*flat)


def add_kernel(a_ref, b_ref, out):
    out[...] = (a_ref[...].astype(f32) + b_ref[...].astype(f32)).astype(bf16)


def add(a, b):
    return pl.pallas_call(
        add_kernel, out_shape=pltpu.HBM(a.shape, bf16), cost_estimate=CHEAP, name="add"
    )(a, b)


def pair_kernel(a_ref, b_ref, out):
    out[0] = a_ref[...]
    out[1] = b_ref[...]


def pair_up(a, b):
    return pl.pallas_call(
        pair_kernel, out_shape=pltpu.HBM((2,) + a.shape, bf16), cost_estimate=CHEAP, name="pair_up"
    )(a, b)


def by_bits(first, second, put):
    for i in range(2):
        for j in range(2):

            @pl.when((first == i) & (second == j))
            def _(i=i, j=j):
                put(i, j)


def place_kernel(at, own, own_x, mate, mate_x, o0, o1, o2):
    block = pl.program_id(0)
    slot = (block % 2) ^ at[1]
    w = o0.shape[2] // 2

    def put(other_x, core):
        refs = (own_x, mate_x) if other_x else (own, mate)
        for side in range(2):
            part = refs[side ^ core][slot].astype(f32)
            for i, out in enumerate((o0, o1, o2)):
                out[0, :, side * w : (side + 1) * w] = part[:, i * w : (i + 1) * w]

    by_bits((block // 2) ^ at[0], at[2], put)


def place_tail(arrays, at):
    _, h, width = arrays[0].shape
    d = width // 3 * 2
    whole = pl.BlockSpec((2, h, width), lambda i, m: (0, 0, 0), pipeline_mode=pl.Buffered(1))
    outs = pl.pallas_call(
        place_kernel,
        out_shape=[pltpu.HBM((4, h, d), f32)] * 3,
        grid_spec=pltpu.PrefetchScalarGridSpec(
            num_scalar_prefetch=1,
            grid=(4,),
            in_specs=[whole] * 4,
            out_specs=[pl.BlockSpec((1, h, d), lambda i, m: (i, 0, 0))] * 3,
        ),
        compiler_params=pltpu.CompilerParams(vmem_limit_bytes=40 << 20),
        cost_estimate=cost(0.001),
        name="place_tail",
    )(at, *arrays)
    return [out.reshape(4 * h, d) for out in outs]


def cross_kernel(at, x_ref, g_ref, *refs):
    s = refs[-1]
    s[...] = lax.dot_general(x_ref[...], g_ref[...], tn_dims, preferred_element_type=f32).astype(bf16)
    step = pl.program_id(0)
    half = s.shape[0] // 2
    for w in range(2):

        @pl.when(step == w)
        def _(w=w):
            for x in range(2):
                rows = pl.ds(pl.multiple_of((at[1] ^ x) * half, 16), half)
                refs[2 * w + x][...] = s[rows, :]


def cross(x, g, at):
    rows, d = x.shape
    w = d // 2
    block = pl.BlockSpec((w // 2, g.shape[1]), lambda i, m: (0, 0))
    return pl.pallas_call(
        cross_kernel,
        out_shape=[pltpu.HBM((w // 2, g.shape[1]), bf16)] * 4,
        grid_spec=pltpu.PrefetchScalarGridSpec(
            num_scalar_prefetch=1,
            grid=(2,),
            in_specs=[
                pl.BlockSpec((rows, w), lambda i, m: (0, m[0] ^ i)),
                pl.BlockSpec(g.shape, lambda i, m: (0, 0)),
            ],
            out_specs=[block] * 4,
            scratch_shapes=[pltpu.VMEM((w, g.shape[1]), bf16)],
        ),
        compiler_params=pltpu.CompilerParams(vmem_limit_bytes=40 << 20),
        cost_estimate=cost(0.001),
        name="cross",
    )(at, x, g)


def spread_kernel(at, *refs, groups, width):
    out = refs[-1]
    step = out.shape[1]
    rows = pl.ds(pl.multiple_of(pl.program_id(1) * step, step), step)

    def put(other_x, core):
        cut = []
        for t in range(3):
            for n in range(2):
                for c in range(2):
                    for g in range(groups):
                        part = refs[4 * g + other_x + 2 * (c ^ core)][n ^ at[1], rows, :]
                        cut.append(part[:, t * width : (t + 1) * width])
        out[0] = jnp.concatenate(cut, axis=1).astype(f32)

    by_bits(pl.program_id(0) ^ at[0], at[2], put)


def spread(arrays, at, used):
    flat = [x for group in arrays for x in group]
    groups = len(arrays)
    _, rows, cols = flat[0].shape
    width = 4 * groups * used
    cuts = 2 if rows % 32 == 0 else 1
    whole = pl.BlockSpec((2, rows, cols), lambda i, j, m: (0, 0, 0), pipeline_mode=pl.Buffered(1))
    return pl.pallas_call(
        functools.partial(spread_kernel, groups=groups, width=used // 3),
        out_shape=pltpu.HBM((2, rows, width), f32),
        grid_spec=pltpu.PrefetchScalarGridSpec(
            num_scalar_prefetch=1,
            grid=(2, cuts),
            in_specs=[whole] * len(flat),
            out_specs=pl.BlockSpec((1, rows // cuts, width), lambda i, j, m: (i, j, 0)),
        ),
        compiler_params=pltpu.CompilerParams(vmem_limit_bytes=40 << 20),
        cost_estimate=CHEAP,
        name="spread",
    )(at, *flat).reshape(2 * rows, width)


nt_dims = (((1,), (1,)), ((), ()))


def back_kernel(shards, *refs, groups, extra):
    grads, weights = refs[:groups], refs[groups : 2 * groups]
    out = refs[-1]
    acc = sum(
        lax.dot_general(g[...], w[...], nt_dims, preferred_element_type=f32)
        for g, w in zip(grads, weights)
    )
    if extra:
        acc = acc + refs[2 * groups][0].astype(f32)
    out[0] = acc.astype(bf16)


def back(grads, weights, shards, rows, got=None):
    groups = len(grads)
    d, c = weights[0].shape
    n = shards.shape[0]
    in_specs = [pl.BlockSpec((rows, c), lambda i, f: (f[i], 0))] * groups
    in_specs += [pl.BlockSpec((d, c), lambda i, f: (0, 0), pipeline_mode=pl.Buffered(1))] * groups
    args = [*map(hbm, grads), *map(hbm, weights)]
    if got is not None:
        in_specs.append(pl.BlockSpec((1, rows, d), lambda i, f: (0, 0, 0)))
        args.append(got)
    return pl.pallas_call(
        functools.partial(back_kernel, groups=groups, extra=got is not None),
        out_shape=pltpu.HBM((n, rows, d), bf16),
        grid_spec=pltpu.PrefetchScalarGridSpec(
            num_scalar_prefetch=1,
            grid=(n,),
            in_specs=in_specs,
            out_specs=pl.BlockSpec((1, rows, d), lambda i, f: (i, 0, 0)),
        ),
        compiler_params=pltpu.CompilerParams(vmem_limit_bytes=40 << 20),
        cost_estimate=CHEAP,
        name="back",
    )(shards, *args)


def finish_kernel(shard, *refs, groups):
    grads, weights = refs[:groups], refs[groups : 2 * groups]
    core, near, x_ref, resid, gain, out, gain_out = refs[2 * groups :]
    grad = sum(
        lax.dot_general(g[...], w[...], nt_dims, preferred_element_type=f32)
        for g, w in zip(grads, weights)
    )
    grad = grad + core[0].astype(f32) + near[0].astype(f32)
    x = x_ref[...].astype(f32)
    inverse = lax.rsqrt(jnp.mean(x * x, axis=-1, keepdims=True) + epsilon)
    part = jnp.sum(grad * x * inverse, axis=0, keepdims=True)

    @pl.when(pl.program_id(0) == 0)
    def _():
        gain_out[...] = jnp.zeros_like(gain_out)

    gain_out[...] += part
    scaled = grad * gain[...]
    out[...] = (
        resid[...]
        + inverse * scaled
        - x * (inverse * inverse * inverse) * jnp.mean(scaled * x, axis=-1, keepdims=True)
    ).astype(bf16)


def finish(grads, weights, shard, core, near, x, resid, gain, tile=256):
    groups = len(grads)
    rows, d = x.shape
    c = weights[0].shape[1]
    tiles = rows // tile
    row = lambda i, f: (i, 0)
    once = pl.Buffered(1)
    return pl.pallas_call(
        functools.partial(finish_kernel, groups=groups),
        out_shape=[pltpu.HBM((rows, d), bf16), jax.ShapeDtypeStruct((1, d), f32)],
        grid_spec=pltpu.PrefetchScalarGridSpec(
            num_scalar_prefetch=1,
            grid=(tiles,),
            in_specs=[pl.BlockSpec((tile, c), lambda i, f: (f[0] * tiles + i, 0))] * groups
            + [pl.BlockSpec((d, c), lambda i, f: (0, 0), pipeline_mode=once)] * groups
            + [
                pl.BlockSpec((1, tile, d), lambda i, f: (1, i, 0)),
                pl.BlockSpec((1, tile, d), lambda i, f: (0, i, 0)),
                pl.BlockSpec((tile, d), row),
                pl.BlockSpec((tile, d), row),
                pl.BlockSpec((1, d), lambda i, f: (0, 0)),
            ],
            out_specs=[pl.BlockSpec((tile, d), row), pl.BlockSpec((1, d), lambda i, f: (0, 0))],
        ),
        compiler_params=pltpu.CompilerParams(vmem_limit_bytes=40 << 20),
        cost_estimate=CHEAP,
        name="finish",
    )(shard.reshape(1), *map(hbm, grads), *map(hbm, weights), core, near, hbm(x), hbm(resid), gain)


def rms_inverse(values):
    return lax.rsqrt(jnp.mean(values * values, axis=-1, keepdims=True) + epsilon)


def norm_back(values, inverse, grad_scaled):
    return inverse * grad_scaled - values * (inverse * inverse * inverse) * jnp.mean(
        grad_scaled * values, axis=-1, keepdims=True
    )


def dot(left, right):
    return jnp.dot(left, right, preferred_element_type=f32)


def times_trans(left, right):
    return lax.dot_general(left, right, (((1,), (1,)), ((), ())), preferred_element_type=f32)


def trans_times(left, right):
    return lax.dot_general(left, right, (((0,), (0,)), ((), ())), preferred_element_type=f32)


def rows_at(array, start, count):
    return lax.dynamic_slice_in_dim(array, start, count, 0)


def put_rows(array, rows, start):
    return lax.dynamic_update_slice_in_dim(array, rows, start, 0)


def make_local(sizes):
    def pairs(target):
        found = []
        for gx in range(sizes["gx"]):
            for gc in range(sizes["gc"]):
                for z in range(4):
                    for w in range(sizes["wt"]):
                        goal = target(gx, gc, z, w)
                        if goal is not None and goal != (gx, gc, z, w):
                            found.append((place(gx, gc, z, w), place(*goal)))
        return found

    def place(gx, gc, z, w):
        return ((gx * sizes["gc"] + gc) * 4 + z) * sizes["wt"] + w

    def send(value, target):
        return lax.ppermute(value, AXES, pairs(target))

    def core_mate(gx, gc, z, w):
        return (gx, 1 - gc, z, w)

    def x_mate(gx, gc, z, w):
        return (1 - gx, gc, z, w)

    def near_mate(gx, gc, z, w):
        return (gx, gc, z ^ 1, w)

    def far_mate(gx, gc, z, w):
        return (gx, gc, z ^ 2, w)

    def cross_mate(gx, gc, z, w):
        return (gx, 1 - gc, z ^ 1, w)

    def wt_mate(gx, gc, z, w):
        return (gx, gc, z, 1 - w)

    def wt_x_mate(gx, gc, z, w):
        return (1 - gx, gc, z, 1 - w)

    def to_host(gx, gc, z, w):
        return (gx, 1 - (z & 1), 2 * gc + (z >> 1), w)

    def to_home(gx, gc, z, w):
        return (gx, z >> 1, 2 * (z & 1) + 1 - gc, w)

    def hop1(gx, gc, z, w):
        if gc == 0:
            return (gx, 0, z - 1, w) if z > 0 else None
        return (gx, 1, z + 1, w) if z < 3 else None

    def hop2(gx, gc, z, w):
        if gc == 0:
            return (gx, 0, z - 1, w) if z in (1, 2) else None
        return (gx, 1, z + 1, w) if z in (1, 2) else None

    def hop3(gx, gc, z, w):
        if gc == 0:
            return (gx, 0, z ^ 1, w) if z < 2 else None
        return (gx, 1, z ^ 1, w) if z > 1 else None

    def lane_share(gx, gc, z, w):
        return (gx, 1 - gc, z, w) if gc == z >> 1 else None

    def sum_all(value):
        for axis in AXES:
            step = 1
            while step < sizes[axis]:

                def mate(gx, gc, z, w, axis=axis, step=step):
                    at = dict(gx=gx, gc=gc, far=z >> 1, near=z & 1, wt=w)
                    at[axis] ^= step
                    return (at["gx"], at["gc"], 2 * at["far"] + at["near"], at["wt"])

                value = value + send(value, mate)
                step *= 2
        return value

    def local(
        tokens, segments, w_qkv, w_proj, w_in, w_out, gain_attn, gain_mlp, query_scale, cotangent
    ):
        gx, gc, host, near, wt = (lax.axis_index(axis) for axis in AXES)
        z = 2 * host + near
        mine = 2 * near + 1 - gc
        parts = 4
        nh = H // parts
        groups = 1
        rows = tokens.shape[1]
        group_len = segments.shape[1]
        wrows = w_qkv.shape[0]
        lane = gc == host
        pair = sizes["wt"] == 2

        def after(value, *others):
            return lax.optimization_barrier((value,) + others)[0]

        picked = pick(w_qkv, mine, parts, groups, nh)
        own = after(tokens[0], picked)
        got1 = send(own, hop1)
        own_share = send(own, lane_share)
        seg_mate = send(segments, core_mate)
        got2 = send(got1, hop2)
        got1_share = send(got1, lane_share)
        end = jnp.where(gc == 0, z == 0, z == 3)
        if pair:
            wide_own = stretch(picked, groups, nh, 2)
            got1 = after(got1, wide_own)
            other_w = send(picked, wt_mate)
            wide_w = (wide_own, stretch(other_w, groups, nh, 10))
        else:
            flat_all = lax.all_gather(picked, "wt", axis=0, tiled=True)[:, : 3 * nh * HD]
            each = flat_all.shape[1] // groups
            flat_w = [
                jnp.pad(flat_all[:, g * each : (g + 1) * each], ((0, 0), (0, lanes_up(each) - each)))
                for g in range(groups)
            ]
            by_head = jnp.transpose(flat_all.reshape(D, groups, 3, nh // groups, HD), (0, 2, 1, 3, 4))
            wide_w = (
                jnp.pad(
                    by_head.reshape(D, 3 * nh, HD), ((0, 0), (0, 0), (0, LN - HD))
                ).reshape(D, -1),
            )
        got3 = send(jnp.where(end, own, got2), hop3)
        got2_share = send(got2, lane_share)
        way = 1 - 2 * host
        last = jnp.where(host == 0, jnp.where(z == 0, 3, 0), jnp.where(z == 3, 0, 3))
        places = (z, z + way, z + 2 * way, last)

        half_rows = wrows // 2
        tail_own = jnp.stack([w_proj, w_in, w_out])
        half_w = lax.dynamic_slice_in_dim(tail_own, gc * half_rows, half_rows, 1)
        if pair:
            half_w = send(after(half_w, other_w), wt_mate)
        else:
            half_w = lax.all_gather(half_w, "wt", axis=0, tiled=False)

        dim_scale = scale_base / math.sqrt(HD) * jax.nn.softplus(query_scale)
        lane_scale = jnp.tile(jnp.pad(dim_scale * log2e, (0, LN - HD)), nh)[None]
        ones = jnp.tile(
            ((jnp.arange(LN) >= HD) & (jnp.arange(LN) < HD + 3)).astype(f32), 2 * nh
        )[None]
        seg_row = jnp.where(lane, segments, seg_mate)[0]
        fixed = (lane, mine, wt, gain_attn[None], wide_w, lane_scale, ones, group_len)
        carried = project(((own, own_share), (got1, got1_share)), places[:2], *fixed)
        got3_share = send(after(got3, carried[0]), lane_share)
        all_normed, queries, keyval, inputs = project(
            ((got2, got2_share), (got3, got3_share)), places[2:], *fixed, carried=carried
        )
        grad_mlp = send(after(cotangent[0], got3_share), to_host)

        att, att_float, q_aug = attn_fwd(queries, keyval, seg_row, nh)
        att = after(att, grad_mlp)

        trades = (core_mate, near_mate, cross_mate)
        att_pieces = [rows_at(att, (mine ^ j) * rows, rows) for j in range(parts)]
        att_pieces = [att_pieces[0]] + [send(att_pieces[j + 1], trades[j]) for j in range(3)]
        if pair:
            flat_w = order(after(picked, att_pieces[1]), other_w, wt, groups, nh)
        half_mate = send(after(half_w, att_pieces[1]), core_mate)
        if pair:
            weights = (tail_own, half_w, half_mate)
            starts = (wt * wrows, (1 - wt) * wrows + gc * half_rows, (1 - wt) * wrows + (1 - gc) * half_rows)
        else:
            one = gc == 0
            tail_w = jnp.stack(
                [jnp.where(one, half_w, half_mate), jnp.where(one, half_mate, half_w)], axis=1
            )
            weights = (jnp.transpose(tail_w, (2, 0, 1, 3, 4)).reshape(3, D, D),)
            starts = ()
        (
            layer_out,
            left,
            right,
            grad_resid,
            *pieces,
            grad_gain_mlp,
        ) = tail(
            jnp.stack([mine, *starts]), att_pieces, after(inputs, flat_w[0]), grad_mlp, weights, gain_mlp[None]
        )
        pieces = [pieces[0]] + [send(pieces[j + 1], trades[j]) for j in range(3)]

        shared = share(after(left, pieces[1]), right, 1 - gc)
        from_core = send(shared, core_mate)
        pieces[2:] = [after(piece, shared) for piece in pieces[2:]]
        home_out = send(after(layer_out, *pieces[1:]), to_home)
        late_gain = tick(after(gain_attn.reshape(-1, LN), *pieces[1:]))
        summed = share(left, right, gc, after(from_core, late_gain))
        kept = lax.all_to_all(summed, ("wt", "gx", "near"), 0, 0, tiled=True)

        scale_row = jnp.tile(dim_scale, nh // groups)[None]

        def backward(group, *others):
            first, *rest = pieces
            return attn_bwd(
                q_aug,
                keyval,
                (after(first, summed, *others), *rest),
                att_float,
                mine,
                seg_row,
                scale_row,
                nh,
                group,
                groups,
            )

        def by_rows(grad):
            if pair:
                own, *rest = cross(all_normed, grad, jnp.stack([wt, gx]))
                got = [send(part, mate) for part, mate in zip(rest, (x_mate, wt_mate, wt_x_mate))]
                return [part[None] for part in (own, *got)]
            part = trans_times(all_normed, grad).astype(bf16)
            sources = sizes["wt"] * 2
            got = lax.all_to_all(part, ("wt", "gx"), 0, 0, tiled=True)
            return [got.reshape(sources, D // sources, -1)]

        grad_project, grad_lanes = backward(0)
        layer_out = after(home_out, grad_project)

        last_step = [layer_out]

        def turn(value):
            return after(value, *last_step)

        def done(value):
            last_step[0] = value
            return value

        sources = sizes["wt"] * 4
        to_core = done(back((turn(grad_project),), flat_w, jnp.stack([mine ^ 3, mine ^ 1]), rows))
        from_core = send(to_core, core_mate)
        by_place = by_rows(turn(grad_project))
        done(by_place[0])
        to_near = done(back((grad_project,), flat_w, (mine ^ 2).reshape(1), rows, turn(from_core)))
        from_near = send(to_near, near_mate)
        t1 = done(total([[turn(kept).reshape(sources, D // sources, -1)]]))
        t1_far = send(t1, far_mate)
        layer_out = done(copy(turn(layer_out)))
        by_place[0] = turn(by_place[0])
        q1 = done(total([by_place]))
        q1_far = send(q1, far_mate)
        grad_tokens, grad_gain_attn = finish(
            (grad_project,),
            flat_w,
            mine,
            from_core,
            turn(from_near),
            inputs,
            grad_resid,
            late_gain.reshape(1, -1),
        )
        done(grad_tokens)
        home_grad = send(grad_tokens, to_home)
        t2 = done(add(turn(t1), t1_far))
        t2_near = send(t2, near_mate)
        q2 = done(add(turn(q1), q1_far))
        q2_near = send(q2, near_mate)
        t4 = done(pair_up(turn(t2), t2_near))
        t4_x = send(t4, x_mate)
        t4_core = send(t4, core_mate)
        grad_tokens = done(turn(home_grad))
        q4 = done(pair_up(turn(q2), q2_near))
        q4_x = send(q4, x_mate)
        q4_core = send(q4, core_mate)
        t4_x = done(turn(t4_x))
        t4_cross = send(t4_x, core_mate)
        at = jnp.stack([gx, near, gc])
        totals = place_tail((turn(t4), t4_x, t4_core, t4_cross), at)
        done(totals[0])
        q4_x = done(turn(q4_x))
        q4_cross = send(q4_x, core_mate)
        total_qkv = spread(
            [(turn(q4), q4_x, q4_core, q4_cross)],
            jnp.stack([gx, near, 1 - gc]),
            3 * nh // groups * HD,
        )

        grad_query_scale = (
            grad_lanes[0, :HD]
            / (dim_scale * log2e)
            * (scale_base / math.sqrt(HD))
            * jax.nn.sigmoid(query_scale)
        )
        small = jnp.concatenate(
            [grad_gain_attn[0], grad_gain_mlp[0], jnp.pad(grad_query_scale, (0, LN - HD))]
        ).reshape(-1, LN)
        small = sum_all(small).reshape(-1)
        return (
            layer_out[None],
            grad_tokens[None],
            total_qkv,
            *totals,
            small[:D],
            small[D : 2 * D],
            small[2 * D : 2 * D + HD],
        )

    return local


def solution(mesh):
    groups, parts, wt = (mesh.shape[axis] for axis in ("grp", "ctx", "wt"))
    inner = Mesh(mesh.devices.reshape(groups // 2, 2, parts // 2, 2, wt), AXES)
    sizes = dict(inner.shape)
    split = P(("gx", "gc", "wt"), ("far", "near"), None)
    weight = P("wt", None)
    return jax.shard_map(
        make_local(sizes),
        mesh=inner,
        in_specs=(
            split,
            P(("gx", "gc", "wt"), None),
            weight,
            weight,
            weight,
            weight,
            P(),
            P(),
            P(),
            split,
        ),
        out_specs=(split, split, weight, weight, weight, weight, P(), P(), P()),
        check_vma=False,
    )
```

```python
import functools
import math

import jax
import jax.numpy as jnp
from jax import lax
from jax.experimental import pallas as pl
from jax.experimental.pallas import tpu as pltpu
from jax.sharding import Mesh
from jax.sharding import PartitionSpec as P

D = 1280
H = 16
HD = 80
LN = 128
epsilon = 1e-06
scale_base = 1.442695041
log2e = 1.4426950408889634
NEG = -1e30
def cost(us):
    return pl.CostEstimate(flops=int(us * 1_000_000_000), transcendentals=0, bytes_accessed=1000)


CHEAP = cost(0.001)
f32 = jnp.float32
bf16 = jnp.bfloat16
AXES = ("gx", "gc", "far", "near", "wt")


def hbm(x):
    return pltpu.with_memory_space_constraint(x, pltpu.HBM)


def block_flags(seg_row, bq, bk):
    n = seg_row.shape[0]
    q = seg_row.reshape(n // bq, bq)
    k = seg_row.reshape(n // bk, bk)
    qf, ql = q[:, 0][:, None], q[:, -1][:, None]
    kf, kl = k[:, 0][None], k[:, -1][None]
    qs = jnp.arange(n // bq, dtype=jnp.int32)[:, None] * bq
    ks = jnp.arange(n // bk, dtype=jnp.int32)[None] * bk
    below = ks + bk - 1 <= qs
    skip = (ks > qs + bq - 1) | ((kf > 0) & (kl < qf))
    same = (qf == ql) & (kl == ql) & ((kf == kl) | ((kf == 0) & (kl == 1)))
    full = below & ((kl == 0) | same)
    return jnp.where(skip, 0, jnp.where(full, 1, 2)).astype(jnp.int32).reshape(-1)


def put_split(base, col, lanes):
    hi = col.astype(bf16).astype(f32)
    rest = col - hi
    mid = rest.astype(bf16).astype(f32)
    out = jnp.where(lanes == HD, hi, base)
    out = jnp.where(lanes == HD + 1, mid, out)
    return jnp.where(lanes == HD + 2, rest - mid, out).astype(bf16)


def fwd_kernel(flags, q_ref, kv, segc, segr, att, of, qaug, m_s, acc_s, *, nh, bq, bk, nk):
    qi = pl.program_id(0)
    count = (qi * bq + bq + bk - 1) // bk
    nt = (((1,), (1,)), ((), ()))
    acc_s[...] = jnp.zeros_like(acc_s)
    m_s[...] = jnp.zeros_like(m_s)

    def mask(ko):
        qpos = qi * bq + lax.broadcasted_iota(jnp.int32, (bq, bk), 0)
        kpos = ko + lax.broadcasted_iota(jnp.int32, (bq, bk), 1)
        ks = segr[:, pl.ds(ko, bk)]
        return (kpos <= qpos) & ((ks == 0) | (ks == segc[...]))

    def step(kb, masked):
        ko = pl.multiple_of(kb * bk, bk)
        if masked:
            allowed = mask(ko)
        for h in range(nh):
            k = kv[pl.ds(ko, bk), h * LN : (h + 1) * LN]
            v = kv[pl.ds(ko, bk), (nh + h) * LN : (nh + h + 1) * LN]
            s = lax.dot_general(q_ref[:, h * LN : (h + 1) * LN], k, nt, preferred_element_type=f32)
            p = jnp.exp2(s)
            if masked:
                p = jnp.where(allowed, p, 0.0)
            acc_s[h] += jnp.dot(p.astype(bf16), v, preferred_element_type=f32)

    def body(kb, carry):
        flag = flags[qi * nk + kb]

        @pl.when(flag == 1)
        def _():
            step(kb, False)

        @pl.when(flag == 2)
        def _():
            step(kb, True)

        return carry

    lax.fori_loop(0, count, body, 0)
    bad = jnp.zeros((bq, 1), f32)
    for h in range(nh):
        total = acc_s[h][:, HD : HD + 1]
        bad = jnp.maximum(bad, jnp.where((total > 2.0**-60) & (total < 2.0**60), 0.0, 1.0))

    @pl.when(jnp.max(bad) > 0.0)
    def _():
        def head(h, carry):
            kc = pl.ds(pl.multiple_of(h * LN, LN), LN)
            vc = pl.ds(pl.multiple_of((nh + h) * LN, LN), LN)
            m_s[h] = jnp.full((bq, LN), NEG, f32)
            acc_s[h] = jnp.zeros((bq, LN), f32)

            def inner(kb, carry):
                @pl.when(flags[qi * nk + kb] > 0)
                def _():
                    ko = pl.multiple_of(kb * bk, bk)
                    s = lax.dot_general(
                        q_ref[:, kc], kv[pl.ds(ko, bk), kc], nt, preferred_element_type=f32
                    )
                    s = jnp.where(mask(ko), s, NEG)
                    old = m_s[h]
                    new = jnp.maximum(old, jnp.max(s, axis=1, keepdims=True))
                    p = jnp.exp2(s - new[:, :1]).astype(bf16)
                    m_s[h] = new
                    acc_s[h] = acc_s[h] * jnp.exp2(old - new) + jnp.dot(
                        p, kv[pl.ds(ko, bk), vc], preferred_element_type=f32
                    )

                return carry

            lax.fori_loop(0, count, inner, 0)
            return carry

        lax.fori_loop(0, nh, head, 0)

    lanes = lax.broadcasted_iota(jnp.int32, (bq, LN), 1)
    outs = []
    for h in range(nh):
        acc = acc_s[h]
        total = acc[:, HD : HD + 1]
        out = acc * (1.0 / total)
        of[:, h * LN : (h + 1) * LN] = jnp.where(lanes < HD, out, 0.0).astype(bf16)
        outs.append(out[:, :HD])
        lse = m_s[h][:, :1] + jnp.log2(total)
        qaug[:, h * LN : (h + 1) * LN] = put_split(
            q_ref[:, h * LN : (h + 1) * LN].astype(f32), -lse, lanes
        )
    att[...] = jnp.concatenate(outs, axis=1).astype(bf16)


def attn_fwd(q, kv, seg_row, nh, bq=512, bk=512):
    n = q.shape[0]
    w = nh * LN
    spec = pltpu.PrefetchScalarGridSpec(
        num_scalar_prefetch=1,
        grid=(n // bq,),
        in_specs=[
            pl.BlockSpec((bq, w), lambda i, f: (i, 0)),
            pl.BlockSpec((n, 2 * w), lambda i, f: (0, 0)),
            pl.BlockSpec((bq, 1), lambda i, f: (i, 0)),
            pl.BlockSpec((1, n), lambda i, f: (0, 0)),
        ],
        out_specs=[
            pl.BlockSpec((bq, nh * HD), lambda i, f: (i, 0)),
            pl.BlockSpec((bq, w), lambda i, f: (i, 0)),
            pl.BlockSpec((bq, w), lambda i, f: (i, 0)),
        ],
        scratch_shapes=[pltpu.VMEM((nh, bq, LN), f32), pltpu.VMEM((nh, bq, LN), f32)],
    )
    return pl.pallas_call(
        functools.partial(fwd_kernel, nh=nh, bq=bq, bk=bk, nk=n // bk),
        out_shape=[
            pltpu.HBM((n, nh * HD), bf16),
            pltpu.HBM((n, w), bf16),
            pltpu.HBM((n, w), bf16),
        ],
        grid_spec=spec,
        compiler_params=pltpu.CompilerParams(vmem_limit_bytes=40 << 20),
        cost_estimate=cost(0.01),
        name="attn_fwd",
    )(block_flags(seg_row, bq, bk), hbm(q), hbm(kv), seg_row[:, None], seg_row[None])


def bwd_kernel(
    flags, mine, qa, kk, vv, do0, do1, do2, do3, of, segc, segr, scale, dqkv, gscale, doa_s, dq_s, dk_s, dv_s, *, first, nh, bq, bk, n
):
    nk = n // bk
    nq = n // bq
    kb = pl.program_id(0)
    part = n // 4
    step_rows = 256 if part % 256 == 0 else part
    lanes = lax.broadcasted_iota(jnp.int32, (step_rows, LN), 1)

    @pl.when(kb == 0)
    def _():
        dq_s[...] = jnp.zeros_like(dq_s)
        for j, piece in enumerate((do0, do1, do2, do3)):
            start = (mine[0] ^ j) * part
            for i in range(part // step_rows):
                d = piece[i * step_rows : (i + 1) * step_rows, :].astype(f32)
                r = pl.ds(pl.multiple_of(start + i * step_rows, step_rows), step_rows)
                for h in range(nh):
                    at = (first + h) * HD
                    dh = jnp.concatenate(
                        [d[:, at : at + HD], jnp.zeros((step_rows, LN - HD), f32)], axis=1
                    )
                    c = slice(h * LN, (h + 1) * LN)
                    delta = jnp.sum(dh * of[r, c].astype(f32), axis=1, keepdims=True)
                    doa_s[r, c] = put_split(dh, -delta, lanes)

    dk_s[...] = jnp.zeros_like(dk_s)
    dv_s[...] = jnp.zeros_like(dv_s)
    ko = kb * bk
    nt = (((1,), (1,)), ((), ()))
    tn = (((0,), (0,)), ((), ()))

    def step(qi, masked):
        qo = pl.multiple_of(qi * bq, bq)
        if masked:
            kpos = ko + lax.broadcasted_iota(jnp.int32, (bk, bq), 0)
            qpos = qo + lax.broadcasted_iota(jnp.int32, (bk, bq), 1)
            ks = segc[...]
            allowed = (kpos <= qpos) & ((ks == 0) | (ks == segr[:, pl.ds(qo, bq)]))
        for h in range(nh):
            c = slice(h * LN, (h + 1) * LN)
            q = qa[pl.ds(qo, bq), c]
            k = kk[:, c]
            d = doa_s[pl.ds(qo, bq), c]
            p = jnp.exp2(lax.dot_general(k, q, nt, preferred_element_type=f32))
            if masked:
                p = jnp.where(allowed, p, 0.0)
            ds = (p * lax.dot_general(vv[:, c], d, nt, preferred_element_type=f32)).astype(bf16)
            dv_s[h] += jnp.dot(p.astype(bf16), d, preferred_element_type=f32)
            dk_s[h] += jnp.dot(ds, q, preferred_element_type=f32)
            dq_s[h, pl.ds(qo, bq), :] += lax.dot_general(ds, k, tn, preferred_element_type=f32)

    def body(qi, carry):
        flag = flags[qi * nk + kb]

        @pl.when(flag == 1)
        def _():
            step(qi, False)

        @pl.when(flag == 2)
        def _():
            step(qi, True)

        return carry

    lax.fori_loop(ko // bq, nq, body, 0)
    r = pl.multiple_of(ko, bk)
    ln2 = math.log(2.0)
    gap = dqkv.shape[1] - 3 * nh * HD
    dqkv[pl.ds(r, bk), nh * HD :] = jnp.concatenate(
        [dk_s[h][:, :HD] * ln2 for h in range(nh)]
        + [dv_s[h][:, :HD] for h in range(nh)]
        + [jnp.zeros((bk, gap), f32)],
        axis=1,
    ).astype(bf16)

    @pl.when(kb == nk - 1)
    def _():
        total = jnp.zeros((1, LN), f32)
        for i in range(nq):
            rows = slice(i * bq, (i + 1) * bq)
            for h in range(nh):
                total = total + jnp.sum(
                    dq_s[h, rows, :] * qa[rows, h * LN : (h + 1) * LN].astype(f32), axis=0, keepdims=True
                )
            grads = jnp.concatenate([dq_s[h, rows, :][:, :HD] for h in range(nh)], axis=1)
            dqkv[rows, 0 : nh * HD] = (grads * scale[...]).astype(bf16)
        gscale[...] = jnp.broadcast_to(total, gscale.shape)


def attn_bwd(qa, kv, pieces, of, mine, seg_row, scale, heads, group, groups, bq=512, bk=512):
    n = qa.shape[0]
    nh = heads // groups
    w = nh * LN
    once = pl.Buffered(1)
    spec = pltpu.PrefetchScalarGridSpec(
        num_scalar_prefetch=2,
        grid=(n // bk,),
        in_specs=[
            pl.BlockSpec((n, w), lambda i, f, m: (0, group), pipeline_mode=once),
            pl.BlockSpec((bk, w), lambda i, f, m: (i, group)),
            pl.BlockSpec((bk, w), lambda i, f, m: (i, groups + group)),
            *[pl.BlockSpec((n // 4, heads * HD), lambda i, f, m: (0, 0), pipeline_mode=once)] * 4,
            pl.BlockSpec((n, w), lambda i, f, m: (0, group), pipeline_mode=once),
            pl.BlockSpec((bk, 1), lambda i, f, m: (i, 0)),
            pl.BlockSpec((1, n), lambda i, f, m: (0, 0)),
            pl.BlockSpec((1, nh * HD), lambda i, f, m: (0, 0)),
        ],
        out_specs=[
            pl.BlockSpec((n, lanes_up(3 * nh * HD)), lambda i, f, m: (0, 0)),
            pl.BlockSpec((8, LN), lambda i, f, m: (0, 0)),
        ],
        scratch_shapes=[
            pltpu.VMEM((n, w), bf16),
            pltpu.VMEM((nh, n, LN), f32),
            pltpu.VMEM((nh, bk, LN), f32),
            pltpu.VMEM((nh, bk, LN), f32),
        ],
    )
    return pl.pallas_call(
        functools.partial(bwd_kernel, first=group * nh, nh=nh, bq=bq, bk=bk, n=n),
        out_shape=[
            pltpu.HBM((n, lanes_up(3 * nh * HD)), bf16),
            pltpu.HBM((8, LN), f32),
        ],
        grid_spec=spec,
        compiler_params=pltpu.CompilerParams(vmem_limit_bytes=48 << 20),
        cost_estimate=cost(300 if group == 0 else 0.001),
        name="attn_bwd",
    )(block_flags(seg_row, bq, bk), mine.reshape(1), hbm(qa), hbm(kv), hbm(kv), *pieces, hbm(of), seg_row[:, None], seg_row[None], scale)


def quarter_columns(place, parts, groups, nh):
    width = nh // groups * HD
    return [
        (t * D + place * nh * HD + g * width, width) for g in range(groups) for t in range(3)
    ]


def pick_kernel(mine, w_ref, out, *, parts, groups, nh):
    for i in range(parts):

        @pl.when(mine[0] == i)
        def _(i=i):
            cut = [w_ref[:, a : a + width] for a, width in quarter_columns(i, parts, groups, nh)]
            used = sum(x.shape[1] for x in cut)
            pad = jnp.zeros((cut[0].shape[0], out.shape[1] - used), out.dtype)
            out[...] = jnp.concatenate(cut + [pad], axis=1)


def lanes_up(n):
    return -(-n // LN) * LN


def pick(w, mine, parts, groups, nh):
    rows = w.shape[0]
    step = 160 if rows % 160 == 0 else rows
    return pl.pallas_call(
        functools.partial(pick_kernel, parts=parts, groups=groups, nh=nh),
        out_shape=pltpu.HBM((rows, lanes_up(3 * nh * HD)), w.dtype),
        grid_spec=pltpu.PrefetchScalarGridSpec(
            num_scalar_prefetch=1,
            grid=(rows // step,),
            in_specs=[pl.BlockSpec((step, 3 * D), lambda i, m: (i, 0))],
            out_specs=pl.BlockSpec((step, lanes_up(3 * nh * HD)), lambda i, m: (i, 0)),
        ),
        cost_estimate=cost(5),
        name="pick",
    )(mine.reshape(1), hbm(w))


def stretch_kernel(x_ref, out, *, groups, nh):
    value = x_ref[...]
    each = 3 * nh * HD // groups
    zero = jnp.zeros((value.shape[0], LN - HD), value.dtype)
    per = nh // groups
    wide = []
    for t in range(3):
        for h in range(nh):
            at = (h // per) * each + t * per * HD + (h % per) * HD
            wide += [value[:, at : at + HD], zero]
    out[...] = jnp.concatenate(wide, axis=1)


def stretch(x, groups, nh, us):
    rows, width = x.shape
    step = 160
    return pl.pallas_call(
        functools.partial(stretch_kernel, groups=groups, nh=nh),
        out_shape=pltpu.HBM((rows, 3 * nh * LN), x.dtype),
        grid=(rows // step,),
        in_specs=[pl.BlockSpec((step, width), lambda i: (i, 0))],
        out_specs=pl.BlockSpec((step, 3 * nh * LN), lambda i: (i, 0)),
        cost_estimate=cost(us),
        name="stretch",
    )(hbm(x))


def order_kernel(own_first, a_ref, b_ref, out):
    half = pl.program_id(0)

    @pl.when(half == 0)
    def _():
        out[...] = a_ref[...].T

    @pl.when(half == 1)
    def _():
        out[...] = b_ref[...].T


def order(own, other, own_at):
    rows, width = own.shape
    step = 256
    return pl.pallas_call(
        order_kernel,
        out_shape=pltpu.HBM((width, 2 * rows), own.dtype),
        grid_spec=pltpu.PrefetchScalarGridSpec(
            num_scalar_prefetch=1,
            grid=(2, width // step),
            in_specs=[
                pl.BlockSpec((rows, step), lambda i, j, m: (0, j * (1 - i))),
                pl.BlockSpec((rows, step), lambda i, j, m: (0, j * i)),
            ],
            out_specs=pl.BlockSpec((step, rows), lambda i, j, m: (j, i ^ m[0])),
        ),
        cost_estimate=cost(200.0),
        name="order",
    )(own_at.reshape(1), hbm(own), hbm(other))


def transpose_kernel(x_ref, out):
    out[...] = x_ref[...].T


def transpose(x):
    rows, cols = x.shape
    step = 256
    return pl.pallas_call(
        transpose_kernel,
        out_shape=pltpu.HBM((cols, rows), x.dtype),
        grid=(rows // step,),
        in_specs=[pl.BlockSpec((step, cols), lambda i: (i, 0))],
        out_specs=pl.BlockSpec((cols, step), lambda i: (0, i)),
        cost_estimate=CHEAP,
        name="transpose",
    )(hbm(x))


def project_kernel(info, *refs, count, halves, width, fresh):
    pairs = refs[: 2 * count]
    gain = refs[2 * count]
    weights = refs[2 * count + 1 : 2 * count + 1 + halves]
    scale, ones = refs[2 * count + 1 + halves : 2 * count + 3 + halves]
    normed_ref, q_ref, kv_ref, mine_ref, w = refs[-5:]
    j, tile = pl.program_id(0), pl.program_id(1)
    step = normed_ref.shape[0]

    @pl.when((j == 0) & (tile == 0))
    def _():
        for i, ref in enumerate(weights):
            h = ref.shape[0]
            start = (info[count + 2] ^ i) * h if halves == 2 else 0
            w[pl.ds(pl.multiple_of(start, 16), h), :] = ref[...]
        if not fresh:
            mine_ref[...] = refs[2 * count + 3 + halves][...]

    def work(x_ref):
        value = x_ref[...]
        x = value.astype(f32)
        inverse = lax.rsqrt(jnp.mean(x * x, axis=-1, keepdims=True) + epsilon)
        normed = (x * inverse * gain[...]).astype(bf16)
        normed_ref[...] = normed
        q_ref[...] = (
            jnp.dot(normed, w[:, :width], preferred_element_type=f32) * scale[...]
        ).astype(bf16)
        kv_ref[...] = (
            jnp.dot(normed, w[:, width:], preferred_element_type=f32) + ones[...]
        ).astype(bf16)

        @pl.when(info[count + 1] == info[j])
        def _():
            mine_ref[pl.ds(pl.multiple_of(tile * step, step), step), :] = value

    for i in range(count):
        for lane in range(2):

            @pl.when((j == i) & (info[count] == lane))
            def _(i=i, lane=lane):
                work(pairs[2 * i + 1 - lane])


def project(pairs, places, lane, mine, wt, gain, weights, scale, ones, group_len, carried=None):
    count = len(pairs)
    rows, d = pairs[0][0].shape
    width = scale.shape[1]
    step = 256
    tiles = rows // step
    full = lambda j, t, f: (0, 0)
    at = lambda j, t, f: (f[j] * tiles + t, 0)
    once = pl.Buffered(1)
    info = jnp.stack(list(places) + [lane.astype(jnp.int32), mine, wt])
    args = [x for pair in pairs for x in pair] + [gain, *map(hbm, weights), scale, ones]
    in_specs = [
        pl.BlockSpec(
            (step, d),
            lambda j, t, f, i=i: (jnp.where(j == i, t, jnp.where(j > i, tiles - 1, 0)), 0),
        )
        for i in range(count)
        for _ in range(2)
    ]
    in_specs += [pl.BlockSpec((1, d), full, pipeline_mode=once)]
    in_specs += [pl.BlockSpec(w.shape, full, pipeline_mode=once) for w in weights]
    in_specs += [
        pl.BlockSpec((1, width), full, pipeline_mode=once),
        pl.BlockSpec((1, 2 * width), full, pipeline_mode=once),
    ]
    aliases = {}
    if carried is not None:
        base = len(args) + 2
        args += [hbm(x) for x in (carried[3], *carried[:3])]
        in_specs += [pl.BlockSpec((rows, d), full, pipeline_mode=once)]
        in_specs += [pl.BlockSpec(memory_space=pl.ANY)] * 3
        aliases = {base: 0, base + 1: 1, base + 2: 2}
    return pl.pallas_call(
        functools.partial(
            project_kernel, count=count, halves=len(weights), width=width, fresh=carried is None
        ),
        out_shape=[
            pltpu.HBM((group_len, d), bf16),
            pltpu.HBM((group_len, width), bf16),
            pltpu.HBM((group_len, 2 * width), bf16),
            pltpu.HBM((rows, d), bf16),
        ],
        grid_spec=pltpu.PrefetchScalarGridSpec(
            num_scalar_prefetch=1,
            grid=(count, tiles),
            in_specs=in_specs,
            out_specs=[
                pl.BlockSpec((step, d), at),
                pl.BlockSpec((step, width), at),
                pl.BlockSpec((step, 2 * width), at),
                pl.BlockSpec((rows, d), full),
            ],
            scratch_shapes=[pltpu.VMEM((d, 3 * width), bf16)],
        ),
        input_output_aliases=aliases,
        compiler_params=pltpu.CompilerParams(vmem_limit_bytes=48 << 20),
        cost_estimate=cost(15),
        name="project",
    )(info, *args)


def tail_body(at, p0, p1, p2, p3, x_ref, g_ref, w_s, gain, outs):
    lo_ref, left_ref, right_ref, gr_ref, c0, c1, c2, c3, gg_ref = outs
    att_ref, nm_ref, act_ref = (left_ref.at[i] for i in range(3))
    gp_ref, gh_ref = (right_ref.at[i] for i in range(2))
    right_ref[2] = g_ref[...]
    mine = at[0]
    pieces = (p0, p1, p2, p3)
    cols = p0.shape[1]
    nt = (((1,), (1,)), ((), ()))
    for i in range(4):

        @pl.when(mine == i)
        def _(i=i):
            att_ref[...] = jnp.concatenate([pieces[i ^ k][...] for k in range(4)], axis=1)

    resid = x_ref[...].astype(f32) + jnp.dot(att_ref[...], w_s[0], preferred_element_type=f32)
    inverse = lax.rsqrt(jnp.mean(resid * resid, axis=-1, keepdims=True) + epsilon)
    normed = (resid * inverse * gain[...]).astype(bf16)
    nm_ref[...] = normed
    hidden = jnp.dot(normed, w_s[1], preferred_element_type=f32)
    sig = 1.0 / (1.0 + jnp.exp(-hidden))
    active = (hidden * sig).astype(bf16)
    act_ref[...] = active
    lo_ref[...] = (resid + jnp.dot(active, w_s[2], preferred_element_type=f32)).astype(bf16)
    grad_active = lax.dot_general(g_ref[...], w_s[2], nt, preferred_element_type=f32)
    grad_hidden = (grad_active * sig * (1.0 + hidden * (1.0 - sig))).astype(bf16)
    gh_ref[...] = grad_hidden
    grad_normed = lax.dot_general(grad_hidden, w_s[1], nt, preferred_element_type=f32)
    gg_ref[...] += jnp.sum(grad_normed * resid * inverse, axis=0, keepdims=True)
    scaled = grad_normed * gain[...]
    grad_resid = (
        g_ref[...].astype(f32)
        + inverse * scaled
        - resid * (inverse * inverse * inverse) * jnp.mean(scaled * resid, axis=-1, keepdims=True)
    )
    gr_ref[...] = grad_resid
    grad_proj = grad_resid.astype(bf16)
    gp_ref[...] = grad_proj
    grad_att = lax.dot_general(grad_proj, w_s[0], nt, preferred_element_type=f32).astype(bf16)
    for i in range(4):

        @pl.when(mine == i)
        def _(i=i):
            for j, out in enumerate((c0, c1, c2, c3)):
                out[...] = grad_att[:, (i ^ j) * cols : ((i ^ j) + 1) * cols]


def tail_kernel(at, p0, p1, p2, p3, x_ref, g_ref, own, half, other, gain, *refs, rows, hrows):
    w_s = refs[-1]
    outs = refs[:-1]

    @pl.when(pl.program_id(0) == 0)
    def _():
        outs[-1][...] = jnp.zeros_like(outs[-1])
        w_s[:, pl.ds(pl.multiple_of(at[1], 16), rows), :] = own[...]
        w_s[:, pl.ds(pl.multiple_of(at[2], 16), hrows), :] = half[...]
        w_s[:, pl.ds(pl.multiple_of(at[3], 16), hrows), :] = other[...]

    tail_body(at, p0, p1, p2, p3, x_ref, g_ref, w_s, gain, outs)


def whole_tail_kernel(at, p0, p1, p2, p3, x_ref, g_ref, w, gain, *outs):
    @pl.when(pl.program_id(0) == 0)
    def _():
        outs[-1][...] = jnp.zeros_like(outs[-1])

    tail_body(at, p0, p1, p2, p3, x_ref, g_ref, w, gain, outs)


def tail(at, pieces, x, g, weights, gain, tile=256):
    rows, d = x.shape
    cols = pieces[0].shape[1]
    row = lambda i, m: (i, 0)
    once = pl.Buffered(1)
    whole = lambda *shape: pl.BlockSpec(shape, lambda i, m: (0,) * len(shape), pipeline_mode=once)
    wide = pl.BlockSpec((tile, d), row)
    slim = pl.BlockSpec((tile, cols), row)
    if len(weights) == 3:
        body = functools.partial(tail_kernel, rows=weights[0].shape[1], hrows=weights[1].shape[1])
        scratch = [pltpu.VMEM((3, d, d), bf16)]
    else:
        body = whole_tail_kernel
        scratch = []
    return pl.pallas_call(
        body,
        out_shape=[pltpu.HBM((rows, d), bf16)]
        + [pltpu.HBM((3, rows, d), bf16)] * 2
        + [pltpu.HBM((rows, d), f32)]
        + [pltpu.HBM((rows, cols), bf16)] * 4
        + [pltpu.HBM((1, d), f32)],
        grid_spec=pltpu.PrefetchScalarGridSpec(
            num_scalar_prefetch=1,
            grid=(rows // tile,),
            in_specs=[slim] * 4 + [wide] * 2 + [whole(*w.shape) for w in weights] + [whole(1, d)],
            out_specs=[wide]
            + [pl.BlockSpec((3, tile, d), lambda i, m: (0, i, 0))] * 2
            + [wide]
            + [slim] * 4
            + [pl.BlockSpec((1, d), lambda i, m: (0, 0))],
            scratch_shapes=scratch,
        ),
        compiler_params=pltpu.CompilerParams(vmem_limit_bytes=52 << 20),
        cost_estimate=cost(0.01),
        name="tail",
    )(at, *pieces, hbm(x), g, *map(hbm, weights), gain)


tn_dims = (((0,), (0,)), ((), ()))


def share_kernel(col, left, right, *refs):
    value = lax.dot_general(left[0], right[0], tn_dims, preferred_element_type=f32)
    if len(refs) == 2:
        value = value + refs[0][...].astype(f32)
    refs[-1][...] = value.astype(bf16)


def share(left, right, col, got=None):
    n, rows, d = left.shape
    w = d // 2
    block = pl.BlockSpec((d, w), lambda i, c: (0, i))
    return pl.pallas_call(
        share_kernel,
        out_shape=pltpu.HBM((d, n * w), bf16),
        grid_spec=pltpu.PrefetchScalarGridSpec(
            num_scalar_prefetch=1,
            grid=(n,),
            in_specs=[
                pl.BlockSpec((1, rows, d), lambda i, c: (i, 0, 0)),
                pl.BlockSpec((1, rows, w), lambda i, c: (i, 0, c[0])),
            ]
            + [block] * (got is not None),
            out_specs=block,
        ),
        compiler_params=pltpu.CompilerParams(vmem_limit_bytes=40 << 20),
        cost_estimate=CHEAP,
        name="share",
    )(col.reshape(1), hbm(left), hbm(right), *(() if got is None else (hbm(got),)))


def copy(x):
    return pl.pallas_call(
        tick_kernel, out_shape=pltpu.HBM(x.shape, x.dtype), cost_estimate=CHEAP, name="copy"
    )(x)


def tick_kernel(x_ref, out):
    out[...] = x_ref[...]


def tick(x):
    return pl.pallas_call(
        tick_kernel, out_shape=jax.ShapeDtypeStruct(x.shape, x.dtype), cost_estimate=cost(200.0), name="tick"
    )(x)


def total_kernel(*refs, counts):
    out = refs[-1]
    start, column = 0, 0
    for count in counts:
        group = refs[start : start + count]
        start += count
        acc = jnp.zeros(group[0].shape[1:], f32)
        for ref in group:
            for i in range(ref.shape[0]):
                acc = acc + ref[i].astype(f32)
        out[:, column : column + acc.shape[1]] = acc.astype(bf16)
        column += acc.shape[1]


def total(groups):
    flat = [x for group in groups for x in group]
    rows = flat[0].shape[1]
    cuts = 2 if rows % 32 == 0 else 1
    width = sum(group[0].shape[2] for group in groups)
    return pl.pallas_call(
        functools.partial(total_kernel, counts=[len(group) for group in groups]),
        out_shape=pltpu.HBM((rows, width), bf16),
        grid=(cuts,),
        in_specs=[
            pl.BlockSpec((x.shape[0], rows // cuts, x.shape[2]), lambda i: (0, i, 0)) for x in flat
        ],
        out_specs=pl.BlockSpec((rows // cuts, width), lambda i: (i, 0)),
        compiler_params=pltpu.CompilerParams(vmem_limit_bytes=40 << 20),
        cost_estimate=cost(0.001),
        name="total",
    )(*flat)


def add_kernel(a_ref, b_ref, out):
    out[...] = (a_ref[...].astype(f32) + b_ref[...].astype(f32)).astype(bf16)


def add(a, b):
    return pl.pallas_call(
        add_kernel, out_shape=pltpu.HBM(a.shape, bf16), cost_estimate=CHEAP, name="add"
    )(a, b)


def pair_kernel(a_ref, b_ref, out):
    out[0] = a_ref[...]
    out[1] = b_ref[...]


def pair_up(a, b, us=0.001):
    return pl.pallas_call(
        pair_kernel, out_shape=pltpu.HBM((2,) + a.shape, bf16), cost_estimate=cost(us), name="pair_up"
    )(a, b)


def by_bits(first, second, put):
    for i in range(2):
        for j in range(2):

            @pl.when((first == i) & (second == j))
            def _(i=i, j=j):
                put(i, j)


def place_kernel(at, own, own_x, mate, mate_x, o0, o1, o2):
    block = pl.program_id(0)
    slot = (block % 2) ^ at[1]
    w = o0.shape[2] // 2

    def put(other_x, core):
        refs = (own_x, mate_x) if other_x else (own, mate)
        for side in range(2):
            part = refs[side ^ core][slot].astype(f32)
            for i, out in enumerate((o0, o1, o2)):
                out[0, :, side * w : (side + 1) * w] = part[:, i * w : (i + 1) * w]

    by_bits((block // 2) ^ at[0], at[2], put)


def place_tail(arrays, at):
    _, h, width = arrays[0].shape
    d = width // 3 * 2
    whole = pl.BlockSpec((2, h, width), lambda i, m: (0, 0, 0), pipeline_mode=pl.Buffered(1))
    outs = pl.pallas_call(
        place_kernel,
        out_shape=[pltpu.HBM((4, h, d), f32)] * 3,
        grid_spec=pltpu.PrefetchScalarGridSpec(
            num_scalar_prefetch=1,
            grid=(4,),
            in_specs=[whole] * 4,
            out_specs=[pl.BlockSpec((1, h, d), lambda i, m: (i, 0, 0))] * 3,
        ),
        compiler_params=pltpu.CompilerParams(vmem_limit_bytes=40 << 20),
        cost_estimate=cost(0.001),
        name="place_tail",
    )(at, *arrays)
    return [out.reshape(4 * h, d) for out in outs]


def cross_kernel(at, x_ref, g_ref, *refs):
    acc = refs[-1]
    w, k = pl.program_id(0), pl.program_id(1)
    value = jnp.dot(x_ref[...], g_ref[...], preferred_element_type=f32)

    @pl.when(k == 0)
    def _():
        acc[...] = value

    @pl.when(k > 0)
    def _():
        acc[...] += value

    half = acc.shape[0] // 2
    for i in range(2):

        @pl.when((w == i) & (k == pl.num_programs(1) - 1))
        def _(i=i):
            for x in range(2):
                rows = pl.ds(pl.multiple_of((at[1] ^ x) * half, 16), half)
                refs[2 * i + x][...] = acc[rows, :].astype(bf16)


def cross(x, g, at):
    d, rows = x.shape
    w = d // 2
    step = 512
    block = pl.BlockSpec((w // 2, g.shape[1]), lambda i, k, m: (0, 0))
    return pl.pallas_call(
        cross_kernel,
        out_shape=[pltpu.HBM((w // 2, g.shape[1]), bf16)] * 4,
        grid_spec=pltpu.PrefetchScalarGridSpec(
            num_scalar_prefetch=1,
            grid=(2, rows // step),
            in_specs=[
                pl.BlockSpec((w, step), lambda i, k, m: (m[0] ^ i, k)),
                pl.BlockSpec((step, g.shape[1]), lambda i, k, m: (k, 0)),
            ],
            out_specs=[block] * 4,
            scratch_shapes=[pltpu.VMEM((w, g.shape[1]), f32)],
        ),
        compiler_params=pltpu.CompilerParams(vmem_limit_bytes=40 << 20),
        cost_estimate=CHEAP,
        name="cross",
    )(at, hbm(x), hbm(g))


def spread_kernel(at, own, mate, *refs, width, other_x):
    out = refs[-1]
    step = out.shape[1]
    rows = pl.ds(pl.multiple_of(pl.program_id(0) * step, step), step)

    def put(core):
        cut = []
        for t in range(3):
            for n in range(2):
                for c in range(2):
                    part = (own, mate)[c ^ core][n ^ at[1], rows, :]
                    cut.append(part[:, t * width : (t + 1) * width])
        out[0] = jnp.concatenate(cut, axis=1).astype(f32)

    for core in range(2):

        @pl.when(at[2] == core)
        def _(core=core):
            put(core)


def spread(own, mate, at, used, other_x, carried=None):
    _, rows, cols = own.shape
    width = 4 * used
    cuts = 2 if rows % 32 == 0 else 1
    whole = pl.BlockSpec((2, rows, cols), lambda j, m: (0, 0, 0), pipeline_mode=pl.Buffered(1))
    more = () if carried is None else (carried,)
    return pl.pallas_call(
        functools.partial(spread_kernel, width=used // 3, other_x=other_x),
        out_shape=pltpu.HBM((2, rows, width), f32),
        grid_spec=pltpu.PrefetchScalarGridSpec(
            num_scalar_prefetch=1,
            grid=(cuts,),
            in_specs=[whole] * 2 + [pl.BlockSpec(memory_space=pl.ANY)] * len(more),
            out_specs=pl.BlockSpec((1, rows // cuts, width), lambda j, m: (m[0] ^ other_x, j, 0)),
        ),
        input_output_aliases={3: 0} if more else {},
        compiler_params=pltpu.CompilerParams(vmem_limit_bytes=40 << 20),
        cost_estimate=CHEAP,
        name="spread",
    )(at, own, mate, *more)


def back_kernel(shards, g_ref, w_ref, *refs):
    acc = jnp.dot(g_ref[...], w_ref[...], preferred_element_type=f32)
    if len(refs) == 2:
        acc = acc + refs[0][0].astype(f32)
    refs[-1][0] = acc.astype(bf16)


def back(grad, w, shards, rows, got=None):
    c, d = w.shape
    n = shards.shape[0]
    in_specs = [
        pl.BlockSpec((rows, c), lambda i, f: (f[i], 0)),
        pl.BlockSpec((c, d), lambda i, f: (0, 0), pipeline_mode=pl.Buffered(1)),
    ]
    args = [hbm(grad), hbm(w)]
    if got is not None:
        in_specs.append(pl.BlockSpec((1, rows, d), lambda i, f: (0, 0, 0)))
        args.append(got)
    return pl.pallas_call(
        back_kernel,
        out_shape=pltpu.HBM((n, rows, d), bf16),
        grid_spec=pltpu.PrefetchScalarGridSpec(
            num_scalar_prefetch=1,
            grid=(n,),
            in_specs=in_specs,
            out_specs=pl.BlockSpec((1, rows, d), lambda i, f: (i, 0, 0)),
        ),
        compiler_params=pltpu.CompilerParams(vmem_limit_bytes=40 << 20),
        cost_estimate=CHEAP,
        name="back",
    )(shards, *args)


def finish_kernel(shard, g_ref, w_ref, core, near, x_ref, resid, gain, out, gain_out):
    grad = jnp.dot(g_ref[...], w_ref[...], preferred_element_type=f32)
    grad = grad + core[0].astype(f32) + near[0].astype(f32)
    x = x_ref[...].astype(f32)
    inverse = lax.rsqrt(jnp.mean(x * x, axis=-1, keepdims=True) + epsilon)
    part = jnp.sum(grad * x * inverse, axis=0, keepdims=True)

    @pl.when(pl.program_id(0) == 0)
    def _():
        gain_out[...] = jnp.zeros_like(gain_out)

    gain_out[...] += part
    scaled = grad * gain[...]
    out[...] = (
        resid[...]
        + inverse * scaled
        - x * (inverse * inverse * inverse) * jnp.mean(scaled * x, axis=-1, keepdims=True)
    ).astype(bf16)


def finish(grad, w, shard, core, near, x, resid, gain, tile=256):
    rows, d = x.shape
    c = w.shape[0]
    tiles = rows // tile
    row = lambda i, f: (i, 0)
    once = pl.Buffered(1)
    return pl.pallas_call(
        finish_kernel,
        out_shape=[pltpu.HBM((rows, d), bf16), jax.ShapeDtypeStruct((1, d), f32)],
        grid_spec=pltpu.PrefetchScalarGridSpec(
            num_scalar_prefetch=1,
            grid=(tiles,),
            in_specs=[
                pl.BlockSpec((tile, c), lambda i, f: (f[0] * tiles + i, 0)),
                pl.BlockSpec((c, d), lambda i, f: (0, 0), pipeline_mode=once),
                pl.BlockSpec((1, tile, d), lambda i, f: (1, i, 0)),
                pl.BlockSpec((1, tile, d), lambda i, f: (0, i, 0)),
                pl.BlockSpec((tile, d), row),
                pl.BlockSpec((tile, d), row),
                pl.BlockSpec((1, d), lambda i, f: (0, 0)),
            ],
            out_specs=[pl.BlockSpec((tile, d), row), pl.BlockSpec((1, d), lambda i, f: (0, 0))],
        ),
        compiler_params=pltpu.CompilerParams(vmem_limit_bytes=40 << 20),
        cost_estimate=CHEAP,
        name="finish",
    )(shard.reshape(1), hbm(grad), hbm(w), core, near, hbm(x), hbm(resid), gain)


def rms_inverse(values):
    return lax.rsqrt(jnp.mean(values * values, axis=-1, keepdims=True) + epsilon)


def norm_back(values, inverse, grad_scaled):
    return inverse * grad_scaled - values * (inverse * inverse * inverse) * jnp.mean(
        grad_scaled * values, axis=-1, keepdims=True
    )


def dot(left, right):
    return jnp.dot(left, right, preferred_element_type=f32)


def times_trans(left, right):
    return lax.dot_general(left, right, (((1,), (1,)), ((), ())), preferred_element_type=f32)


def trans_times(left, right):
    return lax.dot_general(left, right, (((0,), (0,)), ((), ())), preferred_element_type=f32)


def rows_at(array, start, count):
    return lax.dynamic_slice_in_dim(array, start, count, 0)


def put_rows(array, rows, start):
    return lax.dynamic_update_slice_in_dim(array, rows, start, 0)


def make_local(sizes):
    def pairs(target):
        found = []
        for gx in range(sizes["gx"]):
            for gc in range(sizes["gc"]):
                for z in range(4):
                    for w in range(sizes["wt"]):
                        goal = target(gx, gc, z, w)
                        if goal is not None and goal != (gx, gc, z, w):
                            found.append((place(gx, gc, z, w), place(*goal)))
        return found

    def place(gx, gc, z, w):
        return ((gx * sizes["gc"] + gc) * 4 + z) * sizes["wt"] + w

    def send(value, target):
        return lax.ppermute(value, AXES, pairs(target))

    def core_mate(gx, gc, z, w):
        return (gx, 1 - gc, z, w)

    def x_mate(gx, gc, z, w):
        return (1 - gx, gc, z, w)

    def near_mate(gx, gc, z, w):
        return (gx, gc, z ^ 1, w)

    def far_mate(gx, gc, z, w):
        return (gx, gc, z ^ 2, w)

    def cross_mate(gx, gc, z, w):
        return (gx, 1 - gc, z ^ 1, w)

    def wt_mate(gx, gc, z, w):
        return (gx, gc, z, 1 - w)

    def wt_x_mate(gx, gc, z, w):
        return (1 - gx, gc, z, 1 - w)

    def to_host(gx, gc, z, w):
        return (gx, 1 - (z & 1), 2 * gc + (z >> 1), w)

    def to_home(gx, gc, z, w):
        return (gx, z >> 1, 2 * (z & 1) + 1 - gc, w)

    def hop1(gx, gc, z, w):
        if gc == 0:
            return (gx, 0, z - 1, w) if z > 0 else None
        return (gx, 1, z + 1, w) if z < 3 else None

    def hop2(gx, gc, z, w):
        if gc == 0:
            return (gx, 0, z - 1, w) if z in (1, 2) else None
        return (gx, 1, z + 1, w) if z in (1, 2) else None

    def hop3(gx, gc, z, w):
        if gc == 0:
            return (gx, 0, z ^ 1, w) if z < 2 else None
        return (gx, 1, z ^ 1, w) if z > 1 else None

    def lane_share(gx, gc, z, w):
        return (gx, 1 - gc, z, w) if gc == z >> 1 else None

    def sum_all(value):
        for axis in AXES:
            step = 1
            while step < sizes[axis]:

                def mate(gx, gc, z, w, axis=axis, step=step):
                    at = dict(gx=gx, gc=gc, far=z >> 1, near=z & 1, wt=w)
                    at[axis] ^= step
                    return (at["gx"], at["gc"], 2 * at["far"] + at["near"], at["wt"])

                value = value + send(value, mate)
                step *= 2
        return value

    def local(
        tokens, segments, w_qkv, w_proj, w_in, w_out, gain_attn, gain_mlp, query_scale, cotangent
    ):
        gx, gc, host, near, wt = (lax.axis_index(axis) for axis in AXES)
        z = 2 * host + near
        mine = 2 * near + 1 - gc
        parts = 4
        nh = H // parts
        groups = 1
        rows = tokens.shape[1]
        group_len = segments.shape[1]
        wrows = w_qkv.shape[0]
        lane = gc == host
        pair = sizes["wt"] == 2

        def after(value, *others):
            return lax.optimization_barrier((value,) + others)[0]

        picked = pick(w_qkv, mine, parts, groups, nh)
        own = tokens[0]
        got1 = send(own, hop1)
        own_share = send(own, lane_share)
        seg_mate = send(segments, core_mate)
        got2 = send(got1, hop2)
        got1_share = send(got1, lane_share)
        end = jnp.where(gc == 0, z == 0, z == 3)
        if pair:
            wide_own = stretch(picked, groups, nh, 2)
            got1 = after(got1, wide_own)
            other_w = send(picked, wt_mate)
            wide_w = (wide_own, stretch(other_w, groups, nh, 10))
        else:
            flat_all = lax.all_gather(picked, "wt", axis=0, tiled=True)
            by_head = jnp.transpose(
                flat_all[:, : 3 * nh * HD].reshape(D, groups, 3, nh // groups, HD), (0, 2, 1, 3, 4)
            )
            wide_w = (
                jnp.pad(
                    by_head.reshape(D, 3 * nh, HD), ((0, 0), (0, 0), (0, LN - HD))
                ).reshape(D, -1),
            )
        got3 = send(jnp.where(end, own, got2), hop3)
        got2_share = send(got2, lane_share)
        way = 1 - 2 * host
        last = jnp.where(host == 0, jnp.where(z == 0, 3, 0), jnp.where(z == 3, 0, 3))
        places = (z, z + way, z + 2 * way, last)

        half_rows = wrows // 2
        tail_own = jnp.stack([w_proj, w_in, w_out])
        half_w = lax.dynamic_slice_in_dim(tail_own, gc * half_rows, half_rows, 1)
        if pair:
            half_w = send(after(half_w, other_w), wt_mate)
        else:
            half_w = lax.all_gather(half_w, "wt", axis=0, tiled=False)

        dim_scale = scale_base / math.sqrt(HD) * jax.nn.softplus(query_scale)
        lane_scale = jnp.tile(jnp.pad(dim_scale * log2e, (0, LN - HD)), nh)[None]
        ones = jnp.tile(
            ((jnp.arange(LN) >= HD) & (jnp.arange(LN) < HD + 3)).astype(f32), 2 * nh
        )[None]
        seg_row = jnp.where(lane, segments, seg_mate)[0]
        fixed = (lane, mine, wt, gain_attn[None], wide_w, lane_scale, ones, group_len)
        carried = project(((own, own_share), (got1, got1_share)), places[:2], *fixed)
        got3_share = send(after(got3, carried[0]), lane_share)
        all_normed, queries, keyval, inputs = project(
            ((got2, got2_share), (got3, got3_share)), places[2:], *fixed, carried=carried
        )
        grad_mlp = send(after(cotangent[0], got3_share), to_host)

        att, att_float, q_aug = attn_fwd(queries, keyval, seg_row, nh)
        att, half_w, _ = lax.optimization_barrier((att, half_w, grad_mlp))

        trades = (core_mate, near_mate, cross_mate)
        att_pieces = [rows_at(att, (mine ^ j) * rows, rows) for j in range(parts)]
        att_pieces = [att_pieces[0]] + [send(att_pieces[j + 1], trades[j]) for j in range(3)]
        half_mate = send(half_w, core_mate)
        if pair:
            w_trans = order(after(picked, att), other_w, wt)
        else:
            w_trans = flat_all.T
        normed_trans = transpose(after(all_normed, w_trans))
        if pair:
            weights = (tail_own, half_w, half_mate)
            starts = (wt * wrows, (1 - wt) * wrows + gc * half_rows, (1 - wt) * wrows + (1 - gc) * half_rows)
        else:
            one = gc == 0
            tail_w = jnp.stack(
                [jnp.where(one, half_w, half_mate), jnp.where(one, half_mate, half_w)], axis=1
            )
            weights = (jnp.transpose(tail_w, (2, 0, 1, 3, 4)).reshape(3, D, D),)
            starts = ()
        (
            layer_out,
            left,
            right,
            grad_resid,
            *pieces,
            grad_gain_mlp,
        ) = tail(
            jnp.stack([mine, *starts]), att_pieces, after(inputs, normed_trans), grad_mlp, weights, gain_mlp[None]
        )
        pieces = [pieces[0]] + [send(pieces[j + 1], trades[j]) for j in range(3)]

        shared = share(after(left, pieces[1]), right, 1 - gc)
        from_core = send(shared, core_mate)
        pieces[2:] = [after(piece, shared) for piece in pieces[2:]]
        home_out = send(after(layer_out, *pieces[1:]), to_home)
        late_gain = tick(after(gain_attn.reshape(-1, LN), *pieces[1:]))
        summed = share(left, right, gc, after(from_core, late_gain))
        kept = lax.all_to_all(summed, ("wt", "gx", "near"), 0, 0, tiled=True)

        scale_row = jnp.tile(dim_scale, nh // groups)[None]

        def backward(group, *others):
            first, *rest = pieces
            return attn_bwd(
                q_aug,
                keyval,
                (after(first, summed, *others), *rest),
                att_float,
                mine,
                seg_row,
                scale_row,
                nh,
                group,
                groups,
            )

        def by_rows(grad):
            if pair:
                own, *rest = cross(normed_trans, grad, jnp.stack([wt, gx]))
                got = [send(part, mate) for part, mate in zip(rest, (x_mate, wt_mate, wt_x_mate))]
                return [part[None] for part in (own, *got)]
            part = dot(normed_trans, grad).astype(bf16)
            sources = sizes["wt"] * 2
            got = lax.all_to_all(part, ("wt", "gx"), 0, 0, tiled=True)
            return [got.reshape(sources, D // sources, -1)]

        grad_project, grad_lanes = backward(0)
        layer_out = after(home_out, grad_project)

        last_step = [layer_out]

        def turn(value):
            return after(value, *last_step)

        def done(value):
            last_step[0] = value
            return value

        sources = sizes["wt"] * 4
        to_core = done(back(turn(grad_project), w_trans, jnp.stack([mine ^ 3, mine ^ 1]), rows))
        from_core = send(to_core, core_mate)
        by_place = by_rows(turn(grad_project))
        done(by_place[0])
        to_near = done(back(grad_project, w_trans, (mine ^ 2).reshape(1), rows, turn(from_core)))
        from_near = send(to_near, near_mate)
        t1 = done(total([[turn(kept).reshape(sources, D // sources, -1)]]))
        t1_far = send(t1, far_mate)
        layer_out = done(copy(turn(layer_out)))
        by_place[0] = turn(by_place[0])
        q1 = done(total([by_place]))
        q1_far = send(q1, far_mate)
        grad_tokens, grad_gain_attn = finish(
            grad_project,
            w_trans,
            mine,
            from_core,
            turn(from_near),
            inputs,
            grad_resid,
            late_gain.reshape(1, -1),
        )
        done(grad_tokens)
        home_grad = send(grad_tokens, to_home)
        t2 = done(add(turn(t1), t1_far))
        t2_near = send(t2, near_mate)
        grad_query_scale = (
            grad_lanes[0, :HD]
            / (dim_scale * log2e)
            * (scale_base / math.sqrt(HD))
            * jax.nn.sigmoid(query_scale)
        )
        small = jnp.concatenate(
            [grad_gain_attn[0], grad_gain_mlp[0], jnp.pad(grad_query_scale, (0, LN - HD))]
        ).reshape(-1, LN)
        q2 = done(add(turn(q1), q1_far))
        q2_near = send(q2, near_mate)
        t4 = done(pair_up(turn(t2), t2_near))
        t4_x = send(t4, x_mate)
        t4_core = send(t4, core_mate)
        grad_tokens = done(turn(home_grad))
        q4 = done(pair_up(turn(q2), q2_near))
        q4_x = send(q4, x_mate)
        q4_core = send(q4, core_mate)
        t4_x = done(turn(t4_x))
        t4_cross = send(t4_x, core_mate)
        used = 3 * nh * HD
        spread_at = jnp.stack([gx, near, 1 - gc])
        totals = place_tail((turn(t4), t4_x, t4_core, t4_cross), jnp.stack([gx, near, gc]))
        done(totals[0])
        total_qkv = done(spread(turn(q4), q4_core, spread_at, used, 0))
        small = done(sum_all(turn(small))).reshape(-1)
        q4_x = done(turn(q4_x))
        q4_cross = send(q4_x, core_mate)
        total_qkv = spread(turn(q4_x), q4_cross, spread_at, used, 1, total_qkv).reshape(wrows, 3 * D)
        return (
            layer_out[None],
            grad_tokens[None],
            total_qkv,
            *totals,
            small[:D],
            small[D : 2 * D],
            small[2 * D : 2 * D + HD],
        )

    return local


def solution(mesh):
    groups, parts, wt = (mesh.shape[axis] for axis in ("grp", "ctx", "wt"))
    inner = Mesh(mesh.devices.reshape(groups // 2, 2, parts // 2, 2, wt), AXES)
    sizes = dict(inner.shape)
    split = P(("gx", "gc", "wt"), ("far", "near"), None)
    weight = P("wt", None)
    return jax.shard_map(
        make_local(sizes),
        mesh=inner,
        in_specs=(
            split,
            P(("gx", "gc", "wt"), None),
            weight,
            weight,
            weight,
            weight,
            P(),
            P(),
            P(),
            split,
        ),
        out_specs=(split, split, weight, weight, weight, weight, P(), P(), P()),
        check_vma=False,
    )
```

```python
import functools
import math

import jax
import jax.numpy as jnp
from jax import lax
from jax.experimental import pallas as pl
from jax.experimental.pallas import tpu as pltpu
from jax.sharding import Mesh
from jax.sharding import PartitionSpec as P

D = 1280
H = 16
HD = 80
LN = 128
epsilon = 1e-06
scale_base = 1.442695041
log2e = 1.4426950408889634
NEG = -1e30
def cost(us):
    return pl.CostEstimate(flops=int(us * 1_000_000_000), transcendentals=0, bytes_accessed=1000)


CHEAP = cost(0.001)
f32 = jnp.float32
bf16 = jnp.bfloat16
AXES = ("gx", "gc", "far", "near", "wt")


def hbm(x):
    return pltpu.with_memory_space_constraint(x, pltpu.HBM)


def block_flags(seg_row, bq, bk):
    n = seg_row.shape[0]
    q = seg_row.reshape(n // bq, bq)
    k = seg_row.reshape(n // bk, bk)
    qf, ql = q[:, 0][:, None], q[:, -1][:, None]
    kf, kl = k[:, 0][None], k[:, -1][None]
    qs = jnp.arange(n // bq, dtype=jnp.int32)[:, None] * bq
    ks = jnp.arange(n // bk, dtype=jnp.int32)[None] * bk
    below = ks + bk - 1 <= qs
    skip = (ks > qs + bq - 1) | ((kf > 0) & (kl < qf))
    same = (qf == ql) & (kl == ql) & ((kf == kl) | ((kf == 0) & (kl == 1)))
    full = below & ((kl == 0) | same)
    flags = jnp.where(skip, 0, jnp.where(full, 1, 2))
    if bq == bk:
        flags = jnp.where(qs == ks, 3, flags)
    return flags.astype(jnp.int32).reshape(-1)


def put_split(base, col, lanes):
    hi = col.astype(bf16).astype(f32)
    rest = col - hi
    mid = rest.astype(bf16).astype(f32)
    out = jnp.where(lanes == HD, hi, base)
    out = jnp.where(lanes == HD + 1, mid, out)
    return jnp.where(lanes == HD + 2, rest - mid, out).astype(bf16)


def fwd_kernel(flags, q_ref, kv, segc, segr, att, of, qaug, m_s, acc_s, *, nh, bq, bk, nk):
    qi = pl.program_id(0)
    count = (qi * bq + bq + bk - 1) // bk
    nt = (((1,), (1,)), ((), ()))
    acc_s[...] = jnp.zeros_like(acc_s)
    m_s[...] = jnp.zeros_like(m_s)

    def mask(ko, q0=0, qn=bq, kn=bk):
        qpos = qi * bq + q0 + lax.broadcasted_iota(jnp.int32, (qn, kn), 0)
        kpos = ko + lax.broadcasted_iota(jnp.int32, (qn, kn), 1)
        ks = segr[:, pl.ds(ko, kn)]
        return (kpos <= qpos) & ((ks == 0) | (ks == segc[q0 : q0 + qn, :]))

    def step(kb, masked, q0=0, qn=bq, kn=bk):
        ko = pl.multiple_of(kb * bk, bk)
        if masked:
            allowed = mask(ko, q0, qn, kn)
        rows = slice(q0, q0 + qn)
        for h in range(nh):
            k = kv[pl.ds(ko, kn), h * LN : (h + 1) * LN]
            v = kv[pl.ds(ko, kn), (nh + h) * LN : (nh + h + 1) * LN]
            q = q_ref[rows, h * LN : (h + 1) * LN]
            p = jnp.exp2(lax.dot_general(q, k, nt, preferred_element_type=f32))
            if masked:
                p = jnp.where(allowed, p, 0.0)
            acc_s[h, rows, :] += jnp.dot(p.astype(bf16), v, preferred_element_type=f32)

    def body(kb, carry):
        flag = flags[qi * nk + kb]

        @pl.when(flag == 1)
        def _():
            step(kb, False)

        @pl.when(flag == 2)
        def _():
            step(kb, True)

        if bq == bk:

            @pl.when(flag == 3)
            def _():
                step(kb, True, 0, bq // 2, bk // 2)
                step(kb, True, bq // 2, bq // 2, bk)

        return carry

    lax.fori_loop(0, count, body, 0)
    bad = jnp.zeros((bq, 1), f32)
    for h in range(nh):
        total = acc_s[h][:, HD : HD + 1]
        bad = jnp.maximum(bad, jnp.where((total > 2.0**-60) & (total < 2.0**60), 0.0, 1.0))

    @pl.when(jnp.max(bad) > 0.0)
    def _():
        def head(h, carry):
            kc = pl.ds(pl.multiple_of(h * LN, LN), LN)
            vc = pl.ds(pl.multiple_of((nh + h) * LN, LN), LN)
            m_s[h] = jnp.full((bq, LN), NEG, f32)
            acc_s[h] = jnp.zeros((bq, LN), f32)

            def inner(kb, carry):
                @pl.when(flags[qi * nk + kb] > 0)
                def _():
                    ko = pl.multiple_of(kb * bk, bk)
                    s = lax.dot_general(
                        q_ref[:, kc], kv[pl.ds(ko, bk), kc], nt, preferred_element_type=f32
                    )
                    s = jnp.where(mask(ko), s, NEG)
                    old = m_s[h]
                    new = jnp.maximum(old, jnp.max(s, axis=1, keepdims=True))
                    p = jnp.exp2(s - new[:, :1]).astype(bf16)
                    m_s[h] = new
                    acc_s[h] = acc_s[h] * jnp.exp2(old - new) + jnp.dot(
                        p, kv[pl.ds(ko, bk), vc], preferred_element_type=f32
                    )

                return carry

            lax.fori_loop(0, count, inner, 0)
            return carry

        lax.fori_loop(0, nh, head, 0)

    lanes = lax.broadcasted_iota(jnp.int32, (bq, LN), 1)
    outs = []
    for h in range(nh):
        acc = acc_s[h]
        total = acc[:, HD : HD + 1]
        out = acc * (1.0 / total)
        of[:, h * LN : (h + 1) * LN] = jnp.where(lanes < HD, out, 0.0).astype(bf16)
        outs.append(out[:, :HD])
        lse = m_s[h][:, :1] + jnp.log2(total)
        qaug[:, h * LN : (h + 1) * LN] = put_split(
            q_ref[:, h * LN : (h + 1) * LN].astype(f32), -lse, lanes
        )
    att[...] = jnp.concatenate(outs, axis=1).astype(bf16)


def attn_fwd(q, kv, seg_row, nh, bq=512, bk=512):
    n = q.shape[0]
    w = nh * LN
    spec = pltpu.PrefetchScalarGridSpec(
        num_scalar_prefetch=1,
        grid=(n // bq,),
        in_specs=[
            pl.BlockSpec((bq, w), lambda i, f: (i, 0)),
            pl.BlockSpec((n, 2 * w), lambda i, f: (0, 0)),
            pl.BlockSpec((bq, 1), lambda i, f: (i, 0)),
            pl.BlockSpec((1, n), lambda i, f: (0, 0)),
        ],
        out_specs=[
            pl.BlockSpec((bq, nh * HD), lambda i, f: (i, 0)),
            pl.BlockSpec((bq, w), lambda i, f: (i, 0)),
            pl.BlockSpec((bq, w), lambda i, f: (i, 0)),
        ],
        scratch_shapes=[pltpu.VMEM((nh, bq, LN), f32), pltpu.VMEM((nh, bq, LN), f32)],
    )
    return pl.pallas_call(
        functools.partial(fwd_kernel, nh=nh, bq=bq, bk=bk, nk=n // bk),
        out_shape=[
            pltpu.HBM((n, nh * HD), bf16),
            pltpu.HBM((n, w), bf16),
            pltpu.HBM((n, w), bf16),
        ],
        grid_spec=spec,
        compiler_params=pltpu.CompilerParams(vmem_limit_bytes=40 << 20),
        cost_estimate=cost(0.01),
        name="attn_fwd",
    )(block_flags(seg_row, bq, bk), hbm(q), hbm(kv), seg_row[:, None], seg_row[None])


def bwd_kernel(
    flags, mine, qa, kk, vv, do0, do1, do2, do3, of, segc, segr, scale, dqkv, gscale, doa_s, dq_s, dk_s, dv_s, *, first, nh, bq, bk, n
):
    nk = n // bk
    nq = n // bq
    kb = pl.program_id(0)
    part = n // 4
    step_rows = 256 if part % 256 == 0 else part
    lanes = lax.broadcasted_iota(jnp.int32, (step_rows, LN), 1)

    @pl.when(kb == 0)
    def _():
        dq_s[...] = jnp.zeros_like(dq_s)
        for j, piece in enumerate((do0, do1, do2, do3)):
            start = (mine[0] ^ j) * part
            for i in range(part // step_rows):
                d = piece[i * step_rows : (i + 1) * step_rows, :].astype(f32)
                r = pl.ds(pl.multiple_of(start + i * step_rows, step_rows), step_rows)
                for h in range(nh):
                    at = (first + h) * HD
                    dh = jnp.concatenate(
                        [d[:, at : at + HD], jnp.zeros((step_rows, LN - HD), f32)], axis=1
                    )
                    c = slice(h * LN, (h + 1) * LN)
                    delta = jnp.sum(dh * of[r, c].astype(f32), axis=1, keepdims=True)
                    doa_s[r, c] = put_split(dh, -delta, lanes)

    dk_s[...] = jnp.zeros_like(dk_s)
    dv_s[...] = jnp.zeros_like(dv_s)
    ko = kb * bk
    nt = (((1,), (1,)), ((), ()))
    tn = (((0,), (0,)), ((), ()))

    def step(qi, masked, q0=0, qn=bq, kn=bk):
        qo = pl.multiple_of(qi * bq + q0, qn)
        rows = slice(0, kn)
        if masked:
            kpos = ko + lax.broadcasted_iota(jnp.int32, (kn, qn), 0)
            qpos = qo + lax.broadcasted_iota(jnp.int32, (kn, qn), 1)
            ks = segc[rows, :]
            allowed = (kpos <= qpos) & ((ks == 0) | (ks == segr[:, pl.ds(qo, qn)]))
        for h in range(nh):
            c = slice(h * LN, (h + 1) * LN)
            q = qa[pl.ds(qo, qn), c]
            k = kk[rows, c]
            d = doa_s[pl.ds(qo, qn), c]
            p = jnp.exp2(lax.dot_general(k, q, nt, preferred_element_type=f32))
            if masked:
                p = jnp.where(allowed, p, 0.0)
            ds = (p * lax.dot_general(vv[rows, c], d, nt, preferred_element_type=f32)).astype(bf16)
            dv_s[h, rows, :] += jnp.dot(p.astype(bf16), d, preferred_element_type=f32)
            dk_s[h, rows, :] += jnp.dot(ds, q, preferred_element_type=f32)
            dq_s[h, pl.ds(qo, qn), :] += lax.dot_general(ds, k, tn, preferred_element_type=f32)

    def body(qi, carry):
        flag = flags[qi * nk + kb]

        @pl.when(flag == 1)
        def _():
            step(qi, False)

        @pl.when(flag == 2)
        def _():
            step(qi, True)

        if bq == bk:

            @pl.when(flag == 3)
            def _():
                step(qi, True, 0, bq // 2, bk // 2)
                step(qi, True, bq // 2, bq // 2, bk)

        return carry

    lax.fori_loop(ko // bq, nq, body, 0)
    r = pl.multiple_of(ko, bk)
    ln2 = math.log(2.0)
    gap = dqkv.shape[1] - 3 * nh * HD
    dqkv[pl.ds(r, bk), nh * HD :] = jnp.concatenate(
        [dk_s[h][:, :HD] * ln2 for h in range(nh)]
        + [dv_s[h][:, :HD] for h in range(nh)]
        + [jnp.zeros((bk, gap), f32)],
        axis=1,
    ).astype(bf16)

    @pl.when(kb == nk - 1)
    def _():
        total = jnp.zeros((1, LN), f32)
        for i in range(nq):
            rows = slice(i * bq, (i + 1) * bq)
            for h in range(nh):
                total = total + jnp.sum(
                    dq_s[h, rows, :] * qa[rows, h * LN : (h + 1) * LN].astype(f32), axis=0, keepdims=True
                )
            grads = jnp.concatenate([dq_s[h, rows, :][:, :HD] for h in range(nh)], axis=1)
            dqkv[rows, 0 : nh * HD] = (grads * scale[...]).astype(bf16)
        gscale[...] = jnp.broadcast_to(total, gscale.shape)


def attn_bwd(qa, kv, pieces, of, mine, seg_row, scale, heads, group, groups, bq=512, bk=512):
    n = qa.shape[0]
    nh = heads // groups
    w = nh * LN
    once = pl.Buffered(1)
    spec = pltpu.PrefetchScalarGridSpec(
        num_scalar_prefetch=2,
        grid=(n // bk,),
        in_specs=[
            pl.BlockSpec((n, w), lambda i, f, m: (0, group), pipeline_mode=once),
            pl.BlockSpec((bk, w), lambda i, f, m: (i, group)),
            pl.BlockSpec((bk, w), lambda i, f, m: (i, groups + group)),
            *[pl.BlockSpec((n // 4, heads * HD), lambda i, f, m: (0, 0), pipeline_mode=once)] * 4,
            pl.BlockSpec((n, w), lambda i, f, m: (0, group), pipeline_mode=once),
            pl.BlockSpec((bk, 1), lambda i, f, m: (i, 0)),
            pl.BlockSpec((1, n), lambda i, f, m: (0, 0)),
            pl.BlockSpec((1, nh * HD), lambda i, f, m: (0, 0)),
        ],
        out_specs=[
            pl.BlockSpec((n, lanes_up(3 * nh * HD)), lambda i, f, m: (0, 0)),
            pl.BlockSpec((8, LN), lambda i, f, m: (0, 0)),
        ],
        scratch_shapes=[
            pltpu.VMEM((n, w), bf16),
            pltpu.VMEM((nh, n, LN), f32),
            pltpu.VMEM((nh, bk, LN), f32),
            pltpu.VMEM((nh, bk, LN), f32),
        ],
    )
    return pl.pallas_call(
        functools.partial(bwd_kernel, first=group * nh, nh=nh, bq=bq, bk=bk, n=n),
        out_shape=[
            pltpu.HBM((n, lanes_up(3 * nh * HD)), bf16),
            pltpu.HBM((8, LN), f32),
        ],
        grid_spec=spec,
        compiler_params=pltpu.CompilerParams(vmem_limit_bytes=48 << 20),
        cost_estimate=cost(300 if group == 0 else 0.001),
        name="attn_bwd",
    )(block_flags(seg_row, bq, bk), mine.reshape(1), hbm(qa), hbm(kv), hbm(kv), *pieces, hbm(of), seg_row[:, None], seg_row[None], scale)


def quarter_columns(place, parts, groups, nh):
    width = nh // groups * HD
    return [
        (t * D + place * nh * HD + g * width, width) for g in range(groups) for t in range(3)
    ]


def pick_kernel(mine, w_ref, out, *, parts, groups, nh):
    for i in range(parts):

        @pl.when(mine[0] == i)
        def _(i=i):
            cut = [w_ref[:, a : a + width] for a, width in quarter_columns(i, parts, groups, nh)]
            used = sum(x.shape[1] for x in cut)
            pad = jnp.zeros((cut[0].shape[0], out.shape[1] - used), out.dtype)
            out[...] = jnp.concatenate(cut + [pad], axis=1)


def lanes_up(n):
    return -(-n // LN) * LN


def pick(w, mine, parts, groups, nh):
    rows = w.shape[0]
    step = 160 if rows % 160 == 0 else rows
    return pl.pallas_call(
        functools.partial(pick_kernel, parts=parts, groups=groups, nh=nh),
        out_shape=pltpu.HBM((rows, lanes_up(3 * nh * HD)), w.dtype),
        grid_spec=pltpu.PrefetchScalarGridSpec(
            num_scalar_prefetch=1,
            grid=(rows // step,),
            in_specs=[pl.BlockSpec((step, 3 * D), lambda i, m: (i, 0))],
            out_specs=pl.BlockSpec((step, lanes_up(3 * nh * HD)), lambda i, m: (i, 0)),
        ),
        cost_estimate=cost(5),
        name="pick",
    )(mine.reshape(1), hbm(w))


def stretch_kernel(x_ref, out, *, groups, nh):
    value = x_ref[...]
    each = 3 * nh * HD // groups
    zero = jnp.zeros((value.shape[0], LN - HD), value.dtype)
    per = nh // groups
    wide = []
    for t in range(3):
        for h in range(nh):
            at = (h // per) * each + t * per * HD + (h % per) * HD
            wide += [value[:, at : at + HD], zero]
    out[...] = jnp.concatenate(wide, axis=1)


def stretch(x, groups, nh, us):
    rows, width = x.shape
    step = 160
    return pl.pallas_call(
        functools.partial(stretch_kernel, groups=groups, nh=nh),
        out_shape=pltpu.HBM((rows, 3 * nh * LN), x.dtype),
        grid=(rows // step,),
        in_specs=[pl.BlockSpec((step, width), lambda i: (i, 0))],
        out_specs=pl.BlockSpec((step, 3 * nh * LN), lambda i: (i, 0)),
        cost_estimate=cost(us),
        name="stretch",
    )(hbm(x))


def order_kernel(own_first, a_ref, b_ref, out):
    half = pl.program_id(0)

    @pl.when(half == 0)
    def _():
        out[...] = a_ref[...].T

    @pl.when(half == 1)
    def _():
        out[...] = b_ref[...].T


def order(own, other, own_at):
    rows, width = own.shape
    step = 256
    return pl.pallas_call(
        order_kernel,
        out_shape=pltpu.HBM((width, 2 * rows), own.dtype),
        grid_spec=pltpu.PrefetchScalarGridSpec(
            num_scalar_prefetch=1,
            grid=(2, width // step),
            in_specs=[
                pl.BlockSpec((rows, step), lambda i, j, m: (0, j * (1 - i))),
                pl.BlockSpec((rows, step), lambda i, j, m: (0, j * i)),
            ],
            out_specs=pl.BlockSpec((step, rows), lambda i, j, m: (j, i ^ m[0])),
        ),
        cost_estimate=cost(200.0),
        name="order",
    )(own_at.reshape(1), hbm(own), hbm(other))


def transpose_kernel(x_ref, out):
    out[...] = x_ref[...].T


def transpose(x):
    rows, cols = x.shape
    step = 256
    return pl.pallas_call(
        transpose_kernel,
        out_shape=pltpu.HBM((cols, rows), x.dtype),
        grid=(rows // step,),
        in_specs=[pl.BlockSpec((step, cols), lambda i: (i, 0))],
        out_specs=pl.BlockSpec((cols, step), lambda i: (0, i)),
        cost_estimate=CHEAP,
        name="transpose",
    )(hbm(x))


def project_kernel(info, *refs, count, halves, width, fresh):
    pairs = refs[: 2 * count]
    gain = refs[2 * count]
    weights = refs[2 * count + 1 : 2 * count + 1 + halves]
    scale, ones = refs[2 * count + 1 + halves : 2 * count + 3 + halves]
    normed_ref, q_ref, kv_ref, mine_ref, w = refs[-5:]
    j, tile = pl.program_id(0), pl.program_id(1)
    step = normed_ref.shape[0]

    @pl.when((j == 0) & (tile == 0))
    def _():
        for i, ref in enumerate(weights):
            h = ref.shape[0]
            start = (info[count + 2] ^ i) * h if halves == 2 else 0
            w[pl.ds(pl.multiple_of(start, 16), h), :] = ref[...]
        if not fresh:
            mine_ref[...] = refs[2 * count + 3 + halves][...]

    def work(x_ref):
        value = x_ref[...]
        x = value.astype(f32)
        inverse = lax.rsqrt(jnp.mean(x * x, axis=-1, keepdims=True) + epsilon)
        normed = (x * inverse * gain[...]).astype(bf16)
        normed_ref[...] = normed
        q_ref[...] = (
            jnp.dot(normed, w[:, :width], preferred_element_type=f32) * scale[...]
        ).astype(bf16)
        kv_ref[...] = (
            jnp.dot(normed, w[:, width:], preferred_element_type=f32) + ones[...]
        ).astype(bf16)

        @pl.when(info[count + 1] == info[j])
        def _():
            mine_ref[pl.ds(pl.multiple_of(tile * step, step), step), :] = value

    for i in range(count):
        for lane in range(2):

            @pl.when((j == i) & (info[count] == lane))
            def _(i=i, lane=lane):
                work(pairs[2 * i + 1 - lane])


def project(pairs, places, lane, mine, wt, gain, weights, scale, ones, group_len, carried=None):
    count = len(pairs)
    rows, d = pairs[0][0].shape
    width = scale.shape[1]
    step = 256
    tiles = rows // step
    full = lambda j, t, f: (0, 0)
    at = lambda j, t, f: (f[j] * tiles + t, 0)
    once = pl.Buffered(1)
    info = jnp.stack(list(places) + [lane.astype(jnp.int32), mine, wt])
    args = [x for pair in pairs for x in pair] + [gain, *map(hbm, weights), scale, ones]
    in_specs = [
        pl.BlockSpec(
            (step, d),
            lambda j, t, f, i=i: (jnp.where(j == i, t, jnp.where(j > i, tiles - 1, 0)), 0),
        )
        for i in range(count)
        for _ in range(2)
    ]
    in_specs += [pl.BlockSpec((1, d), full, pipeline_mode=once)]
    in_specs += [pl.BlockSpec(w.shape, full, pipeline_mode=once) for w in weights]
    in_specs += [
        pl.BlockSpec((1, width), full, pipeline_mode=once),
        pl.BlockSpec((1, 2 * width), full, pipeline_mode=once),
    ]
    aliases = {}
    if carried is not None:
        base = len(args) + 2
        args += [hbm(x) for x in (carried[3], *carried[:3])]
        in_specs += [pl.BlockSpec((rows, d), full, pipeline_mode=once)]
        in_specs += [pl.BlockSpec(memory_space=pl.ANY)] * 3
        aliases = {base: 0, base + 1: 1, base + 2: 2}
    return pl.pallas_call(
        functools.partial(
            project_kernel, count=count, halves=len(weights), width=width, fresh=carried is None
        ),
        out_shape=[
            pltpu.HBM((group_len, d), bf16),
            pltpu.HBM((group_len, width), bf16),
            pltpu.HBM((group_len, 2 * width), bf16),
            pltpu.HBM((rows, d), bf16),
        ],
        grid_spec=pltpu.PrefetchScalarGridSpec(
            num_scalar_prefetch=1,
            grid=(count, tiles),
            in_specs=in_specs,
            out_specs=[
                pl.BlockSpec((step, d), at),
                pl.BlockSpec((step, width), at),
                pl.BlockSpec((step, 2 * width), at),
                pl.BlockSpec((rows, d), full),
            ],
            scratch_shapes=[pltpu.VMEM((d, 3 * width), bf16)],
        ),
        input_output_aliases=aliases,
        compiler_params=pltpu.CompilerParams(vmem_limit_bytes=48 << 20),
        cost_estimate=cost(15),
        name="project",
    )(info, *args)


def tail_body(at, p0, p1, p2, p3, x_ref, g_ref, w_s, gain, outs, need):
    lo_ref, left_ref, right_ref, gr_ref, c0, c1, c2, c3, gg_ref = outs
    att_ref, nm_ref, act_ref = (left_ref.at[i] for i in range(3))
    gp_ref, gh_ref = (right_ref.at[i] for i in range(2))
    right_ref[2] = g_ref[...]
    mine = at[0]
    pieces = (p0, p1, p2, p3)
    cols = p0.shape[1]
    nt = (((1,), (1,)), ((), ()))
    for i in range(4):

        @pl.when(mine == i)
        def _(i=i):
            att_ref[...] = jnp.concatenate([pieces[i ^ k][...] for k in range(4)], axis=1)

    need(0)
    resid = x_ref[...].astype(f32) + jnp.dot(att_ref[...], w_s[0], preferred_element_type=f32)
    inverse = lax.rsqrt(jnp.mean(resid * resid, axis=-1, keepdims=True) + epsilon)
    normed = (resid * inverse * gain[...]).astype(bf16)
    nm_ref[...] = normed
    need(1)
    hidden = jnp.dot(normed, w_s[1], preferred_element_type=f32)
    sig = 1.0 / (1.0 + jnp.exp(-hidden))
    active = (hidden * sig).astype(bf16)
    act_ref[...] = active
    need(2)
    lo_ref[...] = (resid + jnp.dot(active, w_s[2], preferred_element_type=f32)).astype(bf16)
    grad_active = lax.dot_general(g_ref[...], w_s[2], nt, preferred_element_type=f32)
    grad_hidden = (grad_active * sig * (1.0 + hidden * (1.0 - sig))).astype(bf16)
    gh_ref[...] = grad_hidden
    grad_normed = lax.dot_general(grad_hidden, w_s[1], nt, preferred_element_type=f32)
    gg_ref[...] += jnp.sum(grad_normed * resid * inverse, axis=0, keepdims=True)
    scaled = grad_normed * gain[...]
    grad_resid = (
        g_ref[...].astype(f32)
        + inverse * scaled
        - resid * (inverse * inverse * inverse) * jnp.mean(scaled * resid, axis=-1, keepdims=True)
    )
    gr_ref[...] = grad_resid
    grad_proj = grad_resid.astype(bf16)
    gp_ref[...] = grad_proj
    grad_att = lax.dot_general(grad_proj, w_s[0], nt, preferred_element_type=f32).astype(bf16)
    for i in range(4):

        @pl.when(mine == i)
        def _(i=i):
            for j, out in enumerate((c0, c1, c2, c3)):
                out[...] = grad_att[:, (i ^ j) * cols : ((i ^ j) + 1) * cols]


def tail_kernel(at, p0, p1, p2, p3, x_ref, g_ref, own0, own1, own2, half, other, gain, *refs, rows, hrows):
    w_s, sems = refs[-2:]
    outs = refs[:-2]

    def copies(i):
        parts = (((own0, own1, own2)[i], at[1], rows), (half.at[i], at[2], hrows), (other.at[i], at[3], hrows))
        return [
            pltpu.make_async_copy(
                part, w_s.at[i, pl.ds(pl.multiple_of(start, 16), n), :], sems.at[3 * i + k]
            )
            for k, (part, start, n) in enumerate(parts)
        ]

    @pl.when(pl.program_id(0) == 0)
    def _():
        outs[-1][...] = jnp.zeros_like(outs[-1])
        for i in range(3):
            for c in copies(i):
                c.start()

    def need(i):
        @pl.when(pl.program_id(0) == 0)
        def _():
            for c in copies(i):
                c.wait()

    tail_body(at, p0, p1, p2, p3, x_ref, g_ref, w_s, gain, outs, need)


def whole_tail_kernel(at, p0, p1, p2, p3, x_ref, g_ref, w, gain, *outs):
    @pl.when(pl.program_id(0) == 0)
    def _():
        outs[-1][...] = jnp.zeros_like(outs[-1])

    tail_body(at, p0, p1, p2, p3, x_ref, g_ref, w, gain, outs, lambda i: None)


def tail(at, pieces, x, g, weights, gain, tile=256):
    rows, d = x.shape
    cols = pieces[0].shape[1]
    row = lambda i, m: (i, 0)
    once = pl.Buffered(1)
    whole = lambda *shape: pl.BlockSpec(shape, lambda i, m: (0,) * len(shape), pipeline_mode=once)
    wide = pl.BlockSpec((tile, d), row)
    slim = pl.BlockSpec((tile, cols), row)
    if len(weights) == 5:
        body = functools.partial(tail_kernel, rows=weights[0].shape[0], hrows=weights[3].shape[1])
        scratch = [pltpu.VMEM((3, d, d), bf16), pltpu.SemaphoreType.DMA((9,))]
        weight_specs = [pl.BlockSpec(memory_space=pl.ANY)] * 5
    else:
        body = whole_tail_kernel
        scratch = []
        weight_specs = [whole(*w.shape) for w in weights]
    return pl.pallas_call(
        body,
        out_shape=[pltpu.HBM((rows, d), bf16)]
        + [pltpu.HBM((3, rows, d), bf16)] * 2
        + [pltpu.HBM((rows, d), f32)]
        + [pltpu.HBM((rows, cols), bf16)] * 4
        + [pltpu.HBM((1, d), f32)],
        grid_spec=pltpu.PrefetchScalarGridSpec(
            num_scalar_prefetch=1,
            grid=(rows // tile,),
            in_specs=[slim] * 4 + [wide] * 2 + weight_specs + [whole(1, d)],
            out_specs=[wide]
            + [pl.BlockSpec((3, tile, d), lambda i, m: (0, i, 0))] * 2
            + [wide]
            + [slim] * 4
            + [pl.BlockSpec((1, d), lambda i, m: (0, 0))],
            scratch_shapes=scratch,
        ),
        compiler_params=pltpu.CompilerParams(vmem_limit_bytes=52 << 20),
        cost_estimate=cost(0.01),
        name="tail",
    )(at, *pieces, hbm(x), g, *map(hbm, weights), gain)


tn_dims = (((0,), (0,)), ((), ()))


def share_kernel(col, left, right, *refs):
    value = lax.dot_general(left[0], right[0], tn_dims, preferred_element_type=f32)
    if len(refs) == 2:
        value = value + refs[0][...].astype(f32)
    refs[-1][...] = value.astype(bf16)


def share(left, right, col, got=None):
    n, rows, d = left.shape
    w = d // 2
    block = pl.BlockSpec((d, w), lambda i, c: (0, i))
    return pl.pallas_call(
        share_kernel,
        out_shape=pltpu.HBM((d, n * w), bf16),
        grid_spec=pltpu.PrefetchScalarGridSpec(
            num_scalar_prefetch=1,
            grid=(n,),
            in_specs=[
                pl.BlockSpec((1, rows, d), lambda i, c: (i, 0, 0)),
                pl.BlockSpec((1, rows, w), lambda i, c: (i, 0, c[0])),
            ]
            + [block] * (got is not None),
            out_specs=block,
        ),
        compiler_params=pltpu.CompilerParams(vmem_limit_bytes=40 << 20),
        cost_estimate=CHEAP,
        name="share",
    )(col.reshape(1), hbm(left), hbm(right), *(() if got is None else (hbm(got),)))


def copy(x):
    return pl.pallas_call(
        tick_kernel, out_shape=pltpu.HBM(x.shape, x.dtype), cost_estimate=CHEAP, name="copy"
    )(x)


def tick_kernel(x_ref, out):
    out[...] = x_ref[...]


def tick(x):
    return pl.pallas_call(
        tick_kernel, out_shape=jax.ShapeDtypeStruct(x.shape, x.dtype), cost_estimate=cost(200.0), name="tick"
    )(x)


def total_kernel(*refs, counts):
    out = refs[-1]
    start, column = 0, 0
    for count in counts:
        group = refs[start : start + count]
        start += count
        acc = jnp.zeros(group[0].shape[1:], f32)
        for ref in group:
            for i in range(ref.shape[0]):
                acc = acc + ref[i].astype(f32)
        out[:, column : column + acc.shape[1]] = acc.astype(bf16)
        column += acc.shape[1]


def total(groups):
    flat = [x for group in groups for x in group]
    rows = flat[0].shape[1]
    cuts = 2 if rows % 32 == 0 else 1
    width = sum(group[0].shape[2] for group in groups)
    return pl.pallas_call(
        functools.partial(total_kernel, counts=[len(group) for group in groups]),
        out_shape=pltpu.HBM((rows, width), bf16),
        grid=(cuts,),
        in_specs=[
            pl.BlockSpec((x.shape[0], rows // cuts, x.shape[2]), lambda i: (0, i, 0)) for x in flat
        ],
        out_specs=pl.BlockSpec((rows // cuts, width), lambda i: (i, 0)),
        compiler_params=pltpu.CompilerParams(vmem_limit_bytes=40 << 20),
        cost_estimate=cost(0.001),
        name="total",
    )(*flat)


def add_kernel(a_ref, b_ref, out):
    out[...] = (a_ref[...].astype(f32) + b_ref[...].astype(f32)).astype(bf16)


def add(a, b):
    return pl.pallas_call(
        add_kernel, out_shape=pltpu.HBM(a.shape, bf16), cost_estimate=CHEAP, name="add"
    )(a, b)


def pair_kernel(a_ref, b_ref, out):
    out[0] = a_ref[...]
    out[1] = b_ref[...]


def pair_up(a, b, us=0.001):
    return pl.pallas_call(
        pair_kernel, out_shape=pltpu.HBM((2,) + a.shape, bf16), cost_estimate=cost(us), name="pair_up"
    )(a, b)


def by_bits(first, second, put):
    for i in range(2):
        for j in range(2):

            @pl.when((first == i) & (second == j))
            def _(i=i, j=j):
                put(i, j)


def place_kernel(at, own, own_x, mate, mate_x, o0, o1, o2):
    block = pl.program_id(0)
    slot = (block % 2) ^ at[1]
    w = o0.shape[2] // 2

    def put(other_x, core):
        refs = (own_x, mate_x) if other_x else (own, mate)
        for side in range(2):
            part = refs[side ^ core][slot].astype(f32)
            for i, out in enumerate((o0, o1, o2)):
                out[0, :, side * w : (side + 1) * w] = part[:, i * w : (i + 1) * w]

    by_bits((block // 2) ^ at[0], at[2], put)


def place_tail(arrays, at):
    _, h, width = arrays[0].shape
    d = width // 3 * 2
    whole = pl.BlockSpec((2, h, width), lambda i, m: (0, 0, 0), pipeline_mode=pl.Buffered(1))
    outs = pl.pallas_call(
        place_kernel,
        out_shape=[pltpu.HBM((4, h, d), f32)] * 3,
        grid_spec=pltpu.PrefetchScalarGridSpec(
            num_scalar_prefetch=1,
            grid=(4,),
            in_specs=[whole] * 4,
            out_specs=[pl.BlockSpec((1, h, d), lambda i, m: (i, 0, 0))] * 3,
        ),
        compiler_params=pltpu.CompilerParams(vmem_limit_bytes=40 << 20),
        cost_estimate=cost(0.001),
        name="place_tail",
    )(at, *arrays)
    return [out.reshape(4 * h, d) for out in outs]


def cross_kernel(at, x_ref, g_ref, *refs):
    s = refs[-1]
    s[...] = jnp.dot(x_ref[...], g_ref[...], preferred_element_type=f32)
    half = s.shape[0] // 2
    for w in range(2):

        @pl.when(pl.program_id(0) == w)
        def _(w=w):
            for x in range(2):
                rows = pl.ds(pl.multiple_of((at[1] ^ x) * half, 16), half)
                refs[2 * w + x][...] = s[rows, :].astype(bf16)


def cross(x, g, at):
    d, rows = x.shape
    w = d // 2
    cols = g.shape[1]
    step = 512 if cols % 512 == 0 else cols
    n = cols // step
    first = pl.BlockSpec((w // 2, step), lambda i, j, m: (0, jnp.where(i == 0, j, n - 1)))
    second = pl.BlockSpec((w // 2, step), lambda i, j, m: (0, jnp.where(i == 1, j, 0)))
    return pl.pallas_call(
        cross_kernel,
        out_shape=[pltpu.HBM((w // 2, cols), bf16)] * 4,
        grid_spec=pltpu.PrefetchScalarGridSpec(
            num_scalar_prefetch=1,
            grid=(2, n),
            in_specs=[
                pl.BlockSpec((w, rows), lambda i, j, m: (m[0] ^ i, 0)),
                pl.BlockSpec((rows, step), lambda i, j, m: (0, j)),
            ],
            out_specs=[first, first, second, second],
            scratch_shapes=[pltpu.VMEM((w, step), f32)],
        ),
        compiler_params=pltpu.CompilerParams(vmem_limit_bytes=40 << 20),
        cost_estimate=CHEAP,
        name="cross",
    )(at, hbm(x), hbm(g))


def spread_kernel(at, own, mate, *refs, width, other_x):
    out = refs[-1]
    step = out.shape[1]
    rows = pl.ds(pl.multiple_of(pl.program_id(0) * step, step), step)

    def put(core):
        cut = []
        for t in range(3):
            for n in range(2):
                for c in range(2):
                    part = (own, mate)[c ^ core][n ^ at[1], rows, :]
                    cut.append(part[:, t * width : (t + 1) * width])
        out[0] = jnp.concatenate(cut, axis=1).astype(f32)

    for core in range(2):

        @pl.when(at[2] == core)
        def _(core=core):
            put(core)


def spread(own, mate, at, used, other_x, carried=None):
    _, rows, cols = own.shape
    width = 4 * used
    cuts = 2 if rows % 32 == 0 else 1
    whole = pl.BlockSpec((2, rows, cols), lambda j, m: (0, 0, 0), pipeline_mode=pl.Buffered(1))
    more = () if carried is None else (carried,)
    return pl.pallas_call(
        functools.partial(spread_kernel, width=used // 3, other_x=other_x),
        out_shape=pltpu.HBM((2, rows, width), f32),
        grid_spec=pltpu.PrefetchScalarGridSpec(
            num_scalar_prefetch=1,
            grid=(cuts,),
            in_specs=[whole] * 2 + [pl.BlockSpec(memory_space=pl.ANY)] * len(more),
            out_specs=pl.BlockSpec((1, rows // cuts, width), lambda j, m: (m[0] ^ other_x, j, 0)),
        ),
        input_output_aliases={3: 0} if more else {},
        compiler_params=pltpu.CompilerParams(vmem_limit_bytes=40 << 20),
        cost_estimate=CHEAP,
        name="spread",
    )(at, own, mate, *more)


def back_kernel(shards, g_ref, w_ref, *refs):
    acc = jnp.dot(g_ref[...], w_ref[...], preferred_element_type=f32)
    if len(refs) == 2:
        acc = acc + refs[0][0].astype(f32)
    refs[-1][0] = acc.astype(bf16)


def back(grad, w, shards, rows, got=None):
    c, d = w.shape
    n = shards.shape[0]
    step = 640 if d % 640 == 0 else d
    out = pl.BlockSpec((1, rows, step), lambda j, i, f: (i, 0, j))
    in_specs = [
        pl.BlockSpec((rows, c), lambda j, i, f: (f[i], 0)),
        pl.BlockSpec((c, step), lambda j, i, f: (0, j)),
    ]
    args = [hbm(grad), hbm(w)]
    if got is not None:
        in_specs.append(pl.BlockSpec((1, rows, step), lambda j, i, f: (0, 0, j)))
        args.append(got)
    return pl.pallas_call(
        back_kernel,
        out_shape=pltpu.HBM((n, rows, d), bf16),
        grid_spec=pltpu.PrefetchScalarGridSpec(
            num_scalar_prefetch=1, grid=(d // step, n), in_specs=in_specs, out_specs=out
        ),
        compiler_params=pltpu.CompilerParams(vmem_limit_bytes=40 << 20),
        cost_estimate=CHEAP,
        name="back",
    )(shards, *args)


def finish_kernel(shard, g_ref, w_ref, core, near, x_ref, resid, gain, out, gain_out):
    grad = jnp.dot(g_ref[...], w_ref[...], preferred_element_type=f32)
    grad = grad + core[0].astype(f32) + near[0].astype(f32)
    x = x_ref[...].astype(f32)
    inverse = lax.rsqrt(jnp.mean(x * x, axis=-1, keepdims=True) + epsilon)
    part = jnp.sum(grad * x * inverse, axis=0, keepdims=True)

    @pl.when(pl.program_id(0) == 0)
    def _():
        gain_out[...] = jnp.zeros_like(gain_out)

    gain_out[...] += part
    scaled = grad * gain[...]
    out[...] = (
        resid[...]
        + inverse * scaled
        - x * (inverse * inverse * inverse) * jnp.mean(scaled * x, axis=-1, keepdims=True)
    ).astype(bf16)


def finish(grad, w, shard, core, near, x, resid, gain, tile=256):
    rows, d = x.shape
    c = w.shape[0]
    tiles = rows // tile
    row = lambda i, f: (i, 0)
    once = pl.Buffered(1)
    return pl.pallas_call(
        finish_kernel,
        out_shape=[pltpu.HBM((rows, d), bf16), jax.ShapeDtypeStruct((1, d), f32)],
        grid_spec=pltpu.PrefetchScalarGridSpec(
            num_scalar_prefetch=1,
            grid=(tiles,),
            in_specs=[
                pl.BlockSpec((tile, c), lambda i, f: (f[0] * tiles + i, 0)),
                pl.BlockSpec((c, d), lambda i, f: (0, 0), pipeline_mode=once),
                pl.BlockSpec((1, tile, d), lambda i, f: (1, i, 0)),
                pl.BlockSpec((1, tile, d), lambda i, f: (0, i, 0)),
                pl.BlockSpec((tile, d), row),
                pl.BlockSpec((tile, d), row),
                pl.BlockSpec((1, d), lambda i, f: (0, 0)),
            ],
            out_specs=[pl.BlockSpec((tile, d), row), pl.BlockSpec((1, d), lambda i, f: (0, 0))],
        ),
        compiler_params=pltpu.CompilerParams(vmem_limit_bytes=40 << 20),
        cost_estimate=CHEAP,
        name="finish",
    )(shard.reshape(1), hbm(grad), hbm(w), core, near, hbm(x), hbm(resid), gain)


def rms_inverse(values):
    return lax.rsqrt(jnp.mean(values * values, axis=-1, keepdims=True) + epsilon)


def norm_back(values, inverse, grad_scaled):
    return inverse * grad_scaled - values * (inverse * inverse * inverse) * jnp.mean(
        grad_scaled * values, axis=-1, keepdims=True
    )


def dot(left, right):
    return jnp.dot(left, right, preferred_element_type=f32)


def times_trans(left, right):
    return lax.dot_general(left, right, (((1,), (1,)), ((), ())), preferred_element_type=f32)


def trans_times(left, right):
    return lax.dot_general(left, right, (((0,), (0,)), ((), ())), preferred_element_type=f32)


def rows_at(array, start, count):
    return lax.dynamic_slice_in_dim(array, start, count, 0)


def put_rows(array, rows, start):
    return lax.dynamic_update_slice_in_dim(array, rows, start, 0)


def make_local(sizes):
    def pairs(target):
        found = []
        for gx in range(sizes["gx"]):
            for gc in range(sizes["gc"]):
                for z in range(4):
                    for w in range(sizes["wt"]):
                        goal = target(gx, gc, z, w)
                        if goal is not None and goal != (gx, gc, z, w):
                            found.append((place(gx, gc, z, w), place(*goal)))
        return found

    def place(gx, gc, z, w):
        return ((gx * sizes["gc"] + gc) * 4 + z) * sizes["wt"] + w

    def send(value, target):
        return lax.ppermute(value, AXES, pairs(target))

    def core_mate(gx, gc, z, w):
        return (gx, 1 - gc, z, w)

    def x_mate(gx, gc, z, w):
        return (1 - gx, gc, z, w)

    def near_mate(gx, gc, z, w):
        return (gx, gc, z ^ 1, w)

    def far_mate(gx, gc, z, w):
        return (gx, gc, z ^ 2, w)

    def cross_mate(gx, gc, z, w):
        return (gx, 1 - gc, z ^ 1, w)

    def wt_mate(gx, gc, z, w):
        return (gx, gc, z, 1 - w)

    def wt_x_mate(gx, gc, z, w):
        return (1 - gx, gc, z, 1 - w)

    def to_host(gx, gc, z, w):
        return (gx, 1 - (z & 1), 2 * gc + (z >> 1), w)

    def to_home(gx, gc, z, w):
        return (gx, z >> 1, 2 * (z & 1) + 1 - gc, w)

    def hop1(gx, gc, z, w):
        if gc == 0:
            return (gx, 0, z - 1, w) if z > 0 else None
        return (gx, 1, z + 1, w) if z < 3 else None

    def hop2(gx, gc, z, w):
        if gc == 0:
            return (gx, 0, z - 1, w) if z in (1, 2) else None
        return (gx, 1, z + 1, w) if z in (1, 2) else None

    def hop3(gx, gc, z, w):
        if gc == 0:
            return (gx, 0, z ^ 1, w) if z < 2 else None
        return (gx, 1, z ^ 1, w) if z > 1 else None

    def lane_share(gx, gc, z, w):
        return (gx, 1 - gc, z, w) if gc == z >> 1 else None

    def sum_all(value):
        for axis in AXES:
            step = 1
            while step < sizes[axis]:

                def mate(gx, gc, z, w, axis=axis, step=step):
                    at = dict(gx=gx, gc=gc, far=z >> 1, near=z & 1, wt=w)
                    at[axis] ^= step
                    return (at["gx"], at["gc"], 2 * at["far"] + at["near"], at["wt"])

                value = value + send(value, mate)
                step *= 2
        return value

    def local(
        tokens, segments, w_qkv, w_proj, w_in, w_out, gain_attn, gain_mlp, query_scale, cotangent
    ):
        gx, gc, host, near, wt = (lax.axis_index(axis) for axis in AXES)
        z = 2 * host + near
        mine = 2 * near + 1 - gc
        parts = 4
        nh = H // parts
        groups = 1
        rows = tokens.shape[1]
        group_len = segments.shape[1]
        wrows = w_qkv.shape[0]
        lane = gc == host
        pair = sizes["wt"] == 2

        def after(value, *others):
            return lax.optimization_barrier((value,) + others)[0]

        picked = pick(w_qkv, mine, parts, groups, nh)
        own = tokens[0]
        got1 = send(own, hop1)
        own_share = send(own, lane_share)
        seg_mate = send(segments, core_mate)
        got2 = send(got1, hop2)
        got1_share = send(got1, lane_share)
        end = jnp.where(gc == 0, z == 0, z == 3)
        if pair:
            wide_own = stretch(picked, groups, nh, 2)
            got1 = after(got1, wide_own)
            other_w = send(picked, wt_mate)
            wide_w = (wide_own, stretch(other_w, groups, nh, 10))
        else:
            flat_all = lax.all_gather(picked, "wt", axis=0, tiled=True)
            by_head = jnp.transpose(
                flat_all[:, : 3 * nh * HD].reshape(D, groups, 3, nh // groups, HD), (0, 2, 1, 3, 4)
            )
            wide_w = (
                jnp.pad(
                    by_head.reshape(D, 3 * nh, HD), ((0, 0), (0, 0), (0, LN - HD))
                ).reshape(D, -1),
            )
        got3 = send(jnp.where(end, own, got2), hop3)
        got2_share = send(got2, lane_share)
        way = 1 - 2 * host
        last = jnp.where(host == 0, jnp.where(z == 0, 3, 0), jnp.where(z == 3, 0, 3))
        places = (z, z + way, z + 2 * way, last)

        half_rows = wrows // 2
        half_w = jnp.stack([rows_at(w, gc * half_rows, half_rows) for w in (w_proj, w_in, w_out)])
        if pair:
            half_w = send(after(half_w, other_w), wt_mate)
        else:
            half_w = lax.all_gather(half_w, "wt", axis=0, tiled=False)

        dim_scale = scale_base / math.sqrt(HD) * jax.nn.softplus(query_scale)
        lane_scale = jnp.tile(jnp.pad(dim_scale * log2e, (0, LN - HD)), nh)[None]
        ones = jnp.tile(
            ((jnp.arange(LN) >= HD) & (jnp.arange(LN) < HD + 3)).astype(f32), 2 * nh
        )[None]
        seg_row = jnp.where(lane, segments, seg_mate)[0]
        fixed = (lane, mine, wt, gain_attn[None], wide_w, lane_scale, ones, group_len)
        carried = project(((own, own_share), (got1, got1_share)), places[:2], *fixed)
        got3_share = send(after(got3, carried[0]), lane_share)
        all_normed, queries, keyval, inputs = project(
            ((got2, got2_share), (got3, got3_share)), places[2:], *fixed, carried=carried
        )
        grad_mlp = send(after(cotangent[0], got3_share), to_host)

        att, att_float, q_aug = attn_fwd(queries, keyval, seg_row, nh)
        att, half_w, _ = lax.optimization_barrier((att, half_w, grad_mlp))

        trades = (core_mate, near_mate, cross_mate)
        att_pieces = [rows_at(att, (mine ^ j) * rows, rows) for j in range(parts)]
        att_pieces = [att_pieces[0]] + [send(att_pieces[j + 1], trades[j]) for j in range(3)]
        half_mate = send(half_w, core_mate)
        if pair:
            w_trans = order(after(picked, att), other_w, wt)
        else:
            w_trans = flat_all.T
        normed_trans = transpose(after(all_normed, w_trans))
        if pair:
            weights = (w_proj, w_in, w_out, half_w, half_mate)
            starts = (wt * wrows, (1 - wt) * wrows + gc * half_rows, (1 - wt) * wrows + (1 - gc) * half_rows)
        else:
            one = gc == 0
            tail_w = jnp.stack(
                [jnp.where(one, half_w, half_mate), jnp.where(one, half_mate, half_w)], axis=1
            )
            weights = (jnp.transpose(tail_w, (2, 0, 1, 3, 4)).reshape(3, D, D),)
            starts = ()
        (
            layer_out,
            left,
            right,
            grad_resid,
            *pieces,
            grad_gain_mlp,
        ) = tail(
            jnp.stack([mine, *starts]), att_pieces, after(inputs, normed_trans), grad_mlp, weights, gain_mlp[None]
        )
        pieces = [pieces[0]] + [send(pieces[j + 1], trades[j]) for j in range(3)]

        shared = share(after(left, pieces[1]), right, 1 - gc)
        from_core = send(shared, core_mate)
        pieces[2:] = [after(piece, shared) for piece in pieces[2:]]
        home_out = send(after(layer_out, *pieces[1:]), to_home)
        late_gain = tick(after(gain_attn.reshape(-1, LN), *pieces[1:]))
        summed = share(left, right, gc, after(from_core, late_gain))
        kept = lax.all_to_all(summed, ("wt", "gx", "near"), 0, 0, tiled=True)

        scale_row = jnp.tile(dim_scale, nh // groups)[None]

        def backward(group, *others):
            first, *rest = pieces
            return attn_bwd(
                q_aug,
                keyval,
                (after(first, summed, *others), *rest),
                att_float,
                mine,
                seg_row,
                scale_row,
                nh,
                group,
                groups,
            )

        def by_rows(grad):
            if pair:
                own, *rest = cross(normed_trans, grad, jnp.stack([wt, gx]))
                got = [send(part, mate) for part, mate in zip(rest, (x_mate, wt_mate, wt_x_mate))]
                return [part[None] for part in (own, *got)]
            part = dot(normed_trans, grad).astype(bf16)
            sources = sizes["wt"] * 2
            got = lax.all_to_all(part, ("wt", "gx"), 0, 0, tiled=True)
            return [got.reshape(sources, D // sources, -1)]

        grad_project, grad_lanes = backward(0)
        layer_out = after(home_out, grad_project)

        last_step = [layer_out]

        def turn(value):
            return after(value, *last_step)

        def done(value):
            last_step[0] = value
            return value

        sources = sizes["wt"] * 4
        to_core = done(back(turn(grad_project), w_trans, jnp.stack([mine ^ 3, mine ^ 1]), rows))
        from_core = send(to_core, core_mate)
        by_place = by_rows(turn(grad_project))
        done(by_place[0])
        to_near = done(back(grad_project, w_trans, (mine ^ 2).reshape(1), rows, turn(from_core)))
        from_near = send(to_near, near_mate)
        t1 = done(total([[turn(kept).reshape(sources, D // sources, -1)]]))
        t1_far = send(t1, far_mate)
        layer_out = done(copy(turn(layer_out)))
        by_place[0] = turn(by_place[0])
        q1 = done(total([by_place]))
        q1_far = send(q1, far_mate)
        grad_tokens, grad_gain_attn = finish(
            grad_project,
            w_trans,
            mine,
            from_core,
            turn(from_near),
            inputs,
            grad_resid,
            late_gain.reshape(1, -1),
        )
        done(grad_tokens)
        home_grad = send(grad_tokens, to_home)
        t2 = done(add(turn(t1), t1_far))
        t2_near = send(t2, near_mate)
        grad_query_scale = (
            grad_lanes[0, :HD]
            / (dim_scale * log2e)
            * (scale_base / math.sqrt(HD))
            * jax.nn.sigmoid(query_scale)
        )
        small = jnp.concatenate(
            [grad_gain_attn[0], grad_gain_mlp[0], jnp.pad(grad_query_scale, (0, LN - HD))]
        ).reshape(-1, LN)
        q2 = done(add(turn(q1), q1_far))
        q2_near = send(q2, near_mate)
        t4 = done(pair_up(turn(t2), t2_near))
        t4_x = send(t4, x_mate)
        t4_core = send(t4, core_mate)
        grad_tokens = done(copy(turn(home_grad)))
        q4 = done(pair_up(turn(q2), q2_near))
        q4_x = send(q4, x_mate)
        q4_core = send(q4, core_mate)
        t4_x = done(turn(t4_x))
        t4_cross = send(t4_x, core_mate)
        used = 3 * nh * HD
        spread_at = jnp.stack([gx, near, 1 - gc])
        t4_core = done(after(turn(t4_core), t4_cross))
        q4_core = done(turn(q4_core))
        small = done(sum_all(turn(small))).reshape(-1)
        q4_x = done(turn(q4_x))
        q4_cross = send(q4_x, core_mate)
        totals = place_tail((turn(t4), t4_x, t4_core, t4_cross), jnp.stack([gx, near, gc]))
        done(totals[0])
        total_qkv = done(spread(turn(q4), q4_core, spread_at, used, 0))
        total_qkv = spread(turn(q4_x), q4_cross, spread_at, used, 1, total_qkv).reshape(wrows, 3 * D)
        return (
            layer_out[None],
            grad_tokens[None],
            total_qkv,
            *totals,
            small[:D],
            small[D : 2 * D],
            small[2 * D : 2 * D + HD],
        )

    return local


def solution(mesh):
    groups, parts, wt = (mesh.shape[axis] for axis in ("grp", "ctx", "wt"))
    inner = Mesh(mesh.devices.reshape(groups // 2, 2, parts // 2, 2, wt), AXES)
    sizes = dict(inner.shape)
    split = P(("gx", "gc", "wt"), ("far", "near"), None)
    weight = P("wt", None)
    return jax.shard_map(
        make_local(sizes),
        mesh=inner,
        in_specs=(
            split,
            P(("gx", "gc", "wt"), None),
            weight,
            weight,
            weight,
            weight,
            P(),
            P(),
            P(),
            split,
        ),
        out_specs=(split, split, weight, weight, weight, weight, P(), P(), P()),
        check_vma=False,
    )
```

```python
import functools
import math

import jax
import jax.numpy as jnp
from jax import lax
from jax.experimental import pallas as pl
from jax.experimental.pallas import tpu as pltpu
from jax.sharding import Mesh
from jax.sharding import PartitionSpec as P

D = 1280
H = 16
HD = 80
LN = 128
epsilon = 1e-06
scale_base = 1.442695041
log2e = 1.4426950408889634
NEG = -1e30
def cost(us):
    return pl.CostEstimate(flops=int(us * 1_000_000_000), transcendentals=0, bytes_accessed=1000)


CHEAP = cost(0.001)
f32 = jnp.float32
bf16 = jnp.bfloat16
AXES = ("gx", "gc", "far", "near", "wt")


def hbm(x):
    return pltpu.with_memory_space_constraint(x, pltpu.HBM)


def block_flags(seg_row, bq, bk):
    n = seg_row.shape[0]
    q = seg_row.reshape(n // bq, bq)
    k = seg_row.reshape(n // bk, bk)
    qf, ql = q[:, 0][:, None], q[:, -1][:, None]
    kf, kl = k[:, 0][None], k[:, -1][None]
    qs = jnp.arange(n // bq, dtype=jnp.int32)[:, None] * bq
    ks = jnp.arange(n // bk, dtype=jnp.int32)[None] * bk
    below = ks + bk - 1 <= qs
    skip = (ks > qs + bq - 1) | ((kf > 0) & (kl < qf))
    same = (qf == ql) & (kl == ql) & ((kf == kl) | ((kf == 0) & (kl == 1)))
    full = below & ((kl == 0) | same)
    flags = jnp.where(skip, 0, jnp.where(full, 1, 2))
    if bq == bk:
        flags = jnp.where(qs == ks, 3, flags)
    return flags.astype(jnp.int32).reshape(-1)


def put_split(base, col, lanes):
    hi = col.astype(bf16).astype(f32)
    rest = col - hi
    mid = rest.astype(bf16).astype(f32)
    out = jnp.where(lanes == HD, hi, base)
    out = jnp.where(lanes == HD + 1, mid, out)
    return jnp.where(lanes == HD + 2, rest - mid, out).astype(bf16)


def fwd_kernel(flags, q_ref, kv, segc, segr, att, of, qaug, m_s, acc_s, *, nh, bq, bk, nk):
    qi = pl.program_id(0)
    count = (qi * bq + bq + bk - 1) // bk
    nt = (((1,), (1,)), ((), ()))
    acc_s[...] = jnp.zeros_like(acc_s)
    m_s[...] = jnp.zeros_like(m_s)

    def mask(ko, q0=0, qn=bq, kn=bk):
        qpos = qi * bq + q0 + lax.broadcasted_iota(jnp.int32, (qn, kn), 0)
        kpos = ko + lax.broadcasted_iota(jnp.int32, (qn, kn), 1)
        ks = segr[:, pl.ds(ko, kn)]
        return (kpos <= qpos) & ((ks == 0) | (ks == segc[q0 : q0 + qn, :]))

    def step(kb, masked, q0=0, qn=bq, kn=bk):
        ko = pl.multiple_of(kb * bk, bk)
        if masked:
            allowed = mask(ko, q0, qn, kn)
        rows = slice(q0, q0 + qn)
        for h in range(nh):
            k = kv[pl.ds(ko, kn), h * LN : (h + 1) * LN]
            v = kv[pl.ds(ko, kn), (nh + h) * LN : (nh + h + 1) * LN]
            q = q_ref[rows, h * LN : (h + 1) * LN]
            p = jnp.exp2(lax.dot_general(q, k, nt, preferred_element_type=f32))
            if masked:
                p = jnp.where(allowed, p, 0.0)
            acc_s[h, rows, :] += jnp.dot(p.astype(bf16), v, preferred_element_type=f32)

    def body(kb, carry):
        flag = flags[qi * nk + kb]

        @pl.when(flag == 1)
        def _():
            step(kb, False)

        @pl.when(flag >= 2)
        def _():
            step(kb, True)

        return carry

    lax.fori_loop(0, count, body, 0)
    bad = jnp.zeros((bq, 1), f32)
    for h in range(nh):
        total = acc_s[h][:, HD : HD + 1]
        bad = jnp.maximum(bad, jnp.where((total > 2.0**-60) & (total < 2.0**60), 0.0, 1.0))

    @pl.when(jnp.max(bad) > 0.0)
    def _():
        def head(h, carry):
            kc = pl.ds(pl.multiple_of(h * LN, LN), LN)
            vc = pl.ds(pl.multiple_of((nh + h) * LN, LN), LN)
            m_s[h] = jnp.full((bq, LN), NEG, f32)
            acc_s[h] = jnp.zeros((bq, LN), f32)

            def inner(kb, carry):
                @pl.when(flags[qi * nk + kb] > 0)
                def _():
                    ko = pl.multiple_of(kb * bk, bk)
                    s = lax.dot_general(
                        q_ref[:, kc], kv[pl.ds(ko, bk), kc], nt, preferred_element_type=f32
                    )
                    s = jnp.where(mask(ko), s, NEG)
                    old = m_s[h]
                    new = jnp.maximum(old, jnp.max(s, axis=1, keepdims=True))
                    p = jnp.exp2(s - new[:, :1]).astype(bf16)
                    m_s[h] = new
                    acc_s[h] = acc_s[h] * jnp.exp2(old - new) + jnp.dot(
                        p, kv[pl.ds(ko, bk), vc], preferred_element_type=f32
                    )

                return carry

            lax.fori_loop(0, count, inner, 0)
            return carry

        lax.fori_loop(0, nh, head, 0)

    lanes = lax.broadcasted_iota(jnp.int32, (bq, LN), 1)
    outs = []
    for h in range(nh):
        acc = acc_s[h]
        total = acc[:, HD : HD + 1]
        out = acc * (1.0 / total)
        of[:, h * LN : (h + 1) * LN] = jnp.where(lanes < HD, out, 0.0).astype(bf16)
        outs.append(out[:, :HD])
        lse = m_s[h][:, :1] + jnp.log2(total)
        qaug[:, h * LN : (h + 1) * LN] = put_split(
            q_ref[:, h * LN : (h + 1) * LN].astype(f32), -lse, lanes
        )
    att[...] = jnp.concatenate(outs, axis=1).astype(bf16)


def attn_fwd(q, kv, seg_row, nh, bq=512, bk=512):
    n = q.shape[0]
    w = nh * LN
    spec = pltpu.PrefetchScalarGridSpec(
        num_scalar_prefetch=1,
        grid=(n // bq,),
        in_specs=[
            pl.BlockSpec((bq, w), lambda i, f: (i, 0)),
            pl.BlockSpec((n, 2 * w), lambda i, f: (0, 0)),
            pl.BlockSpec((bq, 1), lambda i, f: (i, 0)),
            pl.BlockSpec((1, n), lambda i, f: (0, 0)),
        ],
        out_specs=[
            pl.BlockSpec((bq, nh * HD), lambda i, f: (i, 0)),
            pl.BlockSpec((bq, w), lambda i, f: (i, 0)),
            pl.BlockSpec((bq, w), lambda i, f: (i, 0)),
        ],
        scratch_shapes=[pltpu.VMEM((nh, bq, LN), f32), pltpu.VMEM((nh, bq, LN), f32)],
    )
    return pl.pallas_call(
        functools.partial(fwd_kernel, nh=nh, bq=bq, bk=bk, nk=n // bk),
        out_shape=[
            pltpu.HBM((n, nh * HD), bf16),
            pltpu.HBM((n, w), bf16),
            pltpu.HBM((n, w), bf16),
        ],
        grid_spec=spec,
        compiler_params=pltpu.CompilerParams(vmem_limit_bytes=40 << 20),
        cost_estimate=cost(0.01),
        name="attn_fwd",
    )(block_flags(seg_row, bq, bk), hbm(q), hbm(kv), seg_row[:, None], seg_row[None])


def bwd_kernel(
    flags, mine, qa, kk, vv, do0, do1, do2, do3, of, segc, segr, scale, dqkv, gscale, doa_s, dq_s, dk_s, dv_s, *, first, nh, bq, bk, n
):
    nk = n // bk
    nq = n // bq
    kb = pl.program_id(0)
    part = n // 4
    step_rows = 256 if part % 256 == 0 else part
    lanes = lax.broadcasted_iota(jnp.int32, (step_rows, LN), 1)

    @pl.when(kb == 0)
    def _():
        dq_s[...] = jnp.zeros_like(dq_s)
        for j, piece in enumerate((do0, do1, do2, do3)):
            start = (mine[0] ^ j) * part
            for i in range(part // step_rows):
                d = piece[i * step_rows : (i + 1) * step_rows, :].astype(f32)
                r = pl.ds(pl.multiple_of(start + i * step_rows, step_rows), step_rows)
                for h in range(nh):
                    at = (first + h) * HD
                    dh = jnp.concatenate(
                        [d[:, at : at + HD], jnp.zeros((step_rows, LN - HD), f32)], axis=1
                    )
                    c = slice(h * LN, (h + 1) * LN)
                    delta = jnp.sum(dh * of[r, c].astype(f32), axis=1, keepdims=True)
                    doa_s[r, c] = put_split(dh, -delta, lanes)

    dk_s[...] = jnp.zeros_like(dk_s)
    dv_s[...] = jnp.zeros_like(dv_s)
    ko = kb * bk
    nt = (((1,), (1,)), ((), ()))
    tn = (((0,), (0,)), ((), ()))

    def step(qi, masked, q0=0, qn=bq, kn=bk):
        qo = pl.multiple_of(qi * bq + q0, qn)
        rows = slice(0, kn)
        if masked:
            kpos = ko + lax.broadcasted_iota(jnp.int32, (kn, qn), 0)
            qpos = qo + lax.broadcasted_iota(jnp.int32, (kn, qn), 1)
            ks = segc[rows, :]
            allowed = (kpos <= qpos) & ((ks == 0) | (ks == segr[:, pl.ds(qo, qn)]))
        for h in range(nh):
            c = slice(h * LN, (h + 1) * LN)
            q = qa[pl.ds(qo, qn), c]
            k = kk[rows, c]
            d = doa_s[pl.ds(qo, qn), c]
            p = jnp.exp2(lax.dot_general(k, q, nt, preferred_element_type=f32))
            if masked:
                p = jnp.where(allowed, p, 0.0)
            ds = (p * lax.dot_general(vv[rows, c], d, nt, preferred_element_type=f32)).astype(bf16)
            dv_s[h, rows, :] += jnp.dot(p.astype(bf16), d, preferred_element_type=f32)
            dk_s[h, rows, :] += jnp.dot(ds, q, preferred_element_type=f32)
            dq_s[h, pl.ds(qo, qn), :] += lax.dot_general(ds, k, tn, preferred_element_type=f32)

    def body(qi, carry):
        flag = flags[qi * nk + kb]

        @pl.when(flag == 1)
        def _():
            step(qi, False)

        @pl.when(flag == 2)
        def _():
            step(qi, True)

        if bq == bk:

            @pl.when(flag == 3)
            def _():
                step(qi, True, 0, bq // 2, bk // 2)
                step(qi, True, bq // 2, bq // 2, bk)

        return carry

    lax.fori_loop(ko // bq, nq, body, 0)
    r = pl.multiple_of(ko, bk)
    ln2 = math.log(2.0)
    gap = dqkv.shape[1] - 3 * nh * HD
    dqkv[pl.ds(r, bk), nh * HD :] = jnp.concatenate(
        [dk_s[h][:, :HD] * ln2 for h in range(nh)]
        + [dv_s[h][:, :HD] for h in range(nh)]
        + [jnp.zeros((bk, gap), f32)],
        axis=1,
    ).astype(bf16)

    @pl.when(kb == nk - 1)
    def _():
        total = jnp.zeros((1, LN), f32)
        for i in range(nq):
            rows = slice(i * bq, (i + 1) * bq)
            for h in range(nh):
                total = total + jnp.sum(
                    dq_s[h, rows, :] * qa[rows, h * LN : (h + 1) * LN].astype(f32), axis=0, keepdims=True
                )
            grads = jnp.concatenate([dq_s[h, rows, :][:, :HD] for h in range(nh)], axis=1)
            dqkv[rows, 0 : nh * HD] = (grads * scale[...]).astype(bf16)
        gscale[...] = jnp.broadcast_to(total, gscale.shape)


def attn_bwd(qa, kv, pieces, of, mine, seg_row, scale, heads, group, groups, bq=512, bk=512):
    n = qa.shape[0]
    nh = heads // groups
    w = nh * LN
    once = pl.Buffered(1)
    spec = pltpu.PrefetchScalarGridSpec(
        num_scalar_prefetch=2,
        grid=(n // bk,),
        in_specs=[
            pl.BlockSpec((n, w), lambda i, f, m: (0, group), pipeline_mode=once),
            pl.BlockSpec((bk, w), lambda i, f, m: (i, group)),
            pl.BlockSpec((bk, w), lambda i, f, m: (i, groups + group)),
            *[pl.BlockSpec((n // 4, heads * HD), lambda i, f, m: (0, 0), pipeline_mode=once)] * 4,
            pl.BlockSpec((n, w), lambda i, f, m: (0, group), pipeline_mode=once),
            pl.BlockSpec((bk, 1), lambda i, f, m: (i, 0)),
            pl.BlockSpec((1, n), lambda i, f, m: (0, 0)),
            pl.BlockSpec((1, nh * HD), lambda i, f, m: (0, 0)),
        ],
        out_specs=[
            pl.BlockSpec((n, lanes_up(3 * nh * HD)), lambda i, f, m: (0, 0)),
            pl.BlockSpec((8, LN), lambda i, f, m: (0, 0)),
        ],
        scratch_shapes=[
            pltpu.VMEM((n, w), bf16),
            pltpu.VMEM((nh, n, LN), f32),
            pltpu.VMEM((nh, bk, LN), f32),
            pltpu.VMEM((nh, bk, LN), f32),
        ],
    )
    return pl.pallas_call(
        functools.partial(bwd_kernel, first=group * nh, nh=nh, bq=bq, bk=bk, n=n),
        out_shape=[
            pltpu.HBM((n, lanes_up(3 * nh * HD)), bf16),
            pltpu.HBM((8, LN), f32),
        ],
        grid_spec=spec,
        compiler_params=pltpu.CompilerParams(vmem_limit_bytes=48 << 20),
        cost_estimate=cost(300 if group == 0 else 0.001),
        name="attn_bwd",
    )(block_flags(seg_row, bq, bk), mine.reshape(1), hbm(qa), hbm(kv), hbm(kv), *pieces, hbm(of), seg_row[:, None], seg_row[None], scale)


def quarter_columns(place, parts, groups, nh):
    width = nh // groups * HD
    return [
        (t * D + place * nh * HD + g * width, width) for g in range(groups) for t in range(3)
    ]


def pick_kernel(mine, w_ref, out, *, parts, groups, nh):
    for i in range(parts):

        @pl.when(mine[0] == i)
        def _(i=i):
            cut = [w_ref[:, a : a + width] for a, width in quarter_columns(i, parts, groups, nh)]
            used = sum(x.shape[1] for x in cut)
            pad = jnp.zeros((cut[0].shape[0], out.shape[1] - used), out.dtype)
            out[...] = jnp.concatenate(cut + [pad], axis=1)


def lanes_up(n):
    return -(-n // LN) * LN


def pick(w, mine, parts, groups, nh):
    rows = w.shape[0]
    step = 160 if rows % 160 == 0 else rows
    return pl.pallas_call(
        functools.partial(pick_kernel, parts=parts, groups=groups, nh=nh),
        out_shape=pltpu.HBM((rows, lanes_up(3 * nh * HD)), w.dtype),
        grid_spec=pltpu.PrefetchScalarGridSpec(
            num_scalar_prefetch=1,
            grid=(rows // step,),
            in_specs=[pl.BlockSpec((step, 3 * D), lambda i, m: (i, 0))],
            out_specs=pl.BlockSpec((step, lanes_up(3 * nh * HD)), lambda i, m: (i, 0)),
        ),
        cost_estimate=cost(5),
        name="pick",
    )(mine.reshape(1), hbm(w))


def stretch_kernel(x_ref, out, *, groups, nh):
    value = x_ref[...]
    each = 3 * nh * HD // groups
    zero = jnp.zeros((value.shape[0], LN - HD), value.dtype)
    per = nh // groups
    wide = []
    for t in range(3):
        for h in range(nh):
            at = (h // per) * each + t * per * HD + (h % per) * HD
            wide += [value[:, at : at + HD], zero]
    out[...] = jnp.concatenate(wide, axis=1)


def stretch(x, groups, nh, us):
    rows, width = x.shape
    step = 160
    return pl.pallas_call(
        functools.partial(stretch_kernel, groups=groups, nh=nh),
        out_shape=pltpu.HBM((rows, 3 * nh * LN), x.dtype),
        grid=(rows // step,),
        in_specs=[pl.BlockSpec((step, width), lambda i: (i, 0))],
        out_specs=pl.BlockSpec((step, 3 * nh * LN), lambda i: (i, 0)),
        cost_estimate=cost(us),
        name="stretch",
    )(hbm(x))


def order_kernel(own_first, a_ref, b_ref, out):
    half = pl.program_id(0)

    @pl.when(half == 0)
    def _():
        out[...] = a_ref[...].T

    @pl.when(half == 1)
    def _():
        out[...] = b_ref[...].T


def order(own, other, own_at):
    rows, width = own.shape
    step = 256
    return pl.pallas_call(
        order_kernel,
        out_shape=pltpu.HBM((width, 2 * rows), own.dtype),
        grid_spec=pltpu.PrefetchScalarGridSpec(
            num_scalar_prefetch=1,
            grid=(2, width // step),
            in_specs=[
                pl.BlockSpec((rows, step), lambda i, j, m: (0, j * (1 - i))),
                pl.BlockSpec((rows, step), lambda i, j, m: (0, j * i)),
            ],
            out_specs=pl.BlockSpec((step, rows), lambda i, j, m: (j, i ^ m[0])),
        ),
        cost_estimate=cost(200.0),
        name="order",
    )(own_at.reshape(1), hbm(own), hbm(other))


def transpose_kernel(x_ref, out):
    out[...] = x_ref[...].T


def transpose(x):
    rows, cols = x.shape
    step = 256
    return pl.pallas_call(
        transpose_kernel,
        out_shape=pltpu.HBM((cols, rows), x.dtype),
        grid=(rows // step,),
        in_specs=[pl.BlockSpec((step, cols), lambda i: (i, 0))],
        out_specs=pl.BlockSpec((cols, step), lambda i: (0, i)),
        cost_estimate=CHEAP,
        name="transpose",
    )(hbm(x))


def project_kernel(info, *refs, count, halves, width, fresh):
    pairs = refs[: 2 * count]
    gain = refs[2 * count]
    weights = refs[2 * count + 1 : 2 * count + 1 + halves]
    scale, ones = refs[2 * count + 1 + halves : 2 * count + 3 + halves]
    normed_ref, q_ref, kv_ref, mine_ref, w = refs[-5:]
    j, tile = pl.program_id(0), pl.program_id(1)
    step = normed_ref.shape[0]

    @pl.when((j == 0) & (tile == 0))
    def _():
        for i, ref in enumerate(weights):
            h = ref.shape[0]
            start = (info[count + 2] ^ i) * h if halves == 2 else 0
            w[pl.ds(pl.multiple_of(start, 16), h), :] = ref[...]
        if not fresh:
            mine_ref[...] = refs[2 * count + 3 + halves][...]

    def work(x_ref):
        value = x_ref[...]
        x = value.astype(f32)
        inverse = lax.rsqrt(jnp.mean(x * x, axis=-1, keepdims=True) + epsilon)
        normed = (x * inverse * gain[...]).astype(bf16)
        normed_ref[...] = normed
        q_ref[...] = (
            jnp.dot(normed, w[:, :width], preferred_element_type=f32) * scale[...]
        ).astype(bf16)
        kv_ref[...] = (
            jnp.dot(normed, w[:, width:], preferred_element_type=f32) + ones[...]
        ).astype(bf16)

        @pl.when(info[count + 1] == info[j])
        def _():
            mine_ref[pl.ds(pl.multiple_of(tile * step, step), step), :] = value

    for i in range(count):
        for lane in range(2):

            @pl.when((j == i) & (info[count] == lane))
            def _(i=i, lane=lane):
                work(pairs[2 * i + 1 - lane])


def project(pairs, places, lane, mine, wt, gain, weights, scale, ones, group_len, carried=None):
    count = len(pairs)
    rows, d = pairs[0][0].shape
    width = scale.shape[1]
    step = 256
    tiles = rows // step
    full = lambda j, t, f: (0, 0)
    at = lambda j, t, f: (f[j] * tiles + t, 0)
    once = pl.Buffered(1)
    info = jnp.stack(list(places) + [lane.astype(jnp.int32), mine, wt])
    args = [x for pair in pairs for x in pair] + [gain, *map(hbm, weights), scale, ones]
    in_specs = [
        pl.BlockSpec(
            (step, d),
            lambda j, t, f, i=i: (jnp.where(j == i, t, jnp.where(j > i, tiles - 1, 0)), 0),
        )
        for i in range(count)
        for _ in range(2)
    ]
    in_specs += [pl.BlockSpec((1, d), full, pipeline_mode=once)]
    in_specs += [pl.BlockSpec(w.shape, full, pipeline_mode=once) for w in weights]
    in_specs += [
        pl.BlockSpec((1, width), full, pipeline_mode=once),
        pl.BlockSpec((1, 2 * width), full, pipeline_mode=once),
    ]
    aliases = {}
    if carried is not None:
        base = len(args) + 2
        args += [hbm(x) for x in (carried[3], *carried[:3])]
        in_specs += [pl.BlockSpec((rows, d), full, pipeline_mode=once)]
        in_specs += [pl.BlockSpec(memory_space=pl.ANY)] * 3
        aliases = {base: 0, base + 1: 1, base + 2: 2}
    return pl.pallas_call(
        functools.partial(
            project_kernel, count=count, halves=len(weights), width=width, fresh=carried is None
        ),
        out_shape=[
            pltpu.HBM((group_len, d), bf16),
            pltpu.HBM((group_len, width), bf16),
            pltpu.HBM((group_len, 2 * width), bf16),
            pltpu.HBM((rows, d), bf16),
        ],
        grid_spec=pltpu.PrefetchScalarGridSpec(
            num_scalar_prefetch=1,
            grid=(count, tiles),
            in_specs=in_specs,
            out_specs=[
                pl.BlockSpec((step, d), at),
                pl.BlockSpec((step, width), at),
                pl.BlockSpec((step, 2 * width), at),
                pl.BlockSpec((rows, d), full),
            ],
            scratch_shapes=[pltpu.VMEM((d, 3 * width), bf16)],
        ),
        input_output_aliases=aliases,
        compiler_params=pltpu.CompilerParams(vmem_limit_bytes=48 << 20),
        cost_estimate=cost(15),
        name="project",
    )(info, *args)


def tail_body(at, p0, p1, p2, p3, x_ref, g_ref, w_s, gain, outs, need):
    lo_ref, left_ref, right_ref, gr_ref, c0, c1, c2, c3, gg_ref = outs
    att_ref, nm_ref, act_ref = (left_ref.at[i] for i in range(3))
    gp_ref, gh_ref = (right_ref.at[i] for i in range(2))
    right_ref[2] = g_ref[...]
    mine = at[0]
    pieces = (p0, p1, p2, p3)
    cols = p0.shape[1]
    nt = (((1,), (1,)), ((), ()))
    for i in range(4):

        @pl.when(mine == i)
        def _(i=i):
            att_ref[...] = jnp.concatenate([pieces[i ^ k][...] for k in range(4)], axis=1)

    need(0)
    resid = x_ref[...].astype(f32) + jnp.dot(att_ref[...], w_s[0], preferred_element_type=f32)
    inverse = lax.rsqrt(jnp.mean(resid * resid, axis=-1, keepdims=True) + epsilon)
    normed = (resid * inverse * gain[...]).astype(bf16)
    nm_ref[...] = normed
    need(1)
    hidden = jnp.dot(normed, w_s[1], preferred_element_type=f32)
    sig = 1.0 / (1.0 + jnp.exp(-hidden))
    active = (hidden * sig).astype(bf16)
    act_ref[...] = active
    need(2)
    lo_ref[...] = (resid + jnp.dot(active, w_s[2], preferred_element_type=f32)).astype(bf16)
    grad_active = lax.dot_general(g_ref[...], w_s[2], nt, preferred_element_type=f32)
    grad_hidden = (grad_active * sig * (1.0 + hidden * (1.0 - sig))).astype(bf16)
    gh_ref[...] = grad_hidden
    grad_normed = lax.dot_general(grad_hidden, w_s[1], nt, preferred_element_type=f32)
    gg_ref[...] += jnp.sum(grad_normed * resid * inverse, axis=0, keepdims=True)
    scaled = grad_normed * gain[...]
    grad_resid = (
        g_ref[...].astype(f32)
        + inverse * scaled
        - resid * (inverse * inverse * inverse) * jnp.mean(scaled * resid, axis=-1, keepdims=True)
    )
    gr_ref[...] = grad_resid
    grad_proj = grad_resid.astype(bf16)
    gp_ref[...] = grad_proj
    grad_att = lax.dot_general(grad_proj, w_s[0], nt, preferred_element_type=f32).astype(bf16)
    for i in range(4):

        @pl.when(mine == i)
        def _(i=i):
            for j, out in enumerate((c0, c1, c2, c3)):
                out[...] = grad_att[:, (i ^ j) * cols : ((i ^ j) + 1) * cols]


def tail_kernel(at, p0, p1, p2, p3, x_ref, g_ref, own0, own1, own2, half, other, gain, *refs, rows, hrows):
    w_s, sems = refs[-2:]
    outs = refs[:-2]

    def copies(i):
        parts = (((own0, own1, own2)[i], at[1], rows), (half.at[i], at[2], hrows), (other.at[i], at[3], hrows))
        return [
            pltpu.make_async_copy(
                part, w_s.at[i, pl.ds(pl.multiple_of(start, 16), n), :], sems.at[3 * i + k]
            )
            for k, (part, start, n) in enumerate(parts)
        ]

    @pl.when(pl.program_id(0) == 0)
    def _():
        outs[-1][...] = jnp.zeros_like(outs[-1])
        for i in range(3):
            for c in copies(i):
                c.start()

    def need(i):
        @pl.when(pl.program_id(0) == 0)
        def _():
            for c in copies(i):
                c.wait()

    tail_body(at, p0, p1, p2, p3, x_ref, g_ref, w_s, gain, outs, need)


def whole_tail_kernel(at, p0, p1, p2, p3, x_ref, g_ref, w, gain, *outs):
    @pl.when(pl.program_id(0) == 0)
    def _():
        outs[-1][...] = jnp.zeros_like(outs[-1])

    tail_body(at, p0, p1, p2, p3, x_ref, g_ref, w, gain, outs, lambda i: None)


def tail(at, pieces, x, g, weights, gain, tile=256):
    rows, d = x.shape
    cols = pieces[0].shape[1]
    row = lambda i, m: (i, 0)
    once = pl.Buffered(1)
    whole = lambda *shape: pl.BlockSpec(shape, lambda i, m: (0,) * len(shape), pipeline_mode=once)
    wide = pl.BlockSpec((tile, d), row)
    slim = pl.BlockSpec((tile, cols), row)
    if len(weights) == 5:
        body = functools.partial(tail_kernel, rows=weights[0].shape[0], hrows=weights[3].shape[1])
        scratch = [pltpu.VMEM((3, d, d), bf16), pltpu.SemaphoreType.DMA((9,))]
        weight_specs = [pl.BlockSpec(memory_space=pl.ANY)] * 5
    else:
        body = whole_tail_kernel
        scratch = []
        weight_specs = [whole(*w.shape) for w in weights]
    return pl.pallas_call(
        body,
        out_shape=[pltpu.HBM((rows, d), bf16)]
        + [pltpu.HBM((3, rows, d), bf16)] * 2
        + [pltpu.HBM((rows, d), f32)]
        + [pltpu.HBM((rows, cols), bf16)] * 4
        + [pltpu.HBM((1, d), f32)],
        grid_spec=pltpu.PrefetchScalarGridSpec(
            num_scalar_prefetch=1,
            grid=(rows // tile,),
            in_specs=[slim] * 4 + [wide] * 2 + weight_specs + [whole(1, d)],
            out_specs=[wide]
            + [pl.BlockSpec((3, tile, d), lambda i, m: (0, i, 0))] * 2
            + [wide]
            + [slim] * 4
            + [pl.BlockSpec((1, d), lambda i, m: (0, 0))],
            scratch_shapes=scratch,
        ),
        compiler_params=pltpu.CompilerParams(vmem_limit_bytes=52 << 20),
        cost_estimate=cost(0.01),
        name="tail",
    )(at, *pieces, hbm(x), g, *map(hbm, weights), gain)


tn_dims = (((0,), (0,)), ((), ()))


def share_kernel(col, left, right, *refs):
    value = lax.dot_general(left[0], right[0], tn_dims, preferred_element_type=f32)
    if len(refs) == 2:
        value = value + refs[0][...].astype(f32)
    refs[-1][...] = value.astype(bf16)


def share(left, right, col, got=None):
    n, rows, d = left.shape
    w = d // 2
    block = pl.BlockSpec((d, w), lambda i, c: (0, i))
    return pl.pallas_call(
        share_kernel,
        out_shape=pltpu.HBM((d, n * w), bf16),
        grid_spec=pltpu.PrefetchScalarGridSpec(
            num_scalar_prefetch=1,
            grid=(n,),
            in_specs=[
                pl.BlockSpec((1, rows, d), lambda i, c: (i, 0, 0)),
                pl.BlockSpec((1, rows, w), lambda i, c: (i, 0, c[0])),
            ]
            + [block] * (got is not None),
            out_specs=block,
        ),
        compiler_params=pltpu.CompilerParams(vmem_limit_bytes=40 << 20),
        cost_estimate=CHEAP,
        name="share",
    )(col.reshape(1), hbm(left), hbm(right), *(() if got is None else (hbm(got),)))


def copy(x):
    return pl.pallas_call(
        tick_kernel, out_shape=pltpu.HBM(x.shape, x.dtype), cost_estimate=CHEAP, name="copy"
    )(x)


def tick_kernel(x_ref, out):
    out[...] = x_ref[...]


def tick(x):
    return pl.pallas_call(
        tick_kernel, out_shape=jax.ShapeDtypeStruct(x.shape, x.dtype), cost_estimate=cost(200.0), name="tick"
    )(x)


def total_kernel(*refs, counts):
    out = refs[-1]
    start, column = 0, 0
    for count in counts:
        group = refs[start : start + count]
        start += count
        acc = jnp.zeros(group[0].shape[1:], f32)
        for ref in group:
            for i in range(ref.shape[0]):
                acc = acc + ref[i].astype(f32)
        out[:, column : column + acc.shape[1]] = acc.astype(bf16)
        column += acc.shape[1]


def total(groups):
    flat = [x for group in groups for x in group]
    rows = flat[0].shape[1]
    cuts = 2 if rows % 32 == 0 else 1
    width = sum(group[0].shape[2] for group in groups)
    return pl.pallas_call(
        functools.partial(total_kernel, counts=[len(group) for group in groups]),
        out_shape=pltpu.HBM((rows, width), bf16),
        grid=(cuts,),
        in_specs=[
            pl.BlockSpec((x.shape[0], rows // cuts, x.shape[2]), lambda i: (0, i, 0)) for x in flat
        ],
        out_specs=pl.BlockSpec((rows // cuts, width), lambda i: (i, 0)),
        compiler_params=pltpu.CompilerParams(vmem_limit_bytes=40 << 20),
        cost_estimate=cost(0.001),
        name="total",
    )(*flat)


def add_kernel(a_ref, b_ref, out):
    out[...] = (a_ref[...].astype(f32) + b_ref[...].astype(f32)).astype(bf16)


def add(a, b):
    return pl.pallas_call(
        add_kernel, out_shape=pltpu.HBM(a.shape, bf16), cost_estimate=CHEAP, name="add"
    )(a, b)


def pair_kernel(a_ref, b_ref, out):
    out[0] = a_ref[...]
    out[1] = b_ref[...]


def pair_up(a, b, us=0.001):
    return pl.pallas_call(
        pair_kernel, out_shape=pltpu.HBM((2,) + a.shape, bf16), cost_estimate=cost(us), name="pair_up"
    )(a, b)


def by_bits(first, second, put):
    for i in range(2):
        for j in range(2):

            @pl.when((first == i) & (second == j))
            def _(i=i, j=j):
                put(i, j)


def place_kernel(at, own, own_x, mate, mate_x, o0, o1, o2):
    block = pl.program_id(0)
    slot = (block % 2) ^ at[1]
    w = o0.shape[2] // 2

    def put(other_x, core):
        refs = (own_x, mate_x) if other_x else (own, mate)
        for side in range(2):
            part = refs[side ^ core][slot].astype(f32)
            for i, out in enumerate((o0, o1, o2)):
                out[0, :, side * w : (side + 1) * w] = part[:, i * w : (i + 1) * w]

    by_bits((block // 2) ^ at[0], at[2], put)


def place_tail(arrays, at):
    _, h, width = arrays[0].shape
    d = width // 3 * 2
    whole = pl.BlockSpec((2, h, width), lambda i, m: (0, 0, 0), pipeline_mode=pl.Buffered(1))
    outs = pl.pallas_call(
        place_kernel,
        out_shape=[pltpu.HBM((4, h, d), f32)] * 3,
        grid_spec=pltpu.PrefetchScalarGridSpec(
            num_scalar_prefetch=1,
            grid=(4,),
            in_specs=[whole] * 4,
            out_specs=[pl.BlockSpec((1, h, d), lambda i, m: (i, 0, 0))] * 3,
        ),
        compiler_params=pltpu.CompilerParams(vmem_limit_bytes=40 << 20),
        cost_estimate=cost(0.001),
        name="place_tail",
    )(at, *arrays)
    return [out.reshape(4 * h, d) for out in outs]


def cross_kernel(at, x_ref, g_ref, *refs):
    s = refs[-1]
    s[...] = jnp.dot(x_ref[...], g_ref[...], preferred_element_type=f32)
    half = s.shape[0] // 2
    for w in range(2):

        @pl.when(pl.program_id(0) == w)
        def _(w=w):
            for x in range(2):
                rows = pl.ds(pl.multiple_of((at[1] ^ x) * half, 16), half)
                refs[2 * w + x][...] = s[rows, :].astype(bf16)


def cross(x, g, at):
    d, rows = x.shape
    w = d // 2
    cols = g.shape[1]
    step = 512 if cols % 512 == 0 else cols
    n = cols // step
    first = pl.BlockSpec((w // 2, step), lambda i, j, m: (0, jnp.where(i == 0, j, n - 1)))
    second = pl.BlockSpec((w // 2, step), lambda i, j, m: (0, jnp.where(i == 1, j, 0)))
    return pl.pallas_call(
        cross_kernel,
        out_shape=[pltpu.HBM((w // 2, cols), bf16)] * 4,
        grid_spec=pltpu.PrefetchScalarGridSpec(
            num_scalar_prefetch=1,
            grid=(2, n),
            in_specs=[
                pl.BlockSpec((w, rows), lambda i, j, m: (m[0] ^ i, 0)),
                pl.BlockSpec((rows, step), lambda i, j, m: (0, j)),
            ],
            out_specs=[first, first, second, second],
            scratch_shapes=[pltpu.VMEM((w, step), f32)],
        ),
        compiler_params=pltpu.CompilerParams(vmem_limit_bytes=40 << 20),
        cost_estimate=CHEAP,
        name="cross",
    )(at, hbm(x), hbm(g))


def spread_kernel(at, own, mate, *refs, width, other_x):
    out = refs[-1]
    step = out.shape[1]
    rows = pl.ds(pl.multiple_of(pl.program_id(0) * step, step), step)

    def put(core):
        cut = []
        for t in range(3):
            for n in range(2):
                for c in range(2):
                    part = (own, mate)[c ^ core][n ^ at[1], rows, :]
                    cut.append(part[:, t * width : (t + 1) * width])
        out[0] = jnp.concatenate(cut, axis=1).astype(f32)

    for core in range(2):

        @pl.when(at[2] == core)
        def _(core=core):
            put(core)


def spread(own, mate, at, used, other_x, carried=None):
    _, rows, cols = own.shape
    width = 4 * used
    cuts = 2 if rows % 32 == 0 else 1
    whole = pl.BlockSpec((2, rows, cols), lambda j, m: (0, 0, 0), pipeline_mode=pl.Buffered(1))
    more = () if carried is None else (carried,)
    return pl.pallas_call(
        functools.partial(spread_kernel, width=used // 3, other_x=other_x),
        out_shape=pltpu.HBM((2, rows, width), f32),
        grid_spec=pltpu.PrefetchScalarGridSpec(
            num_scalar_prefetch=1,
            grid=(cuts,),
            in_specs=[whole] * 2 + [pl.BlockSpec(memory_space=pl.ANY)] * len(more),
            out_specs=pl.BlockSpec((1, rows // cuts, width), lambda j, m: (m[0] ^ other_x, j, 0)),
        ),
        input_output_aliases={3: 0} if more else {},
        compiler_params=pltpu.CompilerParams(vmem_limit_bytes=40 << 20),
        cost_estimate=CHEAP,
        name="spread",
    )(at, own, mate, *more)


def back_kernel(shards, g_ref, w_ref, *refs):
    acc = jnp.dot(g_ref[...], w_ref[...], preferred_element_type=f32)
    if len(refs) == 2:
        acc = acc + refs[0][0].astype(f32)
    refs[-1][0] = acc.astype(bf16)


def back(grad, w, shards, rows, got=None):
    c, d = w.shape
    n = shards.shape[0]
    step = d
    out = pl.BlockSpec((1, rows, step), lambda j, i, f: (i, 0, j))
    in_specs = [
        pl.BlockSpec((rows, c), lambda j, i, f: (f[i], 0)),
        pl.BlockSpec((c, step), lambda j, i, f: (0, j)),
    ]
    args = [hbm(grad), hbm(w)]
    if got is not None:
        in_specs.append(pl.BlockSpec((1, rows, step), lambda j, i, f: (0, 0, j)))
        args.append(got)
    return pl.pallas_call(
        back_kernel,
        out_shape=pltpu.HBM((n, rows, d), bf16),
        grid_spec=pltpu.PrefetchScalarGridSpec(
            num_scalar_prefetch=1, grid=(d // step, n), in_specs=in_specs, out_specs=out
        ),
        compiler_params=pltpu.CompilerParams(vmem_limit_bytes=40 << 20),
        cost_estimate=CHEAP,
        name="back",
    )(shards, *args)


def finish_kernel(shard, g_ref, w_ref, core, near, x_ref, resid, gain, out, gain_out):
    grad = jnp.dot(g_ref[...], w_ref[...], preferred_element_type=f32)
    grad = grad + core[0].astype(f32) + near[0].astype(f32)
    x = x_ref[...].astype(f32)
    inverse = lax.rsqrt(jnp.mean(x * x, axis=-1, keepdims=True) + epsilon)
    part = jnp.sum(grad * x * inverse, axis=0, keepdims=True)

    @pl.when(pl.program_id(0) == 0)
    def _():
        gain_out[...] = jnp.zeros_like(gain_out)

    gain_out[...] += part
    scaled = grad * gain[...]
    out[...] = (
        resid[...]
        + inverse * scaled
        - x * (inverse * inverse * inverse) * jnp.mean(scaled * x, axis=-1, keepdims=True)
    ).astype(bf16)


def finish(grad, w, shard, core, near, x, resid, gain, tile=256):
    rows, d = x.shape
    c = w.shape[0]
    tiles = rows // tile
    row = lambda i, f: (i, 0)
    once = pl.Buffered(1)
    return pl.pallas_call(
        finish_kernel,
        out_shape=[pltpu.HBM((rows, d), bf16), jax.ShapeDtypeStruct((1, d), f32)],
        grid_spec=pltpu.PrefetchScalarGridSpec(
            num_scalar_prefetch=1,
            grid=(tiles,),
            in_specs=[
                pl.BlockSpec((tile, c), lambda i, f: (f[0] * tiles + i, 0)),
                pl.BlockSpec((c, d), lambda i, f: (0, 0), pipeline_mode=once),
                pl.BlockSpec((1, tile, d), lambda i, f: (1, i, 0)),
                pl.BlockSpec((1, tile, d), lambda i, f: (0, i, 0)),
                pl.BlockSpec((tile, d), row),
                pl.BlockSpec((tile, d), row),
                pl.BlockSpec((1, d), lambda i, f: (0, 0)),
            ],
            out_specs=[pl.BlockSpec((tile, d), row), pl.BlockSpec((1, d), lambda i, f: (0, 0))],
        ),
        compiler_params=pltpu.CompilerParams(vmem_limit_bytes=40 << 20),
        cost_estimate=CHEAP,
        name="finish",
    )(shard.reshape(1), hbm(grad), hbm(w), core, near, hbm(x), hbm(resid), gain)


def rms_inverse(values):
    return lax.rsqrt(jnp.mean(values * values, axis=-1, keepdims=True) + epsilon)


def norm_back(values, inverse, grad_scaled):
    return inverse * grad_scaled - values * (inverse * inverse * inverse) * jnp.mean(
        grad_scaled * values, axis=-1, keepdims=True
    )


def dot(left, right):
    return jnp.dot(left, right, preferred_element_type=f32)


def times_trans(left, right):
    return lax.dot_general(left, right, (((1,), (1,)), ((), ())), preferred_element_type=f32)


def trans_times(left, right):
    return lax.dot_general(left, right, (((0,), (0,)), ((), ())), preferred_element_type=f32)


def rows_at(array, start, count):
    return lax.dynamic_slice_in_dim(array, start, count, 0)


def put_rows(array, rows, start):
    return lax.dynamic_update_slice_in_dim(array, rows, start, 0)


def make_local(sizes):
    def pairs(target):
        found = []
        for gx in range(sizes["gx"]):
            for gc in range(sizes["gc"]):
                for z in range(4):
                    for w in range(sizes["wt"]):
                        goal = target(gx, gc, z, w)
                        if goal is not None and goal != (gx, gc, z, w):
                            found.append((place(gx, gc, z, w), place(*goal)))
        return found

    def place(gx, gc, z, w):
        return ((gx * sizes["gc"] + gc) * 4 + z) * sizes["wt"] + w

    def send(value, target):
        return lax.ppermute(value, AXES, pairs(target))

    def core_mate(gx, gc, z, w):
        return (gx, 1 - gc, z, w)

    def x_mate(gx, gc, z, w):
        return (1 - gx, gc, z, w)

    def near_mate(gx, gc, z, w):
        return (gx, gc, z ^ 1, w)

    def far_mate(gx, gc, z, w):
        return (gx, gc, z ^ 2, w)

    def cross_mate(gx, gc, z, w):
        return (gx, 1 - gc, z ^ 1, w)

    def wt_mate(gx, gc, z, w):
        return (gx, gc, z, 1 - w)

    def wt_x_mate(gx, gc, z, w):
        return (1 - gx, gc, z, 1 - w)

    def to_host(gx, gc, z, w):
        return (gx, 1 - (z & 1), 2 * gc + (z >> 1), w)

    def to_home(gx, gc, z, w):
        return (gx, z >> 1, 2 * (z & 1) + 1 - gc, w)

    def hop1(gx, gc, z, w):
        if gc == 0:
            return (gx, 0, z - 1, w) if z > 0 else None
        return (gx, 1, z + 1, w) if z < 3 else None

    def hop2(gx, gc, z, w):
        if gc == 0:
            return (gx, 0, z - 1, w) if z in (1, 2) else None
        return (gx, 1, z + 1, w) if z in (1, 2) else None

    def hop3(gx, gc, z, w):
        if gc == 0:
            return (gx, 0, z ^ 1, w) if z < 2 else None
        return (gx, 1, z ^ 1, w) if z > 1 else None

    def lane_share(gx, gc, z, w):
        return (gx, 1 - gc, z, w) if gc == z >> 1 else None

    def sum_all(value):
        for axis in ("gc", "wt", "near", "far", "gx"):
            step = 1
            while step < sizes[axis]:

                def mate(gx, gc, z, w, axis=axis, step=step):
                    at = dict(gx=gx, gc=gc, far=z >> 1, near=z & 1, wt=w)
                    at[axis] ^= step
                    return (at["gx"], at["gc"], 2 * at["far"] + at["near"], at["wt"])

                value = value + send(value, mate)
                step *= 2
        return value

    def local(
        tokens, segments, w_qkv, w_proj, w_in, w_out, gain_attn, gain_mlp, query_scale, cotangent
    ):
        gx, gc, host, near, wt = (lax.axis_index(axis) for axis in AXES)
        z = 2 * host + near
        mine = 2 * near + 1 - gc
        parts = 4
        nh = H // parts
        groups = 1
        rows = tokens.shape[1]
        group_len = segments.shape[1]
        wrows = w_qkv.shape[0]
        lane = gc == host
        pair = sizes["wt"] == 2

        def after(value, *others):
            return lax.optimization_barrier((value,) + others)[0]

        picked = pick(w_qkv, mine, parts, groups, nh)
        own = tokens[0]
        got1 = send(own, hop1)
        own_share = send(own, lane_share)
        seg_mate = send(segments, core_mate)
        got2 = send(got1, hop2)
        got1_share = send(got1, lane_share)
        end = jnp.where(gc == 0, z == 0, z == 3)
        if pair:
            wide_own = stretch(picked, groups, nh, 2)
            got1 = after(got1, wide_own)
            other_w = send(picked, wt_mate)
            wide_w = (wide_own, stretch(other_w, groups, nh, 10))
        else:
            flat_all = lax.all_gather(picked, "wt", axis=0, tiled=True)
            by_head = jnp.transpose(
                flat_all[:, : 3 * nh * HD].reshape(D, groups, 3, nh // groups, HD), (0, 2, 1, 3, 4)
            )
            wide_w = (
                jnp.pad(
                    by_head.reshape(D, 3 * nh, HD), ((0, 0), (0, 0), (0, LN - HD))
                ).reshape(D, -1),
            )
        got3 = send(jnp.where(end, own, got2), hop3)
        got2_share = send(got2, lane_share)
        way = 1 - 2 * host
        last = jnp.where(host == 0, jnp.where(z == 0, 3, 0), jnp.where(z == 3, 0, 3))
        places = (z, z + way, z + 2 * way, last)

        half_rows = wrows // 2
        half_w = jnp.stack([rows_at(w, gc * half_rows, half_rows) for w in (w_proj, w_in, w_out)])
        if pair:
            half_w = send(after(half_w, other_w), wt_mate)
        else:
            half_w = lax.all_gather(half_w, "wt", axis=0, tiled=False)

        dim_scale = scale_base / math.sqrt(HD) * jax.nn.softplus(query_scale)
        lane_scale = jnp.tile(jnp.pad(dim_scale * log2e, (0, LN - HD)), nh)[None]
        ones = jnp.tile(
            ((jnp.arange(LN) >= HD) & (jnp.arange(LN) < HD + 3)).astype(f32), 2 * nh
        )[None]
        seg_row = jnp.where(lane, segments, seg_mate)[0]
        fixed = (lane, mine, wt, gain_attn[None], wide_w, lane_scale, ones, group_len)
        carried = project(((own, own_share), (got1, got1_share)), places[:2], *fixed)
        got3_share = send(after(got3, carried[0]), lane_share)
        all_normed, queries, keyval, inputs = project(
            ((got2, got2_share), (got3, got3_share)), places[2:], *fixed, carried=carried
        )
        grad_mlp = send(after(cotangent[0], got3_share), to_host)

        att, att_float, q_aug = attn_fwd(queries, keyval, seg_row, nh)
        att, half_w, _ = lax.optimization_barrier((att, half_w, grad_mlp))

        trades = (core_mate, near_mate, cross_mate)
        att_pieces = [rows_at(att, (mine ^ j) * rows, rows) for j in range(parts)]
        att_pieces = [att_pieces[0]] + [send(att_pieces[j + 1], trades[j]) for j in range(3)]
        half_mate = send(half_w, core_mate)
        if pair:
            w_trans = order(after(picked, att), other_w, wt)
        else:
            w_trans = flat_all.T
        normed_trans = transpose(after(all_normed, w_trans))
        if pair:
            weights = (w_proj, w_in, w_out, half_w, half_mate)
            starts = (wt * wrows, (1 - wt) * wrows + gc * half_rows, (1 - wt) * wrows + (1 - gc) * half_rows)
        else:
            one = gc == 0
            tail_w = jnp.stack(
                [jnp.where(one, half_w, half_mate), jnp.where(one, half_mate, half_w)], axis=1
            )
            weights = (jnp.transpose(tail_w, (2, 0, 1, 3, 4)).reshape(3, D, D),)
            starts = ()
        (
            layer_out,
            left,
            right,
            grad_resid,
            *pieces,
            grad_gain_mlp,
        ) = tail(
            jnp.stack([mine, *starts]), att_pieces, after(inputs, normed_trans), grad_mlp, weights, gain_mlp[None]
        )
        pieces = [pieces[0]] + [send(pieces[j + 1], trades[j]) for j in range(3)]

        shared = share(after(left, pieces[1]), right, 1 - gc)
        from_core = send(shared, core_mate)
        pieces[2:] = [after(piece, shared) for piece in pieces[2:]]
        home_out = send(after(layer_out, *pieces[1:]), to_home)
        late_gain = tick(after(gain_attn.reshape(-1, LN), *pieces[1:]))
        summed = share(left, right, gc, after(from_core, late_gain))
        kept = lax.all_to_all(summed, ("wt", "gx", "near"), 0, 0, tiled=True)

        scale_row = jnp.tile(dim_scale, nh // groups)[None]

        def backward(group, *others):
            first, *rest = pieces
            return attn_bwd(
                q_aug,
                keyval,
                (after(first, summed, *others), *rest),
                att_float,
                mine,
                seg_row,
                scale_row,
                nh,
                group,
                groups,
            )

        def by_rows(grad):
            if pair:
                own, *rest = cross(normed_trans, grad, jnp.stack([wt, gx]))
                got = [send(part, mate) for part, mate in zip(rest, (x_mate, wt_mate, wt_x_mate))]
                return [part[None] for part in (own, *got)]
            part = dot(normed_trans, grad).astype(bf16)
            sources = sizes["wt"] * 2
            got = lax.all_to_all(part, ("wt", "gx"), 0, 0, tiled=True)
            return [got.reshape(sources, D // sources, -1)]

        grad_project, grad_lanes = backward(0)
        layer_out = after(home_out, grad_project)

        last_step = [layer_out]

        def turn(value):
            return after(value, *last_step)

        def done(value):
            last_step[0] = value
            return value

        sources = sizes["wt"] * 4
        to_core = done(back(turn(grad_project), w_trans, jnp.stack([mine ^ 3, mine ^ 1]), rows))
        from_core = send(to_core, core_mate)
        by_place = by_rows(turn(grad_project))
        done(by_place[0])
        to_near = done(back(grad_project, w_trans, (mine ^ 2).reshape(1), rows, turn(from_core)))
        from_near = send(to_near, near_mate)
        t1 = done(total([[turn(kept).reshape(sources, D // sources, -1)]]))
        t1_far = send(t1, far_mate)
        layer_out = done(copy(turn(layer_out)))
        by_place[0] = turn(by_place[0])
        q1 = done(total([by_place]))
        q1_far = send(q1, far_mate)
        grad_tokens, grad_gain_attn = finish(
            grad_project,
            w_trans,
            mine,
            from_core,
            turn(from_near),
            inputs,
            grad_resid,
            late_gain.reshape(1, -1),
        )
        done(grad_tokens)
        t2 = done(add(turn(t1), t1_far))
        t2_near = send(t2, near_mate)
        grad_query_scale = (
            grad_lanes[0, :HD]
            / (dim_scale * log2e)
            * (scale_base / math.sqrt(HD))
            * jax.nn.sigmoid(query_scale)
        )
        small = jnp.concatenate(
            [grad_gain_attn[0], grad_gain_mlp[0], jnp.pad(grad_query_scale, (0, LN - HD))]
        ).reshape(-1, LN)
        q2 = done(add(turn(q1), q1_far))
        q2_near = send(q2, near_mate)
        t4 = done(pair_up(turn(t2), t2_near))
        t4_x = send(t4, x_mate)
        t4_core = send(t4, core_mate)
        home_grad = send(turn(grad_tokens), to_home)
        q4 = done(pair_up(turn(q2), q2_near))
        q4_x = send(q4, x_mate)
        q4_core = send(q4, core_mate)
        t4_x = done(turn(t4_x))
        t4_cross = send(t4_x, core_mate)
        used = 3 * nh * HD
        spread_at = jnp.stack([gx, near, 1 - gc])
        totals = place_tail((turn(t4), t4_x, t4_core, t4_cross), jnp.stack([gx, near, gc]))
        done(totals[0])
        q4_core = done(turn(q4_core))
        small = done(sum_all(turn(small))).reshape(-1)
        grad_tokens = done(copy(turn(home_grad)))
        q4_x = done(turn(q4_x))
        q4_cross = send(q4_x, core_mate)
        total_qkv = done(spread(turn(q4), q4_core, spread_at, used, 0))
        total_qkv = spread(turn(q4_x), q4_cross, spread_at, used, 1, total_qkv).reshape(wrows, 3 * D)
        return (
            layer_out[None],
            grad_tokens[None],
            total_qkv,
            *totals,
            small[:D],
            small[D : 2 * D],
            small[2 * D : 2 * D + HD],
        )

    return local


def solution(mesh):
    groups, parts, wt = (mesh.shape[axis] for axis in ("grp", "ctx", "wt"))
    inner = Mesh(mesh.devices.reshape(groups // 2, 2, parts // 2, 2, wt), AXES)
    sizes = dict(inner.shape)
    split = P(("gx", "gc", "wt"), ("far", "near"), None)
    weight = P("wt", None)
    return jax.shard_map(
        make_local(sizes),
        mesh=inner,
        in_specs=(
            split,
            P(("gx", "gc", "wt"), None),
            weight,
            weight,
            weight,
            weight,
            P(),
            P(),
            P(),
            split,
        ),
        out_specs=(split, split, weight, weight, weight, weight, P(), P(), P()),
        check_vma=False,
    )
```

```python
import functools
import math

import jax
import jax.numpy as jnp
from jax import lax
from jax.experimental import pallas as pl
from jax.experimental.pallas import tpu as pltpu
from jax.sharding import Mesh
from jax.sharding import PartitionSpec as P

D = 1280
H = 16
HD = 80
LN = 128
epsilon = 1e-06
scale_base = 1.442695041
log2e = 1.4426950408889634
NEG = -1e30
def cost(us):
    return pl.CostEstimate(flops=int(us * 1_000_000_000), transcendentals=0, bytes_accessed=1000)


CHEAP = cost(0.001)
f32 = jnp.float32
bf16 = jnp.bfloat16
AXES = ("gx", "gc", "far", "near", "wt")


def hbm(x):
    return pltpu.with_memory_space_constraint(x, pltpu.HBM)


def block_flags(seg_row, bq, bk):
    n = seg_row.shape[0]
    q = seg_row.reshape(n // bq, bq)
    k = seg_row.reshape(n // bk, bk)
    qf, ql = q[:, 0][:, None], q[:, -1][:, None]
    kf, kl = k[:, 0][None], k[:, -1][None]
    qs = jnp.arange(n // bq, dtype=jnp.int32)[:, None] * bq
    ks = jnp.arange(n // bk, dtype=jnp.int32)[None] * bk
    below = ks + bk - 1 <= qs
    skip = (ks > qs + bq - 1) | ((kf > 0) & (kl < qf))
    same = (qf == ql) & (kl == ql) & ((kf == kl) | ((kf == 0) & (kl == 1)))
    full = below & ((kl == 0) | same)
    flags = jnp.where(skip, 0, jnp.where(full, 1, 2))
    if bq == bk:
        flags = jnp.where(qs == ks, 3, flags)
    return flags.astype(jnp.int32).reshape(-1)


def put_split(base, col, lanes):
    hi = col.astype(bf16).astype(f32)
    rest = col - hi
    mid = rest.astype(bf16).astype(f32)
    out = jnp.where(lanes == HD, hi, base)
    out = jnp.where(lanes == HD + 1, mid, out)
    return jnp.where(lanes == HD + 2, rest - mid, out).astype(bf16)


def fwd_kernel(flags, q_ref, kv, segc, segr, att, of, qaug, m_s, acc_s, *, nh, bq, bk, nk):
    qi = pl.program_id(0)
    count = (qi * bq + bq + bk - 1) // bk
    nt = (((1,), (1,)), ((), ()))
    acc_s[...] = jnp.zeros_like(acc_s)
    m_s[...] = jnp.zeros_like(m_s)

    def mask(ko, q0=0, qn=bq, kn=bk):
        qpos = qi * bq + q0 + lax.broadcasted_iota(jnp.int32, (qn, kn), 0)
        kpos = ko + lax.broadcasted_iota(jnp.int32, (qn, kn), 1)
        ks = segr[:, pl.ds(ko, kn)]
        return (kpos <= qpos) & ((ks == 0) | (ks == segc[q0 : q0 + qn, :]))

    def step(kb, masked, q0=0, qn=bq, kn=bk):
        ko = pl.multiple_of(kb * bk, bk)
        if masked:
            allowed = mask(ko, q0, qn, kn)
        rows = slice(q0, q0 + qn)
        for h in range(nh):
            k = kv[pl.ds(ko, kn), h * LN : (h + 1) * LN]
            v = kv[pl.ds(ko, kn), (nh + h) * LN : (nh + h + 1) * LN]
            q = q_ref[rows, h * LN : (h + 1) * LN]
            p = jnp.exp2(lax.dot_general(q, k, nt, preferred_element_type=f32))
            if masked:
                p = jnp.where(allowed, p, 0.0)
            acc_s[h, rows, :] += jnp.dot(p.astype(bf16), v, preferred_element_type=f32)

    def body(kb, carry):
        flag = flags[qi * nk + kb]

        @pl.when(flag == 1)
        def _():
            step(kb, False)

        @pl.when(flag >= 2)
        def _():
            step(kb, True)

        return carry

    lax.fori_loop(0, count, body, 0)
    bad = jnp.zeros((bq, 1), f32)
    for h in range(nh):
        total = acc_s[h][:, HD : HD + 1]
        bad = jnp.maximum(bad, jnp.where((total > 2.0**-60) & (total < 2.0**60), 0.0, 1.0))

    @pl.when(jnp.max(bad) > 0.0)
    def _():
        def head(h, carry):
            kc = pl.ds(pl.multiple_of(h * LN, LN), LN)
            vc = pl.ds(pl.multiple_of((nh + h) * LN, LN), LN)
            m_s[h] = jnp.full((bq, LN), NEG, f32)
            acc_s[h] = jnp.zeros((bq, LN), f32)

            def inner(kb, carry):
                @pl.when(flags[qi * nk + kb] > 0)
                def _():
                    ko = pl.multiple_of(kb * bk, bk)
                    s = lax.dot_general(
                        q_ref[:, kc], kv[pl.ds(ko, bk), kc], nt, preferred_element_type=f32
                    )
                    s = jnp.where(mask(ko), s, NEG)
                    old = m_s[h]
                    new = jnp.maximum(old, jnp.max(s, axis=1, keepdims=True))
                    p = jnp.exp2(s - new[:, :1]).astype(bf16)
                    m_s[h] = new
                    acc_s[h] = acc_s[h] * jnp.exp2(old - new) + jnp.dot(
                        p, kv[pl.ds(ko, bk), vc], preferred_element_type=f32
                    )

                return carry

            lax.fori_loop(0, count, inner, 0)
            return carry

        lax.fori_loop(0, nh, head, 0)

    lanes = lax.broadcasted_iota(jnp.int32, (bq, LN), 1)
    outs = []
    for h in range(nh):
        acc = acc_s[h]
        total = acc[:, HD : HD + 1]
        out = acc * (1.0 / total)
        of[:, h * LN : (h + 1) * LN] = jnp.where(lanes < HD, out, 0.0).astype(bf16)
        outs.append(out[:, :HD])
        lse = m_s[h][:, :1] + jnp.log2(total)
        qaug[:, h * LN : (h + 1) * LN] = put_split(
            q_ref[:, h * LN : (h + 1) * LN].astype(f32), -lse, lanes
        )
    att[...] = jnp.concatenate(outs, axis=1).astype(bf16)


def attn_fwd(q, kv, seg_row, nh, bq=512, bk=512):
    n = q.shape[0]
    w = nh * LN
    spec = pltpu.PrefetchScalarGridSpec(
        num_scalar_prefetch=1,
        grid=(n // bq,),
        in_specs=[
            pl.BlockSpec((bq, w), lambda i, f: (i, 0)),
            pl.BlockSpec((n, 2 * w), lambda i, f: (0, 0)),
            pl.BlockSpec((bq, 1), lambda i, f: (i, 0)),
            pl.BlockSpec((1, n), lambda i, f: (0, 0)),
        ],
        out_specs=[
            pl.BlockSpec((bq, nh * HD), lambda i, f: (i, 0)),
            pl.BlockSpec((bq, w), lambda i, f: (i, 0)),
            pl.BlockSpec((bq, w), lambda i, f: (i, 0)),
        ],
        scratch_shapes=[pltpu.VMEM((nh, bq, LN), f32), pltpu.VMEM((nh, bq, LN), f32)],
    )
    return pl.pallas_call(
        functools.partial(fwd_kernel, nh=nh, bq=bq, bk=bk, nk=n // bk),
        out_shape=[
            pltpu.HBM((n, nh * HD), bf16),
            pltpu.HBM((n, w), bf16),
            pltpu.HBM((n, w), bf16),
        ],
        grid_spec=spec,
        compiler_params=pltpu.CompilerParams(vmem_limit_bytes=40 << 20),
        cost_estimate=cost(0.01),
        name="attn_fwd",
    )(block_flags(seg_row, bq, bk), hbm(q), hbm(kv), seg_row[:, None], seg_row[None])


def bwd_kernel(
    flags, mine, qa, kk, vv, do0, do1, do2, do3, of, segc, segr, scale, dqkv, gscale, doa_s, dq_s, dk_s, dv_s, *, first, nh, bq, bk, n
):
    nk = n // bk
    nq = n // bq
    kb = pl.program_id(0)
    part = n // 4
    step_rows = 256 if part % 256 == 0 else part
    lanes = lax.broadcasted_iota(jnp.int32, (step_rows, LN), 1)

    @pl.when(kb == 0)
    def _():
        dq_s[...] = jnp.zeros_like(dq_s)
        for j, piece in enumerate((do0, do1, do2, do3)):
            start = (mine[0] ^ j) * part
            for i in range(part // step_rows):
                d = piece[i * step_rows : (i + 1) * step_rows, :].astype(f32)
                r = pl.ds(pl.multiple_of(start + i * step_rows, step_rows), step_rows)
                for h in range(nh):
                    at = (first + h) * HD
                    dh = jnp.concatenate(
                        [d[:, at : at + HD], jnp.zeros((step_rows, LN - HD), f32)], axis=1
                    )
                    c = slice(h * LN, (h + 1) * LN)
                    delta = jnp.sum(dh * of[r, c].astype(f32), axis=1, keepdims=True)
                    doa_s[r, c] = put_split(dh, -delta, lanes)

    dk_s[...] = jnp.zeros_like(dk_s)
    dv_s[...] = jnp.zeros_like(dv_s)
    ko = kb * bk
    nt = (((1,), (1,)), ((), ()))
    tn = (((0,), (0,)), ((), ()))

    def step(qi, masked, q0=0, qn=bq, kn=bk):
        qo = pl.multiple_of(qi * bq + q0, qn)
        rows = slice(0, kn)
        if masked:
            kpos = ko + lax.broadcasted_iota(jnp.int32, (kn, qn), 0)
            qpos = qo + lax.broadcasted_iota(jnp.int32, (kn, qn), 1)
            ks = segc[rows, :]
            allowed = (kpos <= qpos) & ((ks == 0) | (ks == segr[:, pl.ds(qo, qn)]))
        for h in range(nh):
            c = slice(h * LN, (h + 1) * LN)
            q = qa[pl.ds(qo, qn), c]
            k = kk[rows, c]
            d = doa_s[pl.ds(qo, qn), c]
            p = jnp.exp2(lax.dot_general(k, q, nt, preferred_element_type=f32))
            if masked:
                p = jnp.where(allowed, p, 0.0)
            ds = (p * lax.dot_general(vv[rows, c], d, nt, preferred_element_type=f32)).astype(bf16)
            dv_s[h, rows, :] += jnp.dot(p.astype(bf16), d, preferred_element_type=f32)
            dk_s[h, rows, :] += jnp.dot(ds, q, preferred_element_type=f32)
            dq_s[h, pl.ds(qo, qn), :] += lax.dot_general(ds, k, tn, preferred_element_type=f32)

    def body(qi, carry):
        flag = flags[qi * nk + kb]

        @pl.when(flag == 1)
        def _():
            step(qi, False)

        @pl.when(flag == 2)
        def _():
            step(qi, True)

        if bq == bk:

            @pl.when(flag == 3)
            def _():
                step(qi, True, 0, bq // 2, bk // 2)
                step(qi, True, bq // 2, bq // 2, bk)

        return carry

    lax.fori_loop(ko // bq, nq, body, 0)
    r = pl.multiple_of(ko, bk)
    ln2 = math.log(2.0)
    gap = dqkv.shape[1] - 3 * nh * HD
    dqkv[pl.ds(r, bk), nh * HD :] = jnp.concatenate(
        [dk_s[h][:, :HD] * ln2 for h in range(nh)]
        + [dv_s[h][:, :HD] for h in range(nh)]
        + [jnp.zeros((bk, gap), f32)],
        axis=1,
    ).astype(bf16)

    @pl.when(kb == nk - 1)
    def _():
        total = jnp.zeros((1, LN), f32)
        for i in range(nq):
            rows = slice(i * bq, (i + 1) * bq)
            for h in range(nh):
                total = total + jnp.sum(
                    dq_s[h, rows, :] * qa[rows, h * LN : (h + 1) * LN].astype(f32), axis=0, keepdims=True
                )
            grads = jnp.concatenate([dq_s[h, rows, :][:, :HD] for h in range(nh)], axis=1)
            dqkv[rows, 0 : nh * HD] = (grads * scale[...]).astype(bf16)
        gscale[...] = jnp.broadcast_to(total, gscale.shape)


def attn_bwd(qa, kv, pieces, of, mine, seg_row, scale, heads, group, groups, bq=512, bk=512):
    n = qa.shape[0]
    nh = heads // groups
    w = nh * LN
    once = pl.Buffered(1)
    spec = pltpu.PrefetchScalarGridSpec(
        num_scalar_prefetch=2,
        grid=(n // bk,),
        in_specs=[
            pl.BlockSpec((n, w), lambda i, f, m: (0, group), pipeline_mode=once),
            pl.BlockSpec((bk, w), lambda i, f, m: (i, group)),
            pl.BlockSpec((bk, w), lambda i, f, m: (i, groups + group)),
            *[pl.BlockSpec((n // 4, heads * HD), lambda i, f, m: (0, 0), pipeline_mode=once)] * 4,
            pl.BlockSpec((n, w), lambda i, f, m: (0, group), pipeline_mode=once),
            pl.BlockSpec((bk, 1), lambda i, f, m: (i, 0)),
            pl.BlockSpec((1, n), lambda i, f, m: (0, 0)),
            pl.BlockSpec((1, nh * HD), lambda i, f, m: (0, 0)),
        ],
        out_specs=[
            pl.BlockSpec((n, lanes_up(3 * nh * HD)), lambda i, f, m: (0, 0)),
            pl.BlockSpec((8, LN), lambda i, f, m: (0, 0)),
        ],
        scratch_shapes=[
            pltpu.VMEM((n, w), bf16),
            pltpu.VMEM((nh, n, LN), f32),
            pltpu.VMEM((nh, bk, LN), f32),
            pltpu.VMEM((nh, bk, LN), f32),
        ],
    )
    return pl.pallas_call(
        functools.partial(bwd_kernel, first=group * nh, nh=nh, bq=bq, bk=bk, n=n),
        out_shape=[
            pltpu.HBM((n, lanes_up(3 * nh * HD)), bf16),
            pltpu.HBM((8, LN), f32),
        ],
        grid_spec=spec,
        compiler_params=pltpu.CompilerParams(vmem_limit_bytes=48 << 20),
        cost_estimate=cost(300 if group == 0 else 0.001),
        name="attn_bwd",
    )(block_flags(seg_row, bq, bk), mine.reshape(1), hbm(qa), hbm(kv), hbm(kv), *pieces, hbm(of), seg_row[:, None], seg_row[None], scale)


def quarter_columns(place, parts, groups, nh):
    width = nh // groups * HD
    return [
        (t * D + place * nh * HD + g * width, width) for g in range(groups) for t in range(3)
    ]


def pick_kernel(mine, w_ref, out, *, parts, groups, nh):
    for i in range(parts):

        @pl.when(mine[0] == i)
        def _(i=i):
            cut = [w_ref[:, a : a + width] for a, width in quarter_columns(i, parts, groups, nh)]
            used = sum(x.shape[1] for x in cut)
            pad = jnp.zeros((cut[0].shape[0], out.shape[1] - used), out.dtype)
            out[...] = jnp.concatenate(cut + [pad], axis=1)


def lanes_up(n):
    return -(-n // LN) * LN


def pick(w, mine, parts, groups, nh):
    rows = w.shape[0]
    step = 160 if rows % 160 == 0 else rows
    return pl.pallas_call(
        functools.partial(pick_kernel, parts=parts, groups=groups, nh=nh),
        out_shape=pltpu.HBM((rows, lanes_up(3 * nh * HD)), w.dtype),
        grid_spec=pltpu.PrefetchScalarGridSpec(
            num_scalar_prefetch=1,
            grid=(rows // step,),
            in_specs=[pl.BlockSpec((step, 3 * D), lambda i, m: (i, 0))],
            out_specs=pl.BlockSpec((step, lanes_up(3 * nh * HD)), lambda i, m: (i, 0)),
        ),
        cost_estimate=cost(5),
        name="pick",
    )(mine.reshape(1), hbm(w))


def stretch_kernel(x_ref, out, *, groups, nh):
    value = x_ref[...]
    each = 3 * nh * HD // groups
    zero = jnp.zeros((value.shape[0], LN - HD), value.dtype)
    per = nh // groups
    wide = []
    for t in range(3):
        for h in range(nh):
            at = (h // per) * each + t * per * HD + (h % per) * HD
            wide += [value[:, at : at + HD], zero]
    out[...] = jnp.concatenate(wide, axis=1)


def stretch(x, groups, nh, us):
    rows, width = x.shape
    step = 160
    return pl.pallas_call(
        functools.partial(stretch_kernel, groups=groups, nh=nh),
        out_shape=pltpu.HBM((rows, 3 * nh * LN), x.dtype),
        grid=(rows // step,),
        in_specs=[pl.BlockSpec((step, width), lambda i: (i, 0))],
        out_specs=pl.BlockSpec((step, 3 * nh * LN), lambda i: (i, 0)),
        cost_estimate=cost(us),
        name="stretch",
    )(hbm(x))


def order_kernel(own_first, a_ref, b_ref, out):
    half = pl.program_id(0)

    @pl.when(half == 0)
    def _():
        out[...] = a_ref[...].T

    @pl.when(half == 1)
    def _():
        out[...] = b_ref[...].T


def order(own, other, own_at):
    rows, width = own.shape
    step = 256
    return pl.pallas_call(
        order_kernel,
        out_shape=pltpu.HBM((width, 2 * rows), own.dtype),
        grid_spec=pltpu.PrefetchScalarGridSpec(
            num_scalar_prefetch=1,
            grid=(2, width // step),
            in_specs=[
                pl.BlockSpec((rows, step), lambda i, j, m: (0, j * (1 - i))),
                pl.BlockSpec((rows, step), lambda i, j, m: (0, j * i)),
            ],
            out_specs=pl.BlockSpec((step, rows), lambda i, j, m: (j, i ^ m[0])),
        ),
        cost_estimate=cost(200.0),
        name="order",
    )(own_at.reshape(1), hbm(own), hbm(other))


def transpose_kernel(x_ref, out):
    out[...] = x_ref[...].T


def transpose(x):
    rows, cols = x.shape
    step = 256
    return pl.pallas_call(
        transpose_kernel,
        out_shape=pltpu.HBM((cols, rows), x.dtype),
        grid=(rows // step,),
        in_specs=[pl.BlockSpec((step, cols), lambda i: (i, 0))],
        out_specs=pl.BlockSpec((cols, step), lambda i: (0, i)),
        cost_estimate=CHEAP,
        name="transpose",
    )(hbm(x))


def project_kernel(info, *refs, count, halves, width, fresh):
    pairs = refs[: 2 * count]
    gain = refs[2 * count]
    weights = refs[2 * count + 1 : 2 * count + 1 + halves]
    scale, ones = refs[2 * count + 1 + halves : 2 * count + 3 + halves]
    normed_ref, q_ref, kv_ref, mine_ref, w = refs[-5:]
    j, tile = pl.program_id(0), pl.program_id(1)
    step = normed_ref.shape[0]

    @pl.when((j == 0) & (tile == 0))
    def _():
        for i, ref in enumerate(weights):
            h = ref.shape[0]
            start = (info[count + 2] ^ i) * h if halves == 2 else 0
            w[pl.ds(pl.multiple_of(start, 16), h), :] = ref[...]
        if not fresh:
            mine_ref[...] = refs[2 * count + 3 + halves][...]

    def work(x_ref):
        value = x_ref[...]
        x = value.astype(f32)
        inverse = lax.rsqrt(jnp.mean(x * x, axis=-1, keepdims=True) + epsilon)
        normed = (x * inverse * gain[...]).astype(bf16)
        normed_ref[...] = normed
        q_ref[...] = (
            jnp.dot(normed, w[:, :width], preferred_element_type=f32) * scale[...]
        ).astype(bf16)
        kv_ref[...] = (
            jnp.dot(normed, w[:, width:], preferred_element_type=f32) + ones[...]
        ).astype(bf16)

        @pl.when(info[count + 1] == info[j])
        def _():
            mine_ref[pl.ds(pl.multiple_of(tile * step, step), step), :] = value

    for i in range(count):
        for lane in range(2):

            @pl.when((j == i) & (info[count] == lane))
            def _(i=i, lane=lane):
                work(pairs[2 * i + 1 - lane])


def project(pairs, places, lane, mine, wt, gain, weights, scale, ones, group_len, carried=None):
    count = len(pairs)
    rows, d = pairs[0][0].shape
    width = scale.shape[1]
    step = 256
    tiles = rows // step
    full = lambda j, t, f: (0, 0)
    at = lambda j, t, f: (f[j] * tiles + t, 0)
    once = pl.Buffered(1)
    info = jnp.stack(list(places) + [lane.astype(jnp.int32), mine, wt])
    args = [x for pair in pairs for x in pair] + [gain, *map(hbm, weights), scale, ones]
    in_specs = [
        pl.BlockSpec(
            (step, d),
            lambda j, t, f, i=i: (jnp.where(j == i, t, jnp.where(j > i, tiles - 1, 0)), 0),
        )
        for i in range(count)
        for _ in range(2)
    ]
    in_specs += [pl.BlockSpec((1, d), full, pipeline_mode=once)]
    in_specs += [pl.BlockSpec(w.shape, full, pipeline_mode=once) for w in weights]
    in_specs += [
        pl.BlockSpec((1, width), full, pipeline_mode=once),
        pl.BlockSpec((1, 2 * width), full, pipeline_mode=once),
    ]
    aliases = {}
    if carried is not None:
        base = len(args) + 2
        args += [hbm(x) for x in (carried[3], *carried[:3])]
        in_specs += [pl.BlockSpec((rows, d), full, pipeline_mode=once)]
        in_specs += [pl.BlockSpec(memory_space=pl.ANY)] * 3
        aliases = {base: 0, base + 1: 1, base + 2: 2}
    return pl.pallas_call(
        functools.partial(
            project_kernel, count=count, halves=len(weights), width=width, fresh=carried is None
        ),
        out_shape=[
            pltpu.HBM((group_len, d), bf16),
            pltpu.HBM((group_len, width), bf16),
            pltpu.HBM((group_len, 2 * width), bf16),
            pltpu.HBM((rows, d), bf16),
        ],
        grid_spec=pltpu.PrefetchScalarGridSpec(
            num_scalar_prefetch=1,
            grid=(count, tiles),
            in_specs=in_specs,
            out_specs=[
                pl.BlockSpec((step, d), at),
                pl.BlockSpec((step, width), at),
                pl.BlockSpec((step, 2 * width), at),
                pl.BlockSpec((rows, d), full),
            ],
            scratch_shapes=[pltpu.VMEM((d, 3 * width), bf16)],
        ),
        input_output_aliases=aliases,
        compiler_params=pltpu.CompilerParams(vmem_limit_bytes=48 << 20),
        cost_estimate=cost(15),
        name="project",
    )(info, *args)


def tail_body(at, p0, p1, p2, p3, x_ref, g_ref, w_s, gain, outs, need):
    lo_ref, left_ref, right_ref, gr_ref, c0, c1, c2, c3, gg_ref = outs
    att_ref, nm_ref, act_ref = (left_ref.at[i] for i in range(3))
    gp_ref, gh_ref = (right_ref.at[i] for i in range(2))
    right_ref[2] = g_ref[...]
    mine = at[0]
    pieces = (p0, p1, p2, p3)
    cols = p0.shape[1]
    nt = (((1,), (1,)), ((), ()))
    for i in range(4):

        @pl.when(mine == i)
        def _(i=i):
            att_ref[...] = jnp.concatenate([pieces[i ^ k][...] for k in range(4)], axis=1)

    need(0)
    resid = x_ref[...].astype(f32) + jnp.dot(att_ref[...], w_s[0], preferred_element_type=f32)
    inverse = lax.rsqrt(jnp.mean(resid * resid, axis=-1, keepdims=True) + epsilon)
    normed = (resid * inverse * gain[...]).astype(bf16)
    nm_ref[...] = normed
    need(1)
    hidden = jnp.dot(normed, w_s[1], preferred_element_type=f32)
    sig = 1.0 / (1.0 + jnp.exp(-hidden))
    active = (hidden * sig).astype(bf16)
    act_ref[...] = active
    need(2)
    lo_ref[...] = (resid + jnp.dot(active, w_s[2], preferred_element_type=f32)).astype(bf16)
    grad_active = lax.dot_general(g_ref[...], w_s[2], nt, preferred_element_type=f32)
    grad_hidden = (grad_active * sig * (1.0 + hidden * (1.0 - sig))).astype(bf16)
    gh_ref[...] = grad_hidden
    grad_normed = lax.dot_general(grad_hidden, w_s[1], nt, preferred_element_type=f32)
    gg_ref[...] += jnp.sum(grad_normed * resid * inverse, axis=0, keepdims=True)
    scaled = grad_normed * gain[...]
    grad_resid = (
        g_ref[...].astype(f32)
        + inverse * scaled
        - resid * (inverse * inverse * inverse) * jnp.mean(scaled * resid, axis=-1, keepdims=True)
    )
    gr_ref[...] = grad_resid
    grad_proj = grad_resid.astype(bf16)
    gp_ref[...] = grad_proj
    grad_att = lax.dot_general(grad_proj, w_s[0], nt, preferred_element_type=f32).astype(bf16)
    for i in range(4):

        @pl.when(mine == i)
        def _(i=i):
            for j, out in enumerate((c0, c1, c2, c3)):
                out[...] = grad_att[:, (i ^ j) * cols : ((i ^ j) + 1) * cols]


def tail_kernel(at, p0, p1, p2, p3, x_ref, g_ref, own0, own1, own2, half, other, gain, *refs, rows, hrows):
    w_s, sems = refs[-2:]
    outs = refs[:-2]

    def copies(i):
        parts = (((own0, own1, own2)[i], at[1], rows), (half.at[i], at[2], hrows), (other.at[i], at[3], hrows))
        return [
            pltpu.make_async_copy(
                part, w_s.at[i, pl.ds(pl.multiple_of(start, 16), n), :], sems.at[3 * i + k]
            )
            for k, (part, start, n) in enumerate(parts)
        ]

    @pl.when(pl.program_id(0) == 0)
    def _():
        outs[-1][...] = jnp.zeros_like(outs[-1])
        for i in range(3):
            for c in copies(i):
                c.start()

    def need(i):
        @pl.when(pl.program_id(0) == 0)
        def _():
            for c in copies(i):
                c.wait()

    tail_body(at, p0, p1, p2, p3, x_ref, g_ref, w_s, gain, outs, need)


def whole_tail_kernel(at, p0, p1, p2, p3, x_ref, g_ref, w, gain, *outs):
    @pl.when(pl.program_id(0) == 0)
    def _():
        outs[-1][...] = jnp.zeros_like(outs[-1])

    tail_body(at, p0, p1, p2, p3, x_ref, g_ref, w, gain, outs, lambda i: None)


def tail(at, pieces, x, g, weights, gain, tile=256):
    rows, d = x.shape
    cols = pieces[0].shape[1]
    row = lambda i, m: (i, 0)
    once = pl.Buffered(1)
    whole = lambda *shape: pl.BlockSpec(shape, lambda i, m: (0,) * len(shape), pipeline_mode=once)
    wide = pl.BlockSpec((tile, d), row)
    slim = pl.BlockSpec((tile, cols), row)
    if len(weights) == 5:
        body = functools.partial(tail_kernel, rows=weights[0].shape[0], hrows=weights[3].shape[1])
        scratch = [pltpu.VMEM((3, d, d), bf16), pltpu.SemaphoreType.DMA((9,))]
        weight_specs = [pl.BlockSpec(memory_space=pl.ANY)] * 5
    else:
        body = whole_tail_kernel
        scratch = []
        weight_specs = [whole(*w.shape) for w in weights]
    return pl.pallas_call(
        body,
        out_shape=[pltpu.HBM((rows, d), bf16)]
        + [pltpu.HBM((3, rows, d), bf16)] * 2
        + [pltpu.HBM((rows, d), f32)]
        + [pltpu.HBM((rows, cols), bf16)] * 4
        + [pltpu.HBM((1, d), f32)],
        grid_spec=pltpu.PrefetchScalarGridSpec(
            num_scalar_prefetch=1,
            grid=(rows // tile,),
            in_specs=[slim] * 4 + [wide] * 2 + weight_specs + [whole(1, d)],
            out_specs=[wide]
            + [pl.BlockSpec((3, tile, d), lambda i, m: (0, i, 0))] * 2
            + [wide]
            + [slim] * 4
            + [pl.BlockSpec((1, d), lambda i, m: (0, 0))],
            scratch_shapes=scratch,
        ),
        compiler_params=pltpu.CompilerParams(vmem_limit_bytes=52 << 20),
        cost_estimate=cost(0.01),
        name="tail",
    )(at, *pieces, hbm(x), g, *map(hbm, weights), gain)


tn_dims = (((0,), (0,)), ((), ()))


def share_kernel(col, left, right, *refs):
    value = lax.dot_general(left[0], right[0], tn_dims, preferred_element_type=f32)
    if len(refs) == 2:
        value = value + refs[0][...].astype(f32)
    refs[-1][...] = value.astype(bf16)


def share(left, right, col, got=None):
    n, rows, d = left.shape
    w = d // 2
    block = pl.BlockSpec((d, w), lambda i, c: (0, i))
    return pl.pallas_call(
        share_kernel,
        out_shape=pltpu.HBM((d, n * w), bf16),
        grid_spec=pltpu.PrefetchScalarGridSpec(
            num_scalar_prefetch=1,
            grid=(n,),
            in_specs=[
                pl.BlockSpec((1, rows, d), lambda i, c: (i, 0, 0)),
                pl.BlockSpec((1, rows, w), lambda i, c: (i, 0, c[0])),
            ]
            + [block] * (got is not None),
            out_specs=block,
        ),
        compiler_params=pltpu.CompilerParams(vmem_limit_bytes=40 << 20),
        cost_estimate=CHEAP,
        name="share",
    )(col.reshape(1), hbm(left), hbm(right), *(() if got is None else (hbm(got),)))


def copy(x):
    return pl.pallas_call(
        tick_kernel, out_shape=pltpu.HBM(x.shape, x.dtype), cost_estimate=CHEAP, name="copy"
    )(x)


def tick_kernel(x_ref, out):
    out[...] = x_ref[...]


def tick(x):
    return pl.pallas_call(
        tick_kernel, out_shape=jax.ShapeDtypeStruct(x.shape, x.dtype), cost_estimate=cost(200.0), name="tick"
    )(x)


def total_kernel(*refs, counts):
    out = refs[-1]
    start, column = 0, 0
    for count in counts:
        group = refs[start : start + count]
        start += count
        acc = jnp.zeros(group[0].shape[1:], f32)
        for ref in group:
            for i in range(ref.shape[0]):
                acc = acc + ref[i].astype(f32)
        out[:, column : column + acc.shape[1]] = acc.astype(bf16)
        column += acc.shape[1]


def total(groups):
    flat = [x for group in groups for x in group]
    rows = flat[0].shape[1]
    cuts = 2 if rows % 32 == 0 else 1
    width = sum(group[0].shape[2] for group in groups)
    return pl.pallas_call(
        functools.partial(total_kernel, counts=[len(group) for group in groups]),
        out_shape=pltpu.HBM((rows, width), bf16),
        grid=(cuts,),
        in_specs=[
            pl.BlockSpec((x.shape[0], rows // cuts, x.shape[2]), lambda i: (0, i, 0)) for x in flat
        ],
        out_specs=pl.BlockSpec((rows // cuts, width), lambda i: (i, 0)),
        compiler_params=pltpu.CompilerParams(vmem_limit_bytes=40 << 20),
        cost_estimate=cost(0.001),
        name="total",
    )(*flat)


def add_kernel(a_ref, b_ref, out):
    out[...] = (a_ref[...].astype(f32) + b_ref[...].astype(f32)).astype(bf16)


def add(a, b):
    return pl.pallas_call(
        add_kernel, out_shape=pltpu.HBM(a.shape, bf16), cost_estimate=CHEAP, name="add"
    )(a, b)


def pair_kernel(a_ref, b_ref, out):
    out[0] = a_ref[...]
    out[1] = b_ref[...]


def pair_up(a, b, us=0.001):
    return pl.pallas_call(
        pair_kernel, out_shape=pltpu.HBM((2,) + a.shape, bf16), cost_estimate=cost(us), name="pair_up"
    )(a, b)


def by_bits(first, second, put):
    for i in range(2):
        for j in range(2):

            @pl.when((first == i) & (second == j))
            def _(i=i, j=j):
                put(i, j)


def place_kernel(at, own, own_x, mate, mate_x, o0, o1, o2):
    block = pl.program_id(0)
    slot = (block % 2) ^ at[1]
    w = o0.shape[2] // 2

    def put(other_x, core):
        refs = (own_x, mate_x) if other_x else (own, mate)
        for side in range(2):
            part = refs[side ^ core][slot].astype(f32)
            for i, out in enumerate((o0, o1, o2)):
                out[0, :, side * w : (side + 1) * w] = part[:, i * w : (i + 1) * w]

    by_bits((block // 2) ^ at[0], at[2], put)


def place_tail(arrays, at):
    _, h, width = arrays[0].shape
    d = width // 3 * 2
    whole = pl.BlockSpec((2, h, width), lambda i, m: (0, 0, 0), pipeline_mode=pl.Buffered(1))
    outs = pl.pallas_call(
        place_kernel,
        out_shape=[pltpu.HBM((4, h, d), f32)] * 3,
        grid_spec=pltpu.PrefetchScalarGridSpec(
            num_scalar_prefetch=1,
            grid=(4,),
            in_specs=[whole] * 4,
            out_specs=[pl.BlockSpec((1, h, d), lambda i, m: (i, 0, 0))] * 3,
        ),
        compiler_params=pltpu.CompilerParams(vmem_limit_bytes=40 << 20),
        cost_estimate=cost(0.001),
        name="place_tail",
    )(at, *arrays)
    return [out.reshape(4 * h, d) for out in outs]


def cross_kernel(at, x_ref, g_ref, *refs):
    s = refs[-1]
    s[...] = jnp.dot(x_ref[...], g_ref[...], preferred_element_type=f32)
    half = s.shape[0] // 2
    for w in range(2):

        @pl.when(pl.program_id(0) == w)
        def _(w=w):
            for x in range(2):
                rows = pl.ds(pl.multiple_of((at[1] ^ x) * half, 16), half)
                refs[2 * w + x][...] = s[rows, :].astype(bf16)


def cross(x, g, at):
    d, rows = x.shape
    w = d // 2
    cols = g.shape[1]
    step = 512 if cols % 512 == 0 else cols
    n = cols // step
    first = pl.BlockSpec((w // 2, step), lambda i, j, m: (0, jnp.where(i == 0, j, n - 1)))
    second = pl.BlockSpec((w // 2, step), lambda i, j, m: (0, jnp.where(i == 1, j, 0)))
    return pl.pallas_call(
        cross_kernel,
        out_shape=[pltpu.HBM((w // 2, cols), bf16)] * 4,
        grid_spec=pltpu.PrefetchScalarGridSpec(
            num_scalar_prefetch=1,
            grid=(2, n),
            in_specs=[
                pl.BlockSpec((w, rows), lambda i, j, m: (m[0] ^ i, 0)),
                pl.BlockSpec((rows, step), lambda i, j, m: (0, j)),
            ],
            out_specs=[first, first, second, second],
            scratch_shapes=[pltpu.VMEM((w, step), f32)],
        ),
        compiler_params=pltpu.CompilerParams(vmem_limit_bytes=40 << 20),
        cost_estimate=CHEAP,
        name="cross",
    )(at, hbm(x), hbm(g))


def spread_kernel(at, own, mate, *refs, width, other_x):
    out = refs[-1]
    step = out.shape[1]
    rows = pl.ds(pl.multiple_of(pl.program_id(0) * step, step), step)

    def put(core):
        cut = []
        for t in range(3):
            for n in range(2):
                for c in range(2):
                    part = (own, mate)[c ^ core][n ^ at[1], rows, :]
                    cut.append(part[:, t * width : (t + 1) * width])
        out[0] = jnp.concatenate(cut, axis=1).astype(f32)

    for core in range(2):

        @pl.when(at[2] == core)
        def _(core=core):
            put(core)


def spread(own, mate, at, used, other_x, carried=None):
    _, rows, cols = own.shape
    width = 4 * used
    cuts = 2 if rows % 32 == 0 else 1
    whole = pl.BlockSpec((2, rows, cols), lambda j, m: (0, 0, 0), pipeline_mode=pl.Buffered(1))
    more = () if carried is None else (carried,)
    return pl.pallas_call(
        functools.partial(spread_kernel, width=used // 3, other_x=other_x),
        out_shape=pltpu.HBM((2, rows, width), f32),
        grid_spec=pltpu.PrefetchScalarGridSpec(
            num_scalar_prefetch=1,
            grid=(cuts,),
            in_specs=[whole] * 2 + [pl.BlockSpec(memory_space=pl.ANY)] * len(more),
            out_specs=pl.BlockSpec((1, rows // cuts, width), lambda j, m: (m[0] ^ other_x, j, 0)),
        ),
        input_output_aliases={3: 0} if more else {},
        compiler_params=pltpu.CompilerParams(vmem_limit_bytes=40 << 20),
        cost_estimate=CHEAP,
        name="spread",
    )(at, own, mate, *more)


def back_kernel(shards, g_ref, w_ref, *refs):
    acc = jnp.dot(g_ref[...], w_ref[...], preferred_element_type=f32)
    if len(refs) == 2:
        acc = acc + refs[0][0].astype(f32)
    refs[-1][0] = acc.astype(bf16)


def back(grad, w, shards, rows, got=None):
    c, d = w.shape
    n = shards.shape[0]
    step = d
    out = pl.BlockSpec((1, rows, step), lambda j, i, f: (i, 0, j))
    in_specs = [
        pl.BlockSpec((rows, c), lambda j, i, f: (f[i], 0)),
        pl.BlockSpec((c, step), lambda j, i, f: (0, j)),
    ]
    args = [hbm(grad), hbm(w)]
    if got is not None:
        in_specs.append(pl.BlockSpec((1, rows, step), lambda j, i, f: (0, 0, j)))
        args.append(got)
    return pl.pallas_call(
        back_kernel,
        out_shape=pltpu.HBM((n, rows, d), bf16),
        grid_spec=pltpu.PrefetchScalarGridSpec(
            num_scalar_prefetch=1, grid=(d // step, n), in_specs=in_specs, out_specs=out
        ),
        compiler_params=pltpu.CompilerParams(vmem_limit_bytes=40 << 20),
        cost_estimate=CHEAP,
        name="back",
    )(shards, *args)


def finish_kernel(shard, g_ref, w_ref, core, near, x_ref, resid, gain, out, gain_out):
    grad = jnp.dot(g_ref[...], w_ref[...], preferred_element_type=f32)
    grad = grad + core[0].astype(f32) + near[0].astype(f32)
    x = x_ref[...].astype(f32)
    inverse = lax.rsqrt(jnp.mean(x * x, axis=-1, keepdims=True) + epsilon)
    part = jnp.sum(grad * x * inverse, axis=0, keepdims=True)

    @pl.when(pl.program_id(0) == 0)
    def _():
        gain_out[...] = jnp.zeros_like(gain_out)

    gain_out[...] += part
    scaled = grad * gain[...]
    out[...] = (
        resid[...]
        + inverse * scaled
        - x * (inverse * inverse * inverse) * jnp.mean(scaled * x, axis=-1, keepdims=True)
    ).astype(bf16)


def finish(grad, w, shard, core, near, x, resid, gain, tile=256):
    rows, d = x.shape
    c = w.shape[0]
    tiles = rows // tile
    row = lambda i, f: (i, 0)
    once = pl.Buffered(1)
    return pl.pallas_call(
        finish_kernel,
        out_shape=[pltpu.HBM((rows, d), bf16), jax.ShapeDtypeStruct((1, d), f32)],
        grid_spec=pltpu.PrefetchScalarGridSpec(
            num_scalar_prefetch=1,
            grid=(tiles,),
            in_specs=[
                pl.BlockSpec((tile, c), lambda i, f: (f[0] * tiles + i, 0)),
                pl.BlockSpec((c, d), lambda i, f: (0, 0), pipeline_mode=once),
                pl.BlockSpec((1, tile, d), lambda i, f: (1, i, 0)),
                pl.BlockSpec((1, tile, d), lambda i, f: (0, i, 0)),
                pl.BlockSpec((tile, d), row),
                pl.BlockSpec((tile, d), row),
                pl.BlockSpec((1, d), lambda i, f: (0, 0)),
            ],
            out_specs=[pl.BlockSpec((tile, d), row), pl.BlockSpec((1, d), lambda i, f: (0, 0))],
        ),
        compiler_params=pltpu.CompilerParams(vmem_limit_bytes=40 << 20),
        cost_estimate=CHEAP,
        name="finish",
    )(shard.reshape(1), hbm(grad), hbm(w), core, near, hbm(x), hbm(resid), gain)


def rms_inverse(values):
    return lax.rsqrt(jnp.mean(values * values, axis=-1, keepdims=True) + epsilon)


def norm_back(values, inverse, grad_scaled):
    return inverse * grad_scaled - values * (inverse * inverse * inverse) * jnp.mean(
        grad_scaled * values, axis=-1, keepdims=True
    )


def dot(left, right):
    return jnp.dot(left, right, preferred_element_type=f32)


def times_trans(left, right):
    return lax.dot_general(left, right, (((1,), (1,)), ((), ())), preferred_element_type=f32)


def trans_times(left, right):
    return lax.dot_general(left, right, (((0,), (0,)), ((), ())), preferred_element_type=f32)


def rows_at(array, start, count):
    return lax.dynamic_slice_in_dim(array, start, count, 0)


def put_rows(array, rows, start):
    return lax.dynamic_update_slice_in_dim(array, rows, start, 0)


def make_local(sizes):
    def pairs(target):
        found = []
        for gx in range(sizes["gx"]):
            for gc in range(sizes["gc"]):
                for z in range(4):
                    for w in range(sizes["wt"]):
                        goal = target(gx, gc, z, w)
                        if goal is not None and goal != (gx, gc, z, w):
                            found.append((place(gx, gc, z, w), place(*goal)))
        return found

    def place(gx, gc, z, w):
        return ((gx * sizes["gc"] + gc) * 4 + z) * sizes["wt"] + w

    def send(value, target):
        return lax.ppermute(value, AXES, pairs(target))

    def core_mate(gx, gc, z, w):
        return (gx, 1 - gc, z, w)

    def x_mate(gx, gc, z, w):
        return (1 - gx, gc, z, w)

    def near_mate(gx, gc, z, w):
        return (gx, gc, z ^ 1, w)

    def far_mate(gx, gc, z, w):
        return (gx, gc, z ^ 2, w)

    def cross_mate(gx, gc, z, w):
        return (gx, 1 - gc, z ^ 1, w)

    def wt_mate(gx, gc, z, w):
        return (gx, gc, z, 1 - w)

    def wt_x_mate(gx, gc, z, w):
        return (1 - gx, gc, z, 1 - w)

    def to_host(gx, gc, z, w):
        return (gx, 1 - (z & 1), 2 * gc + (z >> 1), w)

    def to_home(gx, gc, z, w):
        return (gx, z >> 1, 2 * (z & 1) + 1 - gc, w)

    def hop1(gx, gc, z, w):
        if gc == 0:
            return (gx, 0, z - 1, w) if z > 0 else None
        return (gx, 1, z + 1, w) if z < 3 else None

    def hop2(gx, gc, z, w):
        if gc == 0:
            return (gx, 0, z - 1, w) if z in (1, 2) else None
        return (gx, 1, z + 1, w) if z in (1, 2) else None

    def hop3(gx, gc, z, w):
        if gc == 0:
            return (gx, 0, z ^ 1, w) if z < 2 else None
        return (gx, 1, z ^ 1, w) if z > 1 else None

    def lane_share(gx, gc, z, w):
        return (gx, 1 - gc, z, w) if gc == z >> 1 else None

    def sum_all(value):
        for axis in ("gc", "wt", "near", "far", "gx"):
            step = 1
            while step < sizes[axis]:

                def mate(gx, gc, z, w, axis=axis, step=step):
                    at = dict(gx=gx, gc=gc, far=z >> 1, near=z & 1, wt=w)
                    at[axis] ^= step
                    return (at["gx"], at["gc"], 2 * at["far"] + at["near"], at["wt"])

                value = value + send(value, mate)
                step *= 2
        return value

    def local(
        tokens, segments, w_qkv, w_proj, w_in, w_out, gain_attn, gain_mlp, query_scale, cotangent
    ):
        gx, gc, host, near, wt = (lax.axis_index(axis) for axis in AXES)
        z = 2 * host + near
        mine = 2 * near + 1 - gc
        parts = 4
        nh = H // parts
        groups = 1
        rows = tokens.shape[1]
        group_len = segments.shape[1]
        wrows = w_qkv.shape[0]
        lane = gc == host
        pair = sizes["wt"] == 2

        def after(value, *others):
            return lax.optimization_barrier((value,) + others)[0]

        picked = pick(w_qkv, mine, parts, groups, nh)
        own = tokens[0]
        got1 = send(own, hop1)
        own_share = send(own, lane_share)
        seg_mate = send(segments, core_mate)
        got2 = send(got1, hop2)
        got1_share = send(got1, lane_share)
        end = jnp.where(gc == 0, z == 0, z == 3)
        if pair:
            wide_own = stretch(picked, groups, nh, 2)
            got1 = after(got1, wide_own)
            other_w = send(picked, wt_mate)
            wide_w = (wide_own, stretch(other_w, groups, nh, 10))
        else:
            flat_all = lax.all_gather(picked, "wt", axis=0, tiled=True)
            by_head = jnp.transpose(
                flat_all[:, : 3 * nh * HD].reshape(D, groups, 3, nh // groups, HD), (0, 2, 1, 3, 4)
            )
            wide_w = (
                jnp.pad(
                    by_head.reshape(D, 3 * nh, HD), ((0, 0), (0, 0), (0, LN - HD))
                ).reshape(D, -1),
            )
        got3 = send(jnp.where(end, own, got2), hop3)
        got2_share = send(got2, lane_share)
        way = 1 - 2 * host
        last = jnp.where(host == 0, jnp.where(z == 0, 3, 0), jnp.where(z == 3, 0, 3))
        places = (z, z + way, z + 2 * way, last)

        half_rows = wrows // 2
        half_w = jnp.stack([rows_at(w, gc * half_rows, half_rows) for w in (w_proj, w_in, w_out)])
        if pair:
            half_w = send(after(half_w, other_w), wt_mate)
        else:
            half_w = lax.all_gather(half_w, "wt", axis=0, tiled=False)

        dim_scale = scale_base / math.sqrt(HD) * jax.nn.softplus(query_scale)
        lane_scale = jnp.tile(jnp.pad(dim_scale * log2e, (0, LN - HD)), nh)[None]
        ones = jnp.tile(
            ((jnp.arange(LN) >= HD) & (jnp.arange(LN) < HD + 3)).astype(f32), 2 * nh
        )[None]
        seg_row = jnp.where(lane, segments, seg_mate)[0]
        fixed = (lane, mine, wt, gain_attn[None], wide_w, lane_scale, ones, group_len)
        carried = project(((own, own_share), (got1, got1_share)), places[:2], *fixed)
        got3_share = send(after(got3, carried[0]), lane_share)
        all_normed, queries, keyval, inputs = project(
            ((got2, got2_share), (got3, got3_share)), places[2:], *fixed, carried=carried
        )
        grad_mlp = send(after(cotangent[0], got3_share), to_host)

        att, att_float, q_aug = attn_fwd(queries, keyval, seg_row, nh)
        att, half_w, _ = lax.optimization_barrier((att, half_w, grad_mlp))

        trades = (core_mate, near_mate, cross_mate)
        att_pieces = [rows_at(att, (mine ^ j) * rows, rows) for j in range(parts)]
        att_pieces = [att_pieces[0]] + [send(att_pieces[j + 1], trades[j]) for j in range(3)]
        half_mate = send(half_w, core_mate)
        if pair:
            w_trans = order(after(picked, att), other_w, wt)
        else:
            w_trans = flat_all.T
        normed_trans = transpose(after(all_normed, w_trans))
        if pair:
            weights = (w_proj, w_in, w_out, half_w, half_mate)
            starts = (wt * wrows, (1 - wt) * wrows + gc * half_rows, (1 - wt) * wrows + (1 - gc) * half_rows)
        else:
            one = gc == 0
            tail_w = jnp.stack(
                [jnp.where(one, half_w, half_mate), jnp.where(one, half_mate, half_w)], axis=1
            )
            weights = (jnp.transpose(tail_w, (2, 0, 1, 3, 4)).reshape(3, D, D),)
            starts = ()
        (
            layer_out,
            left,
            right,
            grad_resid,
            *pieces,
            grad_gain_mlp,
        ) = tail(
            jnp.stack([mine, *starts]), att_pieces, after(inputs, normed_trans), grad_mlp, weights, gain_mlp[None]
        )
        pieces = [pieces[0]] + [send(pieces[j + 1], trades[j]) for j in range(3)]

        shared = share(after(left, pieces[1]), right, 1 - gc)
        from_core = send(shared, core_mate)
        pieces[2:] = [after(piece, shared) for piece in pieces[2:]]
        home_out = send(after(layer_out, *pieces[1:]), to_home)
        late_gain = tick(after(gain_attn.reshape(-1, LN), *pieces[1:]))
        summed = share(left, right, gc, after(from_core, late_gain))
        kept = lax.all_to_all(summed, ("wt", "gx", "near"), 0, 0, tiled=True)

        scale_row = jnp.tile(dim_scale, nh // groups)[None]

        def backward(group, *others):
            first, *rest = pieces
            return attn_bwd(
                q_aug,
                keyval,
                (after(first, summed, *others), *rest),
                att_float,
                mine,
                seg_row,
                scale_row,
                nh,
                group,
                groups,
            )

        def by_rows(grad):
            if pair:
                own, *rest = cross(normed_trans, grad, jnp.stack([wt, gx]))
                got = [send(part, mate) for part, mate in zip(rest, (x_mate, wt_mate, wt_x_mate))]
                return [part[None] for part in (own, *got)]
            part = dot(normed_trans, grad).astype(bf16)
            sources = sizes["wt"] * 2
            got = lax.all_to_all(part, ("wt", "gx"), 0, 0, tiled=True)
            return [got.reshape(sources, D // sources, -1)]

        grad_project, grad_lanes = backward(0)
        layer_out = after(home_out, grad_project)

        last_step = [layer_out]

        def turn(value):
            return after(value, *last_step)

        def done(value):
            last_step[0] = value
            return value

        sources = sizes["wt"] * 4
        to_core = done(back(turn(grad_project), w_trans, jnp.stack([mine ^ 3, mine ^ 1]), rows))
        from_core = send(to_core, core_mate)
        by_place = by_rows(turn(grad_project))
        done(by_place[0])
        to_near = done(back(grad_project, w_trans, (mine ^ 2).reshape(1), rows, turn(from_core)))
        from_near = send(to_near, near_mate)
        t1 = done(total([[turn(kept).reshape(sources, D // sources, -1)]]))
        t1_far = send(t1, far_mate)
        layer_out = done(copy(turn(layer_out)))
        by_place[0] = turn(by_place[0])
        q1 = done(total([by_place]))
        q1_far = send(q1, far_mate)
        t2 = done(add(turn(t1), t1_far))
        t2_near = send(t2, near_mate)
        grad_tokens, grad_gain_attn = finish(
            grad_project,
            w_trans,
            mine,
            from_core,
            turn(from_near),
            inputs,
            grad_resid,
            late_gain.reshape(1, -1),
        )
        done(grad_tokens)
        grad_query_scale = (
            grad_lanes[0, :HD]
            / (dim_scale * log2e)
            * (scale_base / math.sqrt(HD))
            * jax.nn.sigmoid(query_scale)
        )
        small = jnp.concatenate(
            [grad_gain_attn[0], grad_gain_mlp[0], jnp.pad(grad_query_scale, (0, LN - HD))]
        ).reshape(-1, LN)
        q2 = done(add(turn(q1), q1_far))
        q2_near = send(q2, near_mate)
        t4 = done(pair_up(turn(t2), t2_near))
        t4_x = send(t4, x_mate)
        t4_core = send(t4, core_mate)
        home_grad = send(turn(grad_tokens), to_home)
        q4 = done(pair_up(turn(q2), q2_near))
        q4_x = send(q4, x_mate)
        q4_core = send(q4, core_mate)
        t4_x = done(turn(t4_x))
        t4_cross = send(t4_x, core_mate)
        used = 3 * nh * HD
        spread_at = jnp.stack([gx, near, 1 - gc])
        totals = place_tail((turn(t4), t4_x, t4_core, t4_cross), jnp.stack([gx, near, gc]))
        done(totals[0])
        q4_core = done(turn(q4_core))
        small = done(sum_all(turn(small))).reshape(-1)
        grad_tokens = done(copy(turn(home_grad)))
        q4_x = done(turn(q4_x))
        q4_cross = send(q4_x, core_mate)
        total_qkv = done(spread(turn(q4), q4_core, spread_at, used, 0))
        total_qkv = spread(turn(q4_x), q4_cross, spread_at, used, 1, total_qkv).reshape(wrows, 3 * D)
        return (
            layer_out[None],
            grad_tokens[None],
            total_qkv,
            *totals,
            small[:D],
            small[D : 2 * D],
            small[2 * D : 2 * D + HD],
        )

    return local


def solution(mesh):
    groups, parts, wt = (mesh.shape[axis] for axis in ("grp", "ctx", "wt"))
    inner = Mesh(mesh.devices.reshape(groups // 2, 2, parts // 2, 2, wt), AXES)
    sizes = dict(inner.shape)
    split = P(("gx", "gc", "wt"), ("far", "near"), None)
    weight = P("wt", None)
    return jax.shard_map(
        make_local(sizes),
        mesh=inner,
        in_specs=(
            split,
            P(("gx", "gc", "wt"), None),
            weight,
            weight,
            weight,
            weight,
            P(),
            P(),
            P(),
            split,
        ),
        out_specs=(split, split, weight, weight, weight, weight, P(), P(), P()),
        check_vma=False,
    )
```

```python
import functools
import math

import jax
import jax.numpy as jnp
from jax import lax
from jax.experimental import pallas as pl
from jax.experimental.pallas import tpu as pltpu
from jax.sharding import Mesh
from jax.sharding import PartitionSpec as P

D = 1280
H = 16
HD = 80
LN = 128
epsilon = 1e-06
scale_base = 1.442695041
log2e = 1.4426950408889634
NEG = -1e30
def cost(us):
    return pl.CostEstimate(flops=int(us * 1_000_000_000), transcendentals=0, bytes_accessed=1000)


CHEAP = cost(0.001)
f32 = jnp.float32
bf16 = jnp.bfloat16
AXES = ("gx", "gc", "far", "near", "wt")


def hbm(x):
    return pltpu.with_memory_space_constraint(x, pltpu.HBM)


def block_flags(seg_row, bq, bk):
    n = seg_row.shape[0]
    q = seg_row.reshape(n // bq, bq)
    k = seg_row.reshape(n // bk, bk)
    qf, ql = q[:, 0][:, None], q[:, -1][:, None]
    kf, kl = k[:, 0][None], k[:, -1][None]
    qs = jnp.arange(n // bq, dtype=jnp.int32)[:, None] * bq
    ks = jnp.arange(n // bk, dtype=jnp.int32)[None] * bk
    below = ks + bk - 1 <= qs
    skip = (ks > qs + bq - 1) | ((kf > 0) & (kl < qf))
    same = (qf == ql) & (kl == ql) & ((kf == kl) | ((kf == 0) & (kl == 1)))
    full = below & ((kl == 0) | same)
    flags = jnp.where(skip, 0, jnp.where(full, 1, 2))
    if bq == bk:
        flags = jnp.where(qs == ks, 3, flags)
    return flags.astype(jnp.int32).reshape(-1)


def put_split(base, col, lanes):
    hi = col.astype(bf16).astype(f32)
    rest = col - hi
    mid = rest.astype(bf16).astype(f32)
    out = jnp.where(lanes == HD, hi, base)
    out = jnp.where(lanes == HD + 1, mid, out)
    return jnp.where(lanes == HD + 2, rest - mid, out).astype(bf16)


def fwd_kernel(flags, q_ref, kv, segc, segr, att, of, qaug, m_s, acc_s, *, nh, bq, bk, nk):
    qi = pl.program_id(0)
    count = (qi * bq + bq + bk - 1) // bk
    nt = (((1,), (1,)), ((), ()))
    acc_s[...] = jnp.zeros_like(acc_s)
    m_s[...] = jnp.zeros_like(m_s)

    def mask(ko, q0=0, qn=bq, kn=bk):
        qpos = qi * bq + q0 + lax.broadcasted_iota(jnp.int32, (qn, kn), 0)
        kpos = ko + lax.broadcasted_iota(jnp.int32, (qn, kn), 1)
        ks = segr[:, pl.ds(ko, kn)]
        return (kpos <= qpos) & ((ks == 0) | (ks == segc[q0 : q0 + qn, :]))

    def step(kb, masked, q0=0, qn=bq, kn=bk):
        ko = pl.multiple_of(kb * bk, bk)
        if masked:
            allowed = mask(ko, q0, qn, kn)
        rows = slice(q0, q0 + qn)
        for h in range(nh):
            k = kv[pl.ds(ko, kn), h * LN : (h + 1) * LN]
            v = kv[pl.ds(ko, kn), (nh + h) * LN : (nh + h + 1) * LN]
            q = q_ref[rows, h * LN : (h + 1) * LN]
            p = jnp.exp2(lax.dot_general(q, k, nt, preferred_element_type=f32))
            if masked:
                p = jnp.where(allowed, p, 0.0)
            acc_s[h, rows, :] += jnp.dot(p.astype(bf16), v, preferred_element_type=f32)

    def body(kb, carry):
        flag = flags[qi * nk + kb]

        @pl.when(flag == 1)
        def _():
            step(kb, False)

        @pl.when(flag >= 2)
        def _():
            step(kb, True)

        return carry

    lax.fori_loop(0, count, body, 0)
    bad = jnp.zeros((bq, 1), f32)
    for h in range(nh):
        total = acc_s[h][:, HD : HD + 1]
        bad = jnp.maximum(bad, jnp.where((total > 2.0**-60) & (total < 2.0**60), 0.0, 1.0))

    @pl.when(jnp.max(bad) > 0.0)
    def _():
        def head(h, carry):
            kc = pl.ds(pl.multiple_of(h * LN, LN), LN)
            vc = pl.ds(pl.multiple_of((nh + h) * LN, LN), LN)
            m_s[h] = jnp.full((bq, LN), NEG, f32)
            acc_s[h] = jnp.zeros((bq, LN), f32)

            def inner(kb, carry):
                @pl.when(flags[qi * nk + kb] > 0)
                def _():
                    ko = pl.multiple_of(kb * bk, bk)
                    s = lax.dot_general(
                        q_ref[:, kc], kv[pl.ds(ko, bk), kc], nt, preferred_element_type=f32
                    )
                    s = jnp.where(mask(ko), s, NEG)
                    old = m_s[h]
                    new = jnp.maximum(old, jnp.max(s, axis=1, keepdims=True))
                    p = jnp.exp2(s - new[:, :1]).astype(bf16)
                    m_s[h] = new
                    acc_s[h] = acc_s[h] * jnp.exp2(old - new) + jnp.dot(
                        p, kv[pl.ds(ko, bk), vc], preferred_element_type=f32
                    )

                return carry

            lax.fori_loop(0, count, inner, 0)
            return carry

        lax.fori_loop(0, nh, head, 0)

    lanes = lax.broadcasted_iota(jnp.int32, (bq, LN), 1)
    outs = []
    for h in range(nh):
        acc = acc_s[h]
        total = acc[:, HD : HD + 1]
        out = acc * (1.0 / total)
        of[:, h * LN : (h + 1) * LN] = jnp.where(lanes < HD, out, 0.0).astype(bf16)
        outs.append(out[:, :HD])
        lse = m_s[h][:, :1] + jnp.log2(total)
        qaug[:, h * LN : (h + 1) * LN] = put_split(
            q_ref[:, h * LN : (h + 1) * LN].astype(f32), -lse, lanes
        )
    att[...] = jnp.concatenate(outs, axis=1).astype(bf16)


def attn_fwd(q, kv, seg_row, nh, bq=512, bk=512):
    n = q.shape[0]
    w = nh * LN
    spec = pltpu.PrefetchScalarGridSpec(
        num_scalar_prefetch=1,
        grid=(n // bq,),
        in_specs=[
            pl.BlockSpec((bq, w), lambda i, f: (i, 0)),
            pl.BlockSpec((n, 2 * w), lambda i, f: (0, 0)),
            pl.BlockSpec((bq, 1), lambda i, f: (i, 0)),
            pl.BlockSpec((1, n), lambda i, f: (0, 0)),
        ],
        out_specs=[
            pl.BlockSpec((bq, nh * HD), lambda i, f: (i, 0)),
            pl.BlockSpec((bq, w), lambda i, f: (i, 0)),
            pl.BlockSpec((bq, w), lambda i, f: (i, 0)),
        ],
        scratch_shapes=[pltpu.VMEM((nh, bq, LN), f32), pltpu.VMEM((nh, bq, LN), f32)],
    )
    return pl.pallas_call(
        functools.partial(fwd_kernel, nh=nh, bq=bq, bk=bk, nk=n // bk),
        out_shape=[
            pltpu.HBM((n, nh * HD), bf16),
            pltpu.HBM((n, w), bf16),
            pltpu.HBM((n, w), bf16),
        ],
        grid_spec=spec,
        compiler_params=pltpu.CompilerParams(vmem_limit_bytes=40 << 20),
        cost_estimate=cost(0.01),
        name="attn_fwd",
    )(block_flags(seg_row, bq, bk), hbm(q), hbm(kv), seg_row[:, None], seg_row[None])


def bwd_kernel(
    flags, mine, qa, kk, vv, do0, do1, do2, do3, of, segc, segr, scale, dqkv, gscale, doa_s, dq_s, dk_s, dv_s, *, first, nh, bq, bk, n
):
    nk = n // bk
    nq = n // bq
    kb = pl.program_id(0)
    part = n // 4
    step_rows = 256 if part % 256 == 0 else part
    lanes = lax.broadcasted_iota(jnp.int32, (step_rows, LN), 1)

    @pl.when(kb == 0)
    def _():
        dq_s[...] = jnp.zeros_like(dq_s)
        for j, piece in enumerate((do0, do1, do2, do3)):
            start = (mine[0] ^ j) * part
            for i in range(part // step_rows):
                d = piece[i * step_rows : (i + 1) * step_rows, :].astype(f32)
                r = pl.ds(pl.multiple_of(start + i * step_rows, step_rows), step_rows)
                for h in range(nh):
                    at = (first + h) * HD
                    dh = jnp.concatenate(
                        [d[:, at : at + HD], jnp.zeros((step_rows, LN - HD), f32)], axis=1
                    )
                    c = slice(h * LN, (h + 1) * LN)
                    delta = jnp.sum(dh * of[r, c].astype(f32), axis=1, keepdims=True)
                    doa_s[r, c] = put_split(dh, -delta, lanes)

    dk_s[...] = jnp.zeros_like(dk_s)
    dv_s[...] = jnp.zeros_like(dv_s)
    ko = kb * bk
    nt = (((1,), (1,)), ((), ()))
    tn = (((0,), (0,)), ((), ()))

    def step(qi, masked, q0=0, qn=bq, kn=bk):
        qo = pl.multiple_of(qi * bq + q0, qn)
        rows = slice(0, kn)
        if masked:
            kpos = ko + lax.broadcasted_iota(jnp.int32, (kn, qn), 0)
            qpos = qo + lax.broadcasted_iota(jnp.int32, (kn, qn), 1)
            ks = segc[rows, :]
            allowed = (kpos <= qpos) & ((ks == 0) | (ks == segr[:, pl.ds(qo, qn)]))
        for h in range(nh):
            c = slice(h * LN, (h + 1) * LN)
            q = qa[pl.ds(qo, qn), c]
            k = kk[rows, c]
            d = doa_s[pl.ds(qo, qn), c]
            p = jnp.exp2(lax.dot_general(k, q, nt, preferred_element_type=f32))
            if masked:
                p = jnp.where(allowed, p, 0.0)
            ds = (p * lax.dot_general(vv[rows, c], d, nt, preferred_element_type=f32)).astype(bf16)
            dv_s[h, rows, :] += jnp.dot(p.astype(bf16), d, preferred_element_type=f32)
            dk_s[h, rows, :] += jnp.dot(ds, q, preferred_element_type=f32)
            dq_s[h, pl.ds(qo, qn), :] += lax.dot_general(ds, k, tn, preferred_element_type=f32)

    def body(qi, carry):
        flag = flags[qi * nk + kb]

        @pl.when(flag == 1)
        def _():
            step(qi, False)

        @pl.when(flag == 2)
        def _():
            step(qi, True)

        if bq == bk:

            @pl.when(flag == 3)
            def _():
                step(qi, True, 0, bq // 2, bk // 2)
                step(qi, True, bq // 2, bq // 2, bk)

        return carry

    lax.fori_loop(ko // bq, nq, body, 0)
    r = pl.multiple_of(ko, bk)
    ln2 = math.log(2.0)
    gap = dqkv.shape[1] - 3 * nh * HD
    dqkv[pl.ds(r, bk), nh * HD :] = jnp.concatenate(
        [dk_s[h][:, :HD] * ln2 for h in range(nh)]
        + [dv_s[h][:, :HD] for h in range(nh)]
        + [jnp.zeros((bk, gap), f32)],
        axis=1,
    ).astype(bf16)

    @pl.when(kb == nk - 1)
    def _():
        total = jnp.zeros((1, LN), f32)
        for i in range(nq):
            rows = slice(i * bq, (i + 1) * bq)
            for h in range(nh):
                total = total + jnp.sum(
                    dq_s[h, rows, :] * qa[rows, h * LN : (h + 1) * LN].astype(f32), axis=0, keepdims=True
                )
            grads = jnp.concatenate([dq_s[h, rows, :][:, :HD] for h in range(nh)], axis=1)
            dqkv[rows, 0 : nh * HD] = (grads * scale[...]).astype(bf16)
        gscale[...] = jnp.broadcast_to(total, gscale.shape)


def attn_bwd(qa, kv, pieces, of, mine, seg_row, scale, heads, group, groups, bq=512, bk=512):
    n = qa.shape[0]
    nh = heads // groups
    w = nh * LN
    once = pl.Buffered(1)
    spec = pltpu.PrefetchScalarGridSpec(
        num_scalar_prefetch=2,
        grid=(n // bk,),
        in_specs=[
            pl.BlockSpec((n, w), lambda i, f, m: (0, group), pipeline_mode=once),
            pl.BlockSpec((bk, w), lambda i, f, m: (i, group)),
            pl.BlockSpec((bk, w), lambda i, f, m: (i, groups + group)),
            *[pl.BlockSpec((n // 4, heads * HD), lambda i, f, m: (0, 0), pipeline_mode=once)] * 4,
            pl.BlockSpec((n, w), lambda i, f, m: (0, group), pipeline_mode=once),
            pl.BlockSpec((bk, 1), lambda i, f, m: (i, 0)),
            pl.BlockSpec((1, n), lambda i, f, m: (0, 0)),
            pl.BlockSpec((1, nh * HD), lambda i, f, m: (0, 0)),
        ],
        out_specs=[
            pl.BlockSpec((n, lanes_up(3 * nh * HD)), lambda i, f, m: (0, 0)),
            pl.BlockSpec((8, LN), lambda i, f, m: (0, 0)),
        ],
        scratch_shapes=[
            pltpu.VMEM((n, w), bf16),
            pltpu.VMEM((nh, n, LN), f32),
            pltpu.VMEM((nh, bk, LN), f32),
            pltpu.VMEM((nh, bk, LN), f32),
        ],
    )
    return pl.pallas_call(
        functools.partial(bwd_kernel, first=group * nh, nh=nh, bq=bq, bk=bk, n=n),
        out_shape=[
            pltpu.HBM((n, lanes_up(3 * nh * HD)), bf16),
            pltpu.HBM((8, LN), f32),
        ],
        grid_spec=spec,
        compiler_params=pltpu.CompilerParams(vmem_limit_bytes=48 << 20),
        cost_estimate=cost(300 if group == 0 else 0.001),
        name="attn_bwd",
    )(block_flags(seg_row, bq, bk), mine.reshape(1), hbm(qa), hbm(kv), hbm(kv), *pieces, hbm(of), seg_row[:, None], seg_row[None], scale)


def quarter_columns(place, parts, groups, nh):
    width = nh // groups * HD
    return [
        (t * D + place * nh * HD + g * width, width) for g in range(groups) for t in range(3)
    ]


def pick_kernel(mine, w_ref, out, *, parts, groups, nh):
    for i in range(parts):

        @pl.when(mine[0] == i)
        def _(i=i):
            cut = [w_ref[:, a : a + width] for a, width in quarter_columns(i, parts, groups, nh)]
            used = sum(x.shape[1] for x in cut)
            pad = jnp.zeros((cut[0].shape[0], out.shape[1] - used), out.dtype)
            out[...] = jnp.concatenate(cut + [pad], axis=1)


def lanes_up(n):
    return -(-n // LN) * LN


def pick(w, mine, parts, groups, nh):
    rows = w.shape[0]
    step = 160 if rows % 160 == 0 else rows
    return pl.pallas_call(
        functools.partial(pick_kernel, parts=parts, groups=groups, nh=nh),
        out_shape=pltpu.HBM((rows, lanes_up(3 * nh * HD)), w.dtype),
        grid_spec=pltpu.PrefetchScalarGridSpec(
            num_scalar_prefetch=1,
            grid=(rows // step,),
            in_specs=[pl.BlockSpec((step, 3 * D), lambda i, m: (i, 0))],
            out_specs=pl.BlockSpec((step, lanes_up(3 * nh * HD)), lambda i, m: (i, 0)),
        ),
        cost_estimate=cost(5),
        name="pick",
    )(mine.reshape(1), hbm(w))


def stretch_kernel(x_ref, out, *, groups, nh):
    value = x_ref[...]
    each = 3 * nh * HD // groups
    zero = jnp.zeros((value.shape[0], LN - HD), value.dtype)
    per = nh // groups
    wide = []
    for t in range(3):
        for h in range(nh):
            at = (h // per) * each + t * per * HD + (h % per) * HD
            wide += [value[:, at : at + HD], zero]
    out[...] = jnp.concatenate(wide, axis=1)


def stretch(x, groups, nh, us):
    rows, width = x.shape
    step = 160
    return pl.pallas_call(
        functools.partial(stretch_kernel, groups=groups, nh=nh),
        out_shape=pltpu.HBM((rows, 3 * nh * LN), x.dtype),
        grid=(rows // step,),
        in_specs=[pl.BlockSpec((step, width), lambda i: (i, 0))],
        out_specs=pl.BlockSpec((step, 3 * nh * LN), lambda i: (i, 0)),
        cost_estimate=cost(us),
        name="stretch",
    )(hbm(x))


def order_kernel(own_first, a_ref, b_ref, out):
    half = pl.program_id(0)

    @pl.when(half == 0)
    def _():
        out[...] = a_ref[...].T

    @pl.when(half == 1)
    def _():
        out[...] = b_ref[...].T


def order(own, other, own_at):
    rows, width = own.shape
    step = 256
    return pl.pallas_call(
        order_kernel,
        out_shape=pltpu.HBM((width, 2 * rows), own.dtype),
        grid_spec=pltpu.PrefetchScalarGridSpec(
            num_scalar_prefetch=1,
            grid=(2, width // step),
            in_specs=[
                pl.BlockSpec((rows, step), lambda i, j, m: (0, j * (1 - i))),
                pl.BlockSpec((rows, step), lambda i, j, m: (0, j * i)),
            ],
            out_specs=pl.BlockSpec((step, rows), lambda i, j, m: (j, i ^ m[0])),
        ),
        cost_estimate=cost(200.0),
        name="order",
    )(own_at.reshape(1), hbm(own), hbm(other))


def transpose_kernel(x_ref, out):
    out[...] = x_ref[...].T


def transpose(x):
    rows, cols = x.shape
    step = 256
    return pl.pallas_call(
        transpose_kernel,
        out_shape=pltpu.HBM((cols, rows), x.dtype),
        grid=(rows // step,),
        in_specs=[pl.BlockSpec((step, cols), lambda i: (i, 0))],
        out_specs=pl.BlockSpec((cols, step), lambda i: (0, i)),
        cost_estimate=CHEAP,
        name="transpose",
    )(hbm(x))


def project_kernel(info, *refs, count, halves, width, fresh):
    pairs = refs[: 2 * count]
    gain = refs[2 * count]
    weights = refs[2 * count + 1 : 2 * count + 1 + halves]
    scale, ones = refs[2 * count + 1 + halves : 2 * count + 3 + halves]
    normed_ref, q_ref, kv_ref, mine_ref, w = refs[-5:]
    j, tile = pl.program_id(0), pl.program_id(1)
    step = normed_ref.shape[0]

    @pl.when((j == 0) & (tile == 0))
    def _():
        for i, ref in enumerate(weights):
            h = ref.shape[0]
            start = (info[count + 2] ^ i) * h if halves == 2 else 0
            w[pl.ds(pl.multiple_of(start, 16), h), :] = ref[...]
        if not fresh:
            mine_ref[...] = refs[2 * count + 3 + halves][...]

    def work(x_ref):
        value = x_ref[...]
        x = value.astype(f32)
        inverse = lax.rsqrt(jnp.mean(x * x, axis=-1, keepdims=True) + epsilon)
        normed = (x * inverse * gain[...]).astype(bf16)
        normed_ref[...] = normed
        q_ref[...] = (
            jnp.dot(normed, w[:, :width], preferred_element_type=f32) * scale[...]
        ).astype(bf16)
        kv_ref[...] = (
            jnp.dot(normed, w[:, width:], preferred_element_type=f32) + ones[...]
        ).astype(bf16)

        @pl.when(info[count + 1] == info[j])
        def _():
            mine_ref[pl.ds(pl.multiple_of(tile * step, step), step), :] = value

    for i in range(count):
        for lane in range(2):

            @pl.when((j == i) & (info[count] == lane))
            def _(i=i, lane=lane):
                work(pairs[2 * i + 1 - lane])


def project(pairs, places, lane, mine, wt, gain, weights, scale, ones, group_len, carried=None):
    count = len(pairs)
    rows, d = pairs[0][0].shape
    width = scale.shape[1]
    step = 256
    tiles = rows // step
    full = lambda j, t, f: (0, 0)
    at = lambda j, t, f: (f[j] * tiles + t, 0)
    once = pl.Buffered(1)
    info = jnp.stack(list(places) + [lane.astype(jnp.int32), mine, wt])
    args = [x for pair in pairs for x in pair] + [gain, *map(hbm, weights), scale, ones]
    in_specs = [
        pl.BlockSpec(
            (step, d),
            lambda j, t, f, i=i: (jnp.where(j == i, t, jnp.where(j > i, tiles - 1, 0)), 0),
        )
        for i in range(count)
        for _ in range(2)
    ]
    in_specs += [pl.BlockSpec((1, d), full, pipeline_mode=once)]
    in_specs += [pl.BlockSpec(w.shape, full, pipeline_mode=once) for w in weights]
    in_specs += [
        pl.BlockSpec((1, width), full, pipeline_mode=once),
        pl.BlockSpec((1, 2 * width), full, pipeline_mode=once),
    ]
    aliases = {}
    if carried is not None:
        base = len(args) + 2
        args += [hbm(x) for x in (carried[3], *carried[:3])]
        in_specs += [pl.BlockSpec((rows, d), full, pipeline_mode=once)]
        in_specs += [pl.BlockSpec(memory_space=pl.ANY)] * 3
        aliases = {base: 0, base + 1: 1, base + 2: 2}
    return pl.pallas_call(
        functools.partial(
            project_kernel, count=count, halves=len(weights), width=width, fresh=carried is None
        ),
        out_shape=[
            pltpu.HBM((group_len, d), bf16),
            pltpu.HBM((group_len, width), bf16),
            pltpu.HBM((group_len, 2 * width), bf16),
            pltpu.HBM((rows, d), bf16),
        ],
        grid_spec=pltpu.PrefetchScalarGridSpec(
            num_scalar_prefetch=1,
            grid=(count, tiles),
            in_specs=in_specs,
            out_specs=[
                pl.BlockSpec((step, d), at),
                pl.BlockSpec((step, width), at),
                pl.BlockSpec((step, 2 * width), at),
                pl.BlockSpec((rows, d), full),
            ],
            scratch_shapes=[pltpu.VMEM((d, 3 * width), bf16)],
        ),
        input_output_aliases=aliases,
        compiler_params=pltpu.CompilerParams(vmem_limit_bytes=48 << 20),
        cost_estimate=cost(15),
        name="project",
    )(info, *args)


def tail_body(at, p0, p1, p2, p3, x_ref, g_ref, w_s, gain, outs, need):
    lo_ref, left_ref, right_ref, gr_ref, c0, c1, c2, c3, gg_ref = outs
    att_ref, nm_ref, act_ref = (left_ref.at[i] for i in range(3))
    gp_ref, gh_ref = (right_ref.at[i] for i in range(2))
    right_ref[2] = g_ref[...]
    mine = at[0]
    pieces = (p0, p1, p2, p3)
    cols = p0.shape[1]
    nt = (((1,), (1,)), ((), ()))
    for i in range(4):

        @pl.when(mine == i)
        def _(i=i):
            att_ref[...] = jnp.concatenate([pieces[i ^ k][...] for k in range(4)], axis=1)

    need(0)
    resid = x_ref[...].astype(f32) + jnp.dot(att_ref[...], w_s[0], preferred_element_type=f32)
    inverse = lax.rsqrt(jnp.mean(resid * resid, axis=-1, keepdims=True) + epsilon)
    normed = (resid * inverse * gain[...]).astype(bf16)
    nm_ref[...] = normed
    need(1)
    hidden = jnp.dot(normed, w_s[1], preferred_element_type=f32)
    sig = 1.0 / (1.0 + jnp.exp(-hidden))
    active = (hidden * sig).astype(bf16)
    act_ref[...] = active
    need(2)
    lo_ref[...] = (resid + jnp.dot(active, w_s[2], preferred_element_type=f32)).astype(bf16)
    grad_active = lax.dot_general(g_ref[...], w_s[2], nt, preferred_element_type=f32)
    grad_hidden = (grad_active * sig * (1.0 + hidden * (1.0 - sig))).astype(bf16)
    gh_ref[...] = grad_hidden
    grad_normed = lax.dot_general(grad_hidden, w_s[1], nt, preferred_element_type=f32)
    gg_ref[...] += jnp.sum(grad_normed * resid * inverse, axis=0, keepdims=True)
    scaled = grad_normed * gain[...]
    grad_resid = (
        g_ref[...].astype(f32)
        + inverse * scaled
        - resid * (inverse * inverse * inverse) * jnp.mean(scaled * resid, axis=-1, keepdims=True)
    )
    gr_ref[...] = grad_resid
    grad_proj = grad_resid.astype(bf16)
    gp_ref[...] = grad_proj
    grad_att = lax.dot_general(grad_proj, w_s[0], nt, preferred_element_type=f32).astype(bf16)
    for i in range(4):

        @pl.when(mine == i)
        def _(i=i):
            for j, out in enumerate((c0, c1, c2, c3)):
                out[...] = grad_att[:, (i ^ j) * cols : ((i ^ j) + 1) * cols]


def tail_kernel(at, p0, p1, p2, p3, x_ref, g_ref, own0, own1, own2, half, other, gain, *refs, rows, hrows):
    w_s, sems = refs[-2:]
    outs = refs[:-2]

    def copies(i):
        parts = (((own0, own1, own2)[i], at[1], rows), (half.at[i], at[2], hrows), (other.at[i], at[3], hrows))
        return [
            pltpu.make_async_copy(
                part, w_s.at[i, pl.ds(pl.multiple_of(start, 16), n), :], sems.at[3 * i + k]
            )
            for k, (part, start, n) in enumerate(parts)
        ]

    @pl.when(pl.program_id(0) == 0)
    def _():
        outs[-1][...] = jnp.zeros_like(outs[-1])
        for i in range(3):
            for c in copies(i):
                c.start()

    def need(i):
        @pl.when(pl.program_id(0) == 0)
        def _():
            for c in copies(i):
                c.wait()

    tail_body(at, p0, p1, p2, p3, x_ref, g_ref, w_s, gain, outs, need)


def whole_tail_kernel(at, p0, p1, p2, p3, x_ref, g_ref, w, gain, *outs):
    @pl.when(pl.program_id(0) == 0)
    def _():
        outs[-1][...] = jnp.zeros_like(outs[-1])

    tail_body(at, p0, p1, p2, p3, x_ref, g_ref, w, gain, outs, lambda i: None)


def tail(at, pieces, x, g, weights, gain, tile=256):
    rows, d = x.shape
    cols = pieces[0].shape[1]
    row = lambda i, m: (i, 0)
    once = pl.Buffered(1)
    whole = lambda *shape: pl.BlockSpec(shape, lambda i, m: (0,) * len(shape), pipeline_mode=once)
    wide = pl.BlockSpec((tile, d), row)
    slim = pl.BlockSpec((tile, cols), row)
    if len(weights) == 5:
        body = functools.partial(tail_kernel, rows=weights[0].shape[0], hrows=weights[3].shape[1])
        scratch = [pltpu.VMEM((3, d, d), bf16), pltpu.SemaphoreType.DMA((9,))]
        weight_specs = [pl.BlockSpec(memory_space=pl.ANY)] * 5
    else:
        body = whole_tail_kernel
        scratch = []
        weight_specs = [whole(*w.shape) for w in weights]
    return pl.pallas_call(
        body,
        out_shape=[pltpu.HBM((rows, d), bf16)]
        + [pltpu.HBM((3, rows, d), bf16)] * 2
        + [pltpu.HBM((rows, d), f32)]
        + [pltpu.HBM((rows, cols), bf16)] * 4
        + [pltpu.HBM((1, d), f32)],
        grid_spec=pltpu.PrefetchScalarGridSpec(
            num_scalar_prefetch=1,
            grid=(rows // tile,),
            in_specs=[slim] * 4 + [wide] * 2 + weight_specs + [whole(1, d)],
            out_specs=[wide]
            + [pl.BlockSpec((3, tile, d), lambda i, m: (0, i, 0))] * 2
            + [wide]
            + [slim] * 4
            + [pl.BlockSpec((1, d), lambda i, m: (0, 0))],
            scratch_shapes=scratch,
        ),
        compiler_params=pltpu.CompilerParams(vmem_limit_bytes=52 << 20),
        cost_estimate=cost(0.01),
        name="tail",
    )(at, *pieces, hbm(x), g, *map(hbm, weights), gain)


tn_dims = (((0,), (0,)), ((), ()))


def share_kernel(col, left, right, out):
    value = lax.dot_general(left[0], right[0], tn_dims, preferred_element_type=f32)
    out[...] = value.astype(bf16)


def share(left, right, col):
    n, rows, d = left.shape
    w = d // 2
    block = pl.BlockSpec((d, w), lambda i, c: (0, i))
    return pl.pallas_call(
        share_kernel,
        out_shape=pltpu.HBM((d, n * w), bf16),
        grid_spec=pltpu.PrefetchScalarGridSpec(
            num_scalar_prefetch=1,
            grid=(n,),
            in_specs=[
                pl.BlockSpec((1, rows, d), lambda i, c: (i, 0, 0)),
                pl.BlockSpec((1, rows, w), lambda i, c: (i, 0, c[0])),
            ],
            out_specs=block,
        ),
        compiler_params=pltpu.CompilerParams(vmem_limit_bytes=40 << 20),
        cost_estimate=CHEAP,
        name="share",
    )(col.reshape(1), hbm(left), hbm(right))


def copy(x):
    return pl.pallas_call(
        tick_kernel, out_shape=pltpu.HBM(x.shape, x.dtype), cost_estimate=CHEAP, name="copy"
    )(x)


def tick_kernel(x_ref, out):
    out[...] = x_ref[...]


def tick(x):
    return pl.pallas_call(
        tick_kernel, out_shape=jax.ShapeDtypeStruct(x.shape, x.dtype), cost_estimate=cost(200.0), name="tick"
    )(x)


def total_kernel(*refs, counts):
    out = refs[-1]
    start, column = 0, 0
    for count in counts:
        group = refs[start : start + count]
        start += count
        acc = jnp.zeros(group[0].shape[1:], f32)
        for ref in group:
            for i in range(ref.shape[0]):
                acc = acc + ref[i].astype(f32)
        out[:, column : column + acc.shape[1]] = acc.astype(bf16)
        column += acc.shape[1]


def total(groups):
    flat = [x for group in groups for x in group]
    rows = flat[0].shape[1]
    cuts = 2 if rows % 32 == 0 else 1
    width = sum(group[0].shape[2] for group in groups)
    return pl.pallas_call(
        functools.partial(total_kernel, counts=[len(group) for group in groups]),
        out_shape=pltpu.HBM((rows, width), bf16),
        grid=(cuts,),
        in_specs=[
            pl.BlockSpec((x.shape[0], rows // cuts, x.shape[2]), lambda i: (0, i, 0)) for x in flat
        ],
        out_specs=pl.BlockSpec((rows // cuts, width), lambda i: (i, 0)),
        compiler_params=pltpu.CompilerParams(vmem_limit_bytes=40 << 20),
        cost_estimate=cost(0.001),
        name="total",
    )(*flat)


def add_kernel(a_ref, b_ref, out):
    out[...] = (a_ref[...].astype(f32) + b_ref[...].astype(f32)).astype(bf16)


def add(a, b):
    return pl.pallas_call(
        add_kernel, out_shape=pltpu.HBM(a.shape, bf16), cost_estimate=CHEAP, name="add"
    )(a, b)


def add_rows(a, b):
    rows, cols = a.shape
    block = pl.BlockSpec((rows // 5, cols), lambda i: (i, 0))
    return pl.pallas_call(
        add_kernel,
        out_shape=pltpu.HBM(a.shape, bf16),
        grid=(5,),
        in_specs=[block] * 2,
        out_specs=block,
        compiler_params=pltpu.CompilerParams(vmem_limit_bytes=24 << 20),
        cost_estimate=CHEAP,
        name="add_rows",
    )(hbm(a), hbm(b))


def pair_kernel(a_ref, b_ref, out):
    out[0] = a_ref[...]
    out[1] = b_ref[...]


def pair_up(a, b, us=0.001):
    return pl.pallas_call(
        pair_kernel, out_shape=pltpu.HBM((2,) + a.shape, bf16), cost_estimate=cost(us), name="pair_up"
    )(a, b)


def by_bits(first, second, put):
    for i in range(2):
        for j in range(2):

            @pl.when((first == i) & (second == j))
            def _(i=i, j=j):
                put(i, j)


def place_kernel(at, own, own_x, mate, mate_x, o0, o1, o2):
    block = pl.program_id(0)
    slot = (block % 2) ^ at[1]
    w = o0.shape[2] // 2

    def put(other_x, core):
        refs = (own_x, mate_x) if other_x else (own, mate)
        for side in range(2):
            part = refs[side ^ core][slot].astype(f32)
            for i, out in enumerate((o0, o1, o2)):
                out[0, :, side * w : (side + 1) * w] = part[:, i * w : (i + 1) * w]

    by_bits((block // 2) ^ at[0], at[2], put)


def place_tail(arrays, at):
    _, h, width = arrays[0].shape
    d = width // 3 * 2
    whole = pl.BlockSpec((2, h, width), lambda i, m: (0, 0, 0), pipeline_mode=pl.Buffered(1))
    outs = pl.pallas_call(
        place_kernel,
        out_shape=[pltpu.HBM((4, h, d), f32)] * 3,
        grid_spec=pltpu.PrefetchScalarGridSpec(
            num_scalar_prefetch=1,
            grid=(4,),
            in_specs=[whole] * 4,
            out_specs=[pl.BlockSpec((1, h, d), lambda i, m: (i, 0, 0))] * 3,
        ),
        compiler_params=pltpu.CompilerParams(vmem_limit_bytes=40 << 20),
        cost_estimate=cost(0.001),
        name="place_tail",
    )(at, *arrays)
    return [out.reshape(4 * h, d) for out in outs]


def cross_kernel(at, x_ref, g_ref, *refs):
    s = refs[-1]
    s[...] = jnp.dot(x_ref[...], g_ref[...], preferred_element_type=f32)
    half = s.shape[0] // 2
    for w in range(2):

        @pl.when(pl.program_id(0) == w)
        def _(w=w):
            for x in range(2):
                rows = pl.ds(pl.multiple_of((at[1] ^ x) * half, 16), half)
                refs[2 * w + x][...] = s[rows, :].astype(bf16)


def cross(x, g, at):
    d, rows = x.shape
    w = d // 2
    cols = g.shape[1]
    step = 512 if cols % 512 == 0 else cols
    n = cols // step
    first = pl.BlockSpec((w // 2, step), lambda i, j, m: (0, jnp.where(i == 0, j, n - 1)))
    second = pl.BlockSpec((w // 2, step), lambda i, j, m: (0, jnp.where(i == 1, j, 0)))
    return pl.pallas_call(
        cross_kernel,
        out_shape=[pltpu.HBM((w // 2, cols), bf16)] * 4,
        grid_spec=pltpu.PrefetchScalarGridSpec(
            num_scalar_prefetch=1,
            grid=(2, n),
            in_specs=[
                pl.BlockSpec((w, rows), lambda i, j, m: (m[0] ^ i, 0)),
                pl.BlockSpec((rows, step), lambda i, j, m: (0, j)),
            ],
            out_specs=[first, first, second, second],
            scratch_shapes=[pltpu.VMEM((w, step), f32)],
        ),
        compiler_params=pltpu.CompilerParams(vmem_limit_bytes=40 << 20),
        cost_estimate=CHEAP,
        name="cross",
    )(at, hbm(x), hbm(g))


def spread_kernel(at, own, mate, *refs, width, other_x):
    out = refs[-1]
    step = out.shape[1]
    rows = pl.ds(pl.multiple_of(pl.program_id(0) * step, step), step)

    def put(core):
        cut = []
        for t in range(3):
            for n in range(2):
                for c in range(2):
                    part = (own, mate)[c ^ core][n ^ at[1], rows, :]
                    cut.append(part[:, t * width : (t + 1) * width])
        out[0] = jnp.concatenate(cut, axis=1).astype(f32)

    for core in range(2):

        @pl.when(at[2] == core)
        def _(core=core):
            put(core)


def spread(own, mate, at, used, other_x, carried=None):
    _, rows, cols = own.shape
    width = 4 * used
    cuts = 2 if rows % 32 == 0 else 1
    whole = pl.BlockSpec((2, rows, cols), lambda j, m: (0, 0, 0), pipeline_mode=pl.Buffered(1))
    more = () if carried is None else (carried,)
    return pl.pallas_call(
        functools.partial(spread_kernel, width=used // 3, other_x=other_x),
        out_shape=pltpu.HBM((2, rows, width), f32),
        grid_spec=pltpu.PrefetchScalarGridSpec(
            num_scalar_prefetch=1,
            grid=(cuts,),
            in_specs=[whole] * 2 + [pl.BlockSpec(memory_space=pl.ANY)] * len(more),
            out_specs=pl.BlockSpec((1, rows // cuts, width), lambda j, m: (m[0] ^ other_x, j, 0)),
        ),
        input_output_aliases={3: 0} if more else {},
        compiler_params=pltpu.CompilerParams(vmem_limit_bytes=40 << 20),
        cost_estimate=CHEAP,
        name="spread",
    )(at, own, mate, *more)


def back_kernel(shards, g_ref, w_ref, *refs):
    acc = jnp.dot(g_ref[...], w_ref[...], preferred_element_type=f32)
    if len(refs) == 2:
        acc = acc + refs[0][0].astype(f32)
    refs[-1][0] = acc.astype(bf16)


def back(grad, w, shards, rows, got=None):
    c, d = w.shape
    n = shards.shape[0]
    step = d
    out = pl.BlockSpec((1, rows, step), lambda j, i, f: (i, 0, j))
    in_specs = [
        pl.BlockSpec((rows, c), lambda j, i, f: (f[i], 0)),
        pl.BlockSpec((c, step), lambda j, i, f: (0, j)),
    ]
    args = [hbm(grad), hbm(w)]
    if got is not None:
        in_specs.append(pl.BlockSpec((1, rows, step), lambda j, i, f: (0, 0, j)))
        args.append(got)
    return pl.pallas_call(
        back_kernel,
        out_shape=pltpu.HBM((n, rows, d), bf16),
        grid_spec=pltpu.PrefetchScalarGridSpec(
            num_scalar_prefetch=1, grid=(d // step, n), in_specs=in_specs, out_specs=out
        ),
        compiler_params=pltpu.CompilerParams(vmem_limit_bytes=40 << 20),
        cost_estimate=CHEAP,
        name="back",
    )(shards, *args)


def finish_kernel(shard, g_ref, w_ref, core, near, x_ref, resid, gain, out, gain_out):
    grad = jnp.dot(g_ref[...], w_ref[...], preferred_element_type=f32)
    grad = grad + core[0].astype(f32) + near[0].astype(f32)
    x = x_ref[...].astype(f32)
    inverse = lax.rsqrt(jnp.mean(x * x, axis=-1, keepdims=True) + epsilon)
    part = jnp.sum(grad * x * inverse, axis=0, keepdims=True)

    @pl.when(pl.program_id(0) == 0)
    def _():
        gain_out[...] = jnp.zeros_like(gain_out)

    gain_out[...] += part
    scaled = grad * gain[...]
    out[...] = (
        resid[...]
        + inverse * scaled
        - x * (inverse * inverse * inverse) * jnp.mean(scaled * x, axis=-1, keepdims=True)
    ).astype(bf16)


def finish(grad, w, shard, core, near, x, resid, gain, tile=256):
    rows, d = x.shape
    c = w.shape[0]
    tiles = rows // tile
    row = lambda i, f: (i, 0)
    once = pl.Buffered(1)
    return pl.pallas_call(
        finish_kernel,
        out_shape=[pltpu.HBM((rows, d), bf16), jax.ShapeDtypeStruct((1, d), f32)],
        grid_spec=pltpu.PrefetchScalarGridSpec(
            num_scalar_prefetch=1,
            grid=(tiles,),
            in_specs=[
                pl.BlockSpec((tile, c), lambda i, f: (f[0] * tiles + i, 0)),
                pl.BlockSpec((c, d), lambda i, f: (0, 0), pipeline_mode=once),
                pl.BlockSpec((1, tile, d), lambda i, f: (1, i, 0)),
                pl.BlockSpec((1, tile, d), lambda i, f: (0, i, 0)),
                pl.BlockSpec((tile, d), row),
                pl.BlockSpec((tile, d), row),
                pl.BlockSpec((1, d), lambda i, f: (0, 0)),
            ],
            out_specs=[pl.BlockSpec((tile, d), row), pl.BlockSpec((1, d), lambda i, f: (0, 0))],
        ),
        compiler_params=pltpu.CompilerParams(vmem_limit_bytes=40 << 20),
        cost_estimate=CHEAP,
        name="finish",
    )(shard.reshape(1), hbm(grad), hbm(w), core, near, hbm(x), hbm(resid), gain)


def rms_inverse(values):
    return lax.rsqrt(jnp.mean(values * values, axis=-1, keepdims=True) + epsilon)


def norm_back(values, inverse, grad_scaled):
    return inverse * grad_scaled - values * (inverse * inverse * inverse) * jnp.mean(
        grad_scaled * values, axis=-1, keepdims=True
    )


def dot(left, right):
    return jnp.dot(left, right, preferred_element_type=f32)


def times_trans(left, right):
    return lax.dot_general(left, right, (((1,), (1,)), ((), ())), preferred_element_type=f32)


def trans_times(left, right):
    return lax.dot_general(left, right, (((0,), (0,)), ((), ())), preferred_element_type=f32)


def rows_at(array, start, count):
    return lax.dynamic_slice_in_dim(array, start, count, 0)


def put_rows(array, rows, start):
    return lax.dynamic_update_slice_in_dim(array, rows, start, 0)


def make_local(sizes):
    def pairs(target):
        found = []
        for gx in range(sizes["gx"]):
            for gc in range(sizes["gc"]):
                for z in range(4):
                    for w in range(sizes["wt"]):
                        goal = target(gx, gc, z, w)
                        if goal is not None and goal != (gx, gc, z, w):
                            found.append((place(gx, gc, z, w), place(*goal)))
        return found

    def place(gx, gc, z, w):
        return ((gx * sizes["gc"] + gc) * 4 + z) * sizes["wt"] + w

    def send(value, target):
        return lax.ppermute(value, AXES, pairs(target))

    def core_mate(gx, gc, z, w):
        return (gx, 1 - gc, z, w)

    def x_mate(gx, gc, z, w):
        return (1 - gx, gc, z, w)

    def near_mate(gx, gc, z, w):
        return (gx, gc, z ^ 1, w)

    def far_mate(gx, gc, z, w):
        return (gx, gc, z ^ 2, w)

    def cross_mate(gx, gc, z, w):
        return (gx, 1 - gc, z ^ 1, w)

    def wt_mate(gx, gc, z, w):
        return (gx, gc, z, 1 - w)

    def wt_x_mate(gx, gc, z, w):
        return (1 - gx, gc, z, 1 - w)

    def to_host(gx, gc, z, w):
        return (gx, 1 - (z & 1), 2 * gc + (z >> 1), w)

    def to_home(gx, gc, z, w):
        return (gx, z >> 1, 2 * (z & 1) + 1 - gc, w)

    def hop1(gx, gc, z, w):
        if gc == 0:
            return (gx, 0, z - 1, w) if z > 0 else None
        return (gx, 1, z + 1, w) if z < 3 else None

    def hop2(gx, gc, z, w):
        if gc == 0:
            return (gx, 0, z - 1, w) if z in (1, 2) else None
        return (gx, 1, z + 1, w) if z in (1, 2) else None

    def hop3(gx, gc, z, w):
        if gc == 0:
            return (gx, 0, z ^ 1, w) if z < 2 else None
        return (gx, 1, z ^ 1, w) if z > 1 else None

    def lane_share(gx, gc, z, w):
        return (gx, 1 - gc, z, w) if gc == z >> 1 else None

    def sum_all(value):
        for axis in ("gc", "wt", "near", "far", "gx"):
            step = 1
            while step < sizes[axis]:

                def mate(gx, gc, z, w, axis=axis, step=step):
                    at = dict(gx=gx, gc=gc, far=z >> 1, near=z & 1, wt=w)
                    at[axis] ^= step
                    return (at["gx"], at["gc"], 2 * at["far"] + at["near"], at["wt"])

                value = value + send(value, mate)
                step *= 2
        return value

    def local(
        tokens, segments, w_qkv, w_proj, w_in, w_out, gain_attn, gain_mlp, query_scale, cotangent
    ):
        gx, gc, host, near, wt = (lax.axis_index(axis) for axis in AXES)
        z = 2 * host + near
        mine = 2 * near + 1 - gc
        parts = 4
        nh = H // parts
        groups = 1
        rows = tokens.shape[1]
        group_len = segments.shape[1]
        wrows = w_qkv.shape[0]
        lane = gc == host
        pair = sizes["wt"] == 2

        def after(value, *others):
            return lax.optimization_barrier((value,) + others)[0]

        picked = pick(w_qkv, mine, parts, groups, nh)
        own = tokens[0]
        got1 = send(own, hop1)
        own_share = send(own, lane_share)
        seg_mate = send(segments, core_mate)
        got2 = send(got1, hop2)
        got1_share = send(got1, lane_share)
        end = jnp.where(gc == 0, z == 0, z == 3)
        if pair:
            wide_own = stretch(picked, groups, nh, 2)
            got1 = after(got1, wide_own)
            other_w = send(picked, wt_mate)
            wide_w = (wide_own, stretch(other_w, groups, nh, 10))
        else:
            flat_all = lax.all_gather(picked, "wt", axis=0, tiled=True)
            by_head = jnp.transpose(
                flat_all[:, : 3 * nh * HD].reshape(D, groups, 3, nh // groups, HD), (0, 2, 1, 3, 4)
            )
            wide_w = (
                jnp.pad(
                    by_head.reshape(D, 3 * nh, HD), ((0, 0), (0, 0), (0, LN - HD))
                ).reshape(D, -1),
            )
        got3 = send(jnp.where(end, own, got2), hop3)
        got2_share = send(got2, lane_share)
        way = 1 - 2 * host
        last = jnp.where(host == 0, jnp.where(z == 0, 3, 0), jnp.where(z == 3, 0, 3))
        places = (z, z + way, z + 2 * way, last)

        half_rows = wrows // 2
        half_w = jnp.stack([rows_at(w, gc * half_rows, half_rows) for w in (w_proj, w_in, w_out)])
        if pair:
            half_w = send(after(half_w, other_w), wt_mate)
        else:
            half_w = lax.all_gather(half_w, "wt", axis=0, tiled=False)

        dim_scale = scale_base / math.sqrt(HD) * jax.nn.softplus(query_scale)
        lane_scale = jnp.tile(jnp.pad(dim_scale * log2e, (0, LN - HD)), nh)[None]
        ones = jnp.tile(
            ((jnp.arange(LN) >= HD) & (jnp.arange(LN) < HD + 3)).astype(f32), 2 * nh
        )[None]
        seg_row = jnp.where(lane, segments, seg_mate)[0]
        fixed = (lane, mine, wt, gain_attn[None], wide_w, lane_scale, ones, group_len)
        carried = project(((own, own_share), (got1, got1_share)), places[:2], *fixed)
        got3_share = send(after(got3, carried[0]), lane_share)
        all_normed, queries, keyval, inputs = project(
            ((got2, got2_share), (got3, got3_share)), places[2:], *fixed, carried=carried
        )
        grad_mlp = send(after(cotangent[0], got3_share), to_host)

        att, att_float, q_aug = attn_fwd(queries, keyval, seg_row, nh)
        att, half_w, _ = lax.optimization_barrier((att, half_w, grad_mlp))

        trades = (core_mate, near_mate, cross_mate)
        att_pieces = [rows_at(att, (mine ^ j) * rows, rows) for j in range(parts)]
        half_mate = send(after(half_w, *att_pieces), core_mate)
        att_pieces = [att_pieces[0]] + [send(att_pieces[j + 1], trades[j]) for j in range(3)]
        if pair:
            w_trans = order(after(picked, att), other_w, wt)
        else:
            w_trans = flat_all.T
        normed_trans = transpose(after(all_normed, w_trans))
        if pair:
            weights = (w_proj, w_in, w_out, half_w, half_mate)
            starts = (wt * wrows, (1 - wt) * wrows + gc * half_rows, (1 - wt) * wrows + (1 - gc) * half_rows)
        else:
            one = gc == 0
            tail_w = jnp.stack(
                [jnp.where(one, half_w, half_mate), jnp.where(one, half_mate, half_w)], axis=1
            )
            weights = (jnp.transpose(tail_w, (2, 0, 1, 3, 4)).reshape(3, D, D),)
            starts = ()
        (
            layer_out,
            left,
            right,
            grad_resid,
            *pieces,
            grad_gain_mlp,
        ) = tail(
            jnp.stack([mine, *starts]), att_pieces, after(inputs, normed_trans), grad_mlp, weights, gain_mlp[None]
        )
        pieces = [pieces[0]] + [send(pieces[j + 1], trades[j]) for j in range(3)]

        shared = share(after(left, pieces[1]), right, 1 - gc)
        from_core = send(shared, core_mate)
        own_half = share(left, right, after(gc, shared))
        pieces[2:] = [after(piece, own_half) for piece in pieces[2:]]
        home_out = send(after(layer_out, *pieces[1:]), to_home)
        late_gain = tick(after(gain_attn.reshape(-1, LN), *pieces[1:]))
        summed = add_rows(own_half, after(from_core, late_gain))
        kept = lax.all_to_all(summed, ("wt", "gx", "near"), 0, 0, tiled=True)

        scale_row = jnp.tile(dim_scale, nh // groups)[None]

        def backward(group, *others):
            first, *rest = pieces
            return attn_bwd(
                q_aug,
                keyval,
                (after(first, summed, *others), *rest),
                att_float,
                mine,
                seg_row,
                scale_row,
                nh,
                group,
                groups,
            )

        def by_rows(grad):
            if pair:
                own, *rest = cross(normed_trans, grad, jnp.stack([wt, gx]))
                got = [send(part, mate) for part, mate in zip(rest, (x_mate, wt_mate, wt_x_mate))]
                return [part[None] for part in (own, *got)]
            part = dot(normed_trans, grad).astype(bf16)
            sources = sizes["wt"] * 2
            got = lax.all_to_all(part, ("wt", "gx"), 0, 0, tiled=True)
            return [got.reshape(sources, D // sources, -1)]

        grad_project, grad_lanes = backward(0)
        layer_out = after(home_out, grad_project)

        last_step = [layer_out]

        def turn(value):
            return after(value, *last_step)

        def done(value):
            last_step[0] = value
            return value

        sources = sizes["wt"] * 4
        to_core = done(back(turn(grad_project), w_trans, jnp.stack([mine ^ 3, mine ^ 1]), rows))
        from_core = send(to_core, core_mate)
        by_place = by_rows(turn(grad_project))
        done(by_place[0])
        to_near = done(back(grad_project, w_trans, (mine ^ 2).reshape(1), rows, turn(from_core)))
        from_near = send(to_near, near_mate)
        t1 = done(total([[turn(kept).reshape(sources, D // sources, -1)]]))
        t1_far = send(t1, far_mate)
        layer_out = done(copy(turn(layer_out)))
        by_place[0] = turn(by_place[0])
        q1 = done(total([by_place]))
        q1_far = send(q1, far_mate)
        t2 = done(add(turn(t1), t1_far))
        t2_near = send(t2, near_mate)
        grad_tokens, grad_gain_attn = finish(
            grad_project,
            w_trans,
            mine,
            from_core,
            turn(from_near),
            inputs,
            grad_resid,
            late_gain.reshape(1, -1),
        )
        done(grad_tokens)
        grad_query_scale = (
            grad_lanes[0, :HD]
            / (dim_scale * log2e)
            * (scale_base / math.sqrt(HD))
            * jax.nn.sigmoid(query_scale)
        )
        small = jnp.concatenate(
            [grad_gain_attn[0], grad_gain_mlp[0], jnp.pad(grad_query_scale, (0, LN - HD))]
        ).reshape(-1, LN)
        q2 = done(add(turn(q1), q1_far))
        q2_near = send(q2, near_mate)
        t4 = done(pair_up(turn(t2), t2_near))
        t4_x = send(t4, x_mate)
        t4_core = send(t4, core_mate)
        home_grad = send(turn(grad_tokens), to_home)
        q4 = done(pair_up(turn(q2), q2_near))
        q4_x = send(q4, x_mate)
        q4_core = send(q4, core_mate)
        t4_x = done(turn(t4_x))
        t4_cross = send(t4_x, core_mate)
        used = 3 * nh * HD
        spread_at = jnp.stack([gx, near, 1 - gc])
        totals = place_tail((turn(t4), t4_x, t4_core, t4_cross), jnp.stack([gx, near, gc]))
        done(totals[0])
        q4_core = done(turn(q4_core))
        small = done(sum_all(turn(small))).reshape(-1)
        grad_tokens = done(copy(turn(home_grad)))
        q4_x = done(turn(q4_x))
        q4_cross = send(q4_x, core_mate)
        total_qkv = done(spread(turn(q4), q4_core, spread_at, used, 0))
        total_qkv = spread(turn(q4_x), q4_cross, spread_at, used, 1, total_qkv).reshape(wrows, 3 * D)
        return (
            layer_out[None],
            grad_tokens[None],
            total_qkv,
            *totals,
            small[:D],
            small[D : 2 * D],
            small[2 * D : 2 * D + HD],
        )

    return local


def solution(mesh):
    groups, parts, wt = (mesh.shape[axis] for axis in ("grp", "ctx", "wt"))
    inner = Mesh(mesh.devices.reshape(groups // 2, 2, parts // 2, 2, wt), AXES)
    sizes = dict(inner.shape)
    split = P(("gx", "gc", "wt"), ("far", "near"), None)
    weight = P("wt", None)
    return jax.shard_map(
        make_local(sizes),
        mesh=inner,
        in_specs=(
            split,
            P(("gx", "gc", "wt"), None),
            weight,
            weight,
            weight,
            weight,
            P(),
            P(),
            P(),
            split,
        ),
        out_specs=(split, split, weight, weight, weight, weight, P(), P(), P()),
        check_vma=False,
    )
```

```python
import functools
import math

import jax
import jax.numpy as jnp
from jax import lax
from jax.experimental import pallas as pl
from jax.experimental.pallas import tpu as pltpu
from jax.sharding import Mesh
from jax.sharding import PartitionSpec as P

D = 1280
H = 16
HD = 80
LN = 128
epsilon = 1e-06
scale_base = 1.442695041
log2e = 1.4426950408889634
NEG = -1e30
def cost(us):
    return pl.CostEstimate(flops=int(us * 1_000_000_000), transcendentals=0, bytes_accessed=1000)


CHEAP = cost(0.001)
f32 = jnp.float32
bf16 = jnp.bfloat16
AXES = ("gx", "gc", "far", "near", "wt")


def hbm(x):
    return pltpu.with_memory_space_constraint(x, pltpu.HBM)


def block_flags(seg_row, bq, bk):
    n = seg_row.shape[0]
    q = seg_row.reshape(n // bq, bq)
    k = seg_row.reshape(n // bk, bk)
    qf, ql = q[:, 0][:, None], q[:, -1][:, None]
    kf, kl = k[:, 0][None], k[:, -1][None]
    qs = jnp.arange(n // bq, dtype=jnp.int32)[:, None] * bq
    ks = jnp.arange(n // bk, dtype=jnp.int32)[None] * bk
    below = ks + bk - 1 <= qs
    skip = (ks > qs + bq - 1) | ((kf > 0) & (kl < qf))
    same = (qf == ql) & (kl == ql) & ((kf == kl) | ((kf == 0) & (kl == 1)))
    full = below & ((kl == 0) | same)
    flags = jnp.where(skip, 0, jnp.where(full, 1, 2))
    if bq == bk:
        flags = jnp.where(qs == ks, 3, flags)
    return flags.astype(jnp.int32).reshape(-1)


def put_split(base, col, lanes):
    hi = col.astype(bf16).astype(f32)
    rest = col - hi
    mid = rest.astype(bf16).astype(f32)
    out = jnp.where(lanes == HD, hi, base)
    out = jnp.where(lanes == HD + 1, mid, out)
    return jnp.where(lanes == HD + 2, rest - mid, out).astype(bf16)


def fwd_kernel(flags, q_ref, kv, segc, segr, att, of, qaug, m_s, acc_s, *, nh, bq, bk, nk):
    qi = pl.program_id(0)
    count = (qi * bq + bq + bk - 1) // bk
    nt = (((1,), (1,)), ((), ()))
    acc_s[...] = jnp.zeros_like(acc_s)
    m_s[...] = jnp.zeros_like(m_s)

    def mask(ko, q0=0, qn=bq, kn=bk):
        qpos = qi * bq + q0 + lax.broadcasted_iota(jnp.int32, (qn, kn), 0)
        kpos = ko + lax.broadcasted_iota(jnp.int32, (qn, kn), 1)
        ks = segr[:, pl.ds(ko, kn)]
        return (kpos <= qpos) & ((ks == 0) | (ks == segc[q0 : q0 + qn, :]))

    def step(kb, masked, q0=0, qn=bq, kn=bk):
        ko = pl.multiple_of(kb * bk, bk)
        if masked:
            allowed = mask(ko, q0, qn, kn)
        rows = slice(q0, q0 + qn)
        for h in range(nh):
            k = kv[pl.ds(ko, kn), h * LN : (h + 1) * LN]
            v = kv[pl.ds(ko, kn), (nh + h) * LN : (nh + h + 1) * LN]
            q = q_ref[rows, h * LN : (h + 1) * LN]
            p = jnp.exp2(lax.dot_general(q, k, nt, preferred_element_type=f32))
            if masked:
                p = jnp.where(allowed, p, 0.0)
            acc_s[h, rows, :] += jnp.dot(p.astype(bf16), v, preferred_element_type=f32)

    def body(kb, carry):
        flag = flags[qi * nk + kb]

        @pl.when(flag == 1)
        def _():
            step(kb, False)

        @pl.when(flag >= 2)
        def _():
            step(kb, True)

        return carry

    lax.fori_loop(0, count, body, 0)
    bad = jnp.zeros((bq, 1), f32)
    for h in range(nh):
        total = acc_s[h][:, HD : HD + 1]
        bad = jnp.maximum(bad, jnp.where((total > 2.0**-60) & (total < 2.0**60), 0.0, 1.0))

    @pl.when(jnp.max(bad) > 0.0)
    def _():
        def head(h, carry):
            kc = pl.ds(pl.multiple_of(h * LN, LN), LN)
            vc = pl.ds(pl.multiple_of((nh + h) * LN, LN), LN)
            m_s[h] = jnp.full((bq, LN), NEG, f32)
            acc_s[h] = jnp.zeros((bq, LN), f32)

            def inner(kb, carry):
                @pl.when(flags[qi * nk + kb] > 0)
                def _():
                    ko = pl.multiple_of(kb * bk, bk)
                    s = lax.dot_general(
                        q_ref[:, kc], kv[pl.ds(ko, bk), kc], nt, preferred_element_type=f32
                    )
                    s = jnp.where(mask(ko), s, NEG)
                    old = m_s[h]
                    new = jnp.maximum(old, jnp.max(s, axis=1, keepdims=True))
                    p = jnp.exp2(s - new[:, :1]).astype(bf16)
                    m_s[h] = new
                    acc_s[h] = acc_s[h] * jnp.exp2(old - new) + jnp.dot(
                        p, kv[pl.ds(ko, bk), vc], preferred_element_type=f32
                    )

                return carry

            lax.fori_loop(0, count, inner, 0)
            return carry

        lax.fori_loop(0, nh, head, 0)

    lanes = lax.broadcasted_iota(jnp.int32, (bq, LN), 1)
    outs = []
    for h in range(nh):
        acc = acc_s[h]
        total = acc[:, HD : HD + 1]
        out = acc * (1.0 / total)
        of[:, h * LN : (h + 1) * LN] = jnp.where(lanes < HD, out, 0.0).astype(bf16)
        outs.append(out[:, :HD])
        lse = m_s[h][:, :1] + jnp.log2(total)
        qaug[:, h * LN : (h + 1) * LN] = put_split(
            q_ref[:, h * LN : (h + 1) * LN].astype(f32), -lse, lanes
        )
    att[...] = jnp.concatenate(outs, axis=1).astype(bf16)


def attn_fwd(q, kv, seg_row, nh, bq=512, bk=512):
    n = q.shape[0]
    w = nh * LN
    spec = pltpu.PrefetchScalarGridSpec(
        num_scalar_prefetch=1,
        grid=(n // bq,),
        in_specs=[
            pl.BlockSpec((bq, w), lambda i, f: (i, 0)),
            pl.BlockSpec((n, 2 * w), lambda i, f: (0, 0)),
            pl.BlockSpec((bq, 1), lambda i, f: (i, 0)),
            pl.BlockSpec((1, n), lambda i, f: (0, 0)),
        ],
        out_specs=[
            pl.BlockSpec((bq, nh * HD), lambda i, f: (i, 0)),
            pl.BlockSpec((bq, w), lambda i, f: (i, 0)),
            pl.BlockSpec((bq, w), lambda i, f: (i, 0)),
        ],
        scratch_shapes=[pltpu.VMEM((nh, bq, LN), f32), pltpu.VMEM((nh, bq, LN), f32)],
    )
    return pl.pallas_call(
        functools.partial(fwd_kernel, nh=nh, bq=bq, bk=bk, nk=n // bk),
        out_shape=[
            pltpu.HBM((n, nh * HD), bf16),
            pltpu.HBM((n, w), bf16),
            pltpu.HBM((n, w), bf16),
        ],
        grid_spec=spec,
        compiler_params=pltpu.CompilerParams(vmem_limit_bytes=40 << 20),
        cost_estimate=cost(0.01),
        name="attn_fwd",
    )(block_flags(seg_row, bq, bk), hbm(q), hbm(kv), seg_row[:, None], seg_row[None])


def bwd_kernel(
    flags, mine, qa, kk, vv, do0, do1, do2, do3, of, segc, segr, scale, dqkv, gscale, doa_s, dq_s, dk_s, dv_s, *, first, nh, bq, bk, n
):
    nk = n // bk
    nq = n // bq
    kb = pl.program_id(0)
    part = n // 4
    step_rows = 256 if part % 256 == 0 else part
    lanes = lax.broadcasted_iota(jnp.int32, (step_rows, LN), 1)

    @pl.when(kb == 0)
    def _():
        dq_s[...] = jnp.zeros_like(dq_s)
        for j, piece in enumerate((do0, do1, do2, do3)):
            start = (mine[0] ^ j) * part
            for i in range(part // step_rows):
                d = piece[i * step_rows : (i + 1) * step_rows, :].astype(f32)
                r = pl.ds(pl.multiple_of(start + i * step_rows, step_rows), step_rows)
                for h in range(nh):
                    at = (first + h) * HD
                    dh = jnp.concatenate(
                        [d[:, at : at + HD], jnp.zeros((step_rows, LN - HD), f32)], axis=1
                    )
                    c = slice(h * LN, (h + 1) * LN)
                    delta = jnp.sum(dh * of[r, c].astype(f32), axis=1, keepdims=True)
                    doa_s[r, c] = put_split(dh, -delta, lanes)

    dk_s[...] = jnp.zeros_like(dk_s)
    dv_s[...] = jnp.zeros_like(dv_s)
    ko = kb * bk
    nt = (((1,), (1,)), ((), ()))
    tn = (((0,), (0,)), ((), ()))

    def step(qi, masked, q0=0, qn=bq, kn=bk):
        qo = pl.multiple_of(qi * bq + q0, qn)
        rows = slice(0, kn)
        if masked:
            kpos = ko + lax.broadcasted_iota(jnp.int32, (kn, qn), 0)
            qpos = qo + lax.broadcasted_iota(jnp.int32, (kn, qn), 1)
            ks = segc[rows, :]
            allowed = (kpos <= qpos) & ((ks == 0) | (ks == segr[:, pl.ds(qo, qn)]))
        for h in range(nh):
            c = slice(h * LN, (h + 1) * LN)
            q = qa[pl.ds(qo, qn), c]
            k = kk[rows, c]
            d = doa_s[pl.ds(qo, qn), c]
            p = jnp.exp2(lax.dot_general(k, q, nt, preferred_element_type=f32))
            if masked:
                p = jnp.where(allowed, p, 0.0)
            ds = (p * lax.dot_general(vv[rows, c], d, nt, preferred_element_type=f32)).astype(bf16)
            dv_s[h, rows, :] += jnp.dot(p.astype(bf16), d, preferred_element_type=f32)
            dk_s[h, rows, :] += jnp.dot(ds, q, preferred_element_type=f32)
            dq_s[h, pl.ds(qo, qn), :] += lax.dot_general(ds, k, tn, preferred_element_type=f32)

    def body(qi, carry):
        flag = flags[qi * nk + kb]

        @pl.when(flag == 1)
        def _():
            step(qi, False)

        @pl.when(flag == 2)
        def _():
            step(qi, True)

        if bq == bk:

            @pl.when(flag == 3)
            def _():
                step(qi, True, 0, bq // 2, bk // 2)
                step(qi, True, bq // 2, bq // 2, bk)

        return carry

    lax.fori_loop(ko // bq, nq, body, 0)
    r = pl.multiple_of(ko, bk)
    ln2 = math.log(2.0)
    gap = dqkv.shape[1] - 3 * nh * HD
    dqkv[pl.ds(r, bk), nh * HD :] = jnp.concatenate(
        [dk_s[h][:, :HD] * ln2 for h in range(nh)]
        + [dv_s[h][:, :HD] for h in range(nh)]
        + [jnp.zeros((bk, gap), f32)],
        axis=1,
    ).astype(bf16)

    @pl.when(kb == nk - 1)
    def _():
        total = jnp.zeros((1, LN), f32)
        for i in range(nq):
            rows = slice(i * bq, (i + 1) * bq)
            for h in range(nh):
                total = total + jnp.sum(
                    dq_s[h, rows, :] * qa[rows, h * LN : (h + 1) * LN].astype(f32), axis=0, keepdims=True
                )
            grads = jnp.concatenate([dq_s[h, rows, :][:, :HD] for h in range(nh)], axis=1)
            dqkv[rows, 0 : nh * HD] = (grads * scale[...]).astype(bf16)
        gscale[...] = jnp.broadcast_to(total, gscale.shape)


def attn_bwd(qa, kv, pieces, of, mine, seg_row, scale, heads, group, groups, bq=512, bk=512):
    n = qa.shape[0]
    nh = heads // groups
    w = nh * LN
    once = pl.Buffered(1)
    spec = pltpu.PrefetchScalarGridSpec(
        num_scalar_prefetch=2,
        grid=(n // bk,),
        in_specs=[
            pl.BlockSpec((n, w), lambda i, f, m: (0, group), pipeline_mode=once),
            pl.BlockSpec((bk, w), lambda i, f, m: (i, group)),
            pl.BlockSpec((bk, w), lambda i, f, m: (i, groups + group)),
            *[pl.BlockSpec((n // 4, heads * HD), lambda i, f, m: (0, 0), pipeline_mode=once)] * 4,
            pl.BlockSpec((n, w), lambda i, f, m: (0, group), pipeline_mode=once),
            pl.BlockSpec((bk, 1), lambda i, f, m: (i, 0)),
            pl.BlockSpec((1, n), lambda i, f, m: (0, 0)),
            pl.BlockSpec((1, nh * HD), lambda i, f, m: (0, 0)),
        ],
        out_specs=[
            pl.BlockSpec((n, lanes_up(3 * nh * HD)), lambda i, f, m: (0, 0)),
            pl.BlockSpec((8, LN), lambda i, f, m: (0, 0)),
        ],
        scratch_shapes=[
            pltpu.VMEM((n, w), bf16),
            pltpu.VMEM((nh, n, LN), f32),
            pltpu.VMEM((nh, bk, LN), f32),
            pltpu.VMEM((nh, bk, LN), f32),
        ],
    )
    return pl.pallas_call(
        functools.partial(bwd_kernel, first=group * nh, nh=nh, bq=bq, bk=bk, n=n),
        out_shape=[
            pltpu.HBM((n, lanes_up(3 * nh * HD)), bf16),
            pltpu.HBM((8, LN), f32),
        ],
        grid_spec=spec,
        compiler_params=pltpu.CompilerParams(vmem_limit_bytes=48 << 20),
        cost_estimate=cost(300 if group == 0 else 0.001),
        name="attn_bwd",
    )(block_flags(seg_row, bq, bk), mine.reshape(1), hbm(qa), hbm(kv), hbm(kv), *pieces, hbm(of), seg_row[:, None], seg_row[None], scale)


def quarter_columns(place, parts, groups, nh):
    width = nh // groups * HD
    return [
        (t * D + place * nh * HD + g * width, width) for g in range(groups) for t in range(3)
    ]


def pick_kernel(mine, w_ref, out, *, parts, groups, nh):
    for i in range(parts):

        @pl.when(mine[0] == i)
        def _(i=i):
            cut = [w_ref[:, a : a + width] for a, width in quarter_columns(i, parts, groups, nh)]
            used = sum(x.shape[1] for x in cut)
            pad = jnp.zeros((cut[0].shape[0], out.shape[1] - used), out.dtype)
            out[...] = jnp.concatenate(cut + [pad], axis=1)


def lanes_up(n):
    return -(-n // LN) * LN


def pick(w, mine, parts, groups, nh):
    rows = w.shape[0]
    step = 160 if rows % 160 == 0 else rows
    return pl.pallas_call(
        functools.partial(pick_kernel, parts=parts, groups=groups, nh=nh),
        out_shape=pltpu.HBM((rows, lanes_up(3 * nh * HD)), w.dtype),
        grid_spec=pltpu.PrefetchScalarGridSpec(
            num_scalar_prefetch=1,
            grid=(rows // step,),
            in_specs=[pl.BlockSpec((step, 3 * D), lambda i, m: (i, 0))],
            out_specs=pl.BlockSpec((step, lanes_up(3 * nh * HD)), lambda i, m: (i, 0)),
        ),
        cost_estimate=cost(5),
        name="pick",
    )(mine.reshape(1), hbm(w))


def stretch_kernel(x_ref, out, *, groups, nh):
    value = x_ref[...]
    each = 3 * nh * HD // groups
    zero = jnp.zeros((value.shape[0], LN - HD), value.dtype)
    per = nh // groups
    wide = []
    for t in range(3):
        for h in range(nh):
            at = (h // per) * each + t * per * HD + (h % per) * HD
            wide += [value[:, at : at + HD], zero]
    out[...] = jnp.concatenate(wide, axis=1)


def stretch(x, groups, nh, us):
    rows, width = x.shape
    step = 160
    return pl.pallas_call(
        functools.partial(stretch_kernel, groups=groups, nh=nh),
        out_shape=pltpu.HBM((rows, 3 * nh * LN), x.dtype),
        grid=(rows // step,),
        in_specs=[pl.BlockSpec((step, width), lambda i: (i, 0))],
        out_specs=pl.BlockSpec((step, 3 * nh * LN), lambda i: (i, 0)),
        cost_estimate=cost(us),
        name="stretch",
    )(hbm(x))


def order_kernel(own_first, a_ref, b_ref, out):
    half = pl.program_id(0)

    @pl.when(half == 0)
    def _():
        out[...] = a_ref[...].T

    @pl.when(half == 1)
    def _():
        out[...] = b_ref[...].T


def order(own, other, own_at):
    rows, width = own.shape
    step = 256
    return pl.pallas_call(
        order_kernel,
        out_shape=pltpu.HBM((width, 2 * rows), own.dtype),
        grid_spec=pltpu.PrefetchScalarGridSpec(
            num_scalar_prefetch=1,
            grid=(2, width // step),
            in_specs=[
                pl.BlockSpec((rows, step), lambda i, j, m: (0, j * (1 - i))),
                pl.BlockSpec((rows, step), lambda i, j, m: (0, j * i)),
            ],
            out_specs=pl.BlockSpec((step, rows), lambda i, j, m: (j, i ^ m[0])),
        ),
        cost_estimate=cost(200.0),
        name="order",
    )(own_at.reshape(1), hbm(own), hbm(other))


def transpose_kernel(x_ref, out):
    out[...] = x_ref[...].T


def transpose(x):
    rows, cols = x.shape
    step = 256
    return pl.pallas_call(
        transpose_kernel,
        out_shape=pltpu.HBM((cols, rows), x.dtype),
        grid=(rows // step,),
        in_specs=[pl.BlockSpec((step, cols), lambda i: (i, 0))],
        out_specs=pl.BlockSpec((cols, step), lambda i: (0, i)),
        cost_estimate=CHEAP,
        name="transpose",
    )(hbm(x))


def project_kernel(info, *refs, count, halves, width, fresh):
    pairs = refs[: 2 * count]
    gain = refs[2 * count]
    weights = refs[2 * count + 1 : 2 * count + 1 + halves]
    scale, ones = refs[2 * count + 1 + halves : 2 * count + 3 + halves]
    normed_ref, q_ref, kv_ref, mine_ref, w = refs[-5:]
    j, tile = pl.program_id(0), pl.program_id(1)
    step = normed_ref.shape[0]

    @pl.when((j == 0) & (tile == 0))
    def _():
        for i, ref in enumerate(weights):
            h = ref.shape[0]
            start = (info[count + 2] ^ i) * h if halves == 2 else 0
            w[pl.ds(pl.multiple_of(start, 16), h), :] = ref[...]
        if not fresh:
            mine_ref[...] = refs[2 * count + 3 + halves][...]

    def work(x_ref):
        value = x_ref[...]
        x = value.astype(f32)
        inverse = lax.rsqrt(jnp.mean(x * x, axis=-1, keepdims=True) + epsilon)
        normed = (x * inverse * gain[...]).astype(bf16)
        normed_ref[...] = normed
        q_ref[...] = (
            jnp.dot(normed, w[:, :width], preferred_element_type=f32) * scale[...]
        ).astype(bf16)
        kv_ref[...] = (
            jnp.dot(normed, w[:, width:], preferred_element_type=f32) + ones[...]
        ).astype(bf16)

        @pl.when(info[count + 1] == info[j])
        def _():
            mine_ref[pl.ds(pl.multiple_of(tile * step, step), step), :] = value

    for i in range(count):
        for lane in range(2):

            @pl.when((j == i) & (info[count] == lane))
            def _(i=i, lane=lane):
                work(pairs[2 * i + 1 - lane])


def project(pairs, places, lane, mine, wt, gain, weights, scale, ones, group_len, carried=None):
    count = len(pairs)
    rows, d = pairs[0][0].shape
    width = scale.shape[1]
    step = 256
    tiles = rows // step
    full = lambda j, t, f: (0, 0)
    at = lambda j, t, f: (f[j] * tiles + t, 0)
    once = pl.Buffered(1)
    info = jnp.stack(list(places) + [lane.astype(jnp.int32), mine, wt])
    args = [x for pair in pairs for x in pair] + [gain, *map(hbm, weights), scale, ones]
    in_specs = [
        pl.BlockSpec(
            (step, d),
            lambda j, t, f, i=i: (jnp.where(j == i, t, jnp.where(j > i, tiles - 1, 0)), 0),
        )
        for i in range(count)
        for _ in range(2)
    ]
    in_specs += [pl.BlockSpec((1, d), full, pipeline_mode=once)]
    in_specs += [pl.BlockSpec(w.shape, full, pipeline_mode=once) for w in weights]
    in_specs += [
        pl.BlockSpec((1, width), full, pipeline_mode=once),
        pl.BlockSpec((1, 2 * width), full, pipeline_mode=once),
    ]
    aliases = {}
    if carried is not None:
        base = len(args) + 2
        args += [hbm(x) for x in (carried[3], *carried[:3])]
        in_specs += [pl.BlockSpec((rows, d), full, pipeline_mode=once)]
        in_specs += [pl.BlockSpec(memory_space=pl.ANY)] * 3
        aliases = {base: 0, base + 1: 1, base + 2: 2}
    return pl.pallas_call(
        functools.partial(
            project_kernel, count=count, halves=len(weights), width=width, fresh=carried is None
        ),
        out_shape=[
            pltpu.HBM((group_len, d), bf16),
            pltpu.HBM((group_len, width), bf16),
            pltpu.HBM((group_len, 2 * width), bf16),
            pltpu.HBM((rows, d), bf16),
        ],
        grid_spec=pltpu.PrefetchScalarGridSpec(
            num_scalar_prefetch=1,
            grid=(count, tiles),
            in_specs=in_specs,
            out_specs=[
                pl.BlockSpec((step, d), at),
                pl.BlockSpec((step, width), at),
                pl.BlockSpec((step, 2 * width), at),
                pl.BlockSpec((rows, d), full),
            ],
            scratch_shapes=[pltpu.VMEM((d, 3 * width), bf16)],
        ),
        input_output_aliases=aliases,
        compiler_params=pltpu.CompilerParams(vmem_limit_bytes=48 << 20),
        cost_estimate=cost(15),
        name="project",
    )(info, *args)


def tail_body(at, p0, p1, p2, p3, x_ref, g_ref, w_s, gain, outs, need):
    lo_ref, left_ref, right_ref, gr_ref, c0, c1, c2, c3, gg_ref = outs
    att_ref, nm_ref, act_ref = (left_ref.at[i] for i in range(3))
    gp_ref, gh_ref = (right_ref.at[i] for i in range(2))
    right_ref[2] = g_ref[...]
    mine = at[0]
    pieces = (p0, p1, p2, p3)
    cols = p0.shape[1]
    nt = (((1,), (1,)), ((), ()))
    for i in range(4):

        @pl.when(mine == i)
        def _(i=i):
            att_ref[...] = jnp.concatenate([pieces[i ^ k][...] for k in range(4)], axis=1)

    need(0)
    resid = x_ref[...].astype(f32) + jnp.dot(att_ref[...], w_s[0], preferred_element_type=f32)
    inverse = lax.rsqrt(jnp.mean(resid * resid, axis=-1, keepdims=True) + epsilon)
    normed = (resid * inverse * gain[...]).astype(bf16)
    nm_ref[...] = normed
    need(1)
    hidden = jnp.dot(normed, w_s[1], preferred_element_type=f32)
    sig = 1.0 / (1.0 + jnp.exp(-hidden))
    active = (hidden * sig).astype(bf16)
    act_ref[...] = active
    need(2)
    lo_ref[...] = (resid + jnp.dot(active, w_s[2], preferred_element_type=f32)).astype(bf16)
    grad_active = lax.dot_general(g_ref[...], w_s[2], nt, preferred_element_type=f32)
    grad_hidden = (grad_active * sig * (1.0 + hidden * (1.0 - sig))).astype(bf16)
    gh_ref[...] = grad_hidden
    grad_normed = lax.dot_general(grad_hidden, w_s[1], nt, preferred_element_type=f32)
    gg_ref[...] += jnp.sum(grad_normed * resid * inverse, axis=0, keepdims=True)
    scaled = grad_normed * gain[...]
    grad_resid = (
        g_ref[...].astype(f32)
        + inverse * scaled
        - resid * (inverse * inverse * inverse) * jnp.mean(scaled * resid, axis=-1, keepdims=True)
    )
    gr_ref[...] = grad_resid
    grad_proj = grad_resid.astype(bf16)
    gp_ref[...] = grad_proj
    grad_att = lax.dot_general(grad_proj, w_s[0], nt, preferred_element_type=f32).astype(bf16)
    for i in range(4):

        @pl.when(mine == i)
        def _(i=i):
            for j, out in enumerate((c0, c1, c2, c3)):
                out[...] = grad_att[:, (i ^ j) * cols : ((i ^ j) + 1) * cols]


def tail_kernel(at, p0, p1, p2, p3, x_ref, g_ref, own0, own1, own2, half, other, gain, *refs, rows, hrows):
    w_s, sems = refs[-2:]
    outs = refs[:-2]

    def copies(i):
        parts = (((own0, own1, own2)[i], at[1], rows), (half.at[i], at[2], hrows), (other.at[i], at[3], hrows))
        return [
            pltpu.make_async_copy(
                part, w_s.at[i, pl.ds(pl.multiple_of(start, 16), n), :], sems.at[3 * i + k]
            )
            for k, (part, start, n) in enumerate(parts)
        ]

    @pl.when(pl.program_id(0) == 0)
    def _():
        outs[-1][...] = jnp.zeros_like(outs[-1])
        for i in range(3):
            for c in copies(i):
                c.start()

    def need(i):
        @pl.when(pl.program_id(0) == 0)
        def _():
            for c in copies(i):
                c.wait()

    tail_body(at, p0, p1, p2, p3, x_ref, g_ref, w_s, gain, outs, need)


def whole_tail_kernel(at, p0, p1, p2, p3, x_ref, g_ref, w, gain, *outs):
    @pl.when(pl.program_id(0) == 0)
    def _():
        outs[-1][...] = jnp.zeros_like(outs[-1])

    tail_body(at, p0, p1, p2, p3, x_ref, g_ref, w, gain, outs, lambda i: None)


def tail(at, pieces, x, g, weights, gain, tile=256):
    rows, d = x.shape
    cols = pieces[0].shape[1]
    row = lambda i, m: (i, 0)
    once = pl.Buffered(1)
    whole = lambda *shape: pl.BlockSpec(shape, lambda i, m: (0,) * len(shape), pipeline_mode=once)
    wide = pl.BlockSpec((tile, d), row)
    slim = pl.BlockSpec((tile, cols), row)
    if len(weights) == 5:
        body = functools.partial(tail_kernel, rows=weights[0].shape[0], hrows=weights[3].shape[1])
        scratch = [pltpu.VMEM((3, d, d), bf16), pltpu.SemaphoreType.DMA((9,))]
        weight_specs = [pl.BlockSpec(memory_space=pl.ANY)] * 5
    else:
        body = whole_tail_kernel
        scratch = []
        weight_specs = [whole(*w.shape) for w in weights]
    return pl.pallas_call(
        body,
        out_shape=[pltpu.HBM((rows, d), bf16)]
        + [pltpu.HBM((3, rows, d), bf16)] * 2
        + [pltpu.HBM((rows, d), f32)]
        + [pltpu.HBM((rows, cols), bf16)] * 4
        + [pltpu.HBM((1, d), f32)],
        grid_spec=pltpu.PrefetchScalarGridSpec(
            num_scalar_prefetch=1,
            grid=(rows // tile,),
            in_specs=[slim] * 4 + [wide] * 2 + weight_specs + [whole(1, d)],
            out_specs=[wide]
            + [pl.BlockSpec((3, tile, d), lambda i, m: (0, i, 0))] * 2
            + [wide]
            + [slim] * 4
            + [pl.BlockSpec((1, d), lambda i, m: (0, 0))],
            scratch_shapes=scratch,
        ),
        compiler_params=pltpu.CompilerParams(vmem_limit_bytes=52 << 20),
        cost_estimate=cost(0.01),
        name="tail",
    )(at, *pieces, hbm(x), g, *map(hbm, weights), gain)


tn_dims = (((0,), (0,)), ((), ()))


def share_kernel(col, left, right, out):
    value = lax.dot_general(left[0], right[0], tn_dims, preferred_element_type=f32)
    out[...] = value.astype(bf16)


def share(left, right, col):
    n, rows, d = left.shape
    w = d // 2
    block = pl.BlockSpec((d, w), lambda i, c: (0, i))
    return pl.pallas_call(
        share_kernel,
        out_shape=pltpu.HBM((d, n * w), bf16),
        grid_spec=pltpu.PrefetchScalarGridSpec(
            num_scalar_prefetch=1,
            grid=(n,),
            in_specs=[
                pl.BlockSpec((1, rows, d), lambda i, c: (i, 0, 0)),
                pl.BlockSpec((1, rows, w), lambda i, c: (i, 0, c[0])),
            ],
            out_specs=block,
        ),
        compiler_params=pltpu.CompilerParams(vmem_limit_bytes=40 << 20),
        cost_estimate=CHEAP,
        name="share",
    )(col.reshape(1), hbm(left), hbm(right))


def copy(x):
    return pl.pallas_call(
        tick_kernel, out_shape=pltpu.HBM(x.shape, x.dtype), cost_estimate=CHEAP, name="copy"
    )(x)


def tick_kernel(x_ref, out):
    out[...] = x_ref[...]


def tick(x):
    return pl.pallas_call(
        tick_kernel, out_shape=jax.ShapeDtypeStruct(x.shape, x.dtype), cost_estimate=cost(200.0), name="tick"
    )(x)


def total_kernel(*refs, counts):
    out = refs[-1]
    start, column = 0, 0
    for count in counts:
        group = refs[start : start + count]
        start += count
        acc = jnp.zeros(group[0].shape[1:], f32)
        for ref in group:
            for i in range(ref.shape[0]):
                acc = acc + ref[i].astype(f32)
        out[:, column : column + acc.shape[1]] = acc.astype(bf16)
        column += acc.shape[1]


def total(groups):
    flat = [x for group in groups for x in group]
    rows = flat[0].shape[1]
    cuts = 2 if rows % 32 == 0 else 1
    width = sum(group[0].shape[2] for group in groups)
    return pl.pallas_call(
        functools.partial(total_kernel, counts=[len(group) for group in groups]),
        out_shape=pltpu.HBM((rows, width), bf16),
        grid=(cuts,),
        in_specs=[
            pl.BlockSpec((x.shape[0], rows // cuts, x.shape[2]), lambda i: (0, i, 0)) for x in flat
        ],
        out_specs=pl.BlockSpec((rows // cuts, width), lambda i: (i, 0)),
        compiler_params=pltpu.CompilerParams(vmem_limit_bytes=40 << 20),
        cost_estimate=cost(0.001),
        name="total",
    )(*flat)


def add_kernel(a_ref, b_ref, out):
    out[...] = (a_ref[...].astype(f32) + b_ref[...].astype(f32)).astype(bf16)


def add(a, b):
    return pl.pallas_call(
        add_kernel, out_shape=pltpu.HBM(a.shape, bf16), cost_estimate=CHEAP, name="add"
    )(a, b)


def add_rows(a, b):
    rows, cols = a.shape
    block = pl.BlockSpec((rows // 5, cols), lambda i: (i, 0))
    return pl.pallas_call(
        add_kernel,
        out_shape=pltpu.HBM(a.shape, bf16),
        grid=(5,),
        in_specs=[block] * 2,
        out_specs=block,
        compiler_params=pltpu.CompilerParams(vmem_limit_bytes=24 << 20),
        cost_estimate=CHEAP,
        name="add_rows",
    )(hbm(a), hbm(b))


def by_bits(first, second, put):
    for i in range(2):
        for j in range(2):

            @pl.when((first == i) & (second == j))
            def _(i=i, j=j):
                put(i, j)


def place_kernel(at, *refs):
    o0, o1, o2 = refs[-3:]
    block = pl.program_id(0)
    w = o0.shape[2] // 2

    def put(other_x, other_near):
        for core in range(2):

            @pl.when(at[2] == core)
            def _(core=core):
                for side in range(2):
                    part = refs[4 * (side ^ core) + 2 * other_x + other_near][...].astype(f32)
                    for i, out in enumerate((o0, o1, o2)):
                        out[0, :, side * w : (side + 1) * w] = part[:, i * w : (i + 1) * w]

    by_bits((block // 2) ^ at[0], (block % 2) ^ at[1], put)


def place_tail(arrays, at):
    h, width = arrays[0].shape
    d = width // 3 * 2
    whole = pl.BlockSpec((h, width), lambda i, m: (0, 0), pipeline_mode=pl.Buffered(1))
    outs = pl.pallas_call(
        place_kernel,
        out_shape=[pltpu.HBM((4, h, d), f32)] * 3,
        grid_spec=pltpu.PrefetchScalarGridSpec(
            num_scalar_prefetch=1,
            grid=(4,),
            in_specs=[whole] * 8,
            out_specs=[pl.BlockSpec((1, h, d), lambda i, m: (i, 0, 0))] * 3,
        ),
        compiler_params=pltpu.CompilerParams(vmem_limit_bytes=40 << 20),
        cost_estimate=CHEAP,
        name="place_tail",
    )(at, *arrays)
    return [out.reshape(4 * h, d) for out in outs]


def cross_kernel(at, x_ref, g_ref, *refs):
    s = refs[-1]
    s[...] = jnp.dot(x_ref[...], g_ref[...], preferred_element_type=f32)
    half = s.shape[0] // 2
    for w in range(2):

        @pl.when(pl.program_id(0) == w)
        def _(w=w):
            for x in range(2):
                rows = pl.ds(pl.multiple_of((at[1] ^ x) * half, 16), half)
                refs[2 * w + x][...] = s[rows, :].astype(bf16)


def cross(x, g, at):
    d, rows = x.shape
    w = d // 2
    cols = g.shape[1]
    step = 512 if cols % 512 == 0 else cols
    n = cols // step
    first = pl.BlockSpec((w // 2, step), lambda i, j, m: (0, jnp.where(i == 0, j, n - 1)))
    second = pl.BlockSpec((w // 2, step), lambda i, j, m: (0, jnp.where(i == 1, j, 0)))
    return pl.pallas_call(
        cross_kernel,
        out_shape=[pltpu.HBM((w // 2, cols), bf16)] * 4,
        grid_spec=pltpu.PrefetchScalarGridSpec(
            num_scalar_prefetch=1,
            grid=(2, n),
            in_specs=[
                pl.BlockSpec((w, rows), lambda i, j, m: (m[0] ^ i, 0)),
                pl.BlockSpec((rows, step), lambda i, j, m: (0, j)),
            ],
            out_specs=[first, first, second, second],
            scratch_shapes=[pltpu.VMEM((w, step), f32)],
        ),
        compiler_params=pltpu.CompilerParams(vmem_limit_bytes=40 << 20),
        cost_estimate=CHEAP,
        name="cross",
    )(at, hbm(x), hbm(g))


def spread_kernel(at, *refs, width):
    out = refs[-1]
    step = out.shape[1]
    rows = pl.ds(pl.multiple_of(pl.program_id(0) * step, step), step)

    def put(core, near):
        cut = []
        for t in range(3):
            for n in range(2):
                for c in range(2):
                    part = refs[2 * (c ^ core) + (n ^ near)][rows, :]
                    cut.append(part[:, t * width : (t + 1) * width])
        out[0] = jnp.concatenate(cut, axis=1).astype(f32)

    by_bits(at[2], at[1], put)


def spread(arrays, at, used, other_x, carried=None):
    rows, cols = arrays[0].shape
    width = 4 * used
    cuts = 2 if rows % 32 == 0 else 1
    whole = pl.BlockSpec((rows, cols), lambda j, m: (0, 0), pipeline_mode=pl.Buffered(1))
    more = () if carried is None else (carried,)
    return pl.pallas_call(
        functools.partial(spread_kernel, width=used // 3),
        out_shape=pltpu.HBM((2, rows, width), f32),
        grid_spec=pltpu.PrefetchScalarGridSpec(
            num_scalar_prefetch=1,
            grid=(cuts,),
            in_specs=[whole] * 4 + [pl.BlockSpec(memory_space=pl.ANY)] * len(more),
            out_specs=pl.BlockSpec((1, rows // cuts, width), lambda j, m: (m[0] ^ other_x, j, 0)),
        ),
        input_output_aliases={5: 0} if more else {},
        compiler_params=pltpu.CompilerParams(vmem_limit_bytes=40 << 20),
        cost_estimate=CHEAP,
        name="spread",
    )(at, *arrays, *more)


def back_kernel(shards, g_ref, w_ref, *refs):
    acc = jnp.dot(g_ref[...], w_ref[...], preferred_element_type=f32)
    if len(refs) == 2:
        acc = acc + refs[0][0].astype(f32)
    refs[-1][0] = acc.astype(bf16)


def back(grad, w, shards, rows, got=None):
    c, d = w.shape
    n = shards.shape[0]
    step = d
    out = pl.BlockSpec((1, rows, step), lambda j, i, f: (i, 0, j))
    in_specs = [
        pl.BlockSpec((rows, c), lambda j, i, f: (f[i], 0)),
        pl.BlockSpec((c, step), lambda j, i, f: (0, j)),
    ]
    args = [hbm(grad), hbm(w)]
    if got is not None:
        in_specs.append(pl.BlockSpec((1, rows, step), lambda j, i, f: (0, 0, j)))
        args.append(got)
    return pl.pallas_call(
        back_kernel,
        out_shape=pltpu.HBM((n, rows, d), bf16),
        grid_spec=pltpu.PrefetchScalarGridSpec(
            num_scalar_prefetch=1, grid=(d // step, n), in_specs=in_specs, out_specs=out
        ),
        compiler_params=pltpu.CompilerParams(vmem_limit_bytes=40 << 20),
        cost_estimate=CHEAP,
        name="back",
    )(shards, *args)


def finish_kernel(shard, g_ref, w_ref, core, near, x_ref, resid, gain, out, gain_out):
    grad = jnp.dot(g_ref[...], w_ref[...], preferred_element_type=f32)
    grad = grad + core[0].astype(f32) + near[0].astype(f32)
    x = x_ref[...].astype(f32)
    inverse = lax.rsqrt(jnp.mean(x * x, axis=-1, keepdims=True) + epsilon)
    part = jnp.sum(grad * x * inverse, axis=0, keepdims=True)

    @pl.when(pl.program_id(0) == 0)
    def _():
        gain_out[...] = jnp.zeros_like(gain_out)

    gain_out[...] += part
    scaled = grad * gain[...]
    out[...] = (
        resid[...]
        + inverse * scaled
        - x * (inverse * inverse * inverse) * jnp.mean(scaled * x, axis=-1, keepdims=True)
    ).astype(bf16)


def finish(grad, w, shard, core, near, x, resid, gain, tile=256):
    rows, d = x.shape
    c = w.shape[0]
    tiles = rows // tile
    row = lambda i, f: (i, 0)
    once = pl.Buffered(1)
    return pl.pallas_call(
        finish_kernel,
        out_shape=[pltpu.HBM((rows, d), bf16), jax.ShapeDtypeStruct((1, d), f32)],
        grid_spec=pltpu.PrefetchScalarGridSpec(
            num_scalar_prefetch=1,
            grid=(tiles,),
            in_specs=[
                pl.BlockSpec((tile, c), lambda i, f: (f[0] * tiles + i, 0)),
                pl.BlockSpec((c, d), lambda i, f: (0, 0), pipeline_mode=once),
                pl.BlockSpec((1, tile, d), lambda i, f: (1, i, 0)),
                pl.BlockSpec((1, tile, d), lambda i, f: (0, i, 0)),
                pl.BlockSpec((tile, d), row),
                pl.BlockSpec((tile, d), row),
                pl.BlockSpec((1, d), lambda i, f: (0, 0)),
            ],
            out_specs=[pl.BlockSpec((tile, d), row), pl.BlockSpec((1, d), lambda i, f: (0, 0))],
        ),
        compiler_params=pltpu.CompilerParams(vmem_limit_bytes=40 << 20),
        cost_estimate=CHEAP,
        name="finish",
    )(shard.reshape(1), hbm(grad), hbm(w), core, near, hbm(x), hbm(resid), gain)


def rms_inverse(values):
    return lax.rsqrt(jnp.mean(values * values, axis=-1, keepdims=True) + epsilon)


def norm_back(values, inverse, grad_scaled):
    return inverse * grad_scaled - values * (inverse * inverse * inverse) * jnp.mean(
        grad_scaled * values, axis=-1, keepdims=True
    )


def dot(left, right):
    return jnp.dot(left, right, preferred_element_type=f32)


def times_trans(left, right):
    return lax.dot_general(left, right, (((1,), (1,)), ((), ())), preferred_element_type=f32)


def trans_times(left, right):
    return lax.dot_general(left, right, (((0,), (0,)), ((), ())), preferred_element_type=f32)


def rows_at(array, start, count):
    return lax.dynamic_slice_in_dim(array, start, count, 0)


def put_rows(array, rows, start):
    return lax.dynamic_update_slice_in_dim(array, rows, start, 0)


def make_local(sizes):
    def pairs(target):
        found = []
        for gx in range(sizes["gx"]):
            for gc in range(sizes["gc"]):
                for z in range(4):
                    for w in range(sizes["wt"]):
                        goal = target(gx, gc, z, w)
                        if goal is not None and goal != (gx, gc, z, w):
                            found.append((place(gx, gc, z, w), place(*goal)))
        return found

    def place(gx, gc, z, w):
        return ((gx * sizes["gc"] + gc) * 4 + z) * sizes["wt"] + w

    def send(value, target):
        return lax.ppermute(value, AXES, pairs(target))

    def core_mate(gx, gc, z, w):
        return (gx, 1 - gc, z, w)

    def x_mate(gx, gc, z, w):
        return (1 - gx, gc, z, w)

    def near_mate(gx, gc, z, w):
        return (gx, gc, z ^ 1, w)

    def far_mate(gx, gc, z, w):
        return (gx, gc, z ^ 2, w)

    def cross_mate(gx, gc, z, w):
        return (gx, 1 - gc, z ^ 1, w)

    def wt_mate(gx, gc, z, w):
        return (gx, gc, z, 1 - w)

    def wt_x_mate(gx, gc, z, w):
        return (1 - gx, gc, z, 1 - w)

    def to_host(gx, gc, z, w):
        return (gx, 1 - (z & 1), 2 * gc + (z >> 1), w)

    def to_home(gx, gc, z, w):
        return (gx, z >> 1, 2 * (z & 1) + 1 - gc, w)

    def hop1(gx, gc, z, w):
        if gc == 0:
            return (gx, 0, z - 1, w) if z > 0 else None
        return (gx, 1, z + 1, w) if z < 3 else None

    def hop2(gx, gc, z, w):
        if gc == 0:
            return (gx, 0, z - 1, w) if z in (1, 2) else None
        return (gx, 1, z + 1, w) if z in (1, 2) else None

    def hop3(gx, gc, z, w):
        if gc == 0:
            return (gx, 0, z ^ 1, w) if z < 2 else None
        return (gx, 1, z ^ 1, w) if z > 1 else None

    def lane_share(gx, gc, z, w):
        return (gx, 1 - gc, z, w) if gc == z >> 1 else None

    def sum_all(value):
        for axis in ("gc", "wt", "near", "far", "gx"):
            step = 1
            while step < sizes[axis]:

                def mate(gx, gc, z, w, axis=axis, step=step):
                    at = dict(gx=gx, gc=gc, far=z >> 1, near=z & 1, wt=w)
                    at[axis] ^= step
                    return (at["gx"], at["gc"], 2 * at["far"] + at["near"], at["wt"])

                value = value + send(value, mate)
                step *= 2
        return value

    def local(
        tokens, segments, w_qkv, w_proj, w_in, w_out, gain_attn, gain_mlp, query_scale, cotangent
    ):
        gx, gc, host, near, wt = (lax.axis_index(axis) for axis in AXES)
        z = 2 * host + near
        mine = 2 * near + 1 - gc
        parts = 4
        nh = H // parts
        groups = 1
        rows = tokens.shape[1]
        group_len = segments.shape[1]
        wrows = w_qkv.shape[0]
        lane = gc == host
        pair = sizes["wt"] == 2

        def after(value, *others):
            return lax.optimization_barrier((value,) + others)[0]

        picked = pick(w_qkv, mine, parts, groups, nh)
        own = tokens[0]
        got1 = send(own, hop1)
        own_share = send(own, lane_share)
        seg_mate = send(segments, core_mate)
        got2 = send(got1, hop2)
        got1_share = send(got1, lane_share)
        end = jnp.where(gc == 0, z == 0, z == 3)
        if pair:
            wide_own = stretch(picked, groups, nh, 2)
            got1 = after(got1, wide_own)
            other_w = send(picked, wt_mate)
            wide_w = (wide_own, stretch(other_w, groups, nh, 10))
        else:
            flat_all = lax.all_gather(picked, "wt", axis=0, tiled=True)
            by_head = jnp.transpose(
                flat_all[:, : 3 * nh * HD].reshape(D, groups, 3, nh // groups, HD), (0, 2, 1, 3, 4)
            )
            wide_w = (
                jnp.pad(
                    by_head.reshape(D, 3 * nh, HD), ((0, 0), (0, 0), (0, LN - HD))
                ).reshape(D, -1),
            )
        got3 = send(jnp.where(end, own, got2), hop3)
        got2_share = send(got2, lane_share)
        way = 1 - 2 * host
        last = jnp.where(host == 0, jnp.where(z == 0, 3, 0), jnp.where(z == 3, 0, 3))
        places = (z, z + way, z + 2 * way, last)

        half_rows = wrows // 2
        half_w = jnp.stack([rows_at(w, gc * half_rows, half_rows) for w in (w_proj, w_in, w_out)])
        if pair:
            half_w = send(after(half_w, other_w), wt_mate)
        else:
            half_w = lax.all_gather(half_w, "wt", axis=0, tiled=False)

        dim_scale = scale_base / math.sqrt(HD) * jax.nn.softplus(query_scale)
        lane_scale = jnp.tile(jnp.pad(dim_scale * log2e, (0, LN - HD)), nh)[None]
        ones = jnp.tile(
            ((jnp.arange(LN) >= HD) & (jnp.arange(LN) < HD + 3)).astype(f32), 2 * nh
        )[None]
        seg_row = jnp.where(lane, segments, seg_mate)[0]
        fixed = (lane, mine, wt, gain_attn[None], wide_w, lane_scale, ones, group_len)
        carried = project(((own, own_share), (got1, got1_share)), places[:2], *fixed)
        got3_share = send(after(got3, carried[0]), lane_share)
        all_normed, queries, keyval, inputs = project(
            ((got2, got2_share), (got3, got3_share)), places[2:], *fixed, carried=carried
        )
        grad_mlp = send(after(cotangent[0], got3_share), to_host)

        att, att_float, q_aug = attn_fwd(queries, keyval, seg_row, nh)
        att, half_w, _ = lax.optimization_barrier((att, half_w, grad_mlp))

        trades = (core_mate, near_mate, cross_mate)
        att_pieces = [rows_at(att, (mine ^ j) * rows, rows) for j in range(parts)]
        half_mate = send(after(half_w, *att_pieces), core_mate)
        att_pieces = [att_pieces[0]] + [send(att_pieces[j + 1], trades[j]) for j in range(3)]
        if pair:
            w_trans = order(after(picked, att), other_w, wt)
        else:
            w_trans = flat_all.T
        normed_trans = transpose(after(all_normed, w_trans))
        if pair:
            weights = (w_proj, w_in, w_out, half_w, half_mate)
            starts = (wt * wrows, (1 - wt) * wrows + gc * half_rows, (1 - wt) * wrows + (1 - gc) * half_rows)
        else:
            one = gc == 0
            tail_w = jnp.stack(
                [jnp.where(one, half_w, half_mate), jnp.where(one, half_mate, half_w)], axis=1
            )
            weights = (jnp.transpose(tail_w, (2, 0, 1, 3, 4)).reshape(3, D, D),)
            starts = ()
        (
            layer_out,
            left,
            right,
            grad_resid,
            *pieces,
            grad_gain_mlp,
        ) = tail(
            jnp.stack([mine, *starts]), att_pieces, after(inputs, normed_trans), grad_mlp, weights, gain_mlp[None]
        )
        pieces = [pieces[0]] + [send(pieces[j + 1], trades[j]) for j in range(3)]

        shared = share(after(left, pieces[1]), right, 1 - gc)
        from_core = send(shared, core_mate)
        own_half = share(left, right, after(gc, shared))
        pieces[2:] = [after(piece, own_half) for piece in pieces[2:]]
        home_out = send(after(layer_out, *pieces[1:]), to_home)
        late_gain = tick(after(gain_attn.reshape(-1, LN), *pieces[1:]))
        summed = add_rows(own_half, after(from_core, late_gain))
        kept = lax.all_to_all(summed, ("wt", "gx", "near"), 0, 0, tiled=True)

        scale_row = jnp.tile(dim_scale, nh // groups)[None]

        def backward(group, *others):
            first, *rest = pieces
            return attn_bwd(
                q_aug,
                keyval,
                (after(first, summed, *others), *rest),
                att_float,
                mine,
                seg_row,
                scale_row,
                nh,
                group,
                groups,
            )

        def by_rows(grad):
            if pair:
                own, *rest = cross(normed_trans, grad, jnp.stack([wt, gx]))
                got = [send(part, mate) for part, mate in zip(rest, (x_mate, wt_mate, wt_x_mate))]
                return [part[None] for part in (own, *got)]
            part = dot(normed_trans, grad).astype(bf16)
            sources = sizes["wt"] * 2
            got = lax.all_to_all(part, ("wt", "gx"), 0, 0, tiled=True)
            return [got.reshape(sources, D // sources, -1)]

        grad_project, grad_lanes = backward(0)
        layer_out = after(home_out, grad_project)

        last_step = [layer_out]

        def turn(value):
            return after(value, *last_step)

        def done(value):
            last_step[0] = value
            return value

        sources = sizes["wt"] * 4
        to_core = done(back(turn(grad_project), w_trans, jnp.stack([mine ^ 3, mine ^ 1]), rows))
        from_core = send(to_core, core_mate)
        by_place = by_rows(turn(grad_project))
        done(by_place[0])
        to_near = done(back(grad_project, w_trans, (mine ^ 2).reshape(1), rows, turn(from_core)))
        from_near = send(to_near, near_mate)
        t1 = done(total([[turn(kept).reshape(sources, D // sources, -1)]]))
        t1_far = send(t1, far_mate)
        layer_out = done(copy(turn(layer_out)))
        by_place[0] = turn(by_place[0])
        q1 = done(total([by_place]))
        q1_far = send(q1, far_mate)
        t2 = done(add(turn(t1), t1_far))
        t2_near = send(t2, near_mate)
        t2_x = send(t2, x_mate)
        grad_tokens, grad_gain_attn = finish(
            grad_project,
            w_trans,
            mine,
            from_core,
            turn(from_near),
            inputs,
            grad_resid,
            late_gain.reshape(1, -1),
        )
        done(grad_tokens)
        grad_query_scale = (
            grad_lanes[0, :HD]
            / (dim_scale * log2e)
            * (scale_base / math.sqrt(HD))
            * jax.nn.sigmoid(query_scale)
        )
        small = jnp.concatenate(
            [grad_gain_attn[0], grad_gain_mlp[0], jnp.pad(grad_query_scale, (0, LN - HD))]
        ).reshape(-1, LN)
        t2_x = done(turn(t2_x))
        t2_near = done(turn(t2_near))
        t2_near_x = send(t2_near, x_mate)
        tails = [t2, t2_near, t2_x]
        tails_mate = [send(turn(x), core_mate) for x in tails]
        q2 = done(add(turn(q1), q1_far))
        q2_near = send(q2, near_mate)
        q2_x = send(q2, x_mate)
        home_grad = send(turn(grad_tokens), to_home)
        q2_near = done(turn(q2_near))
        q2_near_x = send(q2_near, x_mate)
        t2_near_x = done(turn(t2_near_x))
        tails += [t2_near_x]
        tails_mate += [send(t2_near_x, core_mate)]
        q2_x = done(turn(q2_x))
        quads_mate = [send(turn(x), core_mate) for x in (q2, q2_near, q2_x)]
        tails_mate[3] = turn(tails_mate[3])
        totals = place_tail(tails + tails_mate, jnp.stack([gx, near, gc]))
        done(totals[0])
        used = 3 * nh * HD
        spread_at = jnp.stack([gx, near, 1 - gc])
        total_qkv = done(
            spread((turn(q2), q2_near, quads_mate[0], quads_mate[1]), spread_at, used, 0)
        )
        small = done(sum_all(turn(small))).reshape(-1)
        grad_tokens = done(copy(turn(home_grad)))
        q2_near_x = done(turn(q2_near_x))
        last_mate = send(q2_near_x, core_mate)
        total_qkv = spread(
            (q2_x, turn(q2_near_x), quads_mate[2], last_mate), spread_at, used, 1, total_qkv
        ).reshape(wrows, 3 * D)
        return (
            layer_out[None],
            grad_tokens[None],
            total_qkv,
            *totals,
            small[:D],
            small[D : 2 * D],
            small[2 * D : 2 * D + HD],
        )

    return local


def solution(mesh):
    groups, parts, wt = (mesh.shape[axis] for axis in ("grp", "ctx", "wt"))
    inner = Mesh(mesh.devices.reshape(groups // 2, 2, parts // 2, 2, wt), AXES)
    sizes = dict(inner.shape)
    split = P(("gx", "gc", "wt"), ("far", "near"), None)
    weight = P("wt", None)
    return jax.shard_map(
        make_local(sizes),
        mesh=inner,
        in_specs=(
            split,
            P(("gx", "gc", "wt"), None),
            weight,
            weight,
            weight,
            weight,
            P(),
            P(),
            P(),
            split,
        ),
        out_specs=(split, split, weight, weight, weight, weight, P(), P(), P()),
        check_vma=False,
    )
```

```python
import functools
import math

import jax
import jax.numpy as jnp
from jax import lax
from jax.experimental import pallas as pl
from jax.experimental.pallas import tpu as pltpu
from jax.sharding import Mesh
from jax.sharding import PartitionSpec as P

D = 1280
H = 16
HD = 80
LN = 128
epsilon = 1e-06
scale_base = 1.442695041
log2e = 1.4426950408889634
NEG = -1e30
def cost(us):
    return pl.CostEstimate(flops=int(us * 1_000_000_000), transcendentals=0, bytes_accessed=1000)


CHEAP = cost(0.001)
f32 = jnp.float32
bf16 = jnp.bfloat16
AXES = ("gx", "gc", "far", "near", "wt")


def hbm(x):
    return pltpu.with_memory_space_constraint(x, pltpu.HBM)


def block_flags(seg_row, bq, bk):
    n = seg_row.shape[0]
    q = seg_row.reshape(n // bq, bq)
    k = seg_row.reshape(n // bk, bk)
    qf, ql = q[:, 0][:, None], q[:, -1][:, None]
    kf, kl = k[:, 0][None], k[:, -1][None]
    qs = jnp.arange(n // bq, dtype=jnp.int32)[:, None] * bq
    ks = jnp.arange(n // bk, dtype=jnp.int32)[None] * bk
    below = ks + bk - 1 <= qs
    skip = (ks > qs + bq - 1) | ((kf > 0) & (kl < qf))
    same = (qf == ql) & (kl == ql) & ((kf == kl) | ((kf == 0) & (kl == 1)))
    full = below & ((kl == 0) | same)
    flags = jnp.where(skip, 0, jnp.where(full, 1, 2))
    if bq == bk:
        flags = jnp.where(qs == ks, 3, flags)
    return flags.astype(jnp.int32).reshape(-1)


def put_split(base, col, lanes):
    hi = col.astype(bf16).astype(f32)
    rest = col - hi
    mid = rest.astype(bf16).astype(f32)
    out = jnp.where(lanes == HD, hi, base)
    out = jnp.where(lanes == HD + 1, mid, out)
    return jnp.where(lanes == HD + 2, rest - mid, out).astype(bf16)


def fwd_kernel(flags, q_ref, kv, segc, segr, att, of, qaug, m_s, acc_s, *, nh, bq, bk, nk):
    qi = pl.program_id(0)
    count = (qi * bq + bq + bk - 1) // bk
    nt = (((1,), (1,)), ((), ()))
    acc_s[...] = jnp.zeros_like(acc_s)
    m_s[...] = jnp.zeros_like(m_s)

    def mask(ko, q0=0, qn=bq, kn=bk):
        qpos = qi * bq + q0 + lax.broadcasted_iota(jnp.int32, (qn, kn), 0)
        kpos = ko + lax.broadcasted_iota(jnp.int32, (qn, kn), 1)
        ks = segr[:, pl.ds(ko, kn)]
        return (kpos <= qpos) & ((ks == 0) | (ks == segc[q0 : q0 + qn, :]))

    def step(kb, masked, q0=0, qn=bq, kn=bk):
        ko = pl.multiple_of(kb * bk, bk)
        if masked:
            allowed = mask(ko, q0, qn, kn)
        rows = slice(q0, q0 + qn)
        for h in range(nh):
            k = kv[pl.ds(ko, kn), h * LN : (h + 1) * LN]
            v = kv[pl.ds(ko, kn), (nh + h) * LN : (nh + h + 1) * LN]
            q = q_ref[rows, h * LN : (h + 1) * LN]
            p = jnp.exp2(lax.dot_general(q, k, nt, preferred_element_type=f32))
            if masked:
                p = jnp.where(allowed, p, 0.0)
            acc_s[h, rows, :] += jnp.dot(p.astype(bf16), v, preferred_element_type=f32)

    def body(kb, carry):
        flag = flags[qi * nk + kb]

        @pl.when(flag == 1)
        def _():
            step(kb, False)

        @pl.when(flag >= 2)
        def _():
            step(kb, True)

        return carry

    lax.fori_loop(0, count, body, 0)
    bad = jnp.zeros((bq, 1), f32)
    for h in range(nh):
        total = acc_s[h][:, HD : HD + 1]
        bad = jnp.maximum(bad, jnp.where((total > 2.0**-60) & (total < 2.0**60), 0.0, 1.0))

    @pl.when(jnp.max(bad) > 0.0)
    def _():
        def head(h, carry):
            kc = pl.ds(pl.multiple_of(h * LN, LN), LN)
            vc = pl.ds(pl.multiple_of((nh + h) * LN, LN), LN)
            m_s[h] = jnp.full((bq, LN), NEG, f32)
            acc_s[h] = jnp.zeros((bq, LN), f32)

            def inner(kb, carry):
                @pl.when(flags[qi * nk + kb] > 0)
                def _():
                    ko = pl.multiple_of(kb * bk, bk)
                    s = lax.dot_general(
                        q_ref[:, kc], kv[pl.ds(ko, bk), kc], nt, preferred_element_type=f32
                    )
                    s = jnp.where(mask(ko), s, NEG)
                    old = m_s[h]
                    new = jnp.maximum(old, jnp.max(s, axis=1, keepdims=True))
                    p = jnp.exp2(s - new[:, :1]).astype(bf16)
                    m_s[h] = new
                    acc_s[h] = acc_s[h] * jnp.exp2(old - new) + jnp.dot(
                        p, kv[pl.ds(ko, bk), vc], preferred_element_type=f32
                    )

                return carry

            lax.fori_loop(0, count, inner, 0)
            return carry

        lax.fori_loop(0, nh, head, 0)

    lanes = lax.broadcasted_iota(jnp.int32, (bq, LN), 1)
    outs = []
    for h in range(nh):
        acc = acc_s[h]
        total = acc[:, HD : HD + 1]
        out = acc * (1.0 / total)
        of[:, h * LN : (h + 1) * LN] = jnp.where(lanes < HD, out, 0.0).astype(bf16)
        outs.append(out[:, :HD])
        lse = m_s[h][:, :1] + jnp.log2(total)
        qaug[:, h * LN : (h + 1) * LN] = put_split(
            q_ref[:, h * LN : (h + 1) * LN].astype(f32), -lse, lanes
        )
    att[...] = jnp.concatenate(outs, axis=1).astype(bf16)


def attn_fwd(q, kv, seg_row, nh, bq=512, bk=512):
    n = q.shape[0]
    w = nh * LN
    spec = pltpu.PrefetchScalarGridSpec(
        num_scalar_prefetch=1,
        grid=(n // bq,),
        in_specs=[
            pl.BlockSpec((bq, w), lambda i, f: (i, 0)),
            pl.BlockSpec((n, 2 * w), lambda i, f: (0, 0)),
            pl.BlockSpec((bq, 1), lambda i, f: (i, 0)),
            pl.BlockSpec((1, n), lambda i, f: (0, 0)),
        ],
        out_specs=[
            pl.BlockSpec((bq, nh * HD), lambda i, f: (i, 0)),
            pl.BlockSpec((bq, w), lambda i, f: (i, 0)),
            pl.BlockSpec((bq, w), lambda i, f: (i, 0)),
        ],
        scratch_shapes=[pltpu.VMEM((nh, bq, LN), f32), pltpu.VMEM((nh, bq, LN), f32)],
    )
    return pl.pallas_call(
        functools.partial(fwd_kernel, nh=nh, bq=bq, bk=bk, nk=n // bk),
        out_shape=[
            pltpu.HBM((n, nh * HD), bf16),
            pltpu.HBM((n, w), bf16),
            pltpu.HBM((n, w), bf16),
        ],
        grid_spec=spec,
        compiler_params=pltpu.CompilerParams(vmem_limit_bytes=28 << 20),
        cost_estimate=cost(0.01),
        name="attn_fwd",
    )(block_flags(seg_row, bq, bk), hbm(q), hbm(kv), seg_row[:, None], seg_row[None])


def bwd_kernel(
    flags, mine, qa, kk, vv, do0, do1, do2, do3, of, segc, segr, scale, dqkv, gscale, doa_s, dq_s, dk_s, dv_s, *, first, nh, bq, bk, n
):
    nk = n // bk
    nq = n // bq
    kb = pl.program_id(0)
    part = n // 4
    step_rows = 256 if part % 256 == 0 else part
    lanes = lax.broadcasted_iota(jnp.int32, (step_rows, LN), 1)

    @pl.when(kb == 0)
    def _():
        dq_s[...] = jnp.zeros_like(dq_s)
        for j, piece in enumerate((do0, do1, do2, do3)):
            start = (mine[0] ^ j) * part
            for i in range(part // step_rows):
                d = piece[i * step_rows : (i + 1) * step_rows, :].astype(f32)
                r = pl.ds(pl.multiple_of(start + i * step_rows, step_rows), step_rows)
                for h in range(nh):
                    at = (first + h) * HD
                    dh = jnp.concatenate(
                        [d[:, at : at + HD], jnp.zeros((step_rows, LN - HD), f32)], axis=1
                    )
                    c = slice(h * LN, (h + 1) * LN)
                    delta = jnp.sum(dh * of[r, c].astype(f32), axis=1, keepdims=True)
                    doa_s[r, c] = put_split(dh, -delta, lanes)

    dk_s[...] = jnp.zeros_like(dk_s)
    dv_s[...] = jnp.zeros_like(dv_s)
    ko = kb * bk
    nt = (((1,), (1,)), ((), ()))
    tn = (((0,), (0,)), ((), ()))

    def step(qi, masked, q0=0, qn=bq, kn=bk):
        qo = pl.multiple_of(qi * bq + q0, qn)
        rows = slice(0, kn)
        if masked:
            kpos = ko + lax.broadcasted_iota(jnp.int32, (kn, qn), 0)
            qpos = qo + lax.broadcasted_iota(jnp.int32, (kn, qn), 1)
            ks = segc[rows, :]
            allowed = (kpos <= qpos) & ((ks == 0) | (ks == segr[:, pl.ds(qo, qn)]))
        for h in range(nh):
            c = slice(h * LN, (h + 1) * LN)
            q = qa[pl.ds(qo, qn), c]
            k = kk[rows, c]
            d = doa_s[pl.ds(qo, qn), c]
            p = jnp.exp2(lax.dot_general(k, q, nt, preferred_element_type=f32))
            if masked:
                p = jnp.where(allowed, p, 0.0)
            ds = (p * lax.dot_general(vv[rows, c], d, nt, preferred_element_type=f32)).astype(bf16)
            dv_s[h, rows, :] += jnp.dot(p.astype(bf16), d, preferred_element_type=f32)
            dk_s[h, rows, :] += jnp.dot(ds, q, preferred_element_type=f32)
            dq_s[h, pl.ds(qo, qn), :] += lax.dot_general(ds, k, tn, preferred_element_type=f32)

    def body(qi, carry):
        flag = flags[qi * nk + kb]

        @pl.when(flag == 1)
        def _():
            step(qi, False)

        @pl.when(flag == 2)
        def _():
            step(qi, True)

        if bq == bk:

            @pl.when(flag == 3)
            def _():
                step(qi, True, 0, bq // 2, bk // 2)
                step(qi, True, bq // 2, bq // 2, bk)

        return carry

    lax.fori_loop(ko // bq, nq, body, 0)
    r = pl.multiple_of(ko, bk)
    ln2 = math.log(2.0)
    gap = dqkv.shape[1] - 3 * nh * HD
    dqkv[pl.ds(r, bk), nh * HD :] = jnp.concatenate(
        [dk_s[h][:, :HD] * ln2 for h in range(nh)]
        + [dv_s[h][:, :HD] for h in range(nh)]
        + [jnp.zeros((bk, gap), f32)],
        axis=1,
    ).astype(bf16)

    @pl.when(kb == nk - 1)
    def _():
        total = jnp.zeros((1, LN), f32)
        for i in range(nq):
            rows = slice(i * bq, (i + 1) * bq)
            for h in range(nh):
                total = total + jnp.sum(
                    dq_s[h, rows, :] * qa[rows, h * LN : (h + 1) * LN].astype(f32), axis=0, keepdims=True
                )
            grads = jnp.concatenate([dq_s[h, rows, :][:, :HD] for h in range(nh)], axis=1)
            dqkv[rows, 0 : nh * HD] = (grads * scale[...]).astype(bf16)
        gscale[...] = jnp.broadcast_to(total, gscale.shape)


def attn_bwd(qa, kv, pieces, of, mine, seg_row, scale, heads, group, groups, bq=512, bk=512):
    n = qa.shape[0]
    nh = heads // groups
    w = nh * LN
    once = pl.Buffered(1)
    spec = pltpu.PrefetchScalarGridSpec(
        num_scalar_prefetch=2,
        grid=(n // bk,),
        in_specs=[
            pl.BlockSpec((n, w), lambda i, f, m: (0, group), pipeline_mode=once),
            pl.BlockSpec((bk, w), lambda i, f, m: (i, group)),
            pl.BlockSpec((bk, w), lambda i, f, m: (i, groups + group)),
            *[pl.BlockSpec((n // 4, heads * HD), lambda i, f, m: (0, 0), pipeline_mode=once)] * 4,
            pl.BlockSpec((n, w), lambda i, f, m: (0, group), pipeline_mode=once),
            pl.BlockSpec((bk, 1), lambda i, f, m: (i, 0)),
            pl.BlockSpec((1, n), lambda i, f, m: (0, 0)),
            pl.BlockSpec((1, nh * HD), lambda i, f, m: (0, 0)),
        ],
        out_specs=[
            pl.BlockSpec((n, lanes_up(3 * nh * HD)), lambda i, f, m: (0, 0)),
            pl.BlockSpec((8, LN), lambda i, f, m: (0, 0)),
        ],
        scratch_shapes=[
            pltpu.VMEM((n, w), bf16),
            pltpu.VMEM((nh, n, LN), f32),
            pltpu.VMEM((nh, bk, LN), f32),
            pltpu.VMEM((nh, bk, LN), f32),
        ],
    )
    return pl.pallas_call(
        functools.partial(bwd_kernel, first=group * nh, nh=nh, bq=bq, bk=bk, n=n),
        out_shape=[
            pltpu.HBM((n, lanes_up(3 * nh * HD)), bf16),
            pltpu.HBM((8, LN), f32),
        ],
        grid_spec=spec,
        compiler_params=pltpu.CompilerParams(vmem_limit_bytes=48 << 20),
        cost_estimate=cost(300 if group == 0 else 0.001),
        name="attn_bwd",
    )(block_flags(seg_row, bq, bk), mine.reshape(1), hbm(qa), hbm(kv), hbm(kv), *pieces, hbm(of), seg_row[:, None], seg_row[None], scale)


def quarter_columns(place, parts, groups, nh):
    width = nh // groups * HD
    return [
        (t * D + place * nh * HD + g * width, width) for g in range(groups) for t in range(3)
    ]


def pick_kernel(mine, w_ref, out, *, parts, groups, nh):
    for i in range(parts):

        @pl.when(mine[0] == i)
        def _(i=i):
            cut = [w_ref[:, a : a + width] for a, width in quarter_columns(i, parts, groups, nh)]
            used = sum(x.shape[1] for x in cut)
            pad = jnp.zeros((cut[0].shape[0], out.shape[1] - used), out.dtype)
            out[...] = jnp.concatenate(cut + [pad], axis=1)


def lanes_up(n):
    return -(-n // LN) * LN


def pick(w, mine, parts, groups, nh):
    rows = w.shape[0]
    step = 160 if rows % 160 == 0 else rows
    return pl.pallas_call(
        functools.partial(pick_kernel, parts=parts, groups=groups, nh=nh),
        out_shape=pltpu.HBM((rows, lanes_up(3 * nh * HD)), w.dtype),
        grid_spec=pltpu.PrefetchScalarGridSpec(
            num_scalar_prefetch=1,
            grid=(rows // step,),
            in_specs=[pl.BlockSpec((step, 3 * D), lambda i, m: (i, 0))],
            out_specs=pl.BlockSpec((step, lanes_up(3 * nh * HD)), lambda i, m: (i, 0)),
        ),
        cost_estimate=cost(5),
        name="pick",
    )(mine.reshape(1), hbm(w))


def stretch_kernel(x_ref, out, *, groups, nh):
    value = x_ref[...]
    each = 3 * nh * HD // groups
    zero = jnp.zeros((value.shape[0], LN - HD), value.dtype)
    per = nh // groups
    wide = []
    for t in range(3):
        for h in range(nh):
            at = (h // per) * each + t * per * HD + (h % per) * HD
            wide += [value[:, at : at + HD], zero]
    out[...] = jnp.concatenate(wide, axis=1)


def stretch(x, groups, nh, us):
    rows, width = x.shape
    step = 160
    return pl.pallas_call(
        functools.partial(stretch_kernel, groups=groups, nh=nh),
        out_shape=pltpu.HBM((rows, 3 * nh * LN), x.dtype),
        grid=(rows // step,),
        in_specs=[pl.BlockSpec((step, width), lambda i: (i, 0))],
        out_specs=pl.BlockSpec((step, 3 * nh * LN), lambda i: (i, 0)),
        cost_estimate=cost(us),
        name="stretch",
    )(hbm(x))


def order_kernel(own_first, a_ref, b_ref, out):
    half = pl.program_id(0)

    @pl.when(half == 0)
    def _():
        out[...] = a_ref[...].T

    @pl.when(half == 1)
    def _():
        out[...] = b_ref[...].T


def order(own, other, own_at):
    rows, width = own.shape
    step = 256
    return pl.pallas_call(
        order_kernel,
        out_shape=pltpu.HBM((width, 2 * rows), own.dtype),
        grid_spec=pltpu.PrefetchScalarGridSpec(
            num_scalar_prefetch=1,
            grid=(2, width // step),
            in_specs=[
                pl.BlockSpec((rows, step), lambda i, j, m: (0, j * (1 - i))),
                pl.BlockSpec((rows, step), lambda i, j, m: (0, j * i)),
            ],
            out_specs=pl.BlockSpec((step, rows), lambda i, j, m: (j, i ^ m[0])),
        ),
        cost_estimate=cost(200.0),
        name="order",
    )(own_at.reshape(1), hbm(own), hbm(other))


def transpose_kernel(x_ref, out):
    out[...] = x_ref[...].T


def transpose(x):
    rows, cols = x.shape
    step = 256
    return pl.pallas_call(
        transpose_kernel,
        out_shape=pltpu.HBM((cols, rows), x.dtype),
        grid=(rows // step,),
        in_specs=[pl.BlockSpec((step, cols), lambda i: (i, 0))],
        out_specs=pl.BlockSpec((cols, step), lambda i: (0, i)),
        cost_estimate=CHEAP,
        name="transpose",
    )(hbm(x))


def project_kernel(info, *refs, count, halves, width, fresh):
    pairs = refs[: 2 * count]
    gain = refs[2 * count]
    weights = refs[2 * count + 1 : 2 * count + 1 + halves]
    scale, ones = refs[2 * count + 1 + halves : 2 * count + 3 + halves]
    normed_ref, q_ref, kv_ref, mine_ref, w = refs[-5:]
    j, tile = pl.program_id(0), pl.program_id(1)
    step = normed_ref.shape[0]

    @pl.when((j == 0) & (tile == 0))
    def _():
        for i, ref in enumerate(weights):
            h = ref.shape[0]
            start = (info[count + 2] ^ i) * h if halves == 2 else 0
            w[pl.ds(pl.multiple_of(start, 16), h), :] = ref[...]
        if not fresh:
            mine_ref[...] = refs[2 * count + 3 + halves][...]

    def work(x_ref):
        value = x_ref[...]
        x = value.astype(f32)
        inverse = lax.rsqrt(jnp.mean(x * x, axis=-1, keepdims=True) + epsilon)
        normed = (x * inverse * gain[...]).astype(bf16)
        normed_ref[...] = normed
        q_ref[...] = (
            jnp.dot(normed, w[:, :width], preferred_element_type=f32) * scale[...]
        ).astype(bf16)
        kv_ref[...] = (
            jnp.dot(normed, w[:, width:], preferred_element_type=f32) + ones[...]
        ).astype(bf16)

        @pl.when(info[count + 1] == info[j])
        def _():
            mine_ref[pl.ds(pl.multiple_of(tile * step, step), step), :] = value

    for i in range(count):
        for lane in range(2):

            @pl.when((j == i) & (info[count] == lane))
            def _(i=i, lane=lane):
                work(pairs[2 * i + 1 - lane])


def project(pairs, places, lane, mine, wt, gain, weights, scale, ones, group_len, carried=None):
    count = len(pairs)
    rows, d = pairs[0][0].shape
    width = scale.shape[1]
    step = 256
    tiles = rows // step
    full = lambda j, t, f: (0, 0)
    at = lambda j, t, f: (f[j] * tiles + t, 0)
    once = pl.Buffered(1)
    info = jnp.stack(list(places) + [lane.astype(jnp.int32), mine, wt])
    args = [x for pair in pairs for x in pair] + [gain, *map(hbm, weights), scale, ones]
    in_specs = [
        pl.BlockSpec(
            (step, d),
            lambda j, t, f, i=i: (jnp.where(j == i, t, jnp.where(j > i, tiles - 1, 0)), 0),
        )
        for i in range(count)
        for _ in range(2)
    ]
    in_specs += [pl.BlockSpec((1, d), full, pipeline_mode=once)]
    in_specs += [pl.BlockSpec(w.shape, full, pipeline_mode=once) for w in weights]
    in_specs += [
        pl.BlockSpec((1, width), full, pipeline_mode=once),
        pl.BlockSpec((1, 2 * width), full, pipeline_mode=once),
    ]
    aliases = {}
    if carried is not None:
        base = len(args) + 2
        args += [hbm(x) for x in (carried[3], *carried[:3])]
        in_specs += [pl.BlockSpec((rows, d), full, pipeline_mode=once)]
        in_specs += [pl.BlockSpec(memory_space=pl.ANY)] * 3
        aliases = {base: 0, base + 1: 1, base + 2: 2}
    return pl.pallas_call(
        functools.partial(
            project_kernel, count=count, halves=len(weights), width=width, fresh=carried is None
        ),
        out_shape=[
            pltpu.HBM((group_len, d), bf16),
            pltpu.HBM((group_len, width), bf16),
            pltpu.HBM((group_len, 2 * width), bf16),
            pltpu.HBM((rows, d), bf16),
        ],
        grid_spec=pltpu.PrefetchScalarGridSpec(
            num_scalar_prefetch=1,
            grid=(count, tiles),
            in_specs=in_specs,
            out_specs=[
                pl.BlockSpec((step, d), at),
                pl.BlockSpec((step, width), at),
                pl.BlockSpec((step, 2 * width), at),
                pl.BlockSpec((rows, d), full),
            ],
            scratch_shapes=[pltpu.VMEM((d, 3 * width), bf16)],
        ),
        input_output_aliases=aliases,
        compiler_params=pltpu.CompilerParams(vmem_limit_bytes=32 << 20),
        cost_estimate=cost(15),
        name="project",
    )(info, *args)


def tail_body(at, p0, p1, p2, p3, x_ref, g_ref, w_s, gain, outs, need):
    lo_ref, left_ref, right_ref, gr_ref, c0, c1, c2, c3, gg_ref = outs
    att_ref, nm_ref, act_ref = (left_ref.at[i] for i in range(3))
    gp_ref, gh_ref = (right_ref.at[i] for i in range(2))
    right_ref[2] = g_ref[...]
    mine = at[0]
    pieces = (p0, p1, p2, p3)
    cols = p0.shape[1]
    nt = (((1,), (1,)), ((), ()))
    for i in range(4):

        @pl.when(mine == i)
        def _(i=i):
            att_ref[...] = jnp.concatenate([pieces[i ^ k][...] for k in range(4)], axis=1)

    need(0)
    resid = x_ref[...].astype(f32) + jnp.dot(att_ref[...], w_s[0], preferred_element_type=f32)
    inverse = lax.rsqrt(jnp.mean(resid * resid, axis=-1, keepdims=True) + epsilon)
    normed = (resid * inverse * gain[...]).astype(bf16)
    nm_ref[...] = normed
    need(1)
    hidden = jnp.dot(normed, w_s[1], preferred_element_type=f32)
    sig = 1.0 / (1.0 + jnp.exp(-hidden))
    active = (hidden * sig).astype(bf16)
    act_ref[...] = active
    need(2)
    lo_ref[...] = (resid + jnp.dot(active, w_s[2], preferred_element_type=f32)).astype(bf16)
    grad_active = lax.dot_general(g_ref[...], w_s[2], nt, preferred_element_type=f32)
    grad_hidden = (grad_active * sig * (1.0 + hidden * (1.0 - sig))).astype(bf16)
    gh_ref[...] = grad_hidden
    grad_normed = lax.dot_general(grad_hidden, w_s[1], nt, preferred_element_type=f32)
    gg_ref[...] += jnp.sum(grad_normed * resid * inverse, axis=0, keepdims=True)
    scaled = grad_normed * gain[...]
    grad_resid = (
        g_ref[...].astype(f32)
        + inverse * scaled
        - resid * (inverse * inverse * inverse) * jnp.mean(scaled * resid, axis=-1, keepdims=True)
    )
    gr_ref[...] = grad_resid
    grad_proj = grad_resid.astype(bf16)
    gp_ref[...] = grad_proj
    grad_att = lax.dot_general(grad_proj, w_s[0], nt, preferred_element_type=f32).astype(bf16)
    for i in range(4):

        @pl.when(mine == i)
        def _(i=i):
            for j, out in enumerate((c0, c1, c2, c3)):
                out[...] = grad_att[:, (i ^ j) * cols : ((i ^ j) + 1) * cols]


def tail_kernel(at, p0, p1, p2, p3, x_ref, g_ref, own0, own1, own2, half, other, gain, *refs, rows, hrows):
    w_s, sems = refs[-2:]
    outs = refs[:-2]

    def copies(i):
        parts = (((own0, own1, own2)[i], at[1], rows), (half.at[i], at[2], hrows), (other.at[i], at[3], hrows))
        return [
            pltpu.make_async_copy(
                part, w_s.at[i, pl.ds(pl.multiple_of(start, 16), n), :], sems.at[3 * i + k]
            )
            for k, (part, start, n) in enumerate(parts)
        ]

    @pl.when(pl.program_id(0) == 0)
    def _():
        outs[-1][...] = jnp.zeros_like(outs[-1])
        for i in range(3):
            for c in copies(i):
                c.start()

    def need(i):
        @pl.when(pl.program_id(0) == 0)
        def _():
            for c in copies(i):
                c.wait()

    tail_body(at, p0, p1, p2, p3, x_ref, g_ref, w_s, gain, outs, need)


def whole_tail_kernel(at, p0, p1, p2, p3, x_ref, g_ref, w, gain, *outs):
    @pl.when(pl.program_id(0) == 0)
    def _():
        outs[-1][...] = jnp.zeros_like(outs[-1])

    tail_body(at, p0, p1, p2, p3, x_ref, g_ref, w, gain, outs, lambda i: None)


def tail(at, pieces, x, g, weights, gain, tile=256):
    rows, d = x.shape
    cols = pieces[0].shape[1]
    row = lambda i, m: (i, 0)
    once = pl.Buffered(1)
    whole = lambda *shape: pl.BlockSpec(shape, lambda i, m: (0,) * len(shape), pipeline_mode=once)
    wide = pl.BlockSpec((tile, d), row)
    slim = pl.BlockSpec((tile, cols), row)
    if len(weights) == 5:
        body = functools.partial(tail_kernel, rows=weights[0].shape[0], hrows=weights[3].shape[1])
        scratch = [pltpu.VMEM((3, d, d), bf16), pltpu.SemaphoreType.DMA((9,))]
        weight_specs = [pl.BlockSpec(memory_space=pl.ANY)] * 5
    else:
        body = whole_tail_kernel
        scratch = []
        weight_specs = [whole(*w.shape) for w in weights]
    return pl.pallas_call(
        body,
        out_shape=[pltpu.HBM((rows, d), bf16)]
        + [pltpu.HBM((3, rows, d), bf16)] * 2
        + [pltpu.HBM((rows, d), f32)]
        + [pltpu.HBM((rows, cols), bf16)] * 4
        + [pltpu.HBM((1, d), f32)],
        grid_spec=pltpu.PrefetchScalarGridSpec(
            num_scalar_prefetch=1,
            grid=(rows // tile,),
            in_specs=[slim] * 4 + [wide] * 2 + weight_specs + [whole(1, d)],
            out_specs=[wide]
            + [pl.BlockSpec((3, tile, d), lambda i, m: (0, i, 0))] * 2
            + [wide]
            + [slim] * 4
            + [pl.BlockSpec((1, d), lambda i, m: (0, 0))],
            scratch_shapes=scratch,
        ),
        compiler_params=pltpu.CompilerParams(vmem_limit_bytes=52 << 20),
        cost_estimate=cost(0.01),
        name="tail",
    )(at, *pieces, hbm(x), g, *map(hbm, weights), gain)


tn_dims = (((0,), (0,)), ((), ()))


def share_kernel(col, left, right, out):
    value = lax.dot_general(left[0], right[0], tn_dims, preferred_element_type=f32)
    out[...] = value.astype(bf16)


def share(left, right, col):
    n, rows, d = left.shape
    w = d // 2
    block = pl.BlockSpec((d, w), lambda i, c: (0, i))
    return pl.pallas_call(
        share_kernel,
        out_shape=pltpu.HBM((d, n * w), bf16),
        grid_spec=pltpu.PrefetchScalarGridSpec(
            num_scalar_prefetch=1,
            grid=(n,),
            in_specs=[
                pl.BlockSpec((1, rows, d), lambda i, c: (i, 0, 0)),
                pl.BlockSpec((1, rows, w), lambda i, c: (i, 0, c[0])),
            ],
            out_specs=block,
        ),
        compiler_params=pltpu.CompilerParams(vmem_limit_bytes=20 << 20),
        cost_estimate=CHEAP,
        name="share",
    )(col.reshape(1), hbm(left), hbm(right))


def copy(x):
    return pl.pallas_call(
        tick_kernel, out_shape=pltpu.HBM(x.shape, x.dtype), cost_estimate=CHEAP, name="copy"
    )(x)


def tick_kernel(x_ref, out):
    out[...] = x_ref[...]


def tick(x):
    return pl.pallas_call(
        tick_kernel, out_shape=jax.ShapeDtypeStruct(x.shape, x.dtype), cost_estimate=cost(200.0), name="tick"
    )(x)


def total_kernel(*refs, counts):
    out = refs[-1]
    start, column = 0, 0
    for count in counts:
        group = refs[start : start + count]
        start += count
        acc = jnp.zeros(group[0].shape[1:], f32)
        for ref in group:
            for i in range(ref.shape[0]):
                acc = acc + ref[i].astype(f32)
        out[:, column : column + acc.shape[1]] = acc.astype(bf16)
        column += acc.shape[1]


def total(groups):
    flat = [x for group in groups for x in group]
    rows = flat[0].shape[1]
    cuts = 2 if rows % 32 == 0 else 1
    width = sum(group[0].shape[2] for group in groups)
    return pl.pallas_call(
        functools.partial(total_kernel, counts=[len(group) for group in groups]),
        out_shape=pltpu.HBM((rows, width), bf16),
        grid=(cuts,),
        in_specs=[
            pl.BlockSpec((x.shape[0], rows // cuts, x.shape[2]), lambda i: (0, i, 0)) for x in flat
        ],
        out_specs=pl.BlockSpec((rows // cuts, width), lambda i: (i, 0)),
        compiler_params=pltpu.CompilerParams(vmem_limit_bytes=16 << 20),
        cost_estimate=cost(0.001),
        name="total",
    )(*flat)


def add_kernel(a_ref, b_ref, out):
    out[...] = (a_ref[...].astype(f32) + b_ref[...].astype(f32)).astype(bf16)


def add(a, b):
    return pl.pallas_call(
        add_kernel, out_shape=pltpu.HBM(a.shape, bf16), cost_estimate=CHEAP, name="add"
    )(a, b)


def add_rows(a, b):
    rows, cols = a.shape
    block = pl.BlockSpec((rows // 5, cols), lambda i: (i, 0))
    return pl.pallas_call(
        add_kernel,
        out_shape=pltpu.HBM(a.shape, bf16),
        grid=(5,),
        in_specs=[block] * 2,
        out_specs=block,
        compiler_params=pltpu.CompilerParams(vmem_limit_bytes=14 << 20),
        cost_estimate=CHEAP,
        name="add_rows",
    )(hbm(a), hbm(b))


def by_bits(first, second, put):
    for i in range(2):
        for j in range(2):

            @pl.when((first == i) & (second == j))
            def _(i=i, j=j):
                put(i, j)


def place_kernel(at, *refs):
    o0, o1, o2 = refs[-3:]
    block = pl.program_id(0)
    w = o0.shape[2] // 2

    def put(other_x, other_near):
        for core in range(2):

            @pl.when(at[2] == core)
            def _(core=core):
                for side in range(2):
                    part = refs[4 * (side ^ core) + 2 * other_x + other_near][...].astype(f32)
                    for i, out in enumerate((o0, o1, o2)):
                        out[0, :, side * w : (side + 1) * w] = part[:, i * w : (i + 1) * w]

    by_bits((block // 2) ^ at[0], (block % 2) ^ at[1], put)


def place_tail(arrays, at):
    h, width = arrays[0].shape
    d = width // 3 * 2
    whole = pl.BlockSpec((h, width), lambda i, m: (0, 0), pipeline_mode=pl.Buffered(1))
    outs = pl.pallas_call(
        place_kernel,
        out_shape=[pltpu.HBM((4, h, d), f32)] * 3,
        grid_spec=pltpu.PrefetchScalarGridSpec(
            num_scalar_prefetch=1,
            grid=(4,),
            in_specs=[whole] * 8,
            out_specs=[pl.BlockSpec((1, h, d), lambda i, m: (i, 0, 0))] * 3,
        ),
        compiler_params=pltpu.CompilerParams(vmem_limit_bytes=16 << 20),
        cost_estimate=CHEAP,
        name="place_tail",
    )(at, *arrays)
    return [out.reshape(4 * h, d) for out in outs]


def cross_kernel(at, x_ref, g_ref, *refs):
    s = refs[-1]
    s[...] = jnp.dot(x_ref[...], g_ref[...], preferred_element_type=f32)
    half = s.shape[0] // 2
    for w in range(2):

        @pl.when(pl.program_id(0) == w)
        def _(w=w):
            for x in range(2):
                rows = pl.ds(pl.multiple_of((at[1] ^ x) * half, 16), half)
                refs[2 * w + x][...] = s[rows, :].astype(bf16)


def cross(x, g, at):
    d, rows = x.shape
    w = d // 2
    cols = g.shape[1]
    step = 512 if cols % 512 == 0 else cols
    n = cols // step
    first = pl.BlockSpec((w // 2, step), lambda i, j, m: (0, jnp.where(i == 0, j, n - 1)))
    second = pl.BlockSpec((w // 2, step), lambda i, j, m: (0, jnp.where(i == 1, j, 0)))
    return pl.pallas_call(
        cross_kernel,
        out_shape=[pltpu.HBM((w // 2, cols), bf16)] * 4,
        grid_spec=pltpu.PrefetchScalarGridSpec(
            num_scalar_prefetch=1,
            grid=(2, n),
            in_specs=[
                pl.BlockSpec((w, rows), lambda i, j, m: (m[0] ^ i, 0)),
                pl.BlockSpec((rows, step), lambda i, j, m: (0, j)),
            ],
            out_specs=[first, first, second, second],
            scratch_shapes=[pltpu.VMEM((w, step), f32)],
        ),
        compiler_params=pltpu.CompilerParams(vmem_limit_bytes=26 << 20),
        cost_estimate=CHEAP,
        name="cross",
    )(at, hbm(x), hbm(g))


def spread_kernel(at, *refs, width):
    out = refs[-1]
    step = out.shape[1]
    rows = pl.ds(pl.multiple_of(pl.program_id(0) * step, step), step)

    def put(core, near):
        cut = []
        for t in range(3):
            for n in range(2):
                for c in range(2):
                    part = refs[2 * (c ^ core) + (n ^ near)][rows, :]
                    cut.append(part[:, t * width : (t + 1) * width])
        out[0] = jnp.concatenate(cut, axis=1).astype(f32)

    by_bits(at[2], at[1], put)


def spread(arrays, at, used, other_x, carried=None):
    rows, cols = arrays[0].shape
    width = 4 * used
    cuts = 2 if rows % 32 == 0 else 1
    whole = pl.BlockSpec((rows, cols), lambda j, m: (0, 0), pipeline_mode=pl.Buffered(1))
    more = () if carried is None else (carried,)
    return pl.pallas_call(
        functools.partial(spread_kernel, width=used // 3),
        out_shape=pltpu.HBM((2, rows, width), f32),
        grid_spec=pltpu.PrefetchScalarGridSpec(
            num_scalar_prefetch=1,
            grid=(cuts,),
            in_specs=[whole] * 4 + [pl.BlockSpec(memory_space=pl.ANY)] * len(more),
            out_specs=pl.BlockSpec((1, rows // cuts, width), lambda j, m: (m[0] ^ other_x, j, 0)),
        ),
        input_output_aliases={5: 0} if more else {},
        compiler_params=pltpu.CompilerParams(vmem_limit_bytes=20 << 20),
        cost_estimate=CHEAP,
        name="spread",
    )(at, *arrays, *more)


def back_kernel(shards, g_ref, w_ref, *refs):
    acc = jnp.dot(g_ref[...], w_ref[...], preferred_element_type=f32)
    if len(refs) == 2:
        acc = acc + refs[0][0].astype(f32)
    refs[-1][0] = acc.astype(bf16)


def back(grad, w, shards, rows, got=None):
    c, d = w.shape
    n = shards.shape[0]
    step = d
    out = pl.BlockSpec((1, rows, step), lambda j, i, f: (i, 0, j))
    in_specs = [
        pl.BlockSpec((rows, c), lambda j, i, f: (f[i], 0)),
        pl.BlockSpec((c, step), lambda j, i, f: (0, j)),
    ]
    args = [hbm(grad), hbm(w)]
    if got is not None:
        in_specs.append(pl.BlockSpec((1, rows, step), lambda j, i, f: (0, 0, j)))
        args.append(got)
    return pl.pallas_call(
        back_kernel,
        out_shape=pltpu.HBM((n, rows, d), bf16),
        grid_spec=pltpu.PrefetchScalarGridSpec(
            num_scalar_prefetch=1, grid=(d // step, n), in_specs=in_specs, out_specs=out
        ),
        compiler_params=pltpu.CompilerParams(vmem_limit_bytes=22 << 20),
        cost_estimate=CHEAP,
        name="back",
    )(shards, *args)


def finish_kernel(shard, g_ref, w_ref, core, near, x_ref, resid, gain, out, gain_out):
    grad = jnp.dot(g_ref[...], w_ref[...], preferred_element_type=f32)
    grad = grad + core[0].astype(f32) + near[0].astype(f32)
    x = x_ref[...].astype(f32)
    inverse = lax.rsqrt(jnp.mean(x * x, axis=-1, keepdims=True) + epsilon)
    part = jnp.sum(grad * x * inverse, axis=0, keepdims=True)

    @pl.when(pl.program_id(0) == 0)
    def _():
        gain_out[...] = jnp.zeros_like(gain_out)

    gain_out[...] += part
    scaled = grad * gain[...]
    out[...] = (
        resid[...]
        + inverse * scaled
        - x * (inverse * inverse * inverse) * jnp.mean(scaled * x, axis=-1, keepdims=True)
    ).astype(bf16)


def finish(grad, w, shard, core, near, x, resid, gain, tile=256):
    rows, d = x.shape
    c = w.shape[0]
    tiles = rows // tile
    row = lambda i, f: (i, 0)
    once = pl.Buffered(1)
    return pl.pallas_call(
        finish_kernel,
        out_shape=[pltpu.HBM((rows, d), bf16), jax.ShapeDtypeStruct((1, d), f32)],
        grid_spec=pltpu.PrefetchScalarGridSpec(
            num_scalar_prefetch=1,
            grid=(tiles,),
            in_specs=[
                pl.BlockSpec((tile, c), lambda i, f: (f[0] * tiles + i, 0)),
                pl.BlockSpec((c, d), lambda i, f: (0, 0), pipeline_mode=once),
                pl.BlockSpec((1, tile, d), lambda i, f: (1, i, 0)),
                pl.BlockSpec((1, tile, d), lambda i, f: (0, i, 0)),
                pl.BlockSpec((tile, d), row),
                pl.BlockSpec((tile, d), row),
                pl.BlockSpec((1, d), lambda i, f: (0, 0)),
            ],
            out_specs=[pl.BlockSpec((tile, d), row), pl.BlockSpec((1, d), lambda i, f: (0, 0))],
        ),
        compiler_params=pltpu.CompilerParams(vmem_limit_bytes=24 << 20),
        cost_estimate=CHEAP,
        name="finish",
    )(shard.reshape(1), hbm(grad), hbm(w), core, near, hbm(x), hbm(resid), gain)


def rms_inverse(values):
    return lax.rsqrt(jnp.mean(values * values, axis=-1, keepdims=True) + epsilon)


def norm_back(values, inverse, grad_scaled):
    return inverse * grad_scaled - values * (inverse * inverse * inverse) * jnp.mean(
        grad_scaled * values, axis=-1, keepdims=True
    )


def dot(left, right):
    return jnp.dot(left, right, preferred_element_type=f32)


def times_trans(left, right):
    return lax.dot_general(left, right, (((1,), (1,)), ((), ())), preferred_element_type=f32)


def trans_times(left, right):
    return lax.dot_general(left, right, (((0,), (0,)), ((), ())), preferred_element_type=f32)


def rows_at(array, start, count):
    return lax.dynamic_slice_in_dim(array, start, count, 0)


def put_rows(array, rows, start):
    return lax.dynamic_update_slice_in_dim(array, rows, start, 0)


def make_local(sizes):
    def pairs(target):
        found = []
        for gx in range(sizes["gx"]):
            for gc in range(sizes["gc"]):
                for z in range(4):
                    for w in range(sizes["wt"]):
                        goal = target(gx, gc, z, w)
                        if goal is not None and goal != (gx, gc, z, w):
                            found.append((place(gx, gc, z, w), place(*goal)))
        return found

    def place(gx, gc, z, w):
        return ((gx * sizes["gc"] + gc) * 4 + z) * sizes["wt"] + w

    def send(value, target):
        return lax.ppermute(value, AXES, pairs(target))

    def core_mate(gx, gc, z, w):
        return (gx, 1 - gc, z, w)

    def x_mate(gx, gc, z, w):
        return (1 - gx, gc, z, w)

    def near_mate(gx, gc, z, w):
        return (gx, gc, z ^ 1, w)

    def far_mate(gx, gc, z, w):
        return (gx, gc, z ^ 2, w)

    def cross_mate(gx, gc, z, w):
        return (gx, 1 - gc, z ^ 1, w)

    def wt_mate(gx, gc, z, w):
        return (gx, gc, z, 1 - w)

    def wt_x_mate(gx, gc, z, w):
        return (1 - gx, gc, z, 1 - w)

    def to_host(gx, gc, z, w):
        return (gx, 1 - (z & 1), 2 * gc + (z >> 1), w)

    def to_home(gx, gc, z, w):
        return (gx, z >> 1, 2 * (z & 1) + 1 - gc, w)

    def hop1(gx, gc, z, w):
        if gc == 0:
            return (gx, 0, z - 1, w) if z > 0 else None
        return (gx, 1, z + 1, w) if z < 3 else None

    def hop2(gx, gc, z, w):
        if gc == 0:
            return (gx, 0, z - 1, w) if z in (1, 2) else None
        return (gx, 1, z + 1, w) if z in (1, 2) else None

    def hop3(gx, gc, z, w):
        if gc == 0:
            return (gx, 0, z ^ 1, w) if z < 2 else None
        return (gx, 1, z ^ 1, w) if z > 1 else None

    def lane_share(gx, gc, z, w):
        return (gx, 1 - gc, z, w) if gc == z >> 1 else None

    def sum_all(value):
        for axis in ("gc", "wt", "near", "far", "gx"):
            step = 1
            while step < sizes[axis]:

                def mate(gx, gc, z, w, axis=axis, step=step):
                    at = dict(gx=gx, gc=gc, far=z >> 1, near=z & 1, wt=w)
                    at[axis] ^= step
                    return (at["gx"], at["gc"], 2 * at["far"] + at["near"], at["wt"])

                value = value + send(value, mate)
                step *= 2
        return value

    def local(
        tokens, segments, w_qkv, w_proj, w_in, w_out, gain_attn, gain_mlp, query_scale, cotangent
    ):
        gx, gc, host, near, wt = (lax.axis_index(axis) for axis in AXES)
        z = 2 * host + near
        mine = 2 * near + 1 - gc
        parts = 4
        nh = H // parts
        groups = 1
        rows = tokens.shape[1]
        group_len = segments.shape[1]
        wrows = w_qkv.shape[0]
        lane = gc == host
        pair = sizes["wt"] == 2

        def after(value, *others):
            return lax.optimization_barrier((value,) + others)[0]

        picked = pick(w_qkv, mine, parts, groups, nh)
        own = tokens[0]
        got1 = send(own, hop1)
        own_share = send(own, lane_share)
        seg_mate = send(segments, core_mate)
        got2 = send(got1, hop2)
        got1_share = send(got1, lane_share)
        end = jnp.where(gc == 0, z == 0, z == 3)
        if pair:
            wide_own = stretch(picked, groups, nh, 2)
            got1 = after(got1, wide_own)
            other_w = send(picked, wt_mate)
            wide_w = (wide_own, stretch(other_w, groups, nh, 10))
        else:
            flat_all = lax.all_gather(picked, "wt", axis=0, tiled=True)
            by_head = jnp.transpose(
                flat_all[:, : 3 * nh * HD].reshape(D, groups, 3, nh // groups, HD), (0, 2, 1, 3, 4)
            )
            wide_w = (
                jnp.pad(
                    by_head.reshape(D, 3 * nh, HD), ((0, 0), (0, 0), (0, LN - HD))
                ).reshape(D, -1),
            )
        got3 = send(jnp.where(end, own, got2), hop3)
        got2_share = send(got2, lane_share)
        way = 1 - 2 * host
        last = jnp.where(host == 0, jnp.where(z == 0, 3, 0), jnp.where(z == 3, 0, 3))
        places = (z, z + way, z + 2 * way, last)

        half_rows = wrows // 2
        half_w = jnp.stack([rows_at(w, gc * half_rows, half_rows) for w in (w_proj, w_in, w_out)])
        if pair:
            half_w = send(after(half_w, other_w), wt_mate)
        else:
            half_w = lax.all_gather(half_w, "wt", axis=0, tiled=False)

        dim_scale = scale_base / math.sqrt(HD) * jax.nn.softplus(query_scale)
        lane_scale = jnp.tile(jnp.pad(dim_scale * log2e, (0, LN - HD)), nh)[None]
        ones = jnp.tile(
            ((jnp.arange(LN) >= HD) & (jnp.arange(LN) < HD + 3)).astype(f32), 2 * nh
        )[None]
        seg_row = jnp.where(lane, segments, seg_mate)[0]
        fixed = (lane, mine, wt, gain_attn[None], wide_w, lane_scale, ones, group_len)
        carried = project(((own, own_share), (got1, got1_share)), places[:2], *fixed)
        got3_share = send(after(got3, carried[0]), lane_share)
        all_normed, queries, keyval, inputs = project(
            ((got2, got2_share), (got3, got3_share)), places[2:], *fixed, carried=carried
        )
        grad_mlp = send(after(cotangent[0], got3_share), to_host)

        att, att_float, q_aug = attn_fwd(queries, keyval, seg_row, nh)
        att, half_w, _ = lax.optimization_barrier((att, half_w, grad_mlp))

        trades = (core_mate, near_mate, cross_mate)
        att_pieces = [rows_at(att, (mine ^ j) * rows, rows) for j in range(parts)]
        half_mate = send(after(half_w, *att_pieces), core_mate)
        att_pieces = [att_pieces[0]] + [send(att_pieces[j + 1], trades[j]) for j in range(3)]
        if pair:
            w_trans = order(after(picked, att), other_w, wt)
        else:
            w_trans = flat_all.T
        normed_trans = transpose(after(all_normed, w_trans))
        if pair:
            weights = (w_proj, w_in, w_out, half_w, half_mate)
            starts = (wt * wrows, (1 - wt) * wrows + gc * half_rows, (1 - wt) * wrows + (1 - gc) * half_rows)
        else:
            one = gc == 0
            tail_w = jnp.stack(
                [jnp.where(one, half_w, half_mate), jnp.where(one, half_mate, half_w)], axis=1
            )
            weights = (jnp.transpose(tail_w, (2, 0, 1, 3, 4)).reshape(3, D, D),)
            starts = ()
        (
            layer_out,
            left,
            right,
            grad_resid,
            *pieces,
            grad_gain_mlp,
        ) = tail(
            jnp.stack([mine, *starts]), att_pieces, after(inputs, normed_trans), grad_mlp, weights, gain_mlp[None]
        )
        pieces = [pieces[0]] + [send(pieces[j + 1], trades[j]) for j in range(3)]

        shared = share(after(left, pieces[1]), right, 1 - gc)
        from_core = send(shared, core_mate)
        own_half = share(left, right, after(gc, shared))
        pieces[2:] = [after(piece, own_half) for piece in pieces[2:]]
        home_out = send(after(layer_out, *pieces[1:]), to_home)
        late_gain = tick(after(gain_attn.reshape(-1, LN), *pieces[1:]))
        summed = add_rows(own_half, after(from_core, late_gain))
        kept = lax.all_to_all(summed, ("wt", "gx", "near"), 0, 0, tiled=True)

        scale_row = jnp.tile(dim_scale, nh // groups)[None]

        def backward(group, *others):
            first, *rest = pieces
            return attn_bwd(
                q_aug,
                keyval,
                (after(first, summed, *others), *rest),
                att_float,
                mine,
                seg_row,
                scale_row,
                nh,
                group,
                groups,
            )

        def by_rows(grad):
            if pair:
                own, *rest = cross(normed_trans, grad, jnp.stack([wt, gx]))
                got = [send(part, mate) for part, mate in zip(rest, (x_mate, wt_mate, wt_x_mate))]
                return [part[None] for part in (own, *got)]
            part = dot(normed_trans, grad).astype(bf16)
            sources = sizes["wt"] * 2
            got = lax.all_to_all(part, ("wt", "gx"), 0, 0, tiled=True)
            return [got.reshape(sources, D // sources, -1)]

        grad_project, grad_lanes = backward(0)
        layer_out = after(home_out, grad_project)

        last_step = [layer_out]

        def turn(value):
            return after(value, *last_step)

        def done(value):
            last_step[0] = value
            return value

        sources = sizes["wt"] * 4
        to_core = done(back(turn(grad_project), w_trans, jnp.stack([mine ^ 3, mine ^ 1]), rows))
        from_core = send(to_core, core_mate)
        by_place = by_rows(turn(grad_project))
        done(by_place[0])
        to_near = done(back(grad_project, w_trans, (mine ^ 2).reshape(1), rows, turn(from_core)))
        from_near = send(to_near, near_mate)
        t1 = done(total([[turn(kept).reshape(sources, D // sources, -1)]]))
        t1_far = send(t1, far_mate)
        layer_out = done(copy(turn(layer_out)))
        by_place[0] = turn(by_place[0])
        q1 = done(total([by_place]))
        q1_far = send(q1, far_mate)
        t2 = done(add(turn(t1), t1_far))
        t2_near = send(t2, near_mate)
        t2_x = send(t2, x_mate)
        grad_tokens, grad_gain_attn = finish(
            grad_project,
            w_trans,
            mine,
            from_core,
            turn(from_near),
            inputs,
            grad_resid,
            late_gain.reshape(1, -1),
        )
        done(grad_tokens)
        grad_query_scale = (
            grad_lanes[0, :HD]
            / (dim_scale * log2e)
            * (scale_base / math.sqrt(HD))
            * jax.nn.sigmoid(query_scale)
        )
        small = jnp.concatenate(
            [grad_gain_attn[0], grad_gain_mlp[0], jnp.pad(grad_query_scale, (0, LN - HD))]
        ).reshape(-1, LN)
        t2_x = done(turn(t2_x))
        t2_near = done(turn(t2_near))
        t2_near_x = send(t2_near, x_mate)
        tails = [t2, t2_near, t2_x]
        tails_mate = [send(turn(x), core_mate) for x in tails]
        q2 = done(add(turn(q1), q1_far))
        q2_near = send(q2, near_mate)
        q2_x = send(q2, x_mate)
        home_grad = send(turn(grad_tokens), to_home)
        q2_near = done(turn(q2_near))
        q2_near_x = send(q2_near, x_mate)
        t2_near_x = done(turn(t2_near_x))
        tails += [t2_near_x]
        tails_mate += [send(t2_near_x, core_mate)]
        q2_x = done(turn(q2_x))
        quads_mate = [send(turn(x), core_mate) for x in (q2, q2_near, q2_x)]
        tails_mate[3] = turn(tails_mate[3])
        totals = place_tail(tails + tails_mate, jnp.stack([gx, near, gc]))
        done(totals[0])
        used = 3 * nh * HD
        spread_at = jnp.stack([gx, near, 1 - gc])
        quads_mate[0] = done(after(turn(quads_mate[0]), quads_mate[1]))
        small = done(sum_all(turn(small))).reshape(-1)
        grad_tokens = done(copy(turn(home_grad)))
        q2_near_x = done(turn(q2_near_x))
        last_mate = send(q2_near_x, core_mate)
        total_qkv = done(
            spread((turn(q2), q2_near, quads_mate[0], quads_mate[1]), spread_at, used, 0)
        )
        total_qkv = spread(
            (q2_x, turn(q2_near_x), quads_mate[2], last_mate), spread_at, used, 1, total_qkv
        ).reshape(wrows, 3 * D)
        return (
            layer_out[None],
            grad_tokens[None],
            total_qkv,
            *totals,
            small[:D],
            small[D : 2 * D],
            small[2 * D : 2 * D + HD],
        )

    return local


def solution(mesh):
    groups, parts, wt = (mesh.shape[axis] for axis in ("grp", "ctx", "wt"))
    inner = Mesh(mesh.devices.reshape(groups // 2, 2, parts // 2, 2, wt), AXES)
    sizes = dict(inner.shape)
    split = P(("gx", "gc", "wt"), ("far", "near"), None)
    weight = P("wt", None)
    return jax.shard_map(
        make_local(sizes),
        mesh=inner,
        in_specs=(
            split,
            P(("gx", "gc", "wt"), None),
            weight,
            weight,
            weight,
            weight,
            P(),
            P(),
            P(),
            split,
        ),
        out_specs=(split, split, weight, weight, weight, weight, P(), P(), P()),
        check_vma=False,
    )
```

```python
import functools
import math

import jax
import jax.numpy as jnp
from jax import lax
from jax.experimental import pallas as pl
from jax.experimental.pallas import tpu as pltpu
from jax.sharding import Mesh
from jax.sharding import PartitionSpec as P

D = 1280
H = 16
HD = 80
LN = 128
epsilon = 1e-06
scale_base = 1.442695041
log2e = 1.4426950408889634
NEG = -1e30
def cost(us):
    return pl.CostEstimate(flops=int(us * 1_000_000_000), transcendentals=0, bytes_accessed=1000)


CHEAP = cost(0.001)
f32 = jnp.float32
bf16 = jnp.bfloat16
AXES = ("gx", "gc", "far", "near", "wt")


def hbm(x):
    return pltpu.with_memory_space_constraint(x, pltpu.HBM)


def block_flags(seg_row, bq, bk):
    n = seg_row.shape[0]
    q = seg_row.reshape(n // bq, bq)
    k = seg_row.reshape(n // bk, bk)
    qf, ql = q[:, 0][:, None], q[:, -1][:, None]
    kf, kl = k[:, 0][None], k[:, -1][None]
    qs = jnp.arange(n // bq, dtype=jnp.int32)[:, None] * bq
    ks = jnp.arange(n // bk, dtype=jnp.int32)[None] * bk
    below = ks + bk - 1 <= qs
    skip = (ks > qs + bq - 1) | ((kf > 0) & (kl < qf))
    same = (qf == ql) & (kl == ql) & ((kf == kl) | ((kf == 0) & (kl == 1)))
    full = below & ((kl == 0) | same)
    flags = jnp.where(skip, 0, jnp.where(full, 1, 2))
    if bq == bk:
        flags = jnp.where(qs == ks, 3, flags)
    return flags.astype(jnp.int32).reshape(-1)


def put_split(base, col, lanes):
    hi = col.astype(bf16).astype(f32)
    rest = col - hi
    mid = rest.astype(bf16).astype(f32)
    out = jnp.where(lanes == HD, hi, base)
    out = jnp.where(lanes == HD + 1, mid, out)
    return jnp.where(lanes == HD + 2, rest - mid, out).astype(bf16)


def fwd_kernel(flags, q_ref, kv, segc, segr, att, of, qaug, m_s, acc_s, *, nh, bq, bk, nk):
    qi = pl.program_id(0)
    count = (qi * bq + bq + bk - 1) // bk
    nt = (((1,), (1,)), ((), ()))
    acc_s[...] = jnp.zeros_like(acc_s)
    m_s[...] = jnp.zeros_like(m_s)

    def mask(ko, q0=0, qn=bq, kn=bk):
        qpos = qi * bq + q0 + lax.broadcasted_iota(jnp.int32, (qn, kn), 0)
        kpos = ko + lax.broadcasted_iota(jnp.int32, (qn, kn), 1)
        ks = segr[:, pl.ds(ko, kn)]
        return (kpos <= qpos) & ((ks == 0) | (ks == segc[q0 : q0 + qn, :]))

    def step(kb, masked, q0=0, qn=bq, kn=bk):
        ko = pl.multiple_of(kb * bk, bk)
        if masked:
            allowed = mask(ko, q0, qn, kn)
        rows = slice(q0, q0 + qn)
        for h in range(nh):
            k = kv[pl.ds(ko, kn), h * LN : (h + 1) * LN]
            v = kv[pl.ds(ko, kn), (nh + h) * LN : (nh + h + 1) * LN]
            q = q_ref[rows, h * LN : (h + 1) * LN]
            p = jnp.exp2(lax.dot_general(q, k, nt, preferred_element_type=f32))
            if masked:
                p = jnp.where(allowed, p, 0.0)
            acc_s[h, rows, :] += jnp.dot(p.astype(bf16), v, preferred_element_type=f32)

    def body(kb, carry):
        flag = flags[qi * nk + kb]

        @pl.when(flag == 1)
        def _():
            step(kb, False)

        @pl.when(flag >= 2)
        def _():
            step(kb, True)

        return carry

    lax.fori_loop(0, count, body, 0)
    bad = jnp.zeros((bq, 1), f32)
    for h in range(nh):
        total = acc_s[h][:, HD : HD + 1]
        bad = jnp.maximum(bad, jnp.where((total > 2.0**-60) & (total < 2.0**60), 0.0, 1.0))

    @pl.when(jnp.max(bad) > 0.0)
    def _():
        def head(h, carry):
            kc = pl.ds(pl.multiple_of(h * LN, LN), LN)
            vc = pl.ds(pl.multiple_of((nh + h) * LN, LN), LN)
            m_s[h] = jnp.full((bq, LN), NEG, f32)
            acc_s[h] = jnp.zeros((bq, LN), f32)

            def inner(kb, carry):
                @pl.when(flags[qi * nk + kb] > 0)
                def _():
                    ko = pl.multiple_of(kb * bk, bk)
                    s = lax.dot_general(
                        q_ref[:, kc], kv[pl.ds(ko, bk), kc], nt, preferred_element_type=f32
                    )
                    s = jnp.where(mask(ko), s, NEG)
                    old = m_s[h]
                    new = jnp.maximum(old, jnp.max(s, axis=1, keepdims=True))
                    p = jnp.exp2(s - new[:, :1]).astype(bf16)
                    m_s[h] = new
                    acc_s[h] = acc_s[h] * jnp.exp2(old - new) + jnp.dot(
                        p, kv[pl.ds(ko, bk), vc], preferred_element_type=f32
                    )

                return carry

            lax.fori_loop(0, count, inner, 0)
            return carry

        lax.fori_loop(0, nh, head, 0)

    lanes = lax.broadcasted_iota(jnp.int32, (bq, LN), 1)
    outs = []
    for h in range(nh):
        acc = acc_s[h]
        total = acc[:, HD : HD + 1]
        out = acc * (1.0 / total)
        of[:, h * LN : (h + 1) * LN] = jnp.where(lanes < HD, out, 0.0).astype(bf16)
        outs.append(out[:, :HD])
        lse = m_s[h][:, :1] + jnp.log2(total)
        qaug[:, h * LN : (h + 1) * LN] = put_split(
            q_ref[:, h * LN : (h + 1) * LN].astype(f32), -lse, lanes
        )
    att[...] = jnp.concatenate(outs, axis=1).astype(bf16)


def attn_fwd(q, kv, seg_row, nh, bq=512, bk=512):
    n = q.shape[0]
    w = nh * LN
    spec = pltpu.PrefetchScalarGridSpec(
        num_scalar_prefetch=1,
        grid=(n // bq,),
        in_specs=[
            pl.BlockSpec((bq, w), lambda i, f: (i, 0)),
            pl.BlockSpec((n, 2 * w), lambda i, f: (0, 0)),
            pl.BlockSpec((bq, 1), lambda i, f: (i, 0)),
            pl.BlockSpec((1, n), lambda i, f: (0, 0)),
        ],
        out_specs=[
            pl.BlockSpec((bq, nh * HD), lambda i, f: (i, 0)),
            pl.BlockSpec((bq, w), lambda i, f: (i, 0)),
            pl.BlockSpec((bq, w), lambda i, f: (i, 0)),
        ],
        scratch_shapes=[pltpu.VMEM((nh, bq, LN), f32), pltpu.VMEM((nh, bq, LN), f32)],
    )
    return pl.pallas_call(
        functools.partial(fwd_kernel, nh=nh, bq=bq, bk=bk, nk=n // bk),
        out_shape=[
            pltpu.HBM((n, nh * HD), bf16),
            pltpu.HBM((n, w), bf16),
            pltpu.HBM((n, w), bf16),
        ],
        grid_spec=spec,
        compiler_params=pltpu.CompilerParams(vmem_limit_bytes=28 << 20),
        cost_estimate=cost(0.01),
        name="attn_fwd",
    )(block_flags(seg_row, bq, bk), hbm(q), hbm(kv), seg_row[:, None], seg_row[None])


def bwd_kernel(
    flags, mine, qa, kk, vv, do0, do1, do2, do3, of, segc, segr, scale, dqkv, gscale, doa_s, dq_s, dk_s, dv_s, *, first, nh, bq, bk, n
):
    nk = n // bk
    nq = n // bq
    kb = pl.program_id(0)
    part = n // 4
    step_rows = 256 if part % 256 == 0 else part
    lanes = lax.broadcasted_iota(jnp.int32, (step_rows, LN), 1)

    @pl.when(kb == 0)
    def _():
        dq_s[...] = jnp.zeros_like(dq_s)
        for j, piece in enumerate((do0, do1, do2, do3)):
            start = (mine[0] ^ j) * part
            for i in range(part // step_rows):
                d = piece[i * step_rows : (i + 1) * step_rows, :].astype(f32)
                r = pl.ds(pl.multiple_of(start + i * step_rows, step_rows), step_rows)
                for h in range(nh):
                    at = (first + h) * HD
                    dh = jnp.concatenate(
                        [d[:, at : at + HD], jnp.zeros((step_rows, LN - HD), f32)], axis=1
                    )
                    c = slice(h * LN, (h + 1) * LN)
                    delta = jnp.sum(dh * of[r, c].astype(f32), axis=1, keepdims=True)
                    doa_s[r, c] = put_split(dh, -delta, lanes)

    dk_s[...] = jnp.zeros_like(dk_s)
    dv_s[...] = jnp.zeros_like(dv_s)
    ko = kb * bk
    nt = (((1,), (1,)), ((), ()))
    tn = (((0,), (0,)), ((), ()))

    def step(qi, masked, q0=0, qn=bq, kn=bk):
        qo = pl.multiple_of(qi * bq + q0, qn)
        rows = slice(0, kn)
        if masked:
            kpos = ko + lax.broadcasted_iota(jnp.int32, (kn, qn), 0)
            qpos = qo + lax.broadcasted_iota(jnp.int32, (kn, qn), 1)
            ks = segc[rows, :]
            allowed = (kpos <= qpos) & ((ks == 0) | (ks == segr[:, pl.ds(qo, qn)]))
        for h in range(nh):
            c = slice(h * LN, (h + 1) * LN)
            q = qa[pl.ds(qo, qn), c]
            k = kk[rows, c]
            d = doa_s[pl.ds(qo, qn), c]
            p = jnp.exp2(lax.dot_general(k, q, nt, preferred_element_type=f32))
            if masked:
                p = jnp.where(allowed, p, 0.0)
            ds = (p * lax.dot_general(vv[rows, c], d, nt, preferred_element_type=f32)).astype(bf16)
            dv_s[h, rows, :] += jnp.dot(p.astype(bf16), d, preferred_element_type=f32)
            dk_s[h, rows, :] += jnp.dot(ds, q, preferred_element_type=f32)
            dq_s[h, pl.ds(qo, qn), :] += lax.dot_general(ds, k, tn, preferred_element_type=f32)

    def body(qi, carry):
        flag = flags[qi * nk + kb]

        @pl.when(flag == 1)
        def _():
            step(qi, False)

        @pl.when(flag == 2)
        def _():
            step(qi, True)

        if bq == bk:

            @pl.when(flag == 3)
            def _():
                step(qi, True, 0, bq // 2, bk // 2)
                step(qi, True, bq // 2, bq // 2, bk)

        return carry

    lax.fori_loop(ko // bq, nq, body, 0)
    r = pl.multiple_of(ko, bk)
    ln2 = math.log(2.0)
    gap = dqkv.shape[1] - 3 * nh * HD
    dqkv[pl.ds(r, bk), nh * HD :] = jnp.concatenate(
        [dk_s[h][:, :HD] * ln2 for h in range(nh)]
        + [dv_s[h][:, :HD] for h in range(nh)]
        + [jnp.zeros((bk, gap), f32)],
        axis=1,
    ).astype(bf16)

    @pl.when(kb == nk - 1)
    def _():
        total = jnp.zeros((1, LN), f32)
        for i in range(nq):
            rows = slice(i * bq, (i + 1) * bq)
            for h in range(nh):
                total = total + jnp.sum(
                    dq_s[h, rows, :] * qa[rows, h * LN : (h + 1) * LN].astype(f32), axis=0, keepdims=True
                )
            grads = jnp.concatenate([dq_s[h, rows, :][:, :HD] for h in range(nh)], axis=1)
            dqkv[rows, 0 : nh * HD] = (grads * scale[...]).astype(bf16)
        gscale[...] = jnp.broadcast_to(total, gscale.shape)


def attn_bwd(qa, kv, pieces, of, mine, seg_row, scale, heads, group, groups, bq=512, bk=512):
    n = qa.shape[0]
    nh = heads // groups
    w = nh * LN
    once = pl.Buffered(1)
    spec = pltpu.PrefetchScalarGridSpec(
        num_scalar_prefetch=2,
        grid=(n // bk,),
        in_specs=[
            pl.BlockSpec((n, w), lambda i, f, m: (0, group), pipeline_mode=once),
            pl.BlockSpec((bk, w), lambda i, f, m: (i, group)),
            pl.BlockSpec((bk, w), lambda i, f, m: (i, groups + group)),
            *[pl.BlockSpec((n // 4, heads * HD), lambda i, f, m: (0, 0), pipeline_mode=once)] * 4,
            pl.BlockSpec((n, w), lambda i, f, m: (0, group), pipeline_mode=once),
            pl.BlockSpec((bk, 1), lambda i, f, m: (i, 0)),
            pl.BlockSpec((1, n), lambda i, f, m: (0, 0)),
            pl.BlockSpec((1, nh * HD), lambda i, f, m: (0, 0)),
        ],
        out_specs=[
            pl.BlockSpec((n, lanes_up(3 * nh * HD)), lambda i, f, m: (0, 0)),
            pl.BlockSpec((8, LN), lambda i, f, m: (0, 0)),
        ],
        scratch_shapes=[
            pltpu.VMEM((n, w), bf16),
            pltpu.VMEM((nh, n, LN), f32),
            pltpu.VMEM((nh, bk, LN), f32),
            pltpu.VMEM((nh, bk, LN), f32),
        ],
    )
    return pl.pallas_call(
        functools.partial(bwd_kernel, first=group * nh, nh=nh, bq=bq, bk=bk, n=n),
        out_shape=[
            pltpu.HBM((n, lanes_up(3 * nh * HD)), bf16),
            pltpu.HBM((8, LN), f32),
        ],
        grid_spec=spec,
        compiler_params=pltpu.CompilerParams(vmem_limit_bytes=48 << 20),
        cost_estimate=cost(300 if group == 0 else 0.001),
        name="attn_bwd",
    )(block_flags(seg_row, bq, bk), mine.reshape(1), hbm(qa), hbm(kv), hbm(kv), *pieces, hbm(of), seg_row[:, None], seg_row[None], scale)


def quarter_columns(place, parts, groups, nh):
    width = nh // groups * HD
    return [
        (t * D + place * nh * HD + g * width, width) for g in range(groups) for t in range(3)
    ]


def pick_kernel(mine, w_ref, out, *, parts, groups, nh):
    for i in range(parts):

        @pl.when(mine[0] == i)
        def _(i=i):
            cut = [w_ref[:, a : a + width] for a, width in quarter_columns(i, parts, groups, nh)]
            used = sum(x.shape[1] for x in cut)
            pad = jnp.zeros((cut[0].shape[0], out.shape[1] - used), out.dtype)
            out[...] = jnp.concatenate(cut + [pad], axis=1)


def lanes_up(n):
    return -(-n // LN) * LN


def pick(w, mine, parts, groups, nh):
    rows = w.shape[0]
    step = 160 if rows % 160 == 0 else rows
    return pl.pallas_call(
        functools.partial(pick_kernel, parts=parts, groups=groups, nh=nh),
        out_shape=pltpu.HBM((rows, lanes_up(3 * nh * HD)), w.dtype),
        grid_spec=pltpu.PrefetchScalarGridSpec(
            num_scalar_prefetch=1,
            grid=(rows // step,),
            in_specs=[pl.BlockSpec((step, 3 * D), lambda i, m: (i, 0))],
            out_specs=pl.BlockSpec((step, lanes_up(3 * nh * HD)), lambda i, m: (i, 0)),
        ),
        cost_estimate=cost(5),
        name="pick",
    )(mine.reshape(1), hbm(w))


def stretch_kernel(x_ref, out, *, groups, nh):
    value = x_ref[...]
    each = 3 * nh * HD // groups
    zero = jnp.zeros((value.shape[0], LN - HD), value.dtype)
    per = nh // groups
    wide = []
    for t in range(3):
        for h in range(nh):
            at = (h // per) * each + t * per * HD + (h % per) * HD
            wide += [value[:, at : at + HD], zero]
    out[...] = jnp.concatenate(wide, axis=1)


def stretch(x, groups, nh, us):
    rows, width = x.shape
    step = 160
    return pl.pallas_call(
        functools.partial(stretch_kernel, groups=groups, nh=nh),
        out_shape=pltpu.HBM((rows, 3 * nh * LN), x.dtype),
        grid=(rows // step,),
        in_specs=[pl.BlockSpec((step, width), lambda i: (i, 0))],
        out_specs=pl.BlockSpec((step, 3 * nh * LN), lambda i: (i, 0)),
        cost_estimate=cost(us),
        name="stretch",
    )(hbm(x))


def order_kernel(own_first, a_ref, b_ref, out):
    half = pl.program_id(0)

    @pl.when(half == 0)
    def _():
        out[...] = a_ref[...].T

    @pl.when(half == 1)
    def _():
        out[...] = b_ref[...].T


def order(own, other, own_at):
    rows, width = own.shape
    step = 256
    return pl.pallas_call(
        order_kernel,
        out_shape=pltpu.HBM((width, 2 * rows), own.dtype),
        grid_spec=pltpu.PrefetchScalarGridSpec(
            num_scalar_prefetch=1,
            grid=(2, width // step),
            in_specs=[
                pl.BlockSpec((rows, step), lambda i, j, m: (0, j * (1 - i))),
                pl.BlockSpec((rows, step), lambda i, j, m: (0, j * i)),
            ],
            out_specs=pl.BlockSpec((step, rows), lambda i, j, m: (j, i ^ m[0])),
        ),
        cost_estimate=cost(200.0),
        name="order",
    )(own_at.reshape(1), hbm(own), hbm(other))


def transpose_kernel(x_ref, out):
    out[...] = x_ref[...].T


def transpose(x):
    rows, cols = x.shape
    step = 256
    return pl.pallas_call(
        transpose_kernel,
        out_shape=pltpu.HBM((cols, rows), x.dtype),
        grid=(rows // step,),
        in_specs=[pl.BlockSpec((step, cols), lambda i: (i, 0))],
        out_specs=pl.BlockSpec((cols, step), lambda i: (0, i)),
        cost_estimate=CHEAP,
        name="transpose",
    )(hbm(x))


def project_kernel(info, *refs, count, halves, width, fresh):
    pairs = refs[: 2 * count]
    gain = refs[2 * count]
    weights = refs[2 * count + 1 : 2 * count + 1 + halves]
    scale, ones = refs[2 * count + 1 + halves : 2 * count + 3 + halves]
    normed_ref, q_ref, kv_ref, mine_ref, w = refs[-5:]
    j, tile = pl.program_id(0), pl.program_id(1)
    step = normed_ref.shape[0]

    @pl.when((j == 0) & (tile == 0))
    def _():
        for i, ref in enumerate(weights):
            h = ref.shape[0]
            start = (info[count + 2] ^ i) * h if halves == 2 else 0
            w[pl.ds(pl.multiple_of(start, 16), h), :] = ref[...]
        if not fresh:
            mine_ref[...] = refs[2 * count + 3 + halves][...]

    def work(x_ref):
        value = x_ref[...]
        x = value.astype(f32)
        inverse = lax.rsqrt(jnp.mean(x * x, axis=-1, keepdims=True) + epsilon)
        normed = (x * inverse * gain[...]).astype(bf16)
        normed_ref[...] = normed
        q_ref[...] = (
            jnp.dot(normed, w[:, :width], preferred_element_type=f32) * scale[...]
        ).astype(bf16)
        kv_ref[...] = (
            jnp.dot(normed, w[:, width:], preferred_element_type=f32) + ones[...]
        ).astype(bf16)

        @pl.when(info[count + 1] == info[j])
        def _():
            mine_ref[pl.ds(pl.multiple_of(tile * step, step), step), :] = value

    for i in range(count):
        for lane in range(2):

            @pl.when((j == i) & (info[count] == lane))
            def _(i=i, lane=lane):
                work(pairs[2 * i + 1 - lane])


def project(pairs, places, lane, mine, wt, gain, weights, scale, ones, group_len, carried=None):
    count = len(pairs)
    rows, d = pairs[0][0].shape
    width = scale.shape[1]
    step = 256
    tiles = rows // step
    full = lambda j, t, f: (0, 0)
    at = lambda j, t, f: (f[j] * tiles + t, 0)
    once = pl.Buffered(1)
    info = jnp.stack(list(places) + [lane.astype(jnp.int32), mine, wt])
    args = [x for pair in pairs for x in pair] + [gain, *map(hbm, weights), scale, ones]
    in_specs = [
        pl.BlockSpec(
            (step, d),
            lambda j, t, f, i=i: (jnp.where(j == i, t, jnp.where(j > i, tiles - 1, 0)), 0),
        )
        for i in range(count)
        for _ in range(2)
    ]
    in_specs += [pl.BlockSpec((1, d), full, pipeline_mode=once)]
    in_specs += [pl.BlockSpec(w.shape, full, pipeline_mode=once) for w in weights]
    in_specs += [
        pl.BlockSpec((1, width), full, pipeline_mode=once),
        pl.BlockSpec((1, 2 * width), full, pipeline_mode=once),
    ]
    aliases = {}
    if carried is not None:
        base = len(args) + 2
        args += [hbm(x) for x in (carried[3], *carried[:3])]
        in_specs += [pl.BlockSpec((rows, d), full, pipeline_mode=once)]
        in_specs += [pl.BlockSpec(memory_space=pl.ANY)] * 3
        aliases = {base: 0, base + 1: 1, base + 2: 2}
    return pl.pallas_call(
        functools.partial(
            project_kernel, count=count, halves=len(weights), width=width, fresh=carried is None
        ),
        out_shape=[
            pltpu.HBM((group_len, d), bf16),
            pltpu.HBM((group_len, width), bf16),
            pltpu.HBM((group_len, 2 * width), bf16),
            pltpu.HBM((rows, d), bf16),
        ],
        grid_spec=pltpu.PrefetchScalarGridSpec(
            num_scalar_prefetch=1,
            grid=(count, tiles),
            in_specs=in_specs,
            out_specs=[
                pl.BlockSpec((step, d), at),
                pl.BlockSpec((step, width), at),
                pl.BlockSpec((step, 2 * width), at),
                pl.BlockSpec((rows, d), full),
            ],
            scratch_shapes=[pltpu.VMEM((d, 3 * width), bf16)],
        ),
        input_output_aliases=aliases,
        compiler_params=pltpu.CompilerParams(vmem_limit_bytes=32 << 20),
        cost_estimate=cost(15),
        name="project",
    )(info, *args)


def tail_body(at, p0, p1, p2, p3, x_ref, g_ref, w_s, gain, outs, need):
    lo_ref, left_ref, right_ref, gr_ref, c0, c1, c2, c3, gg_ref = outs
    att_ref, nm_ref, act_ref = (left_ref.at[i] for i in range(3))
    gp_ref, gh_ref = (right_ref.at[i] for i in range(2))
    right_ref[2] = g_ref[...]
    mine = at[0]
    pieces = (p0, p1, p2, p3)
    cols = p0.shape[1]
    nt = (((1,), (1,)), ((), ()))
    for i in range(4):

        @pl.when(mine == i)
        def _(i=i):
            att_ref[...] = jnp.concatenate([pieces[i ^ k][...] for k in range(4)], axis=1)

    need(0)
    resid = x_ref[...].astype(f32) + jnp.dot(att_ref[...], w_s[0], preferred_element_type=f32)
    inverse = lax.rsqrt(jnp.mean(resid * resid, axis=-1, keepdims=True) + epsilon)
    normed = (resid * inverse * gain[...]).astype(bf16)
    nm_ref[...] = normed
    need(1)
    hidden = jnp.dot(normed, w_s[1], preferred_element_type=f32)
    sig = 1.0 / (1.0 + jnp.exp(-hidden))
    active = (hidden * sig).astype(bf16)
    act_ref[...] = active
    need(2)
    lo_ref[...] = (resid + jnp.dot(active, w_s[2], preferred_element_type=f32)).astype(bf16)
    grad_active = lax.dot_general(g_ref[...], w_s[2], nt, preferred_element_type=f32)
    grad_hidden = (grad_active * sig * (1.0 + hidden * (1.0 - sig))).astype(bf16)
    gh_ref[...] = grad_hidden
    grad_normed = lax.dot_general(grad_hidden, w_s[1], nt, preferred_element_type=f32)
    gg_ref[...] += jnp.sum(grad_normed * resid * inverse, axis=0, keepdims=True)
    scaled = grad_normed * gain[...]
    grad_resid = (
        g_ref[...].astype(f32)
        + inverse * scaled
        - resid * (inverse * inverse * inverse) * jnp.mean(scaled * resid, axis=-1, keepdims=True)
    )
    gr_ref[...] = grad_resid
    grad_proj = grad_resid.astype(bf16)
    gp_ref[...] = grad_proj
    grad_att = lax.dot_general(grad_proj, w_s[0], nt, preferred_element_type=f32).astype(bf16)
    for i in range(4):

        @pl.when(mine == i)
        def _(i=i):
            for j, out in enumerate((c0, c1, c2, c3)):
                out[...] = grad_att[:, (i ^ j) * cols : ((i ^ j) + 1) * cols]


def tail_kernel(at, p0, p1, p2, p3, x_ref, g_ref, own0, own1, own2, half, other, gain, *refs, rows, hrows):
    w_s, sems = refs[-2:]
    outs = refs[:-2]

    def copies(i):
        parts = (((own0, own1, own2)[i], at[1], rows), (half.at[i], at[2], hrows), (other.at[i], at[3], hrows))
        return [
            pltpu.make_async_copy(
                part, w_s.at[i, pl.ds(pl.multiple_of(start, 16), n), :], sems.at[3 * i + k]
            )
            for k, (part, start, n) in enumerate(parts)
        ]

    @pl.when(pl.program_id(0) == 0)
    def _():
        outs[-1][...] = jnp.zeros_like(outs[-1])
        for i in range(3):
            for c in copies(i):
                c.start()

    def need(i):
        @pl.when(pl.program_id(0) == 0)
        def _():
            for c in copies(i):
                c.wait()

    tail_body(at, p0, p1, p2, p3, x_ref, g_ref, w_s, gain, outs, need)


def whole_tail_kernel(at, p0, p1, p2, p3, x_ref, g_ref, w, gain, *outs):
    @pl.when(pl.program_id(0) == 0)
    def _():
        outs[-1][...] = jnp.zeros_like(outs[-1])

    tail_body(at, p0, p1, p2, p3, x_ref, g_ref, w, gain, outs, lambda i: None)


def tail(at, pieces, x, g, weights, gain, tile=256):
    rows, d = x.shape
    cols = pieces[0].shape[1]
    row = lambda i, m: (i, 0)
    once = pl.Buffered(1)
    whole = lambda *shape: pl.BlockSpec(shape, lambda i, m: (0,) * len(shape), pipeline_mode=once)
    wide = pl.BlockSpec((tile, d), row)
    slim = pl.BlockSpec((tile, cols), row)
    if len(weights) == 5:
        body = functools.partial(tail_kernel, rows=weights[0].shape[0], hrows=weights[3].shape[1])
        scratch = [pltpu.VMEM((3, d, d), bf16), pltpu.SemaphoreType.DMA((9,))]
        weight_specs = [pl.BlockSpec(memory_space=pl.ANY)] * 5
    else:
        body = whole_tail_kernel
        scratch = []
        weight_specs = [whole(*w.shape) for w in weights]
    return pl.pallas_call(
        body,
        out_shape=[pltpu.HBM((rows, d), bf16)]
        + [pltpu.HBM((3, rows, d), bf16)] * 2
        + [pltpu.HBM((rows, d), f32)]
        + [pltpu.HBM((rows, cols), bf16)] * 4
        + [pltpu.HBM((1, d), f32)],
        grid_spec=pltpu.PrefetchScalarGridSpec(
            num_scalar_prefetch=1,
            grid=(rows // tile,),
            in_specs=[slim] * 4 + [wide] * 2 + weight_specs + [whole(1, d)],
            out_specs=[wide]
            + [pl.BlockSpec((3, tile, d), lambda i, m: (0, i, 0))] * 2
            + [wide]
            + [slim] * 4
            + [pl.BlockSpec((1, d), lambda i, m: (0, 0))],
            scratch_shapes=scratch,
        ),
        compiler_params=pltpu.CompilerParams(vmem_limit_bytes=52 << 20),
        cost_estimate=cost(0.01),
        name="tail",
    )(at, *pieces, hbm(x), g, *map(hbm, weights), gain)


tn_dims = (((0,), (0,)), ((), ()))


def share_kernel(col, left, right, out):
    value = lax.dot_general(left[0], right[0], tn_dims, preferred_element_type=f32)
    out[...] = value.astype(bf16)


def share(left, right, col):
    n, rows, d = left.shape
    w = d // 2
    block = pl.BlockSpec((d, w), lambda i, c: (0, i))
    return pl.pallas_call(
        share_kernel,
        out_shape=pltpu.HBM((d, n * w), bf16),
        grid_spec=pltpu.PrefetchScalarGridSpec(
            num_scalar_prefetch=1,
            grid=(n,),
            in_specs=[
                pl.BlockSpec((1, rows, d), lambda i, c: (i, 0, 0)),
                pl.BlockSpec((1, rows, w), lambda i, c: (i, 0, c[0])),
            ],
            out_specs=block,
        ),
        compiler_params=pltpu.CompilerParams(vmem_limit_bytes=20 << 20),
        cost_estimate=CHEAP,
        name="share",
    )(col.reshape(1), hbm(left), hbm(right))


def copy(x):
    return pl.pallas_call(
        tick_kernel, out_shape=pltpu.HBM(x.shape, x.dtype), cost_estimate=CHEAP, name="copy"
    )(x)


def tick_kernel(x_ref, out):
    out[...] = x_ref[...]


def tick(x):
    return pl.pallas_call(
        tick_kernel, out_shape=jax.ShapeDtypeStruct(x.shape, x.dtype), cost_estimate=cost(200.0), name="tick"
    )(x)


def total_kernel(*refs, counts):
    out = refs[-1]
    start, column = 0, 0
    for count in counts:
        group = refs[start : start + count]
        start += count
        acc = jnp.zeros(group[0].shape[1:], f32)
        for ref in group:
            for i in range(ref.shape[0]):
                acc = acc + ref[i].astype(f32)
        out[:, column : column + acc.shape[1]] = acc.astype(bf16)
        column += acc.shape[1]


def total(groups):
    flat = [x for group in groups for x in group]
    rows = flat[0].shape[1]
    cuts = 2 if rows % 32 == 0 else 1
    width = sum(group[0].shape[2] for group in groups)
    return pl.pallas_call(
        functools.partial(total_kernel, counts=[len(group) for group in groups]),
        out_shape=pltpu.HBM((rows, width), bf16),
        grid=(cuts,),
        in_specs=[
            pl.BlockSpec((x.shape[0], rows // cuts, x.shape[2]), lambda i: (0, i, 0)) for x in flat
        ],
        out_specs=pl.BlockSpec((rows // cuts, width), lambda i: (i, 0)),
        compiler_params=pltpu.CompilerParams(vmem_limit_bytes=16 << 20),
        cost_estimate=cost(0.001),
        name="total",
    )(*flat)


def add_kernel(a_ref, b_ref, out):
    out[...] = (a_ref[...].astype(f32) + b_ref[...].astype(f32)).astype(bf16)


def add(a, b):
    return pl.pallas_call(
        add_kernel, out_shape=pltpu.HBM(a.shape, bf16), cost_estimate=CHEAP, name="add"
    )(a, b)


def add_rows(a, b):
    rows, cols = a.shape
    block = pl.BlockSpec((rows // 5, cols), lambda i: (i, 0))
    return pl.pallas_call(
        add_kernel,
        out_shape=pltpu.HBM(a.shape, bf16),
        grid=(5,),
        in_specs=[block] * 2,
        out_specs=block,
        compiler_params=pltpu.CompilerParams(vmem_limit_bytes=14 << 20),
        cost_estimate=CHEAP,
        name="add_rows",
    )(hbm(a), hbm(b))


def by_bits(first, second, put):
    for i in range(2):
        for j in range(2):

            @pl.when((first == i) & (second == j))
            def _(i=i, j=j):
                put(i, j)


def place_kernel(at, *refs):
    o0, o1, o2 = refs[-3:]
    block = pl.program_id(0)
    w = o0.shape[2] // 2

    def put(other_x, other_near):
        for core in range(2):

            @pl.when(at[2] == core)
            def _(core=core):
                for side in range(2):
                    part = refs[4 * (side ^ core) + 2 * other_x + other_near][...].astype(f32)
                    for i, out in enumerate((o0, o1, o2)):
                        out[0, :, side * w : (side + 1) * w] = part[:, i * w : (i + 1) * w]

    by_bits((block // 2) ^ at[0], (block % 2) ^ at[1], put)


def place_tail(arrays, at):
    h, width = arrays[0].shape
    d = width // 3 * 2
    whole = pl.BlockSpec((h, width), lambda i, m: (0, 0), pipeline_mode=pl.Buffered(1))
    outs = pl.pallas_call(
        place_kernel,
        out_shape=[pltpu.HBM((4, h, d), f32)] * 3,
        grid_spec=pltpu.PrefetchScalarGridSpec(
            num_scalar_prefetch=1,
            grid=(4,),
            in_specs=[whole] * 8,
            out_specs=[pl.BlockSpec((1, h, d), lambda i, m: (i, 0, 0))] * 3,
        ),
        compiler_params=pltpu.CompilerParams(vmem_limit_bytes=16 << 20),
        cost_estimate=CHEAP,
        name="place_tail",
    )(at, *map(hbm, arrays))
    return [out.reshape(4 * h, d) for out in outs]


def cross_kernel(at, x_ref, g_ref, *refs):
    s = refs[-1]
    s[...] = jnp.dot(x_ref[...], g_ref[...], preferred_element_type=f32)
    half = s.shape[0] // 2
    for w in range(2):

        @pl.when(pl.program_id(0) == w)
        def _(w=w):
            for x in range(2):
                rows = pl.ds(pl.multiple_of((at[1] ^ x) * half, 16), half)
                refs[2 * w + x][...] = s[rows, :].astype(bf16)


def cross(x, g, at):
    d, rows = x.shape
    w = d // 2
    cols = g.shape[1]
    step = 512 if cols % 512 == 0 else cols
    n = cols // step
    first = pl.BlockSpec((w // 2, step), lambda i, j, m: (0, jnp.where(i == 0, j, n - 1)))
    second = pl.BlockSpec((w // 2, step), lambda i, j, m: (0, jnp.where(i == 1, j, 0)))
    return pl.pallas_call(
        cross_kernel,
        out_shape=[pltpu.HBM((w // 2, cols), bf16)] * 4,
        grid_spec=pltpu.PrefetchScalarGridSpec(
            num_scalar_prefetch=1,
            grid=(2, n),
            in_specs=[
                pl.BlockSpec((w, rows), lambda i, j, m: (m[0] ^ i, 0)),
                pl.BlockSpec((rows, step), lambda i, j, m: (0, j)),
            ],
            out_specs=[first, first, second, second],
            scratch_shapes=[pltpu.VMEM((w, step), f32)],
        ),
        compiler_params=pltpu.CompilerParams(vmem_limit_bytes=26 << 20),
        cost_estimate=CHEAP,
        name="cross",
    )(at, hbm(x), hbm(g))


def spread_kernel(at, *refs, width):
    out = refs[-1]
    step = out.shape[1]
    rows = pl.ds(pl.multiple_of(pl.program_id(0) * step, step), step)

    def put(core, near):
        cut = []
        for t in range(3):
            for n in range(2):
                for c in range(2):
                    part = refs[2 * (c ^ core) + (n ^ near)][rows, :]
                    cut.append(part[:, t * width : (t + 1) * width])
        out[0] = jnp.concatenate(cut, axis=1).astype(f32)

    by_bits(at[2], at[1], put)


def spread(arrays, at, used, other_x, carried=None):
    rows, cols = arrays[0].shape
    width = 4 * used
    cuts = 2 if rows % 32 == 0 else 1
    whole = pl.BlockSpec((rows, cols), lambda j, m: (0, 0), pipeline_mode=pl.Buffered(1))
    more = () if carried is None else (carried,)
    return pl.pallas_call(
        functools.partial(spread_kernel, width=used // 3),
        out_shape=pltpu.HBM((2, rows, width), f32),
        grid_spec=pltpu.PrefetchScalarGridSpec(
            num_scalar_prefetch=1,
            grid=(cuts,),
            in_specs=[whole] * 4 + [pl.BlockSpec(memory_space=pl.ANY)] * len(more),
            out_specs=pl.BlockSpec((1, rows // cuts, width), lambda j, m: (m[0] ^ other_x, j, 0)),
        ),
        input_output_aliases={5: 0} if more else {},
        compiler_params=pltpu.CompilerParams(vmem_limit_bytes=20 << 20),
        cost_estimate=CHEAP,
        name="spread",
    )(at, *arrays, *more)


def back_kernel(shards, g_ref, w_ref, *refs):
    acc = jnp.dot(g_ref[...], w_ref[...], preferred_element_type=f32)
    if len(refs) == 2:
        acc = acc + refs[0][0].astype(f32)
    refs[-1][0] = acc.astype(bf16)


def back(grad, w, shards, rows, got=None):
    c, d = w.shape
    n = shards.shape[0]
    step = d
    out = pl.BlockSpec((1, rows, step), lambda j, i, f: (i, 0, j))
    in_specs = [
        pl.BlockSpec((rows, c), lambda j, i, f: (f[i], 0)),
        pl.BlockSpec((c, step), lambda j, i, f: (0, j)),
    ]
    args = [hbm(grad), hbm(w)]
    if got is not None:
        in_specs.append(pl.BlockSpec((1, rows, step), lambda j, i, f: (0, 0, j)))
        args.append(got)
    return pl.pallas_call(
        back_kernel,
        out_shape=pltpu.HBM((n, rows, d), bf16),
        grid_spec=pltpu.PrefetchScalarGridSpec(
            num_scalar_prefetch=1, grid=(d // step, n), in_specs=in_specs, out_specs=out
        ),
        compiler_params=pltpu.CompilerParams(vmem_limit_bytes=22 << 20),
        cost_estimate=CHEAP,
        name="back",
    )(shards, *args)


def finish_kernel(shard, g_ref, w_ref, core, near, x_ref, resid, gain, out, gain_out):
    grad = jnp.dot(g_ref[...], w_ref[...], preferred_element_type=f32)
    grad = grad + core[0].astype(f32) + near[0].astype(f32)
    x = x_ref[...].astype(f32)
    inverse = lax.rsqrt(jnp.mean(x * x, axis=-1, keepdims=True) + epsilon)
    part = jnp.sum(grad * x * inverse, axis=0, keepdims=True)

    @pl.when(pl.program_id(0) == 0)
    def _():
        gain_out[...] = jnp.zeros_like(gain_out)

    gain_out[...] += part
    scaled = grad * gain[...]
    out[...] = (
        resid[...]
        + inverse * scaled
        - x * (inverse * inverse * inverse) * jnp.mean(scaled * x, axis=-1, keepdims=True)
    ).astype(bf16)


def finish(grad, w, shard, core, near, x, resid, gain, tile=256):
    rows, d = x.shape
    c = w.shape[0]
    tiles = rows // tile
    row = lambda i, f: (i, 0)
    once = pl.Buffered(1)
    return pl.pallas_call(
        finish_kernel,
        out_shape=[pltpu.HBM((rows, d), bf16), jax.ShapeDtypeStruct((1, d), f32)],
        grid_spec=pltpu.PrefetchScalarGridSpec(
            num_scalar_prefetch=1,
            grid=(tiles,),
            in_specs=[
                pl.BlockSpec((tile, c), lambda i, f: (f[0] * tiles + i, 0)),
                pl.BlockSpec((c, d), lambda i, f: (0, 0), pipeline_mode=once),
                pl.BlockSpec((1, tile, d), lambda i, f: (1, i, 0)),
                pl.BlockSpec((1, tile, d), lambda i, f: (0, i, 0)),
                pl.BlockSpec((tile, d), row),
                pl.BlockSpec((tile, d), row),
                pl.BlockSpec((1, d), lambda i, f: (0, 0)),
            ],
            out_specs=[pl.BlockSpec((tile, d), row), pl.BlockSpec((1, d), lambda i, f: (0, 0))],
        ),
        compiler_params=pltpu.CompilerParams(vmem_limit_bytes=24 << 20),
        cost_estimate=CHEAP,
        name="finish",
    )(shard.reshape(1), hbm(grad), hbm(w), core, near, hbm(x), hbm(resid), gain)


def rms_inverse(values):
    return lax.rsqrt(jnp.mean(values * values, axis=-1, keepdims=True) + epsilon)


def norm_back(values, inverse, grad_scaled):
    return inverse * grad_scaled - values * (inverse * inverse * inverse) * jnp.mean(
        grad_scaled * values, axis=-1, keepdims=True
    )


def dot(left, right):
    return jnp.dot(left, right, preferred_element_type=f32)


def times_trans(left, right):
    return lax.dot_general(left, right, (((1,), (1,)), ((), ())), preferred_element_type=f32)


def trans_times(left, right):
    return lax.dot_general(left, right, (((0,), (0,)), ((), ())), preferred_element_type=f32)


def rows_at(array, start, count):
    return lax.dynamic_slice_in_dim(array, start, count, 0)


def put_rows(array, rows, start):
    return lax.dynamic_update_slice_in_dim(array, rows, start, 0)


def make_local(sizes):
    def pairs(target):
        found = []
        for gx in range(sizes["gx"]):
            for gc in range(sizes["gc"]):
                for z in range(4):
                    for w in range(sizes["wt"]):
                        goal = target(gx, gc, z, w)
                        if goal is not None and goal != (gx, gc, z, w):
                            found.append((place(gx, gc, z, w), place(*goal)))
        return found

    def place(gx, gc, z, w):
        return ((gx * sizes["gc"] + gc) * 4 + z) * sizes["wt"] + w

    def send(value, target):
        return lax.ppermute(value, AXES, pairs(target))

    def core_mate(gx, gc, z, w):
        return (gx, 1 - gc, z, w)

    def x_mate(gx, gc, z, w):
        return (1 - gx, gc, z, w)

    def near_mate(gx, gc, z, w):
        return (gx, gc, z ^ 1, w)

    def far_mate(gx, gc, z, w):
        return (gx, gc, z ^ 2, w)

    def cross_mate(gx, gc, z, w):
        return (gx, 1 - gc, z ^ 1, w)

    def wt_mate(gx, gc, z, w):
        return (gx, gc, z, 1 - w)

    def wt_x_mate(gx, gc, z, w):
        return (1 - gx, gc, z, 1 - w)

    def to_host(gx, gc, z, w):
        return (gx, 1 - (z & 1), 2 * gc + (z >> 1), w)

    def to_home(gx, gc, z, w):
        return (gx, z >> 1, 2 * (z & 1) + 1 - gc, w)

    def hop1(gx, gc, z, w):
        if gc == 0:
            return (gx, 0, z - 1, w) if z > 0 else None
        return (gx, 1, z + 1, w) if z < 3 else None

    def hop2(gx, gc, z, w):
        if gc == 0:
            return (gx, 0, z - 1, w) if z in (1, 2) else None
        return (gx, 1, z + 1, w) if z in (1, 2) else None

    def hop3(gx, gc, z, w):
        if gc == 0:
            return (gx, 0, z ^ 1, w) if z < 2 else None
        return (gx, 1, z ^ 1, w) if z > 1 else None

    def lane_share(gx, gc, z, w):
        return (gx, 1 - gc, z, w) if gc == z >> 1 else None

    def sum_all(value):
        for axis in ("gc", "wt", "near", "far", "gx"):
            step = 1
            while step < sizes[axis]:

                def mate(gx, gc, z, w, axis=axis, step=step):
                    at = dict(gx=gx, gc=gc, far=z >> 1, near=z & 1, wt=w)
                    at[axis] ^= step
                    return (at["gx"], at["gc"], 2 * at["far"] + at["near"], at["wt"])

                value = value + send(value, mate)
                step *= 2
        return value

    def local(
        tokens, segments, w_qkv, w_proj, w_in, w_out, gain_attn, gain_mlp, query_scale, cotangent
    ):
        gx, gc, host, near, wt = (lax.axis_index(axis) for axis in AXES)
        z = 2 * host + near
        mine = 2 * near + 1 - gc
        parts = 4
        nh = H // parts
        groups = 1
        rows = tokens.shape[1]
        group_len = segments.shape[1]
        wrows = w_qkv.shape[0]
        lane = gc == host
        pair = sizes["wt"] == 2

        def after(value, *others):
            return lax.optimization_barrier((value,) + others)[0]

        picked = pick(w_qkv, mine, parts, groups, nh)
        own = tokens[0]
        got1 = send(own, hop1)
        own_share = send(own, lane_share)
        seg_mate = send(segments, core_mate)
        got2 = send(got1, hop2)
        got1_share = send(got1, lane_share)
        end = jnp.where(gc == 0, z == 0, z == 3)
        if pair:
            wide_own = stretch(picked, groups, nh, 2)
            got1 = after(got1, wide_own)
            other_w = send(picked, wt_mate)
            wide_w = (wide_own, stretch(other_w, groups, nh, 10))
        else:
            flat_all = lax.all_gather(picked, "wt", axis=0, tiled=True)
            by_head = jnp.transpose(
                flat_all[:, : 3 * nh * HD].reshape(D, groups, 3, nh // groups, HD), (0, 2, 1, 3, 4)
            )
            wide_w = (
                jnp.pad(
                    by_head.reshape(D, 3 * nh, HD), ((0, 0), (0, 0), (0, LN - HD))
                ).reshape(D, -1),
            )
        got3 = send(jnp.where(end, own, got2), hop3)
        got2_share = send(got2, lane_share)
        way = 1 - 2 * host
        last = jnp.where(host == 0, jnp.where(z == 0, 3, 0), jnp.where(z == 3, 0, 3))
        places = (z, z + way, z + 2 * way, last)

        half_rows = wrows // 2
        half_w = jnp.stack([rows_at(w, gc * half_rows, half_rows) for w in (w_proj, w_in, w_out)])
        if pair:
            half_w = send(after(half_w, other_w), wt_mate)
        else:
            half_w = lax.all_gather(half_w, "wt", axis=0, tiled=False)

        dim_scale = scale_base / math.sqrt(HD) * jax.nn.softplus(query_scale)
        lane_scale = jnp.tile(jnp.pad(dim_scale * log2e, (0, LN - HD)), nh)[None]
        ones = jnp.tile(
            ((jnp.arange(LN) >= HD) & (jnp.arange(LN) < HD + 3)).astype(f32), 2 * nh
        )[None]
        seg_row = jnp.where(lane, segments, seg_mate)[0]
        fixed = (lane, mine, wt, gain_attn[None], wide_w, lane_scale, ones, group_len)
        carried = project(((own, own_share), (got1, got1_share)), places[:2], *fixed)
        got3_share = send(after(got3, carried[0]), lane_share)
        all_normed, queries, keyval, inputs = project(
            ((got2, got2_share), (got3, got3_share)), places[2:], *fixed, carried=carried
        )
        grad_mlp = send(after(cotangent[0], got3_share), to_host)

        att, att_float, q_aug = attn_fwd(queries, keyval, seg_row, nh)
        att, half_w, _ = lax.optimization_barrier((att, half_w, grad_mlp))

        trades = (core_mate, near_mate, cross_mate)
        att_pieces = [rows_at(att, (mine ^ j) * rows, rows) for j in range(parts)]
        half_mate = send(after(half_w, *att_pieces), core_mate)
        att_pieces = [att_pieces[0]] + [send(att_pieces[j + 1], trades[j]) for j in range(3)]
        if pair:
            w_trans = order(after(picked, att), other_w, wt)
        else:
            w_trans = flat_all.T
        normed_trans = transpose(after(all_normed, w_trans))
        if pair:
            weights = (w_proj, w_in, w_out, half_w, half_mate)
            starts = (wt * wrows, (1 - wt) * wrows + gc * half_rows, (1 - wt) * wrows + (1 - gc) * half_rows)
        else:
            one = gc == 0
            tail_w = jnp.stack(
                [jnp.where(one, half_w, half_mate), jnp.where(one, half_mate, half_w)], axis=1
            )
            weights = (jnp.transpose(tail_w, (2, 0, 1, 3, 4)).reshape(3, D, D),)
            starts = ()
        (
            layer_out,
            left,
            right,
            grad_resid,
            *pieces,
            grad_gain_mlp,
        ) = tail(
            jnp.stack([mine, *starts]), att_pieces, after(inputs, normed_trans), grad_mlp, weights, gain_mlp[None]
        )
        pieces = [pieces[0]] + [send(pieces[j + 1], trades[j]) for j in range(3)]

        shared = share(after(left, pieces[1]), right, 1 - gc)
        from_core = send(shared, core_mate)
        own_half = share(left, right, after(gc, shared))
        pieces[2:] = [after(piece, own_half) for piece in pieces[2:]]
        home_out = send(after(layer_out, *pieces[1:]), to_home)
        late_gain = tick(after(gain_attn.reshape(-1, LN), *pieces[1:]))
        summed = add_rows(own_half, after(from_core, late_gain))
        kept = lax.all_to_all(summed, ("wt", "gx", "near"), 0, 0, tiled=True)

        scale_row = jnp.tile(dim_scale, nh // groups)[None]

        def backward(group, *others):
            first, *rest = pieces
            return attn_bwd(
                q_aug,
                keyval,
                (after(first, summed, *others), *rest),
                att_float,
                mine,
                seg_row,
                scale_row,
                nh,
                group,
                groups,
            )

        def by_rows(grad):
            if pair:
                own, *rest = cross(normed_trans, grad, jnp.stack([wt, gx]))
                got = [send(part, mate) for part, mate in zip(rest, (x_mate, wt_mate, wt_x_mate))]
                return [part[None] for part in (own, *got)]
            part = dot(normed_trans, grad).astype(bf16)
            sources = sizes["wt"] * 2
            got = lax.all_to_all(part, ("wt", "gx"), 0, 0, tiled=True)
            return [got.reshape(sources, D // sources, -1)]

        grad_project, grad_lanes = backward(0)
        layer_out = after(home_out, grad_project)

        last_step = [layer_out]

        def turn(value):
            return after(value, *last_step)

        def done(value):
            last_step[0] = value
            return value

        sources = sizes["wt"] * 4
        to_core = done(back(turn(grad_project), w_trans, jnp.stack([mine ^ 3, mine ^ 1]), rows))
        from_core = send(to_core, core_mate)
        by_place = by_rows(turn(grad_project))
        done(by_place[0])
        to_near = done(back(grad_project, w_trans, (mine ^ 2).reshape(1), rows, turn(from_core)))
        from_near = send(to_near, near_mate)
        t1 = done(total([[turn(kept).reshape(sources, D // sources, -1)]]))
        t1_far = send(t1, far_mate)
        layer_out = done(copy(turn(layer_out)))
        by_place[0] = turn(by_place[0])
        q1 = done(total([by_place]))
        q1_far = send(q1, far_mate)
        t2 = done(add(turn(t1), t1_far))
        t2_near = send(t2, near_mate)
        t2_x = send(t2, x_mate)
        grad_tokens, grad_gain_attn = finish(
            grad_project,
            w_trans,
            mine,
            from_core,
            turn(from_near),
            inputs,
            grad_resid,
            late_gain.reshape(1, -1),
        )
        done(grad_tokens)
        grad_query_scale = (
            grad_lanes[0, :HD]
            / (dim_scale * log2e)
            * (scale_base / math.sqrt(HD))
            * jax.nn.sigmoid(query_scale)
        )
        small = jnp.concatenate(
            [grad_gain_attn[0], grad_gain_mlp[0], jnp.pad(grad_query_scale, (0, LN - HD))]
        ).reshape(-1, LN)
        t2_x = done(turn(t2_x))
        t2_near = done(turn(t2_near))
        t2_near_x = send(t2_near, x_mate)
        tails = [t2, t2_near, t2_x]
        tails_mate = [send(turn(x), core_mate) for x in tails]
        q2 = done(add(turn(q1), q1_far))
        q2_near = send(q2, near_mate)
        q2_x = send(q2, x_mate)
        home_grad = send(turn(grad_tokens), to_home)
        q2_near = done(turn(q2_near))
        q2_near_x = send(q2_near, x_mate)
        t2_near_x = done(turn(t2_near_x))
        tails += [t2_near_x]
        tails_mate += [send(t2_near_x, core_mate)]
        q2_x = done(turn(q2_x))
        quads_mate = [send(turn(x), core_mate) for x in (q2, q2_near, q2_x)]
        tails_mate[3] = turn(tails_mate[3])
        totals = place_tail(tails + tails_mate, jnp.stack([gx, near, gc]))
        done(totals[0])
        used = 3 * nh * HD
        spread_at = jnp.stack([gx, near, 1 - gc])
        quads_mate[0] = done(after(turn(quads_mate[0]), quads_mate[1]))
        small = done(sum_all(turn(small))).reshape(-1)
        grad_tokens = done(copy(turn(home_grad)))
        q2_near_x = done(turn(q2_near_x))
        last_mate = send(q2_near_x, core_mate)
        total_qkv = done(
            spread((turn(q2), q2_near, quads_mate[0], quads_mate[1]), spread_at, used, 0)
        )
        total_qkv = spread(
            (q2_x, turn(q2_near_x), quads_mate[2], last_mate), spread_at, used, 1, total_qkv
        ).reshape(wrows, 3 * D)
        return (
            layer_out[None],
            grad_tokens[None],
            total_qkv,
            *totals,
            small[:D],
            small[D : 2 * D],
            small[2 * D : 2 * D + HD],
        )

    return local


def solution(mesh):
    groups, parts, wt = (mesh.shape[axis] for axis in ("grp", "ctx", "wt"))
    inner = Mesh(mesh.devices.reshape(groups // 2, 2, parts // 2, 2, wt), AXES)
    sizes = dict(inner.shape)
    split = P(("gx", "gc", "wt"), ("far", "near"), None)
    weight = P("wt", None)
    return jax.shard_map(
        make_local(sizes),
        mesh=inner,
        in_specs=(
            split,
            P(("gx", "gc", "wt"), None),
            weight,
            weight,
            weight,
            weight,
            P(),
            P(),
            P(),
            split,
        ),
        out_specs=(split, split, weight, weight, weight, weight, P(), P(), P()),
        check_vma=False,
    )
```

```python
import functools
import math

import jax
import jax.numpy as jnp
from jax import lax
from jax.experimental import pallas as pl
from jax.experimental.pallas import tpu as pltpu
from jax.sharding import Mesh
from jax.sharding import PartitionSpec as P

D = 1280
H = 16
HD = 80
LN = 128
epsilon = 1e-06
scale_base = 1.442695041
log2e = 1.4426950408889634
NEG = -1e30
def cost(us):
    return pl.CostEstimate(flops=int(us * 1_000_000_000), transcendentals=0, bytes_accessed=1000)


CHEAP = cost(0.001)
f32 = jnp.float32
bf16 = jnp.bfloat16
AXES = ("gx", "gc", "far", "near", "wt")


def hbm(x):
    return pltpu.with_memory_space_constraint(x, pltpu.HBM)


def block_flags(seg_row, bq, bk):
    n = seg_row.shape[0]
    q = seg_row.reshape(n // bq, bq)
    k = seg_row.reshape(n // bk, bk)
    qf, ql = q[:, 0][:, None], q[:, -1][:, None]
    kf, kl = k[:, 0][None], k[:, -1][None]
    qs = jnp.arange(n // bq, dtype=jnp.int32)[:, None] * bq
    ks = jnp.arange(n // bk, dtype=jnp.int32)[None] * bk
    below = ks + bk - 1 <= qs
    skip = (ks > qs + bq - 1) | ((kf > 0) & (kl < qf))
    same = (qf == ql) & (kl == ql) & ((kf == kl) | ((kf == 0) & (kl == 1)))
    full = below & ((kl == 0) | same)
    flags = jnp.where(skip, 0, jnp.where(full, 1, 2))
    if bq == bk:
        flags = jnp.where(qs == ks, 3, flags)
    return flags.astype(jnp.int32).reshape(-1)


def put_split(base, col, lanes):
    hi = col.astype(bf16).astype(f32)
    rest = col - hi
    mid = rest.astype(bf16).astype(f32)
    out = jnp.where(lanes == HD, hi, base)
    out = jnp.where(lanes == HD + 1, mid, out)
    return jnp.where(lanes == HD + 2, rest - mid, out).astype(bf16)


def fwd_kernel(flags, q_ref, kv, segc, segr, att, of, qaug, m_s, acc_s, *, nh, bq, bk, nk):
    qi = pl.program_id(0)
    count = (qi * bq + bq + bk - 1) // bk
    nt = (((1,), (1,)), ((), ()))
    acc_s[...] = jnp.zeros_like(acc_s)
    m_s[...] = jnp.zeros_like(m_s)

    def mask(ko, q0=0, qn=bq, kn=bk):
        qpos = qi * bq + q0 + lax.broadcasted_iota(jnp.int32, (qn, kn), 0)
        kpos = ko + lax.broadcasted_iota(jnp.int32, (qn, kn), 1)
        ks = segr[:, pl.ds(ko, kn)]
        return (kpos <= qpos) & ((ks == 0) | (ks == segc[q0 : q0 + qn, :]))

    def step(kb, masked, q0=0, qn=bq, kn=bk):
        ko = pl.multiple_of(kb * bk, bk)
        if masked:
            allowed = mask(ko, q0, qn, kn)
        rows = slice(q0, q0 + qn)
        for h in range(nh):
            k = kv[pl.ds(ko, kn), h * LN : (h + 1) * LN]
            v = kv[pl.ds(ko, kn), (nh + h) * LN : (nh + h + 1) * LN]
            q = q_ref[rows, h * LN : (h + 1) * LN]
            p = jnp.exp2(lax.dot_general(q, k, nt, preferred_element_type=f32))
            if masked:
                p = jnp.where(allowed, p, 0.0)
            acc_s[h, rows, :] += jnp.dot(p.astype(bf16), v, preferred_element_type=f32)

    def body(kb, carry):
        flag = flags[qi * nk + kb]

        @pl.when(flag == 1)
        def _():
            step(kb, False)

        @pl.when(flag >= 2)
        def _():
            step(kb, True)

        return carry

    lax.fori_loop(0, count, body, 0)
    bad = jnp.zeros((bq, 1), f32)
    for h in range(nh):
        total = acc_s[h][:, HD : HD + 1]
        bad = jnp.maximum(bad, jnp.where((total > 2.0**-60) & (total < 2.0**60), 0.0, 1.0))

    @pl.when(jnp.max(bad) > 0.0)
    def _():
        def head(h, carry):
            kc = pl.ds(pl.multiple_of(h * LN, LN), LN)
            vc = pl.ds(pl.multiple_of((nh + h) * LN, LN), LN)
            m_s[h] = jnp.full((bq, LN), NEG, f32)
            acc_s[h] = jnp.zeros((bq, LN), f32)

            def inner(kb, carry):
                @pl.when(flags[qi * nk + kb] > 0)
                def _():
                    ko = pl.multiple_of(kb * bk, bk)
                    s = lax.dot_general(
                        q_ref[:, kc], kv[pl.ds(ko, bk), kc], nt, preferred_element_type=f32
                    )
                    s = jnp.where(mask(ko), s, NEG)
                    old = m_s[h]
                    new = jnp.maximum(old, jnp.max(s, axis=1, keepdims=True))
                    p = jnp.exp2(s - new[:, :1]).astype(bf16)
                    m_s[h] = new
                    acc_s[h] = acc_s[h] * jnp.exp2(old - new) + jnp.dot(
                        p, kv[pl.ds(ko, bk), vc], preferred_element_type=f32
                    )

                return carry

            lax.fori_loop(0, count, inner, 0)
            return carry

        lax.fori_loop(0, nh, head, 0)

    lanes = lax.broadcasted_iota(jnp.int32, (bq, LN), 1)
    outs = []
    for h in range(nh):
        acc = acc_s[h]
        total = acc[:, HD : HD + 1]
        out = acc * (1.0 / total)
        of[:, h * LN : (h + 1) * LN] = jnp.where(lanes < HD, out, 0.0).astype(bf16)
        outs.append(out[:, :HD])
        lse = m_s[h][:, :1] + jnp.log2(total)
        qaug[:, h * LN : (h + 1) * LN] = put_split(
            q_ref[:, h * LN : (h + 1) * LN].astype(f32), -lse, lanes
        )
    att[...] = jnp.concatenate(outs, axis=1).astype(bf16)


def attn_fwd(q, kv, seg_row, nh, bq=512, bk=512):
    n = q.shape[0]
    w = nh * LN
    spec = pltpu.PrefetchScalarGridSpec(
        num_scalar_prefetch=1,
        grid=(n // bq,),
        in_specs=[
            pl.BlockSpec((bq, w), lambda i, f: (i, 0)),
            pl.BlockSpec((n, 2 * w), lambda i, f: (0, 0)),
            pl.BlockSpec((bq, 1), lambda i, f: (i, 0)),
            pl.BlockSpec((1, n), lambda i, f: (0, 0)),
        ],
        out_specs=[
            pl.BlockSpec((bq, nh * HD), lambda i, f: (i, 0)),
            pl.BlockSpec((bq, w), lambda i, f: (i, 0)),
            pl.BlockSpec((bq, w), lambda i, f: (i, 0)),
        ],
        scratch_shapes=[pltpu.VMEM((nh, bq, LN), f32), pltpu.VMEM((nh, bq, LN), f32)],
    )
    return pl.pallas_call(
        functools.partial(fwd_kernel, nh=nh, bq=bq, bk=bk, nk=n // bk),
        out_shape=[
            pltpu.HBM((n, nh * HD), bf16),
            pltpu.HBM((n, w), bf16),
            pltpu.HBM((n, w), bf16),
        ],
        grid_spec=spec,
        compiler_params=pltpu.CompilerParams(vmem_limit_bytes=28 << 20),
        cost_estimate=cost(0.01),
        name="attn_fwd",
    )(block_flags(seg_row, bq, bk), hbm(q), hbm(kv), seg_row[:, None], seg_row[None])


def bwd_kernel(
    flags, mine, qa, kk, vv, do0, do1, do2, do3, of, segc, segr, scale, dqkv, gscale, doa_s, dq_s, dk_s, dv_s, *, first, nh, bq, bk, n
):
    nk = n // bk
    nq = n // bq
    kb = pl.program_id(0)
    part = n // 4
    step_rows = 256 if part % 256 == 0 else part
    lanes = lax.broadcasted_iota(jnp.int32, (step_rows, LN), 1)

    @pl.when(kb == 0)
    def _():
        dq_s[...] = jnp.zeros_like(dq_s)
        for j, piece in enumerate((do0, do1, do2, do3)):
            start = (mine[0] ^ j) * part
            for i in range(part // step_rows):
                d = piece[i * step_rows : (i + 1) * step_rows, :].astype(f32)
                r = pl.ds(pl.multiple_of(start + i * step_rows, step_rows), step_rows)
                for h in range(nh):
                    at = (first + h) * HD
                    dh = jnp.concatenate(
                        [d[:, at : at + HD], jnp.zeros((step_rows, LN - HD), f32)], axis=1
                    )
                    c = slice(h * LN, (h + 1) * LN)
                    delta = jnp.sum(dh * of[r, c].astype(f32), axis=1, keepdims=True)
                    doa_s[r, c] = put_split(dh, -delta, lanes)

    dk_s[...] = jnp.zeros_like(dk_s)
    dv_s[...] = jnp.zeros_like(dv_s)
    ko = kb * bk
    nt = (((1,), (1,)), ((), ()))
    tn = (((0,), (0,)), ((), ()))

    def step(qi, masked, q0=0, qn=bq, kn=bk):
        qo = pl.multiple_of(qi * bq + q0, qn)
        rows = slice(0, kn)
        if masked:
            kpos = ko + lax.broadcasted_iota(jnp.int32, (kn, qn), 0)
            qpos = qo + lax.broadcasted_iota(jnp.int32, (kn, qn), 1)
            ks = segc[rows, :]
            allowed = (kpos <= qpos) & ((ks == 0) | (ks == segr[:, pl.ds(qo, qn)]))
        for h in range(nh):
            c = slice(h * LN, (h + 1) * LN)
            q = qa[pl.ds(qo, qn), c]
            k = kk[rows, c]
            d = doa_s[pl.ds(qo, qn), c]
            p = jnp.exp2(lax.dot_general(k, q, nt, preferred_element_type=f32))
            if masked:
                p = jnp.where(allowed, p, 0.0)
            ds = (p * lax.dot_general(vv[rows, c], d, nt, preferred_element_type=f32)).astype(bf16)
            dv_s[h, rows, :] += jnp.dot(p.astype(bf16), d, preferred_element_type=f32)
            dk_s[h, rows, :] += jnp.dot(ds, q, preferred_element_type=f32)
            dq_s[h, pl.ds(qo, qn), :] += lax.dot_general(ds, k, tn, preferred_element_type=f32)

    def body(qi, carry):
        flag = flags[qi * nk + kb]

        @pl.when(flag == 1)
        def _():
            step(qi, False)

        @pl.when(flag == 2)
        def _():
            step(qi, True)

        if bq == bk:

            @pl.when(flag == 3)
            def _():
                step(qi, True, 0, bq // 2, bk // 2)
                step(qi, True, bq // 2, bq // 2, bk)

        return carry

    lax.fori_loop(ko // bq, nq, body, 0)
    r = pl.multiple_of(ko, bk)
    ln2 = math.log(2.0)
    gap = dqkv.shape[1] - 3 * nh * HD
    dqkv[pl.ds(r, bk), nh * HD :] = jnp.concatenate(
        [dk_s[h][:, :HD] * ln2 for h in range(nh)]
        + [dv_s[h][:, :HD] for h in range(nh)]
        + [jnp.zeros((bk, gap), f32)],
        axis=1,
    ).astype(bf16)

    @pl.when(kb == nk - 1)
    def _():
        total = jnp.zeros((1, LN), f32)
        for i in range(nq):
            rows = slice(i * bq, (i + 1) * bq)
            for h in range(nh):
                total = total + jnp.sum(
                    dq_s[h, rows, :] * qa[rows, h * LN : (h + 1) * LN].astype(f32), axis=0, keepdims=True
                )
            grads = jnp.concatenate([dq_s[h, rows, :][:, :HD] for h in range(nh)], axis=1)
            dqkv[rows, 0 : nh * HD] = (grads * scale[...]).astype(bf16)
        gscale[...] = jnp.broadcast_to(total, gscale.shape)


def attn_bwd(qa, kv, pieces, of, mine, seg_row, scale, heads, group, groups, bq=512, bk=512):
    n = qa.shape[0]
    nh = heads // groups
    w = nh * LN
    once = pl.Buffered(1)
    spec = pltpu.PrefetchScalarGridSpec(
        num_scalar_prefetch=2,
        grid=(n // bk,),
        in_specs=[
            pl.BlockSpec((n, w), lambda i, f, m: (0, group), pipeline_mode=once),
            pl.BlockSpec((bk, w), lambda i, f, m: (i, group)),
            pl.BlockSpec((bk, w), lambda i, f, m: (i, groups + group)),
            *[pl.BlockSpec((n // 4, heads * HD), lambda i, f, m: (0, 0), pipeline_mode=once)] * 4,
            pl.BlockSpec((n, w), lambda i, f, m: (0, group), pipeline_mode=once),
            pl.BlockSpec((bk, 1), lambda i, f, m: (i, 0)),
            pl.BlockSpec((1, n), lambda i, f, m: (0, 0)),
            pl.BlockSpec((1, nh * HD), lambda i, f, m: (0, 0)),
        ],
        out_specs=[
            pl.BlockSpec((n, lanes_up(3 * nh * HD)), lambda i, f, m: (0, 0)),
            pl.BlockSpec((8, LN), lambda i, f, m: (0, 0)),
        ],
        scratch_shapes=[
            pltpu.VMEM((n, w), bf16),
            pltpu.VMEM((nh, n, LN), f32),
            pltpu.VMEM((nh, bk, LN), f32),
            pltpu.VMEM((nh, bk, LN), f32),
        ],
    )
    return pl.pallas_call(
        functools.partial(bwd_kernel, first=group * nh, nh=nh, bq=bq, bk=bk, n=n),
        out_shape=[
            pltpu.HBM((n, lanes_up(3 * nh * HD)), bf16),
            pltpu.HBM((8, LN), f32),
        ],
        grid_spec=spec,
        compiler_params=pltpu.CompilerParams(vmem_limit_bytes=48 << 20),
        cost_estimate=cost(300 if group == 0 else 0.001),
        name="attn_bwd",
    )(block_flags(seg_row, bq, bk), mine.reshape(1), hbm(qa), hbm(kv), hbm(kv), *pieces, hbm(of), seg_row[:, None], seg_row[None], scale)


def quarter_columns(place, parts, groups, nh):
    width = nh // groups * HD
    return [
        (t * D + place * nh * HD + g * width, width) for g in range(groups) for t in range(3)
    ]


def pick_kernel(mine, w_ref, out, *, parts, groups, nh):
    for i in range(parts):

        @pl.when(mine[0] == i)
        def _(i=i):
            cut = [w_ref[:, a : a + width] for a, width in quarter_columns(i, parts, groups, nh)]
            used = sum(x.shape[1] for x in cut)
            pad = jnp.zeros((cut[0].shape[0], out.shape[1] - used), out.dtype)
            out[...] = jnp.concatenate(cut + [pad], axis=1)


def lanes_up(n):
    return -(-n // LN) * LN


def pick(w, mine, parts, groups, nh):
    rows = w.shape[0]
    step = 160 if rows % 160 == 0 else rows
    return pl.pallas_call(
        functools.partial(pick_kernel, parts=parts, groups=groups, nh=nh),
        out_shape=pltpu.HBM((rows, lanes_up(3 * nh * HD)), w.dtype),
        grid_spec=pltpu.PrefetchScalarGridSpec(
            num_scalar_prefetch=1,
            grid=(rows // step,),
            in_specs=[pl.BlockSpec((step, 3 * D), lambda i, m: (i, 0))],
            out_specs=pl.BlockSpec((step, lanes_up(3 * nh * HD)), lambda i, m: (i, 0)),
        ),
        cost_estimate=cost(5),
        name="pick",
    )(mine.reshape(1), hbm(w))


def stretch_kernel(x_ref, out, *, groups, nh):
    value = x_ref[...]
    each = 3 * nh * HD // groups
    zero = jnp.zeros((value.shape[0], LN - HD), value.dtype)
    per = nh // groups
    wide = []
    for t in range(3):
        for h in range(nh):
            at = (h // per) * each + t * per * HD + (h % per) * HD
            wide += [value[:, at : at + HD], zero]
    out[...] = jnp.concatenate(wide, axis=1)


def stretch(x, groups, nh, us):
    rows, width = x.shape
    step = 160
    return pl.pallas_call(
        functools.partial(stretch_kernel, groups=groups, nh=nh),
        out_shape=pltpu.HBM((rows, 3 * nh * LN), x.dtype),
        grid=(rows // step,),
        in_specs=[pl.BlockSpec((step, width), lambda i: (i, 0))],
        out_specs=pl.BlockSpec((step, 3 * nh * LN), lambda i: (i, 0)),
        cost_estimate=cost(us),
        name="stretch",
    )(hbm(x))


def order_kernel(own_first, a_ref, b_ref, out):
    half = pl.program_id(0)

    @pl.when(half == 0)
    def _():
        out[...] = a_ref[...].T

    @pl.when(half == 1)
    def _():
        out[...] = b_ref[...].T


def order(own, other, own_at):
    rows, width = own.shape
    step = 256
    return pl.pallas_call(
        order_kernel,
        out_shape=pltpu.HBM((width, 2 * rows), own.dtype),
        grid_spec=pltpu.PrefetchScalarGridSpec(
            num_scalar_prefetch=1,
            grid=(2, width // step),
            in_specs=[
                pl.BlockSpec((rows, step), lambda i, j, m: (0, j * (1 - i))),
                pl.BlockSpec((rows, step), lambda i, j, m: (0, j * i)),
            ],
            out_specs=pl.BlockSpec((step, rows), lambda i, j, m: (j, i ^ m[0])),
        ),
        cost_estimate=cost(200.0),
        name="order",
    )(own_at.reshape(1), hbm(own), hbm(other))


def transpose_kernel(x_ref, out):
    out[...] = x_ref[...].T


def transpose(x):
    rows, cols = x.shape
    step = 256
    return pl.pallas_call(
        transpose_kernel,
        out_shape=pltpu.HBM((cols, rows), x.dtype),
        grid=(rows // step,),
        in_specs=[pl.BlockSpec((step, cols), lambda i: (i, 0))],
        out_specs=pl.BlockSpec((cols, step), lambda i: (0, i)),
        cost_estimate=CHEAP,
        name="transpose",
    )(hbm(x))


def project_kernel(info, *refs, count, halves, width, fresh):
    pairs = refs[: 2 * count]
    gain = refs[2 * count]
    weights = refs[2 * count + 1 : 2 * count + 1 + halves]
    scale, ones = refs[2 * count + 1 + halves : 2 * count + 3 + halves]
    normed_ref, q_ref, kv_ref, mine_ref, w = refs[-5:]
    j, tile = pl.program_id(0), pl.program_id(1)
    step = normed_ref.shape[0]

    @pl.when((j == 0) & (tile == 0))
    def _():
        for i, ref in enumerate(weights):
            h = ref.shape[0]
            start = (info[count + 2] ^ i) * h if halves == 2 else 0
            w[pl.ds(pl.multiple_of(start, 16), h), :] = ref[...]
        if not fresh:
            mine_ref[...] = refs[2 * count + 3 + halves][...]

    def work(x_ref):
        value = x_ref[...]
        x = value.astype(f32)
        inverse = lax.rsqrt(jnp.mean(x * x, axis=-1, keepdims=True) + epsilon)
        normed = (x * inverse * gain[...]).astype(bf16)
        normed_ref[...] = normed
        q_ref[...] = (
            jnp.dot(normed, w[:, :width], preferred_element_type=f32) * scale[...]
        ).astype(bf16)
        kv_ref[...] = (
            jnp.dot(normed, w[:, width:], preferred_element_type=f32) + ones[...]
        ).astype(bf16)

        @pl.when(info[count + 1] == info[j])
        def _():
            mine_ref[pl.ds(pl.multiple_of(tile * step, step), step), :] = value

    for i in range(count):
        for lane in range(2):

            @pl.when((j == i) & (info[count] == lane))
            def _(i=i, lane=lane):
                work(pairs[2 * i + 1 - lane])


def project(pairs, places, lane, mine, wt, gain, weights, scale, ones, group_len, carried=None):
    count = len(pairs)
    rows, d = pairs[0][0].shape
    width = scale.shape[1]
    step = 256
    tiles = rows // step
    full = lambda j, t, f: (0, 0)
    at = lambda j, t, f: (f[j] * tiles + t, 0)
    once = pl.Buffered(1)
    info = jnp.stack(list(places) + [lane.astype(jnp.int32), mine, wt])
    args = [x for pair in pairs for x in pair] + [gain, *map(hbm, weights), scale, ones]
    in_specs = [
        pl.BlockSpec(
            (step, d),
            lambda j, t, f, i=i: (jnp.where(j == i, t, jnp.where(j > i, tiles - 1, 0)), 0),
        )
        for i in range(count)
        for _ in range(2)
    ]
    in_specs += [pl.BlockSpec((1, d), full, pipeline_mode=once)]
    in_specs += [pl.BlockSpec(w.shape, full, pipeline_mode=once) for w in weights]
    in_specs += [
        pl.BlockSpec((1, width), full, pipeline_mode=once),
        pl.BlockSpec((1, 2 * width), full, pipeline_mode=once),
    ]
    aliases = {}
    if carried is not None:
        base = len(args) + 2
        args += [hbm(x) for x in (carried[3], *carried[:3])]
        in_specs += [pl.BlockSpec((rows, d), full, pipeline_mode=once)]
        in_specs += [pl.BlockSpec(memory_space=pl.ANY)] * 3
        aliases = {base: 0, base + 1: 1, base + 2: 2}
    return pl.pallas_call(
        functools.partial(
            project_kernel, count=count, halves=len(weights), width=width, fresh=carried is None
        ),
        out_shape=[
            pltpu.HBM((group_len, d), bf16),
            pltpu.HBM((group_len, width), bf16),
            pltpu.HBM((group_len, 2 * width), bf16),
            pltpu.HBM((rows, d), bf16),
        ],
        grid_spec=pltpu.PrefetchScalarGridSpec(
            num_scalar_prefetch=1,
            grid=(count, tiles),
            in_specs=in_specs,
            out_specs=[
                pl.BlockSpec((step, d), at),
                pl.BlockSpec((step, width), at),
                pl.BlockSpec((step, 2 * width), at),
                pl.BlockSpec((rows, d), full),
            ],
            scratch_shapes=[pltpu.VMEM((d, 3 * width), bf16)],
        ),
        input_output_aliases=aliases,
        compiler_params=pltpu.CompilerParams(vmem_limit_bytes=32 << 20),
        cost_estimate=cost(15),
        name="project",
    )(info, *args)


def tail_body(at, p0, p1, p2, p3, x_ref, g_ref, w_s, gain, outs, need):
    lo_ref, left_ref, right_ref, gr_ref, c0, c1, c2, c3, gg_ref = outs
    att_ref, nm_ref, act_ref = (left_ref.at[i] for i in range(3))
    gp_ref, gh_ref = (right_ref.at[i] for i in range(2))
    right_ref[2] = g_ref[...]
    mine = at[0]
    pieces = (p0, p1, p2, p3)
    cols = p0.shape[1]
    nt = (((1,), (1,)), ((), ()))
    for i in range(4):

        @pl.when(mine == i)
        def _(i=i):
            att_ref[...] = jnp.concatenate([pieces[i ^ k][...] for k in range(4)], axis=1)

    need(0)
    resid = x_ref[...].astype(f32) + jnp.dot(att_ref[...], w_s[0], preferred_element_type=f32)
    inverse = lax.rsqrt(jnp.mean(resid * resid, axis=-1, keepdims=True) + epsilon)
    normed = (resid * inverse * gain[...]).astype(bf16)
    nm_ref[...] = normed
    need(1)
    hidden = jnp.dot(normed, w_s[1], preferred_element_type=f32)
    sig = 1.0 / (1.0 + jnp.exp(-hidden))
    active = (hidden * sig).astype(bf16)
    act_ref[...] = active
    need(2)
    lo_ref[...] = (resid + jnp.dot(active, w_s[2], preferred_element_type=f32)).astype(bf16)
    grad_active = lax.dot_general(g_ref[...], w_s[2], nt, preferred_element_type=f32)
    grad_hidden = (grad_active * sig * (1.0 + hidden * (1.0 - sig))).astype(bf16)
    gh_ref[...] = grad_hidden
    grad_normed = lax.dot_general(grad_hidden, w_s[1], nt, preferred_element_type=f32)
    gg_ref[...] += jnp.sum(grad_normed * resid * inverse, axis=0, keepdims=True)
    scaled = grad_normed * gain[...]
    grad_resid = (
        g_ref[...].astype(f32)
        + inverse * scaled
        - resid * (inverse * inverse * inverse) * jnp.mean(scaled * resid, axis=-1, keepdims=True)
    )
    gr_ref[...] = grad_resid
    grad_proj = grad_resid.astype(bf16)
    gp_ref[...] = grad_proj
    grad_att = lax.dot_general(grad_proj, w_s[0], nt, preferred_element_type=f32).astype(bf16)
    for i in range(4):

        @pl.when(mine == i)
        def _(i=i):
            for j, out in enumerate((c0, c1, c2, c3)):
                out[...] = grad_att[:, (i ^ j) * cols : ((i ^ j) + 1) * cols]


def tail_kernel(at, p0, p1, p2, p3, x_ref, g_ref, own0, own1, own2, half, other, gain, *refs, rows, hrows):
    w_s, sems = refs[-2:]
    outs = refs[:-2]

    def copies(i):
        parts = (((own0, own1, own2)[i], at[1], rows), (half.at[i], at[2], hrows), (other.at[i], at[3], hrows))
        return [
            pltpu.make_async_copy(
                part, w_s.at[i, pl.ds(pl.multiple_of(start, 16), n), :], sems.at[3 * i + k]
            )
            for k, (part, start, n) in enumerate(parts)
        ]

    @pl.when(pl.program_id(0) == 0)
    def _():
        outs[-1][...] = jnp.zeros_like(outs[-1])
        for i in range(3):
            for c in copies(i):
                c.start()

    def need(i):
        @pl.when(pl.program_id(0) == 0)
        def _():
            for c in copies(i):
                c.wait()

    tail_body(at, p0, p1, p2, p3, x_ref, g_ref, w_s, gain, outs, need)


def whole_tail_kernel(at, p0, p1, p2, p3, x_ref, g_ref, w, gain, *outs):
    @pl.when(pl.program_id(0) == 0)
    def _():
        outs[-1][...] = jnp.zeros_like(outs[-1])

    tail_body(at, p0, p1, p2, p3, x_ref, g_ref, w, gain, outs, lambda i: None)


def tail(at, pieces, x, g, weights, gain, tile=256):
    rows, d = x.shape
    cols = pieces[0].shape[1]
    row = lambda i, m: (i, 0)
    once = pl.Buffered(1)
    whole = lambda *shape: pl.BlockSpec(shape, lambda i, m: (0,) * len(shape), pipeline_mode=once)
    wide = pl.BlockSpec((tile, d), row)
    slim = pl.BlockSpec((tile, cols), row)
    if len(weights) == 5:
        body = functools.partial(tail_kernel, rows=weights[0].shape[0], hrows=weights[3].shape[1])
        scratch = [pltpu.VMEM((3, d, d), bf16), pltpu.SemaphoreType.DMA((9,))]
        weight_specs = [pl.BlockSpec(memory_space=pl.ANY)] * 5
    else:
        body = whole_tail_kernel
        scratch = []
        weight_specs = [whole(*w.shape) for w in weights]
    return pl.pallas_call(
        body,
        out_shape=[pltpu.HBM((rows, d), bf16)]
        + [pltpu.HBM((3, rows, d), bf16)] * 2
        + [pltpu.HBM((rows, d), f32)]
        + [pltpu.HBM((rows, cols), bf16)] * 4
        + [pltpu.HBM((1, d), f32)],
        grid_spec=pltpu.PrefetchScalarGridSpec(
            num_scalar_prefetch=1,
            grid=(rows // tile,),
            in_specs=[slim] * 4 + [wide] * 2 + weight_specs + [whole(1, d)],
            out_specs=[wide]
            + [pl.BlockSpec((3, tile, d), lambda i, m: (0, i, 0))] * 2
            + [wide]
            + [slim] * 4
            + [pl.BlockSpec((1, d), lambda i, m: (0, 0))],
            scratch_shapes=scratch,
        ),
        compiler_params=pltpu.CompilerParams(vmem_limit_bytes=52 << 20),
        cost_estimate=cost(0.01),
        name="tail",
    )(at, *pieces, hbm(x), g, *map(hbm, weights), gain)


tn_dims = (((0,), (0,)), ((), ()))


def share_kernel(col, left, right, out):
    value = lax.dot_general(left[0], right[0], tn_dims, preferred_element_type=f32)
    out[...] = value.astype(bf16)


def share(left, right, col):
    n, rows, d = left.shape
    w = d // 2
    block = pl.BlockSpec((d, w), lambda i, c: (0, i))
    return pl.pallas_call(
        share_kernel,
        out_shape=pltpu.HBM((d, n * w), bf16),
        grid_spec=pltpu.PrefetchScalarGridSpec(
            num_scalar_prefetch=1,
            grid=(n,),
            in_specs=[
                pl.BlockSpec((1, rows, d), lambda i, c: (i, 0, 0)),
                pl.BlockSpec((1, rows, w), lambda i, c: (i, 0, c[0])),
            ],
            out_specs=block,
        ),
        compiler_params=pltpu.CompilerParams(vmem_limit_bytes=20 << 20),
        cost_estimate=CHEAP,
        name="share",
    )(col.reshape(1), hbm(left), hbm(right))


def copy(x):
    return pl.pallas_call(
        tick_kernel, out_shape=pltpu.HBM(x.shape, x.dtype), cost_estimate=CHEAP, name="copy"
    )(x)


def tick_kernel(x_ref, out):
    out[...] = x_ref[...]


def tick(x):
    return pl.pallas_call(
        tick_kernel, out_shape=jax.ShapeDtypeStruct(x.shape, x.dtype), cost_estimate=cost(200.0), name="tick"
    )(x)


def total_kernel(*refs, counts):
    out = refs[-1]
    start, column = 0, 0
    for count in counts:
        group = refs[start : start + count]
        start += count
        acc = jnp.zeros(group[0].shape[1:], f32)
        for ref in group:
            for i in range(ref.shape[0]):
                acc = acc + ref[i].astype(f32)
        out[:, column : column + acc.shape[1]] = acc.astype(bf16)
        column += acc.shape[1]


def total(groups):
    flat = [x for group in groups for x in group]
    rows = flat[0].shape[1]
    cuts = 2 if rows % 32 == 0 else 1
    width = sum(group[0].shape[2] for group in groups)
    return pl.pallas_call(
        functools.partial(total_kernel, counts=[len(group) for group in groups]),
        out_shape=pltpu.HBM((rows, width), bf16),
        grid=(cuts,),
        in_specs=[
            pl.BlockSpec((x.shape[0], rows // cuts, x.shape[2]), lambda i: (0, i, 0)) for x in flat
        ],
        out_specs=pl.BlockSpec((rows // cuts, width), lambda i: (i, 0)),
        compiler_params=pltpu.CompilerParams(vmem_limit_bytes=16 << 20),
        cost_estimate=cost(0.001),
        name="total",
    )(*flat)


def add_kernel(a_ref, b_ref, out):
    out[...] = (a_ref[...].astype(f32) + b_ref[...].astype(f32)).astype(bf16)


def add(a, b):
    return pl.pallas_call(
        add_kernel, out_shape=pltpu.HBM(a.shape, bf16), cost_estimate=CHEAP, name="add"
    )(a, b)


def add_rows(a, b):
    rows, cols = a.shape
    block = pl.BlockSpec((rows // 5, cols), lambda i: (i, 0))
    return pl.pallas_call(
        add_kernel,
        out_shape=pltpu.HBM(a.shape, bf16),
        grid=(5,),
        in_specs=[block] * 2,
        out_specs=block,
        compiler_params=pltpu.CompilerParams(vmem_limit_bytes=14 << 20),
        cost_estimate=CHEAP,
        name="add_rows",
    )(hbm(a), hbm(b))


def by_bits(first, second, put):
    for i in range(2):
        for j in range(2):

            @pl.when((first == i) & (second == j))
            def _(i=i, j=j):
                put(i, j)


def place_kernel(at, *refs):
    o0, o1, o2 = refs[-3:]
    block = pl.program_id(0)
    w = o0.shape[2] // 2

    def put(other_x, other_near):
        for core in range(2):

            @pl.when(at[2] == core)
            def _(core=core):
                for side in range(2):
                    part = refs[4 * (side ^ core) + 2 * other_x + other_near][...].astype(f32)
                    for i, out in enumerate((o0, o1, o2)):
                        out[0, :, side * w : (side + 1) * w] = part[:, i * w : (i + 1) * w]

    by_bits((block // 2) ^ at[0], (block % 2) ^ at[1], put)


def place_tail(arrays, at):
    h, width = arrays[0].shape
    d = width // 3 * 2
    whole = pl.BlockSpec((h, width), lambda i, m: (0, 0), pipeline_mode=pl.Buffered(1))
    outs = pl.pallas_call(
        place_kernel,
        out_shape=[pltpu.HBM((4, h, d), f32)] * 3,
        grid_spec=pltpu.PrefetchScalarGridSpec(
            num_scalar_prefetch=1,
            grid=(4,),
            in_specs=[whole] * 8,
            out_specs=[pl.BlockSpec((1, h, d), lambda i, m: (i, 0, 0))] * 3,
        ),
        compiler_params=pltpu.CompilerParams(vmem_limit_bytes=16 << 20),
        cost_estimate=CHEAP,
        name="place_tail",
    )(at, *map(hbm, arrays))
    return [out.reshape(4 * h, d) for out in outs]


def cross_kernel(at, x_ref, g_ref, *refs):
    s = refs[-1]
    s[...] = jnp.dot(x_ref[...], g_ref[...], preferred_element_type=f32)
    half = s.shape[0] // 2
    for w in range(2):

        @pl.when(pl.program_id(0) == w)
        def _(w=w):
            for x in range(2):
                rows = pl.ds(pl.multiple_of((at[1] ^ x) * half, 16), half)
                refs[2 * w + x][...] = s[rows, :].astype(bf16)


def cross(x, g, at):
    d, rows = x.shape
    w = d // 2
    cols = g.shape[1]
    step = 512 if cols % 512 == 0 else cols
    n = cols // step
    first = pl.BlockSpec((w // 2, step), lambda i, j, m: (0, jnp.where(i == 0, j, n - 1)))
    second = pl.BlockSpec((w // 2, step), lambda i, j, m: (0, jnp.where(i == 1, j, 0)))
    return pl.pallas_call(
        cross_kernel,
        out_shape=[pltpu.HBM((w // 2, cols), bf16)] * 4,
        grid_spec=pltpu.PrefetchScalarGridSpec(
            num_scalar_prefetch=1,
            grid=(2, n),
            in_specs=[
                pl.BlockSpec((w, rows), lambda i, j, m: (m[0] ^ i, 0)),
                pl.BlockSpec((rows, step), lambda i, j, m: (0, j)),
            ],
            out_specs=[first, first, second, second],
            scratch_shapes=[pltpu.VMEM((w, step), f32)],
        ),
        compiler_params=pltpu.CompilerParams(vmem_limit_bytes=26 << 20),
        cost_estimate=CHEAP,
        name="cross",
    )(at, hbm(x), hbm(g))


def spread_kernel(at, *refs, width):
    out = refs[-1]
    step = out.shape[1]
    rows = pl.ds(pl.multiple_of(pl.program_id(0) * step, step), step)

    def put(core, near):
        cut = []
        for t in range(3):
            for n in range(2):
                for c in range(2):
                    part = refs[2 * (c ^ core) + (n ^ near)][rows, :]
                    cut.append(part[:, t * width : (t + 1) * width])
        out[0] = jnp.concatenate(cut, axis=1).astype(f32)

    by_bits(at[2], at[1], put)


def spread(arrays, at, used, other_x, carried=None):
    rows, cols = arrays[0].shape
    width = 4 * used
    cuts = 2 if rows % 32 == 0 else 1
    whole = pl.BlockSpec((rows, cols), lambda j, m: (0, 0), pipeline_mode=pl.Buffered(1))
    more = () if carried is None else (carried,)
    return pl.pallas_call(
        functools.partial(spread_kernel, width=used // 3),
        out_shape=pltpu.HBM((2, rows, width), f32),
        grid_spec=pltpu.PrefetchScalarGridSpec(
            num_scalar_prefetch=1,
            grid=(cuts,),
            in_specs=[whole] * 4 + [pl.BlockSpec(memory_space=pl.ANY)] * len(more),
            out_specs=pl.BlockSpec((1, rows // cuts, width), lambda j, m: (m[0] ^ other_x, j, 0)),
        ),
        input_output_aliases={5: 0} if more else {},
        compiler_params=pltpu.CompilerParams(vmem_limit_bytes=20 << 20),
        cost_estimate=CHEAP,
        name="spread",
    )(at, *arrays, *more)


def back_kernel(shards, g_ref, w_ref, *refs):
    acc = jnp.dot(g_ref[...], w_ref[...], preferred_element_type=f32)
    if len(refs) == 2:
        acc = acc + refs[0][0].astype(f32)
    refs[-1][0] = acc.astype(bf16)


def back(grad, w, shards, rows, got=None):
    c, d = w.shape
    n = shards.shape[0]
    step = d
    out = pl.BlockSpec((1, rows, step), lambda j, i, f: (i, 0, j))
    in_specs = [
        pl.BlockSpec((rows, c), lambda j, i, f: (f[i], 0)),
        pl.BlockSpec((c, step), lambda j, i, f: (0, j)),
    ]
    args = [hbm(grad), hbm(w)]
    if got is not None:
        in_specs.append(pl.BlockSpec((1, rows, step), lambda j, i, f: (0, 0, j)))
        args.append(got)
    return pl.pallas_call(
        back_kernel,
        out_shape=pltpu.HBM((n, rows, d), bf16),
        grid_spec=pltpu.PrefetchScalarGridSpec(
            num_scalar_prefetch=1, grid=(d // step, n), in_specs=in_specs, out_specs=out
        ),
        compiler_params=pltpu.CompilerParams(vmem_limit_bytes=22 << 20),
        cost_estimate=CHEAP,
        name="back",
    )(shards, *args)


def finish_kernel(shard, g_ref, w_ref, core, near, x_ref, resid, gain, out, gain_out):
    grad = jnp.dot(g_ref[...], w_ref[...], preferred_element_type=f32)
    grad = grad + core[0].astype(f32) + near[0].astype(f32)
    x = x_ref[...].astype(f32)
    inverse = lax.rsqrt(jnp.mean(x * x, axis=-1, keepdims=True) + epsilon)
    part = jnp.sum(grad * x * inverse, axis=0, keepdims=True)

    @pl.when(pl.program_id(0) == 0)
    def _():
        gain_out[...] = jnp.zeros_like(gain_out)

    gain_out[...] += part
    scaled = grad * gain[...]
    out[...] = (
        resid[...]
        + inverse * scaled
        - x * (inverse * inverse * inverse) * jnp.mean(scaled * x, axis=-1, keepdims=True)
    ).astype(bf16)


def finish(grad, w, shard, core, near, x, resid, gain, tile=256):
    rows, d = x.shape
    c = w.shape[0]
    tiles = rows // tile
    row = lambda i, f: (i, 0)
    once = pl.Buffered(1)
    return pl.pallas_call(
        finish_kernel,
        out_shape=[pltpu.HBM((rows, d), bf16), jax.ShapeDtypeStruct((1, d), f32)],
        grid_spec=pltpu.PrefetchScalarGridSpec(
            num_scalar_prefetch=1,
            grid=(tiles,),
            in_specs=[
                pl.BlockSpec((tile, c), lambda i, f: (f[0] * tiles + i, 0)),
                pl.BlockSpec((c, d), lambda i, f: (0, 0), pipeline_mode=once),
                pl.BlockSpec((1, tile, d), lambda i, f: (1, i, 0)),
                pl.BlockSpec((1, tile, d), lambda i, f: (0, i, 0)),
                pl.BlockSpec((tile, d), row),
                pl.BlockSpec((tile, d), row),
                pl.BlockSpec((1, d), lambda i, f: (0, 0)),
            ],
            out_specs=[pl.BlockSpec((tile, d), row), pl.BlockSpec((1, d), lambda i, f: (0, 0))],
        ),
        compiler_params=pltpu.CompilerParams(vmem_limit_bytes=24 << 20),
        cost_estimate=CHEAP,
        name="finish",
    )(shard.reshape(1), hbm(grad), hbm(w), core, near, hbm(x), hbm(resid), gain)


def rms_inverse(values):
    return lax.rsqrt(jnp.mean(values * values, axis=-1, keepdims=True) + epsilon)


def norm_back(values, inverse, grad_scaled):
    return inverse * grad_scaled - values * (inverse * inverse * inverse) * jnp.mean(
        grad_scaled * values, axis=-1, keepdims=True
    )


def dot(left, right):
    return jnp.dot(left, right, preferred_element_type=f32)


def times_trans(left, right):
    return lax.dot_general(left, right, (((1,), (1,)), ((), ())), preferred_element_type=f32)


def trans_times(left, right):
    return lax.dot_general(left, right, (((0,), (0,)), ((), ())), preferred_element_type=f32)


def rows_at(array, start, count):
    return lax.dynamic_slice_in_dim(array, start, count, 0)


def put_rows(array, rows, start):
    return lax.dynamic_update_slice_in_dim(array, rows, start, 0)


def make_local(sizes):
    def pairs(target):
        found = []
        for gx in range(sizes["gx"]):
            for gc in range(sizes["gc"]):
                for z in range(4):
                    for w in range(sizes["wt"]):
                        goal = target(gx, gc, z, w)
                        if goal is not None and goal != (gx, gc, z, w):
                            found.append((place(gx, gc, z, w), place(*goal)))
        return found

    def place(gx, gc, z, w):
        return ((gx * sizes["gc"] + gc) * 4 + z) * sizes["wt"] + w

    def send(value, target):
        return lax.ppermute(value, AXES, pairs(target))

    def core_mate(gx, gc, z, w):
        return (gx, 1 - gc, z, w)

    def x_mate(gx, gc, z, w):
        return (1 - gx, gc, z, w)

    def near_mate(gx, gc, z, w):
        return (gx, gc, z ^ 1, w)

    def far_mate(gx, gc, z, w):
        return (gx, gc, z ^ 2, w)

    def cross_mate(gx, gc, z, w):
        return (gx, 1 - gc, z ^ 1, w)

    def wt_mate(gx, gc, z, w):
        return (gx, gc, z, 1 - w)

    def wt_x_mate(gx, gc, z, w):
        return (1 - gx, gc, z, 1 - w)

    def to_host(gx, gc, z, w):
        return (gx, 1 - (z & 1), 2 * gc + (z >> 1), w)

    def to_home(gx, gc, z, w):
        return (gx, z >> 1, 2 * (z & 1) + 1 - gc, w)

    def hop1(gx, gc, z, w):
        if gc == 0:
            return (gx, 0, z - 1, w) if z > 0 else None
        return (gx, 1, z + 1, w) if z < 3 else None

    def hop2(gx, gc, z, w):
        if gc == 0:
            return (gx, 0, z - 1, w) if z in (1, 2) else None
        return (gx, 1, z + 1, w) if z in (1, 2) else None

    def hop3(gx, gc, z, w):
        if gc == 0:
            return (gx, 0, z ^ 1, w) if z < 2 else None
        return (gx, 1, z ^ 1, w) if z > 1 else None

    def lane_share(gx, gc, z, w):
        return (gx, 1 - gc, z, w) if gc == z >> 1 else None

    def sum_all(value):
        for axis in ("gc", "wt", "near", "far", "gx"):
            step = 1
            while step < sizes[axis]:

                def mate(gx, gc, z, w, axis=axis, step=step):
                    at = dict(gx=gx, gc=gc, far=z >> 1, near=z & 1, wt=w)
                    at[axis] ^= step
                    return (at["gx"], at["gc"], 2 * at["far"] + at["near"], at["wt"])

                value = value + send(value, mate)
                step *= 2
        return value

    def local(
        tokens, segments, w_qkv, w_proj, w_in, w_out, gain_attn, gain_mlp, query_scale, cotangent
    ):
        gx, gc, host, near, wt = (lax.axis_index(axis) for axis in AXES)
        z = 2 * host + near
        mine = 2 * near + 1 - gc
        parts = 4
        nh = H // parts
        groups = 1
        rows = tokens.shape[1]
        group_len = segments.shape[1]
        wrows = w_qkv.shape[0]
        lane = gc == host
        pair = sizes["wt"] == 2

        def after(value, *others):
            return lax.optimization_barrier((value,) + others)[0]

        picked = pick(w_qkv, mine, parts, groups, nh)
        own = tokens[0]
        got1 = send(own, hop1)
        own_share = send(own, lane_share)
        seg_mate = send(segments, core_mate)
        got2 = send(got1, hop2)
        got1_share = send(got1, lane_share)
        end = jnp.where(gc == 0, z == 0, z == 3)
        if pair:
            wide_own = stretch(picked, groups, nh, 2)
            got1 = after(got1, wide_own)
            other_w = send(picked, wt_mate)
            wide_w = (wide_own, stretch(other_w, groups, nh, 10))
        else:
            flat_all = lax.all_gather(picked, "wt", axis=0, tiled=True)
            by_head = jnp.transpose(
                flat_all[:, : 3 * nh * HD].reshape(D, groups, 3, nh // groups, HD), (0, 2, 1, 3, 4)
            )
            wide_w = (
                jnp.pad(
                    by_head.reshape(D, 3 * nh, HD), ((0, 0), (0, 0), (0, LN - HD))
                ).reshape(D, -1),
            )
        got3 = send(jnp.where(end, own, got2), hop3)
        got2_share = send(got2, lane_share)
        way = 1 - 2 * host
        last = jnp.where(host == 0, jnp.where(z == 0, 3, 0), jnp.where(z == 3, 0, 3))
        places = (z, z + way, z + 2 * way, last)

        half_rows = wrows // 2
        half_w = jnp.stack([rows_at(w, gc * half_rows, half_rows) for w in (w_proj, w_in, w_out)])
        if pair:
            half_w = send(after(half_w, other_w), wt_mate)
        else:
            half_w = lax.all_gather(half_w, "wt", axis=0, tiled=False)

        dim_scale = scale_base / math.sqrt(HD) * jax.nn.softplus(query_scale)
        lane_scale = jnp.tile(jnp.pad(dim_scale * log2e, (0, LN - HD)), nh)[None]
        ones = jnp.tile(
            ((jnp.arange(LN) >= HD) & (jnp.arange(LN) < HD + 3)).astype(f32), 2 * nh
        )[None]
        seg_row = jnp.where(lane, segments, seg_mate)[0]
        fixed = (lane, mine, wt, gain_attn[None], wide_w, lane_scale, ones, group_len)
        carried = project(((own, own_share), (got1, got1_share)), places[:2], *fixed)
        got3_share = send(after(got3, carried[0]), lane_share)
        all_normed, queries, keyval, inputs = project(
            ((got2, got2_share), (got3, got3_share)), places[2:], *fixed, carried=carried
        )
        grad_mlp = send(after(cotangent[0], got3_share), to_host)

        att, att_float, q_aug = attn_fwd(queries, keyval, seg_row, nh)
        att, half_w, _ = lax.optimization_barrier((att, half_w, grad_mlp))

        trades = (core_mate, near_mate, cross_mate)
        att_pieces = [rows_at(att, (mine ^ j) * rows, rows) for j in range(parts)]
        half_mate = send(after(half_w, *att_pieces), core_mate)
        att_pieces = [att_pieces[0]] + [send(att_pieces[j + 1], trades[j]) for j in range(3)]
        if pair:
            w_trans = order(after(picked, att), other_w, wt)
        else:
            w_trans = flat_all.T
        normed_trans = transpose(after(all_normed, w_trans))
        if pair:
            weights = (w_proj, w_in, w_out, half_w, half_mate)
            starts = (wt * wrows, (1 - wt) * wrows + gc * half_rows, (1 - wt) * wrows + (1 - gc) * half_rows)
        else:
            one = gc == 0
            tail_w = jnp.stack(
                [jnp.where(one, half_w, half_mate), jnp.where(one, half_mate, half_w)], axis=1
            )
            weights = (jnp.transpose(tail_w, (2, 0, 1, 3, 4)).reshape(3, D, D),)
            starts = ()
        (
            layer_out,
            left,
            right,
            grad_resid,
            *pieces,
            grad_gain_mlp,
        ) = tail(
            jnp.stack([mine, *starts]), att_pieces, after(inputs, normed_trans), grad_mlp, weights, gain_mlp[None]
        )
        pieces = [pieces[0]] + [send(pieces[j + 1], trades[j]) for j in range(3)]

        shared = share(after(left, pieces[1]), right, 1 - gc)
        from_core = send(shared, core_mate)
        own_half = share(left, right, after(gc, shared))
        pieces[2:] = [after(piece, own_half) for piece in pieces[2:]]
        home_out = send(after(layer_out, *pieces[1:]), to_home)
        late_gain = tick(after(gain_attn.reshape(-1, LN), *pieces[1:]))
        summed = add_rows(own_half, after(from_core, late_gain))
        kept = lax.all_to_all(summed, ("wt", "gx", "near"), 0, 0, tiled=True)

        scale_row = jnp.tile(dim_scale, nh // groups)[None]

        def backward(group, *others):
            first, *rest = pieces
            return attn_bwd(
                q_aug,
                keyval,
                (after(first, summed, *others), *rest),
                att_float,
                mine,
                seg_row,
                scale_row,
                nh,
                group,
                groups,
            )

        def by_rows(grad):
            if pair:
                own, *rest = cross(normed_trans, grad, jnp.stack([wt, gx]))
                got = [send(part, mate) for part, mate in zip(rest, (x_mate, wt_mate, wt_x_mate))]
                return [part[None] for part in (own, *got)]
            part = dot(normed_trans, grad).astype(bf16)
            sources = sizes["wt"] * 2
            got = lax.all_to_all(part, ("wt", "gx"), 0, 0, tiled=True)
            return [got.reshape(sources, D // sources, -1)]

        grad_project, grad_lanes = backward(0)
        layer_out = after(home_out, grad_project)

        last_step = [layer_out]

        def turn(value):
            return after(value, *last_step)

        def done(value):
            last_step[0] = value
            return value

        sources = sizes["wt"] * 4
        to_core = done(back(turn(grad_project), w_trans, jnp.stack([mine ^ 3, mine ^ 1]), rows))
        from_core = send(to_core, core_mate)
        by_place = by_rows(turn(grad_project))
        done(by_place[0])
        to_near = done(back(grad_project, w_trans, (mine ^ 2).reshape(1), rows, turn(from_core)))
        from_near = send(to_near, near_mate)
        t1 = done(total([[turn(kept).reshape(sources, D // sources, -1)]]))
        t1_far = send(t1, far_mate)
        layer_out = done(copy(turn(layer_out)))
        by_place[0] = turn(by_place[0])
        q1 = done(total([by_place]))
        q1_far = send(q1, far_mate)
        t2 = done(add(turn(t1), t1_far))
        t2_near = send(t2, near_mate)
        t2_x = send(t2, x_mate)
        grad_tokens, grad_gain_attn = finish(
            grad_project,
            w_trans,
            mine,
            from_core,
            turn(from_near),
            inputs,
            grad_resid,
            late_gain.reshape(1, -1),
        )
        done(grad_tokens)
        grad_query_scale = (
            grad_lanes[0, :HD]
            / (dim_scale * log2e)
            * (scale_base / math.sqrt(HD))
            * jax.nn.sigmoid(query_scale)
        )
        small = jnp.concatenate(
            [grad_gain_attn[0], grad_gain_mlp[0], jnp.pad(grad_query_scale, (0, LN - HD))]
        ).reshape(-1, LN)
        t2_x = done(turn(t2_x))
        t2_near = done(turn(t2_near))
        t2_near_x = send(t2_near, x_mate)
        tails = [t2, t2_near, t2_x]
        tails_mate = [send(turn(x), core_mate) for x in tails]
        q2 = done(add(turn(q1), q1_far))
        q2_near = send(q2, near_mate)
        q2_x = send(q2, x_mate)
        home_grad = send(turn(grad_tokens), to_home)
        q2_near = done(turn(q2_near))
        q2_near_x = send(q2_near, x_mate)
        t2_near_x = done(turn(t2_near_x))
        tails += [t2_near_x]
        tails_mate += [send(t2_near_x, core_mate)]
        q2_x = done(turn(q2_x))
        quads_mate = [send(turn(x), core_mate) for x in (q2, q2_near, q2_x)]
        tails_mate[3] = turn(tails_mate[3])
        totals = place_tail(tails + tails_mate, jnp.stack([gx, near, gc]))
        done(totals[0])
        used = 3 * nh * HD
        spread_at = jnp.stack([gx, near, 1 - gc])
        quads_mate[0] = done(after(turn(quads_mate[0]), quads_mate[1]))
        small = done(sum_all(turn(small))).reshape(-1)
        home_grad = done(turn(home_grad))
        q2_near_x = done(turn(q2_near_x))
        last_mate = send(q2_near_x, core_mate)
        total_qkv = done(
            spread((turn(q2), q2_near, quads_mate[0], quads_mate[1]), spread_at, used, 0)
        )
        grad_tokens = done(copy(turn(home_grad)))
        total_qkv = spread(
            (q2_x, turn(q2_near_x), quads_mate[2], last_mate), spread_at, used, 1, total_qkv
        ).reshape(wrows, 3 * D)
        return (
            layer_out[None],
            grad_tokens[None],
            total_qkv,
            *totals,
            small[:D],
            small[D : 2 * D],
            small[2 * D : 2 * D + HD],
        )

    return local


def solution(mesh):
    groups, parts, wt = (mesh.shape[axis] for axis in ("grp", "ctx", "wt"))
    inner = Mesh(mesh.devices.reshape(groups // 2, 2, parts // 2, 2, wt), AXES)
    sizes = dict(inner.shape)
    split = P(("gx", "gc", "wt"), ("far", "near"), None)
    weight = P("wt", None)
    return jax.shard_map(
        make_local(sizes),
        mesh=inner,
        in_specs=(
            split,
            P(("gx", "gc", "wt"), None),
            weight,
            weight,
            weight,
            weight,
            P(),
            P(),
            P(),
            split,
        ),
        out_specs=(split, split, weight, weight, weight, weight, P(), P(), P()),
        check_vma=False,
    )
```

```python
import functools
import math

import jax
import jax.numpy as jnp
from jax import lax
from jax.experimental import pallas as pl
from jax.experimental.pallas import tpu as pltpu
from jax.sharding import Mesh
from jax.sharding import PartitionSpec as P

D = 1280
H = 16
HD = 80
LN = 128
epsilon = 1e-06
scale_base = 1.442695041
log2e = 1.4426950408889634
NEG = -1e30
def cost(us):
    return pl.CostEstimate(flops=int(us * 1_000_000_000), transcendentals=0, bytes_accessed=1000)


CHEAP = cost(0.001)
f32 = jnp.float32
bf16 = jnp.bfloat16
AXES = ("gx", "gc", "far", "near", "wt")


def hbm(x):
    return pltpu.with_memory_space_constraint(x, pltpu.HBM)


def block_flags(seg_row, bq, bk):
    n = seg_row.shape[0]
    q = seg_row.reshape(n // bq, bq)
    k = seg_row.reshape(n // bk, bk)
    qf, ql = q[:, 0][:, None], q[:, -1][:, None]
    kf, kl = k[:, 0][None], k[:, -1][None]
    qs = jnp.arange(n // bq, dtype=jnp.int32)[:, None] * bq
    ks = jnp.arange(n // bk, dtype=jnp.int32)[None] * bk
    below = ks + bk - 1 <= qs
    skip = (ks > qs + bq - 1) | ((kf > 0) & (kl < qf))
    same = (qf == ql) & (kl == ql) & ((kf == kl) | ((kf == 0) & (kl == 1)))
    full = below & ((kl == 0) | same)
    flags = jnp.where(skip, 0, jnp.where(full, 1, 2))
    if bq == bk:
        flags = jnp.where(qs == ks, 3, flags)
    return flags.astype(jnp.int32).reshape(-1)


def put_split(base, col, lanes):
    hi = col.astype(bf16).astype(f32)
    rest = col - hi
    mid = rest.astype(bf16).astype(f32)
    out = jnp.where(lanes == HD, hi, base)
    out = jnp.where(lanes == HD + 1, mid, out)
    return jnp.where(lanes == HD + 2, rest - mid, out).astype(bf16)


def fwd_kernel(flags, q_ref, kv, segc, segr, att, of, qaug, m_s, acc_s, *, nh, bq, bk, nk):
    qi = pl.program_id(0)
    count = (qi * bq + bq + bk - 1) // bk
    nt = (((1,), (1,)), ((), ()))
    acc_s[...] = jnp.zeros_like(acc_s)
    m_s[...] = jnp.zeros_like(m_s)

    def mask(ko, q0=0, qn=bq, kn=bk):
        qpos = qi * bq + q0 + lax.broadcasted_iota(jnp.int32, (qn, kn), 0)
        kpos = ko + lax.broadcasted_iota(jnp.int32, (qn, kn), 1)
        ks = segr[:, pl.ds(ko, kn)]
        return (kpos <= qpos) & ((ks == 0) | (ks == segc[q0 : q0 + qn, :]))

    def step(kb, masked, q0=0, qn=bq, kn=bk):
        ko = pl.multiple_of(kb * bk, bk)
        if masked:
            allowed = mask(ko, q0, qn, kn)
        rows = slice(q0, q0 + qn)
        for h in range(nh):
            k = kv[pl.ds(ko, kn), h * LN : (h + 1) * LN]
            v = kv[pl.ds(ko, kn), (nh + h) * LN : (nh + h + 1) * LN]
            q = q_ref[rows, h * LN : (h + 1) * LN]
            p = jnp.exp2(lax.dot_general(q, k, nt, preferred_element_type=f32))
            if masked:
                p = jnp.where(allowed, p, 0.0)
            acc_s[h, rows, :] += jnp.dot(p.astype(bf16), v, preferred_element_type=f32)

    def body(kb, carry):
        flag = flags[qi * nk + kb]

        @pl.when(flag == 1)
        def _():
            step(kb, False)

        @pl.when(flag >= 2)
        def _():
            step(kb, True)

        return carry

    lax.fori_loop(0, count, body, 0)
    bad = jnp.zeros((bq, 1), f32)
    for h in range(nh):
        total = acc_s[h][:, HD : HD + 1]
        bad = jnp.maximum(bad, jnp.where((total > 2.0**-60) & (total < 2.0**60), 0.0, 1.0))

    @pl.when(jnp.max(bad) > 0.0)
    def _():
        def head(h, carry):
            kc = pl.ds(pl.multiple_of(h * LN, LN), LN)
            vc = pl.ds(pl.multiple_of((nh + h) * LN, LN), LN)
            m_s[h] = jnp.full((bq, LN), NEG, f32)
            acc_s[h] = jnp.zeros((bq, LN), f32)

            def inner(kb, carry):
                @pl.when(flags[qi * nk + kb] > 0)
                def _():
                    ko = pl.multiple_of(kb * bk, bk)
                    s = lax.dot_general(
                        q_ref[:, kc], kv[pl.ds(ko, bk), kc], nt, preferred_element_type=f32
                    )
                    s = jnp.where(mask(ko), s, NEG)
                    old = m_s[h]
                    new = jnp.maximum(old, jnp.max(s, axis=1, keepdims=True))
                    p = jnp.exp2(s - new[:, :1]).astype(bf16)
                    m_s[h] = new
                    acc_s[h] = acc_s[h] * jnp.exp2(old - new) + jnp.dot(
                        p, kv[pl.ds(ko, bk), vc], preferred_element_type=f32
                    )

                return carry

            lax.fori_loop(0, count, inner, 0)
            return carry

        lax.fori_loop(0, nh, head, 0)

    lanes = lax.broadcasted_iota(jnp.int32, (bq, LN), 1)
    outs = []
    for h in range(nh):
        acc = acc_s[h]
        total = acc[:, HD : HD + 1]
        out = acc * (1.0 / total)
        of[:, h * LN : (h + 1) * LN] = jnp.where(lanes < HD, out, 0.0).astype(bf16)
        outs.append(out[:, :HD])
        lse = m_s[h][:, :1] + jnp.log2(total)
        qaug[:, h * LN : (h + 1) * LN] = put_split(
            q_ref[:, h * LN : (h + 1) * LN].astype(f32), -lse, lanes
        )
    att[...] = jnp.concatenate(outs, axis=1).astype(bf16)


def attn_fwd(q, kv, seg_row, nh, bq=512, bk=512):
    n = q.shape[0]
    w = nh * LN
    spec = pltpu.PrefetchScalarGridSpec(
        num_scalar_prefetch=1,
        grid=(n // bq,),
        in_specs=[
            pl.BlockSpec((bq, w), lambda i, f: (i, 0)),
            pl.BlockSpec((n, 2 * w), lambda i, f: (0, 0)),
            pl.BlockSpec((bq, 1), lambda i, f: (i, 0)),
            pl.BlockSpec((1, n), lambda i, f: (0, 0)),
        ],
        out_specs=[
            pl.BlockSpec((bq, nh * HD), lambda i, f: (i, 0)),
            pl.BlockSpec((bq, w), lambda i, f: (i, 0)),
            pl.BlockSpec((bq, w), lambda i, f: (i, 0)),
        ],
        scratch_shapes=[pltpu.VMEM((nh, bq, LN), f32), pltpu.VMEM((nh, bq, LN), f32)],
    )
    return pl.pallas_call(
        functools.partial(fwd_kernel, nh=nh, bq=bq, bk=bk, nk=n // bk),
        out_shape=[
            pltpu.HBM((n, nh * HD), bf16),
            pltpu.HBM((n, w), bf16),
            pltpu.HBM((n, w), bf16),
        ],
        grid_spec=spec,
        compiler_params=pltpu.CompilerParams(vmem_limit_bytes=28 << 20),
        cost_estimate=cost(0.01),
        name="attn_fwd",
    )(block_flags(seg_row, bq, bk), hbm(q), hbm(kv), seg_row[:, None], seg_row[None])


def bwd_kernel(
    flags, mine, qa, kk, vv, do0, do1, do2, do3, of, segc, segr, scale, dqkv, gscale, doa_s, dq_s, dk_s, dv_s, *, first, nh, bq, bk, n
):
    nk = n // bk
    nq = n // bq
    kb = pl.program_id(0)
    part = n // 4
    step_rows = 256 if part % 256 == 0 else part
    lanes = lax.broadcasted_iota(jnp.int32, (step_rows, LN), 1)

    @pl.when(kb == 0)
    def _():
        dq_s[...] = jnp.zeros_like(dq_s)
        for j, piece in enumerate((do0, do1, do2, do3)):
            start = (mine[0] ^ j) * part
            for i in range(part // step_rows):
                d = piece[i * step_rows : (i + 1) * step_rows, :].astype(f32)
                r = pl.ds(pl.multiple_of(start + i * step_rows, step_rows), step_rows)
                for h in range(nh):
                    at = (first + h) * HD
                    dh = jnp.concatenate(
                        [d[:, at : at + HD], jnp.zeros((step_rows, LN - HD), f32)], axis=1
                    )
                    c = slice(h * LN, (h + 1) * LN)
                    delta = jnp.sum(dh * of[r, c].astype(f32), axis=1, keepdims=True)
                    doa_s[r, c] = put_split(dh, -delta, lanes)

    dk_s[...] = jnp.zeros_like(dk_s)
    dv_s[...] = jnp.zeros_like(dv_s)
    ko = kb * bk
    nt = (((1,), (1,)), ((), ()))
    tn = (((0,), (0,)), ((), ()))

    def step(qi, masked, q0=0, qn=bq, kn=bk):
        qo = pl.multiple_of(qi * bq + q0, qn)
        rows = slice(0, kn)
        if masked:
            kpos = ko + lax.broadcasted_iota(jnp.int32, (kn, qn), 0)
            qpos = qo + lax.broadcasted_iota(jnp.int32, (kn, qn), 1)
            ks = segc[rows, :]
            allowed = (kpos <= qpos) & ((ks == 0) | (ks == segr[:, pl.ds(qo, qn)]))
        for h in range(nh):
            c = slice(h * LN, (h + 1) * LN)
            q = qa[pl.ds(qo, qn), c]
            k = kk[rows, c]
            d = doa_s[pl.ds(qo, qn), c]
            p = jnp.exp2(lax.dot_general(k, q, nt, preferred_element_type=f32))
            if masked:
                p = jnp.where(allowed, p, 0.0)
            ds = (p * lax.dot_general(vv[rows, c], d, nt, preferred_element_type=f32)).astype(bf16)
            dv_s[h, rows, :] += jnp.dot(p.astype(bf16), d, preferred_element_type=f32)
            dk_s[h, rows, :] += jnp.dot(ds, q, preferred_element_type=f32)
            dq_s[h, pl.ds(qo, qn), :] += lax.dot_general(ds, k, tn, preferred_element_type=f32)

    def body(qi, carry):
        flag = flags[qi * nk + kb]

        @pl.when(flag == 1)
        def _():
            step(qi, False)

        @pl.when(flag == 2)
        def _():
            step(qi, True)

        if bq == bk:

            @pl.when(flag == 3)
            def _():
                step(qi, True, 0, bq // 2, bk // 2)
                step(qi, True, bq // 2, bq // 2, bk)

        return carry

    lax.fori_loop(ko // bq, nq, body, 0)
    r = pl.multiple_of(ko, bk)
    ln2 = math.log(2.0)
    gap = dqkv.shape[1] - 3 * nh * HD
    dqkv[pl.ds(r, bk), nh * HD :] = jnp.concatenate(
        [dk_s[h][:, :HD] * ln2 for h in range(nh)]
        + [dv_s[h][:, :HD] for h in range(nh)]
        + [jnp.zeros((bk, gap), f32)],
        axis=1,
    ).astype(bf16)

    @pl.when(kb == nk - 1)
    def _():
        total = jnp.zeros((1, LN), f32)
        for i in range(nq):
            rows = slice(i * bq, (i + 1) * bq)
            for h in range(nh):
                total = total + jnp.sum(
                    dq_s[h, rows, :] * qa[rows, h * LN : (h + 1) * LN].astype(f32), axis=0, keepdims=True
                )
            grads = jnp.concatenate([dq_s[h, rows, :][:, :HD] for h in range(nh)], axis=1)
            dqkv[rows, 0 : nh * HD] = (grads * scale[...]).astype(bf16)
        gscale[...] = jnp.broadcast_to(total, gscale.shape)


def attn_bwd(qa, kv, pieces, of, mine, seg_row, scale, heads, group, groups, bq=512, bk=512):
    n = qa.shape[0]
    nh = heads // groups
    w = nh * LN
    once = pl.Buffered(1)
    spec = pltpu.PrefetchScalarGridSpec(
        num_scalar_prefetch=2,
        grid=(n // bk,),
        in_specs=[
            pl.BlockSpec((n, w), lambda i, f, m: (0, group), pipeline_mode=once),
            pl.BlockSpec((bk, w), lambda i, f, m: (i, group)),
            pl.BlockSpec((bk, w), lambda i, f, m: (i, groups + group)),
            *[pl.BlockSpec((n // 4, heads * HD), lambda i, f, m: (0, 0), pipeline_mode=once)] * 4,
            pl.BlockSpec((n, w), lambda i, f, m: (0, group), pipeline_mode=once),
            pl.BlockSpec((bk, 1), lambda i, f, m: (i, 0)),
            pl.BlockSpec((1, n), lambda i, f, m: (0, 0)),
            pl.BlockSpec((1, nh * HD), lambda i, f, m: (0, 0)),
        ],
        out_specs=[
            pl.BlockSpec((n, lanes_up(3 * nh * HD)), lambda i, f, m: (0, 0)),
            pl.BlockSpec((8, LN), lambda i, f, m: (0, 0)),
        ],
        scratch_shapes=[
            pltpu.VMEM((n, w), bf16),
            pltpu.VMEM((nh, n, LN), f32),
            pltpu.VMEM((nh, bk, LN), f32),
            pltpu.VMEM((nh, bk, LN), f32),
        ],
    )
    return pl.pallas_call(
        functools.partial(bwd_kernel, first=group * nh, nh=nh, bq=bq, bk=bk, n=n),
        out_shape=[
            pltpu.HBM((n, lanes_up(3 * nh * HD)), bf16),
            pltpu.HBM((8, LN), f32),
        ],
        grid_spec=spec,
        compiler_params=pltpu.CompilerParams(vmem_limit_bytes=48 << 20),
        cost_estimate=cost(300 if group == 0 else 0.001),
        name="attn_bwd",
    )(block_flags(seg_row, bq, bk), mine.reshape(1), hbm(qa), hbm(kv), hbm(kv), *pieces, hbm(of), seg_row[:, None], seg_row[None], scale)


def quarter_columns(place, parts, groups, nh):
    width = nh // groups * HD
    return [
        (t * D + place * nh * HD + g * width, width) for g in range(groups) for t in range(3)
    ]


def pick_kernel(mine, w_ref, out, *, parts, groups, nh):
    for i in range(parts):

        @pl.when(mine[0] == i)
        def _(i=i):
            cut = [w_ref[:, a : a + width] for a, width in quarter_columns(i, parts, groups, nh)]
            used = sum(x.shape[1] for x in cut)
            pad = jnp.zeros((cut[0].shape[0], out.shape[1] - used), out.dtype)
            out[...] = jnp.concatenate(cut + [pad], axis=1)


def lanes_up(n):
    return -(-n // LN) * LN


def pick(w, mine, parts, groups, nh):
    rows = w.shape[0]
    step = 160 if rows % 160 == 0 else rows
    return pl.pallas_call(
        functools.partial(pick_kernel, parts=parts, groups=groups, nh=nh),
        out_shape=pltpu.HBM((rows, lanes_up(3 * nh * HD)), w.dtype),
        grid_spec=pltpu.PrefetchScalarGridSpec(
            num_scalar_prefetch=1,
            grid=(rows // step,),
            in_specs=[pl.BlockSpec((step, 3 * D), lambda i, m: (i, 0))],
            out_specs=pl.BlockSpec((step, lanes_up(3 * nh * HD)), lambda i, m: (i, 0)),
        ),
        cost_estimate=cost(5),
        name="pick",
    )(mine.reshape(1), hbm(w))


def stretch_kernel(x_ref, out, *, groups, nh):
    value = x_ref[...]
    each = 3 * nh * HD // groups
    zero = jnp.zeros((value.shape[0], LN - HD), value.dtype)
    per = nh // groups
    wide = []
    for t in range(3):
        for h in range(nh):
            at = (h // per) * each + t * per * HD + (h % per) * HD
            wide += [value[:, at : at + HD], zero]
    out[...] = jnp.concatenate(wide, axis=1)


def stretch(x, groups, nh, us):
    rows, width = x.shape
    step = 160
    return pl.pallas_call(
        functools.partial(stretch_kernel, groups=groups, nh=nh),
        out_shape=pltpu.HBM((rows, 3 * nh * LN), x.dtype),
        grid=(rows // step,),
        in_specs=[pl.BlockSpec((step, width), lambda i: (i, 0))],
        out_specs=pl.BlockSpec((step, 3 * nh * LN), lambda i: (i, 0)),
        cost_estimate=cost(us),
        name="stretch",
    )(hbm(x))


def order_kernel(own_first, a_ref, b_ref, out):
    half = pl.program_id(0)

    @pl.when(half == 0)
    def _():
        out[...] = a_ref[...].T

    @pl.when(half == 1)
    def _():
        out[...] = b_ref[...].T


def order(own, other, own_at):
    rows, width = own.shape
    step = 256
    return pl.pallas_call(
        order_kernel,
        out_shape=pltpu.HBM((width, 2 * rows), own.dtype),
        grid_spec=pltpu.PrefetchScalarGridSpec(
            num_scalar_prefetch=1,
            grid=(2, width // step),
            in_specs=[
                pl.BlockSpec((rows, step), lambda i, j, m: (0, j * (1 - i))),
                pl.BlockSpec((rows, step), lambda i, j, m: (0, j * i)),
            ],
            out_specs=pl.BlockSpec((step, rows), lambda i, j, m: (j, i ^ m[0])),
        ),
        cost_estimate=cost(200.0),
        name="order",
    )(own_at.reshape(1), hbm(own), hbm(other))


def transpose_kernel(x_ref, out):
    out[...] = x_ref[...].T


def transpose(x):
    rows, cols = x.shape
    step = 256
    return pl.pallas_call(
        transpose_kernel,
        out_shape=pltpu.HBM((cols, rows), x.dtype),
        grid=(rows // step,),
        in_specs=[pl.BlockSpec((step, cols), lambda i: (i, 0))],
        out_specs=pl.BlockSpec((cols, step), lambda i: (0, i)),
        cost_estimate=CHEAP,
        name="transpose",
    )(hbm(x))


def project_kernel(info, *refs, count, halves, width, fresh):
    pairs = refs[: 2 * count]
    gain = refs[2 * count]
    weights = refs[2 * count + 1 : 2 * count + 1 + halves]
    scale, ones = refs[2 * count + 1 + halves : 2 * count + 3 + halves]
    normed_ref, q_ref, kv_ref, mine_ref, w = refs[-5:]
    j, tile = pl.program_id(0), pl.program_id(1)
    step = normed_ref.shape[0]

    @pl.when((j == 0) & (tile == 0))
    def _():
        for i, ref in enumerate(weights):
            h = ref.shape[0]
            start = (info[count + 2] ^ i) * h if halves == 2 else 0
            w[pl.ds(pl.multiple_of(start, 16), h), :] = ref[...]
        if not fresh:
            mine_ref[...] = refs[2 * count + 3 + halves][...]

    def work(x_ref):
        value = x_ref[...]
        x = value.astype(f32)
        inverse = lax.rsqrt(jnp.mean(x * x, axis=-1, keepdims=True) + epsilon)
        normed = (x * inverse * gain[...]).astype(bf16)
        normed_ref[...] = normed
        q_ref[...] = (
            jnp.dot(normed, w[:, :width], preferred_element_type=f32) * scale[...]
        ).astype(bf16)
        kv_ref[...] = (
            jnp.dot(normed, w[:, width:], preferred_element_type=f32) + ones[...]
        ).astype(bf16)

        @pl.when(info[count + 1] == info[j])
        def _():
            mine_ref[pl.ds(pl.multiple_of(tile * step, step), step), :] = value

    for i in range(count):
        for lane in range(2):

            @pl.when((j == i) & (info[count] == lane))
            def _(i=i, lane=lane):
                work(pairs[2 * i + 1 - lane])


def project(pairs, places, lane, mine, wt, gain, weights, scale, ones, group_len, carried=None):
    count = len(pairs)
    rows, d = pairs[0][0].shape
    width = scale.shape[1]
    step = 256
    tiles = rows // step
    full = lambda j, t, f: (0, 0)
    at = lambda j, t, f: (f[j] * tiles + t, 0)
    once = pl.Buffered(1)
    info = jnp.stack(list(places) + [lane.astype(jnp.int32), mine, wt])
    args = [x for pair in pairs for x in pair] + [gain, *map(hbm, weights), scale, ones]
    in_specs = [
        pl.BlockSpec(
            (step, d),
            lambda j, t, f, i=i: (jnp.where(j == i, t, jnp.where(j > i, tiles - 1, 0)), 0),
        )
        for i in range(count)
        for _ in range(2)
    ]
    in_specs += [pl.BlockSpec((1, d), full, pipeline_mode=once)]
    in_specs += [pl.BlockSpec(w.shape, full, pipeline_mode=once) for w in weights]
    in_specs += [
        pl.BlockSpec((1, width), full, pipeline_mode=once),
        pl.BlockSpec((1, 2 * width), full, pipeline_mode=once),
    ]
    aliases = {}
    if carried is not None:
        base = len(args) + 2
        args += [hbm(x) for x in (carried[3], *carried[:3])]
        in_specs += [pl.BlockSpec((rows, d), full, pipeline_mode=once)]
        in_specs += [pl.BlockSpec(memory_space=pl.ANY)] * 3
        aliases = {base: 0, base + 1: 1, base + 2: 2}
    return pl.pallas_call(
        functools.partial(
            project_kernel, count=count, halves=len(weights), width=width, fresh=carried is None
        ),
        out_shape=[
            pltpu.HBM((group_len, d), bf16),
            pltpu.HBM((group_len, width), bf16),
            pltpu.HBM((group_len, 2 * width), bf16),
            pltpu.HBM((rows, d), bf16),
        ],
        grid_spec=pltpu.PrefetchScalarGridSpec(
            num_scalar_prefetch=1,
            grid=(count, tiles),
            in_specs=in_specs,
            out_specs=[
                pl.BlockSpec((step, d), at),
                pl.BlockSpec((step, width), at),
                pl.BlockSpec((step, 2 * width), at),
                pl.BlockSpec((rows, d), full),
            ],
            scratch_shapes=[pltpu.VMEM((d, 3 * width), bf16)],
        ),
        input_output_aliases=aliases,
        compiler_params=pltpu.CompilerParams(vmem_limit_bytes=32 << 20),
        cost_estimate=cost(15),
        name="project",
    )(info, *args)


def tail_body(at, p0, p1, p2, p3, x_ref, g_ref, w_s, gain, outs, need):
    lo_ref, left_ref, right_ref, gr_ref, c0, c1, c2, c3, gg_ref = outs
    att_ref, nm_ref, act_ref = (left_ref.at[i] for i in range(3))
    gp_ref, gh_ref = (right_ref.at[i] for i in range(2))
    right_ref[2] = g_ref[...]
    mine = at[0]
    pieces = (p0, p1, p2, p3)
    cols = p0.shape[1]
    nt = (((1,), (1,)), ((), ()))
    for i in range(4):

        @pl.when(mine == i)
        def _(i=i):
            att_ref[...] = jnp.concatenate([pieces[i ^ k][...] for k in range(4)], axis=1)

    need(0)
    resid = x_ref[...].astype(f32) + jnp.dot(att_ref[...], w_s[0], preferred_element_type=f32)
    inverse = lax.rsqrt(jnp.mean(resid * resid, axis=-1, keepdims=True) + epsilon)
    normed = (resid * inverse * gain[...]).astype(bf16)
    nm_ref[...] = normed
    need(1)
    hidden = jnp.dot(normed, w_s[1], preferred_element_type=f32)
    sig = 1.0 / (1.0 + jnp.exp(-hidden))
    active = (hidden * sig).astype(bf16)
    act_ref[...] = active
    need(2)
    lo_ref[...] = (resid + jnp.dot(active, w_s[2], preferred_element_type=f32)).astype(bf16)
    grad_active = lax.dot_general(g_ref[...], w_s[2], nt, preferred_element_type=f32)
    grad_hidden = (grad_active * sig * (1.0 + hidden * (1.0 - sig))).astype(bf16)
    gh_ref[...] = grad_hidden
    grad_normed = lax.dot_general(grad_hidden, w_s[1], nt, preferred_element_type=f32)
    gg_ref[...] += jnp.sum(grad_normed * resid * inverse, axis=0, keepdims=True)
    scaled = grad_normed * gain[...]
    grad_resid = (
        g_ref[...].astype(f32)
        + inverse * scaled
        - resid * (inverse * inverse * inverse) * jnp.mean(scaled * resid, axis=-1, keepdims=True)
    )
    gr_ref[...] = grad_resid
    grad_proj = grad_resid.astype(bf16)
    gp_ref[...] = grad_proj
    grad_att = lax.dot_general(grad_proj, w_s[0], nt, preferred_element_type=f32).astype(bf16)
    for i in range(4):

        @pl.when(mine == i)
        def _(i=i):
            for j, out in enumerate((c0, c1, c2, c3)):
                out[...] = grad_att[:, (i ^ j) * cols : ((i ^ j) + 1) * cols]


def tail_kernel(at, p0, p1, p2, p3, x_ref, g_ref, own0, own1, own2, half, other, gain, *refs, rows, hrows):
    w_s, sems = refs[-2:]
    outs = refs[:-2]

    def copies(i):
        parts = (((own0, own1, own2)[i], at[1], rows), (half.at[i], at[2], hrows), (other.at[i], at[3], hrows))
        return [
            pltpu.make_async_copy(
                part, w_s.at[i, pl.ds(pl.multiple_of(start, 16), n), :], sems.at[3 * i + k]
            )
            for k, (part, start, n) in enumerate(parts)
        ]

    @pl.when(pl.program_id(0) == 0)
    def _():
        outs[-1][...] = jnp.zeros_like(outs[-1])
        for i in range(3):
            for c in copies(i):
                c.start()

    def need(i):
        @pl.when(pl.program_id(0) == 0)
        def _():
            for c in copies(i):
                c.wait()

    tail_body(at, p0, p1, p2, p3, x_ref, g_ref, w_s, gain, outs, need)


def whole_tail_kernel(at, p0, p1, p2, p3, x_ref, g_ref, w, gain, *outs):
    @pl.when(pl.program_id(0) == 0)
    def _():
        outs[-1][...] = jnp.zeros_like(outs[-1])

    tail_body(at, p0, p1, p2, p3, x_ref, g_ref, w, gain, outs, lambda i: None)


def tail(at, pieces, x, g, weights, gain, tile=256):
    rows, d = x.shape
    cols = pieces[0].shape[1]
    row = lambda i, m: (i, 0)
    once = pl.Buffered(1)
    whole = lambda *shape: pl.BlockSpec(shape, lambda i, m: (0,) * len(shape), pipeline_mode=once)
    wide = pl.BlockSpec((tile, d), row)
    slim = pl.BlockSpec((tile, cols), row)
    if len(weights) == 5:
        body = functools.partial(tail_kernel, rows=weights[0].shape[0], hrows=weights[3].shape[1])
        scratch = [pltpu.VMEM((3, d, d), bf16), pltpu.SemaphoreType.DMA((9,))]
        weight_specs = [pl.BlockSpec(memory_space=pl.ANY)] * 5
    else:
        body = whole_tail_kernel
        scratch = []
        weight_specs = [whole(*w.shape) for w in weights]
    return pl.pallas_call(
        body,
        out_shape=[pltpu.HBM((rows, d), bf16)]
        + [pltpu.HBM((3, rows, d), bf16)] * 2
        + [pltpu.HBM((rows, d), f32)]
        + [pltpu.HBM((rows, cols), bf16)] * 4
        + [pltpu.HBM((1, d), f32)],
        grid_spec=pltpu.PrefetchScalarGridSpec(
            num_scalar_prefetch=1,
            grid=(rows // tile,),
            in_specs=[slim] * 4 + [wide] * 2 + weight_specs + [whole(1, d)],
            out_specs=[wide]
            + [pl.BlockSpec((3, tile, d), lambda i, m: (0, i, 0))] * 2
            + [wide]
            + [slim] * 4
            + [pl.BlockSpec((1, d), lambda i, m: (0, 0))],
            scratch_shapes=scratch,
        ),
        compiler_params=pltpu.CompilerParams(vmem_limit_bytes=52 << 20),
        cost_estimate=cost(0.01),
        name="tail",
    )(at, *pieces, hbm(x), g, *map(hbm, weights), gain)


tn_dims = (((0,), (0,)), ((), ()))


def share_kernel(col, left, right, out):
    value = lax.dot_general(left[0], right[0], tn_dims, preferred_element_type=f32)
    out[...] = value.astype(bf16)


def share(left, right, col):
    n, rows, d = left.shape
    w = d // 2
    block = pl.BlockSpec((d, w), lambda i, c: (0, i))
    return pl.pallas_call(
        share_kernel,
        out_shape=pltpu.HBM((d, n * w), bf16),
        grid_spec=pltpu.PrefetchScalarGridSpec(
            num_scalar_prefetch=1,
            grid=(n,),
            in_specs=[
                pl.BlockSpec((1, rows, d), lambda i, c: (i, 0, 0)),
                pl.BlockSpec((1, rows, w), lambda i, c: (i, 0, c[0])),
            ],
            out_specs=block,
        ),
        compiler_params=pltpu.CompilerParams(vmem_limit_bytes=20 << 20),
        cost_estimate=CHEAP,
        name="share",
    )(col.reshape(1), hbm(left), hbm(right))


def copy(x):
    return pl.pallas_call(
        tick_kernel, out_shape=pltpu.HBM(x.shape, x.dtype), cost_estimate=CHEAP, name="copy"
    )(x)


def tick_kernel(x_ref, out):
    out[...] = x_ref[...]


def tick(x):
    return pl.pallas_call(
        tick_kernel, out_shape=jax.ShapeDtypeStruct(x.shape, x.dtype), cost_estimate=cost(200.0), name="tick"
    )(x)


def total_kernel(*refs, counts):
    out = refs[-1]
    start, column = 0, 0
    for count in counts:
        group = refs[start : start + count]
        start += count
        acc = jnp.zeros(group[0].shape[1:], f32)
        for ref in group:
            for i in range(ref.shape[0]):
                acc = acc + ref[i].astype(f32)
        out[:, column : column + acc.shape[1]] = acc.astype(bf16)
        column += acc.shape[1]


def total(groups):
    flat = [x for group in groups for x in group]
    rows = flat[0].shape[1]
    cuts = 2 if rows % 32 == 0 else 1
    width = sum(group[0].shape[2] for group in groups)
    return pl.pallas_call(
        functools.partial(total_kernel, counts=[len(group) for group in groups]),
        out_shape=pltpu.HBM((rows, width), bf16),
        grid=(cuts,),
        in_specs=[
            pl.BlockSpec((x.shape[0], rows // cuts, x.shape[2]), lambda i: (0, i, 0)) for x in flat
        ],
        out_specs=pl.BlockSpec((rows // cuts, width), lambda i: (i, 0)),
        compiler_params=pltpu.CompilerParams(vmem_limit_bytes=16 << 20),
        cost_estimate=cost(0.001),
        name="total",
    )(*flat)


def add_kernel(a_ref, b_ref, out):
    out[...] = (a_ref[...].astype(f32) + b_ref[...].astype(f32)).astype(bf16)


def add(a, b):
    return pl.pallas_call(
        add_kernel, out_shape=pltpu.HBM(a.shape, bf16), cost_estimate=CHEAP, name="add"
    )(a, b)


def add_rows(a, b):
    rows, cols = a.shape
    block = pl.BlockSpec((rows // 5, cols), lambda i: (i, 0))
    return pl.pallas_call(
        add_kernel,
        out_shape=pltpu.HBM(a.shape, bf16),
        grid=(5,),
        in_specs=[block] * 2,
        out_specs=block,
        compiler_params=pltpu.CompilerParams(vmem_limit_bytes=14 << 20),
        cost_estimate=CHEAP,
        name="add_rows",
    )(hbm(a), hbm(b))


def by_bits(first, second, put):
    for i in range(2):
        for j in range(2):

            @pl.when((first == i) & (second == j))
            def _(i=i, j=j):
                put(i, j)


def place_kernel(at, *refs):
    o0, o1, o2 = refs[-3:]
    block = pl.program_id(0)
    w = o0.shape[2] // 2

    def put(other_x, other_near):
        for core in range(2):

            @pl.when(at[2] == core)
            def _(core=core):
                for side in range(2):
                    part = refs[4 * (side ^ core) + 2 * other_x + other_near][...].astype(f32)
                    for i, out in enumerate((o0, o1, o2)):
                        out[0, :, side * w : (side + 1) * w] = part[:, i * w : (i + 1) * w]

    by_bits((block // 2) ^ at[0], (block % 2) ^ at[1], put)


def place_tail(arrays, at):
    h, width = arrays[0].shape
    d = width // 3 * 2
    whole = pl.BlockSpec((h, width), lambda i, m: (0, 0), pipeline_mode=pl.Buffered(1))
    outs = pl.pallas_call(
        place_kernel,
        out_shape=[pltpu.HBM((4, h, d), f32)] * 3,
        grid_spec=pltpu.PrefetchScalarGridSpec(
            num_scalar_prefetch=1,
            grid=(4,),
            in_specs=[whole] * 8,
            out_specs=[pl.BlockSpec((1, h, d), lambda i, m: (i, 0, 0))] * 3,
        ),
        compiler_params=pltpu.CompilerParams(vmem_limit_bytes=16 << 20),
        cost_estimate=CHEAP,
        name="place_tail",
    )(at, *map(hbm, arrays))
    return [out.reshape(4 * h, d) for out in outs]


def cross_kernel(at, x_ref, g_ref, *refs):
    s = refs[-1]
    s[...] = jnp.dot(x_ref[...], g_ref[...], preferred_element_type=f32)
    half = s.shape[0] // 2
    for w in range(2):

        @pl.when(pl.program_id(0) == w)
        def _(w=w):
            for x in range(2):
                rows = pl.ds(pl.multiple_of((at[1] ^ x) * half, 16), half)
                refs[2 * w + x][...] = s[rows, :].astype(bf16)


def cross(x, g, at):
    d, rows = x.shape
    w = d // 2
    cols = g.shape[1]
    step = 512 if cols % 512 == 0 else cols
    n = cols // step
    first = pl.BlockSpec((w // 2, step), lambda i, j, m: (0, jnp.where(i == 0, j, n - 1)))
    second = pl.BlockSpec((w // 2, step), lambda i, j, m: (0, jnp.where(i == 1, j, 0)))
    return pl.pallas_call(
        cross_kernel,
        out_shape=[pltpu.HBM((w // 2, cols), bf16)] * 4,
        grid_spec=pltpu.PrefetchScalarGridSpec(
            num_scalar_prefetch=1,
            grid=(2, n),
            in_specs=[
                pl.BlockSpec((w, rows), lambda i, j, m: (m[0] ^ i, 0)),
                pl.BlockSpec((rows, step), lambda i, j, m: (0, j)),
            ],
            out_specs=[first, first, second, second],
            scratch_shapes=[pltpu.VMEM((w, step), f32)],
        ),
        compiler_params=pltpu.CompilerParams(vmem_limit_bytes=26 << 20),
        cost_estimate=CHEAP,
        name="cross",
    )(at, hbm(x), hbm(g))


def spread_kernel(at, *refs, width):
    out = refs[-1]
    step = out.shape[1]
    rows = pl.ds(pl.multiple_of(pl.program_id(0) * step, step), step)

    def put(core, near):
        cut = []
        for t in range(3):
            for n in range(2):
                for c in range(2):
                    part = refs[2 * (c ^ core) + (n ^ near)][rows, :]
                    cut.append(part[:, t * width : (t + 1) * width])
        out[0] = jnp.concatenate(cut, axis=1).astype(f32)

    by_bits(at[2], at[1], put)


def spread(arrays, at, used, other_x, carried=None):
    rows, cols = arrays[0].shape
    width = 4 * used
    cuts = 2 if rows % 32 == 0 else 1
    whole = pl.BlockSpec((rows, cols), lambda j, m: (0, 0), pipeline_mode=pl.Buffered(1))
    more = () if carried is None else (carried,)
    return pl.pallas_call(
        functools.partial(spread_kernel, width=used // 3),
        out_shape=pltpu.HBM((2, rows, width), f32),
        grid_spec=pltpu.PrefetchScalarGridSpec(
            num_scalar_prefetch=1,
            grid=(cuts,),
            in_specs=[whole] * 4 + [pl.BlockSpec(memory_space=pl.ANY)] * len(more),
            out_specs=pl.BlockSpec((1, rows // cuts, width), lambda j, m: (m[0] ^ other_x, j, 0)),
        ),
        input_output_aliases={5: 0} if more else {},
        compiler_params=pltpu.CompilerParams(vmem_limit_bytes=20 << 20),
        cost_estimate=CHEAP,
        name="spread",
    )(at, *arrays, *more)


def back_kernel(shards, g_ref, w_ref, *refs):
    acc = jnp.dot(g_ref[...], w_ref[...], preferred_element_type=f32)
    if len(refs) == 2:
        acc = acc + refs[0][0].astype(f32)
    refs[-1][0] = acc.astype(bf16)


def back(grad, w, shards, rows, got=None):
    c, d = w.shape
    n = shards.shape[0]
    step = d
    out = pl.BlockSpec((1, rows, step), lambda j, i, f: (i, 0, j))
    in_specs = [
        pl.BlockSpec((rows, c), lambda j, i, f: (f[i], 0)),
        pl.BlockSpec((c, step), lambda j, i, f: (0, j)),
    ]
    args = [hbm(grad), hbm(w)]
    if got is not None:
        in_specs.append(pl.BlockSpec((1, rows, step), lambda j, i, f: (0, 0, j)))
        args.append(got)
    return pl.pallas_call(
        back_kernel,
        out_shape=pltpu.HBM((n, rows, d), bf16),
        grid_spec=pltpu.PrefetchScalarGridSpec(
            num_scalar_prefetch=1, grid=(d // step, n), in_specs=in_specs, out_specs=out
        ),
        compiler_params=pltpu.CompilerParams(vmem_limit_bytes=22 << 20),
        cost_estimate=CHEAP,
        name="back",
    )(shards, *args)


def finish_kernel(shard, g_ref, w_ref, core, near, x_ref, resid, gain, out, gain_out):
    grad = jnp.dot(g_ref[...], w_ref[...], preferred_element_type=f32)
    grad = grad + core[0].astype(f32) + near[0].astype(f32)
    x = x_ref[...].astype(f32)
    inverse = lax.rsqrt(jnp.mean(x * x, axis=-1, keepdims=True) + epsilon)
    part = jnp.sum(grad * x * inverse, axis=0, keepdims=True)

    @pl.when(pl.program_id(0) == 0)
    def _():
        gain_out[...] = jnp.zeros_like(gain_out)

    gain_out[...] += part
    scaled = grad * gain[...]
    out[...] = (
        resid[...]
        + inverse * scaled
        - x * (inverse * inverse * inverse) * jnp.mean(scaled * x, axis=-1, keepdims=True)
    ).astype(bf16)


def finish(grad, w, shard, core, near, x, resid, gain, tile=256):
    rows, d = x.shape
    c = w.shape[0]
    tiles = rows // tile
    row = lambda i, f: (i, 0)
    once = pl.Buffered(1)
    return pl.pallas_call(
        finish_kernel,
        out_shape=[pltpu.HBM((rows, d), bf16), jax.ShapeDtypeStruct((1, d), f32)],
        grid_spec=pltpu.PrefetchScalarGridSpec(
            num_scalar_prefetch=1,
            grid=(tiles,),
            in_specs=[
                pl.BlockSpec((tile, c), lambda i, f: (f[0] * tiles + i, 0)),
                pl.BlockSpec((c, d), lambda i, f: (0, 0), pipeline_mode=once),
                pl.BlockSpec((1, tile, d), lambda i, f: (1, i, 0)),
                pl.BlockSpec((1, tile, d), lambda i, f: (0, i, 0)),
                pl.BlockSpec((tile, d), row),
                pl.BlockSpec((tile, d), row),
                pl.BlockSpec((1, d), lambda i, f: (0, 0)),
            ],
            out_specs=[pl.BlockSpec((tile, d), row), pl.BlockSpec((1, d), lambda i, f: (0, 0))],
        ),
        compiler_params=pltpu.CompilerParams(vmem_limit_bytes=24 << 20),
        cost_estimate=CHEAP,
        name="finish",
    )(shard.reshape(1), hbm(grad), hbm(w), core, near, hbm(x), hbm(resid), gain)


def rms_inverse(values):
    return lax.rsqrt(jnp.mean(values * values, axis=-1, keepdims=True) + epsilon)


def norm_back(values, inverse, grad_scaled):
    return inverse * grad_scaled - values * (inverse * inverse * inverse) * jnp.mean(
        grad_scaled * values, axis=-1, keepdims=True
    )


def dot(left, right):
    return jnp.dot(left, right, preferred_element_type=f32)


def times_trans(left, right):
    return lax.dot_general(left, right, (((1,), (1,)), ((), ())), preferred_element_type=f32)


def trans_times(left, right):
    return lax.dot_general(left, right, (((0,), (0,)), ((), ())), preferred_element_type=f32)


def rows_at(array, start, count):
    return lax.dynamic_slice_in_dim(array, start, count, 0)


def put_rows(array, rows, start):
    return lax.dynamic_update_slice_in_dim(array, rows, start, 0)


def make_local(sizes):
    def pairs(target):
        found = []
        for gx in range(sizes["gx"]):
            for gc in range(sizes["gc"]):
                for z in range(4):
                    for w in range(sizes["wt"]):
                        goal = target(gx, gc, z, w)
                        if goal is not None and goal != (gx, gc, z, w):
                            found.append((place(gx, gc, z, w), place(*goal)))
        return found

    def place(gx, gc, z, w):
        return ((gx * sizes["gc"] + gc) * 4 + z) * sizes["wt"] + w

    def send(value, target):
        return lax.ppermute(value, AXES, pairs(target))

    def core_mate(gx, gc, z, w):
        return (gx, 1 - gc, z, w)

    def x_mate(gx, gc, z, w):
        return (1 - gx, gc, z, w)

    def near_mate(gx, gc, z, w):
        return (gx, gc, z ^ 1, w)

    def far_mate(gx, gc, z, w):
        return (gx, gc, z ^ 2, w)

    def cross_mate(gx, gc, z, w):
        return (gx, 1 - gc, z ^ 1, w)

    def wt_mate(gx, gc, z, w):
        return (gx, gc, z, 1 - w)

    def wt_x_mate(gx, gc, z, w):
        return (1 - gx, gc, z, 1 - w)

    def to_host(gx, gc, z, w):
        return (gx, 1 - (z & 1), 2 * gc + (z >> 1), w)

    def to_home(gx, gc, z, w):
        return (gx, z >> 1, 2 * (z & 1) + 1 - gc, w)

    def hop1(gx, gc, z, w):
        if gc == 0:
            return (gx, 0, z - 1, w) if z > 0 else None
        return (gx, 1, z + 1, w) if z < 3 else None

    def hop2(gx, gc, z, w):
        if gc == 0:
            return (gx, 0, z - 1, w) if z in (1, 2) else None
        return (gx, 1, z + 1, w) if z in (1, 2) else None

    def hop3(gx, gc, z, w):
        if gc == 0:
            return (gx, 0, z ^ 1, w) if z < 2 else None
        return (gx, 1, z ^ 1, w) if z > 1 else None

    def lane_share(gx, gc, z, w):
        return (gx, 1 - gc, z, w) if gc == z >> 1 else None

    def sum_all(value):
        for axis in ("gc", "wt", "near", "far", "gx"):
            step = 1
            while step < sizes[axis]:

                def mate(gx, gc, z, w, axis=axis, step=step):
                    at = dict(gx=gx, gc=gc, far=z >> 1, near=z & 1, wt=w)
                    at[axis] ^= step
                    return (at["gx"], at["gc"], 2 * at["far"] + at["near"], at["wt"])

                value = value + send(value, mate)
                step *= 2
        return value

    def local(
        tokens, segments, w_qkv, w_proj, w_in, w_out, gain_attn, gain_mlp, query_scale, cotangent
    ):
        gx, gc, host, near, wt = (lax.axis_index(axis) for axis in AXES)
        z = 2 * host + near
        mine = 2 * near + 1 - gc
        parts = 4
        nh = H // parts
        groups = 1
        rows = tokens.shape[1]
        group_len = segments.shape[1]
        wrows = w_qkv.shape[0]
        lane = gc == host
        pair = sizes["wt"] == 2

        def after(value, *others):
            return lax.optimization_barrier((value,) + others)[0]

        picked = pick(w_qkv, mine, parts, groups, nh)
        own = tokens[0]
        got1 = send(own, hop1)
        own_share = send(after(own, picked), lane_share)
        seg_mate = send(after(segments, picked), core_mate)
        got2 = send(got1, hop2)
        got1_share = send(got1, lane_share)
        end = jnp.where(gc == 0, z == 0, z == 3)
        if pair:
            wide_own = stretch(picked, groups, nh, 2)
            got1 = after(got1, wide_own)
            other_w = send(picked, wt_mate)
            wide_w = (wide_own, stretch(other_w, groups, nh, 10))
        else:
            flat_all = lax.all_gather(picked, "wt", axis=0, tiled=True)
            by_head = jnp.transpose(
                flat_all[:, : 3 * nh * HD].reshape(D, groups, 3, nh // groups, HD), (0, 2, 1, 3, 4)
            )
            wide_w = (
                jnp.pad(
                    by_head.reshape(D, 3 * nh, HD), ((0, 0), (0, 0), (0, LN - HD))
                ).reshape(D, -1),
            )
        got3 = send(jnp.where(end, own, got2), hop3)
        got2_share = send(got2, lane_share)
        way = 1 - 2 * host
        last = jnp.where(host == 0, jnp.where(z == 0, 3, 0), jnp.where(z == 3, 0, 3))
        places = (z, z + way, z + 2 * way, last)

        half_rows = wrows // 2
        half_w = jnp.stack([rows_at(w, gc * half_rows, half_rows) for w in (w_proj, w_in, w_out)])
        if pair:
            half_w = send(after(half_w, other_w), wt_mate)
        else:
            half_w = lax.all_gather(half_w, "wt", axis=0, tiled=False)

        dim_scale = scale_base / math.sqrt(HD) * jax.nn.softplus(query_scale)
        lane_scale = jnp.tile(jnp.pad(dim_scale * log2e, (0, LN - HD)), nh)[None]
        ones = jnp.tile(
            ((jnp.arange(LN) >= HD) & (jnp.arange(LN) < HD + 3)).astype(f32), 2 * nh
        )[None]
        seg_row = jnp.where(lane, segments, seg_mate)[0]
        fixed = (lane, mine, wt, gain_attn[None], wide_w, lane_scale, ones, group_len)
        carried = project(((own, own_share), (got1, got1_share)), places[:2], *fixed)
        got3_share = send(after(got3, carried[0]), lane_share)
        all_normed, queries, keyval, inputs = project(
            ((got2, got2_share), (got3, got3_share)), places[2:], *fixed, carried=carried
        )
        grad_mlp = send(after(cotangent[0], got3_share), to_host)

        att, att_float, q_aug = attn_fwd(queries, keyval, seg_row, nh)
        att, half_w, _ = lax.optimization_barrier((att, half_w, grad_mlp))

        trades = (core_mate, near_mate, cross_mate)
        att_pieces = [rows_at(att, (mine ^ j) * rows, rows) for j in range(parts)]
        half_mate = send(after(half_w, *att_pieces), core_mate)
        att_pieces = [att_pieces[0]] + [send(att_pieces[j + 1], trades[j]) for j in range(3)]
        if pair:
            w_trans = order(after(picked, att), other_w, wt)
        else:
            w_trans = flat_all.T
        normed_trans = transpose(after(all_normed, w_trans))
        if pair:
            weights = (w_proj, w_in, w_out, half_w, half_mate)
            starts = (wt * wrows, (1 - wt) * wrows + gc * half_rows, (1 - wt) * wrows + (1 - gc) * half_rows)
        else:
            one = gc == 0
            tail_w = jnp.stack(
                [jnp.where(one, half_w, half_mate), jnp.where(one, half_mate, half_w)], axis=1
            )
            weights = (jnp.transpose(tail_w, (2, 0, 1, 3, 4)).reshape(3, D, D),)
            starts = ()
        (
            layer_out,
            left,
            right,
            grad_resid,
            *pieces,
            grad_gain_mlp,
        ) = tail(
            jnp.stack([mine, *starts]), att_pieces, after(inputs, normed_trans), grad_mlp, weights, gain_mlp[None]
        )
        pieces = [pieces[0]] + [send(pieces[j + 1], trades[j]) for j in range(3)]

        shared = share(after(left, pieces[1]), right, 1 - gc)
        from_core = send(shared, core_mate)
        own_half = share(left, right, after(gc, shared))
        pieces[2:] = [after(piece, own_half) for piece in pieces[2:]]
        home_out = send(after(layer_out, *pieces[1:]), to_home)
        late_gain = tick(after(gain_attn.reshape(-1, LN), *pieces[1:]))
        summed = add_rows(own_half, after(from_core, late_gain))
        kept = lax.all_to_all(summed, ("wt", "gx", "near"), 0, 0, tiled=True)

        scale_row = jnp.tile(dim_scale, nh // groups)[None]

        def backward(group, *others):
            first, *rest = pieces
            return attn_bwd(
                q_aug,
                keyval,
                (after(first, summed, *others), *rest),
                att_float,
                mine,
                seg_row,
                scale_row,
                nh,
                group,
                groups,
            )

        def by_rows(grad):
            if pair:
                own, *rest = cross(normed_trans, grad, jnp.stack([wt, gx]))
                got = [send(part, mate) for part, mate in zip(rest, (x_mate, wt_mate, wt_x_mate))]
                return [part[None] for part in (own, *got)]
            part = dot(normed_trans, grad).astype(bf16)
            sources = sizes["wt"] * 2
            got = lax.all_to_all(part, ("wt", "gx"), 0, 0, tiled=True)
            return [got.reshape(sources, D // sources, -1)]

        grad_project, grad_lanes = backward(0)
        layer_out = after(home_out, grad_project)

        last_step = [layer_out]

        def turn(value):
            return after(value, *last_step)

        def done(value):
            last_step[0] = value
            return value

        sources = sizes["wt"] * 4
        to_core = done(back(turn(grad_project), w_trans, jnp.stack([mine ^ 3, mine ^ 1]), rows))
        from_core = send(to_core, core_mate)
        by_place = by_rows(turn(grad_project))
        done(by_place[0])
        to_near = done(back(grad_project, w_trans, (mine ^ 2).reshape(1), rows, turn(from_core)))
        from_near = send(to_near, near_mate)
        t1 = done(total([[turn(kept).reshape(sources, D // sources, -1)]]))
        t1_far = send(t1, far_mate)
        layer_out = done(copy(turn(layer_out)))
        by_place[0] = turn(by_place[0])
        q1 = done(total([by_place]))
        q1_far = send(q1, far_mate)
        t2 = done(add(turn(t1), t1_far))
        t2_near = send(t2, near_mate)
        t2_x = send(t2, x_mate)
        grad_tokens, grad_gain_attn = finish(
            grad_project,
            w_trans,
            mine,
            from_core,
            turn(from_near),
            inputs,
            grad_resid,
            late_gain.reshape(1, -1),
        )
        done(grad_tokens)
        grad_query_scale = (
            grad_lanes[0, :HD]
            / (dim_scale * log2e)
            * (scale_base / math.sqrt(HD))
            * jax.nn.sigmoid(query_scale)
        )
        small = jnp.concatenate(
            [grad_gain_attn[0], grad_gain_mlp[0], jnp.pad(grad_query_scale, (0, LN - HD))]
        ).reshape(-1, LN)
        t2_x = done(turn(t2_x))
        t2_near = done(turn(t2_near))
        t2_near_x = send(t2_near, x_mate)
        tails = [t2, t2_near, t2_x]
        tails_mate = [send(turn(x), core_mate) for x in tails]
        q2 = done(add(turn(q1), q1_far))
        q2_near = send(q2, near_mate)
        q2_x = send(q2, x_mate)
        home_grad = send(turn(grad_tokens), to_home)
        q2_near = done(turn(q2_near))
        q2_near_x = send(q2_near, x_mate)
        t2_near_x = done(turn(t2_near_x))
        tails += [t2_near_x]
        tails_mate += [send(t2_near_x, core_mate)]
        q2_x = done(turn(q2_x))
        quads_mate = [send(turn(x), core_mate) for x in (q2, q2_near, q2_x)]
        tails_mate[3] = turn(tails_mate[3])
        totals = place_tail(tails + tails_mate, jnp.stack([gx, near, gc]))
        done(totals[0])
        used = 3 * nh * HD
        spread_at = jnp.stack([gx, near, 1 - gc])
        quads_mate[0] = done(after(turn(quads_mate[0]), quads_mate[1]))
        small = done(sum_all(turn(small))).reshape(-1)
        home_grad = done(turn(home_grad))
        q2_near_x = done(turn(q2_near_x))
        last_mate = send(q2_near_x, core_mate)
        total_qkv = done(
            spread((turn(q2), q2_near, quads_mate[0], quads_mate[1]), spread_at, used, 0)
        )
        grad_tokens = done(copy(turn(home_grad)))
        total_qkv = spread(
            (q2_x, turn(q2_near_x), quads_mate[2], last_mate), spread_at, used, 1, total_qkv
        ).reshape(wrows, 3 * D)
        return (
            layer_out[None],
            grad_tokens[None],
            total_qkv,
            *totals,
            small[:D],
            small[D : 2 * D],
            small[2 * D : 2 * D + HD],
        )

    return local


def solution(mesh):
    groups, parts, wt = (mesh.shape[axis] for axis in ("grp", "ctx", "wt"))
    inner = Mesh(mesh.devices.reshape(groups // 2, 2, parts // 2, 2, wt), AXES)
    sizes = dict(inner.shape)
    split = P(("gx", "gc", "wt"), ("far", "near"), None)
    weight = P("wt", None)
    return jax.shard_map(
        make_local(sizes),
        mesh=inner,
        in_specs=(
            split,
            P(("gx", "gc", "wt"), None),
            weight,
            weight,
            weight,
            weight,
            P(),
            P(),
            P(),
            split,
        ),
        out_specs=(split, split, weight, weight, weight, weight, P(), P(), P()),
        check_vma=False,
    )
```

```python
import functools
import math

import jax
import jax.numpy as jnp
from jax import lax
from jax.experimental import pallas as pl
from jax.experimental.pallas import tpu as pltpu
from jax.sharding import Mesh
from jax.sharding import PartitionSpec as P

D = 1280
H = 16
HD = 80
LN = 128
epsilon = 1e-06
scale_base = 1.442695041
log2e = 1.4426950408889634
NEG = -1e30
def cost(us):
    return pl.CostEstimate(flops=int(us * 1_000_000_000), transcendentals=0, bytes_accessed=1000)


CHEAP = cost(0.001)
f32 = jnp.float32
bf16 = jnp.bfloat16
AXES = ("gx", "gc", "far", "near", "wt")


def hbm(x):
    return pltpu.with_memory_space_constraint(x, pltpu.HBM)


def block_flags(seg_row, bq, bk):
    n = seg_row.shape[0]
    q = seg_row.reshape(n // bq, bq)
    k = seg_row.reshape(n // bk, bk)
    qf, ql = q[:, 0][:, None], q[:, -1][:, None]
    kf, kl = k[:, 0][None], k[:, -1][None]
    qs = jnp.arange(n // bq, dtype=jnp.int32)[:, None] * bq
    ks = jnp.arange(n // bk, dtype=jnp.int32)[None] * bk
    below = ks + bk - 1 <= qs
    skip = (ks > qs + bq - 1) | ((kf > 0) & (kl < qf))
    same = (qf == ql) & (kl == ql) & ((kf == kl) | ((kf == 0) & (kl == 1)))
    full = below & ((kl == 0) | same)
    flags = jnp.where(skip, 0, jnp.where(full, 1, 2))
    if bq == bk:
        flags = jnp.where(qs == ks, 3, flags)
    return flags.astype(jnp.int32).reshape(-1)


def put_split(base, col, lanes):
    hi = col.astype(bf16).astype(f32)
    rest = col - hi
    mid = rest.astype(bf16).astype(f32)
    out = jnp.where(lanes == HD, hi, base)
    out = jnp.where(lanes == HD + 1, mid, out)
    return jnp.where(lanes == HD + 2, rest - mid, out).astype(bf16)


def fwd_kernel(flags, q_ref, kv, segc, segr, att, of, qaug, m_s, acc_s, *, nh, bq, bk, nk):
    qi = pl.program_id(0)
    count = (qi * bq + bq + bk - 1) // bk
    nt = (((1,), (1,)), ((), ()))
    acc_s[...] = jnp.zeros_like(acc_s)
    m_s[...] = jnp.zeros_like(m_s)

    def mask(ko, q0=0, qn=bq, kn=bk):
        qpos = qi * bq + q0 + lax.broadcasted_iota(jnp.int32, (qn, kn), 0)
        kpos = ko + lax.broadcasted_iota(jnp.int32, (qn, kn), 1)
        ks = segr[:, pl.ds(ko, kn)]
        return (kpos <= qpos) & ((ks == 0) | (ks == segc[q0 : q0 + qn, :]))

    def step(kb, masked, q0=0, qn=bq, kn=bk):
        ko = pl.multiple_of(kb * bk, bk)
        if masked:
            allowed = mask(ko, q0, qn, kn)
        rows = slice(q0, q0 + qn)
        for h in range(nh):
            k = kv[pl.ds(ko, kn), h * LN : (h + 1) * LN]
            v = kv[pl.ds(ko, kn), (nh + h) * LN : (nh + h + 1) * LN]
            q = q_ref[rows, h * LN : (h + 1) * LN]
            p = jnp.exp2(lax.dot_general(q, k, nt, preferred_element_type=f32))
            if masked:
                p = jnp.where(allowed, p, 0.0)
            acc_s[h, rows, :] += jnp.dot(p.astype(bf16), v, preferred_element_type=f32)

    def body(kb, carry):
        flag = flags[qi * nk + kb]

        @pl.when(flag == 1)
        def _():
            step(kb, False)

        @pl.when(flag >= 2)
        def _():
            step(kb, True)

        return carry

    lax.fori_loop(0, count, body, 0)
    bad = jnp.zeros((bq, 1), f32)
    for h in range(nh):
        total = acc_s[h][:, HD : HD + 1]
        bad = jnp.maximum(bad, jnp.where((total > 2.0**-60) & (total < 2.0**60), 0.0, 1.0))

    @pl.when(jnp.max(bad) > 0.0)
    def _():
        def head(h, carry):
            kc = pl.ds(pl.multiple_of(h * LN, LN), LN)
            vc = pl.ds(pl.multiple_of((nh + h) * LN, LN), LN)
            m_s[h] = jnp.full((bq, LN), NEG, f32)
            acc_s[h] = jnp.zeros((bq, LN), f32)

            def inner(kb, carry):
                @pl.when(flags[qi * nk + kb] > 0)
                def _():
                    ko = pl.multiple_of(kb * bk, bk)
                    s = lax.dot_general(
                        q_ref[:, kc], kv[pl.ds(ko, bk), kc], nt, preferred_element_type=f32
                    )
                    s = jnp.where(mask(ko), s, NEG)
                    old = m_s[h]
                    new = jnp.maximum(old, jnp.max(s, axis=1, keepdims=True))
                    p = jnp.exp2(s - new[:, :1]).astype(bf16)
                    m_s[h] = new
                    acc_s[h] = acc_s[h] * jnp.exp2(old - new) + jnp.dot(
                        p, kv[pl.ds(ko, bk), vc], preferred_element_type=f32
                    )

                return carry

            lax.fori_loop(0, count, inner, 0)
            return carry

        lax.fori_loop(0, nh, head, 0)

    lanes = lax.broadcasted_iota(jnp.int32, (bq, LN), 1)
    outs = []
    for h in range(nh):
        acc = acc_s[h]
        total = acc[:, HD : HD + 1]
        out = acc * (1.0 / total)
        of[:, h * LN : (h + 1) * LN] = jnp.where(lanes < HD, out, 0.0).astype(bf16)
        outs.append(out[:, :HD])
        lse = m_s[h][:, :1] + jnp.log2(total)
        qaug[:, h * LN : (h + 1) * LN] = put_split(
            q_ref[:, h * LN : (h + 1) * LN].astype(f32), -lse, lanes
        )
    att[...] = jnp.concatenate(outs, axis=1).astype(bf16)


def attn_fwd(q, kv, seg_row, nh, bq=512, bk=512):
    n = q.shape[0]
    w = nh * LN
    spec = pltpu.PrefetchScalarGridSpec(
        num_scalar_prefetch=1,
        grid=(n // bq,),
        in_specs=[
            pl.BlockSpec((bq, w), lambda i, f: (i, 0)),
            pl.BlockSpec((n, 2 * w), lambda i, f: (0, 0)),
            pl.BlockSpec((bq, 1), lambda i, f: (i, 0)),
            pl.BlockSpec((1, n), lambda i, f: (0, 0)),
        ],
        out_specs=[
            pl.BlockSpec((bq, nh * HD), lambda i, f: (i, 0)),
            pl.BlockSpec((bq, w), lambda i, f: (i, 0)),
            pl.BlockSpec((bq, w), lambda i, f: (i, 0)),
        ],
        scratch_shapes=[pltpu.VMEM((nh, bq, LN), f32), pltpu.VMEM((nh, bq, LN), f32)],
    )
    return pl.pallas_call(
        functools.partial(fwd_kernel, nh=nh, bq=bq, bk=bk, nk=n // bk),
        out_shape=[
            pltpu.HBM((n, nh * HD), bf16),
            pltpu.HBM((n, w), bf16),
            pltpu.HBM((n, w), bf16),
        ],
        grid_spec=spec,
        compiler_params=pltpu.CompilerParams(vmem_limit_bytes=28 << 20),
        cost_estimate=cost(0.01),
        name="attn_fwd",
    )(block_flags(seg_row, bq, bk), hbm(q), hbm(kv), seg_row[:, None], seg_row[None])


def bwd_kernel(
    flags, mine, qa, kk, vv, do0, do1, do2, do3, of, segc, segr, scale, dqkv, gscale, doa_s, dq_s, dk_s, dv_s, *, first, nh, bq, bk, n
):
    nk = n // bk
    nq = n // bq
    kb = pl.program_id(0)
    part = n // 4
    step_rows = 256 if part % 256 == 0 else part
    lanes = lax.broadcasted_iota(jnp.int32, (step_rows, LN), 1)

    @pl.when(kb == 0)
    def _():
        dq_s[...] = jnp.zeros_like(dq_s)
        for j, piece in enumerate((do0, do1, do2, do3)):
            start = (mine[0] ^ j) * part
            for i in range(part // step_rows):
                d = piece[i * step_rows : (i + 1) * step_rows, :].astype(f32)
                r = pl.ds(pl.multiple_of(start + i * step_rows, step_rows), step_rows)
                for h in range(nh):
                    at = (first + h) * HD
                    dh = jnp.concatenate(
                        [d[:, at : at + HD], jnp.zeros((step_rows, LN - HD), f32)], axis=1
                    )
                    c = slice(h * LN, (h + 1) * LN)
                    delta = jnp.sum(dh * of[r, c].astype(f32), axis=1, keepdims=True)
                    doa_s[r, c] = put_split(dh, -delta, lanes)

    dk_s[...] = jnp.zeros_like(dk_s)
    dv_s[...] = jnp.zeros_like(dv_s)
    ko = kb * bk
    nt = (((1,), (1,)), ((), ()))
    tn = (((0,), (0,)), ((), ()))

    def step(qi, masked, q0=0, qn=bq, kn=bk):
        qo = pl.multiple_of(qi * bq + q0, qn)
        rows = slice(0, kn)
        if masked:
            kpos = ko + lax.broadcasted_iota(jnp.int32, (kn, qn), 0)
            qpos = qo + lax.broadcasted_iota(jnp.int32, (kn, qn), 1)
            ks = segc[rows, :]
            allowed = (kpos <= qpos) & ((ks == 0) | (ks == segr[:, pl.ds(qo, qn)]))
        for h in range(nh):
            c = slice(h * LN, (h + 1) * LN)
            q = qa[pl.ds(qo, qn), c]
            k = kk[rows, c]
            d = doa_s[pl.ds(qo, qn), c]
            p = jnp.exp2(lax.dot_general(k, q, nt, preferred_element_type=f32))
            if masked:
                p = jnp.where(allowed, p, 0.0)
            ds = (p * lax.dot_general(vv[rows, c], d, nt, preferred_element_type=f32)).astype(bf16)
            dv_s[h, rows, :] += jnp.dot(p.astype(bf16), d, preferred_element_type=f32)
            dk_s[h, rows, :] += jnp.dot(ds, q, preferred_element_type=f32)
            dq_s[h, pl.ds(qo, qn), :] += lax.dot_general(ds, k, tn, preferred_element_type=f32)

    def body(qi, carry):
        flag = flags[qi * nk + kb]

        @pl.when(flag == 1)
        def _():
            step(qi, False)

        @pl.when(flag == 2)
        def _():
            step(qi, True)

        if bq == bk:

            @pl.when(flag == 3)
            def _():
                step(qi, True, 0, bq // 2, bk // 2)
                step(qi, True, bq // 2, bq // 2, bk)

        return carry

    lax.fori_loop(ko // bq, nq, body, 0)
    r = pl.multiple_of(ko, bk)
    ln2 = math.log(2.0)
    gap = dqkv.shape[1] - 3 * nh * HD
    dqkv[pl.ds(r, bk), nh * HD :] = jnp.concatenate(
        [dk_s[h][:, :HD] * ln2 for h in range(nh)]
        + [dv_s[h][:, :HD] for h in range(nh)]
        + [jnp.zeros((bk, gap), f32)],
        axis=1,
    ).astype(bf16)

    @pl.when(kb == nk - 1)
    def _():
        total = jnp.zeros((1, LN), f32)
        for i in range(nq):
            rows = slice(i * bq, (i + 1) * bq)
            for h in range(nh):
                total = total + jnp.sum(
                    dq_s[h, rows, :] * qa[rows, h * LN : (h + 1) * LN].astype(f32), axis=0, keepdims=True
                )
            grads = jnp.concatenate([dq_s[h, rows, :][:, :HD] for h in range(nh)], axis=1)
            dqkv[rows, 0 : nh * HD] = (grads * scale[...]).astype(bf16)
        gscale[...] = jnp.broadcast_to(total, gscale.shape)


def attn_bwd(qa, kv, pieces, of, mine, seg_row, scale, heads, group, groups, bq=512, bk=512):
    n = qa.shape[0]
    nh = heads // groups
    w = nh * LN
    once = pl.Buffered(1)
    spec = pltpu.PrefetchScalarGridSpec(
        num_scalar_prefetch=2,
        grid=(n // bk,),
        in_specs=[
            pl.BlockSpec((n, w), lambda i, f, m: (0, group), pipeline_mode=once),
            pl.BlockSpec((bk, w), lambda i, f, m: (i, group)),
            pl.BlockSpec((bk, w), lambda i, f, m: (i, groups + group)),
            *[pl.BlockSpec((n // 4, heads * HD), lambda i, f, m: (0, 0), pipeline_mode=once)] * 4,
            pl.BlockSpec((n, w), lambda i, f, m: (0, group), pipeline_mode=once),
            pl.BlockSpec((bk, 1), lambda i, f, m: (i, 0)),
            pl.BlockSpec((1, n), lambda i, f, m: (0, 0)),
            pl.BlockSpec((1, nh * HD), lambda i, f, m: (0, 0)),
        ],
        out_specs=[
            pl.BlockSpec((n, lanes_up(3 * nh * HD)), lambda i, f, m: (0, 0)),
            pl.BlockSpec((8, LN), lambda i, f, m: (0, 0)),
        ],
        scratch_shapes=[
            pltpu.VMEM((n, w), bf16),
            pltpu.VMEM((nh, n, LN), f32),
            pltpu.VMEM((nh, bk, LN), f32),
            pltpu.VMEM((nh, bk, LN), f32),
        ],
    )
    return pl.pallas_call(
        functools.partial(bwd_kernel, first=group * nh, nh=nh, bq=bq, bk=bk, n=n),
        out_shape=[
            pltpu.HBM((n, lanes_up(3 * nh * HD)), bf16),
            pltpu.HBM((8, LN), f32),
        ],
        grid_spec=spec,
        compiler_params=pltpu.CompilerParams(vmem_limit_bytes=48 << 20),
        cost_estimate=cost(300 if group == 0 else 0.001),
        name="attn_bwd",
    )(block_flags(seg_row, bq, bk), mine.reshape(1), hbm(qa), hbm(kv), hbm(kv), *pieces, hbm(of), seg_row[:, None], seg_row[None], scale)


def quarter_columns(place, parts, groups, nh):
    width = nh // groups * HD
    return [
        (t * D + place * nh * HD + g * width, width) for g in range(groups) for t in range(3)
    ]


def pick_kernel(mine, w_ref, out, *, parts, groups, nh):
    for i in range(parts):

        @pl.when(mine[0] == i)
        def _(i=i):
            cut = [w_ref[:, a : a + width] for a, width in quarter_columns(i, parts, groups, nh)]
            used = sum(x.shape[1] for x in cut)
            pad = jnp.zeros((cut[0].shape[0], out.shape[1] - used), out.dtype)
            out[...] = jnp.concatenate(cut + [pad], axis=1)


def lanes_up(n):
    return -(-n // LN) * LN


def pick(w, mine, parts, groups, nh):
    rows = w.shape[0]
    step = 160 if rows % 160 == 0 else rows
    return pl.pallas_call(
        functools.partial(pick_kernel, parts=parts, groups=groups, nh=nh),
        out_shape=pltpu.HBM((rows, lanes_up(3 * nh * HD)), w.dtype),
        grid_spec=pltpu.PrefetchScalarGridSpec(
            num_scalar_prefetch=1,
            grid=(rows // step,),
            in_specs=[pl.BlockSpec((step, 3 * D), lambda i, m: (i, 0))],
            out_specs=pl.BlockSpec((step, lanes_up(3 * nh * HD)), lambda i, m: (i, 0)),
        ),
        cost_estimate=cost(5),
        name="pick",
    )(mine.reshape(1), hbm(w))


def stretch_kernel(x_ref, out, *, groups, nh):
    value = x_ref[...]
    each = 3 * nh * HD // groups
    zero = jnp.zeros((value.shape[0], LN - HD), value.dtype)
    per = nh // groups
    wide = []
    for t in range(3):
        for h in range(nh):
            at = (h // per) * each + t * per * HD + (h % per) * HD
            wide += [value[:, at : at + HD], zero]
    out[...] = jnp.concatenate(wide, axis=1)


def stretch(x, groups, nh, us):
    rows, width = x.shape
    step = 160
    return pl.pallas_call(
        functools.partial(stretch_kernel, groups=groups, nh=nh),
        out_shape=pltpu.HBM((rows, 3 * nh * LN), x.dtype),
        grid=(rows // step,),
        in_specs=[pl.BlockSpec((step, width), lambda i: (i, 0))],
        out_specs=pl.BlockSpec((step, 3 * nh * LN), lambda i: (i, 0)),
        cost_estimate=cost(us),
        name="stretch",
    )(hbm(x))


def order_kernel(own_first, a_ref, b_ref, out):
    half = pl.program_id(0)

    @pl.when(half == 0)
    def _():
        out[...] = a_ref[...].T

    @pl.when(half == 1)
    def _():
        out[...] = b_ref[...].T


def order(own, other, own_at):
    rows, width = own.shape
    step = 256
    return pl.pallas_call(
        order_kernel,
        out_shape=pltpu.HBM((width, 2 * rows), own.dtype),
        grid_spec=pltpu.PrefetchScalarGridSpec(
            num_scalar_prefetch=1,
            grid=(2, width // step),
            in_specs=[
                pl.BlockSpec((rows, step), lambda i, j, m: (0, j * (1 - i))),
                pl.BlockSpec((rows, step), lambda i, j, m: (0, j * i)),
            ],
            out_specs=pl.BlockSpec((step, rows), lambda i, j, m: (j, i ^ m[0])),
        ),
        cost_estimate=cost(200.0),
        name="order",
    )(own_at.reshape(1), hbm(own), hbm(other))


def transpose_kernel(x_ref, out):
    out[...] = x_ref[...].T


def transpose(x):
    rows, cols = x.shape
    step = 256
    return pl.pallas_call(
        transpose_kernel,
        out_shape=pltpu.HBM((cols, rows), x.dtype),
        grid=(rows // step,),
        in_specs=[pl.BlockSpec((step, cols), lambda i: (i, 0))],
        out_specs=pl.BlockSpec((cols, step), lambda i: (0, i)),
        cost_estimate=CHEAP,
        name="transpose",
    )(hbm(x))


def project_kernel(info, *refs, count, halves, width, fresh):
    pairs = refs[: 2 * count]
    gain = refs[2 * count]
    weights = refs[2 * count + 1 : 2 * count + 1 + halves]
    scale, ones = refs[2 * count + 1 + halves : 2 * count + 3 + halves]
    normed_ref, q_ref, kv_ref, mine_ref, w = refs[-5:]
    j, tile = pl.program_id(0), pl.program_id(1)
    step = normed_ref.shape[0]

    @pl.when((j == 0) & (tile == 0))
    def _():
        for i, ref in enumerate(weights):
            h = ref.shape[0]
            start = (info[count + 2] ^ i) * h if halves == 2 else 0
            w[pl.ds(pl.multiple_of(start, 16), h), :] = ref[...]
        if not fresh:
            mine_ref[...] = refs[2 * count + 3 + halves][...]

    def work(x_ref):
        value = x_ref[...]
        x = value.astype(f32)
        inverse = lax.rsqrt(jnp.mean(x * x, axis=-1, keepdims=True) + epsilon)
        normed = (x * inverse * gain[...]).astype(bf16)
        normed_ref[...] = normed
        q_ref[...] = (
            jnp.dot(normed, w[:, :width], preferred_element_type=f32) * scale[...]
        ).astype(bf16)
        kv_ref[...] = (
            jnp.dot(normed, w[:, width:], preferred_element_type=f32) + ones[...]
        ).astype(bf16)

        @pl.when(info[count + 1] == info[j])
        def _():
            mine_ref[pl.ds(pl.multiple_of(tile * step, step), step), :] = value

    for i in range(count):
        for lane in range(2):

            @pl.when((j == i) & (info[count] == lane))
            def _(i=i, lane=lane):
                work(pairs[2 * i + 1 - lane])


def project(pairs, places, lane, mine, wt, gain, weights, scale, ones, group_len, carried=None):
    count = len(pairs)
    rows, d = pairs[0][0].shape
    width = scale.shape[1]
    step = 256
    tiles = rows // step
    full = lambda j, t, f: (0, 0)
    at = lambda j, t, f: (f[j] * tiles + t, 0)
    once = pl.Buffered(1)
    info = jnp.stack(list(places) + [lane.astype(jnp.int32), mine, wt])
    args = [x for pair in pairs for x in pair] + [gain, *map(hbm, weights), scale, ones]
    in_specs = [
        pl.BlockSpec(
            (step, d),
            lambda j, t, f, i=i: (jnp.where(j == i, t, jnp.where(j > i, tiles - 1, 0)), 0),
        )
        for i in range(count)
        for _ in range(2)
    ]
    in_specs += [pl.BlockSpec((1, d), full, pipeline_mode=once)]
    in_specs += [pl.BlockSpec(w.shape, full, pipeline_mode=once) for w in weights]
    in_specs += [
        pl.BlockSpec((1, width), full, pipeline_mode=once),
        pl.BlockSpec((1, 2 * width), full, pipeline_mode=once),
    ]
    aliases = {}
    if carried is not None:
        base = len(args) + 2
        args += [hbm(x) for x in (carried[3], *carried[:3])]
        in_specs += [pl.BlockSpec((rows, d), full, pipeline_mode=once)]
        in_specs += [pl.BlockSpec(memory_space=pl.ANY)] * 3
        aliases = {base: 0, base + 1: 1, base + 2: 2}
    return pl.pallas_call(
        functools.partial(
            project_kernel, count=count, halves=len(weights), width=width, fresh=carried is None
        ),
        out_shape=[
            pltpu.HBM((group_len, d), bf16),
            pltpu.HBM((group_len, width), bf16),
            pltpu.HBM((group_len, 2 * width), bf16),
            pltpu.HBM((rows, d), bf16),
        ],
        grid_spec=pltpu.PrefetchScalarGridSpec(
            num_scalar_prefetch=1,
            grid=(count, tiles),
            in_specs=in_specs,
            out_specs=[
                pl.BlockSpec((step, d), at),
                pl.BlockSpec((step, width), at),
                pl.BlockSpec((step, 2 * width), at),
                pl.BlockSpec((rows, d), full),
            ],
            scratch_shapes=[pltpu.VMEM((d, 3 * width), bf16)],
        ),
        input_output_aliases=aliases,
        compiler_params=pltpu.CompilerParams(vmem_limit_bytes=32 << 20),
        cost_estimate=cost(15),
        name="project",
    )(info, *args)


def tail_body(at, p0, p1, p2, p3, x_ref, g_ref, w_s, gain, outs, need):
    lo_ref, left_ref, right_ref, gr_ref, c0, c1, c2, c3, gg_ref = outs
    att_ref, nm_ref, act_ref = (left_ref.at[i] for i in range(3))
    gp_ref, gh_ref = (right_ref.at[i] for i in range(2))
    right_ref[2] = g_ref[...]
    mine = at[0]
    pieces = (p0, p1, p2, p3)
    cols = p0.shape[1]
    nt = (((1,), (1,)), ((), ()))
    for i in range(4):

        @pl.when(mine == i)
        def _(i=i):
            att_ref[...] = jnp.concatenate([pieces[i ^ k][...] for k in range(4)], axis=1)

    need(0)
    resid = x_ref[...].astype(f32) + jnp.dot(att_ref[...], w_s[0], preferred_element_type=f32)
    inverse = lax.rsqrt(jnp.mean(resid * resid, axis=-1, keepdims=True) + epsilon)
    normed = (resid * inverse * gain[...]).astype(bf16)
    nm_ref[...] = normed
    need(1)
    hidden = jnp.dot(normed, w_s[1], preferred_element_type=f32)
    sig = 1.0 / (1.0 + jnp.exp(-hidden))
    active = (hidden * sig).astype(bf16)
    act_ref[...] = active
    need(2)
    lo_ref[...] = (resid + jnp.dot(active, w_s[2], preferred_element_type=f32)).astype(bf16)
    grad_active = lax.dot_general(g_ref[...], w_s[2], nt, preferred_element_type=f32)
    grad_hidden = (grad_active * sig * (1.0 + hidden * (1.0 - sig))).astype(bf16)
    gh_ref[...] = grad_hidden
    grad_normed = lax.dot_general(grad_hidden, w_s[1], nt, preferred_element_type=f32)
    gg_ref[...] += jnp.sum(grad_normed * resid * inverse, axis=0, keepdims=True)
    scaled = grad_normed * gain[...]
    grad_resid = (
        g_ref[...].astype(f32)
        + inverse * scaled
        - resid * (inverse * inverse * inverse) * jnp.mean(scaled * resid, axis=-1, keepdims=True)
    )
    gr_ref[...] = grad_resid
    grad_proj = grad_resid.astype(bf16)
    gp_ref[...] = grad_proj
    grad_att = lax.dot_general(grad_proj, w_s[0], nt, preferred_element_type=f32).astype(bf16)
    for i in range(4):

        @pl.when(mine == i)
        def _(i=i):
            for j, out in enumerate((c0, c1, c2, c3)):
                out[...] = grad_att[:, (i ^ j) * cols : ((i ^ j) + 1) * cols]


def tail_kernel(at, p0, p1, p2, p3, x_ref, g_ref, own0, own1, own2, half0, half, other0, other, gain, *refs, rows, hrows):
    w_s, sems = refs[-2:]
    outs = refs[:-2]

    def copies(i):
        parts = (
            ((own0, own1, own2)[i], at[1], rows),
            (half.at[i - 1] if i else half0, at[2], hrows),
            (other.at[i - 1] if i else other0, at[3], hrows),
        )
        return [
            pltpu.make_async_copy(
                part, w_s.at[i, pl.ds(pl.multiple_of(start, 16), n), :], sems.at[3 * i + k]
            )
            for k, (part, start, n) in enumerate(parts)
        ]

    @pl.when(pl.program_id(0) == 0)
    def _():
        outs[-1][...] = jnp.zeros_like(outs[-1])
        for i in range(3):
            for c in copies(i):
                c.start()

    def need(i):
        @pl.when(pl.program_id(0) == 0)
        def _():
            for c in copies(i):
                c.wait()

    tail_body(at, p0, p1, p2, p3, x_ref, g_ref, w_s, gain, outs, need)


def whole_tail_kernel(at, p0, p1, p2, p3, x_ref, g_ref, w, gain, *outs):
    @pl.when(pl.program_id(0) == 0)
    def _():
        outs[-1][...] = jnp.zeros_like(outs[-1])

    tail_body(at, p0, p1, p2, p3, x_ref, g_ref, w, gain, outs, lambda i: None)


def tail(at, pieces, x, g, weights, gain, tile=256):
    rows, d = x.shape
    cols = pieces[0].shape[1]
    row = lambda i, m: (i, 0)
    once = pl.Buffered(1)
    whole = lambda *shape: pl.BlockSpec(shape, lambda i, m: (0,) * len(shape), pipeline_mode=once)
    wide = pl.BlockSpec((tile, d), row)
    slim = pl.BlockSpec((tile, cols), row)
    if len(weights) == 7:
        body = functools.partial(tail_kernel, rows=weights[0].shape[0], hrows=weights[3].shape[0])
        scratch = [pltpu.VMEM((3, d, d), bf16), pltpu.SemaphoreType.DMA((9,))]
        weight_specs = [pl.BlockSpec(memory_space=pl.ANY)] * 7
    else:
        body = whole_tail_kernel
        scratch = []
        weight_specs = [whole(*w.shape) for w in weights]
    return pl.pallas_call(
        body,
        out_shape=[pltpu.HBM((rows, d), bf16)]
        + [pltpu.HBM((3, rows, d), bf16)] * 2
        + [pltpu.HBM((rows, d), f32)]
        + [pltpu.HBM((rows, cols), bf16)] * 4
        + [pltpu.HBM((1, d), f32)],
        grid_spec=pltpu.PrefetchScalarGridSpec(
            num_scalar_prefetch=1,
            grid=(rows // tile,),
            in_specs=[slim] * 4 + [wide] * 2 + weight_specs + [whole(1, d)],
            out_specs=[wide]
            + [pl.BlockSpec((3, tile, d), lambda i, m: (0, i, 0))] * 2
            + [wide]
            + [slim] * 4
            + [pl.BlockSpec((1, d), lambda i, m: (0, 0))],
            scratch_shapes=scratch,
        ),
        compiler_params=pltpu.CompilerParams(vmem_limit_bytes=52 << 20),
        cost_estimate=cost(0.01),
        name="tail",
    )(at, *pieces, hbm(x), g, *map(hbm, weights), gain)


tn_dims = (((0,), (0,)), ((), ()))


def share_kernel(col, left, right, out):
    value = lax.dot_general(left[0], right[0], tn_dims, preferred_element_type=f32)
    out[...] = value.astype(bf16)


def share(left, right, col):
    n, rows, d = left.shape
    w = d // 2
    block = pl.BlockSpec((d, w), lambda i, c: (0, i))
    return pl.pallas_call(
        share_kernel,
        out_shape=pltpu.HBM((d, n * w), bf16),
        grid_spec=pltpu.PrefetchScalarGridSpec(
            num_scalar_prefetch=1,
            grid=(n,),
            in_specs=[
                pl.BlockSpec((1, rows, d), lambda i, c: (i, 0, 0)),
                pl.BlockSpec((1, rows, w), lambda i, c: (i, 0, c[0])),
            ],
            out_specs=block,
        ),
        compiler_params=pltpu.CompilerParams(vmem_limit_bytes=20 << 20),
        cost_estimate=CHEAP,
        name="share",
    )(col.reshape(1), hbm(left), hbm(right))


def copy(x):
    return pl.pallas_call(
        tick_kernel, out_shape=pltpu.HBM(x.shape, x.dtype), cost_estimate=CHEAP, name="copy"
    )(x)


def tick_kernel(x_ref, out):
    out[...] = x_ref[...]


def tick(x):
    return pl.pallas_call(
        tick_kernel, out_shape=jax.ShapeDtypeStruct(x.shape, x.dtype), cost_estimate=cost(200.0), name="tick"
    )(x)


def total_kernel(*refs, counts):
    out = refs[-1]
    start, column = 0, 0
    for count in counts:
        group = refs[start : start + count]
        start += count
        acc = jnp.zeros(group[0].shape[1:], f32)
        for ref in group:
            for i in range(ref.shape[0]):
                acc = acc + ref[i].astype(f32)
        out[:, column : column + acc.shape[1]] = acc.astype(bf16)
        column += acc.shape[1]


def total(groups):
    flat = [x for group in groups for x in group]
    rows = flat[0].shape[1]
    cuts = 2 if rows % 32 == 0 else 1
    width = sum(group[0].shape[2] for group in groups)
    return pl.pallas_call(
        functools.partial(total_kernel, counts=[len(group) for group in groups]),
        out_shape=pltpu.HBM((rows, width), bf16),
        grid=(cuts,),
        in_specs=[
            pl.BlockSpec((x.shape[0], rows // cuts, x.shape[2]), lambda i: (0, i, 0)) for x in flat
        ],
        out_specs=pl.BlockSpec((rows // cuts, width), lambda i: (i, 0)),
        compiler_params=pltpu.CompilerParams(vmem_limit_bytes=16 << 20),
        cost_estimate=cost(0.001),
        name="total",
    )(*flat)


def add_kernel(a_ref, b_ref, out):
    out[...] = (a_ref[...].astype(f32) + b_ref[...].astype(f32)).astype(bf16)


def add(a, b):
    return pl.pallas_call(
        add_kernel, out_shape=pltpu.HBM(a.shape, bf16), cost_estimate=CHEAP, name="add"
    )(a, b)


def add_rows(a, b):
    rows, cols = a.shape
    block = pl.BlockSpec((rows // 5, cols), lambda i: (i, 0))
    return pl.pallas_call(
        add_kernel,
        out_shape=pltpu.HBM(a.shape, bf16),
        grid=(5,),
        in_specs=[block] * 2,
        out_specs=block,
        compiler_params=pltpu.CompilerParams(vmem_limit_bytes=14 << 20),
        cost_estimate=CHEAP,
        name="add_rows",
    )(hbm(a), hbm(b))


def by_bits(first, second, put):
    for i in range(2):
        for j in range(2):

            @pl.when((first == i) & (second == j))
            def _(i=i, j=j):
                put(i, j)


def place_kernel(at, *refs):
    o0, o1, o2 = refs[-3:]
    block = pl.program_id(0)
    w = o0.shape[2] // 2

    def put(other_x, other_near):
        for core in range(2):

            @pl.when(at[2] == core)
            def _(core=core):
                for side in range(2):
                    part = refs[4 * (side ^ core) + 2 * other_x + other_near][...].astype(f32)
                    for i, out in enumerate((o0, o1, o2)):
                        out[0, :, side * w : (side + 1) * w] = part[:, i * w : (i + 1) * w]

    by_bits((block // 2) ^ at[0], (block % 2) ^ at[1], put)


def place_tail(arrays, at):
    h, width = arrays[0].shape
    d = width // 3 * 2
    whole = pl.BlockSpec((h, width), lambda i, m: (0, 0), pipeline_mode=pl.Buffered(1))
    outs = pl.pallas_call(
        place_kernel,
        out_shape=[pltpu.HBM((4, h, d), f32)] * 3,
        grid_spec=pltpu.PrefetchScalarGridSpec(
            num_scalar_prefetch=1,
            grid=(4,),
            in_specs=[whole] * 8,
            out_specs=[pl.BlockSpec((1, h, d), lambda i, m: (i, 0, 0))] * 3,
        ),
        compiler_params=pltpu.CompilerParams(vmem_limit_bytes=16 << 20),
        cost_estimate=CHEAP,
        name="place_tail",
    )(at, *map(hbm, arrays))
    return [out.reshape(4 * h, d) for out in outs]


def cross_kernel(at, x_ref, g_ref, *refs):
    s = refs[-1]
    s[...] = jnp.dot(x_ref[...], g_ref[...], preferred_element_type=f32)
    half = s.shape[0] // 2
    for w in range(2):

        @pl.when(pl.program_id(0) == w)
        def _(w=w):
            for x in range(2):
                rows = pl.ds(pl.multiple_of((at[1] ^ x) * half, 16), half)
                refs[2 * w + x][...] = s[rows, :].astype(bf16)


def cross(x, g, at):
    d, rows = x.shape
    w = d // 2
    cols = g.shape[1]
    step = 512 if cols % 512 == 0 else cols
    n = cols // step
    first = pl.BlockSpec((w // 2, step), lambda i, j, m: (0, jnp.where(i == 0, j, n - 1)))
    second = pl.BlockSpec((w // 2, step), lambda i, j, m: (0, jnp.where(i == 1, j, 0)))
    return pl.pallas_call(
        cross_kernel,
        out_shape=[pltpu.HBM((w // 2, cols), bf16)] * 4,
        grid_spec=pltpu.PrefetchScalarGridSpec(
            num_scalar_prefetch=1,
            grid=(2, n),
            in_specs=[
                pl.BlockSpec((w, rows), lambda i, j, m: (m[0] ^ i, 0)),
                pl.BlockSpec((rows, step), lambda i, j, m: (0, j)),
            ],
            out_specs=[first, first, second, second],
            scratch_shapes=[pltpu.VMEM((w, step), f32)],
        ),
        compiler_params=pltpu.CompilerParams(vmem_limit_bytes=26 << 20),
        cost_estimate=CHEAP,
        name="cross",
    )(at, hbm(x), hbm(g))


def spread_kernel(at, *refs, width):
    out = refs[-1]
    step = out.shape[1]
    rows = pl.ds(pl.multiple_of(pl.program_id(0) * step, step), step)

    def put(core, near):
        cut = []
        for t in range(3):
            for n in range(2):
                for c in range(2):
                    part = refs[2 * (c ^ core) + (n ^ near)][rows, :]
                    cut.append(part[:, t * width : (t + 1) * width])
        out[0] = jnp.concatenate(cut, axis=1).astype(f32)

    by_bits(at[2], at[1], put)


def spread(arrays, at, used, other_x, carried=None):
    rows, cols = arrays[0].shape
    width = 4 * used
    cuts = 2 if rows % 32 == 0 else 1
    whole = pl.BlockSpec((rows, cols), lambda j, m: (0, 0), pipeline_mode=pl.Buffered(1))
    more = () if carried is None else (carried,)
    return pl.pallas_call(
        functools.partial(spread_kernel, width=used // 3),
        out_shape=pltpu.HBM((2, rows, width), f32),
        grid_spec=pltpu.PrefetchScalarGridSpec(
            num_scalar_prefetch=1,
            grid=(cuts,),
            in_specs=[whole] * 4 + [pl.BlockSpec(memory_space=pl.ANY)] * len(more),
            out_specs=pl.BlockSpec((1, rows // cuts, width), lambda j, m: (m[0] ^ other_x, j, 0)),
        ),
        input_output_aliases={5: 0} if more else {},
        compiler_params=pltpu.CompilerParams(vmem_limit_bytes=20 << 20),
        cost_estimate=CHEAP,
        name="spread",
    )(at, *arrays, *more)


def back_kernel(shards, g_ref, w_ref, *refs):
    acc = jnp.dot(g_ref[...], w_ref[...], preferred_element_type=f32)
    if len(refs) == 2:
        acc = acc + refs[0][0].astype(f32)
    refs[-1][0] = acc.astype(bf16)


def back(grad, w, shards, rows, got=None):
    c, d = w.shape
    n = shards.shape[0]
    step = d
    out = pl.BlockSpec((1, rows, step), lambda j, i, f: (i, 0, j))
    in_specs = [
        pl.BlockSpec((rows, c), lambda j, i, f: (f[i], 0)),
        pl.BlockSpec((c, step), lambda j, i, f: (0, j)),
    ]
    args = [hbm(grad), hbm(w)]
    if got is not None:
        in_specs.append(pl.BlockSpec((1, rows, step), lambda j, i, f: (0, 0, j)))
        args.append(got)
    return pl.pallas_call(
        back_kernel,
        out_shape=pltpu.HBM((n, rows, d), bf16),
        grid_spec=pltpu.PrefetchScalarGridSpec(
            num_scalar_prefetch=1, grid=(d // step, n), in_specs=in_specs, out_specs=out
        ),
        compiler_params=pltpu.CompilerParams(vmem_limit_bytes=22 << 20),
        cost_estimate=CHEAP,
        name="back",
    )(shards, *args)


def finish_kernel(shard, g_ref, w_ref, core, near, x_ref, resid, gain, out, gain_out):
    grad = jnp.dot(g_ref[...], w_ref[...], preferred_element_type=f32)
    grad = grad + core[0].astype(f32) + near[0].astype(f32)
    x = x_ref[...].astype(f32)
    inverse = lax.rsqrt(jnp.mean(x * x, axis=-1, keepdims=True) + epsilon)
    part = jnp.sum(grad * x * inverse, axis=0, keepdims=True)

    @pl.when(pl.program_id(0) == 0)
    def _():
        gain_out[...] = jnp.zeros_like(gain_out)

    gain_out[...] += part
    scaled = grad * gain[...]
    out[...] = (
        resid[...]
        + inverse * scaled
        - x * (inverse * inverse * inverse) * jnp.mean(scaled * x, axis=-1, keepdims=True)
    ).astype(bf16)


def finish(grad, w, shard, core, near, x, resid, gain, tile=256):
    rows, d = x.shape
    c = w.shape[0]
    tiles = rows // tile
    row = lambda i, f: (i, 0)
    once = pl.Buffered(1)
    return pl.pallas_call(
        finish_kernel,
        out_shape=[pltpu.HBM((rows, d), bf16), jax.ShapeDtypeStruct((1, d), f32)],
        grid_spec=pltpu.PrefetchScalarGridSpec(
            num_scalar_prefetch=1,
            grid=(tiles,),
            in_specs=[
                pl.BlockSpec((tile, c), lambda i, f: (f[0] * tiles + i, 0)),
                pl.BlockSpec((c, d), lambda i, f: (0, 0), pipeline_mode=once),
                pl.BlockSpec((1, tile, d), lambda i, f: (1, i, 0)),
                pl.BlockSpec((1, tile, d), lambda i, f: (0, i, 0)),
                pl.BlockSpec((tile, d), row),
                pl.BlockSpec((tile, d), row),
                pl.BlockSpec((1, d), lambda i, f: (0, 0)),
            ],
            out_specs=[pl.BlockSpec((tile, d), row), pl.BlockSpec((1, d), lambda i, f: (0, 0))],
        ),
        compiler_params=pltpu.CompilerParams(vmem_limit_bytes=24 << 20),
        cost_estimate=CHEAP,
        name="finish",
    )(shard.reshape(1), hbm(grad), hbm(w), core, near, hbm(x), hbm(resid), gain)


def rms_inverse(values):
    return lax.rsqrt(jnp.mean(values * values, axis=-1, keepdims=True) + epsilon)


def norm_back(values, inverse, grad_scaled):
    return inverse * grad_scaled - values * (inverse * inverse * inverse) * jnp.mean(
        grad_scaled * values, axis=-1, keepdims=True
    )


def dot(left, right):
    return jnp.dot(left, right, preferred_element_type=f32)


def times_trans(left, right):
    return lax.dot_general(left, right, (((1,), (1,)), ((), ())), preferred_element_type=f32)


def trans_times(left, right):
    return lax.dot_general(left, right, (((0,), (0,)), ((), ())), preferred_element_type=f32)


def rows_at(array, start, count):
    return lax.dynamic_slice_in_dim(array, start, count, 0)


def put_rows(array, rows, start):
    return lax.dynamic_update_slice_in_dim(array, rows, start, 0)


def make_local(sizes):
    def pairs(target):
        found = []
        for gx in range(sizes["gx"]):
            for gc in range(sizes["gc"]):
                for z in range(4):
                    for w in range(sizes["wt"]):
                        goal = target(gx, gc, z, w)
                        if goal is not None and goal != (gx, gc, z, w):
                            found.append((place(gx, gc, z, w), place(*goal)))
        return found

    def place(gx, gc, z, w):
        return ((gx * sizes["gc"] + gc) * 4 + z) * sizes["wt"] + w

    def send(value, target):
        return lax.ppermute(value, AXES, pairs(target))

    def core_mate(gx, gc, z, w):
        return (gx, 1 - gc, z, w)

    def x_mate(gx, gc, z, w):
        return (1 - gx, gc, z, w)

    def near_mate(gx, gc, z, w):
        return (gx, gc, z ^ 1, w)

    def far_mate(gx, gc, z, w):
        return (gx, gc, z ^ 2, w)

    def cross_mate(gx, gc, z, w):
        return (gx, 1 - gc, z ^ 1, w)

    def wt_mate(gx, gc, z, w):
        return (gx, gc, z, 1 - w)

    def wt_x_mate(gx, gc, z, w):
        return (1 - gx, gc, z, 1 - w)

    def to_host(gx, gc, z, w):
        return (gx, 1 - (z & 1), 2 * gc + (z >> 1), w)

    def to_home(gx, gc, z, w):
        return (gx, z >> 1, 2 * (z & 1) + 1 - gc, w)

    def hop1(gx, gc, z, w):
        if gc == 0:
            return (gx, 0, z - 1, w) if z > 0 else None
        return (gx, 1, z + 1, w) if z < 3 else None

    def hop2(gx, gc, z, w):
        if gc == 0:
            return (gx, 0, z - 1, w) if z in (1, 2) else None
        return (gx, 1, z + 1, w) if z in (1, 2) else None

    def hop3(gx, gc, z, w):
        if gc == 0:
            return (gx, 0, z ^ 1, w) if z < 2 else None
        return (gx, 1, z ^ 1, w) if z > 1 else None

    def lane_share(gx, gc, z, w):
        return (gx, 1 - gc, z, w) if gc == z >> 1 else None

    def sum_all(value):
        for axis in ("gc", "wt", "near", "far", "gx"):
            step = 1
            while step < sizes[axis]:

                def mate(gx, gc, z, w, axis=axis, step=step):
                    at = dict(gx=gx, gc=gc, far=z >> 1, near=z & 1, wt=w)
                    at[axis] ^= step
                    return (at["gx"], at["gc"], 2 * at["far"] + at["near"], at["wt"])

                value = value + send(value, mate)
                step *= 2
        return value

    def local(
        tokens, segments, w_qkv, w_proj, w_in, w_out, gain_attn, gain_mlp, query_scale, cotangent
    ):
        gx, gc, host, near, wt = (lax.axis_index(axis) for axis in AXES)
        z = 2 * host + near
        mine = 2 * near + 1 - gc
        parts = 4
        nh = H // parts
        groups = 1
        rows = tokens.shape[1]
        group_len = segments.shape[1]
        wrows = w_qkv.shape[0]
        lane = gc == host
        pair = sizes["wt"] == 2

        def after(value, *others):
            return lax.optimization_barrier((value,) + others)[0]

        picked = pick(w_qkv, mine, parts, groups, nh)
        own = tokens[0]
        got1 = send(own, hop1)
        own_share = send(after(own, picked), lane_share)
        seg_mate = send(after(segments, picked), core_mate)
        got2 = send(got1, hop2)
        got1_share = send(got1, lane_share)
        end = jnp.where(gc == 0, z == 0, z == 3)
        if pair:
            wide_own = stretch(picked, groups, nh, 2)
            got1 = after(got1, wide_own)
            other_w = send(picked, wt_mate)
            wide_w = (wide_own, stretch(other_w, groups, nh, 10))
        else:
            flat_all = lax.all_gather(picked, "wt", axis=0, tiled=True)
            by_head = jnp.transpose(
                flat_all[:, : 3 * nh * HD].reshape(D, groups, 3, nh // groups, HD), (0, 2, 1, 3, 4)
            )
            wide_w = (
                jnp.pad(
                    by_head.reshape(D, 3 * nh, HD), ((0, 0), (0, 0), (0, LN - HD))
                ).reshape(D, -1),
            )
        got3 = send(jnp.where(end, own, got2), hop3)
        got2_share = send(got2, lane_share)
        way = 1 - 2 * host
        last = jnp.where(host == 0, jnp.where(z == 0, 3, 0), jnp.where(z == 3, 0, 3))
        places = (z, z + way, z + 2 * way, last)

        half_rows = wrows // 2
        if pair:
            half_a = send(after(rows_at(w_proj, gc * half_rows, half_rows), other_w), wt_mate)
            half_w = jnp.stack([rows_at(w, gc * half_rows, half_rows) for w in (w_in, w_out)])
            half_w = send(after(half_w, half_a), wt_mate)
        else:
            half_w = jnp.stack([rows_at(w, gc * half_rows, half_rows) for w in (w_proj, w_in, w_out)])
            half_w = lax.all_gather(half_w, "wt", axis=0, tiled=False)

        dim_scale = scale_base / math.sqrt(HD) * jax.nn.softplus(query_scale)
        lane_scale = jnp.tile(jnp.pad(dim_scale * log2e, (0, LN - HD)), nh)[None]
        ones = jnp.tile(
            ((jnp.arange(LN) >= HD) & (jnp.arange(LN) < HD + 3)).astype(f32), 2 * nh
        )[None]
        seg_row = jnp.where(lane, segments, seg_mate)[0]
        fixed = (lane, mine, wt, gain_attn[None], wide_w, lane_scale, ones, group_len)
        carried = project(((own, own_share), (got1, got1_share)), places[:2], *fixed)
        got3_share = send(after(got3, carried[0]), lane_share)
        first_done = (lambda x: after(x, half_a)) if pair else (lambda x: x)
        all_normed, queries, keyval, inputs = project(
            ((got2, got2_share), (got3, first_done(got3_share))), places[2:], *fixed, carried=carried
        )
        grad_mlp = send(after(cotangent[0], got3_share), to_host)

        att, att_float, q_aug = attn_fwd(queries, keyval, seg_row, nh)
        att, half_w, _ = lax.optimization_barrier((att, half_w, grad_mlp))

        trades = (core_mate, near_mate, cross_mate)
        att_pieces = [rows_at(att, (mine ^ j) * rows, rows) for j in range(parts)]
        half_mate = send(after(half_w, *att_pieces), core_mate)
        att_pieces = [att_pieces[0]] + [send(att_pieces[j + 1], trades[j]) for j in range(3)]
        if pair:
            w_trans = order(after(picked, att), other_w, wt)
        else:
            w_trans = flat_all.T
        normed_trans = transpose(after(all_normed, w_trans))
        if pair:
            mate_a = send(after(half_a, *att_pieces[1:2]), core_mate)
            weights = (w_proj, w_in, w_out, half_a, half_w, mate_a, half_mate)
            starts = (wt * wrows, (1 - wt) * wrows + gc * half_rows, (1 - wt) * wrows + (1 - gc) * half_rows)
        else:
            one = gc == 0
            tail_w = jnp.stack(
                [jnp.where(one, half_w, half_mate), jnp.where(one, half_mate, half_w)], axis=1
            )
            weights = (jnp.transpose(tail_w, (2, 0, 1, 3, 4)).reshape(3, D, D),)
            starts = ()
        (
            layer_out,
            left,
            right,
            grad_resid,
            *pieces,
            grad_gain_mlp,
        ) = tail(
            jnp.stack([mine, *starts]), att_pieces, after(inputs, normed_trans), grad_mlp, weights, gain_mlp[None]
        )
        pieces = [pieces[0]] + [send(pieces[j + 1], trades[j]) for j in range(3)]

        shared = share(after(left, pieces[1]), right, 1 - gc)
        from_core = send(shared, core_mate)
        own_half = share(left, right, after(gc, shared))
        pieces[2:] = [after(piece, own_half) for piece in pieces[2:]]
        home_out = send(after(layer_out, *pieces[1:]), to_home)
        late_gain = tick(after(gain_attn.reshape(-1, LN), *pieces[1:]))
        summed = add_rows(own_half, after(from_core, late_gain))
        kept = lax.all_to_all(summed, ("wt", "gx", "near"), 0, 0, tiled=True)

        scale_row = jnp.tile(dim_scale, nh // groups)[None]

        def backward(group, *others):
            first, *rest = pieces
            return attn_bwd(
                q_aug,
                keyval,
                (after(first, summed, *others), *rest),
                att_float,
                mine,
                seg_row,
                scale_row,
                nh,
                group,
                groups,
            )

        def by_rows(grad):
            if pair:
                own, *rest = cross(normed_trans, grad, jnp.stack([wt, gx]))
                got = [send(part, mate) for part, mate in zip(rest, (x_mate, wt_mate, wt_x_mate))]
                return [part[None] for part in (own, *got)]
            part = dot(normed_trans, grad).astype(bf16)
            sources = sizes["wt"] * 2
            got = lax.all_to_all(part, ("wt", "gx"), 0, 0, tiled=True)
            return [got.reshape(sources, D // sources, -1)]

        grad_project, grad_lanes = backward(0)
        layer_out = after(home_out, grad_project)

        last_step = [layer_out]

        def turn(value):
            return after(value, *last_step)

        def done(value):
            last_step[0] = value
            return value

        sources = sizes["wt"] * 4
        to_core = done(back(turn(grad_project), w_trans, jnp.stack([mine ^ 3, mine ^ 1]), rows))
        from_core = send(to_core, core_mate)
        by_place = by_rows(turn(grad_project))
        done(by_place[0])
        to_near = done(back(grad_project, w_trans, (mine ^ 2).reshape(1), rows, turn(from_core)))
        from_near = send(to_near, near_mate)
        t1 = done(total([[turn(kept).reshape(sources, D // sources, -1)]]))
        t1_far = send(t1, far_mate)
        layer_out = done(copy(turn(layer_out)))
        by_place[0] = turn(by_place[0])
        q1 = done(total([by_place]))
        q1_far = send(q1, far_mate)
        t2 = done(add(turn(t1), t1_far))
        t2_near = send(t2, near_mate)
        t2_x = send(t2, x_mate)
        grad_tokens, grad_gain_attn = finish(
            grad_project,
            w_trans,
            mine,
            from_core,
            turn(from_near),
            inputs,
            grad_resid,
            late_gain.reshape(1, -1),
        )
        done(grad_tokens)
        grad_query_scale = (
            grad_lanes[0, :HD]
            / (dim_scale * log2e)
            * (scale_base / math.sqrt(HD))
            * jax.nn.sigmoid(query_scale)
        )
        small = jnp.concatenate(
            [grad_gain_attn[0], grad_gain_mlp[0], jnp.pad(grad_query_scale, (0, LN - HD))]
        ).reshape(-1, LN)
        t2_x = done(turn(t2_x))
        t2_near = done(turn(t2_near))
        t2_near_x = send(t2_near, x_mate)
        tails = [t2, t2_near, t2_x]
        tails_mate = [send(turn(x), core_mate) for x in tails]
        q2 = done(add(turn(q1), q1_far))
        q2_near = send(q2, near_mate)
        q2_x = send(q2, x_mate)
        home_grad = send(turn(grad_tokens), to_home)
        q2_near = done(turn(q2_near))
        q2_near_x = send(q2_near, x_mate)
        t2_near_x = done(turn(t2_near_x))
        tails += [t2_near_x]
        tails_mate += [send(t2_near_x, core_mate)]
        q2_x = done(turn(q2_x))
        quads_mate = [send(turn(x), core_mate) for x in (q2, q2_near, q2_x)]
        tails_mate[3] = turn(tails_mate[3])
        totals = place_tail(tails + tails_mate, jnp.stack([gx, near, gc]))
        done(totals[0])
        used = 3 * nh * HD
        spread_at = jnp.stack([gx, near, 1 - gc])
        quads_mate[0] = done(after(turn(quads_mate[0]), quads_mate[1]))
        small = done(sum_all(turn(small))).reshape(-1)
        home_grad = done(turn(home_grad))
        q2_near_x = done(turn(q2_near_x))
        last_mate = send(q2_near_x, core_mate)
        total_qkv = done(
            spread((turn(q2), q2_near, quads_mate[0], quads_mate[1]), spread_at, used, 0)
        )
        grad_tokens = done(copy(turn(home_grad)))
        total_qkv = spread(
            (q2_x, turn(q2_near_x), quads_mate[2], last_mate), spread_at, used, 1, total_qkv
        ).reshape(wrows, 3 * D)
        return (
            layer_out[None],
            grad_tokens[None],
            total_qkv,
            *totals,
            small[:D],
            small[D : 2 * D],
            small[2 * D : 2 * D + HD],
        )

    return local


def solution(mesh):
    groups, parts, wt = (mesh.shape[axis] for axis in ("grp", "ctx", "wt"))
    inner = Mesh(mesh.devices.reshape(groups // 2, 2, parts // 2, 2, wt), AXES)
    sizes = dict(inner.shape)
    split = P(("gx", "gc", "wt"), ("far", "near"), None)
    weight = P("wt", None)
    return jax.shard_map(
        make_local(sizes),
        mesh=inner,
        in_specs=(
            split,
            P(("gx", "gc", "wt"), None),
            weight,
            weight,
            weight,
            weight,
            P(),
            P(),
            P(),
            split,
        ),
        out_specs=(split, split, weight, weight, weight, weight, P(), P(), P()),
        check_vma=False,
    )
```

```python
import functools
import math

import jax
import jax.numpy as jnp
from jax import lax
from jax.experimental import pallas as pl
from jax.experimental.pallas import tpu as pltpu
from jax.sharding import Mesh
from jax.sharding import PartitionSpec as P

D = 1280
H = 16
HD = 80
LN = 128
epsilon = 1e-06
scale_base = 1.442695041
log2e = 1.4426950408889634
NEG = -1e30
def cost(us):
    return pl.CostEstimate(flops=int(us * 1_000_000_000), transcendentals=0, bytes_accessed=1000)


CHEAP = cost(0.001)
f32 = jnp.float32
bf16 = jnp.bfloat16
AXES = ("gx", "gc", "far", "near", "wt")


def hbm(x):
    return pltpu.with_memory_space_constraint(x, pltpu.HBM)


def block_flags(seg_row, bq, bk):
    n = seg_row.shape[0]
    q = seg_row.reshape(n // bq, bq)
    k = seg_row.reshape(n // bk, bk)
    qf, ql = q[:, 0][:, None], q[:, -1][:, None]
    kf, kl = k[:, 0][None], k[:, -1][None]
    qs = jnp.arange(n // bq, dtype=jnp.int32)[:, None] * bq
    ks = jnp.arange(n // bk, dtype=jnp.int32)[None] * bk
    below = ks + bk - 1 <= qs
    skip = (ks > qs + bq - 1) | ((kf > 0) & (kl < qf))
    same = (qf == ql) & (kl == ql) & ((kf == kl) | ((kf == 0) & (kl == 1)))
    full = below & ((kl == 0) | same)
    flags = jnp.where(skip, 0, jnp.where(full, 1, 2))
    if bq == bk:
        flags = jnp.where(qs == ks, 3, flags)
    return flags.astype(jnp.int32).reshape(-1)


def put_split(base, col, lanes):
    hi = col.astype(bf16).astype(f32)
    rest = col - hi
    mid = rest.astype(bf16).astype(f32)
    out = jnp.where(lanes == HD, hi, base)
    out = jnp.where(lanes == HD + 1, mid, out)
    return jnp.where(lanes == HD + 2, rest - mid, out).astype(bf16)


def fwd_kernel(flags, q_ref, kv, segc, segr, att, of, qaug, m_s, acc_s, *, nh, bq, bk, nk):
    qi = pl.program_id(0)
    count = (qi * bq + bq + bk - 1) // bk
    nt = (((1,), (1,)), ((), ()))
    acc_s[...] = jnp.zeros_like(acc_s)
    m_s[...] = jnp.zeros_like(m_s)

    def mask(ko, q0=0, qn=bq, kn=bk):
        qpos = qi * bq + q0 + lax.broadcasted_iota(jnp.int32, (qn, kn), 0)
        kpos = ko + lax.broadcasted_iota(jnp.int32, (qn, kn), 1)
        ks = segr[:, pl.ds(ko, kn)]
        return (kpos <= qpos) & ((ks == 0) | (ks == segc[q0 : q0 + qn, :]))

    def step(kb, masked, q0=0, qn=bq, kn=bk):
        ko = pl.multiple_of(kb * bk, bk)
        if masked:
            allowed = mask(ko, q0, qn, kn)
        rows = slice(q0, q0 + qn)
        for h in range(nh):
            k = kv[pl.ds(ko, kn), h * LN : (h + 1) * LN]
            v = kv[pl.ds(ko, kn), (nh + h) * LN : (nh + h + 1) * LN]
            q = q_ref[rows, h * LN : (h + 1) * LN]
            p = jnp.exp2(lax.dot_general(q, k, nt, preferred_element_type=f32))
            if masked:
                p = jnp.where(allowed, p, 0.0)
            acc_s[h, rows, :] += jnp.dot(p.astype(bf16), v, preferred_element_type=f32)

    def body(kb, carry):
        flag = flags[qi * nk + kb]

        @pl.when(flag == 1)
        def _():
            step(kb, False)

        @pl.when(flag >= 2)
        def _():
            step(kb, True)

        return carry

    lax.fori_loop(0, count, body, 0)
    bad = jnp.zeros((bq, 1), f32)
    for h in range(nh):
        total = acc_s[h][:, HD : HD + 1]
        bad = jnp.maximum(bad, jnp.where((total > 2.0**-60) & (total < 2.0**60), 0.0, 1.0))

    @pl.when(jnp.max(bad) > 0.0)
    def _():
        def head(h, carry):
            kc = pl.ds(pl.multiple_of(h * LN, LN), LN)
            vc = pl.ds(pl.multiple_of((nh + h) * LN, LN), LN)
            m_s[h] = jnp.full((bq, LN), NEG, f32)
            acc_s[h] = jnp.zeros((bq, LN), f32)

            def inner(kb, carry):
                @pl.when(flags[qi * nk + kb] > 0)
                def _():
                    ko = pl.multiple_of(kb * bk, bk)
                    s = lax.dot_general(
                        q_ref[:, kc], kv[pl.ds(ko, bk), kc], nt, preferred_element_type=f32
                    )
                    s = jnp.where(mask(ko), s, NEG)
                    old = m_s[h]
                    new = jnp.maximum(old, jnp.max(s, axis=1, keepdims=True))
                    p = jnp.exp2(s - new[:, :1]).astype(bf16)
                    m_s[h] = new
                    acc_s[h] = acc_s[h] * jnp.exp2(old - new) + jnp.dot(
                        p, kv[pl.ds(ko, bk), vc], preferred_element_type=f32
                    )

                return carry

            lax.fori_loop(0, count, inner, 0)
            return carry

        lax.fori_loop(0, nh, head, 0)

    lanes = lax.broadcasted_iota(jnp.int32, (bq, LN), 1)
    outs = []
    for h in range(nh):
        acc = acc_s[h]
        total = acc[:, HD : HD + 1]
        out = acc * (1.0 / total)
        of[:, h * LN : (h + 1) * LN] = jnp.where(lanes < HD, out, 0.0).astype(bf16)
        outs.append(out[:, :HD])
        lse = m_s[h][:, :1] + jnp.log2(total)
        qaug[:, h * LN : (h + 1) * LN] = put_split(
            q_ref[:, h * LN : (h + 1) * LN].astype(f32), -lse, lanes
        )
    att[...] = jnp.concatenate(outs, axis=1).astype(bf16)


def attn_fwd(q, kv, seg_row, nh, bq=512, bk=512):
    n = q.shape[0]
    w = nh * LN
    spec = pltpu.PrefetchScalarGridSpec(
        num_scalar_prefetch=1,
        grid=(n // bq,),
        in_specs=[
            pl.BlockSpec((bq, w), lambda i, f: (i, 0)),
            pl.BlockSpec((n, 2 * w), lambda i, f: (0, 0)),
            pl.BlockSpec((bq, 1), lambda i, f: (i, 0)),
            pl.BlockSpec((1, n), lambda i, f: (0, 0)),
        ],
        out_specs=[
            pl.BlockSpec((bq, nh * HD), lambda i, f: (i, 0)),
            pl.BlockSpec((bq, w), lambda i, f: (i, 0)),
            pl.BlockSpec((bq, w), lambda i, f: (i, 0)),
        ],
        scratch_shapes=[pltpu.VMEM((nh, bq, LN), f32), pltpu.VMEM((nh, bq, LN), f32)],
    )
    return pl.pallas_call(
        functools.partial(fwd_kernel, nh=nh, bq=bq, bk=bk, nk=n // bk),
        out_shape=[
            pltpu.HBM((n, nh * HD), bf16),
            pltpu.HBM((n, w), bf16),
            pltpu.HBM((n, w), bf16),
        ],
        grid_spec=spec,
        compiler_params=pltpu.CompilerParams(vmem_limit_bytes=28 << 20),
        cost_estimate=cost(0.01),
        name="attn_fwd",
    )(block_flags(seg_row, bq, bk), hbm(q), hbm(kv), seg_row[:, None], seg_row[None])


def bwd_kernel(
    flags, mine, qa, kk, vv, do0, do1, do2, do3, of, segc, segr, scale, dqkv, gscale, doa_s, dq_s, dk_s, dv_s, *, first, nh, bq, bk, n
):
    nk = n // bk
    nq = n // bq
    kb = pl.program_id(0)
    part = n // 4
    step_rows = 256 if part % 256 == 0 else part
    lanes = lax.broadcasted_iota(jnp.int32, (step_rows, LN), 1)

    @pl.when(kb == 0)
    def _():
        dq_s[...] = jnp.zeros_like(dq_s)
        for j, piece in enumerate((do0, do1, do2, do3)):
            start = (mine[0] ^ j) * part
            for i in range(part // step_rows):
                d = piece[i * step_rows : (i + 1) * step_rows, :].astype(f32)
                r = pl.ds(pl.multiple_of(start + i * step_rows, step_rows), step_rows)
                for h in range(nh):
                    at = (first + h) * HD
                    dh = jnp.concatenate(
                        [d[:, at : at + HD], jnp.zeros((step_rows, LN - HD), f32)], axis=1
                    )
                    c = slice(h * LN, (h + 1) * LN)
                    delta = jnp.sum(dh * of[r, c].astype(f32), axis=1, keepdims=True)
                    doa_s[r, c] = put_split(dh, -delta, lanes)

    dk_s[...] = jnp.zeros_like(dk_s)
    dv_s[...] = jnp.zeros_like(dv_s)
    ko = kb * bk
    nt = (((1,), (1,)), ((), ()))
    tn = (((0,), (0,)), ((), ()))

    def step(qi, masked, q0=0, qn=bq, kn=bk):
        qo = pl.multiple_of(qi * bq + q0, qn)
        rows = slice(0, kn)
        if masked:
            kpos = ko + lax.broadcasted_iota(jnp.int32, (kn, qn), 0)
            qpos = qo + lax.broadcasted_iota(jnp.int32, (kn, qn), 1)
            ks = segc[rows, :]
            allowed = (kpos <= qpos) & ((ks == 0) | (ks == segr[:, pl.ds(qo, qn)]))
        for h in range(nh):
            c = slice(h * LN, (h + 1) * LN)
            q = qa[pl.ds(qo, qn), c]
            k = kk[rows, c]
            d = doa_s[pl.ds(qo, qn), c]
            p = jnp.exp2(lax.dot_general(k, q, nt, preferred_element_type=f32))
            if masked:
                p = jnp.where(allowed, p, 0.0)
            ds = (p * lax.dot_general(vv[rows, c], d, nt, preferred_element_type=f32)).astype(bf16)
            dv_s[h, rows, :] += jnp.dot(p.astype(bf16), d, preferred_element_type=f32)
            dk_s[h, rows, :] += jnp.dot(ds, q, preferred_element_type=f32)
            dq_s[h, pl.ds(qo, qn), :] += lax.dot_general(ds, k, tn, preferred_element_type=f32)

    def body(qi, carry):
        flag = flags[qi * nk + kb]

        @pl.when(flag == 1)
        def _():
            step(qi, False)

        @pl.when(flag == 2)
        def _():
            step(qi, True)

        if bq == bk:

            @pl.when(flag == 3)
            def _():
                step(qi, True, 0, bq // 2, bk // 2)
                step(qi, True, bq // 2, bq // 2, bk)

        return carry

    lax.fori_loop(ko // bq, nq, body, 0)
    r = pl.multiple_of(ko, bk)
    ln2 = math.log(2.0)
    gap = dqkv.shape[1] - 3 * nh * HD
    dqkv[pl.ds(r, bk), nh * HD :] = jnp.concatenate(
        [dk_s[h][:, :HD] * ln2 for h in range(nh)]
        + [dv_s[h][:, :HD] for h in range(nh)]
        + [jnp.zeros((bk, gap), f32)],
        axis=1,
    ).astype(bf16)

    @pl.when(kb == nk - 1)
    def _():
        total = jnp.zeros((1, LN), f32)
        for i in range(nq):
            rows = slice(i * bq, (i + 1) * bq)
            for h in range(nh):
                total = total + jnp.sum(
                    dq_s[h, rows, :] * qa[rows, h * LN : (h + 1) * LN].astype(f32), axis=0, keepdims=True
                )
            grads = jnp.concatenate([dq_s[h, rows, :][:, :HD] for h in range(nh)], axis=1)
            dqkv[rows, 0 : nh * HD] = (grads * scale[...]).astype(bf16)
        gscale[...] = jnp.broadcast_to(total, gscale.shape)


def attn_bwd(qa, kv, pieces, of, mine, seg_row, scale, heads, group, groups, bq=512, bk=512):
    n = qa.shape[0]
    nh = heads // groups
    w = nh * LN
    once = pl.Buffered(1)
    spec = pltpu.PrefetchScalarGridSpec(
        num_scalar_prefetch=2,
        grid=(n // bk,),
        in_specs=[
            pl.BlockSpec((n, w), lambda i, f, m: (0, group), pipeline_mode=once),
            pl.BlockSpec((bk, w), lambda i, f, m: (i, group)),
            pl.BlockSpec((bk, w), lambda i, f, m: (i, groups + group)),
            *[pl.BlockSpec((n // 4, heads * HD), lambda i, f, m: (0, 0), pipeline_mode=once)] * 4,
            pl.BlockSpec((n, w), lambda i, f, m: (0, group), pipeline_mode=once),
            pl.BlockSpec((bk, 1), lambda i, f, m: (i, 0)),
            pl.BlockSpec((1, n), lambda i, f, m: (0, 0)),
            pl.BlockSpec((1, nh * HD), lambda i, f, m: (0, 0)),
        ],
        out_specs=[
            pl.BlockSpec((n, lanes_up(3 * nh * HD)), lambda i, f, m: (0, 0)),
            pl.BlockSpec((8, LN), lambda i, f, m: (0, 0)),
        ],
        scratch_shapes=[
            pltpu.VMEM((n, w), bf16),
            pltpu.VMEM((nh, n, LN), f32),
            pltpu.VMEM((nh, bk, LN), f32),
            pltpu.VMEM((nh, bk, LN), f32),
        ],
    )
    return pl.pallas_call(
        functools.partial(bwd_kernel, first=group * nh, nh=nh, bq=bq, bk=bk, n=n),
        out_shape=[
            pltpu.HBM((n, lanes_up(3 * nh * HD)), bf16),
            pltpu.HBM((8, LN), f32),
        ],
        grid_spec=spec,
        compiler_params=pltpu.CompilerParams(vmem_limit_bytes=48 << 20),
        cost_estimate=cost(300 if group == 0 else 0.001),
        name="attn_bwd",
    )(block_flags(seg_row, bq, bk), mine.reshape(1), hbm(qa), hbm(kv), hbm(kv), *pieces, hbm(of), seg_row[:, None], seg_row[None], scale)


def quarter_columns(place, parts, groups, nh):
    width = nh // groups * HD
    return [
        (t * D + place * nh * HD + g * width, width) for g in range(groups) for t in range(3)
    ]


def pick_kernel(mine, w_ref, out, *, parts, groups, nh):
    for i in range(parts):

        @pl.when(mine[0] == i)
        def _(i=i):
            cut = [w_ref[:, a : a + width] for a, width in quarter_columns(i, parts, groups, nh)]
            used = sum(x.shape[1] for x in cut)
            pad = jnp.zeros((cut[0].shape[0], out.shape[1] - used), out.dtype)
            out[...] = jnp.concatenate(cut + [pad], axis=1)


def lanes_up(n):
    return -(-n // LN) * LN


def pick(w, mine, parts, groups, nh):
    rows = w.shape[0]
    step = 320 if rows % 320 == 0 else rows
    return pl.pallas_call(
        functools.partial(pick_kernel, parts=parts, groups=groups, nh=nh),
        out_shape=pltpu.HBM((rows, lanes_up(3 * nh * HD)), w.dtype),
        grid_spec=pltpu.PrefetchScalarGridSpec(
            num_scalar_prefetch=1,
            grid=(rows // step,),
            in_specs=[pl.BlockSpec((step, 3 * D), lambda i, m: (i, 0))],
            out_specs=pl.BlockSpec((step, lanes_up(3 * nh * HD)), lambda i, m: (i, 0)),
        ),
        cost_estimate=cost(5),
        name="pick",
    )(mine.reshape(1), hbm(w))


def stretch_kernel(x_ref, out, *, groups, nh):
    value = x_ref[...]
    each = 3 * nh * HD // groups
    zero = jnp.zeros((value.shape[0], LN - HD), value.dtype)
    per = nh // groups
    wide = []
    for t in range(3):
        for h in range(nh):
            at = (h // per) * each + t * per * HD + (h % per) * HD
            wide += [value[:, at : at + HD], zero]
    out[...] = jnp.concatenate(wide, axis=1)


def stretch(x, groups, nh, us):
    rows, width = x.shape
    step = 320
    return pl.pallas_call(
        functools.partial(stretch_kernel, groups=groups, nh=nh),
        out_shape=pltpu.HBM((rows, 3 * nh * LN), x.dtype),
        grid=(rows // step,),
        in_specs=[pl.BlockSpec((step, width), lambda i: (i, 0))],
        out_specs=pl.BlockSpec((step, 3 * nh * LN), lambda i: (i, 0)),
        cost_estimate=cost(us),
        name="stretch",
    )(hbm(x))


def order_kernel(own_first, a_ref, b_ref, out):
    half = pl.program_id(0)

    @pl.when(half == 0)
    def _():
        out[...] = a_ref[...].T

    @pl.when(half == 1)
    def _():
        out[...] = b_ref[...].T


def order(own, other, own_at):
    rows, width = own.shape
    step = 256
    return pl.pallas_call(
        order_kernel,
        out_shape=pltpu.HBM((width, 2 * rows), own.dtype),
        grid_spec=pltpu.PrefetchScalarGridSpec(
            num_scalar_prefetch=1,
            grid=(2, width // step),
            in_specs=[
                pl.BlockSpec((rows, step), lambda i, j, m: (0, j * (1 - i))),
                pl.BlockSpec((rows, step), lambda i, j, m: (0, j * i)),
            ],
            out_specs=pl.BlockSpec((step, rows), lambda i, j, m: (j, i ^ m[0])),
        ),
        cost_estimate=cost(200.0),
        name="order",
    )(own_at.reshape(1), hbm(own), hbm(other))


def transpose_kernel(x_ref, out):
    out[...] = x_ref[...].T


def transpose(x):
    rows, cols = x.shape
    step = 256
    return pl.pallas_call(
        transpose_kernel,
        out_shape=pltpu.HBM((cols, rows), x.dtype),
        grid=(rows // step,),
        in_specs=[pl.BlockSpec((step, cols), lambda i: (i, 0))],
        out_specs=pl.BlockSpec((cols, step), lambda i: (0, i)),
        cost_estimate=CHEAP,
        name="transpose",
    )(hbm(x))


def project_kernel(info, *refs, count, halves, width, fresh):
    pairs = refs[: 2 * count]
    gain = refs[2 * count]
    weights = refs[2 * count + 1 : 2 * count + 1 + halves]
    scale, ones = refs[2 * count + 1 + halves : 2 * count + 3 + halves]
    normed_ref, q_ref, kv_ref, mine_ref, w = refs[-5:]
    j, tile = pl.program_id(0), pl.program_id(1)
    step = normed_ref.shape[0]

    @pl.when((j == 0) & (tile == 0))
    def _():
        for i, ref in enumerate(weights):
            h = ref.shape[0]
            start = (info[count + 2] ^ i) * h if halves == 2 else 0
            w[pl.ds(pl.multiple_of(start, 16), h), :] = ref[...]
        if not fresh:
            mine_ref[...] = refs[2 * count + 3 + halves][...]

    def work(x_ref):
        value = x_ref[...]
        x = value.astype(f32)
        inverse = lax.rsqrt(jnp.mean(x * x, axis=-1, keepdims=True) + epsilon)
        normed = (x * inverse * gain[...]).astype(bf16)
        normed_ref[...] = normed
        q_ref[...] = (
            jnp.dot(normed, w[:, :width], preferred_element_type=f32) * scale[...]
        ).astype(bf16)
        kv_ref[...] = (
            jnp.dot(normed, w[:, width:], preferred_element_type=f32) + ones[...]
        ).astype(bf16)

        @pl.when(info[count + 1] == info[j])
        def _():
            mine_ref[pl.ds(pl.multiple_of(tile * step, step), step), :] = value

    for i in range(count):
        for lane in range(2):

            @pl.when((j == i) & (info[count] == lane))
            def _(i=i, lane=lane):
                work(pairs[2 * i + 1 - lane])


def project(pairs, places, lane, mine, wt, gain, weights, scale, ones, group_len, carried=None):
    count = len(pairs)
    rows, d = pairs[0][0].shape
    width = scale.shape[1]
    step = 256
    tiles = rows // step
    full = lambda j, t, f: (0, 0)
    at = lambda j, t, f: (f[j] * tiles + t, 0)
    once = pl.Buffered(1)
    info = jnp.stack(list(places) + [lane.astype(jnp.int32), mine, wt])
    args = [x for pair in pairs for x in pair] + [gain, *map(hbm, weights), scale, ones]
    in_specs = [
        pl.BlockSpec(
            (step, d),
            lambda j, t, f, i=i: (jnp.where(j == i, t, jnp.where(j > i, tiles - 1, 0)), 0),
        )
        for i in range(count)
        for _ in range(2)
    ]
    in_specs += [pl.BlockSpec((1, d), full, pipeline_mode=once)]
    in_specs += [pl.BlockSpec(w.shape, full, pipeline_mode=once) for w in weights]
    in_specs += [
        pl.BlockSpec((1, width), full, pipeline_mode=once),
        pl.BlockSpec((1, 2 * width), full, pipeline_mode=once),
    ]
    aliases = {}
    if carried is not None:
        base = len(args) + 2
        args += [hbm(x) for x in (carried[3], *carried[:3])]
        in_specs += [pl.BlockSpec((rows, d), full, pipeline_mode=once)]
        in_specs += [pl.BlockSpec(memory_space=pl.ANY)] * 3
        aliases = {base: 0, base + 1: 1, base + 2: 2}
    return pl.pallas_call(
        functools.partial(
            project_kernel, count=count, halves=len(weights), width=width, fresh=carried is None
        ),
        out_shape=[
            pltpu.HBM((group_len, d), bf16),
            pltpu.HBM((group_len, width), bf16),
            pltpu.HBM((group_len, 2 * width), bf16),
            pltpu.HBM((rows, d), bf16),
        ],
        grid_spec=pltpu.PrefetchScalarGridSpec(
            num_scalar_prefetch=1,
            grid=(count, tiles),
            in_specs=in_specs,
            out_specs=[
                pl.BlockSpec((step, d), at),
                pl.BlockSpec((step, width), at),
                pl.BlockSpec((step, 2 * width), at),
                pl.BlockSpec((rows, d), full),
            ],
            scratch_shapes=[pltpu.VMEM((d, 3 * width), bf16)],
        ),
        input_output_aliases=aliases,
        compiler_params=pltpu.CompilerParams(vmem_limit_bytes=32 << 20),
        cost_estimate=cost(15),
        name="project",
    )(info, *args)


def tail_body(at, p0, p1, p2, p3, x_ref, g_ref, w_s, gain, outs, need):
    lo_ref, left_ref, right_ref, gr_ref, c0, c1, c2, c3, gg_ref = outs
    att_ref, nm_ref, act_ref = (left_ref.at[i] for i in range(3))
    gp_ref, gh_ref = (right_ref.at[i] for i in range(2))
    right_ref[2] = g_ref[...]
    mine = at[0]
    pieces = (p0, p1, p2, p3)
    cols = p0.shape[1]
    nt = (((1,), (1,)), ((), ()))
    for i in range(4):

        @pl.when(mine == i)
        def _(i=i):
            att_ref[...] = jnp.concatenate([pieces[i ^ k][...] for k in range(4)], axis=1)

    need(0)
    resid = x_ref[...].astype(f32) + jnp.dot(att_ref[...], w_s[0], preferred_element_type=f32)
    inverse = lax.rsqrt(jnp.mean(resid * resid, axis=-1, keepdims=True) + epsilon)
    normed = (resid * inverse * gain[...]).astype(bf16)
    nm_ref[...] = normed
    need(1)
    hidden = jnp.dot(normed, w_s[1], preferred_element_type=f32)
    sig = 1.0 / (1.0 + jnp.exp(-hidden))
    active = (hidden * sig).astype(bf16)
    act_ref[...] = active
    need(2)
    lo_ref[...] = (resid + jnp.dot(active, w_s[2], preferred_element_type=f32)).astype(bf16)
    grad_active = lax.dot_general(g_ref[...], w_s[2], nt, preferred_element_type=f32)
    grad_hidden = (grad_active * sig * (1.0 + hidden * (1.0 - sig))).astype(bf16)
    gh_ref[...] = grad_hidden
    grad_normed = lax.dot_general(grad_hidden, w_s[1], nt, preferred_element_type=f32)
    gg_ref[...] += jnp.sum(grad_normed * resid * inverse, axis=0, keepdims=True)
    scaled = grad_normed * gain[...]
    grad_resid = (
        g_ref[...].astype(f32)
        + inverse * scaled
        - resid * (inverse * inverse * inverse) * jnp.mean(scaled * resid, axis=-1, keepdims=True)
    )
    gr_ref[...] = grad_resid
    grad_proj = grad_resid.astype(bf16)
    gp_ref[...] = grad_proj
    grad_att = lax.dot_general(grad_proj, w_s[0], nt, preferred_element_type=f32).astype(bf16)
    for i in range(4):

        @pl.when(mine == i)
        def _(i=i):
            for j, out in enumerate((c0, c1, c2, c3)):
                out[...] = grad_att[:, (i ^ j) * cols : ((i ^ j) + 1) * cols]


def tail_kernel(at, p0, p1, p2, p3, x_ref, g_ref, own0, own1, own2, half0, half, other0, other, gain, *refs, rows, hrows):
    w_s, sems = refs[-2:]
    outs = refs[:-2]

    def copies(i):
        parts = (
            ((own0, own1, own2)[i], at[1], rows),
            (half.at[i - 1] if i else half0, at[2], hrows),
            (other.at[i - 1] if i else other0, at[3], hrows),
        )
        return [
            pltpu.make_async_copy(
                part, w_s.at[i, pl.ds(pl.multiple_of(start, 16), n), :], sems.at[3 * i + k]
            )
            for k, (part, start, n) in enumerate(parts)
        ]

    @pl.when(pl.program_id(0) == 0)
    def _():
        outs[-1][...] = jnp.zeros_like(outs[-1])
        for i in range(3):
            for c in copies(i):
                c.start()

    def need(i):
        @pl.when(pl.program_id(0) == 0)
        def _():
            for c in copies(i):
                c.wait()

    tail_body(at, p0, p1, p2, p3, x_ref, g_ref, w_s, gain, outs, need)


def whole_tail_kernel(at, p0, p1, p2, p3, x_ref, g_ref, w, gain, *outs):
    @pl.when(pl.program_id(0) == 0)
    def _():
        outs[-1][...] = jnp.zeros_like(outs[-1])

    tail_body(at, p0, p1, p2, p3, x_ref, g_ref, w, gain, outs, lambda i: None)


def tail(at, pieces, x, g, weights, gain, tile=256):
    rows, d = x.shape
    cols = pieces[0].shape[1]
    row = lambda i, m: (i, 0)
    once = pl.Buffered(1)
    whole = lambda *shape: pl.BlockSpec(shape, lambda i, m: (0,) * len(shape), pipeline_mode=once)
    wide = pl.BlockSpec((tile, d), row)
    slim = pl.BlockSpec((tile, cols), row)
    if len(weights) == 7:
        body = functools.partial(tail_kernel, rows=weights[0].shape[0], hrows=weights[3].shape[0])
        scratch = [pltpu.VMEM((3, d, d), bf16), pltpu.SemaphoreType.DMA((9,))]
        weight_specs = [pl.BlockSpec(memory_space=pl.ANY)] * 7
    else:
        body = whole_tail_kernel
        scratch = []
        weight_specs = [whole(*w.shape) for w in weights]
    return pl.pallas_call(
        body,
        out_shape=[pltpu.HBM((rows, d), bf16)]
        + [pltpu.HBM((3, rows, d), bf16)] * 2
        + [pltpu.HBM((rows, d), f32)]
        + [pltpu.HBM((rows, cols), bf16)] * 4
        + [pltpu.HBM((1, d), f32)],
        grid_spec=pltpu.PrefetchScalarGridSpec(
            num_scalar_prefetch=1,
            grid=(rows // tile,),
            in_specs=[slim] * 4 + [wide] * 2 + weight_specs + [whole(1, d)],
            out_specs=[wide]
            + [pl.BlockSpec((3, tile, d), lambda i, m: (0, i, 0))] * 2
            + [wide]
            + [slim] * 4
            + [pl.BlockSpec((1, d), lambda i, m: (0, 0))],
            scratch_shapes=scratch,
        ),
        compiler_params=pltpu.CompilerParams(vmem_limit_bytes=52 << 20),
        cost_estimate=cost(0.01),
        name="tail",
    )(at, *pieces, hbm(x), g, *map(hbm, weights), gain)


tn_dims = (((0,), (0,)), ((), ()))


def share_kernel(col, left, right, out):
    value = lax.dot_general(left[0], right[0], tn_dims, preferred_element_type=f32)
    out[...] = value.astype(bf16)


def share(left, right, col):
    n, rows, d = left.shape
    w = d // 2
    block = pl.BlockSpec((d, w), lambda i, c: (0, i))
    return pl.pallas_call(
        share_kernel,
        out_shape=pltpu.HBM((d, n * w), bf16),
        grid_spec=pltpu.PrefetchScalarGridSpec(
            num_scalar_prefetch=1,
            grid=(n,),
            in_specs=[
                pl.BlockSpec((1, rows, d), lambda i, c: (i, 0, 0)),
                pl.BlockSpec((1, rows, w), lambda i, c: (i, 0, c[0])),
            ],
            out_specs=block,
        ),
        compiler_params=pltpu.CompilerParams(vmem_limit_bytes=20 << 20),
        cost_estimate=CHEAP,
        name="share",
    )(col.reshape(1), hbm(left), hbm(right))


def copy(x):
    return pl.pallas_call(
        tick_kernel, out_shape=pltpu.HBM(x.shape, x.dtype), cost_estimate=CHEAP, name="copy"
    )(x)


def tick_kernel(x_ref, out):
    out[...] = x_ref[...]


def tick(x):
    return pl.pallas_call(
        tick_kernel, out_shape=jax.ShapeDtypeStruct(x.shape, x.dtype), cost_estimate=cost(200.0), name="tick"
    )(x)


def total_kernel(*refs, counts):
    out = refs[-1]
    start, column = 0, 0
    for count in counts:
        group = refs[start : start + count]
        start += count
        acc = jnp.zeros(group[0].shape[1:], f32)
        for ref in group:
            for i in range(ref.shape[0]):
                acc = acc + ref[i].astype(f32)
        out[:, column : column + acc.shape[1]] = acc.astype(bf16)
        column += acc.shape[1]


def total(groups):
    flat = [x for group in groups for x in group]
    rows = flat[0].shape[1]
    cuts = 2 if rows % 32 == 0 else 1
    width = sum(group[0].shape[2] for group in groups)
    return pl.pallas_call(
        functools.partial(total_kernel, counts=[len(group) for group in groups]),
        out_shape=pltpu.HBM((rows, width), bf16),
        grid=(cuts,),
        in_specs=[
            pl.BlockSpec((x.shape[0], rows // cuts, x.shape[2]), lambda i: (0, i, 0)) for x in flat
        ],
        out_specs=pl.BlockSpec((rows // cuts, width), lambda i: (i, 0)),
        compiler_params=pltpu.CompilerParams(vmem_limit_bytes=16 << 20),
        cost_estimate=cost(0.001),
        name="total",
    )(*flat)


def add_kernel(a_ref, b_ref, out):
    out[...] = (a_ref[...].astype(f32) + b_ref[...].astype(f32)).astype(bf16)


def add(a, b):
    return pl.pallas_call(
        add_kernel, out_shape=pltpu.HBM(a.shape, bf16), cost_estimate=CHEAP, name="add"
    )(a, b)


def add_rows(a, b):
    rows, cols = a.shape
    block = pl.BlockSpec((rows // 5, cols), lambda i: (i, 0))
    return pl.pallas_call(
        add_kernel,
        out_shape=pltpu.HBM(a.shape, bf16),
        grid=(5,),
        in_specs=[block] * 2,
        out_specs=block,
        compiler_params=pltpu.CompilerParams(vmem_limit_bytes=14 << 20),
        cost_estimate=CHEAP,
        name="add_rows",
    )(hbm(a), hbm(b))


def by_bits(first, second, put):
    for i in range(2):
        for j in range(2):

            @pl.when((first == i) & (second == j))
            def _(i=i, j=j):
                put(i, j)


def place_kernel(at, *refs):
    o0, o1, o2 = refs[-3:]
    block = pl.program_id(0)
    w = o0.shape[2] // 2

    def put(other_x, other_near):
        for core in range(2):

            @pl.when(at[2] == core)
            def _(core=core):
                for side in range(2):
                    part = refs[4 * (side ^ core) + 2 * other_x + other_near][...].astype(f32)
                    for i, out in enumerate((o0, o1, o2)):
                        out[0, :, side * w : (side + 1) * w] = part[:, i * w : (i + 1) * w]

    by_bits((block // 2) ^ at[0], (block % 2) ^ at[1], put)


def place_tail(arrays, at):
    h, width = arrays[0].shape
    d = width // 3 * 2
    whole = pl.BlockSpec((h, width), lambda i, m: (0, 0), pipeline_mode=pl.Buffered(1))
    outs = pl.pallas_call(
        place_kernel,
        out_shape=[pltpu.HBM((4, h, d), f32)] * 3,
        grid_spec=pltpu.PrefetchScalarGridSpec(
            num_scalar_prefetch=1,
            grid=(4,),
            in_specs=[whole] * 8,
            out_specs=[pl.BlockSpec((1, h, d), lambda i, m: (i, 0, 0))] * 3,
        ),
        compiler_params=pltpu.CompilerParams(vmem_limit_bytes=16 << 20),
        cost_estimate=CHEAP,
        name="place_tail",
    )(at, *map(hbm, arrays))
    return [out.reshape(4 * h, d) for out in outs]


def cross_kernel(at, x_ref, g_ref, *refs):
    s = refs[-1]
    s[...] = jnp.dot(x_ref[...], g_ref[...], preferred_element_type=f32)
    half = s.shape[0] // 2
    for w in range(2):

        @pl.when(pl.program_id(0) == w)
        def _(w=w):
            for x in range(2):
                rows = pl.ds(pl.multiple_of((at[1] ^ x) * half, 16), half)
                refs[2 * w + x][...] = s[rows, :].astype(bf16)


def cross(x, g, at):
    d, rows = x.shape
    w = d // 2
    cols = g.shape[1]
    step = 512 if cols % 512 == 0 else cols
    n = cols // step
    first = pl.BlockSpec((w // 2, step), lambda i, j, m: (0, jnp.where(i == 0, j, n - 1)))
    second = pl.BlockSpec((w // 2, step), lambda i, j, m: (0, jnp.where(i == 1, j, 0)))
    return pl.pallas_call(
        cross_kernel,
        out_shape=[pltpu.HBM((w // 2, cols), bf16)] * 4,
        grid_spec=pltpu.PrefetchScalarGridSpec(
            num_scalar_prefetch=1,
            grid=(2, n),
            in_specs=[
                pl.BlockSpec((w, rows), lambda i, j, m: (m[0] ^ i, 0)),
                pl.BlockSpec((rows, step), lambda i, j, m: (0, j)),
            ],
            out_specs=[first, first, second, second],
            scratch_shapes=[pltpu.VMEM((w, step), f32)],
        ),
        compiler_params=pltpu.CompilerParams(vmem_limit_bytes=26 << 20),
        cost_estimate=CHEAP,
        name="cross",
    )(at, hbm(x), hbm(g))


def spread_kernel(at, *refs, width):
    out = refs[-1]
    step = out.shape[1]
    rows = pl.ds(pl.multiple_of(pl.program_id(0) * step, step), step)

    def put(core, near):
        cut = []
        for t in range(3):
            for n in range(2):
                for c in range(2):
                    part = refs[2 * (c ^ core) + (n ^ near)][rows, :]
                    cut.append(part[:, t * width : (t + 1) * width])
        out[0] = jnp.concatenate(cut, axis=1).astype(f32)

    by_bits(at[2], at[1], put)


def spread(arrays, at, used, other_x, carried=None):
    rows, cols = arrays[0].shape
    width = 4 * used
    cuts = 2 if rows % 32 == 0 else 1
    whole = pl.BlockSpec((rows, cols), lambda j, m: (0, 0), pipeline_mode=pl.Buffered(1))
    more = () if carried is None else (carried,)
    return pl.pallas_call(
        functools.partial(spread_kernel, width=used // 3),
        out_shape=pltpu.HBM((2, rows, width), f32),
        grid_spec=pltpu.PrefetchScalarGridSpec(
            num_scalar_prefetch=1,
            grid=(cuts,),
            in_specs=[whole] * 4 + [pl.BlockSpec(memory_space=pl.ANY)] * len(more),
            out_specs=pl.BlockSpec((1, rows // cuts, width), lambda j, m: (m[0] ^ other_x, j, 0)),
        ),
        input_output_aliases={5: 0} if more else {},
        compiler_params=pltpu.CompilerParams(vmem_limit_bytes=20 << 20),
        cost_estimate=CHEAP,
        name="spread",
    )(at, *arrays, *more)


def back_kernel(shards, g_ref, w_ref, *refs):
    acc = jnp.dot(g_ref[...], w_ref[...], preferred_element_type=f32)
    if len(refs) == 2:
        acc = acc + refs[0][0].astype(f32)
    refs[-1][0] = acc.astype(bf16)


def back(grad, w, shards, rows, got=None):
    c, d = w.shape
    n = shards.shape[0]
    step = d
    out = pl.BlockSpec((1, rows, step), lambda j, i, f: (i, 0, j))
    in_specs = [
        pl.BlockSpec((rows, c), lambda j, i, f: (f[i], 0)),
        pl.BlockSpec((c, step), lambda j, i, f: (0, j)),
    ]
    args = [hbm(grad), hbm(w)]
    if got is not None:
        in_specs.append(pl.BlockSpec((1, rows, step), lambda j, i, f: (0, 0, j)))
        args.append(got)
    return pl.pallas_call(
        back_kernel,
        out_shape=pltpu.HBM((n, rows, d), bf16),
        grid_spec=pltpu.PrefetchScalarGridSpec(
            num_scalar_prefetch=1, grid=(d // step, n), in_specs=in_specs, out_specs=out
        ),
        compiler_params=pltpu.CompilerParams(vmem_limit_bytes=22 << 20),
        cost_estimate=CHEAP,
        name="back",
    )(shards, *args)


def finish_kernel(shard, g_ref, w_ref, core, near, x_ref, resid, gain, out, gain_out):
    grad = jnp.dot(g_ref[...], w_ref[...], preferred_element_type=f32)
    grad = grad + core[0].astype(f32) + near[0].astype(f32)
    x = x_ref[...].astype(f32)
    inverse = lax.rsqrt(jnp.mean(x * x, axis=-1, keepdims=True) + epsilon)
    part = jnp.sum(grad * x * inverse, axis=0, keepdims=True)

    @pl.when(pl.program_id(0) == 0)
    def _():
        gain_out[...] = jnp.zeros_like(gain_out)

    gain_out[...] += part
    scaled = grad * gain[...]
    out[...] = (
        resid[...]
        + inverse * scaled
        - x * (inverse * inverse * inverse) * jnp.mean(scaled * x, axis=-1, keepdims=True)
    ).astype(bf16)


def finish(grad, w, shard, core, near, x, resid, gain, tile=256):
    rows, d = x.shape
    c = w.shape[0]
    tiles = rows // tile
    row = lambda i, f: (i, 0)
    once = pl.Buffered(1)
    return pl.pallas_call(
        finish_kernel,
        out_shape=[pltpu.HBM((rows, d), bf16), jax.ShapeDtypeStruct((1, d), f32)],
        grid_spec=pltpu.PrefetchScalarGridSpec(
            num_scalar_prefetch=1,
            grid=(tiles,),
            in_specs=[
                pl.BlockSpec((tile, c), lambda i, f: (f[0] * tiles + i, 0)),
                pl.BlockSpec((c, d), lambda i, f: (0, 0), pipeline_mode=once),
                pl.BlockSpec((1, tile, d), lambda i, f: (1, i, 0)),
                pl.BlockSpec((1, tile, d), lambda i, f: (0, i, 0)),
                pl.BlockSpec((tile, d), row),
                pl.BlockSpec((tile, d), row),
                pl.BlockSpec((1, d), lambda i, f: (0, 0)),
            ],
            out_specs=[pl.BlockSpec((tile, d), row), pl.BlockSpec((1, d), lambda i, f: (0, 0))],
        ),
        compiler_params=pltpu.CompilerParams(vmem_limit_bytes=24 << 20),
        cost_estimate=CHEAP,
        name="finish",
    )(shard.reshape(1), hbm(grad), hbm(w), core, near, hbm(x), hbm(resid), gain)


def rms_inverse(values):
    return lax.rsqrt(jnp.mean(values * values, axis=-1, keepdims=True) + epsilon)


def norm_back(values, inverse, grad_scaled):
    return inverse * grad_scaled - values * (inverse * inverse * inverse) * jnp.mean(
        grad_scaled * values, axis=-1, keepdims=True
    )


def dot(left, right):
    return jnp.dot(left, right, preferred_element_type=f32)


def times_trans(left, right):
    return lax.dot_general(left, right, (((1,), (1,)), ((), ())), preferred_element_type=f32)


def trans_times(left, right):
    return lax.dot_general(left, right, (((0,), (0,)), ((), ())), preferred_element_type=f32)


def rows_at(array, start, count):
    return lax.dynamic_slice_in_dim(array, start, count, 0)


def put_rows(array, rows, start):
    return lax.dynamic_update_slice_in_dim(array, rows, start, 0)


def make_local(sizes):
    def pairs(target):
        found = []
        for gx in range(sizes["gx"]):
            for gc in range(sizes["gc"]):
                for z in range(4):
                    for w in range(sizes["wt"]):
                        goal = target(gx, gc, z, w)
                        if goal is not None and goal != (gx, gc, z, w):
                            found.append((place(gx, gc, z, w), place(*goal)))
        return found

    def place(gx, gc, z, w):
        return ((gx * sizes["gc"] + gc) * 4 + z) * sizes["wt"] + w

    def send(value, target):
        return lax.ppermute(value, AXES, pairs(target))

    def core_mate(gx, gc, z, w):
        return (gx, 1 - gc, z, w)

    def x_mate(gx, gc, z, w):
        return (1 - gx, gc, z, w)

    def near_mate(gx, gc, z, w):
        return (gx, gc, z ^ 1, w)

    def far_mate(gx, gc, z, w):
        return (gx, gc, z ^ 2, w)

    def cross_mate(gx, gc, z, w):
        return (gx, 1 - gc, z ^ 1, w)

    def wt_mate(gx, gc, z, w):
        return (gx, gc, z, 1 - w)

    def wt_x_mate(gx, gc, z, w):
        return (1 - gx, gc, z, 1 - w)

    def to_host(gx, gc, z, w):
        return (gx, 1 - (z & 1), 2 * gc + (z >> 1), w)

    def to_home(gx, gc, z, w):
        return (gx, z >> 1, 2 * (z & 1) + 1 - gc, w)

    def hop1(gx, gc, z, w):
        if gc == 0:
            return (gx, 0, z - 1, w) if z > 0 else None
        return (gx, 1, z + 1, w) if z < 3 else None

    def hop2(gx, gc, z, w):
        if gc == 0:
            return (gx, 0, z - 1, w) if z in (1, 2) else None
        return (gx, 1, z + 1, w) if z in (1, 2) else None

    def hop3(gx, gc, z, w):
        if gc == 0:
            return (gx, 0, z ^ 1, w) if z < 2 else None
        return (gx, 1, z ^ 1, w) if z > 1 else None

    def lane_share(gx, gc, z, w):
        return (gx, 1 - gc, z, w) if gc == z >> 1 else None

    def sum_all(value):
        for axis in ("gc", "wt", "near", "far", "gx"):
            step = 1
            while step < sizes[axis]:

                def mate(gx, gc, z, w, axis=axis, step=step):
                    at = dict(gx=gx, gc=gc, far=z >> 1, near=z & 1, wt=w)
                    at[axis] ^= step
                    return (at["gx"], at["gc"], 2 * at["far"] + at["near"], at["wt"])

                value = value + send(value, mate)
                step *= 2
        return value

    def local(
        tokens, segments, w_qkv, w_proj, w_in, w_out, gain_attn, gain_mlp, query_scale, cotangent
    ):
        gx, gc, host, near, wt = (lax.axis_index(axis) for axis in AXES)
        z = 2 * host + near
        mine = 2 * near + 1 - gc
        parts = 4
        nh = H // parts
        groups = 1
        rows = tokens.shape[1]
        group_len = segments.shape[1]
        wrows = w_qkv.shape[0]
        lane = gc == host
        pair = sizes["wt"] == 2

        def after(value, *others):
            return lax.optimization_barrier((value,) + others)[0]

        picked = pick(w_qkv, mine, parts, groups, nh)
        own = tokens[0]
        got1 = send(own, hop1)
        own_share = send(after(own, picked), lane_share)
        seg_mate = send(after(segments, picked), core_mate)
        got2 = send(got1, hop2)
        got1_share = send(got1, lane_share)
        end = jnp.where(gc == 0, z == 0, z == 3)
        if pair:
            wide_own = stretch(picked, groups, nh, 2)
            got1 = after(got1, wide_own)
            other_w = send(picked, wt_mate)
            wide_w = (wide_own, stretch(other_w, groups, nh, 10))
        else:
            flat_all = lax.all_gather(picked, "wt", axis=0, tiled=True)
            by_head = jnp.transpose(
                flat_all[:, : 3 * nh * HD].reshape(D, groups, 3, nh // groups, HD), (0, 2, 1, 3, 4)
            )
            wide_w = (
                jnp.pad(
                    by_head.reshape(D, 3 * nh, HD), ((0, 0), (0, 0), (0, LN - HD))
                ).reshape(D, -1),
            )
        got3 = send(jnp.where(end, own, got2), hop3)
        got2_share = send(got2, lane_share)
        way = 1 - 2 * host
        last = jnp.where(host == 0, jnp.where(z == 0, 3, 0), jnp.where(z == 3, 0, 3))
        places = (z, z + way, z + 2 * way, last)

        half_rows = wrows // 2
        if pair:
            half_a = send(after(rows_at(w_proj, gc * half_rows, half_rows), other_w), wt_mate)
            half_w = jnp.stack([rows_at(w, gc * half_rows, half_rows) for w in (w_in, w_out)])
            half_w = send(after(half_w, half_a), wt_mate)
        else:
            half_w = jnp.stack([rows_at(w, gc * half_rows, half_rows) for w in (w_proj, w_in, w_out)])
            half_w = lax.all_gather(half_w, "wt", axis=0, tiled=False)

        dim_scale = scale_base / math.sqrt(HD) * jax.nn.softplus(query_scale)
        lane_scale = jnp.tile(jnp.pad(dim_scale * log2e, (0, LN - HD)), nh)[None]
        ones = jnp.tile(
            ((jnp.arange(LN) >= HD) & (jnp.arange(LN) < HD + 3)).astype(f32), 2 * nh
        )[None]
        seg_row = jnp.where(lane, segments, seg_mate)[0]
        fixed = (lane, mine, wt, gain_attn[None], wide_w, lane_scale, ones, group_len)
        carried = project(((own, own_share), (got1, got1_share)), places[:2], *fixed)
        got3_share = send(after(got3, carried[0]), lane_share)
        first_done = (lambda x: after(x, half_a)) if pair else (lambda x: x)
        all_normed, queries, keyval, inputs = project(
            ((got2, got2_share), (got3, first_done(got3_share))), places[2:], *fixed, carried=carried
        )
        grad_mlp = send(after(cotangent[0], got3_share), to_host)

        att, att_float, q_aug = attn_fwd(queries, keyval, seg_row, nh)
        att, half_w, _ = lax.optimization_barrier((att, half_w, grad_mlp))

        trades = (core_mate, near_mate, cross_mate)
        att_pieces = [rows_at(att, (mine ^ j) * rows, rows) for j in range(parts)]
        half_mate = send(after(half_w, *att_pieces), core_mate)
        att_pieces = [att_pieces[0]] + [send(att_pieces[j + 1], trades[j]) for j in range(3)]
        if pair:
            w_trans = order(after(picked, att), other_w, wt)
        else:
            w_trans = flat_all.T
        normed_trans = transpose(after(all_normed, w_trans))
        if pair:
            mate_a = send(after(half_a, *att_pieces[1:2]), core_mate)
            weights = (w_proj, w_in, w_out, half_a, half_w, mate_a, half_mate)
            starts = (wt * wrows, (1 - wt) * wrows + gc * half_rows, (1 - wt) * wrows + (1 - gc) * half_rows)
        else:
            one = gc == 0
            tail_w = jnp.stack(
                [jnp.where(one, half_w, half_mate), jnp.where(one, half_mate, half_w)], axis=1
            )
            weights = (jnp.transpose(tail_w, (2, 0, 1, 3, 4)).reshape(3, D, D),)
            starts = ()
        (
            layer_out,
            left,
            right,
            grad_resid,
            *pieces,
            grad_gain_mlp,
        ) = tail(
            jnp.stack([mine, *starts]), att_pieces, after(inputs, normed_trans), grad_mlp, weights, gain_mlp[None]
        )
        pieces = [pieces[0]] + [send(pieces[j + 1], trades[j]) for j in range(3)]

        shared = share(after(left, pieces[1]), right, 1 - gc)
        from_core = send(shared, core_mate)
        own_half = share(left, right, after(gc, shared))
        pieces[2:] = [after(piece, own_half) for piece in pieces[2:]]
        home_out = send(after(layer_out, *pieces[1:]), to_home)
        late_gain = tick(after(gain_attn.reshape(-1, LN), *pieces[1:]))
        summed = add_rows(own_half, after(from_core, late_gain))
        kept = lax.all_to_all(summed, ("wt", "gx", "near"), 0, 0, tiled=True)

        scale_row = jnp.tile(dim_scale, nh // groups)[None]

        def backward(group, *others):
            first, *rest = pieces
            return attn_bwd(
                q_aug,
                keyval,
                (after(first, summed, *others), *rest),
                att_float,
                mine,
                seg_row,
                scale_row,
                nh,
                group,
                groups,
            )

        def by_rows(grad):
            if pair:
                own, *rest = cross(normed_trans, grad, jnp.stack([wt, gx]))
                got = [send(part, mate) for part, mate in zip(rest, (x_mate, wt_mate, wt_x_mate))]
                return [part[None] for part in (own, *got)]
            part = dot(normed_trans, grad).astype(bf16)
            sources = sizes["wt"] * 2
            got = lax.all_to_all(part, ("wt", "gx"), 0, 0, tiled=True)
            return [got.reshape(sources, D // sources, -1)]

        grad_project, grad_lanes = backward(0)
        layer_out = after(home_out, grad_project)

        last_step = [layer_out]

        def turn(value):
            return after(value, *last_step)

        def done(value):
            last_step[0] = value
            return value

        sources = sizes["wt"] * 4
        to_core = done(back(turn(grad_project), w_trans, jnp.stack([mine ^ 3, mine ^ 1]), rows))
        from_core = send(to_core, core_mate)
        by_place = by_rows(turn(grad_project))
        done(by_place[0])
        to_near = done(back(grad_project, w_trans, (mine ^ 2).reshape(1), rows, turn(from_core)))
        from_near = send(to_near, near_mate)
        t1 = done(total([[turn(kept).reshape(sources, D // sources, -1)]]))
        t1_far = send(t1, far_mate)
        layer_out = done(copy(turn(layer_out)))
        by_place[0] = turn(by_place[0])
        q1 = done(total([by_place]))
        q1_far = send(q1, far_mate)
        t2 = done(add(turn(t1), t1_far))
        t2_near = send(t2, near_mate)
        t2_x = send(t2, x_mate)
        grad_tokens, grad_gain_attn = finish(
            grad_project,
            w_trans,
            mine,
            from_core,
            turn(from_near),
            inputs,
            grad_resid,
            late_gain.reshape(1, -1),
        )
        done(grad_tokens)
        grad_query_scale = (
            grad_lanes[0, :HD]
            / (dim_scale * log2e)
            * (scale_base / math.sqrt(HD))
            * jax.nn.sigmoid(query_scale)
        )
        small = jnp.concatenate(
            [grad_gain_attn[0], grad_gain_mlp[0], jnp.pad(grad_query_scale, (0, LN - HD))]
        ).reshape(-1, LN)
        t2_x = done(turn(t2_x))
        t2_near = done(turn(t2_near))
        t2_near_x = send(t2_near, x_mate)
        tails = [t2, t2_near, t2_x]
        tails_mate = [send(turn(x), core_mate) for x in tails]
        q2 = done(add(turn(q1), q1_far))
        q2_near = send(q2, near_mate)
        q2_x = send(q2, x_mate)
        home_grad = send(turn(grad_tokens), to_home)
        q2_near = done(turn(q2_near))
        q2_near_x = send(q2_near, x_mate)
        t2_near_x = done(turn(t2_near_x))
        tails += [t2_near_x]
        tails_mate += [send(t2_near_x, core_mate)]
        q2_x = done(turn(q2_x))
        quads_mate = [send(turn(x), core_mate) for x in (q2, q2_near, q2_x)]
        tails_mate[3] = turn(tails_mate[3])
        totals = place_tail(tails + tails_mate, jnp.stack([gx, near, gc]))
        done(totals[0])
        used = 3 * nh * HD
        spread_at = jnp.stack([gx, near, 1 - gc])
        quads_mate[0] = done(after(turn(quads_mate[0]), quads_mate[1]))
        small = done(sum_all(turn(small))).reshape(-1)
        home_grad = done(turn(home_grad))
        q2_near_x = done(turn(q2_near_x))
        last_mate = send(q2_near_x, core_mate)
        total_qkv = done(
            spread((turn(q2), q2_near, quads_mate[0], quads_mate[1]), spread_at, used, 0)
        )
        grad_tokens = done(copy(turn(home_grad)))
        total_qkv = spread(
            (q2_x, turn(q2_near_x), quads_mate[2], last_mate), spread_at, used, 1, total_qkv
        ).reshape(wrows, 3 * D)
        return (
            layer_out[None],
            grad_tokens[None],
            total_qkv,
            *totals,
            small[:D],
            small[D : 2 * D],
            small[2 * D : 2 * D + HD],
        )

    return local


def solution(mesh):
    groups, parts, wt = (mesh.shape[axis] for axis in ("grp", "ctx", "wt"))
    inner = Mesh(mesh.devices.reshape(groups // 2, 2, parts // 2, 2, wt), AXES)
    sizes = dict(inner.shape)
    split = P(("gx", "gc", "wt"), ("far", "near"), None)
    weight = P("wt", None)
    return jax.shard_map(
        make_local(sizes),
        mesh=inner,
        in_specs=(
            split,
            P(("gx", "gc", "wt"), None),
            weight,
            weight,
            weight,
            weight,
            P(),
            P(),
            P(),
            split,
        ),
        out_specs=(split, split, weight, weight, weight, weight, P(), P(), P()),
        check_vma=False,
    )
```

```python
import functools
import math

import jax
import jax.numpy as jnp
from jax import lax
from jax.experimental import pallas as pl
from jax.experimental.pallas import tpu as pltpu
from jax.sharding import Mesh
from jax.sharding import PartitionSpec as P

D = 1280
H = 16
HD = 80
LN = 128
epsilon = 1e-06
scale_base = 1.442695041
log2e = 1.4426950408889634
NEG = -1e30
def cost(us):
    return pl.CostEstimate(flops=int(us * 1_000_000_000), transcendentals=0, bytes_accessed=1000)


CHEAP = cost(0.001)
f32 = jnp.float32
bf16 = jnp.bfloat16
AXES = ("gx", "gc", "far", "near", "wt")


def hbm(x):
    return pltpu.with_memory_space_constraint(x, pltpu.HBM)


def block_flags(seg_row, bq, bk):
    n = seg_row.shape[0]
    q = seg_row.reshape(n // bq, bq)
    k = seg_row.reshape(n // bk, bk)
    qf, ql = q[:, 0][:, None], q[:, -1][:, None]
    kf, kl = k[:, 0][None], k[:, -1][None]
    qs = jnp.arange(n // bq, dtype=jnp.int32)[:, None] * bq
    ks = jnp.arange(n // bk, dtype=jnp.int32)[None] * bk
    below = ks + bk - 1 <= qs
    skip = (ks > qs + bq - 1) | ((kf > 0) & (kl < qf))
    same = (qf == ql) & (kl == ql) & ((kf == kl) | ((kf == 0) & (kl == 1)))
    full = below & ((kl == 0) | same)
    flags = jnp.where(skip, 0, jnp.where(full, 1, 2))
    if bq == bk:
        flags = jnp.where(qs == ks, 3, flags)
    return flags.astype(jnp.int32).reshape(-1)


def put_split(base, col, lanes):
    hi = col.astype(bf16).astype(f32)
    rest = col - hi
    mid = rest.astype(bf16).astype(f32)
    out = jnp.where(lanes == HD, hi, base)
    out = jnp.where(lanes == HD + 1, mid, out)
    return jnp.where(lanes == HD + 2, rest - mid, out).astype(bf16)


def fwd_kernel(flags, q_ref, kv, segc, segr, att, of, qaug, m_s, acc_s, *, nh, bq, bk, nk):
    qi = pl.program_id(0)
    count = (qi * bq + bq + bk - 1) // bk
    nt = (((1,), (1,)), ((), ()))
    acc_s[...] = jnp.zeros_like(acc_s)
    m_s[...] = jnp.zeros_like(m_s)

    def mask(ko, q0=0, qn=bq, kn=bk):
        qpos = qi * bq + q0 + lax.broadcasted_iota(jnp.int32, (qn, kn), 0)
        kpos = ko + lax.broadcasted_iota(jnp.int32, (qn, kn), 1)
        ks = segr[:, pl.ds(ko, kn)]
        return (kpos <= qpos) & ((ks == 0) | (ks == segc[q0 : q0 + qn, :]))

    def step(kb, masked, q0=0, qn=bq, kn=bk):
        ko = pl.multiple_of(kb * bk, bk)
        if masked:
            allowed = mask(ko, q0, qn, kn)
        rows = slice(q0, q0 + qn)
        for h in range(nh):
            k = kv[pl.ds(ko, kn), h * LN : (h + 1) * LN]
            v = kv[pl.ds(ko, kn), (nh + h) * LN : (nh + h + 1) * LN]
            q = q_ref[rows, h * LN : (h + 1) * LN]
            p = jnp.exp2(lax.dot_general(q, k, nt, preferred_element_type=f32))
            if masked:
                p = jnp.where(allowed, p, 0.0)
            acc_s[h, rows, :] += jnp.dot(p.astype(bf16), v, preferred_element_type=f32)

    def body(kb, carry):
        flag = flags[qi * nk + kb]

        @pl.when(flag == 1)
        def _():
            step(kb, False)

        @pl.when(flag >= 2)
        def _():
            step(kb, True)

        return carry

    lax.fori_loop(0, count, body, 0)
    bad = jnp.zeros((bq, 1), f32)
    for h in range(nh):
        total = acc_s[h][:, HD : HD + 1]
        bad = jnp.maximum(bad, jnp.where((total > 2.0**-60) & (total < 2.0**60), 0.0, 1.0))

    @pl.when(jnp.max(bad) > 0.0)
    def _():
        def head(h, carry):
            kc = pl.ds(pl.multiple_of(h * LN, LN), LN)
            vc = pl.ds(pl.multiple_of((nh + h) * LN, LN), LN)
            m_s[h] = jnp.full((bq, LN), NEG, f32)
            acc_s[h] = jnp.zeros((bq, LN), f32)

            def inner(kb, carry):
                @pl.when(flags[qi * nk + kb] > 0)
                def _():
                    ko = pl.multiple_of(kb * bk, bk)
                    s = lax.dot_general(
                        q_ref[:, kc], kv[pl.ds(ko, bk), kc], nt, preferred_element_type=f32
                    )
                    s = jnp.where(mask(ko), s, NEG)
                    old = m_s[h]
                    new = jnp.maximum(old, jnp.max(s, axis=1, keepdims=True))
                    p = jnp.exp2(s - new[:, :1]).astype(bf16)
                    m_s[h] = new
                    acc_s[h] = acc_s[h] * jnp.exp2(old - new) + jnp.dot(
                        p, kv[pl.ds(ko, bk), vc], preferred_element_type=f32
                    )

                return carry

            lax.fori_loop(0, count, inner, 0)
            return carry

        lax.fori_loop(0, nh, head, 0)

    lanes = lax.broadcasted_iota(jnp.int32, (bq, LN), 1)
    outs = []
    for h in range(nh):
        acc = acc_s[h]
        total = acc[:, HD : HD + 1]
        out = acc * (1.0 / total)
        of[:, h * LN : (h + 1) * LN] = jnp.where(lanes < HD, out, 0.0).astype(bf16)
        outs.append(out[:, :HD])
        lse = m_s[h][:, :1] + jnp.log2(total)
        qaug[:, h * LN : (h + 1) * LN] = put_split(
            q_ref[:, h * LN : (h + 1) * LN].astype(f32), -lse, lanes
        )
    att[...] = jnp.concatenate(outs, axis=1).astype(bf16)


def attn_fwd(q, kv, seg_row, nh, bq=512, bk=512):
    n = q.shape[0]
    w = nh * LN
    spec = pltpu.PrefetchScalarGridSpec(
        num_scalar_prefetch=1,
        grid=(n // bq,),
        in_specs=[
            pl.BlockSpec((bq, w), lambda i, f: (i, 0)),
            pl.BlockSpec((n, 2 * w), lambda i, f: (0, 0)),
            pl.BlockSpec((bq, 1), lambda i, f: (i, 0)),
            pl.BlockSpec((1, n), lambda i, f: (0, 0)),
        ],
        out_specs=[
            pl.BlockSpec((bq, nh * HD), lambda i, f: (i, 0)),
            pl.BlockSpec((bq, w), lambda i, f: (i, 0)),
            pl.BlockSpec((bq, w), lambda i, f: (i, 0)),
        ],
        scratch_shapes=[pltpu.VMEM((nh, bq, LN), f32), pltpu.VMEM((nh, bq, LN), f32)],
    )
    return pl.pallas_call(
        functools.partial(fwd_kernel, nh=nh, bq=bq, bk=bk, nk=n // bk),
        out_shape=[
            pltpu.HBM((n, nh * HD), bf16),
            pltpu.HBM((n, w), bf16),
            pltpu.HBM((n, w), bf16),
        ],
        grid_spec=spec,
        compiler_params=pltpu.CompilerParams(vmem_limit_bytes=28 << 20),
        cost_estimate=cost(0.01),
        name="attn_fwd",
    )(block_flags(seg_row, bq, bk), hbm(q), hbm(kv), seg_row[:, None], seg_row[None])


def bwd_kernel(
    flags, mine, qa, kk, vv, do0, do1, do2, do3, of, segc, segr, scale, dqkv, gscale, doa_s, dq_s, dk_s, dv_s, *, first, nh, bq, bk, n
):
    nk = n // bk
    nq = n // bq
    kb = pl.program_id(0)
    part = n // 4
    step_rows = 256 if part % 256 == 0 else part
    lanes = lax.broadcasted_iota(jnp.int32, (step_rows, LN), 1)

    @pl.when(kb == 0)
    def _():
        dq_s[...] = jnp.zeros_like(dq_s)
        for j, piece in enumerate((do0, do1, do2, do3)):
            start = (mine[0] ^ j) * part
            for i in range(part // step_rows):
                d = piece[i * step_rows : (i + 1) * step_rows, :].astype(f32)
                r = pl.ds(pl.multiple_of(start + i * step_rows, step_rows), step_rows)
                for h in range(nh):
                    at = (first + h) * HD
                    dh = jnp.concatenate(
                        [d[:, at : at + HD], jnp.zeros((step_rows, LN - HD), f32)], axis=1
                    )
                    c = slice(h * LN, (h + 1) * LN)
                    delta = jnp.sum(dh * of[r, c].astype(f32), axis=1, keepdims=True)
                    doa_s[r, c] = put_split(dh, -delta, lanes)

    dk_s[...] = jnp.zeros_like(dk_s)
    dv_s[...] = jnp.zeros_like(dv_s)
    ko = kb * bk
    nt = (((1,), (1,)), ((), ()))
    tn = (((0,), (0,)), ((), ()))

    def step(qi, masked, q0=0, qn=bq, kn=bk):
        qo = pl.multiple_of(qi * bq + q0, qn)
        rows = slice(0, kn)
        if masked:
            kpos = ko + lax.broadcasted_iota(jnp.int32, (kn, qn), 0)
            qpos = qo + lax.broadcasted_iota(jnp.int32, (kn, qn), 1)
            ks = segc[rows, :]
            allowed = (kpos <= qpos) & ((ks == 0) | (ks == segr[:, pl.ds(qo, qn)]))
        for h in range(nh):
            c = slice(h * LN, (h + 1) * LN)
            q = qa[pl.ds(qo, qn), c]
            k = kk[rows, c]
            d = doa_s[pl.ds(qo, qn), c]
            p = jnp.exp2(lax.dot_general(k, q, nt, preferred_element_type=f32))
            if masked:
                p = jnp.where(allowed, p, 0.0)
            ds = (p * lax.dot_general(vv[rows, c], d, nt, preferred_element_type=f32)).astype(bf16)
            dv_s[h, rows, :] += jnp.dot(p.astype(bf16), d, preferred_element_type=f32)
            dk_s[h, rows, :] += jnp.dot(ds, q, preferred_element_type=f32)
            dq_s[h, pl.ds(qo, qn), :] += lax.dot_general(ds, k, tn, preferred_element_type=f32)

    def body(qi, carry):
        flag = flags[qi * nk + kb]

        @pl.when(flag == 1)
        def _():
            step(qi, False)

        @pl.when(flag == 2)
        def _():
            step(qi, True)

        if bq == bk:

            @pl.when(flag == 3)
            def _():
                step(qi, True, 0, bq // 2, bk // 2)
                step(qi, True, bq // 2, bq // 2, bk)

        return carry

    lax.fori_loop(ko // bq, nq, body, 0)
    r = pl.multiple_of(ko, bk)
    ln2 = math.log(2.0)
    gap = dqkv.shape[1] - 3 * nh * HD
    dqkv[pl.ds(r, bk), nh * HD :] = jnp.concatenate(
        [dk_s[h][:, :HD] * ln2 for h in range(nh)]
        + [dv_s[h][:, :HD] for h in range(nh)]
        + [jnp.zeros((bk, gap), f32)],
        axis=1,
    ).astype(bf16)

    @pl.when(kb == nk - 1)
    def _():
        total = jnp.zeros((1, LN), f32)
        for i in range(nq):
            rows = slice(i * bq, (i + 1) * bq)
            for h in range(nh):
                total = total + jnp.sum(
                    dq_s[h, rows, :] * qa[rows, h * LN : (h + 1) * LN].astype(f32), axis=0, keepdims=True
                )
            grads = jnp.concatenate([dq_s[h, rows, :][:, :HD] for h in range(nh)], axis=1)
            dqkv[rows, 0 : nh * HD] = (grads * scale[...]).astype(bf16)
        gscale[...] = jnp.broadcast_to(total, gscale.shape)


def attn_bwd(qa, kv, pieces, of, mine, seg_row, scale, heads, group, groups, bq=512, bk=512):
    n = qa.shape[0]
    nh = heads // groups
    w = nh * LN
    once = pl.Buffered(1)
    spec = pltpu.PrefetchScalarGridSpec(
        num_scalar_prefetch=2,
        grid=(n // bk,),
        in_specs=[
            pl.BlockSpec((n, w), lambda i, f, m: (0, group), pipeline_mode=once),
            pl.BlockSpec((bk, w), lambda i, f, m: (i, group)),
            pl.BlockSpec((bk, w), lambda i, f, m: (i, groups + group)),
            *[pl.BlockSpec((n // 4, heads * HD), lambda i, f, m: (0, 0), pipeline_mode=once)] * 4,
            pl.BlockSpec((n, w), lambda i, f, m: (0, group), pipeline_mode=once),
            pl.BlockSpec((bk, 1), lambda i, f, m: (i, 0)),
            pl.BlockSpec((1, n), lambda i, f, m: (0, 0)),
            pl.BlockSpec((1, nh * HD), lambda i, f, m: (0, 0)),
        ],
        out_specs=[
            pl.BlockSpec((n, lanes_up(3 * nh * HD)), lambda i, f, m: (0, 0)),
            pl.BlockSpec((8, LN), lambda i, f, m: (0, 0)),
        ],
        scratch_shapes=[
            pltpu.VMEM((n, w), bf16),
            pltpu.VMEM((nh, n, LN), f32),
            pltpu.VMEM((nh, bk, LN), f32),
            pltpu.VMEM((nh, bk, LN), f32),
        ],
    )
    return pl.pallas_call(
        functools.partial(bwd_kernel, first=group * nh, nh=nh, bq=bq, bk=bk, n=n),
        out_shape=[
            pltpu.HBM((n, lanes_up(3 * nh * HD)), bf16),
            pltpu.HBM((8, LN), f32),
        ],
        grid_spec=spec,
        compiler_params=pltpu.CompilerParams(vmem_limit_bytes=48 << 20),
        cost_estimate=cost(300 if group == 0 else 0.001),
        name="attn_bwd",
    )(block_flags(seg_row, bq, bk), mine.reshape(1), hbm(qa), hbm(kv), hbm(kv), *pieces, hbm(of), seg_row[:, None], seg_row[None], scale)


def quarter_columns(place, parts, groups, nh):
    width = nh // groups * HD
    return [
        (t * D + place * nh * HD + g * width, width) for g in range(groups) for t in range(3)
    ]


def pick_kernel(mine, w_ref, out, *, parts, groups, nh):
    for i in range(parts):

        @pl.when(mine[0] == i)
        def _(i=i):
            cut = [w_ref[:, a : a + width] for a, width in quarter_columns(i, parts, groups, nh)]
            used = sum(x.shape[1] for x in cut)
            pad = jnp.zeros((cut[0].shape[0], out.shape[1] - used), out.dtype)
            out[...] = jnp.concatenate(cut + [pad], axis=1)


def lanes_up(n):
    return -(-n // LN) * LN


def pick(w, mine, parts, groups, nh):
    rows = w.shape[0]
    step = 320 if rows % 320 == 0 else rows
    return pl.pallas_call(
        functools.partial(pick_kernel, parts=parts, groups=groups, nh=nh),
        out_shape=pltpu.HBM((rows, lanes_up(3 * nh * HD)), w.dtype),
        grid_spec=pltpu.PrefetchScalarGridSpec(
            num_scalar_prefetch=1,
            grid=(rows // step,),
            in_specs=[pl.BlockSpec((step, 3 * D), lambda i, m: (i, 0))],
            out_specs=pl.BlockSpec((step, lanes_up(3 * nh * HD)), lambda i, m: (i, 0)),
        ),
        cost_estimate=cost(5),
        name="pick",
    )(mine.reshape(1), hbm(w))


def stretch_kernel(x_ref, out, *, groups, nh):
    value = x_ref[...]
    each = 3 * nh * HD // groups
    zero = jnp.zeros((value.shape[0], LN - HD), value.dtype)
    per = nh // groups
    wide = []
    for t in range(3):
        for h in range(nh):
            at = (h // per) * each + t * per * HD + (h % per) * HD
            wide += [value[:, at : at + HD], zero]
    out[...] = jnp.concatenate(wide, axis=1)


def stretch(x, groups, nh, us):
    rows, width = x.shape
    step = 320
    return pl.pallas_call(
        functools.partial(stretch_kernel, groups=groups, nh=nh),
        out_shape=pltpu.HBM((rows, 3 * nh * LN), x.dtype),
        grid=(rows // step,),
        in_specs=[pl.BlockSpec((step, width), lambda i: (i, 0))],
        out_specs=pl.BlockSpec((step, 3 * nh * LN), lambda i: (i, 0)),
        cost_estimate=cost(us),
        name="stretch",
    )(hbm(x))


def order_kernel(own_first, a_ref, b_ref, out):
    half = pl.program_id(0)

    @pl.when(half == 0)
    def _():
        out[...] = a_ref[...].T

    @pl.when(half == 1)
    def _():
        out[...] = b_ref[...].T


def order(own, other, own_at):
    rows, width = own.shape
    step = 256
    return pl.pallas_call(
        order_kernel,
        out_shape=pltpu.HBM((width, 2 * rows), own.dtype),
        grid_spec=pltpu.PrefetchScalarGridSpec(
            num_scalar_prefetch=1,
            grid=(2, width // step),
            in_specs=[
                pl.BlockSpec((rows, step), lambda i, j, m: (0, j * (1 - i))),
                pl.BlockSpec((rows, step), lambda i, j, m: (0, j * i)),
            ],
            out_specs=pl.BlockSpec((step, rows), lambda i, j, m: (j, i ^ m[0])),
        ),
        cost_estimate=cost(200.0),
        name="order",
    )(own_at.reshape(1), hbm(own), hbm(other))


def transpose_kernel(x_ref, out):
    out[...] = x_ref[...].T


def transpose(x):
    rows, cols = x.shape
    step = 256
    return pl.pallas_call(
        transpose_kernel,
        out_shape=pltpu.HBM((cols, rows), x.dtype),
        grid=(rows // step,),
        in_specs=[pl.BlockSpec((step, cols), lambda i: (i, 0))],
        out_specs=pl.BlockSpec((cols, step), lambda i: (0, i)),
        cost_estimate=CHEAP,
        name="transpose",
    )(hbm(x))


def project_kernel(info, *refs, count, halves, width, fresh):
    pairs = refs[: 2 * count]
    gain = refs[2 * count]
    weights = refs[2 * count + 1 : 2 * count + 1 + halves]
    scale, ones = refs[2 * count + 1 + halves : 2 * count + 3 + halves]
    normed_ref, q_ref, kv_ref, mine_ref, w = refs[-5:]
    j, tile = pl.program_id(0), pl.program_id(1)
    step = normed_ref.shape[0]

    @pl.when((j == 0) & (tile == 0))
    def _():
        for i, ref in enumerate(weights):
            h = ref.shape[0]
            start = (info[count + 2] ^ i) * h if halves == 2 else 0
            w[pl.ds(pl.multiple_of(start, 16), h), :] = ref[...]
        if not fresh:
            mine_ref[...] = refs[2 * count + 3 + halves][...]

    def work(x_ref):
        value = x_ref[...]
        x = value.astype(f32)
        inverse = lax.rsqrt(jnp.mean(x * x, axis=-1, keepdims=True) + epsilon)
        normed = (x * inverse * gain[...]).astype(bf16)
        normed_ref[...] = normed
        q_ref[...] = (
            jnp.dot(normed, w[:, :width], preferred_element_type=f32) * scale[...]
        ).astype(bf16)
        kv_ref[...] = (
            jnp.dot(normed, w[:, width:], preferred_element_type=f32) + ones[...]
        ).astype(bf16)

        @pl.when(info[count + 1] == info[j])
        def _():
            mine_ref[pl.ds(pl.multiple_of(tile * step, step), step), :] = value

    for i in range(count):
        for lane in range(2):

            @pl.when((j == i) & (info[count] == lane))
            def _(i=i, lane=lane):
                work(pairs[2 * i + 1 - lane])


def project(pairs, places, lane, mine, wt, gain, weights, scale, ones, group_len, carried=None):
    count = len(pairs)
    rows, d = pairs[0][0].shape
    width = scale.shape[1]
    step = 256
    tiles = rows // step
    full = lambda j, t, f: (0, 0)
    at = lambda j, t, f: (f[j] * tiles + t, 0)
    once = pl.Buffered(1)
    info = jnp.stack(list(places) + [lane.astype(jnp.int32), mine, wt])
    args = [x for pair in pairs for x in pair] + [gain, *map(hbm, weights), scale, ones]
    in_specs = [
        pl.BlockSpec(
            (step, d),
            lambda j, t, f, i=i: (jnp.where(j == i, t, jnp.where(j > i, tiles - 1, 0)), 0),
        )
        for i in range(count)
        for _ in range(2)
    ]
    in_specs += [pl.BlockSpec((1, d), full, pipeline_mode=once)]
    in_specs += [pl.BlockSpec(w.shape, full, pipeline_mode=once) for w in weights]
    in_specs += [
        pl.BlockSpec((1, width), full, pipeline_mode=once),
        pl.BlockSpec((1, 2 * width), full, pipeline_mode=once),
    ]
    aliases = {}
    if carried is not None:
        base = len(args) + 2
        args += [hbm(x) for x in (carried[3], *carried[:3])]
        in_specs += [pl.BlockSpec((rows, d), full, pipeline_mode=once)]
        in_specs += [pl.BlockSpec(memory_space=pl.ANY)] * 3
        aliases = {base: 0, base + 1: 1, base + 2: 2}
    return pl.pallas_call(
        functools.partial(
            project_kernel, count=count, halves=len(weights), width=width, fresh=carried is None
        ),
        out_shape=[
            pltpu.HBM((group_len, d), bf16),
            pltpu.HBM((group_len, width), bf16),
            pltpu.HBM((group_len, 2 * width), bf16),
            pltpu.HBM((rows, d), bf16),
        ],
        grid_spec=pltpu.PrefetchScalarGridSpec(
            num_scalar_prefetch=1,
            grid=(count, tiles),
            in_specs=in_specs,
            out_specs=[
                pl.BlockSpec((step, d), at),
                pl.BlockSpec((step, width), at),
                pl.BlockSpec((step, 2 * width), at),
                pl.BlockSpec((rows, d), full),
            ],
            scratch_shapes=[pltpu.VMEM((d, 3 * width), bf16)],
        ),
        input_output_aliases=aliases,
        compiler_params=pltpu.CompilerParams(vmem_limit_bytes=32 << 20),
        cost_estimate=cost(15),
        name="project",
    )(info, *args)


def tail_body(at, p0, p1, p2, p3, x_ref, g_ref, w_s, gain, outs, need):
    lo_ref, left_ref, right_ref, gr_ref, c0, c1, c2, c3, gg_ref = outs
    att_ref, nm_ref, act_ref = (left_ref.at[i] for i in range(3))
    gp_ref, gh_ref = (right_ref.at[i] for i in range(2))
    right_ref[2] = g_ref[...]
    mine = at[0]
    pieces = (p0, p1, p2, p3)
    cols = p0.shape[1]
    nt = (((1,), (1,)), ((), ()))
    for i in range(4):

        @pl.when(mine == i)
        def _(i=i):
            att_ref[...] = jnp.concatenate([pieces[i ^ k][...] for k in range(4)], axis=1)

    need(0)
    resid = x_ref[...].astype(f32) + jnp.dot(att_ref[...], w_s[0], preferred_element_type=f32)
    inverse = lax.rsqrt(jnp.mean(resid * resid, axis=-1, keepdims=True) + epsilon)
    normed = (resid * inverse * gain[...]).astype(bf16)
    nm_ref[...] = normed
    need(1)
    hidden = jnp.dot(normed, w_s[1], preferred_element_type=f32)
    sig = 1.0 / (1.0 + jnp.exp(-hidden))
    active = (hidden * sig).astype(bf16)
    act_ref[...] = active
    need(2)
    lo_ref[...] = (resid + jnp.dot(active, w_s[2], preferred_element_type=f32)).astype(bf16)
    grad_active = lax.dot_general(g_ref[...], w_s[2], nt, preferred_element_type=f32)
    grad_hidden = (grad_active * sig * (1.0 + hidden * (1.0 - sig))).astype(bf16)
    gh_ref[...] = grad_hidden
    grad_normed = lax.dot_general(grad_hidden, w_s[1], nt, preferred_element_type=f32)
    gg_ref[...] += jnp.sum(grad_normed * resid * inverse, axis=0, keepdims=True)
    scaled = grad_normed * gain[...]
    grad_resid = (
        g_ref[...].astype(f32)
        + inverse * scaled
        - resid * (inverse * inverse * inverse) * jnp.mean(scaled * resid, axis=-1, keepdims=True)
    )
    gr_ref[...] = grad_resid
    grad_proj = grad_resid.astype(bf16)
    gp_ref[...] = grad_proj
    grad_att = lax.dot_general(grad_proj, w_s[0], nt, preferred_element_type=f32).astype(bf16)
    for i in range(4):

        @pl.when(mine == i)
        def _(i=i):
            for j, out in enumerate((c0, c1, c2, c3)):
                out[...] = grad_att[:, (i ^ j) * cols : ((i ^ j) + 1) * cols]


def tail_kernel(at, p0, p1, p2, p3, x_ref, g_ref, own0, own1, own2, half0, half, other0, other, gain, *refs, rows, hrows):
    w_s, sems = refs[-2:]
    outs = refs[:-2]

    def copies(i):
        parts = (
            ((own0, own1, own2)[i], at[1], rows),
            (half.at[i - 1] if i else half0, at[2], hrows),
            (other.at[i - 1] if i else other0, at[3], hrows),
        )
        return [
            pltpu.make_async_copy(
                part, w_s.at[i, pl.ds(pl.multiple_of(start, 16), n), :], sems.at[3 * i + k]
            )
            for k, (part, start, n) in enumerate(parts)
        ]

    @pl.when(pl.program_id(0) == 0)
    def _():
        outs[-1][...] = jnp.zeros_like(outs[-1])
        for i in range(3):
            for c in copies(i):
                c.start()

    def need(i):
        @pl.when(pl.program_id(0) == 0)
        def _():
            for c in copies(i):
                c.wait()

    tail_body(at, p0, p1, p2, p3, x_ref, g_ref, w_s, gain, outs, need)


def whole_tail_kernel(at, p0, p1, p2, p3, x_ref, g_ref, w, gain, *outs):
    @pl.when(pl.program_id(0) == 0)
    def _():
        outs[-1][...] = jnp.zeros_like(outs[-1])

    tail_body(at, p0, p1, p2, p3, x_ref, g_ref, w, gain, outs, lambda i: None)


def tail(at, pieces, x, g, weights, gain, tile=256):
    rows, d = x.shape
    cols = pieces[0].shape[1]
    row = lambda i, m: (i, 0)
    once = pl.Buffered(1)
    whole = lambda *shape: pl.BlockSpec(shape, lambda i, m: (0,) * len(shape), pipeline_mode=once)
    wide = pl.BlockSpec((tile, d), row)
    slim = pl.BlockSpec((tile, cols), row)
    if len(weights) == 7:
        body = functools.partial(tail_kernel, rows=weights[0].shape[0], hrows=weights[3].shape[0])
        scratch = [pltpu.VMEM((3, d, d), bf16), pltpu.SemaphoreType.DMA((9,))]
        weight_specs = [pl.BlockSpec(memory_space=pl.ANY)] * 7
    else:
        body = whole_tail_kernel
        scratch = []
        weight_specs = [whole(*w.shape) for w in weights]
    return pl.pallas_call(
        body,
        out_shape=[pltpu.HBM((rows, d), bf16)]
        + [pltpu.HBM((3, rows, d), bf16)] * 2
        + [pltpu.HBM((rows, d), f32)]
        + [pltpu.HBM((rows, cols), bf16)] * 4
        + [pltpu.HBM((1, d), f32)],
        grid_spec=pltpu.PrefetchScalarGridSpec(
            num_scalar_prefetch=1,
            grid=(rows // tile,),
            in_specs=[slim] * 4 + [wide] * 2 + weight_specs + [whole(1, d)],
            out_specs=[wide]
            + [pl.BlockSpec((3, tile, d), lambda i, m: (0, i, 0))] * 2
            + [wide]
            + [slim] * 4
            + [pl.BlockSpec((1, d), lambda i, m: (0, 0))],
            scratch_shapes=scratch,
        ),
        compiler_params=pltpu.CompilerParams(vmem_limit_bytes=52 << 20),
        cost_estimate=cost(0.01),
        name="tail",
    )(at, *pieces, hbm(x), g, *map(hbm, weights), gain)


tn_dims = (((0,), (0,)), ((), ()))


def share_kernel(col, left, right, out):
    value = lax.dot_general(left[0], right[0], tn_dims, preferred_element_type=f32)
    out[...] = value.astype(bf16)


def share(left, right, col):
    n, rows, d = left.shape
    w = d // 2
    block = pl.BlockSpec((d, w), lambda i, c: (0, i))
    return pl.pallas_call(
        share_kernel,
        out_shape=pltpu.HBM((d, n * w), bf16),
        grid_spec=pltpu.PrefetchScalarGridSpec(
            num_scalar_prefetch=1,
            grid=(n,),
            in_specs=[
                pl.BlockSpec((1, rows, d), lambda i, c: (i, 0, 0)),
                pl.BlockSpec((1, rows, w), lambda i, c: (i, 0, c[0])),
            ],
            out_specs=block,
        ),
        compiler_params=pltpu.CompilerParams(vmem_limit_bytes=20 << 20),
        cost_estimate=CHEAP,
        name="share",
    )(col.reshape(1), hbm(left), hbm(right))


def copy(x):
    return pl.pallas_call(
        tick_kernel, out_shape=pltpu.HBM(x.shape, x.dtype), cost_estimate=CHEAP, name="copy"
    )(x)


def tick_kernel(x_ref, out):
    out[...] = x_ref[...]


def tick(x):
    return pl.pallas_call(
        tick_kernel, out_shape=jax.ShapeDtypeStruct(x.shape, x.dtype), cost_estimate=cost(200.0), name="tick"
    )(x)


def total_kernel(*refs, counts):
    out = refs[-1]
    start, column = 0, 0
    for count in counts:
        group = refs[start : start + count]
        start += count
        acc = jnp.zeros(group[0].shape[1:], f32)
        for ref in group:
            for i in range(ref.shape[0]):
                acc = acc + ref[i].astype(f32)
        out[:, column : column + acc.shape[1]] = acc.astype(bf16)
        column += acc.shape[1]


def total(groups):
    flat = [x for group in groups for x in group]
    rows = flat[0].shape[1]
    cuts = 2 if rows % 32 == 0 else 1
    width = sum(group[0].shape[2] for group in groups)
    return pl.pallas_call(
        functools.partial(total_kernel, counts=[len(group) for group in groups]),
        out_shape=pltpu.HBM((rows, width), bf16),
        grid=(cuts,),
        in_specs=[
            pl.BlockSpec((x.shape[0], rows // cuts, x.shape[2]), lambda i: (0, i, 0)) for x in flat
        ],
        out_specs=pl.BlockSpec((rows // cuts, width), lambda i: (i, 0)),
        compiler_params=pltpu.CompilerParams(vmem_limit_bytes=16 << 20),
        cost_estimate=cost(0.001),
        name="total",
    )(*flat)


def add_kernel(a_ref, b_ref, out):
    out[...] = (a_ref[...].astype(f32) + b_ref[...].astype(f32)).astype(bf16)


def add(a, b):
    return pl.pallas_call(
        add_kernel, out_shape=pltpu.HBM(a.shape, bf16), cost_estimate=CHEAP, name="add"
    )(a, b)


def add_rows(a, b):
    rows, cols = a.shape
    block = pl.BlockSpec((rows // 2, cols), lambda i: (i, 0))
    return pl.pallas_call(
        add_kernel,
        out_shape=pltpu.HBM(a.shape, bf16),
        grid=(2,),
        in_specs=[block] * 2,
        out_specs=block,
        compiler_params=pltpu.CompilerParams(vmem_limit_bytes=24 << 20),
        cost_estimate=CHEAP,
        name="add_rows",
    )(hbm(a), hbm(b))


def by_bits(first, second, put):
    for i in range(2):
        for j in range(2):

            @pl.when((first == i) & (second == j))
            def _(i=i, j=j):
                put(i, j)


def place_kernel(at, *refs):
    o0, o1, o2 = refs[-3:]
    block = pl.program_id(0)
    w = o0.shape[2] // 2

    def put(other_x, other_near):
        for core in range(2):

            @pl.when(at[2] == core)
            def _(core=core):
                for side in range(2):
                    part = refs[4 * (side ^ core) + 2 * other_x + other_near][...].astype(f32)
                    for i, out in enumerate((o0, o1, o2)):
                        out[0, :, side * w : (side + 1) * w] = part[:, i * w : (i + 1) * w]

    by_bits((block // 2) ^ at[0], (block % 2) ^ at[1], put)


def place_tail(arrays, at):
    h, width = arrays[0].shape
    d = width // 3 * 2
    whole = pl.BlockSpec((h, width), lambda i, m: (0, 0), pipeline_mode=pl.Buffered(1))
    outs = pl.pallas_call(
        place_kernel,
        out_shape=[pltpu.HBM((4, h, d), f32)] * 3,
        grid_spec=pltpu.PrefetchScalarGridSpec(
            num_scalar_prefetch=1,
            grid=(4,),
            in_specs=[whole] * 8,
            out_specs=[pl.BlockSpec((1, h, d), lambda i, m: (i, 0, 0))] * 3,
        ),
        compiler_params=pltpu.CompilerParams(vmem_limit_bytes=16 << 20),
        cost_estimate=CHEAP,
        name="place_tail",
    )(at, *map(hbm, arrays))
    return [out.reshape(4 * h, d) for out in outs]


def cross_kernel(at, x_ref, g_ref, *refs):
    s = refs[-1]
    s[...] = jnp.dot(x_ref[...], g_ref[...], preferred_element_type=f32)
    half = s.shape[0] // 2
    for w in range(2):

        @pl.when(pl.program_id(0) == w)
        def _(w=w):
            for x in range(2):
                rows = pl.ds(pl.multiple_of((at[1] ^ x) * half, 16), half)
                refs[2 * w + x][...] = s[rows, :].astype(bf16)


def cross(x, g, at):
    d, rows = x.shape
    w = d // 2
    cols = g.shape[1]
    step = 512 if cols % 512 == 0 else cols
    n = cols // step
    first = pl.BlockSpec((w // 2, step), lambda i, j, m: (0, jnp.where(i == 0, j, n - 1)))
    second = pl.BlockSpec((w // 2, step), lambda i, j, m: (0, jnp.where(i == 1, j, 0)))
    return pl.pallas_call(
        cross_kernel,
        out_shape=[pltpu.HBM((w // 2, cols), bf16)] * 4,
        grid_spec=pltpu.PrefetchScalarGridSpec(
            num_scalar_prefetch=1,
            grid=(2, n),
            in_specs=[
                pl.BlockSpec((w, rows), lambda i, j, m: (m[0] ^ i, 0)),
                pl.BlockSpec((rows, step), lambda i, j, m: (0, j)),
            ],
            out_specs=[first, first, second, second],
            scratch_shapes=[pltpu.VMEM((w, step), f32)],
        ),
        compiler_params=pltpu.CompilerParams(vmem_limit_bytes=26 << 20),
        cost_estimate=CHEAP,
        name="cross",
    )(at, hbm(x), hbm(g))


def spread_kernel(at, *refs, width):
    out = refs[-1]
    step = out.shape[1]
    rows = pl.ds(pl.multiple_of(pl.program_id(0) * step, step), step)

    def put(core, near):
        cut = []
        for t in range(3):
            for n in range(2):
                for c in range(2):
                    part = refs[2 * (c ^ core) + (n ^ near)][rows, :]
                    cut.append(part[:, t * width : (t + 1) * width])
        out[0] = jnp.concatenate(cut, axis=1).astype(f32)

    by_bits(at[2], at[1], put)


def spread(arrays, at, used, other_x, carried=None):
    rows, cols = arrays[0].shape
    width = 4 * used
    cuts = 2 if rows % 32 == 0 else 1
    whole = pl.BlockSpec((rows, cols), lambda j, m: (0, 0), pipeline_mode=pl.Buffered(1))
    more = () if carried is None else (carried,)
    return pl.pallas_call(
        functools.partial(spread_kernel, width=used // 3),
        out_shape=pltpu.HBM((2, rows, width), f32),
        grid_spec=pltpu.PrefetchScalarGridSpec(
            num_scalar_prefetch=1,
            grid=(cuts,),
            in_specs=[whole] * 4 + [pl.BlockSpec(memory_space=pl.ANY)] * len(more),
            out_specs=pl.BlockSpec((1, rows // cuts, width), lambda j, m: (m[0] ^ other_x, j, 0)),
        ),
        input_output_aliases={5: 0} if more else {},
        compiler_params=pltpu.CompilerParams(vmem_limit_bytes=20 << 20),
        cost_estimate=CHEAP,
        name="spread",
    )(at, *arrays, *more)


def back_kernel(shards, g_ref, w_ref, *refs):
    acc = jnp.dot(g_ref[...], w_ref[...], preferred_element_type=f32)
    if len(refs) == 2:
        acc = acc + refs[0][0].astype(f32)
    refs[-1][0] = acc.astype(bf16)


def back(grad, w, shards, rows, got=None):
    c, d = w.shape
    n = shards.shape[0]
    step = d
    out = pl.BlockSpec((1, rows, step), lambda j, i, f: (i, 0, j))
    in_specs = [
        pl.BlockSpec((rows, c), lambda j, i, f: (f[i], 0)),
        pl.BlockSpec((c, step), lambda j, i, f: (0, j)),
    ]
    args = [hbm(grad), hbm(w)]
    if got is not None:
        in_specs.append(pl.BlockSpec((1, rows, step), lambda j, i, f: (0, 0, j)))
        args.append(got)
    return pl.pallas_call(
        back_kernel,
        out_shape=pltpu.HBM((n, rows, d), bf16),
        grid_spec=pltpu.PrefetchScalarGridSpec(
            num_scalar_prefetch=1, grid=(d // step, n), in_specs=in_specs, out_specs=out
        ),
        compiler_params=pltpu.CompilerParams(vmem_limit_bytes=22 << 20),
        cost_estimate=CHEAP,
        name="back",
    )(shards, *args)


def finish_kernel(shard, g_ref, w_ref, core, near, x_ref, resid, gain, out, gain_out):
    grad = jnp.dot(g_ref[...], w_ref[...], preferred_element_type=f32)
    grad = grad + core[0].astype(f32) + near[0].astype(f32)
    x = x_ref[...].astype(f32)
    inverse = lax.rsqrt(jnp.mean(x * x, axis=-1, keepdims=True) + epsilon)
    part = jnp.sum(grad * x * inverse, axis=0, keepdims=True)

    @pl.when(pl.program_id(0) == 0)
    def _():
        gain_out[...] = jnp.zeros_like(gain_out)

    gain_out[...] += part
    scaled = grad * gain[...]
    out[...] = (
        resid[...]
        + inverse * scaled
        - x * (inverse * inverse * inverse) * jnp.mean(scaled * x, axis=-1, keepdims=True)
    ).astype(bf16)


def finish(grad, w, shard, core, near, x, resid, gain, tile=256):
    rows, d = x.shape
    c = w.shape[0]
    tiles = rows // tile
    row = lambda i, f: (i, 0)
    once = pl.Buffered(1)
    return pl.pallas_call(
        finish_kernel,
        out_shape=[pltpu.HBM((rows, d), bf16), jax.ShapeDtypeStruct((1, d), f32)],
        grid_spec=pltpu.PrefetchScalarGridSpec(
            num_scalar_prefetch=1,
            grid=(tiles,),
            in_specs=[
                pl.BlockSpec((tile, c), lambda i, f: (f[0] * tiles + i, 0)),
                pl.BlockSpec((c, d), lambda i, f: (0, 0), pipeline_mode=once),
                pl.BlockSpec((1, tile, d), lambda i, f: (1, i, 0)),
                pl.BlockSpec((1, tile, d), lambda i, f: (0, i, 0)),
                pl.BlockSpec((tile, d), row),
                pl.BlockSpec((tile, d), row),
                pl.BlockSpec((1, d), lambda i, f: (0, 0)),
            ],
            out_specs=[pl.BlockSpec((tile, d), row), pl.BlockSpec((1, d), lambda i, f: (0, 0))],
        ),
        compiler_params=pltpu.CompilerParams(vmem_limit_bytes=24 << 20),
        cost_estimate=CHEAP,
        name="finish",
    )(shard.reshape(1), hbm(grad), hbm(w), core, near, hbm(x), hbm(resid), gain)


def rms_inverse(values):
    return lax.rsqrt(jnp.mean(values * values, axis=-1, keepdims=True) + epsilon)


def norm_back(values, inverse, grad_scaled):
    return inverse * grad_scaled - values * (inverse * inverse * inverse) * jnp.mean(
        grad_scaled * values, axis=-1, keepdims=True
    )


def dot(left, right):
    return jnp.dot(left, right, preferred_element_type=f32)


def times_trans(left, right):
    return lax.dot_general(left, right, (((1,), (1,)), ((), ())), preferred_element_type=f32)


def trans_times(left, right):
    return lax.dot_general(left, right, (((0,), (0,)), ((), ())), preferred_element_type=f32)


def rows_at(array, start, count):
    return lax.dynamic_slice_in_dim(array, start, count, 0)


def put_rows(array, rows, start):
    return lax.dynamic_update_slice_in_dim(array, rows, start, 0)


def make_local(sizes):
    def pairs(target):
        found = []
        for gx in range(sizes["gx"]):
            for gc in range(sizes["gc"]):
                for z in range(4):
                    for w in range(sizes["wt"]):
                        goal = target(gx, gc, z, w)
                        if goal is not None and goal != (gx, gc, z, w):
                            found.append((place(gx, gc, z, w), place(*goal)))
        return found

    def place(gx, gc, z, w):
        return ((gx * sizes["gc"] + gc) * 4 + z) * sizes["wt"] + w

    def send(value, target):
        return lax.ppermute(value, AXES, pairs(target))

    def core_mate(gx, gc, z, w):
        return (gx, 1 - gc, z, w)

    def x_mate(gx, gc, z, w):
        return (1 - gx, gc, z, w)

    def near_mate(gx, gc, z, w):
        return (gx, gc, z ^ 1, w)

    def far_mate(gx, gc, z, w):
        return (gx, gc, z ^ 2, w)

    def cross_mate(gx, gc, z, w):
        return (gx, 1 - gc, z ^ 1, w)

    def wt_mate(gx, gc, z, w):
        return (gx, gc, z, 1 - w)

    def wt_x_mate(gx, gc, z, w):
        return (1 - gx, gc, z, 1 - w)

    def to_host(gx, gc, z, w):
        return (gx, 1 - (z & 1), 2 * gc + (z >> 1), w)

    def to_home(gx, gc, z, w):
        return (gx, z >> 1, 2 * (z & 1) + 1 - gc, w)

    def hop1(gx, gc, z, w):
        if gc == 0:
            return (gx, 0, z - 1, w) if z > 0 else None
        return (gx, 1, z + 1, w) if z < 3 else None

    def hop2(gx, gc, z, w):
        if gc == 0:
            return (gx, 0, z - 1, w) if z in (1, 2) else None
        return (gx, 1, z + 1, w) if z in (1, 2) else None

    def hop3(gx, gc, z, w):
        if gc == 0:
            return (gx, 0, z ^ 1, w) if z < 2 else None
        return (gx, 1, z ^ 1, w) if z > 1 else None

    def lane_share(gx, gc, z, w):
        return (gx, 1 - gc, z, w) if gc == z >> 1 else None

    def sum_all(value):
        for axis in ("gc", "wt", "near", "far", "gx"):
            step = 1
            while step < sizes[axis]:

                def mate(gx, gc, z, w, axis=axis, step=step):
                    at = dict(gx=gx, gc=gc, far=z >> 1, near=z & 1, wt=w)
                    at[axis] ^= step
                    return (at["gx"], at["gc"], 2 * at["far"] + at["near"], at["wt"])

                value = value + send(value, mate)
                step *= 2
        return value

    def local(
        tokens, segments, w_qkv, w_proj, w_in, w_out, gain_attn, gain_mlp, query_scale, cotangent
    ):
        gx, gc, host, near, wt = (lax.axis_index(axis) for axis in AXES)
        z = 2 * host + near
        mine = 2 * near + 1 - gc
        parts = 4
        nh = H // parts
        groups = 1
        rows = tokens.shape[1]
        group_len = segments.shape[1]
        wrows = w_qkv.shape[0]
        lane = gc == host
        pair = sizes["wt"] == 2

        def after(value, *others):
            return lax.optimization_barrier((value,) + others)[0]

        picked = pick(w_qkv, mine, parts, groups, nh)
        own = tokens[0]
        got1 = send(own, hop1)
        own_share = send(after(own, picked), lane_share)
        seg_mate = send(after(segments, picked), core_mate)
        got2 = send(got1, hop2)
        got1_share = send(got1, lane_share)
        end = jnp.where(gc == 0, z == 0, z == 3)
        if pair:
            wide_own = stretch(picked, groups, nh, 2)
            got1 = after(got1, wide_own)
            other_w = send(picked, wt_mate)
            wide_w = (wide_own, stretch(other_w, groups, nh, 10))
        else:
            flat_all = lax.all_gather(picked, "wt", axis=0, tiled=True)
            by_head = jnp.transpose(
                flat_all[:, : 3 * nh * HD].reshape(D, groups, 3, nh // groups, HD), (0, 2, 1, 3, 4)
            )
            wide_w = (
                jnp.pad(
                    by_head.reshape(D, 3 * nh, HD), ((0, 0), (0, 0), (0, LN - HD))
                ).reshape(D, -1),
            )
        got3 = send(jnp.where(end, own, got2), hop3)
        got2_share = send(got2, lane_share)
        way = 1 - 2 * host
        last = jnp.where(host == 0, jnp.where(z == 0, 3, 0), jnp.where(z == 3, 0, 3))
        places = (z, z + way, z + 2 * way, last)

        half_rows = wrows // 2
        if pair:
            half_a = send(after(rows_at(w_proj, gc * half_rows, half_rows), other_w), wt_mate)
            half_w = jnp.stack([rows_at(w, gc * half_rows, half_rows) for w in (w_in, w_out)])
            half_w = send(after(half_w, half_a), wt_mate)
        else:
            half_w = jnp.stack([rows_at(w, gc * half_rows, half_rows) for w in (w_proj, w_in, w_out)])
            half_w = lax.all_gather(half_w, "wt", axis=0, tiled=False)

        dim_scale = scale_base / math.sqrt(HD) * jax.nn.softplus(query_scale)
        lane_scale = jnp.tile(jnp.pad(dim_scale * log2e, (0, LN - HD)), nh)[None]
        ones = jnp.tile(
            ((jnp.arange(LN) >= HD) & (jnp.arange(LN) < HD + 3)).astype(f32), 2 * nh
        )[None]
        seg_row = jnp.where(lane, segments, seg_mate)[0]
        fixed = (lane, mine, wt, gain_attn[None], wide_w, lane_scale, ones, group_len)
        carried = project(((own, own_share), (got1, got1_share)), places[:2], *fixed)
        got3_share = send(after(got3, carried[0]), lane_share)
        first_done = (lambda x: after(x, half_a)) if pair else (lambda x: x)
        all_normed, queries, keyval, inputs = project(
            ((got2, got2_share), (got3, first_done(got3_share))), places[2:], *fixed, carried=carried
        )
        grad_mlp = send(after(cotangent[0], got3_share), to_host)

        att, att_float, q_aug = attn_fwd(queries, keyval, seg_row, nh)
        att, half_w, _ = lax.optimization_barrier((att, half_w, grad_mlp))

        trades = (core_mate, near_mate, cross_mate)
        att_pieces = [rows_at(att, (mine ^ j) * rows, rows) for j in range(parts)]
        half_mate = send(after(half_w, *att_pieces), core_mate)
        att_pieces = [att_pieces[0]] + [send(att_pieces[j + 1], trades[j]) for j in range(3)]
        if pair:
            w_trans = order(after(picked, att), other_w, wt)
        else:
            w_trans = flat_all.T
        normed_trans = transpose(after(all_normed, w_trans))
        if pair:
            mate_a = send(after(half_a, *att_pieces[1:2]), core_mate)
            weights = (w_proj, w_in, w_out, half_a, half_w, mate_a, half_mate)
            starts = (wt * wrows, (1 - wt) * wrows + gc * half_rows, (1 - wt) * wrows + (1 - gc) * half_rows)
        else:
            one = gc == 0
            tail_w = jnp.stack(
                [jnp.where(one, half_w, half_mate), jnp.where(one, half_mate, half_w)], axis=1
            )
            weights = (jnp.transpose(tail_w, (2, 0, 1, 3, 4)).reshape(3, D, D),)
            starts = ()
        (
            layer_out,
            left,
            right,
            grad_resid,
            *pieces,
            grad_gain_mlp,
        ) = tail(
            jnp.stack([mine, *starts]), att_pieces, after(inputs, normed_trans), grad_mlp, weights, gain_mlp[None]
        )
        pieces = [pieces[0]] + [send(pieces[j + 1], trades[j]) for j in range(3)]

        shared = share(after(left, pieces[1]), right, 1 - gc)
        from_core = send(shared, core_mate)
        own_half = share(left, right, after(gc, shared))
        pieces[2:] = [after(piece, own_half) for piece in pieces[2:]]
        home_out = send(after(layer_out, *pieces[1:]), to_home)
        late_gain = tick(after(gain_attn.reshape(-1, LN), *pieces[1:]))
        summed = add_rows(own_half, after(from_core, late_gain))
        kept = lax.all_to_all(summed, ("wt", "gx", "near"), 0, 0, tiled=True)

        scale_row = jnp.tile(dim_scale, nh // groups)[None]

        def backward(group, *others):
            first, *rest = pieces
            return attn_bwd(
                q_aug,
                keyval,
                (after(first, summed, *others), *rest),
                att_float,
                mine,
                seg_row,
                scale_row,
                nh,
                group,
                groups,
            )

        def by_rows(grad):
            if pair:
                own, *rest = cross(normed_trans, grad, jnp.stack([wt, gx]))
                got = [send(part, mate) for part, mate in zip(rest, (x_mate, wt_mate, wt_x_mate))]
                return [part[None] for part in (own, *got)]
            part = dot(normed_trans, grad).astype(bf16)
            sources = sizes["wt"] * 2
            got = lax.all_to_all(part, ("wt", "gx"), 0, 0, tiled=True)
            return [got.reshape(sources, D // sources, -1)]

        grad_project, grad_lanes = backward(0)
        layer_out = after(home_out, grad_project)

        last_step = [layer_out]

        def turn(value):
            return after(value, *last_step)

        def done(value):
            last_step[0] = value
            return value

        sources = sizes["wt"] * 4
        to_core = done(back(turn(grad_project), w_trans, jnp.stack([mine ^ 3, mine ^ 1]), rows))
        from_core = send(to_core, core_mate)
        by_place = by_rows(turn(grad_project))
        done(by_place[0])
        to_near = done(back(grad_project, w_trans, (mine ^ 2).reshape(1), rows, turn(from_core)))
        from_near = send(to_near, near_mate)
        t1 = done(total([[turn(kept).reshape(sources, D // sources, -1)]]))
        t1_far = send(t1, far_mate)
        layer_out = done(copy(turn(layer_out)))
        by_place[0] = turn(by_place[0])
        q1 = done(total([by_place]))
        q1_far = send(q1, far_mate)
        t2 = done(add(turn(t1), t1_far))
        t2_near = send(t2, near_mate)
        t2_x = send(t2, x_mate)
        grad_tokens, grad_gain_attn = finish(
            grad_project,
            w_trans,
            mine,
            from_core,
            turn(from_near),
            inputs,
            grad_resid,
            late_gain.reshape(1, -1),
        )
        done(grad_tokens)
        grad_query_scale = (
            grad_lanes[0, :HD]
            / (dim_scale * log2e)
            * (scale_base / math.sqrt(HD))
            * jax.nn.sigmoid(query_scale)
        )
        small = jnp.concatenate(
            [grad_gain_attn[0], grad_gain_mlp[0], jnp.pad(grad_query_scale, (0, LN - HD))]
        ).reshape(-1, LN)
        t2_x = done(turn(t2_x))
        t2_near = done(turn(t2_near))
        t2_near_x = send(t2_near, x_mate)
        tails = [t2, t2_near, t2_x]
        tails_mate = [send(turn(x), core_mate) for x in tails]
        q2 = done(add(turn(q1), q1_far))
        q2_near = send(q2, near_mate)
        q2_x = send(q2, x_mate)
        home_grad = send(turn(grad_tokens), to_home)
        q2_near = done(turn(q2_near))
        q2_near_x = send(q2_near, x_mate)
        t2_near_x = done(turn(t2_near_x))
        tails += [t2_near_x]
        tails_mate += [send(t2_near_x, core_mate)]
        q2_x = done(turn(q2_x))
        quads_mate = [send(turn(x), core_mate) for x in (q2, q2_near, q2_x)]
        tails_mate[3] = turn(tails_mate[3])
        totals = place_tail(tails + tails_mate, jnp.stack([gx, near, gc]))
        done(totals[0])
        used = 3 * nh * HD
        spread_at = jnp.stack([gx, near, 1 - gc])
        quads_mate[0] = done(after(turn(quads_mate[0]), quads_mate[1]))
        small = done(sum_all(turn(small))).reshape(-1)
        home_grad = done(turn(home_grad))
        q2_near_x = done(turn(q2_near_x))
        last_mate = send(q2_near_x, core_mate)
        total_qkv = done(
            spread((turn(q2), q2_near, quads_mate[0], quads_mate[1]), spread_at, used, 0)
        )
        grad_tokens = done(copy(turn(home_grad)))
        total_qkv = spread(
            (q2_x, turn(q2_near_x), quads_mate[2], last_mate), spread_at, used, 1, total_qkv
        ).reshape(wrows, 3 * D)
        return (
            layer_out[None],
            grad_tokens[None],
            total_qkv,
            *totals,
            small[:D],
            small[D : 2 * D],
            small[2 * D : 2 * D + HD],
        )

    return local


def solution(mesh):
    groups, parts, wt = (mesh.shape[axis] for axis in ("grp", "ctx", "wt"))
    inner = Mesh(mesh.devices.reshape(groups // 2, 2, parts // 2, 2, wt), AXES)
    sizes = dict(inner.shape)
    split = P(("gx", "gc", "wt"), ("far", "near"), None)
    weight = P("wt", None)
    return jax.shard_map(
        make_local(sizes),
        mesh=inner,
        in_specs=(
            split,
            P(("gx", "gc", "wt"), None),
            weight,
            weight,
            weight,
            weight,
            P(),
            P(),
            P(),
            split,
        ),
        out_specs=(split, split, weight, weight, weight, weight, P(), P(), P()),
        check_vma=False,
    )
```
